32 devices in a mesh: dp: 4 (over y, x), mp: 8 (over z, core).
Axes of the slice: x: 2, y: 2, z: 4, core: 2. Of those that a mesh axis runs over, the one named last changes fastest.
Arguments:
- frames: bfloat16 [1024, 12, 1280], P('mp', 'dp'), may hold values from -6 to 6
- lengths: int32 [12], P('dp'), may hold values from 1 to 1024, 10752 in all
- key_mask: int32 [12, 1024], P('dp'), may hold values from 0 to 1, as said below
- cotangent: bfloat16 [1024, 12, 1280], P('mp', 'dp'), may hold values from -6 to 6
- gain_one: bfloat16 [1280], replicated, may hold values from 0.5 to 1.5
- shift_one: bfloat16 [1280], replicated, may hold values from -1.5 to 1.5
- query_weight: bfloat16 [1280, 1280], P(None, 'mp'), may hold values from -0.25 to 0.25
- query_bias: bfloat16 [1280], P('mp'), may hold values from -2.5 to 2.5
- key_weight: bfloat16 [1280, 1280], P(None, 'mp'), may hold values from -0.25 to 0.25
- value_weight: bfloat16 [1280, 1280], P(None, 'mp'), may hold values from -0.15625 to 0.15625
- value_bias: bfloat16 [1280], P('mp'), may hold values from -2.5 to 2.5
- out_weight: bfloat16 [1280, 1280], P('mp'), may hold values from -0.625 to 0.625
- out_bias: bfloat16 [1280], replicated, may hold values from -1.5 to 1.5
- gain_two: bfloat16 [1280], replicated, may hold values from 0.5 to 1.5
- shift_two: bfloat16 [1280], replicated, may hold values from -1.5 to 1.5
- up_weight: bfloat16 [1280, 5120], P(None, 'mp'), may hold values from -0.15625 to 0.15625
- up_bias: bfloat16 [5120], P('mp'), may hold values from -2.5 to 2.5
- down_weight: bfloat16 [5120, 1280], P('mp'), may hold values from -0.125 to 0.125
- down_bias: bfloat16 [1280], replicated, may hold values from -1.5 to 1.5
- master: float32 [8, 2459520], P('mp', 'dp'), may hold values from -0.15 to 0.15
- moment_one: float32 [8, 2459520], P('mp', 'dp'), may hold values from -60 to 60
- moment_two: float32 [8, 2459520], P('mp', 'dp'), may hold values from 1 to 100
- adam_step: int32 [1], replicated, may hold values from 1 to 999
- hyper_rates: float32 [3], replicated, may hold values from 0.001 to 5, as said below
Outputs:
- layer_out: bfloat16 [1024, 12, 1280], P('mp', 'dp')
- input_grad: float32 [1024, 12, 1280], P('mp', 'dp')
- weight_grads: float32 [8, 2459520], P('mp', 'dp')
- master_new: float32 [8, 2459520], P('mp', 'dp')
- first_moment: float32 [8, 2459520], P('mp', 'dp')
- second_moment: float32 [8, 2459520], P('mp', 'dp')
- weights_new: bfloat16 [8, 2459520], P('mp')
- norm_grads: float32 [7680], P('mp')
The draws below stay inside these ranges and needn't reach their ends.
Inputs may be any that keep to these rules, and one draw needn't show every extreme that they name: `lengths`: valid frames of each clip; they sum to 10752 and the longest is exactly 1024. `key_mask`: the first frame of every clip is 1. `adam_step`: the AdamW step count. `hyper_rates`: learning rate, weight decay and logit cap, in this order.
All inputs are finite; a program needn't handle non-finite values. No bound on the sum of `lengths` on one device may be relied on, other than what follows from the above.
Results may differ from the reference program's by a relative error of at most 0.018.
Values may be sent and summed in bfloat16 or wider, within the bound.
A program may use at most 192 MiB of HBM per device.

```python
import math
import jax
import jax.numpy as jnp
import numpy as np
from jax import lax

D = 1280
HEADS = 16
HD = 80
FF = 5120
LEN = 1024
CLIPS = 12
TOTAL_LEN = 10752
PACK = 2459520
N_MP = 8


def draw_key_mask(key, part):
    picks = jax.random.randint(key, (CLIPS, LEN), 0, 10)
    keep = jnp.where(picks < 9, 1, 0).astype(jnp.int32)
    return keep.at[:, 0].set(1)


def draw_hyper_rates(key, part):
    learn_key, decay_key, limit_key = jax.random.split(key, 3)
    learn = jnp.exp(jax.random.uniform(learn_key, (), jnp.float32, math.log(0.03), math.log(0.3)))
    decay = jax.random.uniform(decay_key, (), jnp.float32, 0.01, 0.1)
    limit = jax.random.uniform(limit_key, (), jnp.float32, 3.0, 5.0)
    return jnp.stack([learn, decay, limit]).astype(jnp.float32)


def steps_of(own_key, dims, shards, least, high):
    factor_of, own = 1.0, jax.random.fold_in(own_key, 6)
    for dim, parts in shards:
        heights = jnp.exp(jax.random.uniform(jax.random.fold_in(own, dim), (parts,), jnp.float32, least / len(shards), high / len(shards)))
        factor_of = factor_of * jnp.repeat(heights, dims[dim] // parts).reshape([-1 if axis == dim else 1 for axis in range(len(dims))])
    return factor_of


def length_profile(count, total, most, lean):
    portions = [(1 << 20) // math.isqrt(standing ** lean) + 1 for standing in range(2, count + 1)]
    rest, given = total - most - (count - 1), [1] * (count - 1)
    while rest > 0:
        movable = [i for i in range(count - 1) if given[i] < most]
        mass, left = sum([portions[i] for i in movable]), rest
        for i in movable:
            more = min(most - given[i], max(1, left * portions[i] // mass), rest)
            given[i] = given[i] + more
            rest = rest - more
    return np.array([most] + given)


def ragged(rng, count, total, bound, lean):
    if count == 2:
        one = jax.random.randint(rng, (), max(1, total - bound), min(bound, total - 1) + 1)
        return jnp.stack([one, total - one])
    sizes = jnp.asarray(length_profile(count, total, bound, lean), jnp.int32)
    couples = (count - 1) // 2
    giver, receiver = sizes[1:1 + 2 * couples:2], sizes[2:2 + 2 * couples:2]
    room = jnp.minimum(giver - 1, bound - receiver)
    passed = jax.random.randint(jax.random.fold_in(rng, 1), (couples,), 0, 1 << 20) % (room + 1)
    sizes = sizes.at[1:1 + 2 * couples:2].set(giver - passed).at[2:2 + 2 * couples:2].set(receiver + passed)
    return sizes[jax.random.permutation(jax.random.fold_in(rng, 2), count)]


def centred(rng, dims, scale, most, shards=(), dtype=jnp.bfloat16):
    level = steps_of(rng, dims, shards, -0.22, 0.18) if shards else 1.0
    array = jax.random.normal(rng, dims, jnp.float32) * scale * level
    return jnp.minimum(jnp.maximum(array, -most), most).astype(dtype)


def setup_inputs(seed: int = 0) -> dict:
    key_of = jax.random.split(jax.random.key(seed), 25)
    frames = centred(key_of[0], (LEN, CLIPS, D), 1.0, 6.0, ((0, 8), (1, 4)))
    lengths = ragged(key_of[1], CLIPS, TOTAL_LEN, LEN, 2).astype(jnp.int32)
    key_mask = draw_key_mask(jax.random.fold_in(key_of[24], 71), 0)
    cotangent = centred(key_of[3], (LEN, CLIPS, D), 1.0, 6.0, ((0, 8), (1, 4)))
    gain_one = jnp.clip(1.0 + 0.1 * jax.random.normal(key_of[4], (D,), jnp.float32), 0.5, 1.5).astype(jnp.bfloat16)
    shift_one = centred(key_of[5], (D,), 0.3, 1.5)
    query_weight = centred(key_of[6], (D, D), (D // 2) ** -0.5, 0.25, ((1, 8),))
    query_bias = centred(key_of[7], (D,), 0.5, 2.5, ((0, 8),))
    key_weight = centred(key_of[8], (D, D), (D // 2) ** -0.5, 0.25, ((1, 8),))
    value_weight = centred(key_of[9], (D, D), D ** -0.5, 0.15625, ((1, 8),))
    value_bias = centred(key_of[10], (D,), 0.5, 2.5, ((0, 8),))
    out_weight = centred(key_of[11], (D, D), (D // 16) ** -0.5, 0.625, ((0, 8),))
    out_bias = centred(key_of[12], (D,), 0.3, 1.5)
    gain_two = jnp.clip(1.0 + 0.1 * jax.random.normal(key_of[13], (D,), jnp.float32), 0.5, 1.5).astype(jnp.bfloat16)
    shift_two = centred(key_of[14], (D,), 0.3, 1.5)
    up_weight = centred(key_of[15], (D, FF), D ** -0.5, 0.15625, ((1, 8),))
    up_bias = centred(key_of[16], (FF,), 0.5, 2.5, ((0, 8),))
    down_weight = centred(key_of[17], (FF, D), (FF // 2) ** -0.5, 0.125, ((0, 8),))
    down_bias = centred(key_of[18], (D,), 0.3, 1.5)
    master = centred(key_of[19], (N_MP, PACK), 0.03, 0.15, ((0, 8), (1, 4)), jnp.float32)
    moment_one = centred(key_of[20], (N_MP, PACK), 10.0, 60.0, ((0, 8), (1, 4)), jnp.float32)
    moment_two = jnp.clip(jnp.exp(math.log(100.0) - 4.6051702 * jax.random.uniform(key_of[21], (N_MP, PACK), jnp.float32) ** steps_of(key_of[21], (N_MP, PACK), ((0, 8), (1, 4)), -0.2, 0.2)), 1.0, 100.0)
    adam_step = jax.random.randint(key_of[22], (1,), 1, 1000).astype(jnp.int32)
    hyper_rates = draw_hyper_rates(jax.random.fold_in(key_of[24], 71), 0)
    return {"frames": frames, "lengths": lengths, "key_mask": key_mask, "cotangent": cotangent, "gain_one": gain_one, "shift_one": shift_one, "query_weight": query_weight, "query_bias": query_bias, "key_weight": key_weight, "value_weight": value_weight, "value_bias": value_bias, "out_weight": out_weight, "out_bias": out_bias, "gain_two": gain_two, "shift_two": shift_two, "up_weight": up_weight, "up_bias": up_bias, "down_weight": down_weight, "down_bias": down_bias, "master": master, "moment_one": moment_one, "moment_two": moment_two, "adam_step": adam_step, "hyper_rates": hyper_rates}


NORM_EPSILON = 1e-05
ADAM_EPSILON = 1e-08
BETA_FIRST = 0.9
BETA_SECOND = 0.999
MASK_VALUE = -1e+30

@jax.custom_vjp
def low(v):
    return lax.optimization_barrier(v.astype(jnp.bfloat16)).astype(jnp.float32)

@jax.custom_vjp
def low_back(v):
    return v

def low_keep(v):
    return (low(v), None)

def low_pass(kept, grad):
    return (grad,)

def back_keep(v):
    return (v, None)

def back_low(kept, grad):
    return (low(grad),)
low.defvjp(low_keep, low_pass)
low_back.defvjp(back_keep, back_low)

def product(left, right):
    return jnp.dot(left, right, precision=lax.Precision.HIGHEST, preferred_element_type=jnp.float32)

def layer_norm(value, gain, shift):
    center = value - lax.optimization_barrier(jnp.mean(value, axis=-1, keepdims=True))
    spread = lax.optimization_barrier(jnp.mean(center * center, axis=-1, keepdims=True))
    return center * lax.rsqrt(spread + NORM_EPSILON) * gain + shift

def clip_pass(params, clip_rows, keep_key, keep_query):
    gain_one, shift_one, query_weight, query_bias, key_weight, value_weight, value_bias, out_weight, out_bias, gain_two, shift_two, up_weight, up_bias, down_weight, down_bias = params
    score_scale = 1.0 / math.sqrt(HD)
    normed = low(layer_norm(clip_rows, gain_one, shift_one))
    query = low_back(low(product(normed, query_weight) + query_bias)).reshape(LEN, HEADS, HD)
    keys = low_back(low(product(normed, key_weight))).reshape(LEN, HEADS, HD)
    values = low_back(low(product(normed, value_weight) + value_bias)).reshape(LEN, HEADS, HD)
    scores = low_back(jnp.einsum('qhd,khd->hqk', query, keys, precision=lax.Precision.HIGHEST) * score_scale)
    masked = jnp.where(keep_key[None, None, :], scores, MASK_VALUE)
    row_peaks = lax.optimization_barrier(jnp.max(masked, axis=-1))
    head_peak = lax.optimization_barrier(jnp.max(jnp.where(keep_query[None, :], row_peaks, MASK_VALUE), axis=-1))
    probability = low(jax.nn.softmax(masked, axis=-1))
    attended = jnp.einsum('hqk,khd->qhd', probability, values, precision=lax.Precision.HIGHEST).reshape(LEN, D)
    attended = low_back(low(attended))
    branch = low_back(product(attended, out_weight) + out_bias)
    middle = clip_rows + branch
    normed_two = low(layer_norm(middle, gain_two, shift_two))
    before = low_back(product(normed_two, up_weight) + up_bias)
    hidden = low(jax.nn.gelu(before, approximate=False))
    feed = low_back(product(hidden, down_weight) + down_bias)
    return (middle + feed, head_peak)

def pack_rows(query_part, query_bias_part, key_part, value_part, value_bias_part, out_part, up_part, up_bias_part, down_part, small_part):
    head_cols = D // N_MP
    unit_cols = FF // N_MP

    def by_cols(matrix, cols):
        return matrix.reshape(matrix.shape[0], N_MP, cols).transpose(1, 0, 2).reshape(N_MP, -1)

    def by_rows(matrix):
        return matrix.reshape(N_MP, -1)
    return jnp.concatenate([by_cols(query_part, head_cols), by_rows(query_bias_part), by_cols(key_part, head_cols), by_cols(value_part, head_cols), by_rows(value_bias_part), by_rows(out_part), by_cols(up_part, unit_cols), by_rows(up_bias_part), by_rows(down_part), by_rows(small_part)], axis=1)

def reference(frames, lengths, key_mask, cotangent, gain_one, shift_one, query_weight, query_bias, key_weight, value_weight, value_bias, out_weight, out_bias, gain_two, shift_two, up_weight, up_bias, down_weight, down_bias, master, moment_one, moment_two, adam_step, hyper_rates):
    position = jnp.arange(LEN).astype(jnp.int32)
    keep_query = position[None, :] < lengths[:, None]
    keep_key = jnp.logical_and(keep_query, key_mask == 1)
    params = tuple((item.astype(jnp.float32) for item in (gain_one, shift_one, query_weight, query_bias, key_weight, value_weight, value_bias, out_weight, out_bias, gain_two, shift_two, up_weight, up_bias, down_weight, down_bias)))
    clip_first = frames.astype(jnp.float32).transpose(1, 0, 2)

    def whole(weights, clip_inputs):

        def one_clip(clip_item):
            return jax.checkpoint(clip_pass)(weights, clip_item[0], clip_item[1], clip_item[2])
        return lax.map(one_clip, (clip_inputs, keep_key, keep_query))
    outputs, pullback, peaks = jax.vjp(whole, params, clip_first, has_aux=True)
    param_grads, clip_grads = pullback(cotangent.astype(jnp.float32).transpose(1, 0, 2))
    layer_out = outputs.transpose(1, 0, 2).astype(jnp.bfloat16)
    input_grad = clip_grads.transpose(1, 0, 2)
    g_gain_one, g_shift_one, g_query, g_query_bias, g_key, g_value, g_value_bias, g_out, g_out_bias, g_gain_two, g_shift_two, g_up, g_up_bias, g_down, g_down_bias = param_grads
    small_terms = jnp.concatenate([g_gain_one, g_shift_one, g_out_bias, g_gain_two, g_shift_two, g_down_bias])
    weight_grads = pack_rows(g_query, g_query_bias, g_key, g_value, g_value_bias, g_out, g_up, g_up_bias, g_down, small_terms)
    head_peak = lax.optimization_barrier(jnp.max(peaks, axis=0))
    learn_rate = hyper_rates[0]
    weight_decay = hyper_rates[1]
    logit_cap = hyper_rates[2]
    head_root = jnp.sqrt(logit_cap / jnp.maximum(head_peak, logit_cap))
    column_root = jnp.repeat(head_root, HD)
    full_query = jnp.broadcast_to(column_root[None, :], (D, D))
    factor = pack_rows(full_query, column_root, full_query, jnp.ones((D, D), jnp.float32), jnp.ones((D,), jnp.float32), jnp.ones((D, D), jnp.float32), jnp.ones((D, FF), jnp.float32), jnp.ones((FF,), jnp.float32), jnp.ones((FF, D), jnp.float32), jnp.ones((6 * D,), jnp.float32))
    step_count = adam_step[0].astype(jnp.float32)
    first_moment = BETA_FIRST * moment_one + (1.0 - BETA_FIRST) * weight_grads
    second_moment = BETA_SECOND * moment_two + (1.0 - BETA_SECOND) * weight_grads * weight_grads
    first_hat = first_moment / (1.0 - jnp.power(BETA_FIRST, step_count))
    second_hat = second_moment / (1.0 - jnp.power(BETA_SECOND, step_count))
    master_new = (master - learn_rate * (first_hat / (jnp.sqrt(second_hat) + ADAM_EPSILON) + weight_decay * master)) * factor
    return (layer_out, input_grad, weight_grads, master_new, first_moment, second_moment, master_new.astype(jnp.bfloat16), small_terms)
```

```python
import functools
import math

import jax
import jax.numpy as jnp
from jax import lax
from jax.experimental import pallas as pl
from jax.experimental.pallas import tpu as pltpu
from jax.sharding import PartitionSpec as P

HD = 80


NORM_EPSILON = 1e-05
ADAM_EPSILON = 1e-08
BETA_FIRST = 0.9
BETA_SECOND = 0.999
MASK_VALUE = -1e30


def layer_norm(value, gain, shift):
    center = value - jnp.mean(value, axis=-1, keepdims=True)
    spread = jnp.mean(center * center, axis=-1, keepdims=True)
    return center * lax.rsqrt(spread + NORM_EPSILON) * gain + shift


def exact_gelu(argument):
    return jax.nn.gelu(argument, approximate=False)


MESH = pl.DeviceIdType.MESH
ANY = pl.BlockSpec(memory_space=pl.ANY)
VMEM = pl.BlockSpec(memory_space=pltpu.VMEM)
LINE = 4
ROWS = 384
BF = jnp.bfloat16
F32 = jnp.float32


class Place:
    def __init__(self):
        self.dp = lax.axis_index("dp")
        self.mp = lax.axis_index("mp")
        self.z = self.mp // 2
        self.c = self.mp % 2
        self.pair = self.z * 2 + 1 - self.c
        self.dpx = self.dp + 1 - 2 * (self.dp % 2)
        self.dpy = (self.dp + 2) % 4
        self.dpd = 3 - self.dp

    def zorder(self, event):
        if event == 0:
            return self.z
        if event == 1:
            return self.z + 1 - 2 * (self.z % 2)
        if event == 2:
            return 2 - self.z // 2
        return 3 - 3 * (self.z // 2)


def greet(place, mp_all=False, line=False, plane=False, pair=True):
    barrier = pltpu.get_barrier_semaphore()
    count = 0

    def signal(dp, mp):
        pl.semaphore_signal(barrier, inc=1, device_id=(dp, mp), device_id_type=MESH)

    if mp_all:
        for hop in range(1, 8):
            signal(place.dp, (place.mp + hop) % 8)
        count += 7
    else:
        if pair:
            signal(place.dp, place.pair)
            count += 1
        if line:

            @pl.when(place.z > 0)
            def _():
                signal(place.dp, place.mp - 2)

            @pl.when(place.z < LINE - 1)
            def _():
                signal(place.dp, place.mp + 2)

    if plane:
        for other in (place.dpx, place.dpy, place.dpd):
            signal(other, place.mp)
        count += 3
    if line and not mp_all:
        pl.semaphore_wait(barrier, count + 1 + (place.z + 1) // 2 % 2)
    else:
        pl.semaphore_wait(barrier, count)


def remote(src, dst, send, recv, dp, mp):
    return pltpu.make_async_remote_copy(
        src_ref=src,
        dst_ref=dst,
        send_sem=send,
        recv_sem=recv,
        device_id=(dp, mp),
        device_id_type=MESH,
    )


def line_gather(place, src, out, local, send, recv, paired, ready=None):
    dp, z, c, mp, pair = place.dp, place.z, place.c, place.mp, place.pair

    def slot_of(level, core):
        return level * 2 + core if paired else level

    def hop(event, slot, source, direction, target):
        return remote(source, out.at[slot], send.at[event, direction], recv.at[slot], dp, target)

    own = slot_of(z, c)
    keep = pltpu.make_async_copy(src, out.at[own], local)
    keep.start()

    def ways(event, level, slot, source, act):
        up = z < LINE - 1
        down = z > 0
        if event > 0:
            up = jnp.logical_and(up, level < z)
            down = jnp.logical_and(down, level > z)

        @pl.when(up)
        def _():
            act(hop(event, slot, source, 1, mp + 2))

        @pl.when(down)
        def _():
            act(hop(event, slot, source, 2, mp - 2))

        if paired:
            act(hop(event, slot, source, 0, pair))

    ways(0, z, own, src, lambda copy: copy.start())
    yield
    if ready is not None:
        keep.wait()
        ready(own)
        if paired:
            other = slot_of(z, 1 - c)
            hop(0, other, out.at[other], 0, pair).wait_recv()
            ready(other)
    for event in range(1, LINE):
        level = place.zorder(event)
        slot = slot_of(level, c)
        hop(event, slot, out.at[slot], 0, pair).wait_recv()
        ways(event, level, slot, out.at[slot], lambda copy: copy.start())
        if ready is not None:
            ready(slot)
            if paired:
                other = slot_of(level, 1 - c)
                hop(event, other, out.at[other], 0, pair).wait_recv()
                ready(other)
        yield
    if ready is None:
        if paired:
            for level in range(LINE):
                other = slot_of(level, 1 - c)
                hop(0, other, out.at[other], 0, pair).wait_recv()
        keep.wait()
    for event in range(LINE):
        level = place.zorder(event)
        slot = slot_of(level, c)
        ways(event, level, slot, out.at[slot], lambda copy: copy.wait_send())
    yield


def plane_gather(place, src, out, local, send, recv):
    dp, c, mp, pair = place.dp, place.c, place.mp, place.pair
    dpx, dpy, dpd = place.dpx, place.dpy, place.dpd
    half = src.shape[0] // 2
    part_a, part_b = pl.ds(0, half), pl.ds(half, half)

    def at(group, core):
        return out.at[group * 2 + core]

    keep = pltpu.make_async_copy(src, at(dp, c), local)
    keep.start()
    here = at(dp, c)
    sends = [
        remote(src, here, send.at[0], recv.at[0], dp, pair),
        remote(src, here, send.at[1], recv.at[1], dpx, mp),
        remote(src, here, send.at[2], recv.at[2], dpy, mp),
    ]
    for copy in sends:
        copy.start()
    yield
    from_x, from_y = at(dpx, c), at(dpy, c)
    remote(from_x, from_x, send.at[1], recv.at[1], dpx, mp).wait_recv()
    sends.append(
        remote(from_x.at[part_a], from_x.at[part_a], send.at[3], recv.at[3], dpy, mp)
    )
    sends[-1].start()
    remote(from_y, from_y, send.at[2], recv.at[2], dpy, mp).wait_recv()
    sends.append(
        remote(from_y.at[part_b], from_y.at[part_b], send.at[4], recv.at[4], dpx, mp)
    )
    sends[-1].start()
    for index, block in ((5, from_x), (6, from_y)):
        sends.append(remote(block, block, send.at[index], recv.at[index], dp, pair))
        sends[-1].start()
    yield
    from_d = at(dpd, c)
    remote(from_d.at[part_a], from_d.at[part_a], send.at[3], recv.at[3], dpy, mp).wait_recv()
    sends.append(
        remote(from_d.at[part_a], from_d.at[part_a], send.at[7], recv.at[7], dp, pair)
    )
    sends[-1].start()
    remote(from_d.at[part_b], from_d.at[part_b], send.at[4], recv.at[4], dpx, mp).wait_recv()
    sends.append(
        remote(from_d.at[part_b], from_d.at[part_b], send.at[8], recv.at[8], dp, pair)
    )
    sends[-1].start()
    yield
    for index, group in ((0, dp), (5, dpx), (6, dpy)):
        block = at(group, 1 - c)
        remote(block, block, send.at[index], recv.at[index], dp, pair).wait_recv()
    other = at(dpd, 1 - c)
    for index, rows in ((7, part_a), (8, part_b)):
        remote(other.at[rows], other.at[rows], send.at[index], recv.at[index], dp, pair).wait_recv()
    for copy in sends:
        copy.wait_send()
    keep.wait()
    yield


def drive(*programs):
    live = list(programs)
    while live:
        for program in list(live):
            try:
                next(program)
            except StopIteration:
                live.remove(program)


def dma(*shape):
    return pltpu.SemaphoreType.DMA(shape)


def params(cid, vmem=40):
    return pltpu.CompilerParams(
        collective_id=cid, has_side_effects=True, vmem_limit_bytes=vmem << 20
    )


def exchange(place, src, out, local, send, recv):
    dp, mp = place.dp, place.mp
    keep = pltpu.make_async_copy(src.at[mp], out.at[mp], local)
    keep.start()
    sends = []
    for hop in range(1, 8):
        target = (mp + hop) % 8
        sends.append(
            remote(src.at[target], out.at[mp], send.at[hop], recv.at[hop], dp, target)
        )
        sends[-1].start()
    yield
    keep.wait()
    for hop in range(1, 8):
        origin = (mp + 8 - hop) % 8
        remote(out.at[origin], out.at[origin], send.at[hop], recv.at[hop], dp, origin).wait_recv()
    for copy in sends:
        copy.wait_send()
    yield


def line_reduce(place, produce, tiles, result, bufs, sems, paired):
    dp, z, c, mp, pair = place.dp, place.z, place.c, place.mp, place.pair
    from_above, from_below, out_block = bufs["above"], bufs["below"], bufs["out"]
    order = [place.zorder(event) for event in (3, 2, 1, 0)]

    @pl.when(z == LINE - 1)
    def _():
        from_above[...] = jnp.zeros(from_above.shape, BF)

    @pl.when(z == 0)
    def _():
        from_below[...] = jnp.zeros(from_below.shape, BF)

    def across(step, level):
        return remote(
            bufs["pair_out"].at[step],
            bufs["pair_in"].at[level],
            sems["pair_send"].at[step],
            sems["pair_recv"].at[level],
            dp,
            pair,
        )

    if paired:
        for step, level in enumerate(order):
            for rows in tiles:
                bufs["pair_out"][step, rows] = produce(level, 1 - c, rows).astype(BF)
            across(step, level).start()
    yield

    def toward(step, level, act):
        @pl.when(level < z)
        def _():
            act(
                remote(
                    out_block.at[step],
                    from_above.at[level],
                    sems["line_send"].at[step],
                    sems["above"].at[level],
                    dp,
                    mp - 2,
                )
            )

        @pl.when(level > z)
        def _():
            act(
                remote(
                    out_block.at[step],
                    from_below.at[level],
                    sems["line_send"].at[step],
                    sems["below"].at[level],
                    dp,
                    mp + 2,
                )
            )

    def arrive(level, above):
        if above:
            remote(
                from_above.at[level],
                from_above.at[level],
                sems["line_send"].at[0],
                sems["above"].at[level],
                dp,
                mp,
            ).wait_recv()
        else:
            remote(
                from_below.at[level],
                from_below.at[level],
                sems["line_send"].at[0],
                sems["below"].at[level],
                dp,
                mp,
            ).wait_recv()

    for step, level in enumerate(order[:3]):
        if paired:
            across(step, level).wait_recv()

        @pl.when(jnp.logical_and(level < z, z < LINE - 1))
        def _():
            arrive(level, True)

        @pl.when(jnp.logical_and(level > z, z > 0))
        def _():
            arrive(level, False)

        for rows in tiles:
            total = produce(level, c, rows)
            if paired:
                total = total + bufs["pair_in"][level, rows].astype(F32)

            @pl.when(level < z)
            def _():
                out_block[step, rows] = (total + from_above[level, rows].astype(F32)).astype(BF)

            @pl.when(level > z)
            def _():
                out_block[step, rows] = (total + from_below[level, rows].astype(F32)).astype(BF)

        toward(step, level, lambda copy: copy.start())
        yield

    if paired:
        across(3, z).wait_recv()

    @pl.when(z < LINE - 1)
    def _():
        arrive(z, True)

    @pl.when(z > 0)
    def _():
        arrive(z, False)

    for rows in tiles:
        total = produce(z, c, rows)
        if paired:
            total = total + bufs["pair_in"][z, rows].astype(F32)
        total = total + from_above[z, rows].astype(F32) + from_below[z, rows].astype(F32)
        result(rows, total)
    for step, level in enumerate(order):
        if paired:
            across(step, level).wait_send()
        if step < 3:
            toward(step, level, lambda copy: copy.wait_send())
    yield


def line_reduce_scratch(rows, cols, paired):
    block = lambda n: pltpu.VMEM((n, rows, cols), BF)
    scratch = {"above": block(4), "below": block(4), "out": block(3)}
    sems = {"line_send": dma(3), "above": dma(4), "below": dma(4)}
    if paired:
        scratch.update({"pair_out": block(4), "pair_in": block(4)})
        sems.update({"pair_send": dma(4), "pair_recv": dma(4)})
    return scratch, sems


def plane_reduce(place, produce, tile, half, result, bufs, sems, paired=True):
    dp, c, mp, pair = place.dp, place.c, place.mp, place.pair
    dpx, dpy, dpd = place.dpx, place.dpy, place.dpd
    order = [dpd, dpx, dpy, dp]
    tiles_a = [pl.ds(start, tile) for start in range(0, half, tile)]
    send, recv = sems["send"], sems["recv"]
    out_block, landed = bufs["out"], bufs["in"]

    def across(step):
        return remote(
            bufs["pair_out"].at[step],
            bufs["pair_in"].at[step],
            sems["pair_send"].at[step],
            sems["pair_recv"].at[step],
            dp,
            pair,
        )

    if paired:
        for step, group in enumerate(order):
            for start in range(0, 2 * half, tile):
                bufs["pair_out"][step, pl.ds(start, tile)] = produce(
                    group, 1 - c, start
                ).astype(BF)
            across(step).start()
    yield

    def share(step, start):
        total = produce(order[step], c, start)
        if paired:
            total = total + bufs["pair_in"][step, pl.ds(start, tile)].astype(F32)
        return total

    def hop(index, target):
        return remote(
            out_block.at[index], landed.at[index], send.at[index], recv.at[index], target, mp
        )

    def fill(index, step, base, extra=None):
        for rows in tiles_a:
            total = share(step, base + rows.start)
            if extra is not None:
                total = total + landed[extra, rows].astype(F32)
            out_block[index, rows] = total.astype(BF)

    targets = [dpx, dpy, dpx, dpx, dpy, dpy]
    if paired:
        across(0).wait_recv()
    fill(0, 0, 0)
    hop(0, dpx).start()
    fill(1, 0, half)
    hop(1, dpy).start()
    yield
    if paired:
        across(1).wait_recv()
        across(2).wait_recv()
    fill(2, 1, 0)
    hop(2, dpx).start()
    fill(4, 2, half)
    hop(4, dpy).start()
    yield
    hop(1, dpy).wait_recv()
    fill(3, 1, half, extra=1)
    hop(3, dpx).start()
    hop(0, dpx).wait_recv()
    fill(5, 2, 0, extra=0)
    hop(5, dpy).start()
    yield
    if paired:
        across(3).wait_recv()
    for index in (2, 3, 4, 5):
        hop(index, targets[index]).wait_recv()
    for base, pieces in ((0, (2, 5)), (half, (3, 4))):
        for rows in tiles_a:
            total = share(3, base + rows.start)
            for piece in pieces:
                total = total + landed[piece, rows].astype(F32)
            result(pl.ds(base + rows.start, tile), total)
    for index in range(6):
        hop(index, targets[index]).wait_send()
    if paired:
        for step in range(4):
            across(step).wait_send()
    yield


def plane_reduce_scratch(half, cols, paired=True):
    block = lambda n, rows: pltpu.VMEM((n, rows, cols), BF)
    scratch = {"out": block(6, half), "in": block(6, half)}
    sems = {"send": dma(6), "recv": dma(6)}
    if paired:
        scratch.update({"pair_out": block(4, 2 * half), "pair_in": block(4, 2 * half)})
        sems.update({"pair_send": dma(4), "pair_recv": dma(4)})
    return scratch, sems


def project_kernel(
    normed_ref, cot_ref, weight_ref, bias_ref, nfull_ref, qkv_ref, cfull_ref,
    local, line_send, line_recv, plane_send, plane_recv,
):
    place = Place()
    greet(place, line=True, plane=True)

    def ready(slot):
        @pl.loop(0, 3)
        def _(step):
            rows = pl.ds(step * 128, 128)
            product = lax.dot_general(
                nfull_ref[slot, rows],
                weight_ref[...],
                (((1,), (1,)), ((), ())),
                preferred_element_type=F32,
            )
            qkv_ref[slot, rows] = (product + bias_ref[...]).astype(BF)

    drive(
        line_gather(
            place, normed_ref, nfull_ref, local.at[0], line_send, line_recv, True, ready
        ),
        plane_gather(place, cot_ref, cfull_ref, local.at[1], plane_send, plane_recv),
    )


def project(normed, cotangent, weight, bias):
    return pl.pallas_call(
        project_kernel,
        out_shape=(
            jax.ShapeDtypeStruct((8,) + normed.shape, BF),
            jax.ShapeDtypeStruct((8, ROWS, weight.shape[0]), BF),
            jax.ShapeDtypeStruct((8,) + cotangent.shape, BF),
        ),
        in_specs=[ANY, ANY, VMEM, VMEM],
        out_specs=(VMEM, VMEM, ANY),
        scratch_shapes=[dma(2), dma(4, 3), dma(8), dma(9), dma(9)],
        compiler_params=params(0),
        name="project",
    )(normed, cotangent, weight, bias)


def attend_kernel(
    qkv_ref, mask_ref, live_ref, weights_ref, att_ref, logs_ref, peak_ref, wfull_ref,
    out_ref, vt_ref, local, send, recv, line_send, line_recv,
):
    place = Place()
    greet(place, mp_all=True)
    gather = line_gather(
        place, weights_ref, wfull_ref, local.at[1], line_send, line_recv, True
    )
    next(gather)
    factor = math.log2(math.e) / math.sqrt(HD)
    peak_ref[...] = jnp.full(peak_ref.shape, MASK_VALUE, F32)

    @pl.loop(0, 6)
    def _(turn):
        clip = turn // 2
        head = turn % 2
        lane = pl.multiple_of(head * 128, 128)
        row = pl.multiple_of(head * HD, 16)
        keys = qkv_ref[:, clip, :, pl.ds(256 + lane, 128)].reshape(1024, 128)
        vt_ref[...] = qkv_ref[:, clip, :, pl.ds(512 + lane, 128)].reshape(1024, 128).T

        @pl.loop(0, 4)
        def _(block):
            query = qkv_ref[pl.ds(block * 2, 2), clip, :, pl.ds(lane, 128)].reshape(256, 128)
            columns = pl.ds(pl.multiple_of(block * 256, 256), 256)
            scores = lax.dot_general(
                keys, query, (((1,), (1,)), ((), ())), preferred_element_type=F32
            )
            scores = scores + mask_ref[clip]
            peak = jnp.max(scores, axis=0, keepdims=True)
            powers = jnp.exp2((scores - peak) * factor)
            total = jnp.sum(powers, axis=0, keepdims=True)
            mixed = lax.dot_general(
                vt_ref[...],
                powers.astype(BF),
                (((1,), (0,)), ((), ())),
                preferred_element_type=F32,
            )
            mixed = (mixed / total).astype(BF)
            for part in range(2):
                out_ref[block * 2 + part, clip, pl.ds(row, HD)] = mixed[
                    :HD, part * 128 : part * 128 + 128
                ]
            logs_ref[turn, :, columns] = peak * factor + jnp.log2(total)
            peak_ref[head] = jnp.maximum(
                peak_ref[head], jnp.where(live_ref[clip, :, columns] > 0, peak, MASK_VALUE)
            )

    drive(exchange(place, out_ref, att_ref, local.at[0], send, recv), gather)


def attend(qkv, mask, live, weights):
    return pl.pallas_call(
        attend_kernel,
        out_shape=(
            jax.ShapeDtypeStruct((8, 3, 160, 128), BF),
            jax.ShapeDtypeStruct((6, 1, 1024), F32),
            jax.ShapeDtypeStruct((2, 1, 256), F32),
            jax.ShapeDtypeStruct((8,) + weights.shape, BF),
        ),
        in_specs=[VMEM, VMEM, VMEM, ANY],
        out_specs=(VMEM, VMEM, VMEM, ANY),
        scratch_shapes=[
            pltpu.VMEM((8, 3, 160, 128), BF),
            pltpu.VMEM((128, 1024), BF),
            dma(2),
            dma(8),
            dma(8),
            dma(4, 3),
            dma(8),
        ],
        compiler_params=params(1),
        name="attend",
    )(qkv, mask, live, weights)


def attend_back_kernel(
    qkv_ref, mask_ref, logs_ref, grads_ref, dqkv_ref,
    grad_ref, kt_ref, dk_ref, dv_ref, block_ref, local, send, recv,
):
    place = Place()
    greet(place, mp_all=True)
    drive(exchange(place, grads_ref, grad_ref, local, send, recv))
    scale = 1.0 / math.sqrt(HD)
    factor = math.log2(math.e) * scale
    block_ref[...] = jnp.zeros(block_ref.shape, BF)

    @pl.loop(0, 6)
    def _(turn):
        clip = turn // 2
        head = turn % 2
        lane = pl.multiple_of(head * 128, 128)
        row = pl.multiple_of(head * HD, 16)
        keys = qkv_ref[:, clip, :, pl.ds(256 + lane, 128)].reshape(1024, 128)
        kt_ref[...] = keys.T
        dk_ref[...] = jnp.zeros(dk_ref.shape, F32)
        dv_ref[...] = jnp.zeros(dv_ref.shape, F32)

        @pl.loop(0, 4)
        def _(block):
            query = qkv_ref[pl.ds(block * 2, 2), clip, :, pl.ds(lane, 128)].reshape(256, 128)
            values = qkv_ref[:, clip, :, pl.ds(512 + lane, 128)].reshape(1024, 128)
            keys = qkv_ref[:, clip, :, pl.ds(256 + lane, 128)].reshape(1024, 128)
            columns = pl.ds(pl.multiple_of(block * 256, 256), 256)
            for part in range(2):
                block_ref[:HD, part * 128 : part * 128 + 128] = grad_ref[
                    block * 2 + part, clip, pl.ds(row, HD)
                ]
            scores = lax.dot_general(
                keys, query, (((1,), (1,)), ((), ())), preferred_element_type=F32
            )
            chance = jnp.exp2((scores + mask_ref[clip]) * factor - logs_ref[turn, :, columns])
            dv_ref[...] += lax.dot_general(
                chance.astype(BF),
                block_ref[...],
                (((1,), (1,)), ((), ())),
                preferred_element_type=F32,
            )
            slope = lax.dot_general(
                values, block_ref[...], (((1,), (0,)), ((), ())), preferred_element_type=F32
            )
            center = jnp.sum(chance * slope, axis=0, keepdims=True)
            change = (chance * (slope - center)).astype(BF)
            dk_ref[...] += lax.dot_general(
                change, query, (((1,), (0,)), ((), ())), preferred_element_type=F32
            )
            dq = lax.dot_general(
                kt_ref[...], change, (((1,), (0,)), ((), ())), preferred_element_type=F32
            )
            dqkv_ref[pl.ds(block * 2, 2), clip, :, pl.ds(lane, 128)] = (
                (dq.T * scale).astype(BF).reshape(2, 128, 128)
            )

        dqkv_ref[:, clip, :, pl.ds(256 + lane, 128)] = (
            (dk_ref[...] * scale).astype(BF).reshape(8, 128, 128)
        )
        dqkv_ref[:, clip, :, pl.ds(512 + lane, 128)] = (
            dv_ref[...].astype(BF).reshape(8, 128, 128)
        )


def attend_back(qkv, mask, logs, grads):
    return pl.pallas_call(
        attend_back_kernel,
        out_shape=jax.ShapeDtypeStruct(qkv.shape, BF),
        in_specs=[VMEM, VMEM, VMEM, ANY],
        out_specs=VMEM,
        scratch_shapes=[
            pltpu.VMEM((8, 3, 160, 128), BF),
            pltpu.VMEM((128, 1024), BF),
            pltpu.VMEM((1024, 128), F32),
            pltpu.VMEM((1024, 128), F32),
            pltpu.VMEM((128, 256), BF),
            pltpu.SemaphoreType.DMA(()),
            dma(8),
            dma(8),
        ],
        compiler_params=params(2),
        name="attend_back",
    )(qkv, mask, logs, grads)


def plane_share_kernel(block_ref, full_ref, local, send, recv):
    place = Place()
    greet(place, plane=True)
    drive(plane_gather(place, block_ref, full_ref, local, send, recv))


def plane_share(block):
    return pl.pallas_call(
        plane_share_kernel,
        out_shape=jax.ShapeDtypeStruct((8,) + block.shape, BF),
        in_specs=[ANY],
        out_specs=ANY,
        scratch_shapes=[pltpu.SemaphoreType.DMA(()), dma(9), dma(9)],
        compiler_params=params(3),
        name="plane_share",
    )(block)


def flatten(*pairs):
    names, shapes = [], []
    for number, group in enumerate(pairs):
        for name, shape in group.items():
            names.append((number, name))
            shapes.append(shape)

    def split(refs):
        groups = [{} for _ in pairs]
        for (number, name), ref in zip(names, refs):
            groups[number][name] = ref
        return groups

    return shapes, split


def plane_sums_kernel(split, first_ref, second_ref, first_out, second_out, *scratch):
    place = Place()
    bufs_one, sems_one, bufs_two, sems_two = split(scratch)
    greet(place, plane=True)

    def reader(ref):
        return lambda group, core, start: ref[group * 2 + core, pl.ds(start, 96)].astype(F32)

    def writer(ref):
        def write(rows, total):
            ref[rows] = total

        return write

    drive(
        plane_reduce(place, reader(first_ref), 96, 192, writer(first_out), bufs_one, sems_one),
        plane_reduce(place, reader(second_ref), 96, 192, writer(second_out), bufs_two, sems_two),
    )


def plane_sums(first, second):
    shapes, split = flatten(*plane_reduce_scratch(192, 1280), *plane_reduce_scratch(192, 1280))
    out = jax.ShapeDtypeStruct(first.shape[1:], F32)
    return pl.pallas_call(
        functools.partial(plane_sums_kernel, split),
        out_shape=(out, out),
        in_specs=[VMEM, VMEM],
        out_specs=(VMEM, VMEM),
        scratch_shapes=shapes,
        compiler_params=params(4, 60),
        name="plane_sums",
    )(first, second)


def line_product_kernel(split, grad_ref, weight_ref, out_ref, *scratch):
    place = Place()
    bufs, sems = split(scratch)
    greet(place, line=True)

    def produce(level, core, rows):
        return jnp.dot(
            grad_ref[level * 2 + core, rows], weight_ref[...], preferred_element_type=F32
        )

    def result(rows, total):
        out_ref[rows] = total

    tiles = [pl.ds(start, 128) for start in range(0, ROWS, 128)]
    drive(line_reduce(place, produce, tiles, result, bufs, sems, True))


def line_product(grads, weight):
    shapes, split = flatten(*line_reduce_scratch(ROWS, 1280, True))
    return pl.pallas_call(
        functools.partial(line_product_kernel, split),
        out_shape=jax.ShapeDtypeStruct((ROWS, 1280), F32),
        in_specs=[VMEM, VMEM],
        out_specs=VMEM,
        scratch_shapes=shapes,
        compiler_params=params(5, 60),
        name="line_product",
    )(grads, weight)


def line_sums_kernel(split, feed_ref, out_grad_ref, feed_out, out_out, *scratch):
    place = Place()
    bufs_one, sems_one, bufs_two, sems_two = split(scratch)
    greet(place, line=True)

    def write_feed(rows, total):
        feed_out[rows] = total

    def write_out(rows, total):
        out_out[rows] = total

    tiles = lambda rows, tile: [pl.ds(start, tile) for start in range(0, rows, tile)]
    drive(
        line_reduce(
            place,
            lambda level, core, rows: feed_ref[level, rows].astype(F32),
            tiles(feed_ref.shape[1], 112),
            write_feed,
            bufs_one,
            sems_one,
            False,
        ),
        line_reduce(
            place,
            lambda level, core, rows: out_grad_ref[level * 2 + core, rows].astype(F32),
            tiles(160, 80),
            write_out,
            bufs_two,
            sems_two,
            True,
        ),
    )


def line_sums(feed, out_grad):
    rows = feed.shape[1]
    shapes, split = flatten(
        *line_reduce_scratch(rows, 1280, False), *line_reduce_scratch(160, 1280, True)
    )
    return pl.pallas_call(
        functools.partial(line_sums_kernel, split),
        out_shape=(
            jax.ShapeDtypeStruct((rows, 1280), F32),
            jax.ShapeDtypeStruct((160, 1280), F32),
        ),
        in_specs=[VMEM, VMEM],
        out_specs=(VMEM, VMEM),
        scratch_shapes=shapes,
        compiler_params=params(6, 60),
        name="line_sums",
    )(feed, out_grad)


def fast_body(
    frames,
    lengths,
    key_mask,
    cotangent,
    gain_one,
    shift_one,
    query_weight,
    query_bias,
    key_weight,
    value_weight,
    value_bias,
    out_weight,
    out_bias,
    gain_two,
    shift_two,
    up_weight,
    up_bias,
    down_weight,
    down_bias,
    master,
    moment_one,
    moment_two,
    adam_step,
    hyper_rates,
):
    group = lax.axis_index("dp")
    position = jnp.arange(1024, dtype=jnp.int32)
    keep_query = position[None, :] < lengths[:, None]
    keep_key = jnp.logical_and(keep_query, key_mask == 1)
    mask = jnp.where(keep_key, 0.0, MASK_VALUE)[:, :, None]
    live = keep_query.astype(F32)[:, None, :]
    gain_first = gain_one.astype(F32)
    shift_first = shift_one.astype(F32)
    gain_second = gain_two.astype(F32)
    shift_second = shift_two.astype(F32)
    inputs = frames.transpose(1, 0, 2).reshape(ROWS, 1280).astype(F32)
    upstream_low = cotangent.transpose(1, 0, 2).reshape(ROWS, 1280)
    upstream = upstream_low.astype(F32)
    normed = layer_norm(inputs, gain_first, shift_first).astype(BF)

    def head_rows(weight):
        rows = weight.T.reshape(2, HD, 1280)
        return jnp.pad(rows, ((0, 0), (0, 128 - HD), (0, 0))).reshape(256, 1280)

    def head_lanes(bias):
        lanes = bias.astype(F32).reshape(2, HD)
        return jnp.pad(lanes, ((0, 0), (0, 128 - HD))).reshape(256)

    joined_weight = jnp.concatenate(
        [head_rows(query_weight), head_rows(key_weight), head_rows(value_weight)]
    )
    joined_bias = jnp.concatenate(
        [head_lanes(query_bias), jnp.zeros((256,), F32), head_lanes(value_bias)]
    )[None]
    normed_full, qkv, upstream_full = project(normed, upstream_low, joined_weight, joined_bias)
    qkv = qkv.reshape(8, 3, 128, 768)

    quarter = group * 160
    up_share = lax.dynamic_slice_in_dim(up_weight, quarter, 160, 1).T
    down_share = lax.dynamic_slice_in_dim(down_weight, quarter, 160, 0)
    bias_share = lax.dynamic_slice_in_dim(up_bias, quarter, 160, 0)
    bias_rows = jnp.pad(bias_share[None], ((0, 15), (0, 1280 - 160)))
    message = jnp.concatenate([up_share, down_share, bias_rows, out_weight])
    attended, logs, peaks, gathered = attend(qkv, mask, live, message)
    core = lax.axis_index("mp") % 2
    own_core = lax.dynamic_slice_in_dim(gathered.reshape(4, 2, 496, 1280), core, 1, 1)[:, 0]
    up_rows = own_core[:, :160].reshape(640, 1280)
    down_rows = own_core[:, 160:320].reshape(640, 1280)
    up_lanes = own_core[:, 320, :160].reshape(640).astype(F32)
    out_rows = gathered[:, 336:]
    head_peak = lax.pmax(jnp.max(peaks, axis=(1, 2)) / math.sqrt(HD), "dp")

    branch = jnp.einsum("schr,shd->crd", attended, out_rows, preferred_element_type=F32)
    middle = inputs + branch.reshape(ROWS, 1280) + out_bias.astype(F32)
    normed_two = layer_norm(middle, gain_second, shift_second).astype(BF)
    normed_two_full = plane_share(normed_two)
    before = (
        jnp.einsum("prd,ud->pru", normed_two_full, up_rows, preferred_element_type=F32)
        + up_lanes
    )
    hidden = exact_gelu(before).astype(BF)
    hidden_grad = jnp.einsum("prd,ud->pru", upstream_full, down_rows, preferred_element_type=F32)
    _, gelu_pull = jax.vjp(exact_gelu, before)
    before_grad = gelu_pull(hidden_grad)[0].astype(BF)
    feed_part = jnp.einsum("pru,ud->prd", hidden, down_rows, preferred_element_type=F32).astype(BF)
    normed_part = jnp.einsum(
        "pru,ud->prd", before_grad, up_rows, preferred_element_type=F32
    ).astype(BF)
    normed_two_grad, feed = plane_sums(normed_part, feed_part)
    layer_out = (middle + feed + down_bias.astype(F32)).astype(BF)
    up_grad = jnp.einsum("pru,prd->ud", before_grad, normed_two_full, preferred_element_type=F32)
    down_grad = jnp.einsum("pru,prd->ud", hidden, upstream_full, preferred_element_type=F32)
    up_bias_grad = jnp.sum(before_grad.astype(F32), axis=(0, 1))

    _, norm_two_pull = jax.vjp(layer_norm, middle, gain_second, shift_second)
    middle_norm_grad, gain_two_grad, shift_two_grad = norm_two_pull(normed_two_grad)
    middle_grad = upstream + middle_norm_grad
    branch_grad = middle_grad.astype(BF)
    branch_clips = branch_grad.reshape(3, 128, 1280)
    out_grad = jnp.einsum("schr,crd->shd", attended, branch_clips, preferred_element_type=F32)
    attended_grad = jnp.einsum(
        "shd,crd->schr", out_rows, branch_clips, preferred_element_type=F32
    ).astype(BF)
    joined_grad = attend_back(qkv, mask, logs, attended_grad).reshape(8, ROWS, 768)
    normed_grad = line_product(joined_grad, joined_weight)
    joined_weight_grad = jnp.einsum(
        "prd,pre->de", normed_full, joined_grad, preferred_element_type=F32
    )
    joined_bias_grad = jnp.sum(joined_grad.astype(F32), axis=(0, 1))

    _, norm_one_pull = jax.vjp(layer_norm, inputs, gain_first, shift_first)
    input_norm_grad, gain_one_grad, shift_one_grad = norm_one_pull(normed_grad)
    input_grad = middle_grad + input_norm_grad

    feed_grads = jnp.concatenate(
        [
            up_grad.astype(BF).reshape(4, 160, 1280),
            down_grad.astype(BF).reshape(4, 160, 1280),
            jnp.pad(up_bias_grad.astype(BF).reshape(4, 1, 160), ((0, 0), (0, 15), (0, 1120))),
        ],
        axis=1,
    )
    feed_sum, out_sum = line_sums(feed_grads, out_grad.astype(BF))

    def spread(rows):
        return lax.dynamic_update_slice(
            jnp.zeros((640,) + rows.shape[1:], F32), rows, (quarter,) + (0,) * (rows.ndim - 1)
        )

    up_whole = spread(feed_sum[:160]).T
    down_whole = spread(feed_sum[160:320])
    up_bias_whole = spread(feed_sum[320, :160])

    out_bias_grad = jnp.sum(branch_grad.astype(F32), axis=0)
    down_bias_grad = jnp.sum(upstream, axis=0)
    small_terms = jnp.concatenate(
        [
            gain_one_grad,
            shift_one_grad,
            out_bias_grad,
            gain_two_grad,
            shift_two_grad,
            down_bias_grad,
        ]
    )
    small_share = lax.psum_scatter(small_terms, "mp", scatter_dimension=0, tiled=True)
    small_total = lax.psum(small_share, "dp")

    def head_columns(first):
        return jnp.concatenate(
            [
                joined_weight_grad[:, first : first + HD],
                joined_weight_grad[:, first + 128 : first + 128 + HD],
            ],
            axis=1,
        ).reshape(-1)

    def head_entries(first):
        return jnp.concatenate(
            [joined_bias_grad[first : first + HD], joined_bias_grad[first + 128 : first + 128 + HD]]
        )

    packed = jnp.concatenate(
        [
            head_columns(0),
            head_entries(0),
            head_columns(256),
            head_columns(512),
            head_entries(512),
            out_sum.reshape(-1),
            up_whole.reshape(-1),
            up_bias_whole,
            down_whole.reshape(-1),
            small_share,
        ]
    )
    owned_grads = lax.psum_scatter(
        packed.astype(jnp.bfloat16), "dp", scatter_dimension=0, tiled=True
    ).astype(jnp.float32)
    share_size = owned_grads.shape[0]
    learn_rate = hyper_rates[0]
    weight_decay = hyper_rates[1]
    logit_cap = hyper_rates[2]
    step_count = adam_step[0].astype(jnp.float32)
    first_new = BETA_FIRST * moment_one[0] + (1.0 - BETA_FIRST) * owned_grads
    second_new = BETA_SECOND * moment_two[0] + (1.0 - BETA_SECOND) * owned_grads * owned_grads
    first_hat = first_new / (1.0 - jnp.power(BETA_FIRST, step_count))
    second_hat = second_new / (1.0 - jnp.power(BETA_SECOND, step_count))
    entry_index = lax.axis_index("dp") * share_size + jnp.arange(share_size, dtype=jnp.int32)
    query_end = 1280 * 160
    query_bias_end = query_end + 160
    key_end = query_bias_end + 1280 * 160
    column = jnp.where(
        entry_index < query_end,
        entry_index % 160,
        jnp.where(
            entry_index < query_bias_end,
            entry_index - query_end,
            (entry_index - query_bias_end) % 160,
        ),
    )
    head_index = column // HD
    root_factor = jnp.sqrt(logit_cap / jnp.maximum(head_peak, logit_cap))
    head_factor = jnp.zeros((share_size,), jnp.float32)
    for head_number in range(2):
        head_factor = head_factor + jnp.where(
            head_index == head_number, root_factor[head_number], 0.0
        )
    factor = jnp.where(entry_index < key_end, head_factor, 1.0)
    master_here = master[0]
    master_new = (
        master_here
        - learn_rate
        * (first_hat / (jnp.sqrt(second_hat) + ADAM_EPSILON) + weight_decay * master_here)
    ) * factor
    weights_full = lax.all_gather(master_new.astype(jnp.bfloat16), "dp", axis=0, tiled=True)
    return (
        layer_out.reshape(3, 128, 1280).transpose(1, 0, 2),
        input_grad.reshape(3, 128, 1280).transpose(1, 0, 2),
        owned_grads[None],
        master_new[None],
        first_new[None],
        second_new[None],
        weights_full[None],
        small_total,
    )


def body(
    frames,
    lengths,
    key_mask,
    cotangent,
    gain_one,
    shift_one,
    query_weight,
    query_bias,
    key_weight,
    value_weight,
    value_bias,
    out_weight,
    out_bias,
    gain_two,
    shift_two,
    up_weight,
    up_bias,
    down_weight,
    down_bias,
    master,
    moment_one,
    moment_two,
    adam_step,
    hyper_rates,
):
    local_rows, clip_count, model_width = frames.shape
    total_rows = key_mask.shape[1]
    head_cols = query_weight.shape[1]
    heads_here = head_cols // HD
    block_rows = min(512, total_rows)
    blocks = total_rows // block_rows
    score_scale = 1.0 / math.sqrt(HD)
    position = jnp.arange(total_rows, dtype=jnp.int32)
    keep_query = position[None, :] < lengths[:, None]
    keep_key = jnp.logical_and(keep_query, key_mask == 1)
    gain_first = gain_one.astype(jnp.float32)
    shift_first = shift_one.astype(jnp.float32)
    gain_second = gain_two.astype(jnp.float32)
    shift_second = shift_two.astype(jnp.float32)
    inputs = frames.astype(jnp.float32)
    normed = layer_norm(inputs, gain_first, shift_first).astype(jnp.bfloat16)
    joined_weight = jnp.concatenate([query_weight, key_weight, value_weight], axis=1)
    joined_bias = jnp.concatenate(
        [
            query_bias.astype(jnp.float32),
            jnp.zeros((head_cols,), jnp.float32),
            value_bias.astype(jnp.float32),
        ]
    )
    normed_full = lax.all_gather(normed, "mp", axis=0, tiled=True)
    projected = (
        jnp.einsum("rcd,de->rce", normed_full, joined_weight, preferred_element_type=jnp.float32)
        + joined_bias
    ).astype(jnp.bfloat16)
    query = projected[:, :, :head_cols].reshape(total_rows, clip_count, heads_here, HD)
    keys = projected[:, :, head_cols : 2 * head_cols].reshape(
        total_rows, clip_count, heads_here, HD
    )
    values = projected[:, :, 2 * head_cols :].reshape(total_rows, clip_count, heads_here, HD)

    def scores_of(row_start):
        query_block = lax.dynamic_slice_in_dim(query, row_start, block_rows, 0)
        raw_scores = (
            jnp.einsum("qchd,kchd->chqk", query_block, keys, preferred_element_type=jnp.float32)
            * score_scale
        )
        return (query_block, jnp.where(keep_key[:, None, None, :], raw_scores, MASK_VALUE))

    def forward_block(block_index):
        row_start = block_index * block_rows
        _, masked = scores_of(row_start)
        row_peak = jnp.max(masked, axis=-1, keepdims=True)
        exp_scores = jnp.exp(masked - row_peak)
        row_total = jnp.sum(exp_scores, axis=-1, keepdims=True)
        probability = (exp_scores / row_total).astype(jnp.bfloat16)
        attended = jnp.einsum(
            "chqk,kchd->qchd", probability, values, preferred_element_type=jnp.float32
        ).astype(jnp.bfloat16)
        live_rows = lax.dynamic_slice_in_dim(keep_query, row_start, block_rows, 1)
        block_peak = jnp.max(
            jnp.where(live_rows[:, None, :], row_peak[..., 0], MASK_VALUE), axis=(0, 2)
        )
        return (attended, (row_peak + jnp.log(row_total))[..., 0], block_peak)

    attended_blocks, log_totals, block_peaks = lax.map(forward_block, jnp.arange(blocks))
    attended_full = attended_blocks.reshape(total_rows, clip_count, head_cols)
    head_peak = lax.pmax(jnp.max(block_peaks, axis=0), "dp")
    rows_here = attended_full
    attn_branch = lax.psum_scatter(
        jnp.einsum("rck,kd->rcd", rows_here, out_weight, preferred_element_type=jnp.float32),
        "mp",
        scatter_dimension=0,
        tiled=True,
    ) + out_bias.astype(jnp.float32)
    middle = inputs + attn_branch
    normed_two = layer_norm(middle, gain_second, shift_second).astype(jnp.bfloat16)
    upstream = cotangent.astype(jnp.float32)
    normed_two_full = lax.all_gather(normed_two, "mp", axis=0, tiled=True)
    before = jnp.einsum(
        "rcd,df->rcf", normed_two_full, up_weight, preferred_element_type=jnp.float32
    ) + up_bias.astype(jnp.float32)
    hidden = exact_gelu(before).astype(jnp.bfloat16)
    rows_here = hidden
    feed = lax.psum_scatter(
        jnp.einsum(
            "rcf,fd->rcd", rows_here, down_weight, preferred_element_type=jnp.float32
        ).astype(jnp.bfloat16),
        "mp",
        scatter_dimension=0,
        tiled=True,
    ).astype(jnp.float32) + down_bias.astype(jnp.float32)
    layer_out = (middle + feed).astype(jnp.bfloat16)
    feed_grad_full = lax.all_gather(cotangent, "mp", axis=0, tiled=True)
    down_grad = jnp.einsum(
        "rcf,rcd->fd", hidden, feed_grad_full, preferred_element_type=jnp.float32
    )
    hidden_grad = jnp.einsum(
        "rcd,fd->rcf", feed_grad_full, down_weight, preferred_element_type=jnp.float32
    )
    _, gelu_pull = jax.vjp(exact_gelu, before)
    before_grad = gelu_pull(hidden_grad)[0].astype(jnp.bfloat16)
    up_bias_grad = jnp.sum(before_grad.astype(jnp.float32), axis=(0, 1))
    up_grad = jnp.einsum(
        "rcd,rcf->df", normed_two_full, before_grad, preferred_element_type=jnp.float32
    )
    rows_here = before_grad
    normed_two_grad = lax.psum_scatter(
        jnp.einsum("rcf,df->rcd", rows_here, up_weight, preferred_element_type=jnp.float32),
        "mp",
        scatter_dimension=0,
        tiled=True,
    )
    _, norm_two_pull = jax.vjp(layer_norm, middle, gain_second, shift_second)
    middle_norm_grad, gain_two_grad, shift_two_grad = norm_two_pull(normed_two_grad)
    middle_grad = upstream + middle_norm_grad
    branch_grad = middle_grad.astype(jnp.bfloat16)
    branch_grad_full = lax.all_gather(branch_grad, "mp", axis=0, tiled=True)
    out_grad = jnp.einsum(
        "rck,rcd->kd", attended_full, branch_grad_full, preferred_element_type=jnp.float32
    )
    attended_grad = jnp.einsum(
        "rcd,kd->rck", branch_grad_full, out_weight, preferred_element_type=jnp.float32
    ).astype(jnp.bfloat16)
    attended_grad = attended_grad.reshape(total_rows, clip_count, heads_here, HD)

    def backward_block(carry, block_index):
        key_total, value_total = carry
        row_start = block_index * block_rows
        query_block, masked = scores_of(row_start)
        log_total = log_totals[block_index]
        probability = jnp.exp(masked - log_total[..., None])
        grad_block = lax.dynamic_slice_in_dim(attended_grad, row_start, block_rows, 0)
        value_total = value_total + jnp.einsum(
            "chqk,qchd->kchd",
            probability.astype(jnp.bfloat16),
            grad_block,
            preferred_element_type=jnp.float32,
        )
        prob_grad = jnp.einsum(
            "qchd,kchd->chqk", grad_block, values, preferred_element_type=jnp.float32
        )
        score_grad = (
            probability * (prob_grad - jnp.sum(probability * prob_grad, axis=-1, keepdims=True))
        ).astype(jnp.bfloat16)
        query_grad = (
            jnp.einsum("chqk,kchd->qchd", score_grad, keys, preferred_element_type=jnp.float32)
            * score_scale
        ).astype(jnp.bfloat16)
        key_total = (
            key_total
            + jnp.einsum(
                "chqk,qchd->kchd", score_grad, query_block, preferred_element_type=jnp.float32
            )
            * score_scale
        )
        return ((key_total, value_total), query_grad)

    empty_grad = jnp.zeros((total_rows, clip_count, heads_here, HD), jnp.float32)
    (key_total, value_total), query_blocks = lax.scan(
        backward_block, (empty_grad, empty_grad), jnp.arange(blocks)
    )
    joined_grad = jnp.concatenate(
        [
            query_blocks.reshape(total_rows, clip_count, head_cols),
            key_total.reshape(total_rows, clip_count, head_cols).astype(jnp.bfloat16),
            value_total.reshape(total_rows, clip_count, head_cols).astype(jnp.bfloat16),
        ],
        axis=-1,
    )
    joined_bias_grad = jnp.sum(joined_grad.astype(jnp.float32), axis=(0, 1))
    normed_back = lax.all_gather(normed, "mp", axis=0, tiled=True)
    joined_weight_grad = jnp.einsum(
        "rcd,rce->de", normed_back, joined_grad, preferred_element_type=jnp.float32
    )
    rows_here = joined_grad
    normed_grad = lax.psum_scatter(
        jnp.einsum(
            "rce,de->rcd", rows_here, joined_weight, preferred_element_type=jnp.float32
        ).astype(jnp.bfloat16),
        "mp",
        scatter_dimension=0,
        tiled=True,
    ).astype(jnp.float32)
    _, norm_one_pull = jax.vjp(layer_norm, inputs, gain_first, shift_first)
    input_norm_grad, gain_one_grad, shift_one_grad = norm_one_pull(normed_grad)
    input_grad = middle_grad + input_norm_grad
    out_bias_grad = jnp.sum(branch_grad.astype(jnp.float32), axis=(0, 1))
    down_bias_grad = jnp.sum(upstream, axis=(0, 1))
    small_terms = jnp.concatenate(
        [
            gain_one_grad,
            shift_one_grad,
            out_bias_grad,
            gain_two_grad,
            shift_two_grad,
            down_bias_grad,
        ]
    )
    small_share = lax.psum_scatter(small_terms, "mp", scatter_dimension=0, tiled=True)
    small_total = lax.psum(small_share, "dp")
    packed = jnp.concatenate(
        [
            joined_weight_grad[:, :head_cols].reshape(-1),
            joined_bias_grad[:head_cols],
            joined_weight_grad[:, head_cols : 2 * head_cols].reshape(-1),
            joined_weight_grad[:, 2 * head_cols :].reshape(-1),
            joined_bias_grad[2 * head_cols :],
            out_grad.reshape(-1),
            up_grad.reshape(-1),
            up_bias_grad,
            down_grad.reshape(-1),
            small_share,
        ]
    )
    owned_grads = lax.psum_scatter(
        packed.astype(jnp.bfloat16), "dp", scatter_dimension=0, tiled=True
    ).astype(jnp.float32)
    share_size = owned_grads.shape[0]
    learn_rate = hyper_rates[0]
    weight_decay = hyper_rates[1]
    logit_cap = hyper_rates[2]
    step_count = adam_step[0].astype(jnp.float32)
    first_new = BETA_FIRST * moment_one[0] + (1.0 - BETA_FIRST) * owned_grads
    second_new = BETA_SECOND * moment_two[0] + (1.0 - BETA_SECOND) * owned_grads * owned_grads
    first_hat = first_new / (1.0 - jnp.power(BETA_FIRST, step_count))
    second_hat = second_new / (1.0 - jnp.power(BETA_SECOND, step_count))
    entry_index = lax.axis_index("dp") * share_size + jnp.arange(share_size, dtype=jnp.int32)
    query_end = model_width * head_cols
    query_bias_end = query_end + head_cols
    key_end = query_bias_end + model_width * head_cols
    column = jnp.where(
        entry_index < query_end,
        entry_index % head_cols,
        jnp.where(
            entry_index < query_bias_end,
            entry_index - query_end,
            (entry_index - query_bias_end) % head_cols,
        ),
    )
    head_index = column // HD
    root_factor = jnp.sqrt(logit_cap / jnp.maximum(head_peak, logit_cap))
    head_factor = jnp.zeros((share_size,), jnp.float32)
    for head_number in range(heads_here):
        head_factor = head_factor + jnp.where(
            head_index == head_number, root_factor[head_number], 0.0
        )
    factor = jnp.where(entry_index < key_end, head_factor, 1.0)
    master_here = master[0]
    master_new = (
        master_here
        - learn_rate
        * (first_hat / (jnp.sqrt(second_hat) + ADAM_EPSILON) + weight_decay * master_here)
    ) * factor
    weights_full = lax.all_gather(master_new.astype(jnp.bfloat16), "dp", axis=0, tiled=True)
    return (
        layer_out,
        input_grad,
        owned_grads[None],
        master_new[None],
        first_new[None],
        second_new[None],
        weights_full[None],
        small_total,
    )


def solution(mesh):
    chosen = fast_body if dict(mesh.shape) == {"dp": 4, "mp": 8} else body
    placed = (
        P("mp", "dp", None),
        P("dp"),
        P("dp", None),
        P("mp", "dp", None),
        P(),
        P(),
        P(None, "mp"),
        P("mp"),
        P(None, "mp"),
        P(None, "mp"),
        P("mp"),
        P("mp", None),
        P(),
        P(),
        P(),
        P(None, "mp"),
        P("mp"),
        P("mp", None),
        P(),
        P("mp", "dp"),
        P("mp", "dp"),
        P("mp", "dp"),
        P(),
        P(),
    )
    return jax.shard_map(
        chosen,
        mesh=mesh,
        in_specs=placed,
        out_specs=(
            P("mp", "dp", None),
            P("mp", "dp", None),
            P("mp", "dp"),
            P("mp", "dp"),
            P("mp", "dp"),
            P("mp", "dp"),
            P("mp", None),
            P("mp"),
        ),
        check_vma=False,
    )
```

```python
import functools
import math

import jax
import jax.numpy as jnp
from jax import lax
from jax.experimental import pallas as pl
from jax.experimental.pallas import tpu as pltpu
from jax.sharding import PartitionSpec as P

HD = 80


NORM_EPSILON = 1e-05
ADAM_EPSILON = 1e-08
BETA_FIRST = 0.9
BETA_SECOND = 0.999
MASK_VALUE = -1e30


def layer_norm(value, gain, shift):
    center = value - jnp.mean(value, axis=-1, keepdims=True)
    spread = jnp.mean(center * center, axis=-1, keepdims=True)
    return center * lax.rsqrt(spread + NORM_EPSILON) * gain + shift


def exact_gelu(argument):
    return jax.nn.gelu(argument, approximate=False)


MESH = pl.DeviceIdType.MESH
ANY = pl.BlockSpec(memory_space=pl.ANY)
VMEM = pl.BlockSpec(memory_space=pltpu.VMEM)
LINE = 4
ROWS = 384
BF = jnp.bfloat16
F32 = jnp.float32


class Place:
    def __init__(self):
        self.dp = lax.axis_index("dp")
        self.mp = lax.axis_index("mp")
        self.z = self.mp // 2
        self.c = self.mp % 2
        self.pair = self.z * 2 + 1 - self.c
        self.dpx = self.dp + 1 - 2 * (self.dp % 2)
        self.dpy = (self.dp + 2) % 4
        self.dpd = 3 - self.dp

    def zorder(self, event):
        if event == 0:
            return self.z
        if event == 1:
            return self.z + 1 - 2 * (self.z % 2)
        if event == 2:
            return 2 - self.z // 2
        return 3 - 3 * (self.z // 2)


def greet(place, mp_all=False, line=False, plane=False, pair=True):
    barrier = pltpu.get_barrier_semaphore()
    count = 0

    def signal(dp, mp):
        pl.semaphore_signal(barrier, inc=1, device_id=(dp, mp), device_id_type=MESH)

    if mp_all:
        for hop in range(1, 8):
            signal(place.dp, (place.mp + hop) % 8)
        count += 7
    else:
        if pair:
            signal(place.dp, place.pair)
            count += 1
        if line:

            @pl.when(place.z > 0)
            def _():
                signal(place.dp, place.mp - 2)

            @pl.when(place.z < LINE - 1)
            def _():
                signal(place.dp, place.mp + 2)

    if plane:
        for other in (place.dpx, place.dpy, place.dpd):
            signal(other, place.mp)
        count += 3
    if line and not mp_all:
        pl.semaphore_wait(barrier, count + 1 + (place.z + 1) // 2 % 2)
    else:
        pl.semaphore_wait(barrier, count)


def remote(src, dst, send, recv, dp, mp):
    return pltpu.make_async_remote_copy(
        src_ref=src,
        dst_ref=dst,
        send_sem=send,
        recv_sem=recv,
        device_id=(dp, mp),
        device_id_type=MESH,
    )


def line_gather(place, src, out, local, send, recv, paired, ready=None):
    dp, z, c, mp, pair = place.dp, place.z, place.c, place.mp, place.pair

    def slot_of(level, core):
        return level * 2 + core if paired else level

    def hop(event, slot, source, direction, target):
        return remote(source, out.at[slot], send.at[event, direction], recv.at[slot], dp, target)

    own = slot_of(z, c)
    keep = pltpu.make_async_copy(src, out.at[own], local)
    keep.start()

    def ways(event, level, slot, source, act):
        up = z < LINE - 1
        down = z > 0
        if event > 0:
            up = jnp.logical_and(up, level < z)
            down = jnp.logical_and(down, level > z)

        @pl.when(up)
        def _():
            act(hop(event, slot, source, 1, mp + 2))

        @pl.when(down)
        def _():
            act(hop(event, slot, source, 2, mp - 2))

        if paired:
            act(hop(event, slot, source, 0, pair))

    ways(0, z, own, src, lambda copy: copy.start())
    yield
    if ready is not None:
        keep.wait()
        ready(own)
        if paired:
            other = slot_of(z, 1 - c)
            hop(0, other, out.at[other], 0, pair).wait_recv()
            ready(other)
    for event in range(1, LINE):
        level = place.zorder(event)
        slot = slot_of(level, c)
        hop(event, slot, out.at[slot], 0, pair).wait_recv()
        ways(event, level, slot, out.at[slot], lambda copy: copy.start())
        if ready is not None:
            ready(slot)
            if paired:
                other = slot_of(level, 1 - c)
                hop(event, other, out.at[other], 0, pair).wait_recv()
                ready(other)
        yield
    if ready is None:
        if paired:
            for level in range(LINE):
                other = slot_of(level, 1 - c)
                hop(0, other, out.at[other], 0, pair).wait_recv()
        keep.wait()
    for event in range(LINE):
        level = place.zorder(event)
        slot = slot_of(level, c)
        ways(event, level, slot, out.at[slot], lambda copy: copy.wait_send())
    yield


def plane_gather(place, src, out, local, send, recv):
    dp, c, mp, pair = place.dp, place.c, place.mp, place.pair
    dpx, dpy, dpd = place.dpx, place.dpy, place.dpd
    half = src.shape[0] // 2
    part_a, part_b = pl.ds(0, half), pl.ds(half, half)

    def at(group, core):
        return out.at[group * 2 + core]

    keep = pltpu.make_async_copy(src, at(dp, c), local)
    keep.start()
    here = at(dp, c)
    sends = [
        remote(src, here, send.at[0], recv.at[0], dp, pair),
        remote(src, here, send.at[1], recv.at[1], dpx, mp),
        remote(src, here, send.at[2], recv.at[2], dpy, mp),
    ]
    for copy in sends:
        copy.start()
    yield
    from_x, from_y = at(dpx, c), at(dpy, c)
    remote(from_x, from_x, send.at[1], recv.at[1], dpx, mp).wait_recv()
    sends.append(
        remote(from_x.at[part_a], from_x.at[part_a], send.at[3], recv.at[3], dpy, mp)
    )
    sends[-1].start()
    remote(from_y, from_y, send.at[2], recv.at[2], dpy, mp).wait_recv()
    sends.append(
        remote(from_y.at[part_b], from_y.at[part_b], send.at[4], recv.at[4], dpx, mp)
    )
    sends[-1].start()
    for index, block in ((5, from_x), (6, from_y)):
        sends.append(remote(block, block, send.at[index], recv.at[index], dp, pair))
        sends[-1].start()
    yield
    from_d = at(dpd, c)
    remote(from_d.at[part_a], from_d.at[part_a], send.at[3], recv.at[3], dpy, mp).wait_recv()
    sends.append(
        remote(from_d.at[part_a], from_d.at[part_a], send.at[7], recv.at[7], dp, pair)
    )
    sends[-1].start()
    remote(from_d.at[part_b], from_d.at[part_b], send.at[4], recv.at[4], dpx, mp).wait_recv()
    sends.append(
        remote(from_d.at[part_b], from_d.at[part_b], send.at[8], recv.at[8], dp, pair)
    )
    sends[-1].start()
    yield
    for index, group in ((0, dp), (5, dpx), (6, dpy)):
        block = at(group, 1 - c)
        remote(block, block, send.at[index], recv.at[index], dp, pair).wait_recv()
    other = at(dpd, 1 - c)
    for index, rows in ((7, part_a), (8, part_b)):
        remote(other.at[rows], other.at[rows], send.at[index], recv.at[index], dp, pair).wait_recv()
    for copy in sends:
        copy.wait_send()
    keep.wait()
    yield


def drive(*programs):
    live = list(programs)
    while live:
        for program in list(live):
            try:
                next(program)
            except StopIteration:
                live.remove(program)


def dma(*shape):
    return pltpu.SemaphoreType.DMA(shape)


def params(cid, vmem=40):
    return pltpu.CompilerParams(
        collective_id=cid, has_side_effects=True, vmem_limit_bytes=vmem << 20
    )


def exchange(place, src, out, local, send, recv):
    dp, mp = place.dp, place.mp
    keep = pltpu.make_async_copy(src.at[mp], out.at[mp], local)
    keep.start()
    sends = []
    for hop in range(1, 8):
        target = (mp + hop) % 8
        sends.append(
            remote(src.at[target], out.at[mp], send.at[hop], recv.at[hop], dp, target)
        )
        sends[-1].start()
    yield
    keep.wait()
    for hop in range(1, 8):
        origin = (mp + 8 - hop) % 8
        remote(out.at[origin], out.at[origin], send.at[hop], recv.at[hop], dp, origin).wait_recv()
    for copy in sends:
        copy.wait_send()
    yield


def line_reduce(place, produce, tiles, result, bufs, sems, paired):
    dp, z, c, mp, pair = place.dp, place.z, place.c, place.mp, place.pair
    from_above, from_below, out_block = bufs["above"], bufs["below"], bufs["out"]
    order = [place.zorder(event) for event in (3, 2, 1, 0)]

    @pl.when(z == LINE - 1)
    def _():
        from_above[...] = jnp.zeros(from_above.shape, BF)

    @pl.when(z == 0)
    def _():
        from_below[...] = jnp.zeros(from_below.shape, BF)

    def across(step, level):
        return remote(
            bufs["pair_out"].at[step],
            bufs["pair_in"].at[level],
            sems["pair_send"].at[step],
            sems["pair_recv"].at[level],
            dp,
            pair,
        )

    if paired:
        for step, level in enumerate(order):
            for rows in tiles:
                bufs["pair_out"][step, rows] = produce(level, 1 - c, rows).astype(BF)
            across(step, level).start()
    yield

    def toward(step, level, act):
        @pl.when(level < z)
        def _():
            act(
                remote(
                    out_block.at[step],
                    from_above.at[level],
                    sems["line_send"].at[step],
                    sems["above"].at[level],
                    dp,
                    mp - 2,
                )
            )

        @pl.when(level > z)
        def _():
            act(
                remote(
                    out_block.at[step],
                    from_below.at[level],
                    sems["line_send"].at[step],
                    sems["below"].at[level],
                    dp,
                    mp + 2,
                )
            )

    def arrive(level, above):
        if above:
            remote(
                from_above.at[level],
                from_above.at[level],
                sems["line_send"].at[0],
                sems["above"].at[level],
                dp,
                mp,
            ).wait_recv()
        else:
            remote(
                from_below.at[level],
                from_below.at[level],
                sems["line_send"].at[0],
                sems["below"].at[level],
                dp,
                mp,
            ).wait_recv()

    for step, level in enumerate(order[:3]):
        if paired:
            across(step, level).wait_recv()

        @pl.when(jnp.logical_and(level < z, z < LINE - 1))
        def _():
            arrive(level, True)

        @pl.when(jnp.logical_and(level > z, z > 0))
        def _():
            arrive(level, False)

        for rows in tiles:
            total = produce(level, c, rows)
            if paired:
                total = total + bufs["pair_in"][level, rows].astype(F32)

            @pl.when(level < z)
            def _():
                out_block[step, rows] = (total + from_above[level, rows].astype(F32)).astype(BF)

            @pl.when(level > z)
            def _():
                out_block[step, rows] = (total + from_below[level, rows].astype(F32)).astype(BF)

        toward(step, level, lambda copy: copy.start())
        yield

    if paired:
        across(3, z).wait_recv()

    @pl.when(z < LINE - 1)
    def _():
        arrive(z, True)

    @pl.when(z > 0)
    def _():
        arrive(z, False)

    for rows in tiles:
        total = produce(z, c, rows)
        if paired:
            total = total + bufs["pair_in"][z, rows].astype(F32)
        total = total + from_above[z, rows].astype(F32) + from_below[z, rows].astype(F32)
        result(rows, total)
    for step, level in enumerate(order):
        if paired:
            across(step, level).wait_send()
        if step < 3:
            toward(step, level, lambda copy: copy.wait_send())
    yield


def line_reduce_scratch(rows, cols, paired):
    block = lambda n: pltpu.VMEM((n, rows, cols), BF)
    scratch = {"above": block(4), "below": block(4), "out": block(3)}
    sems = {"line_send": dma(3), "above": dma(4), "below": dma(4)}
    if paired:
        scratch.update({"pair_out": block(4), "pair_in": block(4)})
        sems.update({"pair_send": dma(4), "pair_recv": dma(4)})
    return scratch, sems


def plane_reduce(place, produce, tile, half, result, bufs, sems, paired=True):
    dp, c, mp, pair = place.dp, place.c, place.mp, place.pair
    dpx, dpy, dpd = place.dpx, place.dpy, place.dpd
    order = [dpd, dpx, dpy, dp]
    tiles_a = [pl.ds(start, tile) for start in range(0, half, tile)]
    send, recv = sems["send"], sems["recv"]
    out_block, landed = bufs["out"], bufs["in"]

    def across(step):
        return remote(
            bufs["pair_out"].at[step],
            bufs["pair_in"].at[step],
            sems["pair_send"].at[step],
            sems["pair_recv"].at[step],
            dp,
            pair,
        )

    if paired:
        for step, group in enumerate(order):
            for start in range(0, 2 * half, tile):
                bufs["pair_out"][step, pl.ds(start, tile)] = produce(
                    group, 1 - c, start
                ).astype(BF)
            across(step).start()
    yield

    def share(step, start):
        total = produce(order[step], c, start)
        if paired:
            total = total + bufs["pair_in"][step, pl.ds(start, tile)].astype(F32)
        return total

    def hop(index, target):
        return remote(
            out_block.at[index], landed.at[index], send.at[index], recv.at[index], target, mp
        )

    def fill(index, step, base, extra=None):
        for rows in tiles_a:
            total = share(step, base + rows.start)
            if extra is not None:
                total = total + landed[extra, rows].astype(F32)
            out_block[index, rows] = total.astype(BF)

    targets = [dpx, dpy, dpx, dpx, dpy, dpy]
    if paired:
        across(0).wait_recv()
    fill(0, 0, 0)
    hop(0, dpx).start()
    fill(1, 0, half)
    hop(1, dpy).start()
    yield
    if paired:
        across(1).wait_recv()
        across(2).wait_recv()
    fill(2, 1, 0)
    hop(2, dpx).start()
    fill(4, 2, half)
    hop(4, dpy).start()
    yield
    hop(1, dpy).wait_recv()
    fill(3, 1, half, extra=1)
    hop(3, dpx).start()
    hop(0, dpx).wait_recv()
    fill(5, 2, 0, extra=0)
    hop(5, dpy).start()
    yield
    if paired:
        across(3).wait_recv()
    for index in (2, 3, 4, 5):
        hop(index, targets[index]).wait_recv()
    for base, pieces in ((0, (2, 5)), (half, (3, 4))):
        for rows in tiles_a:
            total = share(3, base + rows.start)
            for piece in pieces:
                total = total + landed[piece, rows].astype(F32)
            result(pl.ds(base + rows.start, tile), total)
    for index in range(6):
        hop(index, targets[index]).wait_send()
    if paired:
        for step in range(4):
            across(step).wait_send()
    yield


def plane_reduce_scratch(half, cols, paired=True):
    block = lambda n, rows: pltpu.VMEM((n, rows, cols), BF)
    scratch = {"out": block(6, half), "in": block(6, half)}
    sems = {"send": dma(6), "recv": dma(6)}
    if paired:
        scratch.update({"pair_out": block(4, 2 * half), "pair_in": block(4, 2 * half)})
        sems.update({"pair_send": dma(4), "pair_recv": dma(4)})
    return scratch, sems


def project_kernel(
    normed_ref, cot_ref, weight_ref, bias_ref, nfull_ref, qkv_ref, cfull_ref,
    local, line_send, line_recv, plane_send, plane_recv,
):
    place = Place()
    greet(place, line=True, plane=True)

    def ready(slot):
        @pl.loop(0, 3)
        def _(step):
            rows = pl.ds(step * 128, 128)
            product = lax.dot_general(
                nfull_ref[slot, rows],
                weight_ref[...],
                (((1,), (1,)), ((), ())),
                preferred_element_type=F32,
            )
            qkv_ref[slot, rows] = (product + bias_ref[...]).astype(BF)

    drive(
        line_gather(
            place, normed_ref, nfull_ref, local.at[0], line_send, line_recv, True, ready
        ),
        plane_gather(place, cot_ref, cfull_ref, local.at[1], plane_send, plane_recv),
    )


def project(normed, cotangent, weight, bias):
    return pl.pallas_call(
        project_kernel,
        out_shape=(
            jax.ShapeDtypeStruct((8,) + normed.shape, BF),
            jax.ShapeDtypeStruct((8, ROWS, weight.shape[0]), BF),
            jax.ShapeDtypeStruct((8,) + cotangent.shape, BF),
        ),
        in_specs=[ANY, ANY, VMEM, VMEM],
        out_specs=(VMEM, VMEM, ANY),
        scratch_shapes=[dma(2), dma(4, 3), dma(8), dma(9), dma(9)],
        compiler_params=params(0),
        name="project",
    )(normed, cotangent, weight, bias)


def attend_kernel(
    qkv_ref, mask_ref, live_ref, weights_ref, att_ref, logs_ref, peak_ref, wfull_ref,
    out_ref, vt_ref, local, send, recv, line_send, line_recv,
):
    place = Place()
    greet(place, mp_all=True)
    gather = line_gather(
        place, weights_ref, wfull_ref, local.at[1], line_send, line_recv, True
    )
    next(gather)
    factor = math.log2(math.e) / math.sqrt(HD)
    peak_ref[...] = jnp.full(peak_ref.shape, MASK_VALUE, F32)

    @pl.loop(0, 6)
    def _(turn):
        clip = turn // 2
        head = turn % 2
        lane = pl.multiple_of(head * 128, 128)
        row = pl.multiple_of(head * HD, 16)
        keys = qkv_ref[:, clip, :, pl.ds(256 + lane, 128)].reshape(1024, 128)
        vt_ref[...] = qkv_ref[:, clip, :, pl.ds(512 + lane, 128)].reshape(1024, 128).T

        @pl.loop(0, 4)
        def _(block):
            query = qkv_ref[pl.ds(block * 2, 2), clip, :, pl.ds(lane, 128)].reshape(256, 128)
            columns = pl.ds(pl.multiple_of(block * 256, 256), 256)
            scores = lax.dot_general(
                keys, query, (((1,), (1,)), ((), ())), preferred_element_type=F32
            )
            scores = scores + mask_ref[clip]
            peak = jnp.max(scores, axis=0, keepdims=True)
            powers = jnp.exp2((scores - peak) * factor)
            total = jnp.sum(powers, axis=0, keepdims=True)
            mixed = lax.dot_general(
                vt_ref[...],
                powers.astype(BF),
                (((1,), (0,)), ((), ())),
                preferred_element_type=F32,
            )
            mixed = (mixed / total).astype(BF)
            for part in range(2):
                out_ref[block * 2 + part, clip, pl.ds(row, HD)] = mixed[
                    :HD, part * 128 : part * 128 + 128
                ]
            logs_ref[turn, :, columns] = peak * factor + jnp.log2(total)
            peak_ref[head] = jnp.maximum(
                peak_ref[head], jnp.where(live_ref[clip, :, columns] > 0, peak, MASK_VALUE)
            )

    drive(exchange(place, out_ref, att_ref, local.at[0], send, recv), gather)


def attend(qkv, mask, live, weights):
    return pl.pallas_call(
        attend_kernel,
        out_shape=(
            jax.ShapeDtypeStruct((8, 3, 160, 128), BF),
            jax.ShapeDtypeStruct((6, 1, 1024), F32),
            jax.ShapeDtypeStruct((2, 8, 256), F32),
            jax.ShapeDtypeStruct((8,) + weights.shape, BF),
        ),
        in_specs=[VMEM, VMEM, VMEM, ANY],
        out_specs=(VMEM, VMEM, VMEM, ANY),
        scratch_shapes=[
            pltpu.VMEM((8, 3, 160, 128), BF),
            pltpu.VMEM((128, 1024), BF),
            dma(2),
            dma(8),
            dma(8),
            dma(4, 3),
            dma(8),
        ],
        compiler_params=params(1),
        name="attend",
    )(qkv, mask, live, weights)


def attend_back_kernel(
    qkv_ref, mask_ref, logs_ref, grads_ref, dqkv_ref,
    grad_ref, kt_ref, dk_ref, dv_ref, block_ref, local, send, recv,
):
    place = Place()
    greet(place, mp_all=True)
    drive(exchange(place, grads_ref, grad_ref, local, send, recv))
    scale = 1.0 / math.sqrt(HD)
    factor = math.log2(math.e) * scale
    block_ref[...] = jnp.zeros(block_ref.shape, BF)

    @pl.loop(0, 6)
    def _(turn):
        clip = turn // 2
        head = turn % 2
        lane = pl.multiple_of(head * 128, 128)
        row = pl.multiple_of(head * HD, 16)
        keys = qkv_ref[:, clip, :, pl.ds(256 + lane, 128)].reshape(1024, 128)
        kt_ref[...] = keys.T
        dk_ref[...] = jnp.zeros(dk_ref.shape, F32)
        dv_ref[...] = jnp.zeros(dv_ref.shape, F32)

        @pl.loop(0, 4)
        def _(block):
            query = qkv_ref[pl.ds(block * 2, 2), clip, :, pl.ds(lane, 128)].reshape(256, 128)
            values = qkv_ref[:, clip, :, pl.ds(512 + lane, 128)].reshape(1024, 128)
            keys = qkv_ref[:, clip, :, pl.ds(256 + lane, 128)].reshape(1024, 128)
            columns = pl.ds(pl.multiple_of(block * 256, 256), 256)
            for part in range(2):
                block_ref[:HD, part * 128 : part * 128 + 128] = grad_ref[
                    block * 2 + part, clip, pl.ds(row, HD)
                ]
            scores = lax.dot_general(
                keys, query, (((1,), (1,)), ((), ())), preferred_element_type=F32
            )
            chance = jnp.exp2((scores + mask_ref[clip]) * factor - logs_ref[turn, :, columns])
            dv_ref[...] += lax.dot_general(
                chance.astype(BF),
                block_ref[...],
                (((1,), (1,)), ((), ())),
                preferred_element_type=F32,
            )
            slope = lax.dot_general(
                values, block_ref[...], (((1,), (0,)), ((), ())), preferred_element_type=F32
            )
            center = jnp.sum(chance * slope, axis=0, keepdims=True)
            change = (chance * (slope - center)).astype(BF)
            dk_ref[...] += lax.dot_general(
                change, query, (((1,), (0,)), ((), ())), preferred_element_type=F32
            )
            dq = lax.dot_general(
                kt_ref[...], change, (((1,), (0,)), ((), ())), preferred_element_type=F32
            )
            dqkv_ref[pl.ds(block * 2, 2), clip, :, pl.ds(lane, 128)] = (
                (dq.T * scale).astype(BF).reshape(2, 128, 128)
            )

        dqkv_ref[:, clip, :, pl.ds(256 + lane, 128)] = (
            (dk_ref[...] * scale).astype(BF).reshape(8, 128, 128)
        )
        dqkv_ref[:, clip, :, pl.ds(512 + lane, 128)] = (
            dv_ref[...].astype(BF).reshape(8, 128, 128)
        )


def attend_back(qkv, mask, logs, grads):
    return pl.pallas_call(
        attend_back_kernel,
        out_shape=jax.ShapeDtypeStruct(qkv.shape, BF),
        in_specs=[VMEM, VMEM, VMEM, ANY],
        out_specs=VMEM,
        scratch_shapes=[
            pltpu.VMEM((8, 3, 160, 128), BF),
            pltpu.VMEM((128, 1024), BF),
            pltpu.VMEM((1024, 128), F32),
            pltpu.VMEM((1024, 128), F32),
            pltpu.VMEM((128, 256), BF),
            pltpu.SemaphoreType.DMA(()),
            dma(8),
            dma(8),
        ],
        compiler_params=params(2),
        name="attend_back",
    )(qkv, mask, logs, grads)


def plane_share_kernel(block_ref, full_ref, local, send, recv):
    place = Place()
    greet(place, plane=True)
    drive(plane_gather(place, block_ref, full_ref, local, send, recv))


def plane_share(block):
    return pl.pallas_call(
        plane_share_kernel,
        out_shape=jax.ShapeDtypeStruct((8,) + block.shape, BF),
        in_specs=[ANY],
        out_specs=ANY,
        scratch_shapes=[pltpu.SemaphoreType.DMA(()), dma(9), dma(9)],
        compiler_params=params(3),
        name="plane_share",
    )(block)


def flatten(*pairs):
    names, shapes = [], []
    for number, group in enumerate(pairs):
        for name, shape in group.items():
            names.append((number, name))
            shapes.append(shape)

    def split(refs):
        groups = [{} for _ in pairs]
        for (number, name), ref in zip(names, refs):
            groups[number][name] = ref
        return groups

    return shapes, split


def plane_sums_kernel(split, first_ref, second_ref, first_out, second_out, *scratch):
    place = Place()
    bufs_one, sems_one, bufs_two, sems_two = split(scratch)
    greet(place, plane=True)

    def reader(ref):
        return lambda group, core, start: ref[group * 2 + core, pl.ds(start, 96)].astype(F32)

    def writer(ref):
        def write(rows, total):
            ref[rows] = total

        return write

    drive(
        plane_reduce(place, reader(first_ref), 96, 192, writer(first_out), bufs_one, sems_one),
        plane_reduce(place, reader(second_ref), 96, 192, writer(second_out), bufs_two, sems_two),
    )


def plane_sums(first, second):
    shapes, split = flatten(*plane_reduce_scratch(192, 1280), *plane_reduce_scratch(192, 1280))
    out = jax.ShapeDtypeStruct(first.shape[1:], F32)
    return pl.pallas_call(
        functools.partial(plane_sums_kernel, split),
        out_shape=(out, out),
        in_specs=[VMEM, VMEM],
        out_specs=(VMEM, VMEM),
        scratch_shapes=shapes,
        compiler_params=params(4, 60),
        name="plane_sums",
    )(first, second)


def line_product_kernel(split, grad_ref, weight_ref, out_ref, *scratch):
    place = Place()
    bufs, sems = split(scratch)
    greet(place, line=True)

    def produce(level, core, rows):
        return jnp.dot(
            grad_ref[level * 2 + core, rows], weight_ref[...], preferred_element_type=F32
        )

    def result(rows, total):
        out_ref[rows] = total

    tiles = [pl.ds(start, 128) for start in range(0, ROWS, 128)]
    drive(line_reduce(place, produce, tiles, result, bufs, sems, True))


def line_product(grads, weight):
    shapes, split = flatten(*line_reduce_scratch(ROWS, 1280, True))
    return pl.pallas_call(
        functools.partial(line_product_kernel, split),
        out_shape=jax.ShapeDtypeStruct((ROWS, 1280), F32),
        in_specs=[VMEM, VMEM],
        out_specs=VMEM,
        scratch_shapes=shapes,
        compiler_params=params(5, 60),
        name="line_product",
    )(grads, weight)


def line_sums_kernel(split, feed_ref, out_grad_ref, feed_out, out_out, *scratch):
    place = Place()
    bufs_one, sems_one, bufs_two, sems_two = split(scratch)
    greet(place, line=True)

    def write_feed(rows, total):
        feed_out[rows] = total

    def write_out(rows, total):
        out_out[rows] = total

    tiles = lambda rows, tile: [pl.ds(start, tile) for start in range(0, rows, tile)]
    drive(
        line_reduce(
            place,
            lambda level, core, rows: feed_ref[level, rows].astype(F32),
            tiles(feed_ref.shape[1], 112),
            write_feed,
            bufs_one,
            sems_one,
            False,
        ),
        line_reduce(
            place,
            lambda level, core, rows: out_grad_ref[level * 2 + core, rows].astype(F32),
            tiles(160, 80),
            write_out,
            bufs_two,
            sems_two,
            True,
        ),
    )


def line_sums(feed, out_grad):
    rows = feed.shape[1]
    shapes, split = flatten(
        *line_reduce_scratch(rows, 1280, False), *line_reduce_scratch(160, 1280, True)
    )
    return pl.pallas_call(
        functools.partial(line_sums_kernel, split),
        out_shape=(
            jax.ShapeDtypeStruct((rows, 1280), F32),
            jax.ShapeDtypeStruct((160, 1280), F32),
        ),
        in_specs=[VMEM, VMEM],
        out_specs=(VMEM, VMEM),
        scratch_shapes=shapes,
        compiler_params=params(6, 60),
        name="line_sums",
    )(feed, out_grad)


GROUP_ROWS = 4832
GROUP_STEP = 4800
PACK_ROWS = GROUP_STEP * 3 + GROUP_ROWS
SEGMENTS = (
    ("query", 0, 1600),
    ("query_bias", 204800, 2),
    ("key", 204960, 1600),
    ("value", 409760, 1600),
    ("value_bias", 614560, 2),
    ("out", 614720, 1600),
    ("up", 819520, 6400),
    ("up_bias", 1638720, 5),
    ("down", 1639360, 6400),
    ("small", 2458560, 8),
)
PACK_END = 19216


def segment_table():
    table, cursor = {}, 0
    for name, start, rows in SEGMENTS:
        row = start // 128
        cursor += 32
        cursor += (row - cursor) % 8
        table[name] = (cursor, row, rows, start % 128)
        cursor += rows
    return table, (cursor + 32 + 7) // 8 * 8


TABLE, STAGE_ROWS = segment_table()


def lane_of(rows):
    return lax.broadcasted_iota(jnp.int32, (rows, 128), 1)


def pack_rows(stage, packed):
    def piece(name, first, rows):
        base, row, _, shift = TABLE[name]
        at = base - row + first
        here = stage[pl.ds(at, rows)]
        if shift == 0:
            return here
        above = stage[pl.ds(at - 1, rows)]
        return jnp.where(
            lane_of(rows) >= shift, pltpu.roll(here, shift, 1), pltpu.roll(above, shift, 1)
        )

    done = set()
    for name, _, _ in SEGMENTS:
        _, row, rows, shift = TABLE[name]
        low = -(-(row + (1 if shift else 0)) // 16) * 16
        high = (row + rows) // 16 * 16
        if high <= low:
            continue
        done.update(range(low, high, 16))
        turns = (high - low) // 128

        @pl.loop(0, turns)
        def _(turn):
            first = pl.multiple_of(low + turn * 128, 16)
            packed[pl.ds(first, 128)] = piece(name, first, 128).astype(BF)

        for first in range(low + turns * 128, high, 16):
            packed[pl.ds(first, 16)] = piece(name, first, 16).astype(BF)
    for first in range(0, PACK_ROWS, 16):
        if first in done:
            continue
        total = jnp.zeros((16, 128), F32)
        for name, _, _ in SEGMENTS:
            _, row, rows, shift = TABLE[name]
            if row < first + 16 and row + rows + (1 if shift else 0) > first:
                total = total + piece(name, first, 16)
        packed[pl.ds(first, 16)] = total.astype(BF)


def stage_wide(stage, name, ref, step):
    base = TABLE[name][0]
    rows, wide = ref.shape[0], ref.shape[1] // 128

    @pl.loop(0, rows // step)
    def _(turn):
        first = pl.multiple_of(turn * step, step)
        for block in range(wide):
            stage[pl.ds(base + first * wide + block, step, stride=wide), :] = ref[
                pl.ds(first, step), pl.ds(block * 128, 128)
            ].astype(F32)


def stage_heads(stage, name, ref, lanes, column):
    base = TABLE[name][0]
    for head in range(2):
        column[head] = ref[:, pl.ds(lanes + head * 128, 128)]

    @pl.loop(0, 5)
    def _(turn):
        lane = lane_of(64)
        rows = [jnp.zeros((64, 128), F32) for _ in range(5)]
        for block in range(8):
            item, head = block // 2, block % 2
            value = column[head, pl.ds(turn * 256 + item, 64, stride=4)]
            offset = block * HD
            first, shift = offset // 128, offset % 128
            if shift:
                value = pltpu.roll(value, shift, 1)
            if shift + HD > 128:
                rows[first] = rows[first] + jnp.where(lane >= shift, value, 0.0)
                rows[first + 1] = rows[first + 1] + jnp.where(
                    lane < shift + HD - 128, value, 0.0
                )
            else:
                rows[first] = rows[first] + value
        for index in range(5):
            stage[pl.ds(base + turn * 320 + index, 64, stride=5), :] = rows[index]


def stage_head_bias(stage, name, ref, lanes):
    base = TABLE[name][0]
    lane = lane_of(1)
    first = ref[0:1, pl.ds(lanes, 128)]
    second = pltpu.roll(ref[0:1, pl.ds(lanes + 128, 128)], HD, 1)
    stage[pl.ds(base, 1)] = first + jnp.where(lane >= HD, second, 0.0)
    stage[pl.ds(base + 1, 1)] = jnp.where(lane < 2 * HD - 128, second, 0.0)


def pack_reduce_kernel(
    split, joined_ref, bias_ref, out_ref, up_ref, up_bias_ref, down_ref, small_ref, peak_ref,
    grads_ref, small_out, peak_out,
    stage, packed, column, small_in, small_all, peak_all,
    local, small_send, small_recv, plane_send, plane_recv, *scratch,
):
    place = Place()
    bufs, sems = split(scratch)
    greet(place, mp_all=True, plane=True)
    peers = (place.dpx, place.dpy, place.dpd)
    mixing = exchange(place, small_ref, small_in, local, small_send, small_recv)
    next(mixing)

    def tell(index, source, target, group, act):
        act(
            remote(
                source,
                target.at[place.dp],
                plane_send.at[index],
                plane_recv.at[index],
                group,
                place.mp,
            )
        )

    def heard(index, target, group):
        block = target.at[group]
        remote(
            block, block, plane_send.at[index], plane_recv.at[index], group, place.mp
        ).wait_recv()

    for index, group in enumerate(peers):
        tell(index, peak_ref, peak_all, group, lambda copy: copy.start())
    stage[...] = jnp.zeros(stage.shape, F32)
    for name, lanes in (("query", 0), ("key", 256), ("value", 512)):
        stage_heads(stage, name, joined_ref, lanes, column)
    stage_head_bias(stage, "query_bias", bias_ref, 0)
    stage_head_bias(stage, "value_bias", bias_ref, 512)
    stage_wide(stage, "out", out_ref, 160)
    stage_wide(stage, "up", up_ref, 256)
    stage_wide(stage, "down", down_ref, 128)
    stage[pl.ds(TABLE["up_bias"][0], 5)] = up_bias_ref[...]
    for _ in mixing:
        pass
    share = jnp.sum(small_in[...], axis=0)
    small_all[place.dp] = share
    stage[pl.ds(TABLE["small"][0], 8)] = share
    for index, group in enumerate(peers):
        tell(3 + index, small_all.at[place.dp], small_all, group, lambda copy: copy.start())
    pack_rows(stage, packed)

    def produce(group, core, start):
        first = pl.multiple_of(group * GROUP_STEP + start, 16)
        return packed[pl.ds(first, GROUP_ROWS // 2)].astype(F32)

    def result(rows, total):
        grads_ref[rows] = total

    half = GROUP_ROWS // 2
    drive(plane_reduce(place, produce, half, half, result, bufs, sems, False))
    for index, group in enumerate(peers):
        heard(index, peak_all, group)
        heard(3 + index, small_all, group)
    top = peak_ref[...]
    for group in peers:
        top = jnp.maximum(top, peak_all[group])
    peak_out[...] = top
    small_out[...] = jnp.sum(small_all[...], axis=0)
    for index, group in enumerate(peers):
        tell(index, peak_ref, peak_all, group, lambda copy: copy.wait_send())
        tell(3 + index, small_all.at[place.dp], small_all, group, lambda copy: copy.wait_send())


def pack_reduce(joined, bias, out, up, up_bias, down, small, peaks):
    shapes, split = flatten(*plane_reduce_scratch(GROUP_ROWS // 2, 128, False))
    return pl.pallas_call(
        functools.partial(pack_reduce_kernel, split),
        out_shape=(
            jax.ShapeDtypeStruct((GROUP_ROWS, 128), F32),
            jax.ShapeDtypeStruct((8, 128), F32),
            jax.ShapeDtypeStruct(peaks.shape, F32),
        ),
        in_specs=[VMEM] * 8,
        out_specs=(VMEM,) * 3,
        scratch_shapes=[
            pltpu.VMEM((STAGE_ROWS, 128), F32),
            pltpu.VMEM((PACK_ROWS, 128), BF),
            pltpu.VMEM((2, 1280, 128), F32),
            pltpu.VMEM((8, 8, 128), F32),
            pltpu.VMEM((4, 8, 128), F32),
            pltpu.VMEM((4,) + peaks.shape, F32),
            pltpu.SemaphoreType.DMA(()),
            dma(8),
            dma(8),
            dma(6),
            dma(6),
            *shapes,
        ],
        compiler_params=params(7, 60),
        name="pack_reduce",
    )(joined, bias, out, up, up_bias, down, small, peaks)


def share_master_kernel(rows_ref, whole_ref, parts, send, recv):
    place = Place()
    greet(place, plane=True, pair=False)
    dp, mp, dpx, dpy, dpd = place.dp, place.mp, place.dpx, place.dpy, place.dpd
    half = GROUP_ROWS // 2
    part_a, part_b = pl.ds(0, half), pl.ds(half, half)
    parts[dp] = rows_ref[...].astype(BF)

    def hop(index, block, target):
        return remote(block, block, send.at[index], recv.at[index], target, mp)

    own = parts.at[dp]
    sends = [hop(0, own, dpx), hop(1, own, dpy)]
    for copy in sends:
        copy.start()
    hop(0, parts.at[dpx], dpx).wait_recv()
    sends.append(hop(2, parts.at[dpx, part_a], dpy))
    sends[-1].start()
    hop(1, parts.at[dpy], dpy).wait_recv()
    sends.append(hop(3, parts.at[dpy, part_b], dpx))
    sends[-1].start()
    hop(2, parts.at[dpd, part_a], dpy).wait_recv()
    hop(3, parts.at[dpd, part_b], dpx).wait_recv()
    for group in range(4):
        base = group * GROUP_STEP
        first = parts[group, pl.ds(0, 32)].astype(F32)
        if group > 0:
            first = first + parts[group - 1, pl.ds(GROUP_STEP, 32)].astype(F32)
        whole_ref[pl.ds(base, 32)] = first
        for start in range(32, GROUP_STEP, 1192):
            whole_ref[pl.ds(base + start, 1192)] = parts[group, pl.ds(start, 1192)].astype(F32)
    whole_ref[pl.ds(4 * GROUP_STEP, 16)] = parts[3, pl.ds(GROUP_STEP, 16)].astype(F32)
    for copy in sends:
        copy.wait_send()


def share_master(rows):
    return pl.pallas_call(
        share_master_kernel,
        out_shape=jax.ShapeDtypeStruct((PACK_END, 128), F32),
        in_specs=[VMEM],
        out_specs=VMEM,
        scratch_shapes=[pltpu.VMEM((4, GROUP_ROWS, 128), BF), dma(4), dma(4)],
        compiler_params=params(8, 60),
        name="share_master",
    )(rows)


def fast_body(
    frames,
    lengths,
    key_mask,
    cotangent,
    gain_one,
    shift_one,
    query_weight,
    query_bias,
    key_weight,
    value_weight,
    value_bias,
    out_weight,
    out_bias,
    gain_two,
    shift_two,
    up_weight,
    up_bias,
    down_weight,
    down_bias,
    master,
    moment_one,
    moment_two,
    adam_step,
    hyper_rates,
):
    group = lax.axis_index("dp")
    position = jnp.arange(1024, dtype=jnp.int32)
    keep_query = position[None, :] < lengths[:, None]
    keep_key = jnp.logical_and(keep_query, key_mask == 1)
    mask = jnp.where(keep_key, 0.0, MASK_VALUE)[:, :, None]
    live = keep_query.astype(F32)[:, None, :]
    gain_first = gain_one.astype(F32)
    shift_first = shift_one.astype(F32)
    gain_second = gain_two.astype(F32)
    shift_second = shift_two.astype(F32)
    inputs = frames.transpose(1, 0, 2).reshape(ROWS, 1280).astype(F32)
    upstream_low = cotangent.transpose(1, 0, 2).reshape(ROWS, 1280)
    upstream = upstream_low.astype(F32)
    normed = layer_norm(inputs, gain_first, shift_first).astype(BF)

    def head_rows(weight):
        rows = weight.T.reshape(2, HD, 1280)
        return jnp.pad(rows, ((0, 0), (0, 128 - HD), (0, 0))).reshape(256, 1280)

    def head_lanes(bias):
        lanes = bias.astype(F32).reshape(2, HD)
        return jnp.pad(lanes, ((0, 0), (0, 128 - HD))).reshape(256)

    joined_weight = jnp.concatenate(
        [head_rows(query_weight), head_rows(key_weight), head_rows(value_weight)]
    )
    joined_bias = jnp.concatenate(
        [head_lanes(query_bias), jnp.zeros((256,), F32), head_lanes(value_bias)]
    )[None]
    normed_full, qkv, upstream_full = project(normed, upstream_low, joined_weight, joined_bias)
    qkv = qkv.reshape(8, 3, 128, 768)

    quarter = group * 160
    up_share = lax.dynamic_slice_in_dim(up_weight, quarter, 160, 1).T
    down_share = lax.dynamic_slice_in_dim(down_weight, quarter, 160, 0)
    bias_share = lax.dynamic_slice_in_dim(up_bias, quarter, 160, 0)
    bias_rows = jnp.pad(bias_share[None], ((0, 15), (0, 1280 - 160)))
    message = jnp.concatenate([up_share, down_share, bias_rows, out_weight])
    attended, logs, peaks, gathered = attend(qkv, mask, live, message)
    core = lax.axis_index("mp") % 2
    own_core = lax.dynamic_slice_in_dim(gathered.reshape(4, 2, 496, 1280), core, 1, 1)[:, 0]
    up_rows = own_core[:, :160].reshape(640, 1280)
    down_rows = own_core[:, 160:320].reshape(640, 1280)
    up_lanes = own_core[:, 320, :160].reshape(640).astype(F32)
    out_rows = gathered[:, 336:]

    branch = jnp.einsum("schr,shd->crd", attended, out_rows, preferred_element_type=F32)
    middle = inputs + branch.reshape(ROWS, 1280) + out_bias.astype(F32)
    normed_two = layer_norm(middle, gain_second, shift_second).astype(BF)
    normed_two_full = plane_share(normed_two)
    before = (
        jnp.einsum("prd,ud->pru", normed_two_full, up_rows, preferred_element_type=F32)
        + up_lanes
    )
    hidden = exact_gelu(before).astype(BF)
    hidden_grad = jnp.einsum("prd,ud->pru", upstream_full, down_rows, preferred_element_type=F32)
    _, gelu_pull = jax.vjp(exact_gelu, before)
    before_grad = gelu_pull(hidden_grad)[0].astype(BF)
    feed_part = jnp.einsum("pru,ud->prd", hidden, down_rows, preferred_element_type=F32).astype(BF)
    normed_part = jnp.einsum(
        "pru,ud->prd", before_grad, up_rows, preferred_element_type=F32
    ).astype(BF)
    normed_two_grad, feed = plane_sums(normed_part, feed_part)
    layer_out = (middle + feed + down_bias.astype(F32)).astype(BF)
    up_grad = jnp.einsum("pru,prd->ud", before_grad, normed_two_full, preferred_element_type=F32)
    down_grad = jnp.einsum("pru,prd->ud", hidden, upstream_full, preferred_element_type=F32)
    up_bias_grad = jnp.sum(before_grad.astype(F32), axis=(0, 1))

    _, norm_two_pull = jax.vjp(layer_norm, middle, gain_second, shift_second)
    middle_norm_grad, gain_two_grad, shift_two_grad = norm_two_pull(normed_two_grad)
    middle_grad = upstream + middle_norm_grad
    branch_grad = middle_grad.astype(BF)
    branch_clips = branch_grad.reshape(3, 128, 1280)
    out_grad = jnp.einsum("schr,crd->shd", attended, branch_clips, preferred_element_type=F32)
    attended_grad = jnp.einsum(
        "shd,crd->schr", out_rows, branch_clips, preferred_element_type=F32
    ).astype(BF)
    joined_grad = attend_back(qkv, mask, logs, attended_grad).reshape(8, ROWS, 768)
    normed_grad = line_product(joined_grad, joined_weight)
    joined_weight_grad = jnp.einsum(
        "prd,pre->de", normed_full, joined_grad, preferred_element_type=F32
    )
    joined_bias_grad = jnp.sum(joined_grad.astype(F32), axis=(0, 1))

    _, norm_one_pull = jax.vjp(layer_norm, inputs, gain_first, shift_first)
    input_norm_grad, gain_one_grad, shift_one_grad = norm_one_pull(normed_grad)
    input_grad = middle_grad + input_norm_grad

    feed_grads = jnp.concatenate(
        [
            up_grad.astype(BF).reshape(4, 160, 1280),
            down_grad.astype(BF).reshape(4, 160, 1280),
            jnp.pad(up_bias_grad.astype(BF).reshape(4, 1, 160), ((0, 0), (0, 15), (0, 1120))),
        ],
        axis=1,
    )
    feed_sum, out_sum = line_sums(feed_grads, out_grad.astype(BF))

    def spread(rows):
        return lax.dynamic_update_slice(
            jnp.zeros((640,) + rows.shape[1:], F32), rows, (quarter,) + (0,) * (rows.ndim - 1)
        )

    up_whole = spread(feed_sum[:160]).T
    down_whole = spread(feed_sum[160:320])
    up_bias_whole = spread(feed_sum[320, :160])

    out_bias_grad = jnp.sum(branch_grad.astype(F32), axis=0)
    down_bias_grad = jnp.sum(upstream, axis=0)
    small_terms = jnp.concatenate(
        [
            gain_one_grad,
            shift_one_grad,
            out_bias_grad,
            gain_two_grad,
            shift_two_grad,
            down_bias_grad,
        ]
    )
    small_tiles = jnp.pad(small_terms.reshape(8, 960), ((0, 0), (0, 64))).reshape(8, 8, 128)
    grad_rows, small_sum, peak_sum = pack_reduce(
        joined_weight_grad,
        joined_bias_grad[None],
        out_sum,
        up_whole,
        up_bias_whole.reshape(5, 128),
        down_whole,
        small_tiles,
        peaks,
    )
    small_total = small_sum.reshape(1024)[:960]
    head_peak = jnp.max(peak_sum, axis=(1, 2)) / math.sqrt(HD)
    share_size = master.shape[1]
    owned_grads = lax.dynamic_slice(
        grad_rows.reshape(1, GROUP_ROWS * 128), (0, 480 * group), (1, share_size)
    )
    learn_rate = hyper_rates[0]
    weight_decay = hyper_rates[1]
    logit_cap = hyper_rates[2]
    step_count = adam_step[0].astype(F32)
    first_new = BETA_FIRST * moment_one + (1.0 - BETA_FIRST) * owned_grads
    second_new = BETA_SECOND * moment_two + (1.0 - BETA_SECOND) * owned_grads * owned_grads
    first_hat = first_new / (1.0 - jnp.power(BETA_FIRST, step_count))
    second_hat = second_new / (1.0 - jnp.power(BETA_SECOND, step_count))
    entry_index = group * share_size + lax.broadcasted_iota(jnp.int32, (1, share_size), 1)
    query_end = 1280 * 160
    query_bias_end = query_end + 160
    key_end = query_bias_end + 1280 * 160
    column = jnp.where(
        entry_index < query_bias_end, entry_index, entry_index - query_bias_end
    ) % 160
    root_factor = jnp.sqrt(logit_cap / jnp.maximum(head_peak, logit_cap))
    head_factor = jnp.where(column < HD, root_factor[0], root_factor[1])
    factor = jnp.where(entry_index < key_end, head_factor, 1.0)
    master_new = (
        master
        - learn_rate * (first_hat / (jnp.sqrt(second_hat) + ADAM_EPSILON) + weight_decay * master)
    ) * factor

    def placed_rows(offset):
        room = GROUP_ROWS * 128 - share_size - offset
        return lambda value: jnp.pad(value, ((0, 0), (offset, room))).reshape(GROUP_ROWS, 128)

    master_rows = lax.switch(group, [placed_rows(480 * part) for part in range(4)], master_new)
    whole = share_master(master_rows).reshape(1, PACK_END * 128)
    whole = lax.optimization_barrier(whole)
    weights_new = whole[:, : 4 * share_size].astype(BF)
    return (
        layer_out.reshape(3, 128, 1280).transpose(1, 0, 2),
        input_grad.reshape(3, 128, 1280).transpose(1, 0, 2),
        owned_grads,
        master_new,
        first_new,
        second_new,
        weights_new,
        small_total,
    )


def body(
    frames,
    lengths,
    key_mask,
    cotangent,
    gain_one,
    shift_one,
    query_weight,
    query_bias,
    key_weight,
    value_weight,
    value_bias,
    out_weight,
    out_bias,
    gain_two,
    shift_two,
    up_weight,
    up_bias,
    down_weight,
    down_bias,
    master,
    moment_one,
    moment_two,
    adam_step,
    hyper_rates,
):
    local_rows, clip_count, model_width = frames.shape
    total_rows = key_mask.shape[1]
    head_cols = query_weight.shape[1]
    heads_here = head_cols // HD
    block_rows = min(512, total_rows)
    blocks = total_rows // block_rows
    score_scale = 1.0 / math.sqrt(HD)
    position = jnp.arange(total_rows, dtype=jnp.int32)
    keep_query = position[None, :] < lengths[:, None]
    keep_key = jnp.logical_and(keep_query, key_mask == 1)
    gain_first = gain_one.astype(jnp.float32)
    shift_first = shift_one.astype(jnp.float32)
    gain_second = gain_two.astype(jnp.float32)
    shift_second = shift_two.astype(jnp.float32)
    inputs = frames.astype(jnp.float32)
    normed = layer_norm(inputs, gain_first, shift_first).astype(jnp.bfloat16)
    joined_weight = jnp.concatenate([query_weight, key_weight, value_weight], axis=1)
    joined_bias = jnp.concatenate(
        [
            query_bias.astype(jnp.float32),
            jnp.zeros((head_cols,), jnp.float32),
            value_bias.astype(jnp.float32),
        ]
    )
    normed_full = lax.all_gather(normed, "mp", axis=0, tiled=True)
    projected = (
        jnp.einsum("rcd,de->rce", normed_full, joined_weight, preferred_element_type=jnp.float32)
        + joined_bias
    ).astype(jnp.bfloat16)
    query = projected[:, :, :head_cols].reshape(total_rows, clip_count, heads_here, HD)
    keys = projected[:, :, head_cols : 2 * head_cols].reshape(
        total_rows, clip_count, heads_here, HD
    )
    values = projected[:, :, 2 * head_cols :].reshape(total_rows, clip_count, heads_here, HD)

    def scores_of(row_start):
        query_block = lax.dynamic_slice_in_dim(query, row_start, block_rows, 0)
        raw_scores = (
            jnp.einsum("qchd,kchd->chqk", query_block, keys, preferred_element_type=jnp.float32)
            * score_scale
        )
        return (query_block, jnp.where(keep_key[:, None, None, :], raw_scores, MASK_VALUE))

    def forward_block(block_index):
        row_start = block_index * block_rows
        _, masked = scores_of(row_start)
        row_peak = jnp.max(masked, axis=-1, keepdims=True)
        exp_scores = jnp.exp(masked - row_peak)
        row_total = jnp.sum(exp_scores, axis=-1, keepdims=True)
        probability = (exp_scores / row_total).astype(jnp.bfloat16)
        attended = jnp.einsum(
            "chqk,kchd->qchd", probability, values, preferred_element_type=jnp.float32
        ).astype(jnp.bfloat16)
        live_rows = lax.dynamic_slice_in_dim(keep_query, row_start, block_rows, 1)
        block_peak = jnp.max(
            jnp.where(live_rows[:, None, :], row_peak[..., 0], MASK_VALUE), axis=(0, 2)
        )
        return (attended, (row_peak + jnp.log(row_total))[..., 0], block_peak)

    attended_blocks, log_totals, block_peaks = lax.map(forward_block, jnp.arange(blocks))
    attended_full = attended_blocks.reshape(total_rows, clip_count, head_cols)
    head_peak = lax.pmax(jnp.max(block_peaks, axis=0), "dp")
    rows_here = attended_full
    attn_branch = lax.psum_scatter(
        jnp.einsum("rck,kd->rcd", rows_here, out_weight, preferred_element_type=jnp.float32),
        "mp",
        scatter_dimension=0,
        tiled=True,
    ) + out_bias.astype(jnp.float32)
    middle = inputs + attn_branch
    normed_two = layer_norm(middle, gain_second, shift_second).astype(jnp.bfloat16)
    upstream = cotangent.astype(jnp.float32)
    normed_two_full = lax.all_gather(normed_two, "mp", axis=0, tiled=True)
    before = jnp.einsum(
        "rcd,df->rcf", normed_two_full, up_weight, preferred_element_type=jnp.float32
    ) + up_bias.astype(jnp.float32)
    hidden = exact_gelu(before).astype(jnp.bfloat16)
    rows_here = hidden
    feed = lax.psum_scatter(
        jnp.einsum(
            "rcf,fd->rcd", rows_here, down_weight, preferred_element_type=jnp.float32
        ).astype(jnp.bfloat16),
        "mp",
        scatter_dimension=0,
        tiled=True,
    ).astype(jnp.float32) + down_bias.astype(jnp.float32)
    layer_out = (middle + feed).astype(jnp.bfloat16)
    feed_grad_full = lax.all_gather(cotangent, "mp", axis=0, tiled=True)
    down_grad = jnp.einsum(
        "rcf,rcd->fd", hidden, feed_grad_full, preferred_element_type=jnp.float32
    )
    hidden_grad = jnp.einsum(
        "rcd,fd->rcf", feed_grad_full, down_weight, preferred_element_type=jnp.float32
    )
    _, gelu_pull = jax.vjp(exact_gelu, before)
    before_grad = gelu_pull(hidden_grad)[0].astype(jnp.bfloat16)
    up_bias_grad = jnp.sum(before_grad.astype(jnp.float32), axis=(0, 1))
    up_grad = jnp.einsum(
        "rcd,rcf->df", normed_two_full, before_grad, preferred_element_type=jnp.float32
    )
    rows_here = before_grad
    normed_two_grad = lax.psum_scatter(
        jnp.einsum("rcf,df->rcd", rows_here, up_weight, preferred_element_type=jnp.float32),
        "mp",
        scatter_dimension=0,
        tiled=True,
    )
    _, norm_two_pull = jax.vjp(layer_norm, middle, gain_second, shift_second)
    middle_norm_grad, gain_two_grad, shift_two_grad = norm_two_pull(normed_two_grad)
    middle_grad = upstream + middle_norm_grad
    branch_grad = middle_grad.astype(jnp.bfloat16)
    branch_grad_full = lax.all_gather(branch_grad, "mp", axis=0, tiled=True)
    out_grad = jnp.einsum(
        "rck,rcd->kd", attended_full, branch_grad_full, preferred_element_type=jnp.float32
    )
    attended_grad = jnp.einsum(
        "rcd,kd->rck", branch_grad_full, out_weight, preferred_element_type=jnp.float32
    ).astype(jnp.bfloat16)
    attended_grad = attended_grad.reshape(total_rows, clip_count, heads_here, HD)

    def backward_block(carry, block_index):
        key_total, value_total = carry
        row_start = block_index * block_rows
        query_block, masked = scores_of(row_start)
        log_total = log_totals[block_index]
        probability = jnp.exp(masked - log_total[..., None])
        grad_block = lax.dynamic_slice_in_dim(attended_grad, row_start, block_rows, 0)
        value_total = value_total + jnp.einsum(
            "chqk,qchd->kchd",
            probability.astype(jnp.bfloat16),
            grad_block,
            preferred_element_type=jnp.float32,
        )
        prob_grad = jnp.einsum(
            "qchd,kchd->chqk", grad_block, values, preferred_element_type=jnp.float32
        )
        score_grad = (
            probability * (prob_grad - jnp.sum(probability * prob_grad, axis=-1, keepdims=True))
        ).astype(jnp.bfloat16)
        query_grad = (
            jnp.einsum("chqk,kchd->qchd", score_grad, keys, preferred_element_type=jnp.float32)
            * score_scale
        ).astype(jnp.bfloat16)
        key_total = (
            key_total
            + jnp.einsum(
                "chqk,qchd->kchd", score_grad, query_block, preferred_element_type=jnp.float32
            )
            * score_scale
        )
        return ((key_total, value_total), query_grad)

    empty_grad = jnp.zeros((total_rows, clip_count, heads_here, HD), jnp.float32)
    (key_total, value_total), query_blocks = lax.scan(
        backward_block, (empty_grad, empty_grad), jnp.arange(blocks)
    )
    joined_grad = jnp.concatenate(
        [
            query_blocks.reshape(total_rows, clip_count, head_cols),
            key_total.reshape(total_rows, clip_count, head_cols).astype(jnp.bfloat16),
            value_total.reshape(total_rows, clip_count, head_cols).astype(jnp.bfloat16),
        ],
        axis=-1,
    )
    joined_bias_grad = jnp.sum(joined_grad.astype(jnp.float32), axis=(0, 1))
    normed_back = lax.all_gather(normed, "mp", axis=0, tiled=True)
    joined_weight_grad = jnp.einsum(
        "rcd,rce->de", normed_back, joined_grad, preferred_element_type=jnp.float32
    )
    rows_here = joined_grad
    normed_grad = lax.psum_scatter(
        jnp.einsum(
            "rce,de->rcd", rows_here, joined_weight, preferred_element_type=jnp.float32
        ).astype(jnp.bfloat16),
        "mp",
        scatter_dimension=0,
        tiled=True,
    ).astype(jnp.float32)
    _, norm_one_pull = jax.vjp(layer_norm, inputs, gain_first, shift_first)
    input_norm_grad, gain_one_grad, shift_one_grad = norm_one_pull(normed_grad)
    input_grad = middle_grad + input_norm_grad
    out_bias_grad = jnp.sum(branch_grad.astype(jnp.float32), axis=(0, 1))
    down_bias_grad = jnp.sum(upstream, axis=(0, 1))
    small_terms = jnp.concatenate(
        [
            gain_one_grad,
            shift_one_grad,
            out_bias_grad,
            gain_two_grad,
            shift_two_grad,
            down_bias_grad,
        ]
    )
    small_share = lax.psum_scatter(small_terms, "mp", scatter_dimension=0, tiled=True)
    small_total = lax.psum(small_share, "dp")
    packed = jnp.concatenate(
        [
            joined_weight_grad[:, :head_cols].reshape(-1),
            joined_bias_grad[:head_cols],
            joined_weight_grad[:, head_cols : 2 * head_cols].reshape(-1),
            joined_weight_grad[:, 2 * head_cols :].reshape(-1),
            joined_bias_grad[2 * head_cols :],
            out_grad.reshape(-1),
            up_grad.reshape(-1),
            up_bias_grad,
            down_grad.reshape(-1),
            small_share,
        ]
    )
    owned_grads = lax.psum_scatter(
        packed.astype(jnp.bfloat16), "dp", scatter_dimension=0, tiled=True
    ).astype(jnp.float32)
    share_size = owned_grads.shape[0]
    learn_rate = hyper_rates[0]
    weight_decay = hyper_rates[1]
    logit_cap = hyper_rates[2]
    step_count = adam_step[0].astype(jnp.float32)
    first_new = BETA_FIRST * moment_one[0] + (1.0 - BETA_FIRST) * owned_grads
    second_new = BETA_SECOND * moment_two[0] + (1.0 - BETA_SECOND) * owned_grads * owned_grads
    first_hat = first_new / (1.0 - jnp.power(BETA_FIRST, step_count))
    second_hat = second_new / (1.0 - jnp.power(BETA_SECOND, step_count))
    entry_index = lax.axis_index("dp") * share_size + jnp.arange(share_size, dtype=jnp.int32)
    query_end = model_width * head_cols
    query_bias_end = query_end + head_cols
    key_end = query_bias_end + model_width * head_cols
    column = jnp.where(
        entry_index < query_end,
        entry_index % head_cols,
        jnp.where(
            entry_index < query_bias_end,
            entry_index - query_end,
            (entry_index - query_bias_end) % head_cols,
        ),
    )
    head_index = column // HD
    root_factor = jnp.sqrt(logit_cap / jnp.maximum(head_peak, logit_cap))
    head_factor = jnp.zeros((share_size,), jnp.float32)
    for head_number in range(heads_here):
        head_factor = head_factor + jnp.where(
            head_index == head_number, root_factor[head_number], 0.0
        )
    factor = jnp.where(entry_index < key_end, head_factor, 1.0)
    master_here = master[0]
    master_new = (
        master_here
        - learn_rate
        * (first_hat / (jnp.sqrt(second_hat) + ADAM_EPSILON) + weight_decay * master_here)
    ) * factor
    weights_full = lax.all_gather(master_new.astype(jnp.bfloat16), "dp", axis=0, tiled=True)
    return (
        layer_out,
        input_grad,
        owned_grads[None],
        master_new[None],
        first_new[None],
        second_new[None],
        weights_full[None],
        small_total,
    )


def solution(mesh):
    chosen = fast_body if dict(mesh.shape) == {"dp": 4, "mp": 8} else body
    placed = (
        P("mp", "dp", None),
        P("dp"),
        P("dp", None),
        P("mp", "dp", None),
        P(),
        P(),
        P(None, "mp"),
        P("mp"),
        P(None, "mp"),
        P(None, "mp"),
        P("mp"),
        P("mp", None),
        P(),
        P(),
        P(),
        P(None, "mp"),
        P("mp"),
        P("mp", None),
        P(),
        P("mp", "dp"),
        P("mp", "dp"),
        P("mp", "dp"),
        P(),
        P(),
    )
    return jax.shard_map(
        chosen,
        mesh=mesh,
        in_specs=placed,
        out_specs=(
            P("mp", "dp", None),
            P("mp", "dp", None),
            P("mp", "dp"),
            P("mp", "dp"),
            P("mp", "dp"),
            P("mp", "dp"),
            P("mp", None),
            P("mp"),
        ),
        check_vma=False,
    )
```

```python
import functools
import math

import jax
import jax.numpy as jnp
from jax import lax
from jax.experimental import pallas as pl
from jax.experimental.pallas import tpu as pltpu
from jax.sharding import PartitionSpec as P

HD = 80


NORM_EPSILON = 1e-05
ADAM_EPSILON = 1e-08
BETA_FIRST = 0.9
BETA_SECOND = 0.999
MASK_VALUE = -1e30


def layer_norm(value, gain, shift):
    center = value - jnp.mean(value, axis=-1, keepdims=True)
    spread = jnp.mean(center * center, axis=-1, keepdims=True)
    return center * lax.rsqrt(spread + NORM_EPSILON) * gain + shift


def exact_gelu(argument):
    return jax.nn.gelu(argument, approximate=False)


MESH = pl.DeviceIdType.MESH
ANY = pl.BlockSpec(memory_space=pl.ANY)
VMEM = pl.BlockSpec(memory_space=pltpu.VMEM)
LINE = 4
ROWS = 384
BF = jnp.bfloat16
F32 = jnp.float32


class Place:
    def __init__(self):
        self.dp = lax.axis_index("dp")
        self.mp = lax.axis_index("mp")
        self.z = self.mp // 2
        self.c = self.mp % 2
        self.pair = self.z * 2 + 1 - self.c
        self.dpx = self.dp + 1 - 2 * (self.dp % 2)
        self.dpy = (self.dp + 2) % 4
        self.dpd = 3 - self.dp

    def zorder(self, event):
        if event == 0:
            return self.z
        if event == 1:
            return self.z + 1 - 2 * (self.z % 2)
        if event == 2:
            return 2 - self.z // 2
        return 3 - 3 * (self.z // 2)


def greet(place, mp_all=False, line=False, plane=False, pair=True):
    barrier = pltpu.get_barrier_semaphore()
    count = 0

    def signal(dp, mp):
        pl.semaphore_signal(barrier, inc=1, device_id=(dp, mp), device_id_type=MESH)

    if mp_all:
        for hop in range(1, 8):
            signal(place.dp, (place.mp + hop) % 8)
        count += 7
    else:
        if pair:
            signal(place.dp, place.pair)
            count += 1
        if line:

            @pl.when(place.z > 0)
            def _():
                signal(place.dp, place.mp - 2)

            @pl.when(place.z < LINE - 1)
            def _():
                signal(place.dp, place.mp + 2)

    if plane:
        for other in (place.dpx, place.dpy, place.dpd):
            signal(other, place.mp)
        count += 3
    if line and not mp_all:
        pl.semaphore_wait(barrier, count + 1 + (place.z + 1) // 2 % 2)
    else:
        pl.semaphore_wait(barrier, count)


def remote(src, dst, send, recv, dp, mp):
    return pltpu.make_async_remote_copy(
        src_ref=src,
        dst_ref=dst,
        send_sem=send,
        recv_sem=recv,
        device_id=(dp, mp),
        device_id_type=MESH,
    )


def line_gather(place, src, out, local, send, recv, paired, ready=None):
    dp, z, c, mp, pair = place.dp, place.z, place.c, place.mp, place.pair

    def slot_of(level, core):
        return level * 2 + core if paired else level

    def hop(event, slot, source, direction, target):
        return remote(source, out.at[slot], send.at[event, direction], recv.at[slot], dp, target)

    own = slot_of(z, c)
    keep = pltpu.make_async_copy(src, out.at[own], local)
    keep.start()

    def ways(event, level, slot, source, act):
        up = z < LINE - 1
        down = z > 0
        if event > 0:
            up = jnp.logical_and(up, level < z)
            down = jnp.logical_and(down, level > z)

        @pl.when(up)
        def _():
            act(hop(event, slot, source, 1, mp + 2))

        @pl.when(down)
        def _():
            act(hop(event, slot, source, 2, mp - 2))

        if paired:
            act(hop(event, slot, source, 0, pair))

    ways(0, z, own, src, lambda copy: copy.start())
    yield
    if ready is not None:
        keep.wait()
        ready(own)
        if paired:
            other = slot_of(z, 1 - c)
            hop(0, other, out.at[other], 0, pair).wait_recv()
            ready(other)

    def settle(event):
        level = place.zorder(event)
        ready(slot_of(level, c))
        if paired:
            other = slot_of(level, 1 - c)
            hop(event, other, out.at[other], 0, pair).wait_recv()
            ready(other)

    for event in range(1, LINE):
        level = place.zorder(event)
        slot = slot_of(level, c)
        hop(event, slot, out.at[slot], 0, pair).wait_recv()
        ways(event, level, slot, out.at[slot], lambda copy: copy.start())
        if ready is not None and event > 1:
            if event == 2:
                settle(1)
            settle(event)
        yield
    if ready is None:
        if paired:
            for level in range(LINE):
                other = slot_of(level, 1 - c)
                hop(0, other, out.at[other], 0, pair).wait_recv()
        keep.wait()
    for event in range(LINE):
        level = place.zorder(event)
        slot = slot_of(level, c)
        ways(event, level, slot, out.at[slot], lambda copy: copy.wait_send())
    yield


def plane_gather(place, src, out, local, send, recv, ready=None):
    dp, c, mp, pair = place.dp, place.c, place.mp, place.pair
    dpx, dpy, dpd = place.dpx, place.dpy, place.dpd
    half = src.shape[0] // 2
    part_a, part_b = pl.ds(0, half), pl.ds(half, half)

    def at(group, core):
        return out.at[group * 2 + core]

    def hop(index, block, group, target):
        return remote(block, block, send.at[index], recv.at[index], group, target)

    def done(group, core):
        if ready is not None:
            ready(group * 2 + core)

    keep = pltpu.make_async_copy(src, at(dp, c), local)
    keep.start()
    here = at(dp, c)
    from_x, from_y, from_d = at(dpx, c), at(dpy, c), at(dpd, c)
    firsts = [
        remote(src, here, send.at[0], recv.at[0], dp, pair),
        remote(src, here, send.at[1], recv.at[1], dpx, mp),
        remote(src, here, send.at[2], recv.at[2], dpy, mp),
    ]
    seconds = [
        hop(3, from_x.at[part_a], dpy, mp),
        hop(4, from_y.at[part_b], dpx, mp),
        hop(5, from_x, dp, pair),
        hop(6, from_y, dp, pair),
        hop(7, from_d.at[part_a], dp, pair),
        hop(8, from_d.at[part_b], dp, pair),
    ]
    for copy in firsts:
        copy.start()
    yield
    if ready is not None:
        keep.wait()
        done(dp, c)
        hop(0, at(dp, 1 - c), dp, pair).wait_recv()
        done(dp, 1 - c)
    hop(1, from_x, dpx, mp).wait_recv()
    seconds[0].start()
    hop(2, from_y, dpy, mp).wait_recv()
    seconds[1].start()
    seconds[2].start()
    seconds[3].start()
    done(dpx, c)
    hop(5, at(dpx, 1 - c), dp, pair).wait_recv()
    done(dpx, 1 - c)
    yield
    done(dpy, c)
    hop(6, at(dpy, 1 - c), dp, pair).wait_recv()
    done(dpy, 1 - c)
    yield
    hop(3, from_d.at[part_a], dpy, mp).wait_recv()
    seconds[4].start()
    hop(4, from_d.at[part_b], dpx, mp).wait_recv()
    seconds[5].start()
    done(dpd, c)
    other = at(dpd, 1 - c)
    hop(7, other.at[part_a], dp, pair).wait_recv()
    hop(8, other.at[part_b], dp, pair).wait_recv()
    done(dpd, 1 - c)
    yield
    if ready is None:
        hop(0, at(dp, 1 - c), dp, pair).wait_recv()
        keep.wait()
    for copy in firsts + seconds:
        copy.wait_send()
    yield


def drive(*programs):
    live = list(programs)
    while live:
        for program in list(live):
            try:
                next(program)
            except StopIteration:
                live.remove(program)


def dma(*shape):
    return pltpu.SemaphoreType.DMA(shape)


def params(cid, vmem=40):
    return pltpu.CompilerParams(
        collective_id=cid, has_side_effects=True, vmem_limit_bytes=vmem << 20
    )


def exchange(place, src, out, local, send, recv):
    dp, mp = place.dp, place.mp
    keep = pltpu.make_async_copy(src.at[mp], out.at[mp], local)
    keep.start()
    sends = []
    for hop in range(1, 8):
        target = (mp + hop) % 8
        sends.append(
            remote(src.at[target], out.at[mp], send.at[hop], recv.at[hop], dp, target)
        )
        sends[-1].start()
    yield
    keep.wait()
    for hop in range(1, 8):
        origin = (mp + 8 - hop) % 8
        remote(out.at[origin], out.at[origin], send.at[hop], recv.at[hop], dp, origin).wait_recv()
    for copy in sends:
        copy.wait_send()
    yield


def line_reduce(place, produce, tiles, result, bufs, sems, paired):
    dp, z, c, mp, pair = place.dp, place.z, place.c, place.mp, place.pair
    from_above, from_below, out_block = bufs["above"], bufs["below"], bufs["out"]
    order = [place.zorder(event) for event in (3, 2, 1, 0)]

    @pl.when(z == LINE - 1)
    def _():
        from_above[...] = jnp.zeros(from_above.shape, BF)

    @pl.when(z == 0)
    def _():
        from_below[...] = jnp.zeros(from_below.shape, BF)

    def across(step, level):
        return remote(
            bufs["pair_out"].at[step],
            bufs["pair_in"].at[level],
            sems["pair_send"].at[step],
            sems["pair_recv"].at[level],
            dp,
            pair,
        )

    if paired:
        for step, level in enumerate(order):
            for rows in tiles:
                bufs["pair_out"][step, rows] = produce(level, 1 - c, rows).astype(BF)
            across(step, level).start()
    yield

    def toward(step, level, act):
        @pl.when(level < z)
        def _():
            act(
                remote(
                    out_block.at[step],
                    from_above.at[level],
                    sems["line_send"].at[step],
                    sems["above"].at[level],
                    dp,
                    mp - 2,
                )
            )

        @pl.when(level > z)
        def _():
            act(
                remote(
                    out_block.at[step],
                    from_below.at[level],
                    sems["line_send"].at[step],
                    sems["below"].at[level],
                    dp,
                    mp + 2,
                )
            )

    def arrive(level, above):
        if above:
            remote(
                from_above.at[level],
                from_above.at[level],
                sems["line_send"].at[0],
                sems["above"].at[level],
                dp,
                mp,
            ).wait_recv()
        else:
            remote(
                from_below.at[level],
                from_below.at[level],
                sems["line_send"].at[0],
                sems["below"].at[level],
                dp,
                mp,
            ).wait_recv()

    for step, level in enumerate(order[:3]):
        if paired:
            across(step, level).wait_recv()

        @pl.when(jnp.logical_and(level < z, z < LINE - 1))
        def _():
            arrive(level, True)

        @pl.when(jnp.logical_and(level > z, z > 0))
        def _():
            arrive(level, False)

        for rows in tiles:
            total = produce(level, c, rows)
            if paired:
                total = total + bufs["pair_in"][level, rows].astype(F32)

            @pl.when(level < z)
            def _():
                out_block[step, rows] = (total + from_above[level, rows].astype(F32)).astype(BF)

            @pl.when(level > z)
            def _():
                out_block[step, rows] = (total + from_below[level, rows].astype(F32)).astype(BF)

        toward(step, level, lambda copy: copy.start())
        yield

    if paired:
        across(3, z).wait_recv()

    @pl.when(z < LINE - 1)
    def _():
        arrive(z, True)

    @pl.when(z > 0)
    def _():
        arrive(z, False)

    for rows in tiles:
        total = produce(z, c, rows)
        if paired:
            total = total + bufs["pair_in"][z, rows].astype(F32)
        total = total + from_above[z, rows].astype(F32) + from_below[z, rows].astype(F32)
        result(rows, total)
    for step, level in enumerate(order):
        if paired:
            across(step, level).wait_send()
        if step < 3:
            toward(step, level, lambda copy: copy.wait_send())
    yield


def line_reduce_scratch(rows, cols, paired):
    block = lambda n: pltpu.VMEM((n, rows, cols), BF)
    scratch = {"above": block(4), "below": block(4), "out": block(3)}
    sems = {"line_send": dma(3), "above": dma(4), "below": dma(4)}
    if paired:
        scratch.update({"pair_out": block(4), "pair_in": block(4)})
        sems.update({"pair_send": dma(4), "pair_recv": dma(4)})
    return scratch, sems


def plane_reduce(place, produce, tile, half, result, bufs, sems, paired=True, early=False):
    dp, c, mp, pair = place.dp, place.c, place.mp, place.pair
    dpx, dpy, dpd = place.dpx, place.dpy, place.dpd
    starts = range(0, half, tile)
    send, recv = sems["send"], sems["recv"]
    out_block, landed = bufs["out"], bufs["in"]
    groups = {"far": dpd, "x": dpx, "y": dpy, "own": dp}
    steps = ["x", "y", "far", "own"] if early else ["far", "x", "y", "own"]

    def across(name):
        step = steps.index(name)
        return remote(
            bufs["pair_out"].at[step % 2],
            bufs["pair_in"].at[step],
            sems["pair_send"].at[step % 2],
            sems["pair_recv"].at[step],
            dp,
            pair,
        )

    def cross(name):
        if not paired:
            return
        step = steps.index(name)
        if step > 1:
            across(steps[step - 2]).wait_send()
        for start in range(0, 2 * half, tile):
            bufs["pair_out"][step % 2, pl.ds(start, tile)] = produce(
                groups[name], 1 - c, start
            ).astype(BF)
        across(name).start()

    def crossed(name):
        if paired:
            across(name).wait_recv()

    def share(name, start):
        total = produce(groups[name], c, start)
        if paired:
            total = total + bufs["pair_in"][steps.index(name), pl.ds(start, tile)].astype(F32)
        return total

    def hop(index):
        target = (dpx, dpy, dpx, dpx, dpy, dpy)[index]
        return remote(
            out_block.at[index], landed.at[index], send.at[index], recv.at[index], target, mp
        )

    def fill(index, name, base, extra=None):
        for start in starts:
            total = share(name, base + start)
            if extra is not None:
                total = total + landed[extra, pl.ds(start, tile)].astype(F32)
            out_block[index, pl.ds(start, tile)] = total.astype(BF)
        hop(index).start()

    def far():
        crossed("far")
        fill(0, "far", 0)
        fill(1, "far", half)

    def near():
        crossed("x")
        fill(2, "x", 0)
        crossed("y")
        fill(4, "y", half)

    if early:
        cross("x")
        yield
        cross("y")
        near()
        yield
        cross("far")
        far()
        cross("own")
    else:
        cross("far")
        cross("x")
        yield
        far()
        cross("y")
        near()
        cross("own")
    yield
    hop(1).wait_recv()
    fill(3, "x", half, extra=1)
    hop(0).wait_recv()
    fill(5, "y", 0, extra=0)
    yield
    crossed("own")
    for index in (2, 3, 4, 5):
        hop(index).wait_recv()
    for base, pieces in ((0, (2, 5)), (half, (3, 4))):
        for start in starts:
            total = share("own", base + start)
            for piece in pieces:
                total = total + landed[piece, pl.ds(start, tile)].astype(F32)
            result(pl.ds(base + start, tile), total)
    for index in range(6):
        hop(index).wait_send()
    if paired:
        for name in steps[2:]:
            across(name).wait_send()
    yield


def plane_reduce_scratch(half, cols, paired=True):
    block = lambda n, rows: pltpu.VMEM((n, rows, cols), BF)
    scratch = {"out": block(6, half), "in": block(6, half)}
    sems = {"send": dma(6), "recv": dma(6)}
    if paired:
        scratch.update({"pair_out": block(2, 2 * half), "pair_in": block(4, 2 * half)})
        sems.update({"pair_send": dma(2), "pair_recv": dma(4)})
    return scratch, sems


def project_kernel(
    normed_ref, cot_ref, weight_ref, bias_ref, nfull_ref, qkv_ref, cfull_ref,
    local, line_send, line_recv, plane_send, plane_recv,
):
    place = Place()
    greet(place, line=True, plane=True)

    def ready(slot):
        @pl.loop(0, 3)
        def _(step):
            rows = pl.ds(step * 128, 128)
            product = lax.dot_general(
                nfull_ref[slot, rows],
                weight_ref[...],
                (((1,), (1,)), ((), ())),
                preferred_element_type=F32,
            )
            qkv_ref[slot, rows] = (product + bias_ref[...]).astype(BF)

    drive(
        line_gather(
            place, normed_ref, nfull_ref, local.at[0], line_send, line_recv, True, ready
        ),
        plane_gather(place, cot_ref, cfull_ref, local.at[1], plane_send, plane_recv),
    )


def project(normed, cotangent, weight, bias):
    return pl.pallas_call(
        project_kernel,
        out_shape=(
            jax.ShapeDtypeStruct((8,) + normed.shape, BF),
            jax.ShapeDtypeStruct((8, ROWS, weight.shape[0]), BF),
            jax.ShapeDtypeStruct((8,) + cotangent.shape, BF),
        ),
        in_specs=[ANY, ANY, VMEM, VMEM],
        out_specs=(VMEM, VMEM, ANY),
        scratch_shapes=[dma(2), dma(4, 3), dma(8), dma(9), dma(9)],
        compiler_params=params(0),
        name="project",
    )(normed, cotangent, weight, bias)


def attend_kernel(
    qkv_ref, mask_ref, live_ref, weights_ref, att_ref, logs_ref, peak_ref, wfull_ref,
    out_ref, vt_ref, local, send, recv, line_send, line_recv,
):
    place = Place()
    greet(place, mp_all=True)
    gather = line_gather(
        place, weights_ref, wfull_ref, local.at[1], line_send, line_recv, True
    )
    next(gather)
    factor = math.log2(math.e) / math.sqrt(HD)
    peak_ref[...] = jnp.full(peak_ref.shape, MASK_VALUE, F32)

    @pl.loop(0, 6)
    def _(turn):
        clip = turn // 2
        head = turn % 2
        lane = pl.multiple_of(head * 128, 128)
        row = pl.multiple_of(head * HD, 16)
        keys = qkv_ref[:, clip, :, pl.ds(256 + lane, 128)].reshape(1024, 128)
        vt_ref[...] = qkv_ref[:, clip, :, pl.ds(512 + lane, 128)].reshape(1024, 128).T

        @pl.loop(0, 4)
        def _(block):
            query = qkv_ref[pl.ds(block * 2, 2), clip, :, pl.ds(lane, 128)].reshape(256, 128)
            columns = pl.ds(pl.multiple_of(block * 256, 256), 256)
            scores = lax.dot_general(
                keys, query, (((1,), (1,)), ((), ())), preferred_element_type=F32
            )
            scores = scores + mask_ref[clip]
            peak = jnp.max(scores, axis=0, keepdims=True)
            powers = jnp.exp2((scores - peak) * factor)
            total = jnp.sum(powers, axis=0, keepdims=True)
            mixed = lax.dot_general(
                vt_ref[...],
                powers.astype(BF),
                (((1,), (0,)), ((), ())),
                preferred_element_type=F32,
            )
            mixed = (mixed / total).astype(BF)
            for part in range(2):
                out_ref[block * 2 + part, clip, pl.ds(row, HD)] = mixed[
                    :HD, part * 128 : part * 128 + 128
                ]
            logs_ref[turn, :, columns] = peak * factor + jnp.log2(total)
            peak_ref[head] = jnp.maximum(
                peak_ref[head], jnp.where(live_ref[clip, :, columns] > 0, peak, MASK_VALUE)
            )

    drive(exchange(place, out_ref, att_ref, local.at[0], send, recv), gather)


def attend(qkv, mask, live, weights):
    return pl.pallas_call(
        attend_kernel,
        out_shape=(
            jax.ShapeDtypeStruct((8, 3, 160, 128), BF),
            jax.ShapeDtypeStruct((6, 1, 1024), F32),
            jax.ShapeDtypeStruct((2, 8, 256), F32),
            jax.ShapeDtypeStruct((8,) + weights.shape, BF),
        ),
        in_specs=[VMEM, VMEM, VMEM, ANY],
        out_specs=(VMEM, VMEM, VMEM, ANY),
        scratch_shapes=[
            pltpu.VMEM((8, 3, 160, 128), BF),
            pltpu.VMEM((128, 1024), BF),
            dma(2),
            dma(8),
            dma(8),
            dma(4, 3),
            dma(8),
        ],
        compiler_params=params(1),
        name="attend",
    )(qkv, mask, live, weights)


def flatten(*pairs):
    names, shapes = [], []
    for number, group in enumerate(pairs):
        for name, shape in group.items():
            names.append((number, name))
            shapes.append(shape)

    def split(refs):
        groups = [{} for _ in pairs]
        for (number, name), ref in zip(names, refs):
            groups[number][name] = ref
        return groups

    return shapes, split


def feed_forward_kernel(
    split, normed_ref, upstream_ref, up_ref, down_ref, bias_ref,
    total_ref, hidden_ref, grads_ref, bias_out,
    normed_all, upstream_all, slope_all, sum_ref, load, local, gather_send, gather_recv, *scratch,
):
    place = Place()
    bufs, sems = split(scratch)
    loads = []
    for slot in range(8):
        loads.append(
            pltpu.make_async_copy(upstream_ref.at[slot], upstream_all.at[slot], load.at[slot])
        )
        loads[-1].start()
    greet(place, plane=True)
    bias_out[...] = jnp.zeros(bias_out.shape, F32)

    def ready(slot):
        @pl.loop(0, 3)
        def _(step):
            rows = pl.ds(step * 128, 128)
            before = (
                lax.dot_general(
                    normed_all[slot, rows],
                    up_ref[...],
                    (((1,), (1,)), ((), ())),
                    preferred_element_type=F32,
                )
                + bias_ref[...]
            )
            pull = lax.dot_general(
                upstream_all[slot, rows],
                down_ref[...],
                (((1,), (1,)), ((), ())),
                preferred_element_type=F32,
            )
            share = 0.5 + 0.5 * lax.erf(before * math.sqrt(0.5))
            hidden_ref[slot, rows] = (before * share).astype(BF)
            density = jnp.exp(before * before * -0.5) * (1.0 / math.sqrt(2.0 * math.pi))
            slope = (pull * (share + before * density)).astype(BF)
            slope_all[slot, rows] = slope
            bias_out[...] += jnp.sum(slope.astype(F32), axis=0, keepdims=True)

    gather = plane_gather(
        place, normed_ref, normed_all, local, gather_send, gather_recv, ready
    )

    def produce(group, core, start):
        return jnp.dot(
            slope_all[group * 2 + core, pl.ds(start, 192)],
            up_ref[...],
            preferred_element_type=F32,
        )

    def result(rows, total):
        total_ref[rows] = total

    reduce = plane_reduce(place, produce, 192, 192, result, bufs, sems, True, True)
    next(gather)
    for copy in loads:
        copy.wait()
    next(gather)
    next(reduce)
    next(gather)
    next(reduce)
    next(gather)
    next(reduce)

    def weight_grads(left_all, right_all, base):
        for block in range(5):
            lanes = pl.ds(block * 128, 128)

            @pl.loop(0, 8)
            def _(slot):
                product = lax.dot_general(
                    left_all[slot, :, lanes],
                    right_all[slot],
                    (((0,), (0,)), ((), ())),
                    preferred_element_type=F32,
                )
                sum_ref[...] = jnp.where(slot == 0, product, sum_ref[...] + product)

            for part in range(4):
                unit = block * 128 + part * 32
                grads_ref[unit // 160, pl.ds(base + unit % 160, 32)] = sum_ref[
                    pl.ds(part * 32, 32)
                ].astype(BF)

    weight_grads(slope_all, normed_all, 0)
    next(reduce)
    weight_grads(hidden_ref, upstream_all, 160)
    for level in range(4):
        grads_ref[level, pl.ds(320, 16)] = jnp.zeros((16, 1280), BF)
        grads_ref[level, pl.ds(320, 16), pl.ds(0, 640)] = jnp.broadcast_to(
            bias_out[...], (16, 640)
        ).astype(BF)
    drive(reduce, gather)


def feed_forward(normed, upstream, up, down, bias):
    shapes, split = flatten(*plane_reduce_scratch(192, 1280))
    return pl.pallas_call(
        functools.partial(feed_forward_kernel, split),
        out_shape=(
            jax.ShapeDtypeStruct((ROWS, 1280), F32),
            jax.ShapeDtypeStruct((8, ROWS, 640), BF),
            jax.ShapeDtypeStruct((4, 336, 1280), BF),
            jax.ShapeDtypeStruct((1, 640), F32),
        ),
        in_specs=[ANY, ANY, VMEM, VMEM, VMEM],
        out_specs=(VMEM,) * 4,
        scratch_shapes=[
            pltpu.VMEM((8, ROWS, 1280), BF),
            pltpu.VMEM((8, ROWS, 1280), BF),
            pltpu.VMEM((8, ROWS, 640), BF),
            pltpu.VMEM((128, 1280), F32),
            dma(8),
            pltpu.SemaphoreType.DMA(()),
            dma(9),
            dma(9),
            *shapes,
        ],
        compiler_params=params(3, 60),
        name="feed_forward",
    )(normed, upstream, up, down, bias)


def attend_back_kernel(
    split, qkv_ref, mask_ref, logs_ref, pull_ref, hidden_ref, down_ref, feed_grads_ref,
    dqkv_ref, feed_ref, feed_sum_ref,
    grad_ref, kt_ref, dk_ref, dv_ref, block_ref, local, send, recv, *scratch,
):
    place = Place()
    line_bufs, line_sems, plane_bufs, plane_sems = split(scratch)
    greet(place, mp_all=True, plane=True)
    scale = 1.0 / math.sqrt(HD)
    factor = math.log2(math.e) * scale
    arriving = exchange(place, pull_ref, grad_ref, local, send, recv)
    next(arriving)

    def feed_block(group, core, start):
        return jnp.dot(
            hidden_ref[group * 2 + core, pl.ds(start, 192)],
            down_ref[...],
            preferred_element_type=F32,
        )

    def feed_result(rows, total):
        feed_ref[rows] = total

    def sum_result(rows, total):
        feed_sum_ref[rows] = total

    plane = plane_reduce(
        place, feed_block, 192, 192, feed_result, plane_bufs, plane_sems, True
    )
    line = line_reduce(
        place,
        lambda level, core, rows: feed_grads_ref[level, rows].astype(F32),
        [pl.ds(start, 112) for start in range(0, 336, 112)],
        sum_result,
        line_bufs,
        line_sems,
        False,
    )
    next(plane)
    next(line)
    next(plane)
    for _ in arriving:
        pass
    next(line)
    block_ref[...] = jnp.zeros(block_ref.shape, BF)

    @pl.loop(0, 6)
    def _(turn):
        clip = turn // 2
        head = turn % 2
        lane = pl.multiple_of(head * 128, 128)
        row = pl.multiple_of(head * HD, 16)
        kt_ref[...] = qkv_ref[:, clip, :, pl.ds(256 + lane, 128)].reshape(1024, 128).T
        dk_ref[...] = jnp.zeros(dk_ref.shape, F32)
        dv_ref[...] = jnp.zeros(dv_ref.shape, F32)

        @pl.loop(0, 4)
        def _(block):
            query = qkv_ref[pl.ds(block * 2, 2), clip, :, pl.ds(lane, 128)].reshape(256, 128)
            values = qkv_ref[:, clip, :, pl.ds(512 + lane, 128)].reshape(1024, 128)
            keys = qkv_ref[:, clip, :, pl.ds(256 + lane, 128)].reshape(1024, 128)
            columns = pl.ds(pl.multiple_of(block * 256, 256), 256)
            for part in range(2):
                block_ref[:HD, part * 128 : part * 128 + 128] = grad_ref[
                    block * 2 + part, clip, pl.ds(row, HD)
                ]
            scores = lax.dot_general(
                keys, query, (((1,), (1,)), ((), ())), preferred_element_type=F32
            )
            chance = jnp.exp2((scores + mask_ref[clip]) * factor - logs_ref[turn, :, columns])
            dv_ref[...] += lax.dot_general(
                chance.astype(BF),
                block_ref[...],
                (((1,), (1,)), ((), ())),
                preferred_element_type=F32,
            )
            slope = lax.dot_general(
                values, block_ref[...], (((1,), (0,)), ((), ())), preferred_element_type=F32
            )
            center = jnp.sum(chance * slope, axis=0, keepdims=True)
            change = (chance * (slope - center)).astype(BF)
            dk_ref[...] += lax.dot_general(
                change, query, (((1,), (0,)), ((), ())), preferred_element_type=F32
            )
            dq = lax.dot_general(
                kt_ref[...], change, (((1,), (0,)), ((), ())), preferred_element_type=F32
            )
            dqkv_ref[pl.ds(block * 2, 2), clip, :, pl.ds(lane, 128)] = (
                (dq.T * scale).astype(BF).reshape(2, 128, 128)
            )

        dqkv_ref[:, clip, :, pl.ds(256 + lane, 128)] = (
            (dk_ref[...] * scale).astype(BF).reshape(8, 128, 128)
        )
        dqkv_ref[:, clip, :, pl.ds(512 + lane, 128)] = (
            dv_ref[...].astype(BF).reshape(8, 128, 128)
        )

        @pl.when(turn == 2)
        def _():
            next(plane)

        @pl.when(turn == 4)
        def _():
            next(line)

    drive(line, plane)


def attend_back(qkv, mask, logs, pull, hidden, down, feed_grads):
    shapes, split = flatten(
        *line_reduce_scratch(336, 1280, False), *plane_reduce_scratch(192, 1280)
    )
    return pl.pallas_call(
        functools.partial(attend_back_kernel, split),
        out_shape=(
            jax.ShapeDtypeStruct(qkv.shape, BF),
            jax.ShapeDtypeStruct((ROWS, 1280), F32),
            jax.ShapeDtypeStruct((336, 1280), F32),
        ),
        in_specs=[VMEM, VMEM, VMEM, ANY, VMEM, VMEM, VMEM],
        out_specs=(VMEM,) * 3,
        scratch_shapes=[
            pltpu.VMEM((8, 3, 160, 128), BF),
            pltpu.VMEM((128, 1024), BF),
            pltpu.VMEM((1024, 128), F32),
            pltpu.VMEM((1024, 128), F32),
            pltpu.VMEM((128, 256), BF),
            pltpu.SemaphoreType.DMA(()),
            dma(8),
            dma(8),
            *shapes,
        ],
        compiler_params=params(2, 61),
        name="attend_back",
    )(qkv, mask, logs, pull, hidden, down, feed_grads)


def line_product_kernel(
    split, grad_ref, weight_ref, out_grad_ref, total_ref, out_ref, middle_ref, *scratch
):
    place = Place()
    bufs, sems, plane_bufs, plane_sems, out_bufs, out_sems = split(scratch)
    greet(place, line=True, plane=True)

    def produce(level, core, rows):
        return jnp.dot(
            grad_ref[level * 2 + core, rows], weight_ref[...], preferred_element_type=F32
        )

    def result(rows, total):
        total_ref[rows] = total

    def middle(rows, total):
        middle_ref[rows] = total

    def out_result(rows, total):
        out_ref[rows] = total

    line = line_reduce(
        place,
        produce,
        [pl.ds(start, 128) for start in range(0, ROWS, 128)],
        result,
        bufs,
        sems,
        True,
    )
    plane = plane_reduce(
        place,
        lambda group, core, start: out_grad_ref[group, core, pl.ds(start, 96)].astype(F32),
        96,
        96,
        middle,
        plane_bufs,
        plane_sems,
    )
    outer = line_reduce(
        place,
        lambda level, core, rows: middle_ref[
            pl.ds(pl.multiple_of(level * 48 + rows.start, 16), rows.size)
        ],
        [pl.ds(0, 48)],
        out_result,
        out_bufs,
        out_sems,
        False,
    )
    drive(plane, line)
    drive(outer)


def line_product(grads, weight, out_grad):
    shapes, split = flatten(
        *line_reduce_scratch(ROWS, 1280, True),
        *plane_reduce_scratch(96, 1280),
        *line_reduce_scratch(48, 1280, False),
    )
    return pl.pallas_call(
        functools.partial(line_product_kernel, split),
        out_shape=(
            jax.ShapeDtypeStruct((ROWS, 1280), F32),
            jax.ShapeDtypeStruct((48, 1280), F32),
        ),
        in_specs=[VMEM, VMEM, VMEM],
        out_specs=(VMEM, VMEM),
        scratch_shapes=[pltpu.VMEM((192, 1280), F32), *shapes],
        compiler_params=params(5, 60),
        name="line_product",
    )(grads, weight, out_grad)


GROUP_ROWS = 4832
GROUP_STEP = 4800
PACK_ROWS = GROUP_STEP * 3 + GROUP_ROWS
SEGMENTS = (
    ("query", 0, 1600),
    ("query_bias", 204800, 2),
    ("key", 204960, 1600),
    ("value", 409760, 1600),
    ("value_bias", 614560, 2),
    ("out", 614720, 1600),
    ("up", 819520, 6400),
    ("up_bias", 1638720, 5),
    ("down", 1639360, 6400),
    ("small", 2458560, 8),
)
PACK_END = 19216


def segment_table():
    table, cursor = {}, 0
    for name, start, rows in SEGMENTS:
        row = start // 128
        cursor += 32
        cursor += (row - cursor) % 8
        table[name] = (cursor, row, rows, start % 128)
        cursor += rows
    return table, (cursor + 32 + 7) // 8 * 8


TABLE, STAGE_ROWS = segment_table()


def lane_of(rows):
    return lax.broadcasted_iota(jnp.int32, (rows, 128), 1)


def pack_rows(stage, packed):
    def piece(name, first, rows):
        base, row, _, shift = TABLE[name]
        at = base - row + first
        here = stage[pl.ds(at, rows)]
        if shift == 0:
            return here
        above = stage[pl.ds(at - 1, rows)]
        return jnp.where(
            lane_of(rows) >= shift, pltpu.roll(here, shift, 1), pltpu.roll(above, shift, 1)
        )

    done = set()
    for name, _, _ in SEGMENTS:
        _, row, rows, shift = TABLE[name]
        low = -(-(row + (1 if shift else 0)) // 16) * 16
        high = (row + rows) // 16 * 16
        if high <= low:
            continue
        done.update(range(low, high, 16))
        turns = (high - low) // 128

        @pl.loop(0, turns)
        def _(turn):
            first = pl.multiple_of(low + turn * 128, 16)
            packed[pl.ds(first, 128)] = piece(name, first, 128).astype(BF)

        for first in range(low + turns * 128, high, 16):
            packed[pl.ds(first, 16)] = piece(name, first, 16).astype(BF)
    for first in range(0, PACK_ROWS, 16):
        if first in done:
            continue
        total = jnp.zeros((16, 128), F32)
        for name, _, _ in SEGMENTS:
            _, row, rows, shift = TABLE[name]
            if row < first + 16 and row + rows + (1 if shift else 0) > first:
                total = total + piece(name, first, 16)
        packed[pl.ds(first, 16)] = total.astype(BF)


def stage_wide(stage, name, ref, step):
    base = TABLE[name][0]
    rows, wide = ref.shape[0], ref.shape[1] // 128

    @pl.loop(0, rows // step)
    def _(turn):
        first = pl.multiple_of(turn * step, step)
        for block in range(wide):
            stage[pl.ds(base + first * wide + block, step, stride=wide), :] = ref[
                pl.ds(first, step), pl.ds(block * 128, 128)
            ].astype(F32)


def stage_heads(stage, name, ref, lanes, column):
    base = TABLE[name][0]
    for head in range(2):
        column[head] = ref[:, pl.ds(lanes + head * 128, 128)]

    @pl.loop(0, 5)
    def _(turn):
        lane = lane_of(64)
        rows = [jnp.zeros((64, 128), F32) for _ in range(5)]
        for block in range(8):
            item, head = block // 2, block % 2
            value = column[head, pl.ds(turn * 256 + item, 64, stride=4)]
            offset = block * HD
            first, shift = offset // 128, offset % 128
            if shift:
                value = pltpu.roll(value, shift, 1)
            if shift + HD > 128:
                rows[first] = rows[first] + jnp.where(lane >= shift, value, 0.0)
                rows[first + 1] = rows[first + 1] + jnp.where(
                    lane < shift + HD - 128, value, 0.0
                )
            else:
                rows[first] = rows[first] + value
        for index in range(5):
            stage[pl.ds(base + turn * 320 + index, 64, stride=5), :] = rows[index]


def stage_head_bias(stage, name, ref, lanes):
    base = TABLE[name][0]
    lane = lane_of(1)
    first = ref[0:1, pl.ds(lanes, 128)]
    second = pltpu.roll(ref[0:1, pl.ds(lanes + 128, 128)], HD, 1)
    stage[pl.ds(base, 1)] = first + jnp.where(lane >= HD, second, 0.0)
    stage[pl.ds(base + 1, 1)] = jnp.where(lane < 2 * HD - 128, second, 0.0)


def pack_reduce_kernel(
    split, joined_ref, bias_ref, out_ref, up_ref, up_bias_ref, down_ref, small_ref, peak_ref,
    grads_ref, small_out, peak_out,
    stage, packed, column, small_in, small_all, peak_all,
    local, small_send, small_recv, plane_send, plane_recv, *scratch,
):
    place = Place()
    bufs, sems = split(scratch)
    greet(place, mp_all=True, plane=True)
    peers = (place.dpx, place.dpy, place.dpd)
    mixing = exchange(place, small_ref, small_in, local, small_send, small_recv)
    next(mixing)

    def tell(index, source, target, group, act):
        act(
            remote(
                source,
                target.at[place.dp],
                plane_send.at[index],
                plane_recv.at[index],
                group,
                place.mp,
            )
        )

    def heard(index, target, group):
        block = target.at[group]
        remote(
            block, block, plane_send.at[index], plane_recv.at[index], group, place.mp
        ).wait_recv()

    for index, group in enumerate(peers):
        tell(index, peak_ref, peak_all, group, lambda copy: copy.start())
    stage[...] = jnp.zeros(stage.shape, F32)
    for name, lanes in (("query", 0), ("key", 256), ("value", 512)):
        stage_heads(stage, name, joined_ref, lanes, column)
    stage_head_bias(stage, "query_bias", bias_ref, 0)
    stage_head_bias(stage, "value_bias", bias_ref, 512)
    stage_wide(stage, "out", out_ref, 160)
    stage_wide(stage, "up", up_ref, 256)
    stage_wide(stage, "down", down_ref, 128)
    stage[pl.ds(TABLE["up_bias"][0], 5)] = up_bias_ref[...]
    for _ in mixing:
        pass
    share = jnp.sum(small_in[...], axis=0)
    small_all[place.dp] = share
    stage[pl.ds(TABLE["small"][0], 8)] = share
    for index, group in enumerate(peers):
        tell(3 + index, small_all.at[place.dp], small_all, group, lambda copy: copy.start())
    pack_rows(stage, packed)

    def produce(group, core, start):
        first = pl.multiple_of(group * GROUP_STEP + start, 16)
        return packed[pl.ds(first, GROUP_ROWS // 2)].astype(F32)

    def result(rows, total):
        grads_ref[rows] = total

    half = GROUP_ROWS // 2
    drive(plane_reduce(place, produce, half, half, result, bufs, sems, False))
    for index, group in enumerate(peers):
        heard(index, peak_all, group)
        heard(3 + index, small_all, group)
    top = peak_ref[...]
    for group in peers:
        top = jnp.maximum(top, peak_all[group])
    peak_out[...] = top
    small_out[...] = jnp.sum(small_all[...], axis=0)
    for index, group in enumerate(peers):
        tell(index, peak_ref, peak_all, group, lambda copy: copy.wait_send())
        tell(3 + index, small_all.at[place.dp], small_all, group, lambda copy: copy.wait_send())


def pack_reduce(joined, bias, out, up, up_bias, down, small, peaks):
    shapes, split = flatten(*plane_reduce_scratch(GROUP_ROWS // 2, 128, False))
    return pl.pallas_call(
        functools.partial(pack_reduce_kernel, split),
        out_shape=(
            jax.ShapeDtypeStruct((GROUP_ROWS, 128), F32),
            jax.ShapeDtypeStruct((8, 128), F32),
            jax.ShapeDtypeStruct(peaks.shape, F32),
        ),
        in_specs=[VMEM] * 8,
        out_specs=(VMEM,) * 3,
        scratch_shapes=[
            pltpu.VMEM((STAGE_ROWS, 128), F32),
            pltpu.VMEM((PACK_ROWS, 128), BF),
            pltpu.VMEM((2, 1280, 128), F32),
            pltpu.VMEM((8, 8, 128), F32),
            pltpu.VMEM((4, 8, 128), F32),
            pltpu.VMEM((4,) + peaks.shape, F32),
            pltpu.SemaphoreType.DMA(()),
            dma(8),
            dma(8),
            dma(6),
            dma(6),
            *shapes,
        ],
        compiler_params=params(7, 60),
        name="pack_reduce",
    )(joined, bias, out, up, up_bias, down, small, peaks)


def share_master_kernel(rows_ref, whole_ref, parts, send, recv):
    place = Place()
    greet(place, plane=True, pair=False)
    dp, mp, dpx, dpy, dpd = place.dp, place.mp, place.dpx, place.dpy, place.dpd
    half = GROUP_ROWS // 2
    part_a, part_b = pl.ds(0, half), pl.ds(half, half)
    parts[dp] = rows_ref[...].astype(BF)

    def hop(index, block, target):
        return remote(block, block, send.at[index], recv.at[index], target, mp)

    own = parts.at[dp]
    sends = [hop(0, own, dpx), hop(1, own, dpy)]
    for copy in sends:
        copy.start()
    hop(0, parts.at[dpx], dpx).wait_recv()
    sends.append(hop(2, parts.at[dpx, part_a], dpy))
    sends[-1].start()
    hop(1, parts.at[dpy], dpy).wait_recv()
    sends.append(hop(3, parts.at[dpy, part_b], dpx))
    sends[-1].start()
    hop(2, parts.at[dpd, part_a], dpy).wait_recv()
    hop(3, parts.at[dpd, part_b], dpx).wait_recv()
    for group in range(4):
        base = group * GROUP_STEP
        first = parts[group, pl.ds(0, 32)].astype(F32)
        if group > 0:
            first = first + parts[group - 1, pl.ds(GROUP_STEP, 32)].astype(F32)
        whole_ref[pl.ds(base, 32)] = first
        for start in range(32, GROUP_STEP, 1192):
            whole_ref[pl.ds(base + start, 1192)] = parts[group, pl.ds(start, 1192)].astype(F32)
    whole_ref[pl.ds(4 * GROUP_STEP, 16)] = parts[3, pl.ds(GROUP_STEP, 16)].astype(F32)
    for copy in sends:
        copy.wait_send()


def share_master(rows):
    return pl.pallas_call(
        share_master_kernel,
        out_shape=jax.ShapeDtypeStruct((PACK_END, 128), F32),
        in_specs=[VMEM],
        out_specs=VMEM,
        scratch_shapes=[pltpu.VMEM((4, GROUP_ROWS, 128), BF), dma(4), dma(4)],
        compiler_params=params(8, 60),
        name="share_master",
    )(rows)


def fast_body(
    frames,
    lengths,
    key_mask,
    cotangent,
    gain_one,
    shift_one,
    query_weight,
    query_bias,
    key_weight,
    value_weight,
    value_bias,
    out_weight,
    out_bias,
    gain_two,
    shift_two,
    up_weight,
    up_bias,
    down_weight,
    down_bias,
    master,
    moment_one,
    moment_two,
    adam_step,
    hyper_rates,
):
    group = lax.axis_index("dp")
    position = jnp.arange(1024, dtype=jnp.int32)
    keep_query = position[None, :] < lengths[:, None]
    keep_key = jnp.logical_and(keep_query, key_mask == 1)
    mask = jnp.where(keep_key, 0.0, MASK_VALUE)[:, :, None]
    live = keep_query.astype(F32)[:, None, :]
    gain_first = gain_one.astype(F32)
    shift_first = shift_one.astype(F32)
    gain_second = gain_two.astype(F32)
    shift_second = shift_two.astype(F32)
    inputs = frames.transpose(1, 0, 2).reshape(ROWS, 1280).astype(F32)
    upstream_low = cotangent.transpose(1, 0, 2).reshape(ROWS, 1280)
    upstream = upstream_low.astype(F32)
    normed = layer_norm(inputs, gain_first, shift_first).astype(BF)

    def head_rows(weight):
        rows = weight.T.reshape(2, HD, 1280)
        return jnp.pad(rows, ((0, 0), (0, 128 - HD), (0, 0))).reshape(256, 1280)

    def head_lanes(bias):
        lanes = bias.astype(F32).reshape(2, HD)
        return jnp.pad(lanes, ((0, 0), (0, 128 - HD))).reshape(256)

    joined_weight = jnp.concatenate(
        [head_rows(query_weight), head_rows(key_weight), head_rows(value_weight)]
    )
    joined_bias = jnp.concatenate(
        [head_lanes(query_bias), jnp.zeros((256,), F32), head_lanes(value_bias)]
    )[None]
    normed_full, qkv, upstream_full = project(normed, upstream_low, joined_weight, joined_bias)
    qkv = qkv.reshape(8, 3, 128, 768)

    quarter = group * 160
    up_share = lax.dynamic_slice_in_dim(up_weight, quarter, 160, 1).T
    down_share = lax.dynamic_slice_in_dim(down_weight, quarter, 160, 0)
    bias_share = lax.dynamic_slice_in_dim(up_bias, quarter, 160, 0)
    bias_rows = jnp.pad(bias_share[None], ((0, 15), (0, 1280 - 160)))
    message = jnp.concatenate([up_share, down_share, bias_rows, out_weight])
    attended, logs, peaks, gathered = attend(qkv, mask, live, message)
    core = lax.axis_index("mp") % 2
    own_core = lax.dynamic_slice_in_dim(gathered.reshape(4, 2, 496, 1280), core, 1, 1)[:, 0]
    up_rows = own_core[:, :160].reshape(640, 1280)
    down_rows = own_core[:, 160:320].reshape(640, 1280)
    up_lanes = own_core[:, 320, :160].reshape(640).astype(F32)
    out_rows = gathered[:, 336:]

    branch = jnp.einsum("schr,shd->crd", attended, out_rows, preferred_element_type=F32)
    middle = inputs + branch.reshape(ROWS, 1280) + out_bias.astype(F32)
    normed_two = layer_norm(middle, gain_second, shift_second).astype(BF)
    normed_two_grad, hidden, feed_grads, _ = feed_forward(
        normed_two, upstream_full, up_rows, down_rows, up_lanes[None]
    )

    _, norm_two_pull = jax.vjp(layer_norm, middle, gain_second, shift_second)
    middle_norm_grad, gain_two_grad, shift_two_grad = norm_two_pull(normed_two_grad)
    middle_grad = upstream + middle_norm_grad
    branch_grad = middle_grad.astype(BF)
    branch_clips = branch_grad.reshape(3, 128, 1280)
    out_grad = jnp.einsum("schr,crd->shd", attended, branch_clips, preferred_element_type=F32)
    attended_grad = jnp.einsum(
        "shd,crd->schr", out_rows, branch_clips, preferred_element_type=F32
    ).astype(BF)
    out_quarters = jnp.pad(
        out_grad.astype(BF).reshape(4, 2, 4, 40, 1280), ((0, 0),) * 3 + ((0, 8), (0, 0))
    )
    out_quarters = out_quarters.transpose(2, 1, 0, 3, 4).reshape(4, 2, 192, 1280)
    joined_grad, feed, feed_sum = attend_back(
        qkv, mask, logs, attended_grad, hidden, down_rows, feed_grads
    )
    layer_out = (middle + feed + down_bias.astype(F32)).astype(BF)
    joined_grad = joined_grad.reshape(8, ROWS, 768)
    normed_grad, out_sum = line_product(joined_grad, joined_weight, out_quarters)
    joined_weight_grad = jnp.einsum(
        "prd,pre->de", normed_full, joined_grad, preferred_element_type=F32
    )
    joined_bias_grad = jnp.sum(joined_grad.astype(F32), axis=(0, 1))

    _, norm_one_pull = jax.vjp(layer_norm, inputs, gain_first, shift_first)
    input_norm_grad, gain_one_grad, shift_one_grad = norm_one_pull(normed_grad)
    input_grad = middle_grad + input_norm_grad

    def spread(rows):
        size = rows.shape[0]
        return lax.dynamic_update_slice(
            jnp.zeros((4 * size,) + rows.shape[1:], F32),
            rows,
            (size * group,) + (0,) * (rows.ndim - 1),
        )

    up_whole = spread(feed_sum[:160]).T
    down_whole = spread(feed_sum[160:320])
    level = lax.axis_index("mp") // 2
    up_bias_whole = spread(lax.dynamic_slice_in_dim(feed_sum[320], level * 160, 160, 0))
    out_whole = spread(out_sum[:40])

    out_bias_grad = jnp.sum(branch_grad.astype(F32), axis=0)
    down_bias_grad = jnp.sum(upstream, axis=0)
    small_terms = jnp.concatenate(
        [
            gain_one_grad,
            shift_one_grad,
            out_bias_grad,
            gain_two_grad,
            shift_two_grad,
            down_bias_grad,
        ]
    )
    small_tiles = jnp.pad(small_terms.reshape(8, 960), ((0, 0), (0, 64))).reshape(8, 8, 128)
    grad_rows, small_sum, peak_sum = pack_reduce(
        joined_weight_grad,
        joined_bias_grad[None],
        out_whole,
        up_whole,
        up_bias_whole.reshape(5, 128),
        down_whole,
        small_tiles,
        peaks,
    )
    small_total = small_sum.reshape(1024)[:960]
    head_peak = jnp.max(peak_sum, axis=(1, 2)) / math.sqrt(HD)
    share_size = master.shape[1]
    owned_grads = lax.dynamic_slice(
        grad_rows.reshape(1, GROUP_ROWS * 128), (0, 480 * group), (1, share_size)
    )
    learn_rate = hyper_rates[0]
    weight_decay = hyper_rates[1]
    logit_cap = hyper_rates[2]
    step_count = adam_step[0].astype(F32)
    first_new = BETA_FIRST * moment_one + (1.0 - BETA_FIRST) * owned_grads
    second_new = BETA_SECOND * moment_two + (1.0 - BETA_SECOND) * owned_grads * owned_grads
    first_hat = first_new / (1.0 - jnp.power(BETA_FIRST, step_count))
    second_hat = second_new / (1.0 - jnp.power(BETA_SECOND, step_count))
    entry_index = group * share_size + lax.broadcasted_iota(jnp.int32, (1, share_size), 1)
    query_end = 1280 * 160
    query_bias_end = query_end + 160
    key_end = query_bias_end + 1280 * 160
    block = jnp.floor((entry_index.astype(F32) + 0.5) * (1.0 / HD))
    odd = block - 2.0 * jnp.floor(block * 0.5) > 0.5
    root_factor = jnp.sqrt(logit_cap / jnp.maximum(head_peak, logit_cap))
    head_factor = jnp.where(odd, root_factor[1], root_factor[0])
    factor = jnp.where(entry_index < key_end, head_factor, 1.0)
    master_new = (
        master
        - learn_rate * (first_hat / (jnp.sqrt(second_hat) + ADAM_EPSILON) + weight_decay * master)
    ) * factor

    def placed_rows(offset):
        room = GROUP_ROWS * 128 - share_size - offset
        return lambda value: jnp.pad(value, ((0, 0), (offset, room))).reshape(GROUP_ROWS, 128)

    master_rows = lax.switch(group, [placed_rows(480 * part) for part in range(4)], master_new)
    whole = share_master(master_rows).reshape(1, PACK_END * 128)
    whole = lax.optimization_barrier(whole)
    weights_new = whole[:, : 4 * share_size].astype(BF)
    return (
        layer_out.reshape(3, 128, 1280).transpose(1, 0, 2),
        input_grad.reshape(3, 128, 1280).transpose(1, 0, 2),
        owned_grads,
        master_new,
        first_new,
        second_new,
        weights_new,
        small_total,
    )


def body(
    frames,
    lengths,
    key_mask,
    cotangent,
    gain_one,
    shift_one,
    query_weight,
    query_bias,
    key_weight,
    value_weight,
    value_bias,
    out_weight,
    out_bias,
    gain_two,
    shift_two,
    up_weight,
    up_bias,
    down_weight,
    down_bias,
    master,
    moment_one,
    moment_two,
    adam_step,
    hyper_rates,
):
    local_rows, clip_count, model_width = frames.shape
    total_rows = key_mask.shape[1]
    head_cols = query_weight.shape[1]
    heads_here = head_cols // HD
    block_rows = min(512, total_rows)
    blocks = total_rows // block_rows
    score_scale = 1.0 / math.sqrt(HD)
    position = jnp.arange(total_rows, dtype=jnp.int32)
    keep_query = position[None, :] < lengths[:, None]
    keep_key = jnp.logical_and(keep_query, key_mask == 1)
    gain_first = gain_one.astype(jnp.float32)
    shift_first = shift_one.astype(jnp.float32)
    gain_second = gain_two.astype(jnp.float32)
    shift_second = shift_two.astype(jnp.float32)
    inputs = frames.astype(jnp.float32)
    normed = layer_norm(inputs, gain_first, shift_first).astype(jnp.bfloat16)
    joined_weight = jnp.concatenate([query_weight, key_weight, value_weight], axis=1)
    joined_bias = jnp.concatenate(
        [
            query_bias.astype(jnp.float32),
            jnp.zeros((head_cols,), jnp.float32),
            value_bias.astype(jnp.float32),
        ]
    )
    normed_full = lax.all_gather(normed, "mp", axis=0, tiled=True)
    projected = (
        jnp.einsum("rcd,de->rce", normed_full, joined_weight, preferred_element_type=jnp.float32)
        + joined_bias
    ).astype(jnp.bfloat16)
    query = projected[:, :, :head_cols].reshape(total_rows, clip_count, heads_here, HD)
    keys = projected[:, :, head_cols : 2 * head_cols].reshape(
        total_rows, clip_count, heads_here, HD
    )
    values = projected[:, :, 2 * head_cols :].reshape(total_rows, clip_count, heads_here, HD)

    def scores_of(row_start):
        query_block = lax.dynamic_slice_in_dim(query, row_start, block_rows, 0)
        raw_scores = (
            jnp.einsum("qchd,kchd->chqk", query_block, keys, preferred_element_type=jnp.float32)
            * score_scale
        )
        return (query_block, jnp.where(keep_key[:, None, None, :], raw_scores, MASK_VALUE))

    def forward_block(block_index):
        row_start = block_index * block_rows
        _, masked = scores_of(row_start)
        row_peak = jnp.max(masked, axis=-1, keepdims=True)
        exp_scores = jnp.exp(masked - row_peak)
        row_total = jnp.sum(exp_scores, axis=-1, keepdims=True)
        probability = (exp_scores / row_total).astype(jnp.bfloat16)
        attended = jnp.einsum(
            "chqk,kchd->qchd", probability, values, preferred_element_type=jnp.float32
        ).astype(jnp.bfloat16)
        live_rows = lax.dynamic_slice_in_dim(keep_query, row_start, block_rows, 1)
        block_peak = jnp.max(
            jnp.where(live_rows[:, None, :], row_peak[..., 0], MASK_VALUE), axis=(0, 2)
        )
        return (attended, (row_peak + jnp.log(row_total))[..., 0], block_peak)

    attended_blocks, log_totals, block_peaks = lax.map(forward_block, jnp.arange(blocks))
    attended_full = attended_blocks.reshape(total_rows, clip_count, head_cols)
    head_peak = lax.pmax(jnp.max(block_peaks, axis=0), "dp")
    rows_here = attended_full
    attn_branch = lax.psum_scatter(
        jnp.einsum("rck,kd->rcd", rows_here, out_weight, preferred_element_type=jnp.float32),
        "mp",
        scatter_dimension=0,
        tiled=True,
    ) + out_bias.astype(jnp.float32)
    middle = inputs + attn_branch
    normed_two = layer_norm(middle, gain_second, shift_second).astype(jnp.bfloat16)
    upstream = cotangent.astype(jnp.float32)
    normed_two_full = lax.all_gather(normed_two, "mp", axis=0, tiled=True)
    before = jnp.einsum(
        "rcd,df->rcf", normed_two_full, up_weight, preferred_element_type=jnp.float32
    ) + up_bias.astype(jnp.float32)
    hidden = exact_gelu(before).astype(jnp.bfloat16)
    rows_here = hidden
    feed = lax.psum_scatter(
        jnp.einsum(
            "rcf,fd->rcd", rows_here, down_weight, preferred_element_type=jnp.float32
        ).astype(jnp.bfloat16),
        "mp",
        scatter_dimension=0,
        tiled=True,
    ).astype(jnp.float32) + down_bias.astype(jnp.float32)
    layer_out = (middle + feed).astype(jnp.bfloat16)
    feed_grad_full = lax.all_gather(cotangent, "mp", axis=0, tiled=True)
    down_grad = jnp.einsum(
        "rcf,rcd->fd", hidden, feed_grad_full, preferred_element_type=jnp.float32
    )
    hidden_grad = jnp.einsum(
        "rcd,fd->rcf", feed_grad_full, down_weight, preferred_element_type=jnp.float32
    )
    _, gelu_pull = jax.vjp(exact_gelu, before)
    before_grad = gelu_pull(hidden_grad)[0].astype(jnp.bfloat16)
    up_bias_grad = jnp.sum(before_grad.astype(jnp.float32), axis=(0, 1))
    up_grad = jnp.einsum(
        "rcd,rcf->df", normed_two_full, before_grad, preferred_element_type=jnp.float32
    )
    rows_here = before_grad
    normed_two_grad = lax.psum_scatter(
        jnp.einsum("rcf,df->rcd", rows_here, up_weight, preferred_element_type=jnp.float32),
        "mp",
        scatter_dimension=0,
        tiled=True,
    )
    _, norm_two_pull = jax.vjp(layer_norm, middle, gain_second, shift_second)
    middle_norm_grad, gain_two_grad, shift_two_grad = norm_two_pull(normed_two_grad)
    middle_grad = upstream + middle_norm_grad
    branch_grad = middle_grad.astype(jnp.bfloat16)
    branch_grad_full = lax.all_gather(branch_grad, "mp", axis=0, tiled=True)
    out_grad = jnp.einsum(
        "rck,rcd->kd", attended_full, branch_grad_full, preferred_element_type=jnp.float32
    )
    attended_grad = jnp.einsum(
        "rcd,kd->rck", branch_grad_full, out_weight, preferred_element_type=jnp.float32
    ).astype(jnp.bfloat16)
    attended_grad = attended_grad.reshape(total_rows, clip_count, heads_here, HD)

    def backward_block(carry, block_index):
        key_total, value_total = carry
        row_start = block_index * block_rows
        query_block, masked = scores_of(row_start)
        log_total = log_totals[block_index]
        probability = jnp.exp(masked - log_total[..., None])
        grad_block = lax.dynamic_slice_in_dim(attended_grad, row_start, block_rows, 0)
        value_total = value_total + jnp.einsum(
            "chqk,qchd->kchd",
            probability.astype(jnp.bfloat16),
            grad_block,
            preferred_element_type=jnp.float32,
        )
        prob_grad = jnp.einsum(
            "qchd,kchd->chqk", grad_block, values, preferred_element_type=jnp.float32
        )
        score_grad = (
            probability * (prob_grad - jnp.sum(probability * prob_grad, axis=-1, keepdims=True))
        ).astype(jnp.bfloat16)
        query_grad = (
            jnp.einsum("chqk,kchd->qchd", score_grad, keys, preferred_element_type=jnp.float32)
            * score_scale
        ).astype(jnp.bfloat16)
        key_total = (
            key_total
            + jnp.einsum(
                "chqk,qchd->kchd", score_grad, query_block, preferred_element_type=jnp.float32
            )
            * score_scale
        )
        return ((key_total, value_total), query_grad)

    empty_grad = jnp.zeros((total_rows, clip_count, heads_here, HD), jnp.float32)
    (key_total, value_total), query_blocks = lax.scan(
        backward_block, (empty_grad, empty_grad), jnp.arange(blocks)
    )
    joined_grad = jnp.concatenate(
        [
            query_blocks.reshape(total_rows, clip_count, head_cols),
            key_total.reshape(total_rows, clip_count, head_cols).astype(jnp.bfloat16),
            value_total.reshape(total_rows, clip_count, head_cols).astype(jnp.bfloat16),
        ],
        axis=-1,
    )
    joined_bias_grad = jnp.sum(joined_grad.astype(jnp.float32), axis=(0, 1))
    normed_back = lax.all_gather(normed, "mp", axis=0, tiled=True)
    joined_weight_grad = jnp.einsum(
        "rcd,rce->de", normed_back, joined_grad, preferred_element_type=jnp.float32
    )
    rows_here = joined_grad
    normed_grad = lax.psum_scatter(
        jnp.einsum(
            "rce,de->rcd", rows_here, joined_weight, preferred_element_type=jnp.float32
        ).astype(jnp.bfloat16),
        "mp",
        scatter_dimension=0,
        tiled=True,
    ).astype(jnp.float32)
    _, norm_one_pull = jax.vjp(layer_norm, inputs, gain_first, shift_first)
    input_norm_grad, gain_one_grad, shift_one_grad = norm_one_pull(normed_grad)
    input_grad = middle_grad + input_norm_grad
    out_bias_grad = jnp.sum(branch_grad.astype(jnp.float32), axis=(0, 1))
    down_bias_grad = jnp.sum(upstream, axis=(0, 1))
    small_terms = jnp.concatenate(
        [
            gain_one_grad,
            shift_one_grad,
            out_bias_grad,
            gain_two_grad,
            shift_two_grad,
            down_bias_grad,
        ]
    )
    small_share = lax.psum_scatter(small_terms, "mp", scatter_dimension=0, tiled=True)
    small_total = lax.psum(small_share, "dp")
    packed = jnp.concatenate(
        [
            joined_weight_grad[:, :head_cols].reshape(-1),
            joined_bias_grad[:head_cols],
            joined_weight_grad[:, head_cols : 2 * head_cols].reshape(-1),
            joined_weight_grad[:, 2 * head_cols :].reshape(-1),
            joined_bias_grad[2 * head_cols :],
            out_grad.reshape(-1),
            up_grad.reshape(-1),
            up_bias_grad,
            down_grad.reshape(-1),
            small_share,
        ]
    )
    owned_grads = lax.psum_scatter(
        packed.astype(jnp.bfloat16), "dp", scatter_dimension=0, tiled=True
    ).astype(jnp.float32)
    share_size = owned_grads.shape[0]
    learn_rate = hyper_rates[0]
    weight_decay = hyper_rates[1]
    logit_cap = hyper_rates[2]
    step_count = adam_step[0].astype(jnp.float32)
    first_new = BETA_FIRST * moment_one[0] + (1.0 - BETA_FIRST) * owned_grads
    second_new = BETA_SECOND * moment_two[0] + (1.0 - BETA_SECOND) * owned_grads * owned_grads
    first_hat = first_new / (1.0 - jnp.power(BETA_FIRST, step_count))
    second_hat = second_new / (1.0 - jnp.power(BETA_SECOND, step_count))
    entry_index = lax.axis_index("dp") * share_size + jnp.arange(share_size, dtype=jnp.int32)
    query_end = model_width * head_cols
    query_bias_end = query_end + head_cols
    key_end = query_bias_end + model_width * head_cols
    column = jnp.where(
        entry_index < query_end,
        entry_index % head_cols,
        jnp.where(
            entry_index < query_bias_end,
            entry_index - query_end,
            (entry_index - query_bias_end) % head_cols,
        ),
    )
    head_index = column // HD
    root_factor = jnp.sqrt(logit_cap / jnp.maximum(head_peak, logit_cap))
    head_factor = jnp.zeros((share_size,), jnp.float32)
    for head_number in range(heads_here):
        head_factor = head_factor + jnp.where(
            head_index == head_number, root_factor[head_number], 0.0
        )
    factor = jnp.where(entry_index < key_end, head_factor, 1.0)
    master_here = master[0]
    master_new = (
        master_here
        - learn_rate
        * (first_hat / (jnp.sqrt(second_hat) + ADAM_EPSILON) + weight_decay * master_here)
    ) * factor
    weights_full = lax.all_gather(master_new.astype(jnp.bfloat16), "dp", axis=0, tiled=True)
    return (
        layer_out,
        input_grad,
        owned_grads[None],
        master_new[None],
        first_new[None],
        second_new[None],
        weights_full[None],
        small_total,
    )


def solution(mesh):
    chosen = fast_body if dict(mesh.shape) == {"dp": 4, "mp": 8} else body
    placed = (
        P("mp", "dp", None),
        P("dp"),
        P("dp", None),
        P("mp", "dp", None),
        P(),
        P(),
        P(None, "mp"),
        P("mp"),
        P(None, "mp"),
        P(None, "mp"),
        P("mp"),
        P("mp", None),
        P(),
        P(),
        P(),
        P(None, "mp"),
        P("mp"),
        P("mp", None),
        P(),
        P("mp", "dp"),
        P("mp", "dp"),
        P("mp", "dp"),
        P(),
        P(),
    )
    return jax.shard_map(
        chosen,
        mesh=mesh,
        in_specs=placed,
        out_specs=(
            P("mp", "dp", None),
            P("mp", "dp", None),
            P("mp", "dp"),
            P("mp", "dp"),
            P("mp", "dp"),
            P("mp", "dp"),
            P("mp", None),
            P("mp"),
        ),
        check_vma=False,
    )
```

```python
import functools
import math

import jax
import jax.numpy as jnp
from jax import lax
from jax.experimental import pallas as pl
from jax.experimental.pallas import tpu as pltpu
from jax.sharding import PartitionSpec as P

HD = 80


NORM_EPSILON = 1e-05
ADAM_EPSILON = 1e-08
BETA_FIRST = 0.9
BETA_SECOND = 0.999
MASK_VALUE = -1e30


def layer_norm(value, gain, shift):
    center = value - jnp.mean(value, axis=-1, keepdims=True)
    spread = jnp.mean(center * center, axis=-1, keepdims=True)
    return center * lax.rsqrt(spread + NORM_EPSILON) * gain + shift


def exact_gelu(argument):
    return jax.nn.gelu(argument, approximate=False)


MESH = pl.DeviceIdType.MESH
ANY = pl.BlockSpec(memory_space=pl.ANY)
VMEM = pl.BlockSpec(memory_space=pltpu.VMEM)
LINE = 4
ROWS = 384
BF = jnp.bfloat16
F32 = jnp.float32


class Place:
    def __init__(self):
        self.dp = lax.axis_index("dp")
        self.mp = lax.axis_index("mp")
        self.z = self.mp // 2
        self.c = self.mp % 2
        self.pair = self.z * 2 + 1 - self.c
        self.dpx = self.dp + 1 - 2 * (self.dp % 2)
        self.dpy = (self.dp + 2) % 4
        self.dpd = 3 - self.dp

    def zorder(self, event):
        if event == 0:
            return self.z
        if event == 1:
            return self.z + 1 - 2 * (self.z % 2)
        if event == 2:
            return 2 - self.z // 2
        return 3 - 3 * (self.z // 2)


def greet(place, mp_all=False, line=False, plane=False, pair=True):
    barrier = pltpu.get_barrier_semaphore()
    count = 0

    def signal(dp, mp):
        pl.semaphore_signal(barrier, inc=1, device_id=(dp, mp), device_id_type=MESH)

    if mp_all:
        for hop in range(1, 8):
            signal(place.dp, (place.mp + hop) % 8)
        count += 7
    else:
        if pair:
            signal(place.dp, place.pair)
            count += 1
        if line:

            @pl.when(place.z > 0)
            def _():
                signal(place.dp, place.mp - 2)

            @pl.when(place.z < LINE - 1)
            def _():
                signal(place.dp, place.mp + 2)

    if plane:
        for other in (place.dpx, place.dpy, place.dpd):
            signal(other, place.mp)
        count += 3
    if line and not mp_all:
        pl.semaphore_wait(barrier, count + 1 + (place.z + 1) // 2 % 2)
    else:
        pl.semaphore_wait(barrier, count)


def remote(src, dst, send, recv, dp, mp):
    return pltpu.make_async_remote_copy(
        src_ref=src,
        dst_ref=dst,
        send_sem=send,
        recv_sem=recv,
        device_id=(dp, mp),
        device_id_type=MESH,
    )


def line_gather(place, src, out, local, send, recv, paired, ready=None, rows=None):
    dp, z, c, mp, pair = place.dp, place.z, place.c, place.mp, place.pair

    def at(slot):
        if rows is None:
            return out.at[slot]
        return out.at[pl.ds(pl.multiple_of(slot * rows, 16), rows)]

    def slot_of(level, core):
        return level * 2 + core if paired else level

    def hop(event, slot, source, direction, target):
        return remote(source, at(slot), send.at[event, direction], recv.at[slot], dp, target)

    own = slot_of(z, c)
    keep = pltpu.make_async_copy(src, at(own), local)
    keep.start()

    def ways(event, level, slot, source, act):
        up = z < LINE - 1
        down = z > 0
        if event > 0:
            up = jnp.logical_and(up, level < z)
            down = jnp.logical_and(down, level > z)

        @pl.when(up)
        def _():
            act(hop(event, slot, source, 1, mp + 2))

        @pl.when(down)
        def _():
            act(hop(event, slot, source, 2, mp - 2))

        if paired:
            act(hop(event, slot, source, 0, pair))

    ways(0, z, own, src, lambda copy: copy.start())
    yield
    if ready is not None:
        keep.wait()
        ready(own)
        if paired:
            other = slot_of(z, 1 - c)
            hop(0, other, at(other), 0, pair).wait_recv()
            ready(other)

    def settle(event):
        level = place.zorder(event)
        ready(slot_of(level, c))
        if paired:
            other = slot_of(level, 1 - c)
            hop(event, other, at(other), 0, pair).wait_recv()
            ready(other)

    for event in range(1, LINE):
        level = place.zorder(event)
        slot = slot_of(level, c)
        hop(event, slot, at(slot), 0, pair).wait_recv()
        ways(event, level, slot, at(slot), lambda copy: copy.start())
        if ready is not None and event > 1:
            if event == 2:
                settle(1)
            settle(event)
        yield
    if ready is None:
        if paired:
            for level in range(LINE):
                other = slot_of(level, 1 - c)
                hop(0, other, at(other), 0, pair).wait_recv()
        keep.wait()
    for event in range(LINE):
        level = place.zorder(event)
        slot = slot_of(level, c)
        ways(event, level, slot, at(slot), lambda copy: copy.wait_send())
    yield


def plane_gather(place, src, out, local, send, recv, ready=None, primed=False):
    dp, c, mp, pair = place.dp, place.c, place.mp, place.pair
    dpx, dpy, dpd = place.dpx, place.dpy, place.dpd
    half = src.shape[0] // 2
    part_a, part_b = pl.ds(0, half), pl.ds(half, half)

    def at(group, core):
        return out.at[group * 2 + core]

    def hop(index, block, group, target):
        return remote(block, block, send.at[index], recv.at[index], group, target)

    def done(group, core):
        if ready is not None:
            ready(group * 2 + core)

    keep = pltpu.make_async_copy(src, at(dp, c), local)
    here = at(dp, c)
    from_x, from_y, from_d = at(dpx, c), at(dpy, c), at(dpd, c)
    firsts = [
        remote(src, here, send.at[0], recv.at[0], dp, pair),
        remote(src, here, send.at[1], recv.at[1], dpx, mp),
        remote(src, here, send.at[2], recv.at[2], dpy, mp),
    ]
    seconds = [
        hop(3, from_x.at[part_a], dpy, mp),
        hop(4, from_y.at[part_b], dpx, mp),
        hop(5, from_x, dp, pair),
        hop(6, from_y, dp, pair),
        hop(7, from_d.at[part_a], dp, pair),
        hop(8, from_d.at[part_b], dp, pair),
    ]
    if primed:
        yield
    keep.start()
    for copy in firsts:
        copy.start()
    yield
    if ready is not None:
        keep.wait()
        done(dp, c)
        hop(0, at(dp, 1 - c), dp, pair).wait_recv()
        done(dp, 1 - c)
    hop(1, from_x, dpx, mp).wait_recv()
    seconds[0].start()
    hop(2, from_y, dpy, mp).wait_recv()
    seconds[1].start()
    seconds[2].start()
    seconds[3].start()
    if ready is None:
        yield
    done(dpx, c)
    hop(5, at(dpx, 1 - c), dp, pair).wait_recv()
    done(dpx, 1 - c)
    if ready is not None:
        yield
    hop(3, from_d.at[part_a], dpy, mp).wait_recv()
    seconds[4].start()
    hop(4, from_d.at[part_b], dpx, mp).wait_recv()
    seconds[5].start()
    done(dpy, c)
    hop(6, at(dpy, 1 - c), dp, pair).wait_recv()
    done(dpy, 1 - c)
    yield
    done(dpd, c)
    other = at(dpd, 1 - c)
    hop(7, other.at[part_a], dp, pair).wait_recv()
    hop(8, other.at[part_b], dp, pair).wait_recv()
    done(dpd, 1 - c)
    yield
    if ready is None:
        hop(0, at(dp, 1 - c), dp, pair).wait_recv()
        keep.wait()
    for copy in firsts + seconds:
        copy.wait_send()
    yield


def drive(*programs):
    live = list(programs)
    while live:
        for program in list(live):
            try:
                next(program)
            except StopIteration:
                live.remove(program)


def dma(*shape):
    return pltpu.SemaphoreType.DMA(shape)


def params(cid, vmem=40):
    return pltpu.CompilerParams(
        collective_id=cid, has_side_effects=True, vmem_limit_bytes=vmem << 20
    )


def exchange(place, src, out, local, send, recv):
    dp, mp = place.dp, place.mp
    keep = pltpu.make_async_copy(src.at[mp], out.at[mp], local)
    keep.start()
    sends = []
    for hop in range(1, 8):
        target = (mp + hop) % 8
        sends.append(
            remote(src.at[target], out.at[mp], send.at[hop], recv.at[hop], dp, target)
        )
        sends[-1].start()
    yield
    keep.wait()
    for hop in range(1, 8):
        origin = (mp + 8 - hop) % 8
        remote(out.at[origin], out.at[origin], send.at[hop], recv.at[hop], dp, origin).wait_recv()
    for copy in sends:
        copy.wait_send()
    yield


def line_reduce(place, produce, tiles, result, bufs, sems, paired):
    dp, z, c, mp, pair = place.dp, place.z, place.c, place.mp, place.pair
    above_block, below_block, out_block = bufs["above"], bufs["below"], bufs["out"]
    order = [place.zorder(event) for event in (3, 2, 1, 0)]

    @pl.when(z == LINE - 1)
    def _():
        above_block[...] = jnp.zeros(above_block.shape, BF)

    @pl.when(z == 0)
    def _():
        below_block[...] = jnp.zeros(below_block.shape, BF)

    def from_above(level):
        return above_block.at[jnp.minimum(level, LINE - 2)]

    def from_below(level):
        return below_block.at[jnp.maximum(level - 1, 0)]

    def across(step, level):
        return remote(
            bufs["pair_out"].at[step % 2],
            bufs["pair_in"].at[level],
            sems["pair_send"].at[step % 2],
            sems["pair_recv"].at[level],
            dp,
            pair,
        )

    if paired:
        for step, level in enumerate(order):
            if step > 1:
                across(step - 2, order[step - 2]).wait_send()
            for rows in tiles:
                bufs["pair_out"][step % 2, rows] = produce(level, 1 - c, rows).astype(BF)
            across(step, level).start()
    yield

    def toward(step, level, act):
        @pl.when(level < z)
        def _():
            act(
                remote(
                    out_block.at[step],
                    from_above(level),
                    sems["line_send"].at[step],
                    sems["above"].at[level],
                    dp,
                    mp - 2,
                )
            )

        @pl.when(level > z)
        def _():
            act(
                remote(
                    out_block.at[step],
                    from_below(level),
                    sems["line_send"].at[step],
                    sems["below"].at[level],
                    dp,
                    mp + 2,
                )
            )

    def arrive(level, above):
        if above:
            remote(
                from_above(level),
                from_above(level),
                sems["line_send"].at[0],
                sems["above"].at[level],
                dp,
                mp,
            ).wait_recv()
        else:
            remote(
                from_below(level),
                from_below(level),
                sems["line_send"].at[0],
                sems["below"].at[level],
                dp,
                mp,
            ).wait_recv()

    for step, level in enumerate(order[:3]):
        if paired:
            across(step, level).wait_recv()

        @pl.when(jnp.logical_and(level < z, z < LINE - 1))
        def _():
            arrive(level, True)

        @pl.when(jnp.logical_and(level > z, z > 0))
        def _():
            arrive(level, False)

        for rows in tiles:
            total = produce(level, c, rows)
            if paired:
                total = total + bufs["pair_in"][level, rows].astype(F32)

            @pl.when(level < z)
            def _():
                out_block[step, rows] = (total + from_above(level)[rows].astype(F32)).astype(BF)

            @pl.when(level > z)
            def _():
                out_block[step, rows] = (total + from_below(level)[rows].astype(F32)).astype(BF)

        toward(step, level, lambda copy: copy.start())
        yield

    if paired:
        across(3, z).wait_recv()

    @pl.when(z < LINE - 1)
    def _():
        arrive(z, True)

    @pl.when(z > 0)
    def _():
        arrive(z, False)

    for rows in tiles:
        total = produce(z, c, rows)
        if paired:
            total = total + bufs["pair_in"][z, rows].astype(F32)
        total = total + from_above(z)[rows].astype(F32) + from_below(z)[rows].astype(F32)
        result(rows, total)
    for step, level in enumerate(order):
        if paired and step > 1:
            across(step, level).wait_send()
        if step < 3:
            toward(step, level, lambda copy: copy.wait_send())
    yield


def line_reduce_scratch(rows, cols, paired):
    block = lambda n: pltpu.VMEM((n, rows, cols), BF)
    scratch = {"above": block(3), "below": block(3), "out": block(3)}
    sems = {"line_send": dma(3), "above": dma(4), "below": dma(4)}
    if paired:
        scratch.update({"pair_out": block(2), "pair_in": block(4)})
        sems.update({"pair_send": dma(2), "pair_recv": dma(4)})
    return scratch, sems


def plane_reduce(place, produce, tile, half, result, bufs, sems, paired=True, early=False):
    dp, c, mp, pair = place.dp, place.c, place.mp, place.pair
    dpx, dpy, dpd = place.dpx, place.dpy, place.dpd
    starts = range(0, half, tile)
    send, recv = sems["send"], sems["recv"]
    out_block, landed = bufs["out"], bufs["in"]
    groups = {"far": dpd, "x": dpx, "y": dpy, "own": dp}
    steps = ["x", "y", "far", "own"] if early else ["far", "x", "y", "own"]

    def across(name):
        step = steps.index(name)
        return remote(
            bufs["pair_out"].at[step % 2],
            bufs["pair_in"].at[step],
            sems["pair_send"].at[step % 2],
            sems["pair_recv"].at[step],
            dp,
            pair,
        )

    def cross(name):
        if not paired:
            return
        step = steps.index(name)
        if step > 1:
            across(steps[step - 2]).wait_send()
        for start in range(0, 2 * half, tile):
            bufs["pair_out"][step % 2, pl.ds(start, tile)] = produce(
                groups[name], 1 - c, start
            ).astype(BF)
        across(name).start()

    def crossed(name):
        if paired:
            across(name).wait_recv()

    def share(name, start):
        total = produce(groups[name], c, start)
        if paired:
            total = total + bufs["pair_in"][steps.index(name), pl.ds(start, tile)].astype(F32)
        return total

    def hop(index):
        target = (dpx, dpy, dpx, dpx, dpy, dpy)[index]
        return remote(
            out_block.at[index], landed.at[index], send.at[index], recv.at[index], target, mp
        )

    def fill(index, name, base, extra=None):
        for start in starts:
            total = share(name, base + start)
            if extra is not None:
                total = total + landed[extra, pl.ds(start, tile)].astype(F32)
            out_block[index, pl.ds(start, tile)] = total.astype(BF)
        hop(index).start()

    def far():
        crossed("far")
        fill(0, "far", 0)
        fill(1, "far", half)

    def near():
        crossed("x")
        fill(2, "x", 0)
        crossed("y")
        fill(4, "y", half)

    if early:
        cross("x")
        yield
        cross("y")
        near()
        yield
        cross("far")
        far()
        cross("own")
    else:
        cross("far")
        cross("x")
        yield
        far()
        cross("y")
        near()
        cross("own")
    yield
    hop(1).wait_recv()
    fill(3, "x", half, extra=1)
    hop(0).wait_recv()
    fill(5, "y", 0, extra=0)
    yield
    crossed("own")
    for index in (2, 3, 4, 5):
        hop(index).wait_recv()
    for base, pieces in ((0, (2, 5)), (half, (3, 4))):
        for start in starts:
            total = share("own", base + start)
            for piece in pieces:
                total = total + landed[piece, pl.ds(start, tile)].astype(F32)
            result(pl.ds(base + start, tile), total)
    for index in range(6):
        hop(index).wait_send()
    if paired:
        for name in steps[2:]:
            across(name).wait_send()
    yield


def plane_reduce_scratch(half, cols, paired=True):
    block = lambda n, rows: pltpu.VMEM((n, rows, cols), BF)
    scratch = {"out": block(6, half), "in": block(6, half)}
    sems = {"send": dma(6), "recv": dma(6)}
    if paired:
        scratch.update({"pair_out": block(2, 2 * half), "pair_in": block(4, 2 * half)})
        sems.update({"pair_send": dma(2), "pair_recv": dma(4)})
    return scratch, sems


def project_kernel(
    normed_ref, cot_ref, weight_ref, bias_ref, nfull_ref, qkv_ref, cfull_ref,
    local, line_send, line_recv, plane_send, plane_recv,
):
    place = Place()
    greet(place, line=True, plane=True)

    def ready(slot):
        @pl.loop(0, 3)
        def _(step):
            rows = pl.ds(step * 128, 128)
            product = lax.dot_general(
                nfull_ref[slot, rows],
                weight_ref[...],
                (((1,), (1,)), ((), ())),
                preferred_element_type=F32,
            )
            qkv_ref[slot, rows] = (product + bias_ref[...]).astype(BF)

    drive(
        line_gather(
            place, normed_ref, nfull_ref, local.at[0], line_send, line_recv, True, ready
        ),
        plane_gather(place, cot_ref, cfull_ref, local.at[1], plane_send, plane_recv),
    )


def project(normed, cotangent, weight, bias):
    return pl.pallas_call(
        project_kernel,
        out_shape=(
            jax.ShapeDtypeStruct((8,) + normed.shape, BF),
            jax.ShapeDtypeStruct((8, ROWS, weight.shape[0]), BF),
            jax.ShapeDtypeStruct((8,) + cotangent.shape, BF),
        ),
        in_specs=[ANY, ANY, VMEM, VMEM],
        out_specs=(VMEM, VMEM, ANY),
        scratch_shapes=[dma(2), dma(4, 3), dma(8), dma(9), dma(9)],
        compiler_params=params(0),
        name="project",
    )(normed, cotangent, weight, bias)


def attend_kernel(
    qkv_ref, mask_ref, live_ref, weights_ref, outer_ref,
    att_ref, logs_ref, peak_ref, wfull_ref, ofull_ref,
    out_ref, vt_ref, outer_all, local, send, recv, line_send, line_recv,
    outer_send, outer_recv, plane_send, plane_recv,
):
    place = Place()
    greet(place, mp_all=True, plane=True)
    outer = line_gather(
        place, outer_ref, outer_all, local.at[2], outer_send, outer_recv, False, None, 48
    )
    next(outer)
    gather = line_gather(
        place, weights_ref, wfull_ref, local.at[1], line_send, line_recv, False
    )
    next(gather)
    factor = math.log2(math.e) / math.sqrt(HD)
    peak_ref[...] = jnp.full(peak_ref.shape, MASK_VALUE, F32)

    @pl.loop(0, 6)
    def _(turn):
        clip = turn // 2
        head = turn % 2
        lane = pl.multiple_of(head * 128, 128)
        row = pl.multiple_of(head * HD, 16)
        keys = qkv_ref[:, clip, :, pl.ds(256 + lane, 128)].reshape(1024, 128)
        vt_ref[...] = qkv_ref[:, clip, :, pl.ds(512 + lane, 128)].reshape(1024, 128).T

        @pl.loop(0, 4)
        def _(block):
            query = qkv_ref[pl.ds(block * 2, 2), clip, :, pl.ds(lane, 128)].reshape(256, 128)
            columns = pl.ds(pl.multiple_of(block * 256, 256), 256)
            scores = lax.dot_general(
                keys, query, (((1,), (1,)), ((), ())), preferred_element_type=F32
            )
            scores = scores + mask_ref[clip]
            peak = jnp.max(scores, axis=0, keepdims=True)
            powers = jnp.exp2((scores - peak) * factor)
            total = jnp.sum(powers, axis=0, keepdims=True)
            mixed = lax.dot_general(
                vt_ref[...],
                powers.astype(BF),
                (((1,), (0,)), ((), ())),
                preferred_element_type=F32,
            )
            mixed = (mixed / total).astype(BF)
            for part in range(2):
                out_ref[block * 2 + part, clip, pl.ds(row, HD)] = mixed[
                    :HD, part * 128 : part * 128 + 128
                ]
            logs_ref[turn, :, columns] = peak * factor + jnp.log2(total)
            peak_ref[head] = jnp.maximum(
                peak_ref[head], jnp.where(live_ref[clip, :, columns] > 0, peak, MASK_VALUE)
            )

        @pl.when(turn == 2)
        def _():
            next(outer)

        @pl.when(turn == 4)
        def _():
            next(outer)
            next(gather)

    mixing = exchange(place, out_ref, att_ref, local.at[0], send, recv)
    next(mixing)
    for _ in outer:
        pass
    spread = plane_gather(place, outer_all, ofull_ref, local.at[3], plane_send, plane_recv)
    drive(spread, gather, mixing)


def attend(qkv, mask, live, weights, outer):
    return pl.pallas_call(
        attend_kernel,
        out_shape=(
            jax.ShapeDtypeStruct((8, 3, 160, 128), BF),
            jax.ShapeDtypeStruct((6, 1, 1024), F32),
            jax.ShapeDtypeStruct((2, 8, 256), F32),
            jax.ShapeDtypeStruct((4,) + weights.shape, BF),
            jax.ShapeDtypeStruct((8, 192, 1280), BF),
        ),
        in_specs=[VMEM, VMEM, VMEM, ANY, ANY],
        out_specs=(VMEM, VMEM, VMEM, ANY, ANY),
        scratch_shapes=[
            pltpu.VMEM((8, 3, 160, 128), BF),
            pltpu.VMEM((128, 1024), BF),
            pltpu.VMEM((192, 1280), BF),
            dma(4),
            dma(8),
            dma(8),
            dma(4, 3),
            dma(4),
            dma(4, 3),
            dma(4),
            dma(9),
            dma(9),
        ],
        compiler_params=params(1),
        name="attend",
    )(qkv, mask, live, weights, outer)


def flatten(*pairs):
    names, shapes = [], []
    for number, group in enumerate(pairs):
        for name, shape in group.items():
            names.append((number, name))
            shapes.append(shape)

    def split(refs):
        groups = [{} for _ in pairs]
        for (number, name), ref in zip(names, refs):
            groups[number][name] = ref
        return groups

    return shapes, split


def feed_forward_kernel(
    split, normed_ref, upstream_ref, weights_ref, bias_ref,
    total_ref, hidden_ref, grads_ref, bias_out,
    normed_all, upstream_all, slope_all, sum_ref, load, local, gather_send, gather_recv, *scratch,
):
    place = Place()
    bufs, sems = split(scratch)
    loads = []
    for slot in range(8):
        loads.append(
            pltpu.make_async_copy(upstream_ref.at[slot], upstream_all.at[slot], load.at[slot])
        )
        loads[-1].start()
    greet(place, plane=True)
    bias_out[...] = jnp.zeros(bias_out.shape, F32)

    def up_rows():
        return weights_ref[:, pl.ds(0, 160)].reshape(640, 1280)

    def down_rows():
        return weights_ref[:, pl.ds(160, 160)].reshape(640, 1280)

    def ready(slot):
        @pl.loop(0, 3)
        def _(step):
            rows = pl.ds(step * 128, 128)
            before = (
                lax.dot_general(
                    normed_all[slot, rows],
                    up_rows(),
                    (((1,), (1,)), ((), ())),
                    preferred_element_type=F32,
                )
                + bias_ref[...]
            )
            pull = lax.dot_general(
                upstream_all[slot, rows],
                down_rows(),
                (((1,), (1,)), ((), ())),
                preferred_element_type=F32,
            )
            share = 0.5 + 0.5 * lax.erf(before * math.sqrt(0.5))
            hidden_ref[slot, rows] = (before * share).astype(BF)
            density = jnp.exp(before * before * -0.5) * (1.0 / math.sqrt(2.0 * math.pi))
            slope = (pull * (share + before * density)).astype(BF)
            slope_all[slot, rows] = slope
            bias_out[...] += jnp.sum(slope.astype(F32), axis=0, keepdims=True)

    gather = plane_gather(
        place, normed_ref, normed_all, local, gather_send, gather_recv, ready
    )

    def produce(group, core, start):
        return jnp.dot(
            slope_all[group * 2 + core, pl.ds(start, 192)],
            up_rows(),
            preferred_element_type=F32,
        )

    def result(rows, total):
        total_ref[rows] = total

    reduce = plane_reduce(place, produce, 192, 192, result, bufs, sems, True, True)
    next(gather)
    for copy in loads:
        copy.wait()
    next(gather)
    next(reduce)
    next(gather)
    next(reduce)
    next(gather)
    next(reduce)

    def weight_grads(left_all, right_all, base):
        for block in range(5):
            lanes = pl.ds(block * 128, 128)

            @pl.loop(0, 8)
            def _(slot):
                product = lax.dot_general(
                    left_all[slot, :, lanes],
                    right_all[slot],
                    (((0,), (0,)), ((), ())),
                    preferred_element_type=F32,
                )
                sum_ref[...] = jnp.where(slot == 0, product, sum_ref[...] + product)

            for part in range(4):
                unit = block * 128 + part * 32
                grads_ref[unit // 160, pl.ds(base + unit % 160, 32)] = sum_ref[
                    pl.ds(part * 32, 32)
                ].astype(BF)

    weight_grads(slope_all, normed_all, 0)
    next(reduce)
    weight_grads(hidden_ref, upstream_all, 160)
    for level in range(4):
        grads_ref[level, pl.ds(320, 16)] = jnp.zeros((16, 1280), BF)
        grads_ref[level, pl.ds(320, 16), pl.ds(0, 640)] = jnp.broadcast_to(
            bias_out[...], (16, 640)
        ).astype(BF)
    drive(reduce, gather)


def feed_forward(normed, upstream, weights, bias):
    shapes, split = flatten(*plane_reduce_scratch(192, 1280))
    return pl.pallas_call(
        functools.partial(feed_forward_kernel, split),
        out_shape=(
            jax.ShapeDtypeStruct((ROWS, 1280), F32),
            jax.ShapeDtypeStruct((8, ROWS, 640), BF),
            jax.ShapeDtypeStruct((4, 336, 1280), BF),
            jax.ShapeDtypeStruct((1, 640), F32),
        ),
        in_specs=[ANY, ANY, VMEM, VMEM],
        out_specs=(VMEM,) * 4,
        scratch_shapes=[
            pltpu.VMEM((8, ROWS, 1280), BF),
            pltpu.VMEM((8, ROWS, 1280), BF),
            pltpu.VMEM((8, ROWS, 640), BF),
            pltpu.VMEM((128, 1280), F32),
            dma(8),
            pltpu.SemaphoreType.DMA(()),
            dma(9),
            dma(9),
            *shapes,
        ],
        compiler_params=params(3, 60),
        name="feed_forward",
    )(normed, upstream, weights, bias)


def attend_back_kernel(
    split, qkv_ref, mask_ref, logs_ref, pull_ref, hidden_ref, weights_ref, feed_grads_ref,
    out_grad_ref, dqkv_ref, feed_ref, feed_sum_ref, out_sum_ref,
    grad_ref, kt_ref, dk_ref, dv_ref, block_ref, middle_ref, local, send, recv, *scratch,
):
    place = Place()
    (
        line_bufs, line_sems, plane_bufs, plane_sems,
        out_plane_bufs, out_plane_sems, out_line_bufs, out_line_sems,
    ) = split(scratch)
    greet(place, mp_all=True, plane=True)
    scale = 1.0 / math.sqrt(HD)
    factor = math.log2(math.e) * scale
    arriving = exchange(place, pull_ref, grad_ref, local, send, recv)
    next(arriving)

    def feed_block(group, core, start):
        return jnp.dot(
            hidden_ref[group * 2 + core, pl.ds(start, 192)],
            weights_ref[:, pl.ds(160, 160)].reshape(640, 1280),
            preferred_element_type=F32,
        )

    def feed_result(rows, total):
        feed_ref[rows] = total

    def sum_result(rows, total):
        feed_sum_ref[rows] = total

    plane = plane_reduce(
        place, feed_block, 192, 192, feed_result, plane_bufs, plane_sems, True
    )
    line = line_reduce(
        place,
        lambda level, core, rows: feed_grads_ref[level, rows].astype(F32),
        [pl.ds(start, 112) for start in range(0, 336, 112)],
        sum_result,
        line_bufs,
        line_sems,
        False,
    )
    def middle(rows, total):
        middle_ref[rows] = total

    def out_result(rows, total):
        out_sum_ref[rows] = total

    out_plane = plane_reduce(
        place,
        lambda group, core, start: out_grad_ref[group, core, pl.ds(start, 96)].astype(F32),
        96,
        96,
        middle,
        out_plane_bufs,
        out_plane_sems,
    )
    out_line = line_reduce(
        place,
        lambda level, core, rows: middle_ref[
            pl.ds(pl.multiple_of(level * 48 + rows.start, 16), rows.size)
        ],
        [pl.ds(0, 48)],
        out_result,
        out_line_bufs,
        out_line_sems,
        False,
    )
    next(line)
    next(line)
    next(plane)
    next(plane)
    next(out_plane)
    for _ in arriving:
        pass
    block_ref[...] = jnp.zeros(block_ref.shape, BF)

    @pl.loop(0, 6)
    def _(turn):
        clip = turn // 2
        head = turn % 2
        lane = pl.multiple_of(head * 128, 128)
        row = pl.multiple_of(head * HD, 16)
        kt_ref[...] = qkv_ref[:, clip, :, pl.ds(256 + lane, 128)].reshape(1024, 128).T
        dk_ref[...] = jnp.zeros(dk_ref.shape, F32)
        dv_ref[...] = jnp.zeros(dv_ref.shape, F32)

        @pl.loop(0, 4)
        def _(block):
            query = qkv_ref[pl.ds(block * 2, 2), clip, :, pl.ds(lane, 128)].reshape(256, 128)
            values = qkv_ref[:, clip, :, pl.ds(512 + lane, 128)].reshape(1024, 128)
            keys = qkv_ref[:, clip, :, pl.ds(256 + lane, 128)].reshape(1024, 128)
            columns = pl.ds(pl.multiple_of(block * 256, 256), 256)
            for part in range(2):
                block_ref[:HD, part * 128 : part * 128 + 128] = grad_ref[
                    block * 2 + part, clip, pl.ds(row, HD)
                ]
            scores = lax.dot_general(
                keys, query, (((1,), (1,)), ((), ())), preferred_element_type=F32
            )
            chance = jnp.exp2((scores + mask_ref[clip]) * factor - logs_ref[turn, :, columns])
            dv_ref[...] += lax.dot_general(
                chance.astype(BF),
                block_ref[...],
                (((1,), (1,)), ((), ())),
                preferred_element_type=F32,
            )
            slope = lax.dot_general(
                values, block_ref[...], (((1,), (0,)), ((), ())), preferred_element_type=F32
            )
            center = jnp.sum(chance * slope, axis=0, keepdims=True)
            change = (chance * (slope - center)).astype(BF)
            dk_ref[...] += lax.dot_general(
                change, query, (((1,), (0,)), ((), ())), preferred_element_type=F32
            )
            dq = lax.dot_general(
                kt_ref[...], change, (((1,), (0,)), ((), ())), preferred_element_type=F32
            )
            dqkv_ref[pl.ds(block * 2, 2), clip, :, pl.ds(lane, 128)] = (
                (dq.T * scale).astype(BF).reshape(2, 128, 128)
            )

        dqkv_ref[:, clip, :, pl.ds(256 + lane, 128)] = (
            (dk_ref[...] * scale).astype(BF).reshape(8, 128, 128)
        )
        dqkv_ref[:, clip, :, pl.ds(512 + lane, 128)] = (
            dv_ref[...].astype(BF).reshape(8, 128, 128)
        )

        @pl.when(turn == 1)
        def _():
            next(out_plane)

        @pl.when(turn == 2)
        def _():
            next(plane)

        @pl.when(turn == 3)
        def _():
            next(line)

        @pl.when(turn == 4)
        def _():
            next(out_plane)

    drive(out_plane)
    drive(out_line, line, plane)


def attend_back(qkv, mask, logs, pull, hidden, weights, feed_grads, out_grad):
    shapes, split = flatten(
        *line_reduce_scratch(336, 1280, False),
        *plane_reduce_scratch(192, 1280),
        *plane_reduce_scratch(96, 1280),
        *line_reduce_scratch(48, 1280, False),
    )
    return pl.pallas_call(
        functools.partial(attend_back_kernel, split),
        out_shape=(
            jax.ShapeDtypeStruct(qkv.shape, BF),
            jax.ShapeDtypeStruct((ROWS, 1280), F32),
            jax.ShapeDtypeStruct((336, 1280), F32),
            jax.ShapeDtypeStruct((48, 1280), F32),
        ),
        in_specs=[VMEM, VMEM, VMEM, ANY, VMEM, VMEM, VMEM, VMEM],
        out_specs=(VMEM,) * 4,
        scratch_shapes=[
            pltpu.VMEM((8, 3, 160, 128), BF),
            pltpu.VMEM((128, 1024), BF),
            pltpu.VMEM((1024, 128), F32),
            pltpu.VMEM((1024, 128), F32),
            pltpu.VMEM((128, 256), BF),
            pltpu.VMEM((192, 1280), F32),
            pltpu.SemaphoreType.DMA(()),
            dma(8),
            dma(8),
            *shapes,
        ],
        compiler_params=params(2, 62),
        name="attend_back",
    )(qkv, mask, logs, pull, hidden, weights, feed_grads, out_grad)


GROUP_ROWS = 4832
GROUP_STEP = 4800
PACK_ROWS = GROUP_STEP * 3 + GROUP_ROWS
SEGMENTS = (
    ("query", 0, 1600),
    ("query_bias", 204800, 2),
    ("key", 204960, 1600),
    ("value", 409760, 1600),
    ("value_bias", 614560, 2),
    ("out", 614720, 1600),
    ("up", 819520, 6400),
    ("up_bias", 1638720, 5),
    ("down", 1639360, 6400),
)
PACK_END = 19216


def segment_table():
    table, cursor = {}, 0
    for name, start, rows in SEGMENTS:
        row = start // 128
        cursor += 32
        cursor += (row - cursor) % 8
        table[name] = (cursor, row, rows, start % 128)
        cursor += rows
    return table, (cursor + 32 + 7) // 8 * 8


TABLE, STAGE_ROWS = segment_table()


def lane_of(rows):
    return lax.broadcasted_iota(jnp.int32, (rows, 128), 1)


def pack_rows(stage, packed):
    def piece(name, first, rows):
        base, row, _, shift = TABLE[name]
        at = base - row + first
        here = stage[pl.ds(at, rows)]
        if shift == 0:
            return here
        above = stage[pl.ds(at - 1, rows)]
        return jnp.where(
            lane_of(rows) >= shift, pltpu.roll(here, shift, 1), pltpu.roll(above, shift, 1)
        )

    done = set()
    for name, _, _ in SEGMENTS:
        _, row, rows, shift = TABLE[name]
        low = -(-(row + (1 if shift else 0)) // 16) * 16
        high = (row + rows) // 16 * 16
        if high <= low:
            continue
        done.update(range(low, high, 16))
        turns = (high - low) // 128

        @pl.loop(0, turns)
        def _(turn):
            first = pl.multiple_of(low + turn * 128, 16)
            packed[pl.ds(first, 128)] = piece(name, first, 128).astype(BF)

        for first in range(low + turns * 128, high, 16):
            packed[pl.ds(first, 16)] = piece(name, first, 16).astype(BF)
    for first in range(0, PACK_ROWS, 16):
        if first in done:
            continue
        total = jnp.zeros((16, 128), F32)
        for name, _, _ in SEGMENTS:
            _, row, rows, shift = TABLE[name]
            if row < first + 16 and row + rows + (1 if shift else 0) > first:
                total = total + piece(name, first, 16)
        packed[pl.ds(first, 16)] = total.astype(BF)


def stage_wide(stage, name, ref, step):
    base = TABLE[name][0]
    rows, wide = ref.shape[0], ref.shape[1] // 128

    @pl.loop(0, rows // step)
    def _(turn):
        first = pl.multiple_of(turn * step, step)
        for block in range(wide):
            stage[pl.ds(base + first * wide + block, step, stride=wide), :] = ref[
                pl.ds(first, step), pl.ds(block * 128, 128)
            ].astype(F32)


def stage_heads(stage, name, ref, lanes, column):
    base = TABLE[name][0]
    for head in range(2):
        column[head] = ref[:, pl.ds(lanes + head * 128, 128)]

    @pl.loop(0, 5)
    def _(turn):
        lane = lane_of(64)
        rows = [jnp.zeros((64, 128), F32) for _ in range(5)]
        for block in range(8):
            item, head = block // 2, block % 2
            value = column[head, pl.ds(turn * 256 + item, 64, stride=4)]
            offset = block * HD
            first, shift = offset // 128, offset % 128
            if shift:
                value = pltpu.roll(value, shift, 1)
            if shift + HD > 128:
                rows[first] = rows[first] + jnp.where(lane >= shift, value, 0.0)
                rows[first + 1] = rows[first + 1] + jnp.where(
                    lane < shift + HD - 128, value, 0.0
                )
            else:
                rows[first] = rows[first] + value
        for index in range(5):
            stage[pl.ds(base + turn * 320 + index, 64, stride=5), :] = rows[index]


def stage_head_bias(stage, name, ref, lanes):
    base = TABLE[name][0]
    lane = lane_of(1)
    first = ref[0:1, pl.ds(lanes, 128)]
    second = pltpu.roll(ref[0:1, pl.ds(lanes + 128, 128)], HD, 1)
    stage[pl.ds(base, 1)] = first + jnp.where(lane >= HD, second, 0.0)
    stage[pl.ds(base + 1, 1)] = jnp.where(lane < 2 * HD - 128, second, 0.0)


def stage_share(stage, name, ref, first, count, place):
    base = TABLE[name][0] + place.dp * count * 10
    for block in range(10):
        stage[pl.ds(base + block, count, stride=10), :] = ref[
            pl.ds(first, count), pl.ds(block * 128, 128)
        ]


def stage_up(stage, ref, place):
    base = TABLE["up"][0]
    lane = lane_of(128)
    for quarter in range(4):

        @pl.when(place.dp == quarter)
        def _():
            for block in range(10):
                columns = pl.ds(block * 128, 128)
                first = ref[pl.ds(0, 128), columns].T
                second = jnp.where(lane < 32, ref[pl.ds(128, 128), columns].T, 0.0)
                shift = 32 * quarter
                if shift:
                    first = pltpu.roll(first, shift, 1)
                    second = pltpu.roll(second, shift, 1)
                    second = second + jnp.where(lane < shift, first, 0.0)
                    first = jnp.where(lane >= shift, first, 0.0)
                at = base + block * 640 + quarter
                stage[pl.ds(at, 128, stride=5), :] = first
                stage[pl.ds(at + 1, 128, stride=5), :] = second


def finish_kernel(
    split, grad_ref, weight_ref, joined_ref, bias_ref, sum_ref, out_ref, up_bias_ref,
    small_ref, peak_ref, frames_ref, middle_ref, gain_ref,
    input_grad_ref, grads_ref, small_out, peak_out,
    stage, packed, column, gains, tiles, small_in, small_all, peak_all, edge,
    local, small_send, small_recv, plane_send, plane_recv, *scratch,
):
    place = Place()
    line_bufs, line_sems, bufs, sems = split(scratch)
    greet(place, mp_all=True, plane=True)
    peers = (place.dpx, place.dpy, place.dpd)

    def tell(index, source, target, group, act):
        act(
            remote(
                source,
                target.at[place.dp],
                plane_send.at[index],
                plane_recv.at[index],
                group,
                place.mp,
            )
        )

    def heard(index, target, group):
        block = target.at[group]
        remote(
            block, block, plane_send.at[index], plane_recv.at[index], group, place.mp
        ).wait_recv()

    def produce_rows(level, core, rows):
        return jnp.dot(
            grad_ref[level * 2 + core, rows], weight_ref[...], preferred_element_type=F32
        )

    def norm_back(rows, total):
        value = frames_ref[rows].astype(F32)
        center = value - jnp.mean(value, axis=-1, keepdims=True)
        spread = jnp.mean(center * center, axis=-1, keepdims=True)
        root = lax.rsqrt(spread + NORM_EPSILON)
        scaled = center * root
        gains[pl.ds(0, 1)] += jnp.sum(total * scaled, axis=0, keepdims=True)
        gains[pl.ds(8, 1)] += jnp.sum(total, axis=0, keepdims=True)
        pull = total * gain_ref[...]
        along = jnp.mean(pull * scaled, axis=-1, keepdims=True)
        input_grad_ref[rows] = middle_ref[rows] + root * (
            pull - jnp.mean(pull, axis=-1, keepdims=True) - scaled * along
        )

    gains[...] = jnp.zeros(gains.shape, F32)
    line = line_reduce(
        place,
        produce_rows,
        [pl.ds(start, 128) for start in range(0, ROWS, 128)],
        norm_back,
        line_bufs,
        line_sems,
        True,
    )
    next(line)
    for index, group in enumerate(peers):
        tell(index, peak_ref, peak_all, group, lambda copy: copy.start())
    next(line)
    stage[...] = jnp.zeros(stage.shape, F32)
    for name, lanes in (("query", 0), ("key", 256), ("value", 512)):
        stage_heads(stage, name, joined_ref, lanes, column)
    stage_head_bias(stage, "query_bias", bias_ref, 0)
    stage_head_bias(stage, "value_bias", bias_ref, 512)
    stage_share(stage, "out", out_ref, 0, 40, place)
    stage_share(stage, "down", sum_ref, 160, 160, place)
    stage_up(stage, sum_ref, place)
    stage[pl.ds(TABLE["up_bias"][0], 5)] = up_bias_ref[...]
    pack_rows(stage, packed)

    def produce(group, core, start):
        first = pl.multiple_of(group * GROUP_STEP + start, 16)
        return packed[pl.ds(first, GROUP_ROWS // 2)].astype(F32)

    def result(rows, total):
        grads_ref[rows] = total

    half = GROUP_ROWS // 2
    plane = plane_reduce(place, produce, half, half, result, bufs, sems, False)
    next(plane)
    next(plane)
    next(line)
    next(plane)
    next(line)
    next(plane)
    drive(line, plane)

    for row in range(10):
        tiles[pl.ds(row, 1)] = gains[pl.ds(0, 1), pl.ds(row * 128, 128)]
        tiles[pl.ds(10 + row, 1)] = gains[pl.ds(8, 1), pl.ds(row * 128, 128)]
    tiles[pl.ds(20, 44)] = small_ref[...]
    for run in range(8):
        edge[run] = tiles[pl.ds(run * 15 // 2, 8)]
    mixing = exchange(place, edge, small_in, local, small_send, small_recv)
    for _ in mixing:
        pass
    small_all[place.dp] = jnp.sum(small_in[...], axis=0)
    for index, group in enumerate(peers):
        tell(3 + index, small_all.at[place.dp], small_all, group, lambda copy: copy.start())
    for index, group in enumerate(peers):
        heard(index, peak_all, group)
        heard(3 + index, small_all, group)
    top = peak_ref[...]
    for group in peers:
        top = jnp.maximum(top, peak_all[group])
    peak_out[...] = top
    whole = jnp.sum(small_all[...], axis=0)
    lane = lane_of(8)
    row = lax.broadcasted_iota(jnp.int32, (8, 128), 0)
    tiles[pl.ds(0, 64)] = jnp.zeros((64, 128), F32)
    tiles[pl.ds(8, 8)] = whole
    ahead = pltpu.roll(tiles[pl.ds(9, 8)], 64, 1)
    here = pltpu.roll(whole, 64, 1)
    odd = jnp.where(lane < 64, here, ahead)
    run_of = jnp.where(place.c == 1, odd, whole)
    run_of = jnp.where(jnp.logical_and(row == 7, lane >= 64), 0.0, run_of)
    small_out[...] = run_of
    tiles[pl.ds(8, 8)] = run_of
    wide = lane_of(16)
    entry = jnp.where(
        wide >= 64, pltpu.roll(tiles[pl.ds(1, 16)], 64, 1), pltpu.roll(tiles[pl.ds(0, 16)], 64, 1)
    )

    @pl.when(place.dp == 3)
    def _():
        grads_ref[pl.ds(GROUP_STEP, 16)] += entry

    for index, group in enumerate(peers):
        tell(index, peak_ref, peak_all, group, lambda copy: copy.wait_send())
        tell(3 + index, small_all.at[place.dp], small_all, group, lambda copy: copy.wait_send())


def finish(grads, weight, joined, bias, sums, out, up_bias, small, peaks, frames, middle, gain):
    shapes, split = flatten(
        *line_reduce_scratch(ROWS, 1280, True),
        *plane_reduce_scratch(GROUP_ROWS // 2, 128, False),
    )
    return pl.pallas_call(
        functools.partial(finish_kernel, split),
        out_shape=(
            jax.ShapeDtypeStruct((ROWS, 1280), F32),
            jax.ShapeDtypeStruct((GROUP_ROWS, 128), F32),
            jax.ShapeDtypeStruct((8, 128), F32),
            jax.ShapeDtypeStruct(peaks.shape, F32),
        ),
        in_specs=[VMEM] * 12,
        out_specs=(VMEM,) * 4,
        scratch_shapes=[
            pltpu.VMEM((STAGE_ROWS, 128), F32),
            pltpu.VMEM((PACK_ROWS, 128), BF),
            pltpu.VMEM((2, 1280, 128), F32),
            pltpu.VMEM((16, 1280), F32),
            pltpu.VMEM((64, 128), F32),
            pltpu.VMEM((8, 8, 128), F32),
            pltpu.VMEM((4, 8, 128), F32),
            pltpu.VMEM((4,) + peaks.shape, F32),
            pltpu.VMEM((8, 8, 128), F32),
            pltpu.SemaphoreType.DMA(()),
            dma(8),
            dma(8),
            dma(6),
            dma(6),
            *shapes,
        ],
        compiler_params=params(7, 62),
        name="finish",
    )(grads, weight, joined, bias, sums, out, up_bias, small, peaks, frames, middle, gain)


def share_master_kernel(rows_ref, whole_ref, parts, send, recv):
    place = Place()
    greet(place, plane=True, pair=False)
    dp, mp, dpx, dpy, dpd = place.dp, place.mp, place.dpx, place.dpy, place.dpd
    half = GROUP_ROWS // 2
    part_a, part_b = pl.ds(0, half), pl.ds(half, half)
    parts[dp] = rows_ref[...].astype(BF)

    def hop(index, block, target):
        return remote(block, block, send.at[index], recv.at[index], target, mp)

    own = parts.at[dp]
    sends = [hop(0, own, dpx), hop(1, own, dpy)]
    for copy in sends:
        copy.start()
    hop(0, parts.at[dpx], dpx).wait_recv()
    sends.append(hop(2, parts.at[dpx, part_a], dpy))
    sends[-1].start()
    hop(1, parts.at[dpy], dpy).wait_recv()
    sends.append(hop(3, parts.at[dpy, part_b], dpx))
    sends[-1].start()
    hop(2, parts.at[dpd, part_a], dpy).wait_recv()
    hop(3, parts.at[dpd, part_b], dpx).wait_recv()
    for group in range(4):
        base = group * GROUP_STEP
        first = parts[group, pl.ds(0, 32)].astype(F32)
        if group > 0:
            first = first + parts[group - 1, pl.ds(GROUP_STEP, 32)].astype(F32)
        whole_ref[pl.ds(base, 32)] = first
        for start in range(32, GROUP_STEP, 1192):
            whole_ref[pl.ds(base + start, 1192)] = parts[group, pl.ds(start, 1192)].astype(F32)
    whole_ref[pl.ds(4 * GROUP_STEP, 16)] = parts[3, pl.ds(GROUP_STEP, 16)].astype(F32)
    for copy in sends:
        copy.wait_send()


def share_master(rows):
    return pl.pallas_call(
        share_master_kernel,
        out_shape=jax.ShapeDtypeStruct((PACK_END, 128), F32),
        in_specs=[VMEM],
        out_specs=VMEM,
        scratch_shapes=[pltpu.VMEM((4, GROUP_ROWS, 128), BF), dma(4), dma(4)],
        compiler_params=params(8, 60),
        name="share_master",
    )(rows)


def fast_body(
    frames,
    lengths,
    key_mask,
    cotangent,
    gain_one,
    shift_one,
    query_weight,
    query_bias,
    key_weight,
    value_weight,
    value_bias,
    out_weight,
    out_bias,
    gain_two,
    shift_two,
    up_weight,
    up_bias,
    down_weight,
    down_bias,
    master,
    moment_one,
    moment_two,
    adam_step,
    hyper_rates,
):
    group = lax.axis_index("dp")
    position = jnp.arange(1024, dtype=jnp.int32)
    keep_query = position[None, :] < lengths[:, None]
    keep_key = jnp.logical_and(keep_query, key_mask == 1)
    mask = jnp.where(keep_key, 0.0, MASK_VALUE)[:, :, None]
    live = keep_query.astype(F32)[:, None, :]
    gain_first = gain_one.astype(F32)
    shift_first = shift_one.astype(F32)
    gain_second = gain_two.astype(F32)
    shift_second = shift_two.astype(F32)
    inputs = frames.transpose(1, 0, 2).reshape(ROWS, 1280).astype(F32)
    upstream_low = cotangent.transpose(1, 0, 2).reshape(ROWS, 1280)
    upstream = upstream_low.astype(F32)
    normed = layer_norm(inputs, gain_first, shift_first).astype(BF)

    def head_rows(weight):
        rows = weight.T.reshape(2, HD, 1280)
        return jnp.pad(rows, ((0, 0), (0, 128 - HD), (0, 0))).reshape(256, 1280)

    def head_lanes(bias):
        lanes = bias.astype(F32).reshape(2, HD)
        return jnp.pad(lanes, ((0, 0), (0, 128 - HD))).reshape(256)

    joined_weight = jnp.concatenate(
        [head_rows(query_weight), head_rows(key_weight), head_rows(value_weight)]
    )
    joined_bias = jnp.concatenate(
        [head_lanes(query_bias), jnp.zeros((256,), F32), head_lanes(value_bias)]
    )[None]
    normed_full, qkv, upstream_full = project(normed, upstream_low, joined_weight, joined_bias)
    qkv = qkv.reshape(8, 3, 128, 768)

    quarter = group * 160
    up_share = lax.dynamic_slice_in_dim(up_weight, quarter, 160, 1).T
    down_share = lax.dynamic_slice_in_dim(down_weight, quarter, 160, 0)
    bias_share = lax.dynamic_slice_in_dim(up_bias, quarter, 160, 0)
    bias_rows = jnp.pad(bias_share[None], ((0, 15), (0, 1280 - 160)))
    message = jnp.concatenate([up_share, down_share, bias_rows])
    outer = jnp.pad(lax.dynamic_slice_in_dim(out_weight, group * 40, 40, 0), ((0, 8), (0, 0)))
    attended, logs, peaks, gathered, outer_all = attend(qkv, mask, live, message, outer)
    up_lanes = gathered[:, 320, :160].reshape(1, 640).astype(F32)
    out_rows = outer_all.reshape(4, 2, 4, 48, 1280)[:, :, :, :40]
    out_rows = out_rows.transpose(2, 1, 0, 3, 4).reshape(8, 160, 1280)

    branch = jnp.einsum("schr,shd->crd", attended, out_rows, preferred_element_type=F32)
    middle = inputs + branch.reshape(ROWS, 1280) + out_bias.astype(F32)
    normed_two = layer_norm(middle, gain_second, shift_second).astype(BF)
    normed_two_grad, hidden, feed_grads, _ = feed_forward(
        normed_two, upstream_full, gathered, up_lanes
    )

    _, norm_two_pull = jax.vjp(layer_norm, middle, gain_second, shift_second)
    middle_norm_grad, gain_two_grad, shift_two_grad = norm_two_pull(normed_two_grad)
    middle_grad = upstream + middle_norm_grad
    branch_grad = middle_grad.astype(BF)
    branch_clips = branch_grad.reshape(3, 128, 1280)
    out_grad = jnp.einsum("schr,crd->shd", attended, branch_clips, preferred_element_type=F32)
    attended_grad = jnp.einsum(
        "shd,crd->schr", out_rows, branch_clips, preferred_element_type=F32
    ).astype(BF)
    out_quarters = jnp.pad(
        out_grad.astype(BF).reshape(4, 2, 4, 40, 1280), ((0, 0),) * 3 + ((0, 8), (0, 0))
    )
    out_quarters = out_quarters.transpose(2, 1, 0, 3, 4).reshape(4, 2, 192, 1280)
    joined_grad, feed, feed_sum, out_sum = attend_back(
        qkv, mask, logs, attended_grad, hidden, gathered, feed_grads, out_quarters
    )
    layer_out = (middle + feed + down_bias.astype(F32)).astype(BF)
    joined_grad = joined_grad.reshape(8, ROWS, 768)
    joined_weight_grad = jnp.einsum(
        "prd,pre->de", normed_full, joined_grad, preferred_element_type=F32
    )
    joined_bias_grad = jnp.sum(joined_grad.astype(F32), axis=(0, 1))

    level = lax.axis_index("mp") // 2
    up_bias_share = lax.dynamic_slice_in_dim(feed_sum[320], level * 160, 160, 0)
    up_bias_rows = lax.dynamic_update_slice(
        jnp.zeros((640,), F32), up_bias_share, (quarter,)
    ).reshape(5, 128)
    small_rows = jnp.concatenate(
        [
            jnp.sum(branch_grad.astype(F32), axis=0),
            gain_two_grad,
            shift_two_grad,
            jnp.sum(upstream, axis=0),
            jnp.zeros((512,), F32),
        ]
    ).reshape(44, 128)
    input_grad, grad_rows, small_sum, peak_sum = finish(
        joined_grad,
        joined_weight,
        joined_weight_grad,
        joined_bias_grad[None],
        feed_sum,
        out_sum,
        up_bias_rows,
        small_rows,
        peaks,
        frames.transpose(1, 0, 2).reshape(ROWS, 1280),
        middle_grad,
        gain_first[None],
    )
    small_total = small_sum.reshape(1024)[:960]
    head_peak = jnp.max(peak_sum, axis=(1, 2)) / math.sqrt(HD)
    share_size = master.shape[1]
    owned_grads = lax.dynamic_slice(
        grad_rows.reshape(1, GROUP_ROWS * 128), (0, 480 * group), (1, share_size)
    )
    learn_rate = hyper_rates[0]
    weight_decay = hyper_rates[1]
    logit_cap = hyper_rates[2]
    step_count = adam_step[0].astype(F32)
    first_new = BETA_FIRST * moment_one + (1.0 - BETA_FIRST) * owned_grads
    second_new = BETA_SECOND * moment_two + (1.0 - BETA_SECOND) * owned_grads * owned_grads
    first_hat = first_new * (learn_rate / (1.0 - jnp.power(BETA_FIRST, step_count)))
    second_hat = second_new * (1.0 / (1.0 - jnp.power(BETA_SECOND, step_count)))
    entry_index = group * share_size + lax.broadcasted_iota(jnp.int32, (1, share_size), 1)
    query_end = 1280 * 160
    query_bias_end = query_end + 160
    key_end = query_bias_end + 1280 * 160
    block = jnp.floor((entry_index.astype(F32) + 0.5) * (1.0 / HD))
    odd = block - 2.0 * jnp.floor(block * 0.5) > 0.5
    root_factor = jnp.sqrt(logit_cap / jnp.maximum(head_peak, logit_cap))
    head_factor = jnp.where(odd, root_factor[1], root_factor[0])
    factor = jnp.where(entry_index < key_end, head_factor, 1.0)
    master_new = (
        master * (1.0 - learn_rate * weight_decay)
        - first_hat / (jnp.sqrt(second_hat) + ADAM_EPSILON)
    ) * factor

    def placed_rows(offset):
        room = GROUP_ROWS * 128 - share_size - offset
        return lambda value: jnp.pad(value, ((0, 0), (offset, room))).reshape(GROUP_ROWS, 128)

    master_rows = lax.switch(group, [placed_rows(480 * part) for part in range(4)], master_new)
    whole = share_master(master_rows).reshape(1, PACK_END * 128)
    whole = lax.optimization_barrier(whole)
    weights_new = whole[:, : 4 * share_size].astype(BF)
    return (
        layer_out.reshape(3, 128, 1280).transpose(1, 0, 2),
        input_grad.reshape(3, 128, 1280).transpose(1, 0, 2),
        owned_grads,
        master_new,
        first_new,
        second_new,
        weights_new,
        small_total,
    )


def body(
    frames,
    lengths,
    key_mask,
    cotangent,
    gain_one,
    shift_one,
    query_weight,
    query_bias,
    key_weight,
    value_weight,
    value_bias,
    out_weight,
    out_bias,
    gain_two,
    shift_two,
    up_weight,
    up_bias,
    down_weight,
    down_bias,
    master,
    moment_one,
    moment_two,
    adam_step,
    hyper_rates,
):
    local_rows, clip_count, model_width = frames.shape
    total_rows = key_mask.shape[1]
    head_cols = query_weight.shape[1]
    heads_here = head_cols // HD
    block_rows = min(512, total_rows)
    blocks = total_rows // block_rows
    score_scale = 1.0 / math.sqrt(HD)
    position = jnp.arange(total_rows, dtype=jnp.int32)
    keep_query = position[None, :] < lengths[:, None]
    keep_key = jnp.logical_and(keep_query, key_mask == 1)
    gain_first = gain_one.astype(jnp.float32)
    shift_first = shift_one.astype(jnp.float32)
    gain_second = gain_two.astype(jnp.float32)
    shift_second = shift_two.astype(jnp.float32)
    inputs = frames.astype(jnp.float32)
    normed = layer_norm(inputs, gain_first, shift_first).astype(jnp.bfloat16)
    joined_weight = jnp.concatenate([query_weight, key_weight, value_weight], axis=1)
    joined_bias = jnp.concatenate(
        [
            query_bias.astype(jnp.float32),
            jnp.zeros((head_cols,), jnp.float32),
            value_bias.astype(jnp.float32),
        ]
    )
    normed_full = lax.all_gather(normed, "mp", axis=0, tiled=True)
    projected = (
        jnp.einsum("rcd,de->rce", normed_full, joined_weight, preferred_element_type=jnp.float32)
        + joined_bias
    ).astype(jnp.bfloat16)
    query = projected[:, :, :head_cols].reshape(total_rows, clip_count, heads_here, HD)
    keys = projected[:, :, head_cols : 2 * head_cols].reshape(
        total_rows, clip_count, heads_here, HD
    )
    values = projected[:, :, 2 * head_cols :].reshape(total_rows, clip_count, heads_here, HD)

    def scores_of(row_start):
        query_block = lax.dynamic_slice_in_dim(query, row_start, block_rows, 0)
        raw_scores = (
            jnp.einsum("qchd,kchd->chqk", query_block, keys, preferred_element_type=jnp.float32)
            * score_scale
        )
        return (query_block, jnp.where(keep_key[:, None, None, :], raw_scores, MASK_VALUE))

    def forward_block(block_index):
        row_start = block_index * block_rows
        _, masked = scores_of(row_start)
        row_peak = jnp.max(masked, axis=-1, keepdims=True)
        exp_scores = jnp.exp(masked - row_peak)
        row_total = jnp.sum(exp_scores, axis=-1, keepdims=True)
        probability = (exp_scores / row_total).astype(jnp.bfloat16)
        attended = jnp.einsum(
            "chqk,kchd->qchd", probability, values, preferred_element_type=jnp.float32
        ).astype(jnp.bfloat16)
        live_rows = lax.dynamic_slice_in_dim(keep_query, row_start, block_rows, 1)
        block_peak = jnp.max(
            jnp.where(live_rows[:, None, :], row_peak[..., 0], MASK_VALUE), axis=(0, 2)
        )
        return (attended, (row_peak + jnp.log(row_total))[..., 0], block_peak)

    attended_blocks, log_totals, block_peaks = lax.map(forward_block, jnp.arange(blocks))
    attended_full = attended_blocks.reshape(total_rows, clip_count, head_cols)
    head_peak = lax.pmax(jnp.max(block_peaks, axis=0), "dp")
    rows_here = attended_full
    attn_branch = lax.psum_scatter(
        jnp.einsum("rck,kd->rcd", rows_here, out_weight, preferred_element_type=jnp.float32),
        "mp",
        scatter_dimension=0,
        tiled=True,
    ) + out_bias.astype(jnp.float32)
    middle = inputs + attn_branch
    normed_two = layer_norm(middle, gain_second, shift_second).astype(jnp.bfloat16)
    upstream = cotangent.astype(jnp.float32)
    normed_two_full = lax.all_gather(normed_two, "mp", axis=0, tiled=True)
    before = jnp.einsum(
        "rcd,df->rcf", normed_two_full, up_weight, preferred_element_type=jnp.float32
    ) + up_bias.astype(jnp.float32)
    hidden = exact_gelu(before).astype(jnp.bfloat16)
    rows_here = hidden
    feed = lax.psum_scatter(
        jnp.einsum(
            "rcf,fd->rcd", rows_here, down_weight, preferred_element_type=jnp.float32
        ).astype(jnp.bfloat16),
        "mp",
        scatter_dimension=0,
        tiled=True,
    ).astype(jnp.float32) + down_bias.astype(jnp.float32)
    layer_out = (middle + feed).astype(jnp.bfloat16)
    feed_grad_full = lax.all_gather(cotangent, "mp", axis=0, tiled=True)
    down_grad = jnp.einsum(
        "rcf,rcd->fd", hidden, feed_grad_full, preferred_element_type=jnp.float32
    )
    hidden_grad = jnp.einsum(
        "rcd,fd->rcf", feed_grad_full, down_weight, preferred_element_type=jnp.float32
    )
    _, gelu_pull = jax.vjp(exact_gelu, before)
    before_grad = gelu_pull(hidden_grad)[0].astype(jnp.bfloat16)
    up_bias_grad = jnp.sum(before_grad.astype(jnp.float32), axis=(0, 1))
    up_grad = jnp.einsum(
        "rcd,rcf->df", normed_two_full, before_grad, preferred_element_type=jnp.float32
    )
    rows_here = before_grad
    normed_two_grad = lax.psum_scatter(
        jnp.einsum("rcf,df->rcd", rows_here, up_weight, preferred_element_type=jnp.float32),
        "mp",
        scatter_dimension=0,
        tiled=True,
    )
    _, norm_two_pull = jax.vjp(layer_norm, middle, gain_second, shift_second)
    middle_norm_grad, gain_two_grad, shift_two_grad = norm_two_pull(normed_two_grad)
    middle_grad = upstream + middle_norm_grad
    branch_grad = middle_grad.astype(jnp.bfloat16)
    branch_grad_full = lax.all_gather(branch_grad, "mp", axis=0, tiled=True)
    out_grad = jnp.einsum(
        "rck,rcd->kd", attended_full, branch_grad_full, preferred_element_type=jnp.float32
    )
    attended_grad = jnp.einsum(
        "rcd,kd->rck", branch_grad_full, out_weight, preferred_element_type=jnp.float32
    ).astype(jnp.bfloat16)
    attended_grad = attended_grad.reshape(total_rows, clip_count, heads_here, HD)

    def backward_block(carry, block_index):
        key_total, value_total = carry
        row_start = block_index * block_rows
        query_block, masked = scores_of(row_start)
        log_total = log_totals[block_index]
        probability = jnp.exp(masked - log_total[..., None])
        grad_block = lax.dynamic_slice_in_dim(attended_grad, row_start, block_rows, 0)
        value_total = value_total + jnp.einsum(
            "chqk,qchd->kchd",
            probability.astype(jnp.bfloat16),
            grad_block,
            preferred_element_type=jnp.float32,
        )
        prob_grad = jnp.einsum(
            "qchd,kchd->chqk", grad_block, values, preferred_element_type=jnp.float32
        )
        score_grad = (
            probability * (prob_grad - jnp.sum(probability * prob_grad, axis=-1, keepdims=True))
        ).astype(jnp.bfloat16)
        query_grad = (
            jnp.einsum("chqk,kchd->qchd", score_grad, keys, preferred_element_type=jnp.float32)
            * score_scale
        ).astype(jnp.bfloat16)
        key_total = (
            key_total
            + jnp.einsum(
                "chqk,qchd->kchd", score_grad, query_block, preferred_element_type=jnp.float32
            )
            * score_scale
        )
        return ((key_total, value_total), query_grad)

    empty_grad = jnp.zeros((total_rows, clip_count, heads_here, HD), jnp.float32)
    (key_total, value_total), query_blocks = lax.scan(
        backward_block, (empty_grad, empty_grad), jnp.arange(blocks)
    )
    joined_grad = jnp.concatenate(
        [
            query_blocks.reshape(total_rows, clip_count, head_cols),
            key_total.reshape(total_rows, clip_count, head_cols).astype(jnp.bfloat16),
            value_total.reshape(total_rows, clip_count, head_cols).astype(jnp.bfloat16),
        ],
        axis=-1,
    )
    joined_bias_grad = jnp.sum(joined_grad.astype(jnp.float32), axis=(0, 1))
    normed_back = lax.all_gather(normed, "mp", axis=0, tiled=True)
    joined_weight_grad = jnp.einsum(
        "rcd,rce->de", normed_back, joined_grad, preferred_element_type=jnp.float32
    )
    rows_here = joined_grad
    normed_grad = lax.psum_scatter(
        jnp.einsum(
            "rce,de->rcd", rows_here, joined_weight, preferred_element_type=jnp.float32
        ).astype(jnp.bfloat16),
        "mp",
        scatter_dimension=0,
        tiled=True,
    ).astype(jnp.float32)
    _, norm_one_pull = jax.vjp(layer_norm, inputs, gain_first, shift_first)
    input_norm_grad, gain_one_grad, shift_one_grad = norm_one_pull(normed_grad)
    input_grad = middle_grad + input_norm_grad
    out_bias_grad = jnp.sum(branch_grad.astype(jnp.float32), axis=(0, 1))
    down_bias_grad = jnp.sum(upstream, axis=(0, 1))
    small_terms = jnp.concatenate(
        [
            gain_one_grad,
            shift_one_grad,
            out_bias_grad,
            gain_two_grad,
            shift_two_grad,
            down_bias_grad,
        ]
    )
    small_share = lax.psum_scatter(small_terms, "mp", scatter_dimension=0, tiled=True)
    small_total = lax.psum(small_share, "dp")
    packed = jnp.concatenate(
        [
            joined_weight_grad[:, :head_cols].reshape(-1),
            joined_bias_grad[:head_cols],
            joined_weight_grad[:, head_cols : 2 * head_cols].reshape(-1),
            joined_weight_grad[:, 2 * head_cols :].reshape(-1),
            joined_bias_grad[2 * head_cols :],
            out_grad.reshape(-1),
            up_grad.reshape(-1),
            up_bias_grad,
            down_grad.reshape(-1),
            small_share,
        ]
    )
    owned_grads = lax.psum_scatter(
        packed.astype(jnp.bfloat16), "dp", scatter_dimension=0, tiled=True
    ).astype(jnp.float32)
    share_size = owned_grads.shape[0]
    learn_rate = hyper_rates[0]
    weight_decay = hyper_rates[1]
    logit_cap = hyper_rates[2]
    step_count = adam_step[0].astype(jnp.float32)
    first_new = BETA_FIRST * moment_one[0] + (1.0 - BETA_FIRST) * owned_grads
    second_new = BETA_SECOND * moment_two[0] + (1.0 - BETA_SECOND) * owned_grads * owned_grads
    first_hat = first_new / (1.0 - jnp.power(BETA_FIRST, step_count))
    second_hat = second_new / (1.0 - jnp.power(BETA_SECOND, step_count))
    entry_index = lax.axis_index("dp") * share_size + jnp.arange(share_size, dtype=jnp.int32)
    query_end = model_width * head_cols
    query_bias_end = query_end + head_cols
    key_end = query_bias_end + model_width * head_cols
    column = jnp.where(
        entry_index < query_end,
        entry_index % head_cols,
        jnp.where(
            entry_index < query_bias_end,
            entry_index - query_end,
            (entry_index - query_bias_end) % head_cols,
        ),
    )
    head_index = column // HD
    root_factor = jnp.sqrt(logit_cap / jnp.maximum(head_peak, logit_cap))
    head_factor = jnp.zeros((share_size,), jnp.float32)
    for head_number in range(heads_here):
        head_factor = head_factor + jnp.where(
            head_index == head_number, root_factor[head_number], 0.0
        )
    factor = jnp.where(entry_index < key_end, head_factor, 1.0)
    master_here = master[0]
    master_new = (
        master_here
        - learn_rate
        * (first_hat / (jnp.sqrt(second_hat) + ADAM_EPSILON) + weight_decay * master_here)
    ) * factor
    weights_full = lax.all_gather(master_new.astype(jnp.bfloat16), "dp", axis=0, tiled=True)
    return (
        layer_out,
        input_grad,
        owned_grads[None],
        master_new[None],
        first_new[None],
        second_new[None],
        weights_full[None],
        small_total,
    )


def solution(mesh):
    chosen = fast_body if dict(mesh.shape) == {"dp": 4, "mp": 8} else body
    placed = (
        P("mp", "dp", None),
        P("dp"),
        P("dp", None),
        P("mp", "dp", None),
        P(),
        P(),
        P(None, "mp"),
        P("mp"),
        P(None, "mp"),
        P(None, "mp"),
        P("mp"),
        P("mp", None),
        P(),
        P(),
        P(),
        P(None, "mp"),
        P("mp"),
        P("mp", None),
        P(),
        P("mp", "dp"),
        P("mp", "dp"),
        P("mp", "dp"),
        P(),
        P(),
    )
    return jax.shard_map(
        chosen,
        mesh=mesh,
        in_specs=placed,
        out_specs=(
            P("mp", "dp", None),
            P("mp", "dp", None),
            P("mp", "dp"),
            P("mp", "dp"),
            P("mp", "dp"),
            P("mp", "dp"),
            P("mp", None),
            P("mp"),
        ),
        check_vma=False,
    )
```

```python
import functools
import math

import jax
import jax.numpy as jnp
from jax import lax
from jax.experimental import pallas as pl
from jax.experimental.pallas import tpu as pltpu
from jax.sharding import PartitionSpec as P

HD = 80


NORM_EPSILON = 1e-05
ADAM_EPSILON = 1e-08
BETA_FIRST = 0.9
BETA_SECOND = 0.999
MASK_VALUE = -1e30


def layer_norm(value, gain, shift):
    center = value - jnp.mean(value, axis=-1, keepdims=True)
    spread = jnp.mean(center * center, axis=-1, keepdims=True)
    return center * lax.rsqrt(spread + NORM_EPSILON) * gain + shift


def exact_gelu(argument):
    return jax.nn.gelu(argument, approximate=False)


MESH = pl.DeviceIdType.MESH
ANY = pl.BlockSpec(memory_space=pl.ANY)
VMEM = pl.BlockSpec(memory_space=pltpu.VMEM)
LINE = 4
ROWS = 384
BF = jnp.bfloat16
F32 = jnp.float32


class Place:
    def __init__(self):
        self.dp = lax.axis_index("dp")
        self.mp = lax.axis_index("mp")
        self.z = self.mp // 2
        self.c = self.mp % 2
        self.pair = self.z * 2 + 1 - self.c
        self.dpx = self.dp + 1 - 2 * (self.dp % 2)
        self.dpy = (self.dp + 2) % 4
        self.dpd = 3 - self.dp

    def zorder(self, event):
        if event == 0:
            return self.z
        if event == 1:
            return self.z + 1 - 2 * (self.z % 2)
        if event == 2:
            return 2 - self.z // 2
        return 3 - 3 * (self.z // 2)


def greet(place, mp_all=False, line=False, plane=False, pair=True):
    barrier = pltpu.get_barrier_semaphore()
    count = 0

    def signal(dp, mp):
        pl.semaphore_signal(barrier, inc=1, device_id=(dp, mp), device_id_type=MESH)

    if mp_all:
        for hop in range(1, 8):
            signal(place.dp, (place.mp + hop) % 8)
        count += 7
    else:
        if pair:
            signal(place.dp, place.pair)
            count += 1
        if line:

            @pl.when(place.z > 0)
            def _():
                signal(place.dp, place.mp - 2)

            @pl.when(place.z < LINE - 1)
            def _():
                signal(place.dp, place.mp + 2)

    if plane:
        for other in (place.dpx, place.dpy, place.dpd):
            signal(other, place.mp)
        count += 3
    if line and not mp_all:
        pl.semaphore_wait(barrier, count + 1 + (place.z + 1) // 2 % 2)
    else:
        pl.semaphore_wait(barrier, count)


def remote(src, dst, send, recv, dp, mp):
    return pltpu.make_async_remote_copy(
        src_ref=src,
        dst_ref=dst,
        send_sem=send,
        recv_sem=recv,
        device_id=(dp, mp),
        device_id_type=MESH,
    )


def line_gather(place, src, out, local, send, recv, paired, ready=None, rows=None):
    dp, z, c, mp, pair = place.dp, place.z, place.c, place.mp, place.pair

    def at(slot):
        if rows is None:
            return out.at[slot]
        return out.at[pl.ds(pl.multiple_of(slot * rows, 16), rows)]

    def slot_of(level, core):
        return level * 2 + core if paired else level

    def hop(event, slot, source, direction, target):
        return remote(source, at(slot), send.at[event, direction], recv.at[slot], dp, target)

    own = slot_of(z, c)
    keep = pltpu.make_async_copy(src, at(own), local)
    keep.start()

    def ways(event, level, slot, source, act):
        up = z < LINE - 1
        down = z > 0
        if event > 0:
            up = jnp.logical_and(up, level < z)
            down = jnp.logical_and(down, level > z)

        @pl.when(up)
        def _():
            act(hop(event, slot, source, 1, mp + 2))

        @pl.when(down)
        def _():
            act(hop(event, slot, source, 2, mp - 2))

        if paired:
            act(hop(event, slot, source, 0, pair))

    ways(0, z, own, src, lambda copy: copy.start())
    yield
    if ready is not None:
        keep.wait()
        ready(own)
        if paired:
            other = slot_of(z, 1 - c)
            hop(0, other, at(other), 0, pair).wait_recv()
            ready(other)

    def settle(event):
        level = place.zorder(event)
        ready(slot_of(level, c))
        if paired:
            other = slot_of(level, 1 - c)
            hop(event, other, at(other), 0, pair).wait_recv()
            ready(other)

    for event in range(1, LINE):
        level = place.zorder(event)
        slot = slot_of(level, c)
        hop(event, slot, at(slot), 0, pair).wait_recv()
        ways(event, level, slot, at(slot), lambda copy: copy.start())
        if ready is not None and event > 1:
            if event == 2:
                settle(1)
            settle(event)
        yield
    if ready is None:
        if paired:
            for level in range(LINE):
                other = slot_of(level, 1 - c)
                hop(0, other, at(other), 0, pair).wait_recv()
        keep.wait()
    for event in range(LINE):
        level = place.zorder(event)
        slot = slot_of(level, c)
        ways(event, level, slot, at(slot), lambda copy: copy.wait_send())
    yield


def plane_gather(place, src, out, local, send, recv, ready=None, primed=False):
    dp, c, mp, pair = place.dp, place.c, place.mp, place.pair
    dpx, dpy, dpd = place.dpx, place.dpy, place.dpd
    half = src.shape[0] // 2
    part_a, part_b = pl.ds(0, half), pl.ds(half, half)

    def at(group, core):
        return out.at[group * 2 + core]

    def hop(index, block, group, target):
        return remote(block, block, send.at[index], recv.at[index], group, target)

    def done(group, core):
        if ready is not None:
            ready(group * 2 + core)

    keep = pltpu.make_async_copy(src, at(dp, c), local)
    here = at(dp, c)
    from_x, from_y, from_d = at(dpx, c), at(dpy, c), at(dpd, c)
    firsts = [
        remote(src, here, send.at[0], recv.at[0], dp, pair),
        remote(src, here, send.at[1], recv.at[1], dpx, mp),
        remote(src, here, send.at[2], recv.at[2], dpy, mp),
    ]
    seconds = [
        hop(3, from_x.at[part_a], dpy, mp),
        hop(4, from_y.at[part_b], dpx, mp),
        hop(5, from_x, dp, pair),
        hop(6, from_y, dp, pair),
        hop(7, from_d.at[part_a], dp, pair),
        hop(8, from_d.at[part_b], dp, pair),
    ]
    if primed:
        yield
    keep.start()
    for copy in firsts:
        copy.start()
    yield
    if ready is not None:
        keep.wait()
        done(dp, c)
        hop(0, at(dp, 1 - c), dp, pair).wait_recv()
        done(dp, 1 - c)
    hop(1, from_x, dpx, mp).wait_recv()
    seconds[0].start()
    hop(2, from_y, dpy, mp).wait_recv()
    seconds[1].start()
    seconds[2].start()
    seconds[3].start()
    if ready is None:
        yield
    done(dpx, c)
    hop(5, at(dpx, 1 - c), dp, pair).wait_recv()
    done(dpx, 1 - c)
    if ready is not None:
        yield
    done(dpy, c)
    hop(6, at(dpy, 1 - c), dp, pair).wait_recv()
    done(dpy, 1 - c)
    if ready is not None:
        yield
    hop(3, from_d.at[part_a], dpy, mp).wait_recv()
    seconds[4].start()
    hop(4, from_d.at[part_b], dpx, mp).wait_recv()
    seconds[5].start()
    done(dpd, c)
    other = at(dpd, 1 - c)
    hop(7, other.at[part_a], dp, pair).wait_recv()
    hop(8, other.at[part_b], dp, pair).wait_recv()
    done(dpd, 1 - c)
    yield
    if ready is None:
        hop(0, at(dp, 1 - c), dp, pair).wait_recv()
        keep.wait()
    for copy in firsts + seconds:
        copy.wait_send()
    yield


def drive(*programs):
    live = list(programs)
    while live:
        for program in list(live):
            try:
                next(program)
            except StopIteration:
                live.remove(program)


def dma(*shape):
    return pltpu.SemaphoreType.DMA(shape)


def params(cid, vmem=40):
    return pltpu.CompilerParams(
        collective_id=cid, has_side_effects=True, vmem_limit_bytes=vmem << 20
    )


def exchange(place, src, out, local, send, recv):
    dp, mp = place.dp, place.mp
    keep = pltpu.make_async_copy(src.at[mp], out.at[mp], local)
    keep.start()
    sends = []
    for hop in range(1, 8):
        target = (mp + hop) % 8
        sends.append(
            remote(src.at[target], out.at[mp], send.at[hop], recv.at[hop], dp, target)
        )
        sends[-1].start()
    yield
    keep.wait()
    for hop in range(1, 8):
        origin = (mp + 8 - hop) % 8
        remote(out.at[origin], out.at[origin], send.at[hop], recv.at[hop], dp, origin).wait_recv()
    for copy in sends:
        copy.wait_send()
    yield


def line_reduce(place, produce, tiles, result, bufs, sems, paired):
    dp, z, c, mp, pair = place.dp, place.z, place.c, place.mp, place.pair
    above_block, below_block, out_block = bufs["above"], bufs["below"], bufs["out"]
    order = [place.zorder(event) for event in (3, 2, 1, 0)]
    inner = jnp.logical_and(z > 0, z < LINE - 1)
    outer = jnp.logical_or(z == 0, z == LINE - 1)

    @pl.when(z == LINE - 1)
    def _():
        above_block[...] = jnp.zeros(above_block.shape, BF)

    @pl.when(z == 0)
    def _():
        below_block[...] = jnp.zeros(below_block.shape, BF)

    def from_above(level):
        return above_block.at[jnp.minimum(level, LINE - 2)]

    def from_below(level):
        return below_block.at[jnp.maximum(level - 1, 0)]

    def across(step, level):
        return remote(
            bufs["pair_out"].at[step % 2],
            bufs["pair_in"].at[level],
            sems["pair_send"].at[step % 2],
            sems["pair_recv"].at[level],
            dp,
            pair,
        )

    if paired:
        for step, level in enumerate(order):
            if step > 1:
                across(step - 2, order[step - 2]).wait_send()
            for rows in tiles:
                bufs["pair_out"][step % 2, rows] = produce(level, 1 - c, rows).astype(BF)
            across(step, level).start()
    yield

    def toward(step, level, act):
        @pl.when(level < z)
        def _():
            act(
                remote(
                    out_block.at[step],
                    from_above(level),
                    sems["line_send"].at[step],
                    sems["above"].at[level],
                    dp,
                    mp - 2,
                )
            )

        @pl.when(level > z)
        def _():
            act(
                remote(
                    out_block.at[step],
                    from_below(level),
                    sems["line_send"].at[step],
                    sems["below"].at[level],
                    dp,
                    mp + 2,
                )
            )

    def arrive(level, above):
        if above:
            remote(
                from_above(level),
                from_above(level),
                sems["line_send"].at[0],
                sems["above"].at[level],
                dp,
                mp,
            ).wait_recv()
        else:
            remote(
                from_below(level),
                from_below(level),
                sems["line_send"].at[0],
                sems["below"].at[level],
                dp,
                mp,
            ).wait_recv()

    def advance(step):
        level = order[step]
        if paired:
            across(step, level).wait_recv()

        @pl.when(jnp.logical_and(level < z, z < LINE - 1))
        def _():
            arrive(level, True)

        @pl.when(jnp.logical_and(level > z, z > 0))
        def _():
            arrive(level, False)

        for rows in tiles:
            total = produce(level, c, rows)
            if paired:
                total = total + bufs["pair_in"][level, rows].astype(F32)

            @pl.when(level < z)
            def _():
                out_block[step, rows] = (total + from_above(level)[rows].astype(F32)).astype(BF)

            @pl.when(level > z)
            def _():
                out_block[step, rows] = (total + from_below(level)[rows].astype(F32)).astype(BF)

        toward(step, level, lambda copy: copy.start())

    advance(0)
    for step in (1, 2):

        @pl.when(outer)
        def _():
            advance(step)

    yield
    for step in (1, 2):

        @pl.when(inner)
        def _():
            advance(step)

        yield

    if paired:
        across(3, z).wait_recv()

    @pl.when(z < LINE - 1)
    def _():
        arrive(z, True)

    @pl.when(z > 0)
    def _():
        arrive(z, False)

    for rows in tiles:
        total = produce(z, c, rows)
        if paired:
            total = total + bufs["pair_in"][z, rows].astype(F32)
        total = total + from_above(z)[rows].astype(F32) + from_below(z)[rows].astype(F32)
        result(rows, total)
    for step, level in enumerate(order):
        if paired and step > 1:
            across(step, level).wait_send()
        if step < 3:
            toward(step, level, lambda copy: copy.wait_send())
    yield


def line_reduce_scratch(rows, cols, paired):
    block = lambda n: pltpu.VMEM((n, rows, cols), BF)
    scratch = {"above": block(3), "below": block(3), "out": block(3)}
    sems = {"line_send": dma(3), "above": dma(4), "below": dma(4)}
    if paired:
        scratch.update({"pair_out": block(2), "pair_in": block(4)})
        sems.update({"pair_send": dma(2), "pair_recv": dma(4)})
    return scratch, sems


def plane_reduce(place, produce, tile, half, result, bufs, sems, paired=True, early=False):
    dp, c, mp, pair = place.dp, place.c, place.mp, place.pair
    dpx, dpy, dpd = place.dpx, place.dpy, place.dpd
    starts = range(0, half, tile)
    send, recv = sems["send"], sems["recv"]
    out_block, landed = bufs["out"], bufs["in"]
    groups = {"far": dpd, "x": dpx, "y": dpy, "own": dp}
    steps = ["x", "y", "far", "own"] if early else ["far", "x", "y", "own"]

    def across(name):
        step = steps.index(name)
        return remote(
            bufs["pair_out"].at[step % 2],
            bufs["pair_in"].at[step],
            sems["pair_send"].at[step % 2],
            sems["pair_recv"].at[step],
            dp,
            pair,
        )

    def cross(name):
        if not paired:
            return
        step = steps.index(name)
        if step > 1:
            across(steps[step - 2]).wait_send()
        for start in range(0, 2 * half, tile):
            bufs["pair_out"][step % 2, pl.ds(start, tile)] = produce(
                groups[name], 1 - c, start
            ).astype(BF)
        across(name).start()

    def crossed(name):
        if paired:
            across(name).wait_recv()

    def share(name, start):
        total = produce(groups[name], c, start)
        if paired:
            total = total + bufs["pair_in"][steps.index(name), pl.ds(start, tile)].astype(F32)
        return total

    def hop(index):
        target = (dpx, dpy, dpx, dpx, dpy, dpy)[index]
        return remote(
            out_block.at[index], landed.at[index], send.at[index], recv.at[index], target, mp
        )

    def fill(index, name, base, extra=None):
        for start in starts:
            total = share(name, base + start)
            if extra is not None:
                total = total + landed[extra, pl.ds(start, tile)].astype(F32)
            out_block[index, pl.ds(start, tile)] = total.astype(BF)
        hop(index).start()

    def far():
        crossed("far")
        fill(0, "far", 0)
        fill(1, "far", half)

    def near():
        crossed("x")
        fill(2, "x", 0)
        crossed("y")
        fill(4, "y", half)

    if early:
        cross("x")
        yield
        cross("y")
        near()
        yield
        cross("far")
        far()
        cross("own")
    else:
        cross("far")
        cross("x")
        yield
        far()
        cross("y")
        near()
        cross("own")
    yield
    hop(1).wait_recv()
    fill(3, "x", half, extra=1)
    hop(0).wait_recv()
    fill(5, "y", 0, extra=0)
    yield
    crossed("own")
    for index in (2, 3, 4, 5):
        hop(index).wait_recv()
    for base, pieces in ((0, (2, 5)), (half, (3, 4))):
        for start in starts:
            total = share("own", base + start)
            for piece in pieces:
                total = total + landed[piece, pl.ds(start, tile)].astype(F32)
            result(pl.ds(base + start, tile), total)
    for index in range(6):
        hop(index).wait_send()
    if paired:
        for name in steps[2:]:
            across(name).wait_send()
    yield


def plane_reduce_scratch(half, cols, paired=True):
    block = lambda n, rows: pltpu.VMEM((n, rows, cols), BF)
    scratch = {"out": block(6, half), "in": block(6, half)}
    sems = {"send": dma(6), "recv": dma(6)}
    if paired:
        scratch.update({"pair_out": block(2, 2 * half), "pair_in": block(4, 2 * half)})
        sems.update({"pair_send": dma(2), "pair_recv": dma(4)})
    return scratch, sems


def project_kernel(
    normed_ref, cot_ref, weight_ref, bias_ref, nfull_ref, qkv_ref, cfull_ref,
    local, line_send, line_recv, plane_send, plane_recv,
):
    place = Place()
    greet(place, line=True, plane=True)

    def ready(slot):
        @pl.loop(0, 3)
        def _(step):
            rows = pl.ds(step * 128, 128)
            product = lax.dot_general(
                nfull_ref[slot, rows],
                weight_ref[...],
                (((1,), (1,)), ((), ())),
                preferred_element_type=F32,
            )
            qkv_ref[slot, rows] = (product + bias_ref[...]).astype(BF)

    drive(
        line_gather(
            place, normed_ref, nfull_ref, local.at[0], line_send, line_recv, True, ready
        ),
        plane_gather(place, cot_ref, cfull_ref, local.at[1], plane_send, plane_recv),
    )


def project(normed, cotangent, weight, bias):
    return pl.pallas_call(
        project_kernel,
        out_shape=(
            jax.ShapeDtypeStruct((8,) + normed.shape, BF),
            jax.ShapeDtypeStruct((8, ROWS, weight.shape[0]), BF),
            jax.ShapeDtypeStruct((8,) + cotangent.shape, BF),
        ),
        in_specs=[ANY, ANY, VMEM, VMEM],
        out_specs=(VMEM, VMEM, ANY),
        scratch_shapes=[dma(2), dma(4, 3), dma(8), dma(9), dma(9)],
        compiler_params=params(0),
        name="project",
    )(normed, cotangent, weight, bias)


def attend_kernel(
    qkv_ref, mask_ref, live_ref, weights_ref, outer_ref,
    att_ref, logs_ref, peak_ref, wfull_ref, ofull_ref,
    out_ref, vt_ref, outer_all, local, send, recv, line_send, line_recv,
    outer_send, outer_recv, plane_send, plane_recv,
):
    place = Place()
    greet(place, mp_all=True, plane=True)
    outer = line_gather(
        place, outer_ref, outer_all, local.at[2], outer_send, outer_recv, False, None, 48
    )
    next(outer)
    gather = line_gather(
        place, weights_ref, wfull_ref, local.at[1], line_send, line_recv, False
    )
    next(gather)
    factor = math.log2(math.e) / math.sqrt(HD)
    peak_ref[...] = jnp.full(peak_ref.shape, MASK_VALUE, F32)

    @pl.loop(0, 6)
    def _(turn):
        clip = turn // 2
        head = turn % 2
        lane = pl.multiple_of(head * 128, 128)
        row = pl.multiple_of(head * HD, 16)
        keys = qkv_ref[:, clip, :, pl.ds(256 + lane, 128)].reshape(1024, 128)
        vt_ref[...] = qkv_ref[:, clip, :, pl.ds(512 + lane, 128)].reshape(1024, 128).T

        @pl.loop(0, 4)
        def _(block):
            query = qkv_ref[pl.ds(block * 2, 2), clip, :, pl.ds(lane, 128)].reshape(256, 128)
            columns = pl.ds(pl.multiple_of(block * 256, 256), 256)
            scores = lax.dot_general(
                keys, query, (((1,), (1,)), ((), ())), preferred_element_type=F32
            )
            scores = scores + mask_ref[clip]
            peak = jnp.max(scores, axis=0, keepdims=True)
            powers = jnp.exp2((scores - peak) * factor)
            total = jnp.sum(powers, axis=0, keepdims=True)
            mixed = lax.dot_general(
                vt_ref[...],
                powers.astype(BF),
                (((1,), (0,)), ((), ())),
                preferred_element_type=F32,
            )
            mixed = (mixed / total).astype(BF)
            for part in range(2):
                out_ref[block * 2 + part, clip, pl.ds(row, HD)] = mixed[
                    :HD, part * 128 : part * 128 + 128
                ]
            logs_ref[turn, :, columns] = peak * factor + jnp.log2(total)
            peak_ref[head] = jnp.maximum(
                peak_ref[head], jnp.where(live_ref[clip, :, columns] > 0, peak, MASK_VALUE)
            )

        @pl.when(turn == 2)
        def _():
            next(outer)

        @pl.when(turn == 4)
        def _():
            next(outer)
            next(gather)

    mixing = exchange(place, out_ref, att_ref, local.at[0], send, recv)
    next(mixing)
    for _ in outer:
        pass
    spread = plane_gather(place, outer_all, ofull_ref, local.at[3], plane_send, plane_recv)
    drive(spread, gather, mixing)


def attend(qkv, mask, live, weights, outer):
    return pl.pallas_call(
        attend_kernel,
        out_shape=(
            jax.ShapeDtypeStruct((8, 3, 160, 128), BF),
            jax.ShapeDtypeStruct((6, 1, 1024), F32),
            jax.ShapeDtypeStruct((2, 8, 256), F32),
            jax.ShapeDtypeStruct((4,) + weights.shape, BF),
            jax.ShapeDtypeStruct((8, 192, 1280), BF),
        ),
        in_specs=[VMEM, VMEM, VMEM, ANY, ANY],
        out_specs=(VMEM, VMEM, VMEM, ANY, ANY),
        scratch_shapes=[
            pltpu.VMEM((8, 3, 160, 128), BF),
            pltpu.VMEM((128, 1024), BF),
            pltpu.VMEM((192, 1280), BF),
            dma(4),
            dma(8),
            dma(8),
            dma(4, 3),
            dma(4),
            dma(4, 3),
            dma(4),
            dma(9),
            dma(9),
        ],
        compiler_params=params(1),
        name="attend",
    )(qkv, mask, live, weights, outer)


def flatten(*pairs):
    names, shapes = [], []
    for number, group in enumerate(pairs):
        for name, shape in group.items():
            names.append((number, name))
            shapes.append(shape)

    def split(refs):
        groups = [{} for _ in pairs]
        for (number, name), ref in zip(names, refs):
            groups[number][name] = ref
        return groups

    return shapes, split


def feed_forward_kernel(
    split, normed_ref, upstream_ref, weights_ref, bias_ref,
    total_ref, hidden_ref, grads_ref, bias_out,
    normed_all, upstream_all, slope_all, sum_ref, load, local, gather_send, gather_recv, *scratch,
):
    place = Place()
    bufs, sems = split(scratch)
    loads = []
    for slot in range(8):
        loads.append(
            pltpu.make_async_copy(upstream_ref.at[slot], upstream_all.at[slot], load.at[slot])
        )
        loads[-1].start()
    greet(place, plane=True)
    bias_out[...] = jnp.zeros(bias_out.shape, F32)

    def up_rows():
        return weights_ref[:, pl.ds(0, 160)].reshape(640, 1280)

    def down_rows():
        return weights_ref[:, pl.ds(160, 160)].reshape(640, 1280)

    def ready(slot):
        @pl.loop(0, 3)
        def _(step):
            rows = pl.ds(step * 128, 128)
            before = (
                lax.dot_general(
                    normed_all[slot, rows],
                    up_rows(),
                    (((1,), (1,)), ((), ())),
                    preferred_element_type=F32,
                )
                + bias_ref[...]
            )
            pull = lax.dot_general(
                upstream_all[slot, rows],
                down_rows(),
                (((1,), (1,)), ((), ())),
                preferred_element_type=F32,
            )
            share = 0.5 + 0.5 * lax.erf(before * math.sqrt(0.5))
            hidden_ref[slot, rows] = (before * share).astype(BF)
            density = jnp.exp(before * before * -0.5) * (1.0 / math.sqrt(2.0 * math.pi))
            slope = (pull * (share + before * density)).astype(BF)
            slope_all[slot, rows] = slope
            bias_out[...] += jnp.sum(slope.astype(F32), axis=0, keepdims=True)

    gather = plane_gather(
        place, normed_ref, normed_all, local, gather_send, gather_recv, ready
    )

    def produce(group, core, start):
        return jnp.dot(
            slope_all[group * 2 + core, pl.ds(start, 192)],
            up_rows(),
            preferred_element_type=F32,
        )

    def result(rows, total):
        total_ref[rows] = total

    reduce = plane_reduce(place, produce, 192, 192, result, bufs, sems, True, True)
    next(gather)
    for copy in loads:
        copy.wait()
    next(gather)
    next(reduce)
    next(gather)
    next(reduce)
    next(gather)
    next(reduce)

    def weight_grads(left_all, right_all, base):
        for block in range(5):
            lanes = pl.ds(block * 128, 128)

            @pl.loop(0, 8)
            def _(slot):
                product = lax.dot_general(
                    left_all[slot, :, lanes],
                    right_all[slot],
                    (((0,), (0,)), ((), ())),
                    preferred_element_type=F32,
                )
                sum_ref[...] = jnp.where(slot == 0, product, sum_ref[...] + product)

            for part in range(4):
                unit = block * 128 + part * 32
                grads_ref[unit // 160, pl.ds(base + unit % 160, 32)] = sum_ref[
                    pl.ds(part * 32, 32)
                ].astype(BF)

    weight_grads(slope_all, normed_all, 0)
    next(reduce)
    weight_grads(hidden_ref, upstream_all, 160)
    for level in range(4):
        grads_ref[level, pl.ds(320, 16)] = jnp.zeros((16, 1280), BF)
        grads_ref[level, pl.ds(320, 16), pl.ds(0, 640)] = jnp.broadcast_to(
            bias_out[...], (16, 640)
        ).astype(BF)
    drive(reduce, gather)


def feed_forward(normed, upstream, weights, bias):
    shapes, split = flatten(*plane_reduce_scratch(192, 1280))
    return pl.pallas_call(
        functools.partial(feed_forward_kernel, split),
        out_shape=(
            jax.ShapeDtypeStruct((ROWS, 1280), F32),
            jax.ShapeDtypeStruct((8, ROWS, 640), BF),
            jax.ShapeDtypeStruct((4, 336, 1280), BF),
            jax.ShapeDtypeStruct((1, 640), F32),
        ),
        in_specs=[ANY, ANY, VMEM, VMEM],
        out_specs=(VMEM,) * 4,
        scratch_shapes=[
            pltpu.VMEM((8, ROWS, 1280), BF),
            pltpu.VMEM((8, ROWS, 1280), BF),
            pltpu.VMEM((8, ROWS, 640), BF),
            pltpu.VMEM((128, 1280), F32),
            dma(8),
            pltpu.SemaphoreType.DMA(()),
            dma(9),
            dma(9),
            *shapes,
        ],
        compiler_params=params(3, 60),
        name="feed_forward",
    )(normed, upstream, weights, bias)


def attend_back_kernel(
    split, qkv_in, mask_ref, logs_ref, pull_ref, hidden_in, weights_ref, feed_grads_in,
    out_grad_in, dqkv_ref, feed_ref, feed_sum_ref, out_sum_ref,
    qkv_ref, hidden_ref, feed_grads_ref, out_grad_ref, load,
    grad_ref, kt_ref, dk_ref, dv_ref, block_ref, middle_ref, local, send, recv, *scratch,
):
    place = Place()
    (
        line_bufs, line_sems, plane_bufs, plane_sems,
        out_plane_bufs, out_plane_sems, out_line_bufs, out_line_sems,
    ) = split(scratch)
    loads = [
        pltpu.make_async_copy(source, target, load.at[index])
        for index, (source, target) in enumerate(
            (
                (out_grad_in, out_grad_ref),
                (feed_grads_in, feed_grads_ref),
                (hidden_in, hidden_ref),
                (qkv_in, qkv_ref),
            )
        )
    ]
    for copy in loads:
        copy.start()
    greet(place, mp_all=True, plane=True)
    scale = 1.0 / math.sqrt(HD)
    factor = math.log2(math.e) * scale
    arriving = exchange(place, pull_ref, grad_ref, local, send, recv)
    next(arriving)

    def feed_block(group, core, start):
        return jnp.dot(
            hidden_ref[group * 2 + core, pl.ds(start, 192)],
            weights_ref[:, pl.ds(160, 160)].reshape(640, 1280),
            preferred_element_type=F32,
        )

    def feed_result(rows, total):
        feed_ref[rows] = total

    def sum_result(rows, total):
        feed_sum_ref[rows] = total

    plane = plane_reduce(
        place, feed_block, 192, 192, feed_result, plane_bufs, plane_sems, True
    )
    line = line_reduce(
        place,
        lambda level, core, rows: feed_grads_ref[level, rows].astype(F32),
        [pl.ds(start, 112) for start in range(0, 336, 112)],
        sum_result,
        line_bufs,
        line_sems,
        False,
    )
    def middle(rows, total):
        middle_ref[rows] = total

    def out_result(rows, total):
        out_sum_ref[rows] = total

    out_plane = plane_reduce(
        place,
        lambda group, core, start: out_grad_ref[group, core, pl.ds(start, 96)].astype(F32),
        96,
        96,
        middle,
        out_plane_bufs,
        out_plane_sems,
    )
    out_line = line_reduce(
        place,
        lambda level, core, rows: middle_ref[
            pl.ds(pl.multiple_of(level * 48 + rows.start, 16), rows.size)
        ],
        [pl.ds(0, 48)],
        out_result,
        out_line_bufs,
        out_line_sems,
        False,
    )
    loads[0].wait()
    next(out_plane)
    next(line)
    next(out_line)
    loads[1].wait()
    next(line)
    next(out_plane)
    loads[2].wait()
    next(plane)
    next(plane)
    next(out_plane)
    loads[3].wait()
    for _ in arriving:
        pass
    block_ref[...] = jnp.zeros(block_ref.shape, BF)

    @pl.loop(0, 6)
    def _(turn):
        clip = turn // 2
        head = turn % 2
        lane = pl.multiple_of(head * 128, 128)
        row = pl.multiple_of(head * HD, 16)
        kt_ref[...] = qkv_ref[:, clip, :, pl.ds(256 + lane, 128)].reshape(1024, 128).T
        dk_ref[...] = jnp.zeros(dk_ref.shape, F32)
        dv_ref[...] = jnp.zeros(dv_ref.shape, F32)

        @pl.loop(0, 4)
        def _(block):
            query = qkv_ref[pl.ds(block * 2, 2), clip, :, pl.ds(lane, 128)].reshape(256, 128)
            values = qkv_ref[:, clip, :, pl.ds(512 + lane, 128)].reshape(1024, 128)
            keys = qkv_ref[:, clip, :, pl.ds(256 + lane, 128)].reshape(1024, 128)
            columns = pl.ds(pl.multiple_of(block * 256, 256), 256)
            for part in range(2):
                block_ref[:HD, part * 128 : part * 128 + 128] = grad_ref[
                    block * 2 + part, clip, pl.ds(row, HD)
                ]
            scores = lax.dot_general(
                keys, query, (((1,), (1,)), ((), ())), preferred_element_type=F32
            )
            chance = jnp.exp2((scores + mask_ref[clip]) * factor - logs_ref[turn, :, columns])
            dv_ref[...] += lax.dot_general(
                chance.astype(BF),
                block_ref[...],
                (((1,), (1,)), ((), ())),
                preferred_element_type=F32,
            )
            slope = lax.dot_general(
                values, block_ref[...], (((1,), (0,)), ((), ())), preferred_element_type=F32
            )
            center = jnp.sum(chance * slope, axis=0, keepdims=True)
            change = (chance * (slope - center)).astype(BF)
            dk_ref[...] += lax.dot_general(
                change, query, (((1,), (0,)), ((), ())), preferred_element_type=F32
            )
            dq = lax.dot_general(
                kt_ref[...], change, (((1,), (0,)), ((), ())), preferred_element_type=F32
            )
            dqkv_ref[pl.ds(block * 2, 2), clip, :, pl.ds(lane, 128)] = (
                (dq.T * scale).astype(BF).reshape(2, 128, 128)
            )

        dqkv_ref[:, clip, :, pl.ds(256 + lane, 128)] = (
            (dk_ref[...] * scale).astype(BF).reshape(8, 128, 128)
        )
        dqkv_ref[:, clip, :, pl.ds(512 + lane, 128)] = (
            dv_ref[...].astype(BF).reshape(8, 128, 128)
        )

        for when, programs in (
            (0, (out_plane, out_line)),
            (1, (line,)),
            (2, (plane,)),
            (3, (out_line,)),
            (4, (line,)),
            (5, (out_line,)),
        ):

            @pl.when(turn == when)
            def _():
                for program in programs:
                    next(program)

    drive(line, out_line, plane, out_plane)


def attend_back(qkv, mask, logs, pull, hidden, weights, feed_grads, out_grad):
    shapes, split = flatten(
        *line_reduce_scratch(336, 1280, False),
        *plane_reduce_scratch(192, 1280),
        *plane_reduce_scratch(96, 1280),
        *line_reduce_scratch(48, 1280, False),
    )
    return pl.pallas_call(
        functools.partial(attend_back_kernel, split),
        out_shape=(
            jax.ShapeDtypeStruct(qkv.shape, BF),
            jax.ShapeDtypeStruct((ROWS, 1280), F32),
            jax.ShapeDtypeStruct((336, 1280), F32),
            jax.ShapeDtypeStruct((48, 1280), F32),
        ),
        in_specs=[ANY, VMEM, VMEM, ANY, ANY, VMEM, ANY, ANY],
        out_specs=(VMEM,) * 4,
        scratch_shapes=[
            *(pltpu.VMEM(ref.shape, BF) for ref in (qkv, hidden, feed_grads, out_grad)),
            dma(4),
            pltpu.VMEM((8, 3, 160, 128), BF),
            pltpu.VMEM((128, 1024), BF),
            pltpu.VMEM((1024, 128), F32),
            pltpu.VMEM((1024, 128), F32),
            pltpu.VMEM((128, 256), BF),
            pltpu.VMEM((192, 1280), F32),
            pltpu.SemaphoreType.DMA(()),
            dma(8),
            dma(8),
            *shapes,
        ],
        compiler_params=params(2, 62),
        name="attend_back",
    )(qkv, mask, logs, pull, hidden, weights, feed_grads, out_grad)


GROUP_ROWS = 4832
GROUP_STEP = 4800
PACK_ROWS = GROUP_STEP * 3 + GROUP_ROWS
SEGMENTS = (
    ("query", 0, 1600),
    ("query_bias", 204800, 2),
    ("key", 204960, 1600),
    ("value", 409760, 1600),
    ("value_bias", 614560, 2),
    ("out", 614720, 1600),
    ("up", 819520, 6400),
    ("up_bias", 1638720, 5),
    ("down", 1639360, 6400),
)
PACK_END = 19216


def segment_table():
    table, cursor = {}, 0
    for name, start, rows in SEGMENTS:
        row = start // 128
        cursor += 32
        cursor += (row - cursor) % 8
        table[name] = (cursor, row, rows, start % 128)
        cursor += rows
    return table, (cursor + 32 + 7) // 8 * 8


TABLE, STAGE_ROWS = segment_table()


def lane_of(rows):
    return lax.broadcasted_iota(jnp.int32, (rows, 128), 1)


def pack_rows(stage, packed):
    def piece(name, first, rows):
        base, row, _, shift = TABLE[name]
        at = base - row + first
        here = stage[pl.ds(at, rows)]
        if shift == 0:
            return here
        above = stage[pl.ds(at - 1, rows)]
        return jnp.where(
            lane_of(rows) >= shift, pltpu.roll(here, shift, 1), pltpu.roll(above, shift, 1)
        )

    done = set()
    for name, _, _ in SEGMENTS:
        _, row, rows, shift = TABLE[name]
        low = -(-(row + (1 if shift else 0)) // 16) * 16
        high = (row + rows) // 16 * 16
        if high <= low:
            continue
        done.update(range(low, high, 16))
        turns = (high - low) // 128

        @pl.loop(0, turns)
        def _(turn):
            first = pl.multiple_of(low + turn * 128, 16)
            packed[pl.ds(first, 128)] = piece(name, first, 128).astype(BF)

        for first in range(low + turns * 128, high, 16):
            packed[pl.ds(first, 16)] = piece(name, first, 16).astype(BF)
    for first in range(0, PACK_ROWS, 16):
        if first in done:
            continue
        total = jnp.zeros((16, 128), F32)
        for name, _, _ in SEGMENTS:
            _, row, rows, shift = TABLE[name]
            if row < first + 16 and row + rows + (1 if shift else 0) > first:
                total = total + piece(name, first, 16)
        packed[pl.ds(first, 16)] = total.astype(BF)


def stage_wide(stage, name, ref, step):
    base = TABLE[name][0]
    rows, wide = ref.shape[0], ref.shape[1] // 128

    @pl.loop(0, rows // step)
    def _(turn):
        first = pl.multiple_of(turn * step, step)
        for block in range(wide):
            stage[pl.ds(base + first * wide + block, step, stride=wide), :] = ref[
                pl.ds(first, step), pl.ds(block * 128, 128)
            ].astype(F32)


def stage_heads(stage, name, ref, lanes, column):
    base = TABLE[name][0]
    for head in range(2):
        column[head] = ref[:, pl.ds(lanes + head * 128, 128)]

    @pl.loop(0, 5)
    def _(turn):
        lane = lane_of(64)
        rows = [jnp.zeros((64, 128), F32) for _ in range(5)]
        for block in range(8):
            item, head = block // 2, block % 2
            value = column[head, pl.ds(turn * 256 + item, 64, stride=4)]
            offset = block * HD
            first, shift = offset // 128, offset % 128
            if shift:
                value = pltpu.roll(value, shift, 1)
            if shift + HD > 128:
                rows[first] = rows[first] + jnp.where(lane >= shift, value, 0.0)
                rows[first + 1] = rows[first + 1] + jnp.where(
                    lane < shift + HD - 128, value, 0.0
                )
            else:
                rows[first] = rows[first] + value
        for index in range(5):
            stage[pl.ds(base + turn * 320 + index, 64, stride=5), :] = rows[index]


def stage_head_bias(stage, name, ref, lanes):
    base = TABLE[name][0]
    lane = lane_of(1)
    first = ref[0:1, pl.ds(lanes, 128)]
    second = pltpu.roll(ref[0:1, pl.ds(lanes + 128, 128)], HD, 1)
    stage[pl.ds(base, 1)] = first + jnp.where(lane >= HD, second, 0.0)
    stage[pl.ds(base + 1, 1)] = jnp.where(lane < 2 * HD - 128, second, 0.0)


def stage_share(stage, name, ref, first, count, place):
    base = TABLE[name][0] + place.dp * count * 10
    for block in range(10):
        stage[pl.ds(base + block, count, stride=10), :] = ref[
            pl.ds(first, count), pl.ds(block * 128, 128)
        ]


def stage_up(stage, ref, place):
    base = TABLE["up"][0]
    lane = lane_of(128)
    for quarter in range(4):

        @pl.when(place.dp == quarter)
        def _():
            for block in range(10):
                columns = pl.ds(block * 128, 128)
                first = ref[pl.ds(0, 128), columns].T
                second = jnp.where(lane < 32, ref[pl.ds(128, 128), columns].T, 0.0)
                shift = 32 * quarter
                if shift:
                    first = pltpu.roll(first, shift, 1)
                    second = pltpu.roll(second, shift, 1)
                    second = second + jnp.where(lane < shift, first, 0.0)
                    first = jnp.where(lane >= shift, first, 0.0)
                at = base + block * 640 + quarter
                stage[pl.ds(at, 128, stride=5), :] = first
                stage[pl.ds(at + 1, 128, stride=5), :] = second


def norm_back(place, frames_ref, middle_ref, gain_ref, grad_ref, offset):
    def write(rows, total):
        rows_in = pl.ds(offset + rows.start, rows.size)
        value = frames_ref[rows_in].astype(F32)
        center = value - jnp.mean(value, axis=-1, keepdims=True)
        spread = jnp.mean(center * center, axis=-1, keepdims=True)
        root = lax.rsqrt(spread + NORM_EPSILON)
        scaled = center * root
        pull = total * gain_ref[...]
        along = jnp.mean(pull * scaled, axis=-1, keepdims=True)
        grad_ref[rows] = middle_ref[rows_in] + root * (
            pull - jnp.mean(pull, axis=-1, keepdims=True) - scaled * along
        )

    return write


def line_product(place, grad_ref, weight_ref, offset, rows, result, bufs, sems):
    def produce(level, core, tile):
        return jnp.dot(
            grad_ref[level * 2 + core, pl.ds(offset + tile.start, tile.size)],
            weight_ref[...],
            preferred_element_type=F32,
        )

    tiles = [pl.ds(start, 128) for start in range(0, rows, 128)]
    return line_reduce(place, produce, tiles, result, bufs, sems, True)


FIRST_ROWS = 256


def finish_kernel(
    split, grad_ref, weight_ref, joined_ref, bias_ref, bias_column_ref, sum_ref, out_ref,
    up_bias_ref, small_ref, peak_ref, frames_ref, middle_ref, gain_ref, shift_ref,
    input_grad_ref, grads_ref, small_out, peak_out,
    stage, packed, column, tiles, small_in, small_all, peak_all, edge,
    local, small_send, small_recv, plane_send, plane_recv, *scratch,
):
    place = Place()
    line_bufs, line_sems, bufs, sems = split(scratch)
    greet(place, mp_all=True, plane=True)
    peers = (place.dpx, place.dpy, place.dpd)

    def tell(index, source, target, group, act):
        act(
            remote(
                source,
                target.at[place.dp],
                plane_send.at[index],
                plane_recv.at[index],
                group,
                place.mp,
            )
        )

    def heard(index, target, group):
        block = target.at[group]
        remote(
            block, block, plane_send.at[index], plane_recv.at[index], group, place.mp
        ).wait_recv()

    line = line_product(
        place,
        grad_ref,
        weight_ref,
        0,
        FIRST_ROWS,
        norm_back(place, frames_ref, middle_ref, gain_ref, input_grad_ref, 0),
        line_bufs,
        line_sems,
    )
    for index, group in enumerate(peers):
        tell(index, peak_ref, peak_all, group, lambda copy: copy.start())
    next(line)
    next(line)

    for block in range(10):
        lanes = pl.ds(block * 128, 128)
        weight = weight_ref[:, lanes].astype(F32)
        turned = joined_ref[lanes].T
        whole = jnp.sum(weight * bias_column_ref[...], axis=0, keepdims=True)
        along = jnp.sum(weight * turned, axis=0, keepdims=True)
        tiles[pl.ds(block, 1)] = (along - shift_ref[:, lanes] * whole) / gain_ref[:, lanes]
        tiles[pl.ds(10 + block, 1)] = whole
    tiles[pl.ds(20, 44)] = small_ref[...]
    for run in range(8):
        edge[run] = tiles[pl.ds(run * 15 // 2, 8)]
    mixing = exchange(place, edge, small_in, local, small_send, small_recv)
    next(mixing)

    stage[...] = jnp.zeros(stage.shape, F32)
    for name, lanes in (("query", 0), ("key", 256), ("value", 512)):
        stage_heads(stage, name, joined_ref, lanes, column)
    stage_head_bias(stage, "query_bias", bias_ref, 0)
    stage_head_bias(stage, "value_bias", bias_ref, 512)
    stage_share(stage, "out", out_ref, 0, 40, place)
    stage_share(stage, "down", sum_ref, 160, 160, place)
    stage_up(stage, sum_ref, place)
    stage[pl.ds(TABLE["up_bias"][0], 5)] = up_bias_ref[...]
    pack_rows(stage, packed)

    def produce(group, core, start):
        first = pl.multiple_of(group * GROUP_STEP + start, 16)
        return packed[pl.ds(first, GROUP_ROWS // 2)].astype(F32)

    def result(rows, total):
        grads_ref[rows] = total

    half = GROUP_ROWS // 2
    plane = plane_reduce(place, produce, half, half, result, bufs, sems, False)
    next(plane)
    next(plane)
    for _ in mixing:
        pass
    small_all[place.dp] = jnp.sum(small_in[...], axis=0)
    for index, group in enumerate(peers):
        tell(3 + index, small_all.at[place.dp], small_all, group, lambda copy: copy.start())
    next(line)
    next(plane)
    next(line)
    next(plane)
    drive(line, plane)
    for index, group in enumerate(peers):
        heard(index, peak_all, group)
        heard(3 + index, small_all, group)
    top = peak_ref[...]
    for group in peers:
        top = jnp.maximum(top, peak_all[group])
    peak_out[...] = top
    whole = jnp.sum(small_all[...], axis=0)
    lane = lane_of(8)
    row = lax.broadcasted_iota(jnp.int32, (8, 128), 0)
    tiles[...] = jnp.zeros((64, 128), F32)
    tiles[pl.ds(8, 8)] = whole
    ahead = pltpu.roll(tiles[pl.ds(9, 8)], 64, 1)
    here = pltpu.roll(whole, 64, 1)
    odd = jnp.where(lane < 64, here, ahead)
    run_of = jnp.where(place.c == 1, odd, whole)
    run_of = jnp.where(jnp.logical_and(row == 7, lane >= 64), 0.0, run_of)
    small_out[...] = run_of
    tiles[pl.ds(8, 8)] = run_of
    wide = lane_of(16)
    entry = jnp.where(
        wide >= 64, pltpu.roll(tiles[pl.ds(1, 16)], 64, 1), pltpu.roll(tiles[pl.ds(0, 16)], 64, 1)
    )

    @pl.when(place.dp == 3)
    def _():
        grads_ref[pl.ds(GROUP_STEP, 16)] += entry

    for index, group in enumerate(peers):
        tell(index, peak_ref, peak_all, group, lambda copy: copy.wait_send())
        tell(3 + index, small_all.at[place.dp], small_all, group, lambda copy: copy.wait_send())


def finish(grads, weight, joined, bias, sums, out, up_bias, small, peaks, frames, middle, gain, shift):
    shapes, split = flatten(
        *line_reduce_scratch(FIRST_ROWS, 1280, True),
        *plane_reduce_scratch(GROUP_ROWS // 2, 128, False),
    )
    return pl.pallas_call(
        functools.partial(finish_kernel, split),
        out_shape=(
            jax.ShapeDtypeStruct((FIRST_ROWS, 1280), F32),
            jax.ShapeDtypeStruct((GROUP_ROWS, 128), F32),
            jax.ShapeDtypeStruct((8, 128), F32),
            jax.ShapeDtypeStruct(peaks.shape, F32),
        ),
        in_specs=[VMEM] * 14,
        out_specs=(VMEM,) * 4,
        scratch_shapes=[
            pltpu.VMEM((STAGE_ROWS, 128), F32),
            pltpu.VMEM((PACK_ROWS, 128), BF),
            pltpu.VMEM((2, 1280, 128), F32),
            pltpu.VMEM((64, 128), F32),
            pltpu.VMEM((8, 8, 128), F32),
            pltpu.VMEM((4, 8, 128), F32),
            pltpu.VMEM((4,) + peaks.shape, F32),
            pltpu.VMEM((8, 8, 128), F32),
            pltpu.SemaphoreType.DMA(()),
            dma(8),
            dma(8),
            dma(6),
            dma(6),
            *shapes,
        ],
        compiler_params=params(7, 62),
        name="finish",
    )(
        grads, weight, joined, bias[None], bias[:, None], sums, out, up_bias, small, peaks,
        frames, middle, gain, shift,
    )


def share_master_kernel(
    split, rows_ref, grad_ref, weight_ref, frames_ref, middle_ref, gain_ref,
    whole_ref, input_grad_ref, parts, send, recv, *scratch,
):
    place = Place()
    line_bufs, line_sems = split(scratch)
    greet(place, line=True, plane=True)
    line = line_product(
        place,
        grad_ref,
        weight_ref,
        FIRST_ROWS,
        ROWS - FIRST_ROWS,
        norm_back(place, frames_ref, middle_ref, gain_ref, input_grad_ref, FIRST_ROWS),
        line_bufs,
        line_sems,
    )
    dp, mp, dpx, dpy, dpd = place.dp, place.mp, place.dpx, place.dpy, place.dpd
    half = GROUP_ROWS // 2
    part_a, part_b = pl.ds(0, half), pl.ds(half, half)
    parts[dp] = rows_ref[...].astype(BF)

    def hop(index, block, target):
        return remote(block, block, send.at[index], recv.at[index], target, mp)

    own = parts.at[dp]
    sends = [hop(0, own, dpx), hop(1, own, dpy)]
    for copy in sends:
        copy.start()
    next(line)
    next(line)
    hop(0, parts.at[dpx], dpx).wait_recv()
    sends.append(hop(2, parts.at[dpx, part_a], dpy))
    sends[-1].start()
    hop(1, parts.at[dpy], dpy).wait_recv()
    sends.append(hop(3, parts.at[dpy, part_b], dpx))
    sends[-1].start()
    next(line)
    next(line)
    hop(2, parts.at[dpd, part_a], dpy).wait_recv()
    hop(3, parts.at[dpd, part_b], dpx).wait_recv()
    for group in range(4):
        base = group * GROUP_STEP
        first = parts[group, pl.ds(0, 32)].astype(F32)
        if group > 0:
            first = first + parts[group - 1, pl.ds(GROUP_STEP, 32)].astype(F32)
        whole_ref[pl.ds(base, 32)] = first
        for start in range(32, GROUP_STEP, 1192):
            whole_ref[pl.ds(base + start, 1192)] = parts[group, pl.ds(start, 1192)].astype(F32)
    whole_ref[pl.ds(4 * GROUP_STEP, 16)] = parts[3, pl.ds(GROUP_STEP, 16)].astype(F32)
    for copy in sends:
        copy.wait_send()
    drive(line)


def share_master(rows, grads, weight, frames, middle, gain):
    shapes, split = flatten(*line_reduce_scratch(ROWS - FIRST_ROWS, 1280, True))
    return pl.pallas_call(
        functools.partial(share_master_kernel, split),
        out_shape=(
            jax.ShapeDtypeStruct((PACK_END, 128), F32),
            jax.ShapeDtypeStruct((ROWS - FIRST_ROWS, 1280), F32),
        ),
        in_specs=[VMEM] * 6,
        out_specs=(VMEM, VMEM),
        scratch_shapes=[pltpu.VMEM((4, GROUP_ROWS, 128), BF), dma(4), dma(4), *shapes],
        compiler_params=params(8, 60),
        name="share_master",
    )(rows, grads, weight, frames, middle, gain)


def fast_body(
    frames,
    lengths,
    key_mask,
    cotangent,
    gain_one,
    shift_one,
    query_weight,
    query_bias,
    key_weight,
    value_weight,
    value_bias,
    out_weight,
    out_bias,
    gain_two,
    shift_two,
    up_weight,
    up_bias,
    down_weight,
    down_bias,
    master,
    moment_one,
    moment_two,
    adam_step,
    hyper_rates,
):
    group = lax.axis_index("dp")
    position = jnp.arange(1024, dtype=jnp.int32)
    keep_query = position[None, :] < lengths[:, None]
    keep_key = jnp.logical_and(keep_query, key_mask == 1)
    mask = jnp.where(keep_key, 0.0, MASK_VALUE)[:, :, None]
    live = keep_query.astype(F32)[:, None, :]
    gain_first = gain_one.astype(F32)
    shift_first = shift_one.astype(F32)
    gain_second = gain_two.astype(F32)
    shift_second = shift_two.astype(F32)
    inputs = frames.transpose(1, 0, 2).reshape(ROWS, 1280).astype(F32)
    upstream_low = cotangent.transpose(1, 0, 2).reshape(ROWS, 1280)
    upstream = upstream_low.astype(F32)
    normed = layer_norm(inputs, gain_first, shift_first).astype(BF)

    def head_rows(weight):
        rows = weight.T.reshape(2, HD, 1280)
        return jnp.pad(rows, ((0, 0), (0, 128 - HD), (0, 0))).reshape(256, 1280)

    def head_lanes(bias):
        lanes = bias.astype(F32).reshape(2, HD)
        return jnp.pad(lanes, ((0, 0), (0, 128 - HD))).reshape(256)

    joined_weight = jnp.concatenate(
        [head_rows(query_weight), head_rows(key_weight), head_rows(value_weight)]
    )
    joined_bias = jnp.concatenate(
        [head_lanes(query_bias), jnp.zeros((256,), F32), head_lanes(value_bias)]
    )[None]
    normed_full, qkv, upstream_full = project(normed, upstream_low, joined_weight, joined_bias)
    qkv = qkv.reshape(8, 3, 128, 768)

    quarter = group * 160
    up_share = lax.dynamic_slice_in_dim(up_weight, quarter, 160, 1).T
    down_share = lax.dynamic_slice_in_dim(down_weight, quarter, 160, 0)
    bias_share = lax.dynamic_slice_in_dim(up_bias, quarter, 160, 0)
    bias_rows = jnp.pad(bias_share[None], ((0, 15), (0, 1280 - 160)))
    message = jnp.concatenate([up_share, down_share, bias_rows])
    outer = jnp.pad(lax.dynamic_slice_in_dim(out_weight, group * 40, 40, 0), ((0, 8), (0, 0)))
    attended, logs, peaks, gathered, outer_all = attend(qkv, mask, live, message, outer)
    up_lanes = gathered[:, 320, :160].reshape(1, 640).astype(F32)
    out_rows = outer_all.reshape(4, 2, 4, 48, 1280)[:, :, :, :40]
    out_rows = out_rows.transpose(2, 1, 0, 3, 4).reshape(8, 160, 1280)

    branch = jnp.einsum("schr,shd->crd", attended, out_rows, preferred_element_type=F32)
    middle = inputs + branch.reshape(ROWS, 1280) + out_bias.astype(F32)
    normed_two = layer_norm(middle, gain_second, shift_second).astype(BF)
    normed_two_grad, hidden, feed_grads, _ = feed_forward(
        normed_two, upstream_full, gathered, up_lanes
    )

    _, norm_two_pull = jax.vjp(layer_norm, middle, gain_second, shift_second)
    middle_norm_grad, gain_two_grad, shift_two_grad = norm_two_pull(normed_two_grad)
    middle_grad = upstream + middle_norm_grad
    branch_grad = middle_grad.astype(BF)
    branch_clips = branch_grad.reshape(3, 128, 1280)
    out_grad = jnp.einsum("schr,crd->shd", attended, branch_clips, preferred_element_type=F32)
    attended_grad = jnp.einsum(
        "shd,crd->schr", out_rows, branch_clips, preferred_element_type=F32
    ).astype(BF)
    out_quarters = jnp.pad(
        out_grad.astype(BF).reshape(4, 2, 4, 40, 1280), ((0, 0),) * 3 + ((0, 8), (0, 0))
    )
    out_quarters = out_quarters.transpose(2, 1, 0, 3, 4).reshape(4, 2, 192, 1280)
    joined_grad, feed, feed_sum, out_sum = attend_back(
        qkv, mask, logs, attended_grad, hidden, gathered, feed_grads, out_quarters
    )
    layer_out = (middle + feed + down_bias.astype(F32)).astype(BF)
    joined_grad = joined_grad.reshape(8, ROWS, 768)
    joined_weight_grad = jnp.einsum(
        "prd,pre->de", normed_full, joined_grad, preferred_element_type=F32
    )
    joined_bias_grad = jnp.sum(joined_grad.astype(F32), axis=(0, 1))

    level = lax.axis_index("mp") // 2
    up_bias_share = lax.dynamic_slice_in_dim(feed_sum[320], level * 160, 160, 0)
    up_bias_rows = lax.dynamic_update_slice(
        jnp.zeros((640,), F32), up_bias_share, (quarter,)
    ).reshape(5, 128)
    small_rows = jnp.concatenate(
        [
            jnp.sum(branch_grad.astype(F32), axis=0),
            gain_two_grad,
            shift_two_grad,
            jnp.sum(upstream, axis=0),
            jnp.zeros((512,), F32),
        ]
    ).reshape(44, 128)
    frame_rows = frames.transpose(1, 0, 2).reshape(ROWS, 1280)
    first_grad, grad_rows, small_sum, peak_sum = finish(
        joined_grad,
        joined_weight,
        joined_weight_grad,
        joined_bias_grad,
        feed_sum,
        out_sum,
        up_bias_rows,
        small_rows,
        peaks,
        frame_rows,
        middle_grad,
        gain_first[None],
        shift_first[None],
    )
    small_total = small_sum.reshape(1024)[:960]
    head_peak = jnp.max(peak_sum, axis=(1, 2)) / math.sqrt(HD)
    share_size = master.shape[1]
    owned_grads = lax.dynamic_slice(
        grad_rows.reshape(1, GROUP_ROWS * 128), (0, 480 * group), (1, share_size)
    )
    learn_rate = hyper_rates[0]
    weight_decay = hyper_rates[1]
    logit_cap = hyper_rates[2]
    step_count = adam_step[0].astype(F32)
    first_new = BETA_FIRST * moment_one + (1.0 - BETA_FIRST) * owned_grads
    second_new = BETA_SECOND * moment_two + (1.0 - BETA_SECOND) * owned_grads * owned_grads
    first_hat = first_new * (learn_rate / (1.0 - jnp.power(BETA_FIRST, step_count)))
    second_hat = second_new * (1.0 / (1.0 - jnp.power(BETA_SECOND, step_count)))
    entry_index = group * share_size + lax.broadcasted_iota(jnp.int32, (1, share_size), 1)
    query_end = 1280 * 160
    query_bias_end = query_end + 160
    key_end = query_bias_end + 1280 * 160
    block = jnp.floor((entry_index.astype(F32) + 0.5) * (1.0 / HD))
    odd = block - 2.0 * jnp.floor(block * 0.5) > 0.5
    root_factor = jnp.sqrt(logit_cap / jnp.maximum(head_peak, logit_cap))
    head_factor = jnp.where(odd, root_factor[1], root_factor[0])
    factor = jnp.where(entry_index < key_end, head_factor, 1.0)
    master_new = (
        master * (1.0 - learn_rate * weight_decay)
        - first_hat / (jnp.sqrt(second_hat) + ADAM_EPSILON)
    ) * factor

    def placed_rows(offset):
        room = GROUP_ROWS * 128 - share_size - offset
        return lambda value: jnp.pad(value, ((0, 0), (offset, room))).reshape(GROUP_ROWS, 128)

    master_rows = lax.switch(group, [placed_rows(480 * part) for part in range(4)], master_new)
    whole, second_grad = share_master(
        master_rows, joined_grad, joined_weight, frame_rows, middle_grad, gain_first[None]
    )
    input_grad = jnp.concatenate([first_grad, second_grad])
    whole = lax.optimization_barrier(whole.reshape(1, PACK_END * 128))
    weights_new = whole[:, : 4 * share_size].astype(BF)
    return (
        layer_out.reshape(3, 128, 1280).transpose(1, 0, 2),
        input_grad.reshape(3, 128, 1280).transpose(1, 0, 2),
        owned_grads,
        master_new,
        first_new,
        second_new,
        weights_new,
        small_total,
    )


def body(
    frames,
    lengths,
    key_mask,
    cotangent,
    gain_one,
    shift_one,
    query_weight,
    query_bias,
    key_weight,
    value_weight,
    value_bias,
    out_weight,
    out_bias,
    gain_two,
    shift_two,
    up_weight,
    up_bias,
    down_weight,
    down_bias,
    master,
    moment_one,
    moment_two,
    adam_step,
    hyper_rates,
):
    local_rows, clip_count, model_width = frames.shape
    total_rows = key_mask.shape[1]
    head_cols = query_weight.shape[1]
    heads_here = head_cols // HD
    block_rows = min(512, total_rows)
    blocks = total_rows // block_rows
    score_scale = 1.0 / math.sqrt(HD)
    position = jnp.arange(total_rows, dtype=jnp.int32)
    keep_query = position[None, :] < lengths[:, None]
    keep_key = jnp.logical_and(keep_query, key_mask == 1)
    gain_first = gain_one.astype(jnp.float32)
    shift_first = shift_one.astype(jnp.float32)
    gain_second = gain_two.astype(jnp.float32)
    shift_second = shift_two.astype(jnp.float32)
    inputs = frames.astype(jnp.float32)
    normed = layer_norm(inputs, gain_first, shift_first).astype(jnp.bfloat16)
    joined_weight = jnp.concatenate([query_weight, key_weight, value_weight], axis=1)
    joined_bias = jnp.concatenate(
        [
            query_bias.astype(jnp.float32),
            jnp.zeros((head_cols,), jnp.float32),
            value_bias.astype(jnp.float32),
        ]
    )
    normed_full = lax.all_gather(normed, "mp", axis=0, tiled=True)
    projected = (
        jnp.einsum("rcd,de->rce", normed_full, joined_weight, preferred_element_type=jnp.float32)
        + joined_bias
    ).astype(jnp.bfloat16)
    query = projected[:, :, :head_cols].reshape(total_rows, clip_count, heads_here, HD)
    keys = projected[:, :, head_cols : 2 * head_cols].reshape(
        total_rows, clip_count, heads_here, HD
    )
    values = projected[:, :, 2 * head_cols :].reshape(total_rows, clip_count, heads_here, HD)

    def scores_of(row_start):
        query_block = lax.dynamic_slice_in_dim(query, row_start, block_rows, 0)
        raw_scores = (
            jnp.einsum("qchd,kchd->chqk", query_block, keys, preferred_element_type=jnp.float32)
            * score_scale
        )
        return (query_block, jnp.where(keep_key[:, None, None, :], raw_scores, MASK_VALUE))

    def forward_block(block_index):
        row_start = block_index * block_rows
        _, masked = scores_of(row_start)
        row_peak = jnp.max(masked, axis=-1, keepdims=True)
        exp_scores = jnp.exp(masked - row_peak)
        row_total = jnp.sum(exp_scores, axis=-1, keepdims=True)
        probability = (exp_scores / row_total).astype(jnp.bfloat16)
        attended = jnp.einsum(
            "chqk,kchd->qchd", probability, values, preferred_element_type=jnp.float32
        ).astype(jnp.bfloat16)
        live_rows = lax.dynamic_slice_in_dim(keep_query, row_start, block_rows, 1)
        block_peak = jnp.max(
            jnp.where(live_rows[:, None, :], row_peak[..., 0], MASK_VALUE), axis=(0, 2)
        )
        return (attended, (row_peak + jnp.log(row_total))[..., 0], block_peak)

    attended_blocks, log_totals, block_peaks = lax.map(forward_block, jnp.arange(blocks))
    attended_full = attended_blocks.reshape(total_rows, clip_count, head_cols)
    head_peak = lax.pmax(jnp.max(block_peaks, axis=0), "dp")
    rows_here = attended_full
    attn_branch = lax.psum_scatter(
        jnp.einsum("rck,kd->rcd", rows_here, out_weight, preferred_element_type=jnp.float32),
        "mp",
        scatter_dimension=0,
        tiled=True,
    ) + out_bias.astype(jnp.float32)
    middle = inputs + attn_branch
    normed_two = layer_norm(middle, gain_second, shift_second).astype(jnp.bfloat16)
    upstream = cotangent.astype(jnp.float32)
    normed_two_full = lax.all_gather(normed_two, "mp", axis=0, tiled=True)
    before = jnp.einsum(
        "rcd,df->rcf", normed_two_full, up_weight, preferred_element_type=jnp.float32
    ) + up_bias.astype(jnp.float32)
    hidden = exact_gelu(before).astype(jnp.bfloat16)
    rows_here = hidden
    feed = lax.psum_scatter(
        jnp.einsum(
            "rcf,fd->rcd", rows_here, down_weight, preferred_element_type=jnp.float32
        ).astype(jnp.bfloat16),
        "mp",
        scatter_dimension=0,
        tiled=True,
    ).astype(jnp.float32) + down_bias.astype(jnp.float32)
    layer_out = (middle + feed).astype(jnp.bfloat16)
    feed_grad_full = lax.all_gather(cotangent, "mp", axis=0, tiled=True)
    down_grad = jnp.einsum(
        "rcf,rcd->fd", hidden, feed_grad_full, preferred_element_type=jnp.float32
    )
    hidden_grad = jnp.einsum(
        "rcd,fd->rcf", feed_grad_full, down_weight, preferred_element_type=jnp.float32
    )
    _, gelu_pull = jax.vjp(exact_gelu, before)
    before_grad = gelu_pull(hidden_grad)[0].astype(jnp.bfloat16)
    up_bias_grad = jnp.sum(before_grad.astype(jnp.float32), axis=(0, 1))
    up_grad = jnp.einsum(
        "rcd,rcf->df", normed_two_full, before_grad, preferred_element_type=jnp.float32
    )
    rows_here = before_grad
    normed_two_grad = lax.psum_scatter(
        jnp.einsum("rcf,df->rcd", rows_here, up_weight, preferred_element_type=jnp.float32),
        "mp",
        scatter_dimension=0,
        tiled=True,
    )
    _, norm_two_pull = jax.vjp(layer_norm, middle, gain_second, shift_second)
    middle_norm_grad, gain_two_grad, shift_two_grad = norm_two_pull(normed_two_grad)
    middle_grad = upstream + middle_norm_grad
    branch_grad = middle_grad.astype(jnp.bfloat16)
    branch_grad_full = lax.all_gather(branch_grad, "mp", axis=0, tiled=True)
    out_grad = jnp.einsum(
        "rck,rcd->kd", attended_full, branch_grad_full, preferred_element_type=jnp.float32
    )
    attended_grad = jnp.einsum(
        "rcd,kd->rck", branch_grad_full, out_weight, preferred_element_type=jnp.float32
    ).astype(jnp.bfloat16)
    attended_grad = attended_grad.reshape(total_rows, clip_count, heads_here, HD)

    def backward_block(carry, block_index):
        key_total, value_total = carry
        row_start = block_index * block_rows
        query_block, masked = scores_of(row_start)
        log_total = log_totals[block_index]
        probability = jnp.exp(masked - log_total[..., None])
        grad_block = lax.dynamic_slice_in_dim(attended_grad, row_start, block_rows, 0)
        value_total = value_total + jnp.einsum(
            "chqk,qchd->kchd",
            probability.astype(jnp.bfloat16),
            grad_block,
            preferred_element_type=jnp.float32,
        )
        prob_grad = jnp.einsum(
            "qchd,kchd->chqk", grad_block, values, preferred_element_type=jnp.float32
        )
        score_grad = (
            probability * (prob_grad - jnp.sum(probability * prob_grad, axis=-1, keepdims=True))
        ).astype(jnp.bfloat16)
        query_grad = (
            jnp.einsum("chqk,kchd->qchd", score_grad, keys, preferred_element_type=jnp.float32)
            * score_scale
        ).astype(jnp.bfloat16)
        key_total = (
            key_total
            + jnp.einsum(
                "chqk,qchd->kchd", score_grad, query_block, preferred_element_type=jnp.float32
            )
            * score_scale
        )
        return ((key_total, value_total), query_grad)

    empty_grad = jnp.zeros((total_rows, clip_count, heads_here, HD), jnp.float32)
    (key_total, value_total), query_blocks = lax.scan(
        backward_block, (empty_grad, empty_grad), jnp.arange(blocks)
    )
    joined_grad = jnp.concatenate(
        [
            query_blocks.reshape(total_rows, clip_count, head_cols),
            key_total.reshape(total_rows, clip_count, head_cols).astype(jnp.bfloat16),
            value_total.reshape(total_rows, clip_count, head_cols).astype(jnp.bfloat16),
        ],
        axis=-1,
    )
    joined_bias_grad = jnp.sum(joined_grad.astype(jnp.float32), axis=(0, 1))
    normed_back = lax.all_gather(normed, "mp", axis=0, tiled=True)
    joined_weight_grad = jnp.einsum(
        "rcd,rce->de", normed_back, joined_grad, preferred_element_type=jnp.float32
    )
    rows_here = joined_grad
    normed_grad = lax.psum_scatter(
        jnp.einsum(
            "rce,de->rcd", rows_here, joined_weight, preferred_element_type=jnp.float32
        ).astype(jnp.bfloat16),
        "mp",
        scatter_dimension=0,
        tiled=True,
    ).astype(jnp.float32)
    _, norm_one_pull = jax.vjp(layer_norm, inputs, gain_first, shift_first)
    input_norm_grad, gain_one_grad, shift_one_grad = norm_one_pull(normed_grad)
    input_grad = middle_grad + input_norm_grad
    out_bias_grad = jnp.sum(branch_grad.astype(jnp.float32), axis=(0, 1))
    down_bias_grad = jnp.sum(upstream, axis=(0, 1))
    small_terms = jnp.concatenate(
        [
            gain_one_grad,
            shift_one_grad,
            out_bias_grad,
            gain_two_grad,
            shift_two_grad,
            down_bias_grad,
        ]
    )
    small_share = lax.psum_scatter(small_terms, "mp", scatter_dimension=0, tiled=True)
    small_total = lax.psum(small_share, "dp")
    packed = jnp.concatenate(
        [
            joined_weight_grad[:, :head_cols].reshape(-1),
            joined_bias_grad[:head_cols],
            joined_weight_grad[:, head_cols : 2 * head_cols].reshape(-1),
            joined_weight_grad[:, 2 * head_cols :].reshape(-1),
            joined_bias_grad[2 * head_cols :],
            out_grad.reshape(-1),
            up_grad.reshape(-1),
            up_bias_grad,
            down_grad.reshape(-1),
            small_share,
        ]
    )
    owned_grads = lax.psum_scatter(
        packed.astype(jnp.bfloat16), "dp", scatter_dimension=0, tiled=True
    ).astype(jnp.float32)
    share_size = owned_grads.shape[0]
    learn_rate = hyper_rates[0]
    weight_decay = hyper_rates[1]
    logit_cap = hyper_rates[2]
    step_count = adam_step[0].astype(jnp.float32)
    first_new = BETA_FIRST * moment_one[0] + (1.0 - BETA_FIRST) * owned_grads
    second_new = BETA_SECOND * moment_two[0] + (1.0 - BETA_SECOND) * owned_grads * owned_grads
    first_hat = first_new / (1.0 - jnp.power(BETA_FIRST, step_count))
    second_hat = second_new / (1.0 - jnp.power(BETA_SECOND, step_count))
    entry_index = lax.axis_index("dp") * share_size + jnp.arange(share_size, dtype=jnp.int32)
    query_end = model_width * head_cols
    query_bias_end = query_end + head_cols
    key_end = query_bias_end + model_width * head_cols
    column = jnp.where(
        entry_index < query_end,
        entry_index % head_cols,
        jnp.where(
            entry_index < query_bias_end,
            entry_index - query_end,
            (entry_index - query_bias_end) % head_cols,
        ),
    )
    head_index = column // HD
    root_factor = jnp.sqrt(logit_cap / jnp.maximum(head_peak, logit_cap))
    head_factor = jnp.zeros((share_size,), jnp.float32)
    for head_number in range(heads_here):
        head_factor = head_factor + jnp.where(
            head_index == head_number, root_factor[head_number], 0.0
        )
    factor = jnp.where(entry_index < key_end, head_factor, 1.0)
    master_here = master[0]
    master_new = (
        master_here
        - learn_rate
        * (first_hat / (jnp.sqrt(second_hat) + ADAM_EPSILON) + weight_decay * master_here)
    ) * factor
    weights_full = lax.all_gather(master_new.astype(jnp.bfloat16), "dp", axis=0, tiled=True)
    return (
        layer_out,
        input_grad,
        owned_grads[None],
        master_new[None],
        first_new[None],
        second_new[None],
        weights_full[None],
        small_total,
    )


def solution(mesh):
    chosen = fast_body if dict(mesh.shape) == {"dp": 4, "mp": 8} else body
    placed = (
        P("mp", "dp", None),
        P("dp"),
        P("dp", None),
        P("mp", "dp", None),
        P(),
        P(),
        P(None, "mp"),
        P("mp"),
        P(None, "mp"),
        P(None, "mp"),
        P("mp"),
        P("mp", None),
        P(),
        P(),
        P(),
        P(None, "mp"),
        P("mp"),
        P("mp", None),
        P(),
        P("mp", "dp"),
        P("mp", "dp"),
        P("mp", "dp"),
        P(),
        P(),
    )
    return jax.shard_map(
        chosen,
        mesh=mesh,
        in_specs=placed,
        out_specs=(
            P("mp", "dp", None),
            P("mp", "dp", None),
            P("mp", "dp"),
            P("mp", "dp"),
            P("mp", "dp"),
            P("mp", "dp"),
            P("mp", None),
            P("mp"),
        ),
        check_vma=False,
    )
```

```python
import functools
import math

import jax
import jax.numpy as jnp
from jax import lax
from jax.experimental import pallas as pl
from jax.experimental.pallas import tpu as pltpu
from jax.sharding import PartitionSpec as P

HD = 80


NORM_EPSILON = 1e-05
ADAM_EPSILON = 1e-08
BETA_FIRST = 0.9
BETA_SECOND = 0.999
MASK_VALUE = -1e30


def layer_norm(value, gain, shift):
    center = value - jnp.mean(value, axis=-1, keepdims=True)
    spread = jnp.mean(center * center, axis=-1, keepdims=True)
    return center * lax.rsqrt(spread + NORM_EPSILON) * gain + shift


def exact_gelu(argument):
    return jax.nn.gelu(argument, approximate=False)


MESH = pl.DeviceIdType.MESH
ANY = pl.BlockSpec(memory_space=pl.ANY)
VMEM = pl.BlockSpec(memory_space=pltpu.VMEM)
LINE = 4
ROWS = 384
BF = jnp.bfloat16
F32 = jnp.float32


class Place:
    def __init__(self):
        self.dp = lax.axis_index("dp")
        self.mp = lax.axis_index("mp")
        self.z = self.mp // 2
        self.c = self.mp % 2
        self.pair = self.z * 2 + 1 - self.c
        self.dpx = self.dp + 1 - 2 * (self.dp % 2)
        self.dpy = (self.dp + 2) % 4
        self.dpd = 3 - self.dp

    def zorder(self, event):
        if event == 0:
            return self.z
        if event == 1:
            return self.z + 1 - 2 * (self.z % 2)
        if event == 2:
            return 2 - self.z // 2
        return 3 - 3 * (self.z // 2)


def greet(place, mp_all=False, line=False, plane=False, pair=True):
    barrier = pltpu.get_barrier_semaphore()
    count = 0

    def signal(dp, mp):
        pl.semaphore_signal(barrier, inc=1, device_id=(dp, mp), device_id_type=MESH)

    if mp_all:
        for hop in range(1, 8):
            signal(place.dp, (place.mp + hop) % 8)
        count += 7
    else:
        if pair:
            signal(place.dp, place.pair)
            count += 1
        if line:

            @pl.when(place.z > 0)
            def _():
                signal(place.dp, place.mp - 2)

            @pl.when(place.z < LINE - 1)
            def _():
                signal(place.dp, place.mp + 2)

    if plane:
        for other in (place.dpx, place.dpy, place.dpd):
            signal(other, place.mp)
        count += 3
    if line and not mp_all:
        pl.semaphore_wait(barrier, count + 1 + (place.z + 1) // 2 % 2)
    else:
        pl.semaphore_wait(barrier, count)


def remote(src, dst, send, recv, dp, mp):
    return pltpu.make_async_remote_copy(
        src_ref=src,
        dst_ref=dst,
        send_sem=send,
        recv_sem=recv,
        device_id=(dp, mp),
        device_id_type=MESH,
    )


def line_gather(place, src, out, local, send, recv, paired, ready=None, rows=None):
    dp, z, c, mp, pair = place.dp, place.z, place.c, place.mp, place.pair

    def at(slot):
        if rows is None:
            return out.at[slot]
        return out.at[pl.ds(pl.multiple_of(slot * rows, 16), rows)]

    def slot_of(level, core):
        return level * 2 + core if paired else level

    def hop(event, slot, source, direction, target):
        return remote(source, at(slot), send.at[event, direction], recv.at[slot], dp, target)

    own = slot_of(z, c)
    keep = pltpu.make_async_copy(src, at(own), local)
    keep.start()

    def ways(event, level, slot, source, act):
        up = z < LINE - 1
        down = z > 0
        if event > 0:
            up = jnp.logical_and(up, level < z)
            down = jnp.logical_and(down, level > z)

        @pl.when(up)
        def _():
            act(hop(event, slot, source, 1, mp + 2))

        @pl.when(down)
        def _():
            act(hop(event, slot, source, 2, mp - 2))

        if paired:
            act(hop(event, slot, source, 0, pair))

    ways(0, z, own, src, lambda copy: copy.start())
    yield
    if ready is not None:
        keep.wait()
        ready(own)
        if paired:
            other = slot_of(z, 1 - c)
            hop(0, other, at(other), 0, pair).wait_recv()
            ready(other)

    def settle(event):
        level = place.zorder(event)
        ready(slot_of(level, c))
        if paired:
            other = slot_of(level, 1 - c)
            hop(event, other, at(other), 0, pair).wait_recv()
            ready(other)

    for event in range(1, LINE):
        level = place.zorder(event)
        slot = slot_of(level, c)
        hop(event, slot, at(slot), 0, pair).wait_recv()
        ways(event, level, slot, at(slot), lambda copy: copy.start())
        if ready is not None and event > 1:
            if event == 2:
                settle(1)
            settle(event)
        yield
    if ready is None:
        if paired:
            for level in range(LINE):
                other = slot_of(level, 1 - c)
                hop(0, other, at(other), 0, pair).wait_recv()
        keep.wait()
    for event in range(LINE):
        level = place.zorder(event)
        slot = slot_of(level, c)
        ways(event, level, slot, at(slot), lambda copy: copy.wait_send())
    yield


def plane_gather(place, src, out, local, send, recv, ready=None, primed=False):
    dp, c, mp, pair = place.dp, place.c, place.mp, place.pair
    dpx, dpy, dpd = place.dpx, place.dpy, place.dpd
    half = src.shape[0] // 2
    part_a, part_b = pl.ds(0, half), pl.ds(half, half)

    def at(group, core):
        return out.at[group * 2 + core]

    def hop(index, block, group, target):
        return remote(block, block, send.at[index], recv.at[index], group, target)

    def done(group, core):
        if ready is not None:
            ready(group * 2 + core)

    keep = pltpu.make_async_copy(src, at(dp, c), local)
    here = at(dp, c)
    from_x, from_y, from_d = at(dpx, c), at(dpy, c), at(dpd, c)
    firsts = [
        remote(src, here, send.at[0], recv.at[0], dp, pair),
        remote(src, here, send.at[1], recv.at[1], dpx, mp),
        remote(src, here, send.at[2], recv.at[2], dpy, mp),
    ]
    seconds = [
        hop(3, from_x.at[part_a], dpy, mp),
        hop(4, from_y.at[part_b], dpx, mp),
        hop(5, from_x, dp, pair),
        hop(6, from_y, dp, pair),
        hop(7, from_d.at[part_a], dp, pair),
        hop(8, from_d.at[part_b], dp, pair),
    ]
    if primed:
        yield
    keep.start()
    for copy in firsts:
        copy.start()
    yield
    if ready is not None:
        keep.wait()
        done(dp, c)
        hop(0, at(dp, 1 - c), dp, pair).wait_recv()
        done(dp, 1 - c)
    hop(1, from_x, dpx, mp).wait_recv()
    seconds[0].start()
    hop(2, from_y, dpy, mp).wait_recv()
    seconds[1].start()
    seconds[2].start()
    seconds[3].start()
    yield
    done(dpx, c)
    hop(5, at(dpx, 1 - c), dp, pair).wait_recv()
    done(dpx, 1 - c)
    if ready is not None:
        yield
    done(dpy, c)
    hop(6, at(dpy, 1 - c), dp, pair).wait_recv()
    done(dpy, 1 - c)
    if ready is not None:
        yield
    hop(3, from_d.at[part_a], dpy, mp).wait_recv()
    seconds[4].start()
    hop(4, from_d.at[part_b], dpx, mp).wait_recv()
    seconds[5].start()
    done(dpd, c)
    other = at(dpd, 1 - c)
    hop(7, other.at[part_a], dp, pair).wait_recv()
    hop(8, other.at[part_b], dp, pair).wait_recv()
    done(dpd, 1 - c)
    yield
    if ready is None:
        hop(0, at(dp, 1 - c), dp, pair).wait_recv()
        keep.wait()
    for copy in firsts + seconds:
        copy.wait_send()
    yield


def drive(*programs):
    live = list(programs)
    while live:
        for program in list(live):
            try:
                next(program)
            except StopIteration:
                live.remove(program)


def dma(*shape):
    return pltpu.SemaphoreType.DMA(shape)


def params(cid, vmem=40):
    return pltpu.CompilerParams(
        collective_id=cid, has_side_effects=True, vmem_limit_bytes=vmem << 20
    )


def exchange(place, src, out, local, send, recv):
    dp, mp = place.dp, place.mp
    keep = pltpu.make_async_copy(src.at[mp], out.at[mp], local)
    keep.start()
    sends = []
    for hop in range(1, 8):
        target = (mp + hop) % 8
        sends.append(
            remote(src.at[target], out.at[mp], send.at[hop], recv.at[hop], dp, target)
        )
        sends[-1].start()
    yield
    keep.wait()
    for hop in range(1, 8):
        origin = (mp + 8 - hop) % 8
        remote(out.at[origin], out.at[origin], send.at[hop], recv.at[hop], dp, origin).wait_recv()
    for copy in sends:
        copy.wait_send()
    yield


def line_reduce(place, produce, tiles, result, bufs, sems, paired):
    dp, z, c, mp, pair = place.dp, place.z, place.c, place.mp, place.pair
    above_block, below_block, out_block = bufs["above"], bufs["below"], bufs["out"]
    order = [place.zorder(event) for event in (3, 2, 1, 0)]
    inner = jnp.logical_and(z > 0, z < LINE - 1)
    outer = jnp.logical_or(z == 0, z == LINE - 1)

    @pl.when(z == LINE - 1)
    def _():
        above_block[...] = jnp.zeros(above_block.shape, BF)

    @pl.when(z == 0)
    def _():
        below_block[...] = jnp.zeros(below_block.shape, BF)

    def from_above(level):
        return above_block.at[jnp.minimum(level, LINE - 2)]

    def from_below(level):
        return below_block.at[jnp.maximum(level - 1, 0)]

    def across(step, level):
        return remote(
            bufs["pair_out"].at[step % 2],
            bufs["pair_in"].at[level],
            sems["pair_send"].at[step % 2],
            sems["pair_recv"].at[level],
            dp,
            pair,
        )

    if paired:
        for step, level in enumerate(order):
            if step > 1:
                across(step - 2, order[step - 2]).wait_send()
            for rows in tiles:
                bufs["pair_out"][step % 2, rows] = produce(level, 1 - c, rows).astype(BF)
            across(step, level).start()
    yield

    def toward(step, level, act):
        @pl.when(level < z)
        def _():
            act(
                remote(
                    out_block.at[step],
                    from_above(level),
                    sems["line_send"].at[step],
                    sems["above"].at[level],
                    dp,
                    mp - 2,
                )
            )

        @pl.when(level > z)
        def _():
            act(
                remote(
                    out_block.at[step],
                    from_below(level),
                    sems["line_send"].at[step],
                    sems["below"].at[level],
                    dp,
                    mp + 2,
                )
            )

    def arrive(level, above):
        if above:
            remote(
                from_above(level),
                from_above(level),
                sems["line_send"].at[0],
                sems["above"].at[level],
                dp,
                mp,
            ).wait_recv()
        else:
            remote(
                from_below(level),
                from_below(level),
                sems["line_send"].at[0],
                sems["below"].at[level],
                dp,
                mp,
            ).wait_recv()

    def advance(step):
        level = order[step]
        if paired:
            across(step, level).wait_recv()

        @pl.when(jnp.logical_and(level < z, z < LINE - 1))
        def _():
            arrive(level, True)

        @pl.when(jnp.logical_and(level > z, z > 0))
        def _():
            arrive(level, False)

        for rows in tiles:
            total = produce(level, c, rows)
            if paired:
                total = total + bufs["pair_in"][level, rows].astype(F32)

            @pl.when(level < z)
            def _():
                out_block[step, rows] = (total + from_above(level)[rows].astype(F32)).astype(BF)

            @pl.when(level > z)
            def _():
                out_block[step, rows] = (total + from_below(level)[rows].astype(F32)).astype(BF)

        toward(step, level, lambda copy: copy.start())

    advance(0)
    for step in (1, 2):

        @pl.when(outer)
        def _():
            advance(step)

    yield
    for step in (1, 2):

        @pl.when(inner)
        def _():
            advance(step)

        yield

    if paired:
        across(3, z).wait_recv()

    @pl.when(z < LINE - 1)
    def _():
        arrive(z, True)

    @pl.when(z > 0)
    def _():
        arrive(z, False)

    for rows in tiles:
        total = produce(z, c, rows)
        if paired:
            total = total + bufs["pair_in"][z, rows].astype(F32)
        total = total + from_above(z)[rows].astype(F32) + from_below(z)[rows].astype(F32)
        result(rows, total)
    for step, level in enumerate(order):
        if paired and step > 1:
            across(step, level).wait_send()
        if step < 3:
            toward(step, level, lambda copy: copy.wait_send())
    yield


def line_reduce_scratch(rows, cols, paired):
    block = lambda n: pltpu.VMEM((n, rows, cols), BF)
    scratch = {"above": block(3), "below": block(3), "out": block(3)}
    sems = {"line_send": dma(3), "above": dma(4), "below": dma(4)}
    if paired:
        scratch.update({"pair_out": block(2), "pair_in": block(4)})
        sems.update({"pair_send": dma(2), "pair_recv": dma(4)})
    return scratch, sems


def plane_reduce(place, produce, tile, half, result, bufs, sems, paired=True, early=False):
    dp, c, mp, pair = place.dp, place.c, place.mp, place.pair
    dpx, dpy, dpd = place.dpx, place.dpy, place.dpd
    starts = range(0, half, tile)
    send, recv = sems["send"], sems["recv"]
    out_block, landed = bufs["out"], bufs["in"]
    groups = {"far": dpd, "x": dpx, "y": dpy, "own": dp}
    steps = ["x", "y", "far", "own"] if early else ["far", "x", "y", "own"]

    def across(name):
        step = steps.index(name)
        return remote(
            bufs["pair_out"].at[step % 2],
            bufs["pair_in"].at[step],
            sems["pair_send"].at[step % 2],
            sems["pair_recv"].at[step],
            dp,
            pair,
        )

    def cross(name):
        if not paired:
            return
        step = steps.index(name)
        if step > 1:
            across(steps[step - 2]).wait_send()
        for start in range(0, 2 * half, tile):
            bufs["pair_out"][step % 2, pl.ds(start, tile)] = produce(
                groups[name], 1 - c, start
            ).astype(BF)
        across(name).start()

    def crossed(name):
        if paired:
            across(name).wait_recv()

    def share(name, start):
        total = produce(groups[name], c, start)
        if paired:
            total = total + bufs["pair_in"][steps.index(name), pl.ds(start, tile)].astype(F32)
        return total

    def hop(index):
        target = (dpx, dpy, dpx, dpx, dpy, dpy)[index]
        return remote(
            out_block.at[index], landed.at[index], send.at[index], recv.at[index], target, mp
        )

    def fill(index, name, base, extra=None):
        for start in starts:
            total = share(name, base + start)
            if extra is not None:
                total = total + landed[extra, pl.ds(start, tile)].astype(F32)
            out_block[index, pl.ds(start, tile)] = total.astype(BF)
        hop(index).start()

    def far():
        crossed("far")
        fill(0, "far", 0)
        fill(1, "far", half)

    def near():
        crossed("x")
        fill(2, "x", 0)
        crossed("y")
        fill(4, "y", half)

    if early:
        cross("x")
        yield
        cross("y")
        near()
        yield
        cross("far")
        far()
        yield
        cross("own")
    else:
        cross("far")
        cross("x")
        yield
        far()
        cross("y")
        near()
        cross("own")
    yield
    hop(1).wait_recv()
    fill(3, "x", half, extra=1)
    hop(0).wait_recv()
    fill(5, "y", 0, extra=0)
    yield
    crossed("own")
    for index in (2, 3, 4, 5):
        hop(index).wait_recv()
    for base, pieces in ((0, (2, 5)), (half, (3, 4))):
        for start in starts:
            total = share("own", base + start)
            for piece in pieces:
                total = total + landed[piece, pl.ds(start, tile)].astype(F32)
            result(pl.ds(base + start, tile), total)
    for index in range(6):
        hop(index).wait_send()
    if paired:
        for name in steps[2:]:
            across(name).wait_send()
    yield


def plane_reduce_scratch(half, cols, paired=True):
    block = lambda n, rows: pltpu.VMEM((n, rows, cols), BF)
    scratch = {"out": block(6, half), "in": block(6, half)}
    sems = {"send": dma(6), "recv": dma(6)}
    if paired:
        scratch.update({"pair_out": block(2, 2 * half), "pair_in": block(4, 2 * half)})
        sems.update({"pair_send": dma(2), "pair_recv": dma(4)})
    return scratch, sems


def project_kernel(
    frames_ref, gain_ref, shift_ref, cot_ref, query_ref, key_ref, value_ref, bias_ref,
    nfull_ref, qkv_ref, cfull_ref, weight_ref,
    normed_ref, local, line_send, line_recv, plane_send, plane_recv,
):
    place = Place()
    weight_ref[...] = jnp.zeros(weight_ref.shape, BF)
    for index, ref in enumerate((query_ref, key_ref, value_ref)):
        for head in range(2):
            weight_ref[pl.ds(index * 256 + head * 128, HD)] = ref[pl.ds(head * HD, HD)]
    for start in range(0, ROWS, 128):
        rows = pl.ds(start, 128)
        normed_ref[rows] = layer_norm(
            frames_ref[rows].astype(F32), gain_ref[...], shift_ref[...]
        ).astype(BF)
    greet(place, line=True, plane=True)

    def ready(slot):
        @pl.loop(0, 3)
        def _(step):
            rows = pl.ds(step * 128, 128)
            product = lax.dot_general(
                nfull_ref[slot, rows],
                weight_ref[...],
                (((1,), (1,)), ((), ())),
                preferred_element_type=F32,
            )
            qkv_ref[slot, rows] = (product + bias_ref[...]).astype(BF)

    drive(
        line_gather(
            place, normed_ref, nfull_ref, local.at[0], line_send, line_recv, True, ready
        ),
        plane_gather(place, cot_ref, cfull_ref, local.at[1], plane_send, plane_recv),
    )


def project(frames, gain, shift, cotangent, query, key, value, bias):
    return pl.pallas_call(
        project_kernel,
        out_shape=(
            jax.ShapeDtypeStruct((8,) + frames.shape, BF),
            jax.ShapeDtypeStruct((8, ROWS, 768), BF),
            jax.ShapeDtypeStruct((8,) + cotangent.shape, BF),
            jax.ShapeDtypeStruct((768, 1280), BF),
        ),
        in_specs=[VMEM, VMEM, VMEM, ANY, VMEM, VMEM, VMEM, VMEM],
        out_specs=(VMEM, VMEM, ANY, VMEM),
        scratch_shapes=[pltpu.VMEM((ROWS, 1280), BF), dma(2), dma(4, 3), dma(8), dma(9), dma(9)],
        compiler_params=params(0),
        name="project",
    )(frames, gain, shift, cotangent, query, key, value, bias)


def attend_kernel(
    qkv_ref, mask_ref, live_ref, weights_ref, outer_ref,
    att_ref, logs_ref, peak_ref, wfull_ref, ofull_ref,
    out_ref, vt_ref, outer_all, local, send, recv, line_send, line_recv,
    outer_send, outer_recv, plane_send, plane_recv,
):
    place = Place()
    greet(place, mp_all=True, plane=True)
    outer = line_gather(
        place, outer_ref, outer_all, local.at[2], outer_send, outer_recv, False, None, 48
    )
    next(outer)
    gather = line_gather(
        place, weights_ref, wfull_ref, local.at[1], line_send, line_recv, False
    )
    next(gather)
    factor = math.log2(math.e) / math.sqrt(HD)
    peak_ref[...] = jnp.full(peak_ref.shape, MASK_VALUE, F32)

    @pl.loop(0, 6)
    def _(turn):
        clip = turn // 2
        head = turn % 2
        lane = pl.multiple_of(head * 128, 128)
        row = pl.multiple_of(head * HD, 16)
        keys = qkv_ref[:, clip, :, pl.ds(256 + lane, 128)].reshape(1024, 128)
        vt_ref[...] = qkv_ref[:, clip, :, pl.ds(512 + lane, 128)].reshape(1024, 128).T

        @pl.loop(0, 4)
        def _(block):
            query = qkv_ref[pl.ds(block * 2, 2), clip, :, pl.ds(lane, 128)].reshape(256, 128)
            columns = pl.ds(pl.multiple_of(block * 256, 256), 256)
            scores = lax.dot_general(
                keys, query, (((1,), (1,)), ((), ())), preferred_element_type=F32
            )
            scores = scores + mask_ref[clip]
            peak = jnp.max(scores, axis=0, keepdims=True)
            powers = jnp.exp2((scores - peak) * factor)
            total = jnp.sum(powers, axis=0, keepdims=True)
            mixed = lax.dot_general(
                vt_ref[...],
                powers.astype(BF),
                (((1,), (0,)), ((), ())),
                preferred_element_type=F32,
            )
            mixed = (mixed / total).astype(BF)
            for part in range(2):
                out_ref[block * 2 + part, clip, pl.ds(row, HD)] = mixed[
                    :HD, part * 128 : part * 128 + 128
                ]
            logs_ref[turn, :, columns] = peak * factor + jnp.log2(total)
            peak_ref[head] = jnp.maximum(
                peak_ref[head], jnp.where(live_ref[clip, :, columns] > 0, peak, MASK_VALUE)
            )

        @pl.when(turn == 2)
        def _():
            next(outer)

        @pl.when(turn == 4)
        def _():
            next(outer)
            next(gather)

    mixing = exchange(place, out_ref, att_ref, local.at[0], send, recv)
    next(mixing)
    for _ in outer:
        pass
    spread = plane_gather(place, outer_all, ofull_ref, local.at[3], plane_send, plane_recv)
    drive(spread, gather, mixing)


def attend(qkv, mask, live, weights, outer):
    return pl.pallas_call(
        attend_kernel,
        out_shape=(
            jax.ShapeDtypeStruct((8, 3, 160, 128), BF),
            jax.ShapeDtypeStruct((6, 1, 1024), F32),
            jax.ShapeDtypeStruct((2, 8, 256), F32),
            jax.ShapeDtypeStruct((4,) + weights.shape, BF),
            jax.ShapeDtypeStruct((8, 192, 1280), BF),
        ),
        in_specs=[VMEM, VMEM, VMEM, ANY, ANY],
        out_specs=(VMEM, VMEM, VMEM, ANY, ANY),
        scratch_shapes=[
            pltpu.VMEM((8, 3, 160, 128), BF),
            pltpu.VMEM((128, 1024), BF),
            pltpu.VMEM((192, 1280), BF),
            dma(4),
            dma(8),
            dma(8),
            dma(4, 3),
            dma(4),
            dma(4, 3),
            dma(4),
            dma(9),
            dma(9),
        ],
        compiler_params=params(1),
        name="attend",
    )(qkv, mask, live, weights, outer)


def flatten(*pairs):
    names, shapes = [], []
    for number, group in enumerate(pairs):
        for name, shape in group.items():
            names.append((number, name))
            shapes.append(shape)

    def split(refs):
        groups = [{} for _ in pairs]
        for (number, name), ref in zip(names, refs):
            groups[number][name] = ref
        return groups

    return shapes, split


def feed_forward_kernel(
    split, normed_ref, upstream_ref, weights_ref, down_ref, bias_ref,
    total_ref, hidden_ref, grads_ref, bias_out, down_all,
    normed_all, upstream_all, slope_all, rate_ref, sum_ref,
    load, local, line_local, gather_send, gather_recv, line_send, line_recv, *scratch,
):
    place = Place()
    bufs, sems = split(scratch)
    loads = []
    for slot in range(8):
        loads.append(
            pltpu.make_async_copy(upstream_ref.at[slot], upstream_all.at[slot], load.at[slot])
        )
        loads[-1].start()
    greet(place, line=True, plane=True)
    bias_out[...] = jnp.zeros(bias_out.shape, F32)

    def up_rows():
        return weights_ref[:, pl.ds(0, 160)].reshape(640, 1280)

    def down_rows():
        return down_all[...].reshape(640, 1280)

    def activate(slot, rows):
        before = (
            lax.dot_general(
                normed_all[slot, rows],
                up_rows(),
                (((1,), (1,)), ((), ())),
                preferred_element_type=F32,
            )
            + bias_ref[...]
        )
        share = 0.5 + 0.5 * lax.erf(before * math.sqrt(0.5))
        hidden_ref[slot, rows] = (before * share).astype(BF)
        density = jnp.exp(before * before * -0.5) * (1.0 / math.sqrt(2.0 * math.pi))
        return share + before * density

    def pull_back(slot, rows, rate):
        pull = lax.dot_general(
            upstream_all[slot, rows],
            down_rows(),
            (((1,), (1,)), ((), ())),
            preferred_element_type=F32,
        )
        slope = (pull * rate).astype(BF)
        slope_all[slot, rows] = slope
        bias_out[...] += jnp.sum(slope.astype(F32), axis=0, keepdims=True)

    here = [place.dp * 2 + place.c, place.dp * 2 + 1 - place.c]
    seen = []

    def ready(slot):
        index = len(seen)
        seen.append(slot)

        @pl.loop(0, 3)
        def _(step):
            rows = pl.ds(pl.multiple_of(step * 128, 128), 128)
            rate = activate(slot, rows)
            if index < 2:
                rate_ref[index, rows] = rate
            else:
                pull_back(slot, rows, rate)

        if index < 2:
            next(down)

    def finish_here():
        for index in range(2):

            @pl.loop(0, 3)
            def _(step):
                rows = pl.ds(pl.multiple_of(step * 128, 128), 128)
                pull_back(here[index], rows, rate_ref[index, rows])

    down = line_gather(
        place, down_ref, down_all, line_local, line_send, line_recv, False
    )
    gather = plane_gather(
        place, normed_ref, normed_all, local, gather_send, gather_recv, ready
    )

    def produce(group, core, start):
        return jnp.dot(
            slope_all[group * 2 + core, pl.ds(start, 192)],
            up_rows(),
            preferred_element_type=F32,
        )

    def result(rows, total):
        total_ref[rows] = total

    reduce = plane_reduce(place, produce, 192, 192, result, bufs, sems, True, True)
    next(down)
    next(gather)
    for copy in loads:
        copy.wait()
    next(gather)
    for _ in down:
        pass
    next(gather)
    next(reduce)
    next(gather)
    next(reduce)
    next(gather)
    next(reduce)
    finish_here()
    next(reduce)

    def weight_grads(left_all, right_all, base):
        for block in range(5):
            lanes = pl.ds(block * 128, 128)

            @pl.loop(0, 8)
            def _(slot):
                product = lax.dot_general(
                    left_all[slot, :, lanes],
                    right_all[slot],
                    (((0,), (0,)), ((), ())),
                    preferred_element_type=F32,
                )
                sum_ref[...] = jnp.where(slot == 0, product, sum_ref[...] + product)

            for part in range(4):
                unit = block * 128 + part * 32
                grads_ref[unit // 160, pl.ds(base + unit % 160, 32)] = sum_ref[
                    pl.ds(part * 32, 32)
                ].astype(BF)

    weight_grads(slope_all, normed_all, 0)
    next(reduce)
    weight_grads(hidden_ref, upstream_all, 160)
    for level in range(4):
        grads_ref[level, pl.ds(320, 16)] = jnp.zeros((16, 1280), BF)
        grads_ref[level, pl.ds(320, 16), pl.ds(0, 640)] = jnp.broadcast_to(
            bias_out[...], (16, 640)
        ).astype(BF)
    drive(reduce, gather)


def feed_forward(normed, upstream, weights, down, bias):
    shapes, split = flatten(*plane_reduce_scratch(192, 1280))
    return pl.pallas_call(
        functools.partial(feed_forward_kernel, split),
        out_shape=(
            jax.ShapeDtypeStruct((ROWS, 1280), F32),
            jax.ShapeDtypeStruct((8, ROWS, 640), BF),
            jax.ShapeDtypeStruct((4, 336, 1280), BF),
            jax.ShapeDtypeStruct((1, 640), F32),
            jax.ShapeDtypeStruct((4, 160, 1280), BF),
        ),
        in_specs=[ANY, ANY, VMEM, ANY, VMEM],
        out_specs=(VMEM,) * 5,
        scratch_shapes=[
            pltpu.VMEM((8, ROWS, 1280), BF),
            pltpu.VMEM((8, ROWS, 1280), BF),
            pltpu.VMEM((8, ROWS, 640), BF),
            pltpu.VMEM((2, ROWS, 640), F32),
            pltpu.VMEM((128, 1280), F32),
            dma(8),
            pltpu.SemaphoreType.DMA(()),
            pltpu.SemaphoreType.DMA(()),
            dma(9),
            dma(9),
            dma(4, 3),
            dma(4),
            *shapes,
        ],
        compiler_params=params(3, 60),
        name="feed_forward",
    )(normed, upstream, weights, down, bias)


def attend_back_kernel(
    split, qkv_in, mask_ref, logs_ref, pull_ref, hidden_in, weights_ref, feed_grads_in,
    out_grad_in, dqkv_ref, feed_ref, feed_sum_ref, out_sum_ref,
    qkv_ref, hidden_ref, feed_grads_ref, out_grad_ref, load,
    grad_ref, kt_ref, dk_ref, dv_ref, block_ref, middle_ref, local, send, recv, *scratch,
):
    place = Place()
    (
        line_bufs, line_sems, plane_bufs, plane_sems,
        out_plane_bufs, out_plane_sems, out_line_bufs, out_line_sems,
    ) = split(scratch)
    loads = [
        pltpu.make_async_copy(source, target, load.at[index])
        for index, (source, target) in enumerate(
            (
                (out_grad_in, out_grad_ref),
                (feed_grads_in, feed_grads_ref),
                (hidden_in, hidden_ref),
                (qkv_in, qkv_ref),
            )
        )
    ]
    for copy in loads:
        copy.start()
    greet(place, mp_all=True, plane=True)
    scale = 1.0 / math.sqrt(HD)
    factor = math.log2(math.e) * scale
    arriving = exchange(place, pull_ref, grad_ref, local, send, recv)
    next(arriving)

    def feed_block(group, core, start):
        return jnp.dot(
            hidden_ref[group * 2 + core, pl.ds(start, 192)],
            weights_ref[...].reshape(640, 1280),
            preferred_element_type=F32,
        )

    def feed_result(rows, total):
        feed_ref[rows] = total

    def sum_result(rows, total):
        feed_sum_ref[rows] = total

    plane = plane_reduce(
        place, feed_block, 192, 192, feed_result, plane_bufs, plane_sems, True
    )
    line = line_reduce(
        place,
        lambda level, core, rows: feed_grads_ref[level, rows].astype(F32),
        [pl.ds(start, 112) for start in range(0, 336, 112)],
        sum_result,
        line_bufs,
        line_sems,
        False,
    )
    def middle(rows, total):
        middle_ref[rows] = total

    def out_result(rows, total):
        out_sum_ref[rows] = total

    out_plane = plane_reduce(
        place,
        lambda group, core, start: out_grad_ref[group, core, pl.ds(start, 96)].astype(F32),
        96,
        96,
        middle,
        out_plane_bufs,
        out_plane_sems,
    )
    out_line = line_reduce(
        place,
        lambda level, core, rows: middle_ref[
            pl.ds(pl.multiple_of(level * 48 + rows.start, 16), rows.size)
        ],
        [pl.ds(0, 48)],
        out_result,
        out_line_bufs,
        out_line_sems,
        False,
    )
    loads[0].wait()
    next(out_plane)
    next(out_plane)
    loads[2].wait()
    next(plane)
    next(plane)
    loads[1].wait()
    next(line)
    next(line)
    next(out_line)
    loads[3].wait()
    for _ in arriving:
        pass
    block_ref[...] = jnp.zeros(block_ref.shape, BF)

    @pl.loop(0, 6)
    def _(turn):
        clip = turn // 2
        head = turn % 2
        lane = pl.multiple_of(head * 128, 128)
        row = pl.multiple_of(head * HD, 16)
        kt_ref[...] = qkv_ref[:, clip, :, pl.ds(256 + lane, 128)].reshape(1024, 128).T
        dk_ref[...] = jnp.zeros(dk_ref.shape, F32)
        dv_ref[...] = jnp.zeros(dv_ref.shape, F32)

        @pl.loop(0, 4)
        def _(block):
            query = qkv_ref[pl.ds(block * 2, 2), clip, :, pl.ds(lane, 128)].reshape(256, 128)
            values = qkv_ref[:, clip, :, pl.ds(512 + lane, 128)].reshape(1024, 128)
            keys = qkv_ref[:, clip, :, pl.ds(256 + lane, 128)].reshape(1024, 128)
            columns = pl.ds(pl.multiple_of(block * 256, 256), 256)
            for part in range(2):
                block_ref[:HD, part * 128 : part * 128 + 128] = grad_ref[
                    block * 2 + part, clip, pl.ds(row, HD)
                ]
            scores = lax.dot_general(
                keys, query, (((1,), (1,)), ((), ())), preferred_element_type=F32
            )
            chance = jnp.exp2((scores + mask_ref[clip]) * factor - logs_ref[turn, :, columns])
            dv_ref[...] += lax.dot_general(
                chance.astype(BF),
                block_ref[...],
                (((1,), (1,)), ((), ())),
                preferred_element_type=F32,
            )
            slope = lax.dot_general(
                values, block_ref[...], (((1,), (0,)), ((), ())), preferred_element_type=F32
            )
            center = jnp.sum(chance * slope, axis=0, keepdims=True)
            change = (chance * (slope - center)).astype(BF)
            dk_ref[...] += lax.dot_general(
                change, query, (((1,), (0,)), ((), ())), preferred_element_type=F32
            )
            dq = lax.dot_general(
                kt_ref[...], change, (((1,), (0,)), ((), ())), preferred_element_type=F32
            )
            dqkv_ref[pl.ds(block * 2, 2), clip, :, pl.ds(lane, 128)] = (
                (dq.T * scale).astype(BF).reshape(2, 128, 128)
            )

        dqkv_ref[:, clip, :, pl.ds(256 + lane, 128)] = (
            (dk_ref[...] * scale).astype(BF).reshape(8, 128, 128)
        )
        dqkv_ref[:, clip, :, pl.ds(512 + lane, 128)] = (
            dv_ref[...].astype(BF).reshape(8, 128, 128)
        )

        @pl.when(turn == 2)
        def _():
            next(out_plane)
            next(plane)

        @pl.when(turn == 5)
        def _():
            next(out_plane)

    drive(line, out_line, plane, out_plane)


def attend_back(qkv, mask, logs, pull, hidden, weights, feed_grads, out_grad):
    shapes, split = flatten(
        *line_reduce_scratch(336, 1280, False),
        *plane_reduce_scratch(192, 1280),
        *plane_reduce_scratch(96, 1280),
        *line_reduce_scratch(48, 1280, False),
    )
    return pl.pallas_call(
        functools.partial(attend_back_kernel, split),
        out_shape=(
            jax.ShapeDtypeStruct(qkv.shape, BF),
            jax.ShapeDtypeStruct((ROWS, 1280), F32),
            jax.ShapeDtypeStruct((336, 1280), F32),
            jax.ShapeDtypeStruct((48, 1280), F32),
        ),
        in_specs=[ANY, VMEM, VMEM, ANY, ANY, VMEM, ANY, ANY],
        out_specs=(VMEM,) * 4,
        scratch_shapes=[
            *(pltpu.VMEM(ref.shape, BF) for ref in (qkv, hidden, feed_grads, out_grad)),
            dma(4),
            pltpu.VMEM((8, 3, 160, 128), BF),
            pltpu.VMEM((128, 1024), BF),
            pltpu.VMEM((1024, 128), F32),
            pltpu.VMEM((1024, 128), F32),
            pltpu.VMEM((128, 256), BF),
            pltpu.VMEM((192, 1280), F32),
            pltpu.SemaphoreType.DMA(()),
            dma(8),
            dma(8),
            *shapes,
        ],
        compiler_params=params(2, 62),
        name="attend_back",
    )(qkv, mask, logs, pull, hidden, weights, feed_grads, out_grad)


GROUP_ROWS = 4832
GROUP_STEP = 4800
PACK_ROWS = GROUP_STEP * 3 + GROUP_ROWS
SEGMENTS = (
    ("query", 0, 1600),
    ("query_bias", 204800, 2),
    ("key", 204960, 1600),
    ("value", 409760, 1600),
    ("value_bias", 614560, 2),
    ("out", 614720, 1600),
    ("up", 819520, 6400),
    ("up_bias", 1638720, 5),
    ("down", 1639360, 6400),
)
PACK_END = 19216
SHARE_ROWS = 4808


def segment_table():
    table, cursor = {}, 0
    for name, start, rows in SEGMENTS:
        row = start // 128
        cursor += 32
        cursor += (row - cursor) % 8
        table[name] = (cursor, row, rows, start % 128)
        cursor += rows
    return table, (cursor + 32 + 7) // 8 * 8


TABLE, STAGE_ROWS = segment_table()


def lane_of(rows):
    return lax.broadcasted_iota(jnp.int32, (rows, 128), 1)


def pack_rows(stage, packed):
    def piece(name, first, rows):
        base, row, _, shift = TABLE[name]
        at = base - row + first
        here = stage[pl.ds(at, rows)]
        if shift == 0:
            return here
        above = stage[pl.ds(at - 1, rows)]
        return jnp.where(
            lane_of(rows) >= shift, pltpu.roll(here, shift, 1), pltpu.roll(above, shift, 1)
        )

    done = set()
    for name, _, _ in SEGMENTS:
        _, row, rows, shift = TABLE[name]
        low = -(-(row + (1 if shift else 0)) // 16) * 16
        high = (row + rows) // 16 * 16
        if high <= low:
            continue
        done.update(range(low, high, 16))
        turns = (high - low) // 128

        @pl.loop(0, turns)
        def _(turn):
            first = pl.multiple_of(low + turn * 128, 16)
            packed[pl.ds(first, 128)] = piece(name, first, 128).astype(BF)

        for first in range(low + turns * 128, high, 16):
            packed[pl.ds(first, 16)] = piece(name, first, 16).astype(BF)
    for first in range(0, PACK_ROWS, 16):
        if first in done:
            continue
        total = jnp.zeros((16, 128), F32)
        for name, _, _ in SEGMENTS:
            _, row, rows, shift = TABLE[name]
            if row < first + 16 and row + rows + (1 if shift else 0) > first:
                total = total + piece(name, first, 16)
        packed[pl.ds(first, 16)] = total.astype(BF)


def stage_wide(stage, name, ref, step):
    base = TABLE[name][0]
    rows, wide = ref.shape[0], ref.shape[1] // 128

    @pl.loop(0, rows // step)
    def _(turn):
        first = pl.multiple_of(turn * step, step)
        for block in range(wide):
            stage[pl.ds(base + first * wide + block, step, stride=wide), :] = ref[
                pl.ds(first, step), pl.ds(block * 128, 128)
            ].astype(F32)


def stage_heads(stage, name, ref, lanes, column):
    base = TABLE[name][0]
    for head in range(2):
        column[head] = ref[:, pl.ds(lanes + head * 128, 128)]

    @pl.loop(0, 5)
    def _(turn):
        lane = lane_of(64)
        rows = [jnp.zeros((64, 128), F32) for _ in range(5)]
        for block in range(8):
            item, head = block // 2, block % 2
            value = column[head, pl.ds(turn * 256 + item, 64, stride=4)]
            offset = block * HD
            first, shift = offset // 128, offset % 128
            if shift:
                value = pltpu.roll(value, shift, 1)
            if shift + HD > 128:
                rows[first] = rows[first] + jnp.where(lane >= shift, value, 0.0)
                rows[first + 1] = rows[first + 1] + jnp.where(
                    lane < shift + HD - 128, value, 0.0
                )
            else:
                rows[first] = rows[first] + value
        for index in range(5):
            stage[pl.ds(base + turn * 320 + index, 64, stride=5), :] = rows[index]


def stage_head_bias(stage, name, ref, lanes):
    base = TABLE[name][0]
    lane = lane_of(1)
    first = ref[0:1, pl.ds(lanes, 128)]
    second = pltpu.roll(ref[0:1, pl.ds(lanes + 128, 128)], HD, 1)
    stage[pl.ds(base, 1)] = first + jnp.where(lane >= HD, second, 0.0)
    stage[pl.ds(base + 1, 1)] = jnp.where(lane < 2 * HD - 128, second, 0.0)


def stage_share(stage, name, ref, first, count, place):
    base = TABLE[name][0] + place.dp * count * 10
    for block in range(10):
        stage[pl.ds(base + block, count, stride=10), :] = ref[
            pl.ds(first, count), pl.ds(block * 128, 128)
        ]


def stage_up(stage, ref, place):
    base = TABLE["up"][0]
    lane = lane_of(128)
    for quarter in range(4):

        @pl.when(place.dp == quarter)
        def _():
            for block in range(10):
                columns = pl.ds(block * 128, 128)
                first = ref[pl.ds(0, 128), columns].T
                second = jnp.where(lane < 32, ref[pl.ds(128, 128), columns].T, 0.0)
                shift = 32 * quarter
                if shift:
                    first = pltpu.roll(first, shift, 1)
                    second = pltpu.roll(second, shift, 1)
                    second = second + jnp.where(lane < shift, first, 0.0)
                    first = jnp.where(lane >= shift, first, 0.0)
                at = base + block * 640 + quarter
                stage[pl.ds(at, 128, stride=5), :] = first
                stage[pl.ds(at + 1, 128, stride=5), :] = second


def norm_back(place, frames_ref, middle_ref, gain_ref, grad_ref, offset):
    def write(rows, total):
        rows_in = pl.ds(offset + rows.start, rows.size)
        value = frames_ref[rows_in].astype(F32)
        center = value - jnp.mean(value, axis=-1, keepdims=True)
        spread = jnp.mean(center * center, axis=-1, keepdims=True)
        root = lax.rsqrt(spread + NORM_EPSILON)
        scaled = center * root
        pull = total * gain_ref[...]
        along = jnp.mean(pull * scaled, axis=-1, keepdims=True)
        grad_ref[rows] = middle_ref[rows_in] + root * (
            pull - jnp.mean(pull, axis=-1, keepdims=True) - scaled * along
        )

    return write


def line_product(place, grad_ref, weight_ref, offset, rows, result, bufs, sems):
    def produce(level, core, tile):
        return jnp.dot(
            grad_ref[level * 2 + core, pl.ds(offset + tile.start, tile.size)],
            weight_ref[...],
            preferred_element_type=F32,
        )

    tiles = [pl.ds(start, 128) for start in range(0, rows, 128)]
    return line_reduce(place, produce, tiles, result, bufs, sems, True)


FIRST_ROWS = 256


def finish_kernel(
    split, grad_ref, weight_ref, joined_ref, bias_ref, bias_column_ref, sum_ref, out_ref,
    up_bias_ref, small_ref, peak_ref, frames_ref, middle_ref, gain_ref, shift_ref,
    input_grad_ref, grads_ref, small_out, peak_out,
    stage, packed, sum_rows, column, tiles, small_in, small_all, peak_all, edge,
    local, small_send, small_recv, plane_send, plane_recv, *scratch,
):
    place = Place()
    line_bufs, line_sems, bufs, sems = split(scratch)
    greet(place, mp_all=True, plane=True)
    peers = (place.dpx, place.dpy, place.dpd)

    def tell(index, source, target, group, act):
        act(
            remote(
                source,
                target.at[place.dp],
                plane_send.at[index],
                plane_recv.at[index],
                group,
                place.mp,
            )
        )

    def heard(index, target, group):
        block = target.at[group]
        remote(
            block, block, plane_send.at[index], plane_recv.at[index], group, place.mp
        ).wait_recv()

    line = line_product(
        place,
        grad_ref,
        weight_ref,
        0,
        FIRST_ROWS,
        norm_back(place, frames_ref, middle_ref, gain_ref, input_grad_ref, 0),
        line_bufs,
        line_sems,
    )
    for index, group in enumerate(peers):
        tell(index, peak_ref, peak_all, group, lambda copy: copy.start())
    next(line)
    next(line)

    for block in range(10):
        lanes = pl.ds(block * 128, 128)
        weight = weight_ref[:, lanes].astype(F32)
        turned = joined_ref[lanes].T
        whole = jnp.sum(weight * bias_column_ref[...], axis=0, keepdims=True)
        along = jnp.sum(weight * turned, axis=0, keepdims=True)
        tiles[pl.ds(block, 1)] = (along - shift_ref[:, lanes] * whole) / gain_ref[:, lanes]
        tiles[pl.ds(10 + block, 1)] = whole
    tiles[pl.ds(20, 44)] = small_ref[...]
    for run in range(8):
        edge[run] = tiles[pl.ds(run * 15 // 2, 8)]
    mixing = exchange(place, edge, small_in, local, small_send, small_recv)
    next(mixing)

    stage[...] = jnp.zeros(stage.shape, F32)
    for name, lanes in (("query", 0), ("key", 256), ("value", 512)):
        stage_heads(stage, name, joined_ref, lanes, column)
    stage_head_bias(stage, "query_bias", bias_ref, 0)
    stage_head_bias(stage, "value_bias", bias_ref, 512)
    stage_share(stage, "out", out_ref, 0, 40, place)
    stage_share(stage, "down", sum_ref, 160, 160, place)
    stage_up(stage, sum_ref, place)
    stage[pl.ds(TABLE["up_bias"][0], 5)] = up_bias_ref[...]
    pack_rows(stage, packed)

    def produce(group, core, start):
        first = pl.multiple_of(group * GROUP_STEP + start, 16)
        return packed[pl.ds(first, GROUP_ROWS // 2)].astype(F32)

    def result(rows, total):
        sum_rows[rows] = total

    half = GROUP_ROWS // 2
    plane = plane_reduce(place, produce, half, half, result, bufs, sems, False)
    next(plane)
    next(plane)
    for _ in mixing:
        pass
    small_all[place.dp] = jnp.sum(small_in[...], axis=0)
    for index, group in enumerate(peers):
        tell(3 + index, small_all.at[place.dp], small_all, group, lambda copy: copy.start())
    next(line)
    next(plane)
    next(line)
    next(plane)
    drive(line, plane)
    for index, group in enumerate(peers):
        heard(index, peak_all, group)
        heard(3 + index, small_all, group)
    top = peak_ref[...]
    for group in peers:
        top = jnp.maximum(top, peak_all[group])
    peak_out[...] = top
    whole = jnp.sum(small_all[...], axis=0)
    lane = lane_of(8)
    row = lax.broadcasted_iota(jnp.int32, (8, 128), 0)
    tiles[...] = jnp.zeros((64, 128), F32)
    tiles[pl.ds(8, 8)] = whole
    ahead = pltpu.roll(tiles[pl.ds(9, 8)], 64, 1)
    here = pltpu.roll(whole, 64, 1)
    odd = jnp.where(lane < 64, here, ahead)
    run_of = jnp.where(place.c == 1, odd, whole)
    run_of = jnp.where(jnp.logical_and(row == 7, lane >= 64), 0.0, run_of)
    small_out[...] = run_of
    tiles[pl.ds(8, 8)] = run_of
    wide = lane_of(16)
    entry = jnp.where(
        wide >= 64, pltpu.roll(tiles[pl.ds(1, 16)], 64, 1), pltpu.roll(tiles[pl.ds(0, 16)], 64, 1)
    )

    @pl.when(place.dp == 3)
    def _():
        sum_rows[pl.ds(GROUP_STEP, 16)] += entry

    for group in range(4):

        @pl.when(place.dp == group)
        def _():
            down, shift = 480 * group // 128, 480 * group % 128
            if shift == 0:
                grads_ref[...] = sum_rows[pl.ds(0, SHARE_ROWS)]
            else:
                for first in range(0, SHARE_ROWS, 1208):
                    size = min(1208, SHARE_ROWS - first)
                    grads_ref[pl.ds(first, size)] = jnp.where(
                        lane_of(size) < 128 - shift,
                        pltpu.roll(sum_rows[pl.ds(first + down, size)], 128 - shift, 1),
                        pltpu.roll(sum_rows[pl.ds(first + down + 1, size)], 128 - shift, 1),
                    )

    for index, group in enumerate(peers):
        tell(index, peak_ref, peak_all, group, lambda copy: copy.wait_send())
        tell(3 + index, small_all.at[place.dp], small_all, group, lambda copy: copy.wait_send())


def finish(grads, weight, joined, bias, sums, out, up_bias, small, peaks, frames, middle, gain, shift):
    shapes, split = flatten(
        *line_reduce_scratch(FIRST_ROWS, 1280, True),
        *plane_reduce_scratch(GROUP_ROWS // 2, 128, False),
    )
    return pl.pallas_call(
        functools.partial(finish_kernel, split),
        out_shape=(
            jax.ShapeDtypeStruct((FIRST_ROWS, 1280), F32),
            jax.ShapeDtypeStruct((SHARE_ROWS, 128), F32),
            jax.ShapeDtypeStruct((8, 128), F32),
            jax.ShapeDtypeStruct(peaks.shape, F32),
        ),
        in_specs=[VMEM] * 14,
        out_specs=(VMEM,) * 4,
        scratch_shapes=[
            pltpu.VMEM((STAGE_ROWS, 128), F32),
            pltpu.VMEM((PACK_ROWS, 128), BF),
            pltpu.VMEM((GROUP_ROWS, 128), F32),
            pltpu.VMEM((2, 1280, 128), F32),
            pltpu.VMEM((64, 128), F32),
            pltpu.VMEM((8, 8, 128), F32),
            pltpu.VMEM((4, 8, 128), F32),
            pltpu.VMEM((4,) + peaks.shape, F32),
            pltpu.VMEM((8, 8, 128), F32),
            pltpu.SemaphoreType.DMA(()),
            dma(8),
            dma(8),
            dma(6),
            dma(6),
            *shapes,
        ],
        compiler_params=params(7, 62),
        name="finish",
    )(
        grads, weight, joined, bias[None], bias[:, None], sums, out, up_bias, small, peaks,
        frames, middle, gain, shift,
    )


def share_master_kernel(
    split, rows_ref, grad_ref, weight_ref, frames_ref, middle_ref, gain_ref,
    whole_ref, input_grad_ref, parts, turned, send, recv, *scratch,
):
    place = Place()
    line_bufs, line_sems = split(scratch)
    greet(place, line=True, plane=True)
    line = line_product(
        place,
        grad_ref,
        weight_ref,
        FIRST_ROWS,
        ROWS - FIRST_ROWS,
        norm_back(place, frames_ref, middle_ref, gain_ref, input_grad_ref, FIRST_ROWS),
        line_bufs,
        line_sems,
    )
    dp, mp, dpx, dpy, dpd = place.dp, place.mp, place.dpx, place.dpy, place.dpd
    half = GROUP_ROWS // 2
    part_a, part_b = pl.ds(0, half), pl.ds(half, half)
    for group in range(4):

        @pl.when(dp == group)
        def _():
            down, shift = 480 * group // 128, 480 * group % 128
            turned[pl.ds(0, 16)] = jnp.zeros((16, 128), F32)
            turned[pl.ds(16, SHARE_ROWS)] = rows_ref[...]
            turned[pl.ds(16 + SHARE_ROWS, 24)] = jnp.zeros((24, 128), F32)
            for first in range(0, GROUP_ROWS, 1208):
                here = turned[pl.ds(16 + first - down, 1208)]
                if shift:
                    here = jnp.where(
                        lane_of(1208) >= shift,
                        pltpu.roll(here, shift, 1),
                        pltpu.roll(turned[pl.ds(15 + first - down, 1208)], shift, 1),
                    )
                parts[dp, pl.ds(first, 1208)] = here.astype(BF)


    def hop(index, block, target):
        return remote(block, block, send.at[index], recv.at[index], target, mp)

    own = parts.at[dp]
    sends = [hop(0, own, dpx), hop(1, own, dpy)]
    for copy in sends:
        copy.start()
    next(line)
    next(line)
    hop(0, parts.at[dpx], dpx).wait_recv()
    sends.append(hop(2, parts.at[dpx, part_a], dpy))
    sends[-1].start()
    hop(1, parts.at[dpy], dpy).wait_recv()
    sends.append(hop(3, parts.at[dpy, part_b], dpx))
    sends[-1].start()
    next(line)
    next(line)
    hop(2, parts.at[dpd, part_a], dpy).wait_recv()
    hop(3, parts.at[dpd, part_b], dpx).wait_recv()
    for group in range(4):
        base = group * GROUP_STEP
        first = parts[group, pl.ds(0, 32)].astype(F32)
        if group > 0:
            first = first + parts[group - 1, pl.ds(GROUP_STEP, 32)].astype(F32)
        whole_ref[pl.ds(base, 32)] = first
        for start in range(32, GROUP_STEP, 1192):
            whole_ref[pl.ds(base + start, 1192)] = parts[group, pl.ds(start, 1192)].astype(F32)
    whole_ref[pl.ds(4 * GROUP_STEP, 16)] = parts[3, pl.ds(GROUP_STEP, 16)].astype(F32)
    for copy in sends:
        copy.wait_send()
    drive(line)


def share_master(rows, grads, weight, frames, middle, gain):
    shapes, split = flatten(*line_reduce_scratch(ROWS - FIRST_ROWS, 1280, True))
    return pl.pallas_call(
        functools.partial(share_master_kernel, split),
        out_shape=(
            jax.ShapeDtypeStruct((PACK_END, 128), F32),
            jax.ShapeDtypeStruct((ROWS - FIRST_ROWS, 1280), F32),
        ),
        in_specs=[VMEM] * 6,
        out_specs=(VMEM, VMEM),
        scratch_shapes=[
            pltpu.VMEM((4, GROUP_ROWS, 128), BF),
            pltpu.VMEM((SHARE_ROWS + 40, 128), F32),
            dma(4),
            dma(4),
            *shapes,
        ],
        compiler_params=params(8, 60),
        name="share_master",
    )(rows, grads, weight, frames, middle, gain)


STEP_ENTRIES = 1024 * 76


def optimize_kernel(
    rates_ref, grads_ref, master_ref, first_ref, second_ref,
    owned_out, master_out, first_out, second_out, padded_out,
):
    entry = lax.broadcasted_iota(jnp.int32, (1, STEP_ENTRIES), 1)
    entry = entry + pl.program_id(0) * STEP_ENTRIES
    grads = grads_ref[...]
    first = BETA_FIRST * first_ref[...] + (1.0 - BETA_FIRST) * grads
    second = BETA_SECOND * second_ref[...] + (1.0 - BETA_SECOND) * grads * grads
    change = first * rates_ref[0] / (jnp.sqrt(second * rates_ref[1]) + ADAM_EPSILON)
    block = jnp.floor((entry.astype(F32) + 0.5) * (1.0 / HD))
    odd = block - 2.0 * jnp.floor(block * 0.5) > 0.5
    factor = jnp.where(
        entry < KEY_END, jnp.where(odd, rates_ref[4], rates_ref[3]), 1.0
    )
    master = (master_ref[...] * rates_ref[2] - change) * factor
    owned_out[...] = grads
    master_out[...] = master
    first_out[...] = first
    second_out[...] = second
    padded_out[...] = jnp.where(entry < SHARE_ENTRIES, master, 0.0)


KEY_END = 409760
SHARE_ENTRIES = 614880


def optimize(rates, grads, master, first, second):
    block = pl.BlockSpec((1, STEP_ENTRIES), lambda step: (0, step))
    share = jax.ShapeDtypeStruct((1, SHARE_ENTRIES), F32)
    return pl.pallas_call(
        optimize_kernel,
        grid=(pl.cdiv(SHARE_ENTRIES, STEP_ENTRIES),),
        out_shape=(share,) * 4 + (jax.ShapeDtypeStruct((1, SHARE_ROWS * 128), F32),),
        in_specs=[pl.BlockSpec(memory_space=pltpu.SMEM)] + [block] * 4,
        out_specs=(block,) * 5,
        compiler_params=pltpu.CompilerParams(vmem_limit_bytes=32 << 20),
        name="optimize",
    )(rates, grads, master, first, second)


def fast_body(
    frames,
    lengths,
    key_mask,
    cotangent,
    gain_one,
    shift_one,
    query_weight,
    query_bias,
    key_weight,
    value_weight,
    value_bias,
    out_weight,
    out_bias,
    gain_two,
    shift_two,
    up_weight,
    up_bias,
    down_weight,
    down_bias,
    master,
    moment_one,
    moment_two,
    adam_step,
    hyper_rates,
):
    group = lax.axis_index("dp")
    position = jnp.arange(1024, dtype=jnp.int32)
    keep_query = position[None, :] < lengths[:, None]
    keep_key = jnp.logical_and(keep_query, key_mask == 1)
    mask = jnp.where(keep_key, 0.0, MASK_VALUE)[:, :, None]
    live = keep_query.astype(F32)[:, None, :]
    gain_first = gain_one.astype(F32)
    shift_first = shift_one.astype(F32)
    gain_second = gain_two.astype(F32)
    shift_second = shift_two.astype(F32)
    inputs = frames.transpose(1, 0, 2).reshape(ROWS, 1280).astype(F32)
    upstream_low = cotangent.transpose(1, 0, 2).reshape(ROWS, 1280)
    upstream = upstream_low.astype(F32)
    def head_lanes(bias):
        lanes = bias.astype(F32).reshape(2, HD)
        return jnp.pad(lanes, ((0, 0), (0, 128 - HD))).reshape(256)

    joined_bias = jnp.concatenate(
        [head_lanes(query_bias), jnp.zeros((256,), F32), head_lanes(value_bias)]
    )[None]
    frame_rows = frames.transpose(1, 0, 2).reshape(ROWS, 1280)
    normed_full, qkv, upstream_full, joined_weight = project(
        frame_rows,
        gain_first[None],
        shift_first[None],
        upstream_low,
        query_weight.T,
        key_weight.T,
        value_weight.T,
        joined_bias,
    )
    qkv = qkv.reshape(8, 3, 128, 768)

    quarter = group * 160
    up_share = lax.dynamic_slice_in_dim(up_weight, quarter, 160, 1).T
    down_share = lax.dynamic_slice_in_dim(down_weight, quarter, 160, 0)
    bias_share = lax.dynamic_slice_in_dim(up_bias, quarter, 160, 0)
    bias_rows = jnp.pad(bias_share[None], ((0, 15), (0, 1280 - 160)))
    message = jnp.concatenate([up_share, bias_rows])
    outer = jnp.pad(lax.dynamic_slice_in_dim(out_weight, group * 40, 40, 0), ((0, 8), (0, 0)))
    attended, logs, peaks, gathered, outer_all = attend(qkv, mask, live, message, outer)
    up_lanes = gathered[:, 160, :160].reshape(1, 640).astype(F32)
    out_rows = outer_all.reshape(4, 2, 4, 48, 1280)[:, :, :, :40]
    out_rows = out_rows.transpose(2, 1, 0, 3, 4).reshape(8, 160, 1280)

    branch = jnp.einsum("schr,shd->crd", attended, out_rows, preferred_element_type=F32)
    middle = inputs + branch.reshape(ROWS, 1280) + out_bias.astype(F32)
    normed_two = layer_norm(middle, gain_second, shift_second).astype(BF)
    normed_two_grad, hidden, feed_grads, _, down_all = feed_forward(
        normed_two, upstream_full, gathered, down_share, up_lanes
    )

    _, norm_two_pull = jax.vjp(layer_norm, middle, gain_second, shift_second)
    middle_norm_grad, gain_two_grad, shift_two_grad = norm_two_pull(normed_two_grad)
    middle_grad = upstream + middle_norm_grad
    branch_grad = middle_grad.astype(BF)
    branch_clips = branch_grad.reshape(3, 128, 1280)
    out_grad = jnp.einsum("schr,crd->shd", attended, branch_clips, preferred_element_type=F32)
    attended_grad = jnp.einsum(
        "shd,crd->schr", out_rows, branch_clips, preferred_element_type=F32
    ).astype(BF)
    out_quarters = jnp.pad(
        out_grad.astype(BF).reshape(4, 2, 4, 40, 1280), ((0, 0),) * 3 + ((0, 8), (0, 0))
    )
    out_quarters = out_quarters.transpose(2, 1, 0, 3, 4).reshape(4, 2, 192, 1280)
    joined_grad, feed, feed_sum, out_sum = attend_back(
        qkv, mask, logs, attended_grad, hidden, down_all, feed_grads, out_quarters
    )
    layer_out = (middle + feed + down_bias.astype(F32)).astype(BF)
    joined_grad = joined_grad.reshape(8, ROWS, 768)
    joined_weight_grad = jnp.einsum(
        "prd,pre->de", normed_full, joined_grad, preferred_element_type=F32
    )
    joined_bias_grad = jnp.sum(joined_grad.astype(F32), axis=(0, 1))

    level = lax.axis_index("mp") // 2
    up_bias_share = lax.dynamic_slice_in_dim(feed_sum[320], level * 160, 160, 0)
    up_bias_rows = lax.dynamic_update_slice(
        jnp.zeros((640,), F32), up_bias_share, (quarter,)
    ).reshape(5, 128)
    small_rows = jnp.concatenate(
        [
            jnp.sum(branch_grad.astype(F32), axis=0),
            gain_two_grad,
            shift_two_grad,
            jnp.sum(upstream, axis=0),
            jnp.zeros((512,), F32),
        ]
    ).reshape(44, 128)
    first_grad, grad_rows, small_sum, peak_sum = finish(
        joined_grad,
        joined_weight,
        joined_weight_grad,
        joined_bias_grad,
        feed_sum,
        out_sum,
        up_bias_rows,
        small_rows,
        peaks,
        frame_rows,
        middle_grad,
        gain_first[None],
        shift_first[None],
    )
    small_total = small_sum.reshape(1024)[:960]
    head_peak = jnp.max(peak_sum, axis=(1, 2)) / math.sqrt(HD)
    learn_rate = hyper_rates[0]
    weight_decay = hyper_rates[1]
    logit_cap = hyper_rates[2]
    step_count = adam_step[0].astype(F32)
    root_factor = jnp.sqrt(logit_cap / jnp.maximum(head_peak, logit_cap))
    root_factor = jnp.where(group == 0, root_factor, 1.0)
    rates = jnp.stack(
        [
            learn_rate / (1.0 - jnp.power(BETA_FIRST, step_count)),
            1.0 / (1.0 - jnp.power(BETA_SECOND, step_count)),
            1.0 - learn_rate * weight_decay,
            root_factor[0],
            root_factor[1],
        ]
    )
    owned_grads, master_new, first_new, second_new, padded = optimize(
        rates, grad_rows.reshape(1, SHARE_ROWS * 128), master, moment_one, moment_two
    )
    whole, second_grad = share_master(
        padded.reshape(SHARE_ROWS, 128),
        joined_grad,
        joined_weight,
        frame_rows,
        middle_grad,
        gain_first[None],
    )
    input_grad = jnp.concatenate([first_grad, second_grad])
    whole = lax.optimization_barrier(whole.reshape(1, PACK_END * 128))
    weights_new = whole[:, : 4 * SHARE_ENTRIES].astype(BF)
    return (
        layer_out.reshape(3, 128, 1280).transpose(1, 0, 2),
        input_grad.reshape(3, 128, 1280).transpose(1, 0, 2),
        owned_grads,
        master_new,
        first_new,
        second_new,
        weights_new,
        small_total,
    )


def body(
    frames,
    lengths,
    key_mask,
    cotangent,
    gain_one,
    shift_one,
    query_weight,
    query_bias,
    key_weight,
    value_weight,
    value_bias,
    out_weight,
    out_bias,
    gain_two,
    shift_two,
    up_weight,
    up_bias,
    down_weight,
    down_bias,
    master,
    moment_one,
    moment_two,
    adam_step,
    hyper_rates,
):
    local_rows, clip_count, model_width = frames.shape
    total_rows = key_mask.shape[1]
    head_cols = query_weight.shape[1]
    heads_here = head_cols // HD
    block_rows = min(512, total_rows)
    blocks = total_rows // block_rows
    score_scale = 1.0 / math.sqrt(HD)
    position = jnp.arange(total_rows, dtype=jnp.int32)
    keep_query = position[None, :] < lengths[:, None]
    keep_key = jnp.logical_and(keep_query, key_mask == 1)
    gain_first = gain_one.astype(jnp.float32)
    shift_first = shift_one.astype(jnp.float32)
    gain_second = gain_two.astype(jnp.float32)
    shift_second = shift_two.astype(jnp.float32)
    inputs = frames.astype(jnp.float32)
    normed = layer_norm(inputs, gain_first, shift_first).astype(jnp.bfloat16)
    joined_weight = jnp.concatenate([query_weight, key_weight, value_weight], axis=1)
    joined_bias = jnp.concatenate(
        [
            query_bias.astype(jnp.float32),
            jnp.zeros((head_cols,), jnp.float32),
            value_bias.astype(jnp.float32),
        ]
    )
    normed_full = lax.all_gather(normed, "mp", axis=0, tiled=True)
    projected = (
        jnp.einsum("rcd,de->rce", normed_full, joined_weight, preferred_element_type=jnp.float32)
        + joined_bias
    ).astype(jnp.bfloat16)
    query = projected[:, :, :head_cols].reshape(total_rows, clip_count, heads_here, HD)
    keys = projected[:, :, head_cols : 2 * head_cols].reshape(
        total_rows, clip_count, heads_here, HD
    )
    values = projected[:, :, 2 * head_cols :].reshape(total_rows, clip_count, heads_here, HD)

    def scores_of(row_start):
        query_block = lax.dynamic_slice_in_dim(query, row_start, block_rows, 0)
        raw_scores = (
            jnp.einsum("qchd,kchd->chqk", query_block, keys, preferred_element_type=jnp.float32)
            * score_scale
        )
        return (query_block, jnp.where(keep_key[:, None, None, :], raw_scores, MASK_VALUE))

    def forward_block(block_index):
        row_start = block_index * block_rows
        _, masked = scores_of(row_start)
        row_peak = jnp.max(masked, axis=-1, keepdims=True)
        exp_scores = jnp.exp(masked - row_peak)
        row_total = jnp.sum(exp_scores, axis=-1, keepdims=True)
        probability = (exp_scores / row_total).astype(jnp.bfloat16)
        attended = jnp.einsum(
            "chqk,kchd->qchd", probability, values, preferred_element_type=jnp.float32
        ).astype(jnp.bfloat16)
        live_rows = lax.dynamic_slice_in_dim(keep_query, row_start, block_rows, 1)
        block_peak = jnp.max(
            jnp.where(live_rows[:, None, :], row_peak[..., 0], MASK_VALUE), axis=(0, 2)
        )
        return (attended, (row_peak + jnp.log(row_total))[..., 0], block_peak)

    attended_blocks, log_totals, block_peaks = lax.map(forward_block, jnp.arange(blocks))
    attended_full = attended_blocks.reshape(total_rows, clip_count, head_cols)
    head_peak = lax.pmax(jnp.max(block_peaks, axis=0), "dp")
    rows_here = attended_full
    attn_branch = lax.psum_scatter(
        jnp.einsum("rck,kd->rcd", rows_here, out_weight, preferred_element_type=jnp.float32),
        "mp",
        scatter_dimension=0,
        tiled=True,
    ) + out_bias.astype(jnp.float32)
    middle = inputs + attn_branch
    normed_two = layer_norm(middle, gain_second, shift_second).astype(jnp.bfloat16)
    upstream = cotangent.astype(jnp.float32)
    normed_two_full = lax.all_gather(normed_two, "mp", axis=0, tiled=True)
    before = jnp.einsum(
        "rcd,df->rcf", normed_two_full, up_weight, preferred_element_type=jnp.float32
    ) + up_bias.astype(jnp.float32)
    hidden = exact_gelu(before).astype(jnp.bfloat16)
    rows_here = hidden
    feed = lax.psum_scatter(
        jnp.einsum(
            "rcf,fd->rcd", rows_here, down_weight, preferred_element_type=jnp.float32
        ).astype(jnp.bfloat16),
        "mp",
        scatter_dimension=0,
        tiled=True,
    ).astype(jnp.float32) + down_bias.astype(jnp.float32)
    layer_out = (middle + feed).astype(jnp.bfloat16)
    feed_grad_full = lax.all_gather(cotangent, "mp", axis=0, tiled=True)
    down_grad = jnp.einsum(
        "rcf,rcd->fd", hidden, feed_grad_full, preferred_element_type=jnp.float32
    )
    hidden_grad = jnp.einsum(
        "rcd,fd->rcf", feed_grad_full, down_weight, preferred_element_type=jnp.float32
    )
    _, gelu_pull = jax.vjp(exact_gelu, before)
    before_grad = gelu_pull(hidden_grad)[0].astype(jnp.bfloat16)
    up_bias_grad = jnp.sum(before_grad.astype(jnp.float32), axis=(0, 1))
    up_grad = jnp.einsum(
        "rcd,rcf->df", normed_two_full, before_grad, preferred_element_type=jnp.float32
    )
    rows_here = before_grad
    normed_two_grad = lax.psum_scatter(
        jnp.einsum("rcf,df->rcd", rows_here, up_weight, preferred_element_type=jnp.float32),
        "mp",
        scatter_dimension=0,
        tiled=True,
    )
    _, norm_two_pull = jax.vjp(layer_norm, middle, gain_second, shift_second)
    middle_norm_grad, gain_two_grad, shift_two_grad = norm_two_pull(normed_two_grad)
    middle_grad = upstream + middle_norm_grad
    branch_grad = middle_grad.astype(jnp.bfloat16)
    branch_grad_full = lax.all_gather(branch_grad, "mp", axis=0, tiled=True)
    out_grad = jnp.einsum(
        "rck,rcd->kd", attended_full, branch_grad_full, preferred_element_type=jnp.float32
    )
    attended_grad = jnp.einsum(
        "rcd,kd->rck", branch_grad_full, out_weight, preferred_element_type=jnp.float32
    ).astype(jnp.bfloat16)
    attended_grad = attended_grad.reshape(total_rows, clip_count, heads_here, HD)

    def backward_block(carry, block_index):
        key_total, value_total = carry
        row_start = block_index * block_rows
        query_block, masked = scores_of(row_start)
        log_total = log_totals[block_index]
        probability = jnp.exp(masked - log_total[..., None])
        grad_block = lax.dynamic_slice_in_dim(attended_grad, row_start, block_rows, 0)
        value_total = value_total + jnp.einsum(
            "chqk,qchd->kchd",
            probability.astype(jnp.bfloat16),
            grad_block,
            preferred_element_type=jnp.float32,
        )
        prob_grad = jnp.einsum(
            "qchd,kchd->chqk", grad_block, values, preferred_element_type=jnp.float32
        )
        score_grad = (
            probability * (prob_grad - jnp.sum(probability * prob_grad, axis=-1, keepdims=True))
        ).astype(jnp.bfloat16)
        query_grad = (
            jnp.einsum("chqk,kchd->qchd", score_grad, keys, preferred_element_type=jnp.float32)
            * score_scale
        ).astype(jnp.bfloat16)
        key_total = (
            key_total
            + jnp.einsum(
                "chqk,qchd->kchd", score_grad, query_block, preferred_element_type=jnp.float32
            )
            * score_scale
        )
        return ((key_total, value_total), query_grad)

    empty_grad = jnp.zeros((total_rows, clip_count, heads_here, HD), jnp.float32)
    (key_total, value_total), query_blocks = lax.scan(
        backward_block, (empty_grad, empty_grad), jnp.arange(blocks)
    )
    joined_grad = jnp.concatenate(
        [
            query_blocks.reshape(total_rows, clip_count, head_cols),
            key_total.reshape(total_rows, clip_count, head_cols).astype(jnp.bfloat16),
            value_total.reshape(total_rows, clip_count, head_cols).astype(jnp.bfloat16),
        ],
        axis=-1,
    )
    joined_bias_grad = jnp.sum(joined_grad.astype(jnp.float32), axis=(0, 1))
    normed_back = lax.all_gather(normed, "mp", axis=0, tiled=True)
    joined_weight_grad = jnp.einsum(
        "rcd,rce->de", normed_back, joined_grad, preferred_element_type=jnp.float32
    )
    rows_here = joined_grad
    normed_grad = lax.psum_scatter(
        jnp.einsum(
            "rce,de->rcd", rows_here, joined_weight, preferred_element_type=jnp.float32
        ).astype(jnp.bfloat16),
        "mp",
        scatter_dimension=0,
        tiled=True,
    ).astype(jnp.float32)
    _, norm_one_pull = jax.vjp(layer_norm, inputs, gain_first, shift_first)
    input_norm_grad, gain_one_grad, shift_one_grad = norm_one_pull(normed_grad)
    input_grad = middle_grad + input_norm_grad
    out_bias_grad = jnp.sum(branch_grad.astype(jnp.float32), axis=(0, 1))
    down_bias_grad = jnp.sum(upstream, axis=(0, 1))
    small_terms = jnp.concatenate(
        [
            gain_one_grad,
            shift_one_grad,
            out_bias_grad,
            gain_two_grad,
            shift_two_grad,
            down_bias_grad,
        ]
    )
    small_share = lax.psum_scatter(small_terms, "mp", scatter_dimension=0, tiled=True)
    small_total = lax.psum(small_share, "dp")
    packed = jnp.concatenate(
        [
            joined_weight_grad[:, :head_cols].reshape(-1),
            joined_bias_grad[:head_cols],
            joined_weight_grad[:, head_cols : 2 * head_cols].reshape(-1),
            joined_weight_grad[:, 2 * head_cols :].reshape(-1),
            joined_bias_grad[2 * head_cols :],
            out_grad.reshape(-1),
            up_grad.reshape(-1),
            up_bias_grad,
            down_grad.reshape(-1),
            small_share,
        ]
    )
    owned_grads = lax.psum_scatter(
        packed.astype(jnp.bfloat16), "dp", scatter_dimension=0, tiled=True
    ).astype(jnp.float32)
    share_size = owned_grads.shape[0]
    learn_rate = hyper_rates[0]
    weight_decay = hyper_rates[1]
    logit_cap = hyper_rates[2]
    step_count = adam_step[0].astype(jnp.float32)
    first_new = BETA_FIRST * moment_one[0] + (1.0 - BETA_FIRST) * owned_grads
    second_new = BETA_SECOND * moment_two[0] + (1.0 - BETA_SECOND) * owned_grads * owned_grads
    first_hat = first_new / (1.0 - jnp.power(BETA_FIRST, step_count))
    second_hat = second_new / (1.0 - jnp.power(BETA_SECOND, step_count))
    entry_index = lax.axis_index("dp") * share_size + jnp.arange(share_size, dtype=jnp.int32)
    query_end = model_width * head_cols
    query_bias_end = query_end + head_cols
    key_end = query_bias_end + model_width * head_cols
    column = jnp.where(
        entry_index < query_end,
        entry_index % head_cols,
        jnp.where(
            entry_index < query_bias_end,
            entry_index - query_end,
            (entry_index - query_bias_end) % head_cols,
        ),
    )
    head_index = column // HD
    root_factor = jnp.sqrt(logit_cap / jnp.maximum(head_peak, logit_cap))
    head_factor = jnp.zeros((share_size,), jnp.float32)
    for head_number in range(heads_here):
        head_factor = head_factor + jnp.where(
            head_index == head_number, root_factor[head_number], 0.0
        )
    factor = jnp.where(entry_index < key_end, head_factor, 1.0)
    master_here = master[0]
    master_new = (
        master_here
        - learn_rate
        * (first_hat / (jnp.sqrt(second_hat) + ADAM_EPSILON) + weight_decay * master_here)
    ) * factor
    weights_full = lax.all_gather(master_new.astype(jnp.bfloat16), "dp", axis=0, tiled=True)
    return (
        layer_out,
        input_grad,
        owned_grads[None],
        master_new[None],
        first_new[None],
        second_new[None],
        weights_full[None],
        small_total,
    )


def solution(mesh):
    chosen = fast_body if dict(mesh.shape) == {"dp": 4, "mp": 8} else body
    placed = (
        P("mp", "dp", None),
        P("dp"),
        P("dp", None),
        P("mp", "dp", None),
        P(),
        P(),
        P(None, "mp"),
        P("mp"),
        P(None, "mp"),
        P(None, "mp"),
        P("mp"),
        P("mp", None),
        P(),
        P(),
        P(),
        P(None, "mp"),
        P("mp"),
        P("mp", None),
        P(),
        P("mp", "dp"),
        P("mp", "dp"),
        P("mp", "dp"),
        P(),
        P(),
    )
    return jax.shard_map(
        chosen,
        mesh=mesh,
        in_specs=placed,
        out_specs=(
            P("mp", "dp", None),
            P("mp", "dp", None),
            P("mp", "dp"),
            P("mp", "dp"),
            P("mp", "dp"),
            P("mp", "dp"),
            P("mp", None),
            P("mp"),
        ),
        check_vma=False,
    )
```

```python
import functools
import math

import jax
import jax.numpy as jnp
from jax import lax
from jax.experimental import pallas as pl
from jax.experimental.pallas import tpu as pltpu
from jax.sharding import PartitionSpec as P

HD = 80


NORM_EPSILON = 1e-05
ADAM_EPSILON = 1e-08
BETA_FIRST = 0.9
BETA_SECOND = 0.999
MASK_VALUE = -1e30


def layer_norm(value, gain, shift):
    center = value - jnp.mean(value, axis=-1, keepdims=True)
    spread = jnp.mean(center * center, axis=-1, keepdims=True)
    return center * lax.rsqrt(spread + NORM_EPSILON) * gain + shift


def exact_gelu(argument):
    return jax.nn.gelu(argument, approximate=False)


MESH = pl.DeviceIdType.MESH
ANY = pl.BlockSpec(memory_space=pl.ANY)
VMEM = pl.BlockSpec(memory_space=pltpu.VMEM)
LINE = 4
ROWS = 384
BF = jnp.bfloat16
F32 = jnp.float32


class Place:
    def __init__(self):
        self.dp = lax.axis_index("dp")
        self.mp = lax.axis_index("mp")
        self.z = self.mp // 2
        self.c = self.mp % 2
        self.pair = self.z * 2 + 1 - self.c
        self.dpx = self.dp + 1 - 2 * (self.dp % 2)
        self.dpy = (self.dp + 2) % 4
        self.dpd = 3 - self.dp

    def zorder(self, event):
        if event == 0:
            return self.z
        if event == 1:
            return self.z + 1 - 2 * (self.z % 2)
        if event == 2:
            return 2 - self.z // 2
        return 3 - 3 * (self.z // 2)


def greet(place, mp_all=False, line=False, plane=False, pair=True):
    barrier = pltpu.get_barrier_semaphore()
    count = 0

    def signal(dp, mp):
        pl.semaphore_signal(barrier, inc=1, device_id=(dp, mp), device_id_type=MESH)

    if mp_all:
        for hop in range(1, 8):
            signal(place.dp, (place.mp + hop) % 8)
        count += 7
    else:
        if pair:
            signal(place.dp, place.pair)
            count += 1
        if line:

            @pl.when(place.z > 0)
            def _():
                signal(place.dp, place.mp - 2)

            @pl.when(place.z < LINE - 1)
            def _():
                signal(place.dp, place.mp + 2)

    if plane:
        for other in (place.dpx, place.dpy, place.dpd):
            signal(other, place.mp)
        count += 3
    if line and not mp_all:
        pl.semaphore_wait(barrier, count + 1 + (place.z + 1) // 2 % 2)
    else:
        pl.semaphore_wait(barrier, count)


def remote(src, dst, send, recv, dp, mp):
    return pltpu.make_async_remote_copy(
        src_ref=src,
        dst_ref=dst,
        send_sem=send,
        recv_sem=recv,
        device_id=(dp, mp),
        device_id_type=MESH,
    )


def line_gather(place, src, out, local, send, recv, paired, ready=None, rows=None):
    dp, z, c, mp, pair = place.dp, place.z, place.c, place.mp, place.pair

    def at(slot):
        if rows is None:
            return out.at[slot]
        return out.at[pl.ds(pl.multiple_of(slot * rows, 16), rows)]

    def slot_of(level, core):
        return level * 2 + core if paired else level

    def hop(event, slot, source, direction, target):
        return remote(source, at(slot), send.at[event, direction], recv.at[slot], dp, target)

    own = slot_of(z, c)
    keep = pltpu.make_async_copy(src, at(own), local)
    keep.start()

    def ways(event, level, slot, source, act):
        up = z < LINE - 1
        down = z > 0
        if event > 0:
            up = jnp.logical_and(up, level < z)
            down = jnp.logical_and(down, level > z)

        @pl.when(up)
        def _():
            act(hop(event, slot, source, 1, mp + 2))

        @pl.when(down)
        def _():
            act(hop(event, slot, source, 2, mp - 2))

        if paired:
            act(hop(event, slot, source, 0, pair))

    ways(0, z, own, src, lambda copy: copy.start())
    yield
    if ready is not None:
        keep.wait()
        ready(own)
        if paired:
            other = slot_of(z, 1 - c)
            hop(0, other, at(other), 0, pair).wait_recv()
            ready(other)

    def settle(event):
        level = place.zorder(event)
        ready(slot_of(level, c))
        if paired:
            other = slot_of(level, 1 - c)
            hop(event, other, at(other), 0, pair).wait_recv()
            ready(other)

    for event in range(1, LINE):
        level = place.zorder(event)
        slot = slot_of(level, c)
        hop(event, slot, at(slot), 0, pair).wait_recv()
        ways(event, level, slot, at(slot), lambda copy: copy.start())
        if ready is not None and event > 1:
            if event == 2:
                settle(1)
            settle(event)
        yield
    if ready is None:
        if paired:
            for level in range(LINE):
                other = slot_of(level, 1 - c)
                hop(0, other, at(other), 0, pair).wait_recv()
        keep.wait()
    for event in range(LINE):
        level = place.zorder(event)
        slot = slot_of(level, c)
        ways(event, level, slot, at(slot), lambda copy: copy.wait_send())
    yield


def plane_gather(place, src, out, local, send, recv, ready=None, primed=False):
    dp, c, mp, pair = place.dp, place.c, place.mp, place.pair
    dpx, dpy, dpd = place.dpx, place.dpy, place.dpd
    half = src.shape[0] // 2
    part_a, part_b = pl.ds(0, half), pl.ds(half, half)

    def at(group, core):
        return out.at[group * 2 + core]

    def hop(index, block, group, target):
        return remote(block, block, send.at[index], recv.at[index], group, target)

    def done(group, core):
        if ready is not None:
            ready(group * 2 + core)

    keep = pltpu.make_async_copy(src, at(dp, c), local)
    here = at(dp, c)
    from_x, from_y, from_d = at(dpx, c), at(dpy, c), at(dpd, c)
    firsts = [
        remote(src, here, send.at[0], recv.at[0], dp, pair),
        remote(src, here, send.at[1], recv.at[1], dpx, mp),
        remote(src, here, send.at[2], recv.at[2], dpy, mp),
    ]
    seconds = [
        hop(3, from_x.at[part_a], dpy, mp),
        hop(4, from_y.at[part_b], dpx, mp),
        hop(5, from_x, dp, pair),
        hop(6, from_y, dp, pair),
        hop(7, from_d.at[part_a], dp, pair),
        hop(8, from_d.at[part_b], dp, pair),
    ]
    if primed:
        yield
    keep.start()
    for copy in firsts:
        copy.start()
    yield
    if ready is not None:
        keep.wait()
        done(dp, c)
        hop(0, at(dp, 1 - c), dp, pair).wait_recv()
        done(dp, 1 - c)
    hop(1, from_x, dpx, mp).wait_recv()
    seconds[0].start()
    hop(2, from_y, dpy, mp).wait_recv()
    seconds[1].start()
    seconds[2].start()
    seconds[3].start()
    yield
    done(dpx, c)
    hop(5, at(dpx, 1 - c), dp, pair).wait_recv()
    done(dpx, 1 - c)
    if ready is not None:
        yield
    done(dpy, c)
    hop(6, at(dpy, 1 - c), dp, pair).wait_recv()
    done(dpy, 1 - c)
    if ready is not None:
        yield
    hop(3, from_d.at[part_a], dpy, mp).wait_recv()
    seconds[4].start()
    hop(4, from_d.at[part_b], dpx, mp).wait_recv()
    seconds[5].start()
    done(dpd, c)
    other = at(dpd, 1 - c)
    hop(7, other.at[part_a], dp, pair).wait_recv()
    hop(8, other.at[part_b], dp, pair).wait_recv()
    done(dpd, 1 - c)
    yield
    if ready is None:
        hop(0, at(dp, 1 - c), dp, pair).wait_recv()
        keep.wait()
    for copy in firsts + seconds:
        copy.wait_send()
    yield


def drive(*programs):
    live = list(programs)
    while live:
        for program in list(live):
            try:
                next(program)
            except StopIteration:
                live.remove(program)


def dma(*shape):
    return pltpu.SemaphoreType.DMA(shape)


def params(cid, vmem=40):
    return pltpu.CompilerParams(
        collective_id=cid, has_side_effects=True, vmem_limit_bytes=vmem << 20
    )


def exchange(place, src, out, local, send, recv):
    dp, mp = place.dp, place.mp
    keep = pltpu.make_async_copy(src.at[mp], out.at[mp], local)
    keep.start()
    sends = []
    for hop in range(1, 8):
        target = (mp + hop) % 8
        sends.append(
            remote(src.at[target], out.at[mp], send.at[hop], recv.at[hop], dp, target)
        )
        sends[-1].start()
    yield
    keep.wait()
    for hop in range(1, 8):
        origin = (mp + 8 - hop) % 8
        remote(out.at[origin], out.at[origin], send.at[hop], recv.at[hop], dp, origin).wait_recv()
    for copy in sends:
        copy.wait_send()
    yield


def line_reduce(place, produce, tiles, result, bufs, sems, paired):
    dp, z, c, mp, pair = place.dp, place.z, place.c, place.mp, place.pair
    above_block, below_block, out_block = bufs["above"], bufs["below"], bufs["out"]
    order = [place.zorder(event) for event in (3, 2, 1, 0)]
    inner = jnp.logical_and(z > 0, z < LINE - 1)
    outer = jnp.logical_or(z == 0, z == LINE - 1)

    @pl.when(z == LINE - 1)
    def _():
        above_block[...] = jnp.zeros(above_block.shape, BF)

    @pl.when(z == 0)
    def _():
        below_block[...] = jnp.zeros(below_block.shape, BF)

    def from_above(level):
        return above_block.at[jnp.minimum(level, LINE - 2)]

    def from_below(level):
        return below_block.at[jnp.maximum(level - 1, 0)]

    def across(step, level):
        return remote(
            bufs["pair_out"].at[step % 2],
            bufs["pair_in"].at[level],
            sems["pair_send"].at[step % 2],
            sems["pair_recv"].at[level],
            dp,
            pair,
        )

    if paired:
        for step, level in enumerate(order):
            if step > 1:
                across(step - 2, order[step - 2]).wait_send()
            for rows in tiles:
                bufs["pair_out"][step % 2, rows] = produce(level, 1 - c, rows).astype(BF)
            across(step, level).start()
    yield

    def toward(step, level, act):
        @pl.when(level < z)
        def _():
            act(
                remote(
                    out_block.at[step],
                    from_above(level),
                    sems["line_send"].at[step],
                    sems["above"].at[level],
                    dp,
                    mp - 2,
                )
            )

        @pl.when(level > z)
        def _():
            act(
                remote(
                    out_block.at[step],
                    from_below(level),
                    sems["line_send"].at[step],
                    sems["below"].at[level],
                    dp,
                    mp + 2,
                )
            )

    def arrive(level, above):
        if above:
            remote(
                from_above(level),
                from_above(level),
                sems["line_send"].at[0],
                sems["above"].at[level],
                dp,
                mp,
            ).wait_recv()
        else:
            remote(
                from_below(level),
                from_below(level),
                sems["line_send"].at[0],
                sems["below"].at[level],
                dp,
                mp,
            ).wait_recv()

    def advance(step):
        level = order[step]
        if paired:
            across(step, level).wait_recv()

        @pl.when(jnp.logical_and(level < z, z < LINE - 1))
        def _():
            arrive(level, True)

        @pl.when(jnp.logical_and(level > z, z > 0))
        def _():
            arrive(level, False)

        for rows in tiles:
            total = produce(level, c, rows)
            if paired:
                total = total + bufs["pair_in"][level, rows].astype(F32)

            @pl.when(level < z)
            def _():
                out_block[step, rows] = (total + from_above(level)[rows].astype(F32)).astype(BF)

            @pl.when(level > z)
            def _():
                out_block[step, rows] = (total + from_below(level)[rows].astype(F32)).astype(BF)

        toward(step, level, lambda copy: copy.start())

    advance(0)
    for step in (1, 2):

        @pl.when(outer)
        def _():
            advance(step)

    yield
    for step in (1, 2):

        @pl.when(inner)
        def _():
            advance(step)

        yield

    if paired:
        across(3, z).wait_recv()

    @pl.when(z < LINE - 1)
    def _():
        arrive(z, True)

    @pl.when(z > 0)
    def _():
        arrive(z, False)

    for rows in tiles:
        total = produce(z, c, rows)
        if paired:
            total = total + bufs["pair_in"][z, rows].astype(F32)
        total = total + from_above(z)[rows].astype(F32) + from_below(z)[rows].astype(F32)
        result(rows, total)
    for step, level in enumerate(order):
        if paired and step > 1:
            across(step, level).wait_send()
        if step < 3:
            toward(step, level, lambda copy: copy.wait_send())
    yield


def line_reduce_scratch(rows, cols, paired):
    block = lambda n: pltpu.VMEM((n, rows, cols), BF)
    scratch = {"above": block(3), "below": block(3), "out": block(3)}
    sems = {"line_send": dma(3), "above": dma(4), "below": dma(4)}
    if paired:
        scratch.update({"pair_out": block(2), "pair_in": block(4)})
        sems.update({"pair_send": dma(2), "pair_recv": dma(4)})
    return scratch, sems


def plane_reduce(place, produce, tile, half, result, bufs, sems, paired=True, early=False):
    dp, c, mp, pair = place.dp, place.c, place.mp, place.pair
    dpx, dpy, dpd = place.dpx, place.dpy, place.dpd
    starts = range(0, half, tile)
    send, recv = sems["send"], sems["recv"]
    out_block, landed = bufs["out"], bufs["in"]
    groups = {"far": dpd, "x": dpx, "y": dpy, "own": dp}
    steps = ["x", "y", "far", "own"] if early else ["far", "x", "y", "own"]

    def across(name):
        step = steps.index(name)
        return remote(
            bufs["pair_out"].at[step % 2],
            bufs["pair_in"].at[step],
            sems["pair_send"].at[step % 2],
            sems["pair_recv"].at[step],
            dp,
            pair,
        )

    def cross(name):
        if not paired:
            return
        step = steps.index(name)
        if step > 1:
            across(steps[step - 2]).wait_send()
        bufs["pair_out"][step % 2] = produce(groups[name], 1 - c, 0, 2 * half).astype(BF)
        across(name).start()

    def crossed(name):
        if paired:
            across(name).wait_recv()

    def share(name, start):
        total = produce(groups[name], c, start, tile)
        if paired:
            total = total + bufs["pair_in"][steps.index(name), pl.ds(start, tile)].astype(F32)
        return total

    def hop(index):
        target = (dpx, dpy, dpx, dpx, dpy, dpy)[index]
        return remote(
            out_block.at[index], landed.at[index], send.at[index], recv.at[index], target, mp
        )

    def fill(index, name, base, extra=None):
        for start in starts:
            total = share(name, base + start)
            if extra is not None:
                total = total + landed[extra, pl.ds(start, tile)].astype(F32)
            out_block[index, pl.ds(start, tile)] = total.astype(BF)
        hop(index).start()

    def far():
        crossed("far")
        fill(0, "far", 0)
        fill(1, "far", half)

    def near():
        crossed("x")
        fill(2, "x", 0)
        crossed("y")
        fill(4, "y", half)

    if early:
        cross("x")
        yield
        cross("y")
        near()
        yield
        cross("far")
        far()
        yield
        cross("own")
    else:
        cross("far")
        cross("x")
        yield
        far()
        cross("y")
        near()
        cross("own")
    yield
    hop(1).wait_recv()
    fill(3, "x", half, extra=1)
    hop(0).wait_recv()
    fill(5, "y", 0, extra=0)
    yield
    crossed("own")
    for index in (2, 3, 4, 5):
        hop(index).wait_recv()
    for base, pieces in ((0, (2, 5)), (half, (3, 4))):
        for start in starts:
            total = share("own", base + start)
            for piece in pieces:
                total = total + landed[piece, pl.ds(start, tile)].astype(F32)
            result(pl.ds(base + start, tile), total)
    for index in range(6):
        hop(index).wait_send()
    if paired:
        for name in steps[2:]:
            across(name).wait_send()
    yield


def plane_reduce_scratch(half, cols, paired=True):
    block = lambda n, rows: pltpu.VMEM((n, rows, cols), BF)
    scratch = {"out": block(6, half), "in": block(6, half)}
    sems = {"send": dma(6), "recv": dma(6)}
    if paired:
        scratch.update({"pair_out": block(2, 2 * half), "pair_in": block(4, 2 * half)})
        sems.update({"pair_send": dma(2), "pair_recv": dma(4)})
    return scratch, sems


def project_kernel(
    frames_ref, gain_ref, shift_ref, cot_ref, query_ref, key_ref, value_ref, bias_ref,
    nfull_ref, qkv_ref, cfull_ref, weight_ref,
    normed_ref, local, line_send, line_recv, plane_send, plane_recv,
):
    place = Place()
    weight_ref[...] = jnp.zeros(weight_ref.shape, BF)
    for index, ref in enumerate((query_ref, key_ref, value_ref)):
        for head in range(2):
            weight_ref[pl.ds(index * 256 + head * 128, HD)] = ref[pl.ds(head * HD, HD)]
    for start in range(0, ROWS, 128):
        rows = pl.ds(start, 128)
        normed_ref[rows] = layer_norm(
            frames_ref[rows].astype(F32), gain_ref[...], shift_ref[...]
        ).astype(BF)
    greet(place, line=True, plane=True)

    def ready(slot):
        product = lax.dot_general(
            nfull_ref[slot],
            weight_ref[...],
            (((1,), (1,)), ((), ())),
            preferred_element_type=F32,
        )
        qkv_ref[slot] = (product + bias_ref[...]).astype(BF)

    drive(
        line_gather(
            place, normed_ref, nfull_ref, local.at[0], line_send, line_recv, True, ready
        ),
        plane_gather(place, cot_ref, cfull_ref, local.at[1], plane_send, plane_recv),
    )


def project(frames, gain, shift, cotangent, query, key, value, bias):
    return pl.pallas_call(
        project_kernel,
        out_shape=(
            jax.ShapeDtypeStruct((8,) + frames.shape, BF),
            jax.ShapeDtypeStruct((8, ROWS, 768), BF),
            jax.ShapeDtypeStruct((8,) + cotangent.shape, BF),
            jax.ShapeDtypeStruct((768, 1280), BF),
        ),
        in_specs=[VMEM, VMEM, VMEM, ANY, VMEM, VMEM, VMEM, VMEM],
        out_specs=(VMEM, VMEM, ANY, VMEM),
        scratch_shapes=[pltpu.VMEM((ROWS, 1280), BF), dma(2), dma(4, 3), dma(8), dma(9), dma(9)],
        compiler_params=params(0),
        name="project",
    )(frames, gain, shift, cotangent, query, key, value, bias)


def attend_kernel(
    qkv_ref, mask_ref, live_ref, weights_ref, outer_ref,
    att_ref, logs_ref, peak_ref, wfull_ref, ofull_ref,
    out_ref, vt_ref, outer_all, local, send, recv, line_send, line_recv,
    outer_send, outer_recv, plane_send, plane_recv,
):
    place = Place()
    greet(place, mp_all=True, plane=True)
    outer = line_gather(
        place, outer_ref, outer_all, local.at[2], outer_send, outer_recv, False, None, 48
    )
    next(outer)
    gather = line_gather(
        place, weights_ref, wfull_ref, local.at[1], line_send, line_recv, False
    )
    next(gather)
    factor = math.log2(math.e) / math.sqrt(HD)
    peak_ref[...] = jnp.full(peak_ref.shape, MASK_VALUE, F32)

    @pl.loop(0, 6)
    def _(turn):
        clip = turn // 2
        head = turn % 2
        lane = pl.multiple_of(head * 128, 128)
        row = pl.multiple_of(head * HD, 16)
        keys = qkv_ref[:, clip, :, pl.ds(256 + lane, 128)].reshape(1024, 128)
        vt_ref[...] = qkv_ref[:, clip, :, pl.ds(512 + lane, 128)].reshape(1024, 128).T

        @pl.loop(0, 4)
        def _(block):
            query = qkv_ref[pl.ds(block * 2, 2), clip, :, pl.ds(lane, 128)].reshape(256, 128)
            columns = pl.ds(pl.multiple_of(block * 256, 256), 256)
            scores = lax.dot_general(
                keys, query, (((1,), (1,)), ((), ())), preferred_element_type=F32
            )
            scores = scores + mask_ref[clip]
            peak = jnp.max(scores, axis=0, keepdims=True)
            powers = jnp.exp2((scores - peak) * factor)
            total = jnp.sum(powers, axis=0, keepdims=True)
            mixed = lax.dot_general(
                vt_ref[...],
                powers.astype(BF),
                (((1,), (0,)), ((), ())),
                preferred_element_type=F32,
            )
            mixed = (mixed / total).astype(BF)
            for part in range(2):
                out_ref[block * 2 + part, clip, pl.ds(row, HD)] = mixed[
                    :HD, part * 128 : part * 128 + 128
                ]
            logs_ref[turn, :, columns] = peak * factor + jnp.log2(total)
            peak_ref[head] = jnp.maximum(
                peak_ref[head], jnp.where(live_ref[clip, :, columns] > 0, peak, MASK_VALUE)
            )

        @pl.when(turn == 2)
        def _():
            next(outer)

        @pl.when(turn == 4)
        def _():
            next(outer)
            next(gather)

    mixing = exchange(place, out_ref, att_ref, local.at[0], send, recv)
    next(mixing)
    for _ in outer:
        pass
    spread = plane_gather(place, outer_all, ofull_ref, local.at[3], plane_send, plane_recv)
    drive(spread, gather, mixing)


def attend(qkv, mask, live, weights, outer):
    return pl.pallas_call(
        attend_kernel,
        out_shape=(
            jax.ShapeDtypeStruct((8, 3, 160, 128), BF),
            jax.ShapeDtypeStruct((6, 1, 1024), F32),
            jax.ShapeDtypeStruct((2, 8, 256), F32),
            jax.ShapeDtypeStruct((4,) + weights.shape, BF),
            jax.ShapeDtypeStruct((8, 192, 1280), BF),
        ),
        in_specs=[VMEM, VMEM, VMEM, ANY, ANY],
        out_specs=(VMEM, VMEM, VMEM, ANY, ANY),
        scratch_shapes=[
            pltpu.VMEM((8, 3, 160, 128), BF),
            pltpu.VMEM((128, 1024), BF),
            pltpu.VMEM((192, 1280), BF),
            dma(4),
            dma(8),
            dma(8),
            dma(4, 3),
            dma(4),
            dma(4, 3),
            dma(4),
            dma(9),
            dma(9),
        ],
        compiler_params=params(1),
        name="attend",
    )(qkv, mask, live, weights, outer)


def flatten(*pairs):
    names, shapes = [], []
    for number, group in enumerate(pairs):
        for name, shape in group.items():
            names.append((number, name))
            shapes.append(shape)

    def split(refs):
        groups = [{} for _ in pairs]
        for (number, name), ref in zip(names, refs):
            groups[number][name] = ref
        return groups

    return shapes, split


def feed_forward_kernel(
    split, normed_ref, upstream_ref, weights_ref, down_ref, bias_ref,
    total_ref, hidden_ref, grads_ref, bias_out, down_all,
    normed_all, upstream_all, slope_all, rate_ref, sum_ref,
    load, local, line_local, gather_send, gather_recv, line_send, line_recv, *scratch,
):
    place = Place()
    bufs, sems = split(scratch)
    loads = []
    for slot in range(8):
        loads.append(
            pltpu.make_async_copy(upstream_ref.at[slot], upstream_all.at[slot], load.at[slot])
        )
        loads[-1].start()
    greet(place, line=True, plane=True)
    bias_out[...] = jnp.zeros(bias_out.shape, F32)

    def up_rows():
        return weights_ref[:, pl.ds(0, 160)].reshape(640, 1280)

    def down_rows():
        return down_all[...].reshape(640, 1280)

    def activate(slot, rows):
        before = (
            lax.dot_general(
                normed_all[slot, rows],
                up_rows(),
                (((1,), (1,)), ((), ())),
                preferred_element_type=F32,
            )
            + bias_ref[...]
        )
        share = 0.5 + 0.5 * lax.erf(before * math.sqrt(0.5))
        hidden_ref[slot, rows] = (before * share).astype(BF)
        density = jnp.exp(before * before * -0.5) * (1.0 / math.sqrt(2.0 * math.pi))
        return share + before * density

    def pull_back(slot, rows, rate):
        pull = lax.dot_general(
            upstream_all[slot, rows],
            down_rows(),
            (((1,), (1,)), ((), ())),
            preferred_element_type=F32,
        )
        slope = (pull * rate).astype(BF)
        slope_all[slot, rows] = slope
        bias_out[...] += jnp.sum(slope.astype(F32), axis=0, keepdims=True)

    here = [place.dp * 2 + place.c, place.dp * 2 + 1 - place.c]
    seen = []

    def ready(slot):
        index = len(seen)
        seen.append(slot)

        rows = pl.ds(0, ROWS)
        rate = activate(slot, rows)
        if index < 2:
            rate_ref[index] = rate
        else:
            pull_back(slot, rows, rate)

        if index < 2:
            next(down)

    def finish_here():
        for index in range(2):
            pull_back(here[index], pl.ds(0, ROWS), rate_ref[index])

    down = line_gather(
        place, down_ref, down_all, line_local, line_send, line_recv, False
    )
    gather = plane_gather(
        place, normed_ref, normed_all, local, gather_send, gather_recv, ready
    )

    def produce(group, core, start, rows):
        return jnp.dot(
            slope_all[group * 2 + core, pl.ds(start, rows)],
            up_rows(),
            preferred_element_type=F32,
        )

    def result(rows, total):
        total_ref[rows] = total

    reduce = plane_reduce(place, produce, 192, 192, result, bufs, sems, True, True)
    next(down)
    next(gather)
    for copy in loads:
        copy.wait()
    next(gather)
    for _ in down:
        pass
    next(gather)
    next(reduce)
    next(gather)
    next(reduce)
    next(gather)
    next(reduce)
    finish_here()
    next(reduce)

    def weight_grads(left_all, right_all, base):
        @pl.loop(0, 8)
        def _(slot):
            product = lax.dot_general(
                left_all[slot],
                right_all[slot],
                (((0,), (0,)), ((), ())),
                preferred_element_type=F32,
            )
            sum_ref[...] = jnp.where(slot == 0, product, sum_ref[...] + product)

        for level in range(4):
            grads_ref[level, pl.ds(base, 160)] = sum_ref[pl.ds(level * 160, 160)].astype(BF)

    weight_grads(slope_all, normed_all, 0)
    next(reduce)
    weight_grads(hidden_ref, upstream_all, 160)
    for level in range(4):
        grads_ref[level, pl.ds(320, 16)] = jnp.zeros((16, 1280), BF)
        grads_ref[level, pl.ds(320, 16), pl.ds(0, 640)] = jnp.broadcast_to(
            bias_out[...], (16, 640)
        ).astype(BF)
    drive(reduce, gather)


def feed_forward(normed, upstream, weights, down, bias):
    shapes, split = flatten(*plane_reduce_scratch(192, 1280))
    return pl.pallas_call(
        functools.partial(feed_forward_kernel, split),
        out_shape=(
            jax.ShapeDtypeStruct((ROWS, 1280), F32),
            jax.ShapeDtypeStruct((8, ROWS, 640), BF),
            jax.ShapeDtypeStruct((4, 336, 1280), BF),
            jax.ShapeDtypeStruct((1, 640), F32),
            jax.ShapeDtypeStruct((4, 160, 1280), BF),
        ),
        in_specs=[ANY, ANY, VMEM, ANY, VMEM],
        out_specs=(VMEM,) * 5,
        scratch_shapes=[
            pltpu.VMEM((8, ROWS, 1280), BF),
            pltpu.VMEM((8, ROWS, 1280), BF),
            pltpu.VMEM((8, ROWS, 640), BF),
            pltpu.VMEM((2, ROWS, 640), F32),
            pltpu.VMEM((640, 1280), F32),
            dma(8),
            pltpu.SemaphoreType.DMA(()),
            pltpu.SemaphoreType.DMA(()),
            dma(9),
            dma(9),
            dma(4, 3),
            dma(4),
            *shapes,
        ],
        compiler_params=params(3, 60),
        name="feed_forward",
    )(normed, upstream, weights, down, bias)


def attend_back_kernel(
    split, qkv_in, mask_ref, logs_ref, pull_ref, hidden_in, weights_ref, feed_grads_in,
    out_grad_in, dqkv_ref, feed_ref, feed_sum_ref, out_sum_ref,
    qkv_ref, hidden_ref, feed_grads_ref, out_grad_ref, load,
    grad_ref, kt_ref, dk_ref, dv_ref, block_ref, middle_ref, local, send, recv, *scratch,
):
    place = Place()
    (
        line_bufs, line_sems, plane_bufs, plane_sems,
        out_plane_bufs, out_plane_sems, out_line_bufs, out_line_sems,
    ) = split(scratch)
    loads = [
        pltpu.make_async_copy(source, target, load.at[index])
        for index, (source, target) in enumerate(
            (
                (out_grad_in, out_grad_ref),
                (feed_grads_in, feed_grads_ref),
                (hidden_in, hidden_ref),
                (qkv_in, qkv_ref),
            )
        )
    ]
    for copy in loads:
        copy.start()
    greet(place, mp_all=True, plane=True)
    scale = 1.0 / math.sqrt(HD)
    factor = math.log2(math.e) * scale
    arriving = exchange(place, pull_ref, grad_ref, local, send, recv)
    next(arriving)

    def feed_block(group, core, start, rows):
        return jnp.dot(
            hidden_ref[group * 2 + core, pl.ds(start, rows)],
            weights_ref[...].reshape(640, 1280),
            preferred_element_type=F32,
        )

    def feed_result(rows, total):
        feed_ref[rows] = total

    def sum_result(rows, total):
        feed_sum_ref[rows] = total

    plane = plane_reduce(
        place, feed_block, 192, 192, feed_result, plane_bufs, plane_sems, True
    )
    line = line_reduce(
        place,
        lambda level, core, rows: feed_grads_ref[level, rows].astype(F32),
        [pl.ds(start, 112) for start in range(0, 336, 112)],
        sum_result,
        line_bufs,
        line_sems,
        False,
    )
    def middle(rows, total):
        middle_ref[rows] = total

    def out_result(rows, total):
        out_sum_ref[rows] = total

    out_plane = plane_reduce(
        place,
        lambda group, core, start, rows: out_grad_ref[group, core, pl.ds(start, rows)].astype(F32),
        96,
        96,
        middle,
        out_plane_bufs,
        out_plane_sems,
    )
    out_line = line_reduce(
        place,
        lambda level, core, rows: middle_ref[
            pl.ds(pl.multiple_of(level * 48 + rows.start, 16), rows.size)
        ],
        [pl.ds(0, 48)],
        out_result,
        out_line_bufs,
        out_line_sems,
        False,
    )
    loads[0].wait()
    next(out_plane)
    next(out_plane)
    loads[2].wait()
    next(plane)
    next(plane)
    loads[1].wait()
    next(line)
    next(line)
    next(out_line)
    loads[3].wait()
    for _ in arriving:
        pass
    block_ref[...] = jnp.zeros(block_ref.shape, BF)

    @pl.loop(0, 6)
    def _(turn):
        clip = turn // 2
        head = turn % 2
        lane = pl.multiple_of(head * 128, 128)
        row = pl.multiple_of(head * HD, 16)
        kt_ref[...] = qkv_ref[:, clip, :, pl.ds(256 + lane, 128)].reshape(1024, 128).T
        dk_ref[...] = jnp.zeros(dk_ref.shape, F32)
        dv_ref[...] = jnp.zeros(dv_ref.shape, F32)

        @pl.loop(0, 4)
        def _(block):
            query = qkv_ref[pl.ds(block * 2, 2), clip, :, pl.ds(lane, 128)].reshape(256, 128)
            values = qkv_ref[:, clip, :, pl.ds(512 + lane, 128)].reshape(1024, 128)
            keys = qkv_ref[:, clip, :, pl.ds(256 + lane, 128)].reshape(1024, 128)
            columns = pl.ds(pl.multiple_of(block * 256, 256), 256)
            for part in range(2):
                block_ref[:HD, part * 128 : part * 128 + 128] = grad_ref[
                    block * 2 + part, clip, pl.ds(row, HD)
                ]
            scores = lax.dot_general(
                keys, query, (((1,), (1,)), ((), ())), preferred_element_type=F32
            )
            chance = jnp.exp2((scores + mask_ref[clip]) * factor - logs_ref[turn, :, columns])
            dv_ref[...] += lax.dot_general(
                chance.astype(BF),
                block_ref[...],
                (((1,), (1,)), ((), ())),
                preferred_element_type=F32,
            )
            slope = lax.dot_general(
                values, block_ref[...], (((1,), (0,)), ((), ())), preferred_element_type=F32
            )
            center = jnp.sum(chance * slope, axis=0, keepdims=True)
            change = (chance * (slope - center)).astype(BF)
            dk_ref[...] += lax.dot_general(
                change, query, (((1,), (0,)), ((), ())), preferred_element_type=F32
            )
            dq = lax.dot_general(
                kt_ref[...], change, (((1,), (0,)), ((), ())), preferred_element_type=F32
            )
            dqkv_ref[pl.ds(block * 2, 2), clip, :, pl.ds(lane, 128)] = (
                (dq.T * scale).astype(BF).reshape(2, 128, 128)
            )

        dqkv_ref[:, clip, :, pl.ds(256 + lane, 128)] = (
            (dk_ref[...] * scale).astype(BF).reshape(8, 128, 128)
        )
        dqkv_ref[:, clip, :, pl.ds(512 + lane, 128)] = (
            dv_ref[...].astype(BF).reshape(8, 128, 128)
        )

        @pl.when(turn == 2)
        def _():
            next(out_plane)
            next(plane)

        @pl.when(turn == 5)
        def _():
            next(out_plane)

    drive(line, out_line, plane, out_plane)


def attend_back(qkv, mask, logs, pull, hidden, weights, feed_grads, out_grad):
    shapes, split = flatten(
        *line_reduce_scratch(336, 1280, False),
        *plane_reduce_scratch(192, 1280),
        *plane_reduce_scratch(96, 1280),
        *line_reduce_scratch(48, 1280, False),
    )
    return pl.pallas_call(
        functools.partial(attend_back_kernel, split),
        out_shape=(
            jax.ShapeDtypeStruct(qkv.shape, BF),
            jax.ShapeDtypeStruct((ROWS, 1280), F32),
            jax.ShapeDtypeStruct((336, 1280), F32),
            jax.ShapeDtypeStruct((48, 1280), F32),
        ),
        in_specs=[ANY, VMEM, VMEM, ANY, ANY, VMEM, ANY, ANY],
        out_specs=(VMEM,) * 4,
        scratch_shapes=[
            *(pltpu.VMEM(ref.shape, BF) for ref in (qkv, hidden, feed_grads, out_grad)),
            dma(4),
            pltpu.VMEM((8, 3, 160, 128), BF),
            pltpu.VMEM((128, 1024), BF),
            pltpu.VMEM((1024, 128), F32),
            pltpu.VMEM((1024, 128), F32),
            pltpu.VMEM((128, 256), BF),
            pltpu.VMEM((192, 1280), F32),
            pltpu.SemaphoreType.DMA(()),
            dma(8),
            dma(8),
            *shapes,
        ],
        compiler_params=params(2, 62),
        name="attend_back",
    )(qkv, mask, logs, pull, hidden, weights, feed_grads, out_grad)


GROUP_ROWS = 4832
GROUP_STEP = 4800
PACK_ROWS = GROUP_STEP * 3 + GROUP_ROWS
SEGMENTS = (
    ("query", 0, 1600),
    ("query_bias", 204800, 2),
    ("key", 204960, 1600),
    ("value", 409760, 1600),
    ("value_bias", 614560, 2),
    ("out", 614720, 1600),
    ("up", 819520, 6400),
    ("up_bias", 1638720, 5),
    ("down", 1639360, 6400),
)
PACK_END = 19216
SHARE_ROWS = 4808


def segment_table():
    table, cursor = {}, 0
    for name, start, rows in SEGMENTS:
        row = start // 128
        cursor += 32
        cursor += (row - cursor) % 8
        table[name] = (cursor, row, rows, start % 128)
        cursor += rows
    return table, (cursor + 32 + 7) // 8 * 8


TABLE, STAGE_ROWS = segment_table()


def lane_of(rows):
    return lax.broadcasted_iota(jnp.int32, (rows, 128), 1)


def pack_rows(stage, packed):
    def piece(name, first, rows):
        base, row, _, shift = TABLE[name]
        at = base - row + first
        here = stage[pl.ds(at, rows)]
        if shift == 0:
            return here
        above = stage[pl.ds(at - 1, rows)]
        return jnp.where(
            lane_of(rows) >= shift, pltpu.roll(here, shift, 1), pltpu.roll(above, shift, 1)
        )

    done = set()
    for name, _, _ in SEGMENTS:
        _, row, rows, shift = TABLE[name]
        low = -(-(row + (1 if shift else 0)) // 16) * 16
        high = (row + rows) // 16 * 16
        if high <= low:
            continue
        done.update(range(low, high, 16))
        turns = (high - low) // 128

        @pl.loop(0, turns)
        def _(turn):
            first = pl.multiple_of(low + turn * 128, 16)
            packed[pl.ds(first, 128)] = piece(name, first, 128).astype(BF)

        for first in range(low + turns * 128, high, 16):
            packed[pl.ds(first, 16)] = piece(name, first, 16).astype(BF)
    for first in range(0, PACK_ROWS, 16):
        if first in done:
            continue
        total = jnp.zeros((16, 128), F32)
        for name, _, _ in SEGMENTS:
            _, row, rows, shift = TABLE[name]
            if row < first + 16 and row + rows + (1 if shift else 0) > first:
                total = total + piece(name, first, 16)
        packed[pl.ds(first, 16)] = total.astype(BF)


def stage_wide(stage, name, ref, step):
    base = TABLE[name][0]
    rows, wide = ref.shape[0], ref.shape[1] // 128

    @pl.loop(0, rows // step)
    def _(turn):
        first = pl.multiple_of(turn * step, step)
        for block in range(wide):
            stage[pl.ds(base + first * wide + block, step, stride=wide), :] = ref[
                pl.ds(first, step), pl.ds(block * 128, 128)
            ].astype(F32)


def stage_heads(stage, name, ref, lanes, column):
    base = TABLE[name][0]
    for head in range(2):
        column[head] = ref[:, pl.ds(lanes + head * 128, 128)]

    @pl.loop(0, 5)
    def _(turn):
        lane = lane_of(64)
        rows = [jnp.zeros((64, 128), F32) for _ in range(5)]
        for block in range(8):
            item, head = block // 2, block % 2
            value = column[head, pl.ds(turn * 256 + item, 64, stride=4)]
            offset = block * HD
            first, shift = offset // 128, offset % 128
            if shift:
                value = pltpu.roll(value, shift, 1)
            if shift + HD > 128:
                rows[first] = rows[first] + jnp.where(lane >= shift, value, 0.0)
                rows[first + 1] = rows[first + 1] + jnp.where(
                    lane < shift + HD - 128, value, 0.0
                )
            else:
                rows[first] = rows[first] + value
        for index in range(5):
            stage[pl.ds(base + turn * 320 + index, 64, stride=5), :] = rows[index]


def stage_head_bias(stage, name, ref, lanes):
    base = TABLE[name][0]
    lane = lane_of(1)
    first = ref[0:1, pl.ds(lanes, 128)]
    second = pltpu.roll(ref[0:1, pl.ds(lanes + 128, 128)], HD, 1)
    stage[pl.ds(base, 1)] = first + jnp.where(lane >= HD, second, 0.0)
    stage[pl.ds(base + 1, 1)] = jnp.where(lane < 2 * HD - 128, second, 0.0)


def stage_share(stage, name, ref, first, count, place):
    base = TABLE[name][0] + place.dp * count * 10
    for block in range(10):
        stage[pl.ds(base + block, count, stride=10), :] = ref[
            pl.ds(first, count), pl.ds(block * 128, 128)
        ]


def stage_up(stage, ref, place):
    base = TABLE["up"][0]
    lane = lane_of(128)
    for quarter in range(4):

        @pl.when(place.dp == quarter)
        def _():
            for block in range(10):
                columns = pl.ds(block * 128, 128)
                first = ref[pl.ds(0, 128), columns].T
                second = jnp.where(lane < 32, ref[pl.ds(128, 128), columns].T, 0.0)
                shift = 32 * quarter
                if shift:
                    first = pltpu.roll(first, shift, 1)
                    second = pltpu.roll(second, shift, 1)
                    second = second + jnp.where(lane < shift, first, 0.0)
                    first = jnp.where(lane >= shift, first, 0.0)
                at = base + block * 640 + quarter
                stage[pl.ds(at, 128, stride=5), :] = first
                stage[pl.ds(at + 1, 128, stride=5), :] = second


def norm_back(frames_ref, middle_ref, gain_ref, grad_ref):
    def write(rows, total):
        value = frames_ref[rows].astype(F32)
        center = value - jnp.mean(value, axis=-1, keepdims=True)
        spread = jnp.mean(center * center, axis=-1, keepdims=True)
        root = lax.rsqrt(spread + NORM_EPSILON)
        scaled = center * root
        pull = total * gain_ref[...]
        along = jnp.mean(pull * scaled, axis=-1, keepdims=True)
        grad_ref[rows] = middle_ref[rows] + root * (
            pull - jnp.mean(pull, axis=-1, keepdims=True) - scaled * along
        )

    return write


def fetch(first, rows, sems, grad, weight, frames, middle):
    span = pl.ds(first, rows)
    pairs = (
        (grad[0].at[:, span], grad[1]),
        weight,
        (frames[0].at[span], frames[1]),
        (middle[0].at[span], middle[1]),
    )
    copies = [
        pltpu.make_async_copy(source, target, sems.at[index])
        for index, (source, target) in enumerate(pairs)
    ]
    for copy in copies:
        copy.start()
    return copies


def fetch_scratch(rows):
    return [
        pltpu.VMEM((8, rows, 768), BF),
        pltpu.VMEM((768, 1280), BF),
        pltpu.VMEM((rows, 1280), BF),
        pltpu.VMEM((rows, 1280), F32),
        dma(4),
    ]


def line_product(place, grad_ref, weight_ref, rows, result, bufs, sems):
    def produce(level, core, tile):
        return jnp.dot(
            grad_ref[level * 2 + core, tile],
            weight_ref[...],
            preferred_element_type=F32,
        )

    tiles = [pl.ds(0, rows)]
    return line_reduce(place, produce, tiles, result, bufs, sems, True)


FIRST_ROWS = 128


def finish_kernel(
    split, grad_in, weight_in, joined_ref, bias_ref, bias_column_ref, sum_ref, out_ref,
    up_bias_ref, small_ref, peak_ref, frames_in, middle_in, gain_ref, shift_ref,
    input_grad_ref, grads_ref, small_out, peak_out,
    grad_ref, weight_ref, frames_ref, middle_ref, load,
    stage, packed, sum_rows, column, tiles, small_in, small_all, peak_all, edge,
    local, small_send, small_recv, plane_send, plane_recv, *scratch,
):
    place = Place()
    line_bufs, line_sems, bufs, sems = split(scratch)
    loads = fetch(
        0,
        FIRST_ROWS,
        load,
        (grad_in, grad_ref),
        (weight_in, weight_ref),
        (frames_in, frames_ref),
        (middle_in, middle_ref),
    )
    greet(place, mp_all=True, plane=True)
    peers = (place.dpx, place.dpy, place.dpd)

    def tell(index, source, target, group, act):
        act(
            remote(
                source,
                target.at[place.dp],
                plane_send.at[index],
                plane_recv.at[index],
                group,
                place.mp,
            )
        )

    def heard(index, target, group):
        block = target.at[group]
        remote(
            block, block, plane_send.at[index], plane_recv.at[index], group, place.mp
        ).wait_recv()

    line = line_product(
        place,
        grad_ref,
        weight_ref,
        FIRST_ROWS,
        norm_back(frames_ref, middle_ref, gain_ref, input_grad_ref),
        line_bufs,
        line_sems,
    )
    for index, group in enumerate(peers):
        tell(index, peak_ref, peak_all, group, lambda copy: copy.start())
    for copy in loads:
        copy.wait()

    for block in range(10):
        lanes = pl.ds(block * 128, 128)
        weight = weight_ref[:, lanes].astype(F32)
        turned = joined_ref[lanes].T
        whole = jnp.sum(weight * bias_column_ref[...], axis=0, keepdims=True)
        along = jnp.sum(weight * turned, axis=0, keepdims=True)
        tiles[pl.ds(block, 1)] = (along - shift_ref[:, lanes] * whole) / gain_ref[:, lanes]
        tiles[pl.ds(10 + block, 1)] = whole
    tiles[pl.ds(20, 44)] = small_ref[...]
    for run in range(8):
        edge[run] = tiles[pl.ds(run * 15 // 2, 8)]
    mixing = exchange(place, edge, small_in, local, small_send, small_recv)
    next(mixing)

    stage[...] = jnp.zeros(stage.shape, F32)
    for name, lanes in (("query", 0), ("key", 256), ("value", 512)):
        stage_heads(stage, name, joined_ref, lanes, column)
    stage_head_bias(stage, "query_bias", bias_ref, 0)
    stage_head_bias(stage, "value_bias", bias_ref, 512)
    stage_share(stage, "out", out_ref, 0, 40, place)
    stage_share(stage, "down", sum_ref, 160, 160, place)
    stage_up(stage, sum_ref, place)
    stage[pl.ds(TABLE["up_bias"][0], 5)] = up_bias_ref[...]
    pack_rows(stage, packed)

    def produce(group, core, start, rows):
        first = pl.multiple_of(group * GROUP_STEP + start, 16)
        return packed[pl.ds(first, GROUP_ROWS // 2)].astype(F32)

    def result(rows, total):
        sum_rows[rows] = total

    half = GROUP_ROWS // 2
    plane = plane_reduce(place, produce, half, half, result, bufs, sems, False)
    next(plane)
    next(plane)
    next(line)
    next(line)
    for _ in mixing:
        pass
    small_all[place.dp] = jnp.sum(small_in[...], axis=0)
    for index, group in enumerate(peers):
        tell(3 + index, small_all.at[place.dp], small_all, group, lambda copy: copy.start())
    next(plane)
    next(line)
    next(line)
    drive(line, plane)
    for index, group in enumerate(peers):
        heard(index, peak_all, group)
        heard(3 + index, small_all, group)
    top = peak_ref[...]
    for group in peers:
        top = jnp.maximum(top, peak_all[group])
    peak_out[...] = top
    whole = jnp.sum(small_all[...], axis=0)
    lane = lane_of(8)
    row = lax.broadcasted_iota(jnp.int32, (8, 128), 0)
    tiles[...] = jnp.zeros((64, 128), F32)
    tiles[pl.ds(8, 8)] = whole
    ahead = pltpu.roll(tiles[pl.ds(9, 8)], 64, 1)
    here = pltpu.roll(whole, 64, 1)
    odd = jnp.where(lane < 64, here, ahead)
    run_of = jnp.where(place.c == 1, odd, whole)
    run_of = jnp.where(jnp.logical_and(row == 7, lane >= 64), 0.0, run_of)
    small_out[...] = run_of
    tiles[pl.ds(8, 8)] = run_of
    wide = lane_of(16)
    entry = jnp.where(
        wide >= 64, pltpu.roll(tiles[pl.ds(1, 16)], 64, 1), pltpu.roll(tiles[pl.ds(0, 16)], 64, 1)
    )

    @pl.when(place.dp == 3)
    def _():
        sum_rows[pl.ds(GROUP_STEP, 16)] += entry

    for group in range(4):

        @pl.when(place.dp == group)
        def _():
            down, shift = 480 * group // 128, 480 * group % 128
            if shift == 0:
                grads_ref[...] = sum_rows[pl.ds(0, SHARE_ROWS)]
            else:
                for first in range(0, SHARE_ROWS, 1208):
                    size = min(1208, SHARE_ROWS - first)
                    grads_ref[pl.ds(first, size)] = jnp.where(
                        lane_of(size) < 128 - shift,
                        pltpu.roll(sum_rows[pl.ds(first + down, size)], 128 - shift, 1),
                        pltpu.roll(sum_rows[pl.ds(first + down + 1, size)], 128 - shift, 1),
                    )

    for index, group in enumerate(peers):
        tell(index, peak_ref, peak_all, group, lambda copy: copy.wait_send())
        tell(3 + index, small_all.at[place.dp], small_all, group, lambda copy: copy.wait_send())


def finish(grads, weight, joined, bias, sums, out, up_bias, small, peaks, frames, middle, gain, shift):
    shapes, split = flatten(
        *line_reduce_scratch(FIRST_ROWS, 1280, True),
        *plane_reduce_scratch(GROUP_ROWS // 2, 128, False),
    )
    return pl.pallas_call(
        functools.partial(finish_kernel, split),
        out_shape=(
            jax.ShapeDtypeStruct((FIRST_ROWS, 1280), F32),
            jax.ShapeDtypeStruct((SHARE_ROWS, 128), F32),
            jax.ShapeDtypeStruct((8, 128), F32),
            jax.ShapeDtypeStruct(peaks.shape, F32),
        ),
        in_specs=[ANY, ANY] + [VMEM] * 8 + [ANY, ANY, VMEM, VMEM],
        out_specs=(VMEM,) * 4,
        scratch_shapes=[
            *fetch_scratch(FIRST_ROWS),
            pltpu.VMEM((STAGE_ROWS, 128), F32),
            pltpu.VMEM((PACK_ROWS, 128), BF),
            pltpu.VMEM((GROUP_ROWS, 128), F32),
            pltpu.VMEM((2, 1280, 128), F32),
            pltpu.VMEM((64, 128), F32),
            pltpu.VMEM((8, 8, 128), F32),
            pltpu.VMEM((4, 8, 128), F32),
            pltpu.VMEM((4,) + peaks.shape, F32),
            pltpu.VMEM((8, 8, 128), F32),
            pltpu.SemaphoreType.DMA(()),
            dma(8),
            dma(8),
            dma(6),
            dma(6),
            *shapes,
        ],
        compiler_params=params(7, 62),
        name="finish",
    )(
        grads, weight, joined, bias[None], bias[:, None], sums, out, up_bias, small, peaks,
        frames, middle, gain, shift,
    )


def share_master_kernel(
    split, rows_ref, grad_in, weight_in, frames_in, middle_in, gain_ref,
    whole_out, input_grad_ref,
    grad_ref, weight_ref, frames_ref, middle_ref, load,
    whole_ref, parts, turned, store, send, recv, *scratch,
):
    place = Place()
    line_bufs, line_sems = split(scratch)
    loads = fetch(
        FIRST_ROWS,
        ROWS - FIRST_ROWS,
        load,
        (grad_in, grad_ref),
        (weight_in, weight_ref),
        (frames_in, frames_ref),
        (middle_in, middle_ref),
    )
    greet(place, line=True, plane=True)
    line = line_product(
        place,
        grad_ref,
        weight_ref,
        ROWS - FIRST_ROWS,
        norm_back(frames_ref, middle_ref, gain_ref, input_grad_ref),
        line_bufs,
        line_sems,
    )
    dp, mp, dpx, dpy, dpd = place.dp, place.mp, place.dpx, place.dpy, place.dpd
    half = GROUP_ROWS // 2
    part_a, part_b = pl.ds(0, half), pl.ds(half, half)
    for group in range(4):

        @pl.when(dp == group)
        def _():
            down, shift = 480 * group // 128, 480 * group % 128
            turned[pl.ds(0, 16)] = jnp.zeros((16, 128), F32)
            turned[pl.ds(16, SHARE_ROWS)] = rows_ref[...]
            turned[pl.ds(16 + SHARE_ROWS, 24)] = jnp.zeros((24, 128), F32)
            for first in range(0, GROUP_ROWS, 1208):
                here = turned[pl.ds(16 + first - down, 1208)]
                if shift:
                    here = jnp.where(
                        lane_of(1208) >= shift,
                        pltpu.roll(here, shift, 1),
                        pltpu.roll(turned[pl.ds(15 + first - down, 1208)], shift, 1),
                    )
                parts[dp, pl.ds(first, 1208)] = here.astype(BF)


    def hop(index, block, target):
        return remote(block, block, send.at[index], recv.at[index], target, mp)

    own = parts.at[dp]
    sends = [hop(0, own, dpx), hop(1, own, dpy)]
    for copy in sends:
        copy.start()

    stores = []

    def keep(index, first, rows):
        span = pl.ds(pl.multiple_of(first, 16), rows)
        stores.append(
            pltpu.make_async_copy(whole_ref.at[span], whole_out.at[span], store.at[index])
        )
        stores[-1].start()

    def unpack(group):
        for start in range(32, GROUP_STEP, 2384):
            at = pl.multiple_of(group * GROUP_STEP + start, 16)
            whole_ref[pl.ds(at, 2384)] = parts[group, pl.ds(start, 2384)].astype(F32)
        keep(len(stores), group * GROUP_STEP + 32, GROUP_STEP - 32)

    for copy in loads:
        copy.wait()
    next(line)
    next(line)
    unpack(dp)
    hop(0, parts.at[dpx], dpx).wait_recv()
    sends.append(hop(2, parts.at[dpx, part_a], dpy))
    sends[-1].start()
    hop(1, parts.at[dpy], dpy).wait_recv()
    sends.append(hop(3, parts.at[dpy, part_b], dpx))
    sends[-1].start()
    unpack(dpx)
    unpack(dpy)
    next(line)
    next(line)
    hop(2, parts.at[dpd, part_a], dpy).wait_recv()
    hop(3, parts.at[dpd, part_b], dpx).wait_recv()
    unpack(dpd)
    for group in range(4):
        first = parts[group, pl.ds(0, 32)].astype(F32)
        if group > 0:
            first = first + parts[group - 1, pl.ds(GROUP_STEP, 32)].astype(F32)
        whole_ref[pl.ds(group * GROUP_STEP, 32)] = first
        keep(4 + group, group * GROUP_STEP, 32)
    whole_ref[pl.ds(4 * GROUP_STEP, 16)] = parts[3, pl.ds(GROUP_STEP, 16)].astype(F32)
    keep(8, 4 * GROUP_STEP, 16)
    for copy in sends:
        copy.wait_send()
    drive(line)
    for copy in stores:
        copy.wait()


def share_master(rows, grads, weight, frames, middle, gain):
    shapes, split = flatten(*line_reduce_scratch(ROWS - FIRST_ROWS, 1280, True))
    return pl.pallas_call(
        functools.partial(share_master_kernel, split),
        out_shape=(
            jax.ShapeDtypeStruct((PACK_END, 128), F32),
            jax.ShapeDtypeStruct((ROWS - FIRST_ROWS, 1280), F32),
        ),
        in_specs=[VMEM, ANY, ANY, ANY, ANY, VMEM],
        out_specs=(ANY, VMEM),
        scratch_shapes=[
            *fetch_scratch(ROWS - FIRST_ROWS),
            pltpu.VMEM((PACK_END, 128), F32),
            pltpu.VMEM((4, GROUP_ROWS, 128), BF),
            pltpu.VMEM((SHARE_ROWS + 40, 128), F32),
            dma(9),
            dma(4),
            dma(4),
            *shapes,
        ],
        compiler_params=params(8, 60),
        name="share_master",
    )(rows, grads, weight, frames, middle, gain)


STEP_ENTRIES = 1024 * 76


def optimize_kernel(
    rates_ref, grads_ref, master_ref, first_ref, second_ref,
    owned_out, master_out, first_out, second_out, padded_out,
):
    entry = lax.broadcasted_iota(jnp.int32, (1, STEP_ENTRIES), 1)
    entry = entry + pl.program_id(0) * STEP_ENTRIES
    grads = grads_ref[...]
    first = BETA_FIRST * first_ref[...] + (1.0 - BETA_FIRST) * grads
    second = BETA_SECOND * second_ref[...] + (1.0 - BETA_SECOND) * grads * grads
    change = first * rates_ref[0] / (jnp.sqrt(second * rates_ref[1]) + ADAM_EPSILON)
    block = jnp.floor((entry.astype(F32) + 0.5) * (1.0 / HD))
    odd = block - 2.0 * jnp.floor(block * 0.5) > 0.5
    factor = jnp.where(
        entry < KEY_END, jnp.where(odd, rates_ref[4], rates_ref[3]), 1.0
    )
    master = (master_ref[...] * rates_ref[2] - change) * factor
    owned_out[...] = grads
    master_out[...] = master
    first_out[...] = first
    second_out[...] = second
    padded_out[...] = jnp.where(entry < SHARE_ENTRIES, master, 0.0)


KEY_END = 409760
SHARE_ENTRIES = 614880


def optimize(rates, grads, master, first, second):
    block = pl.BlockSpec((1, STEP_ENTRIES), lambda step: (0, step))
    share = jax.ShapeDtypeStruct((1, SHARE_ENTRIES), F32)
    return pl.pallas_call(
        optimize_kernel,
        grid=(pl.cdiv(SHARE_ENTRIES, STEP_ENTRIES),),
        out_shape=(share,) * 4 + (jax.ShapeDtypeStruct((1, SHARE_ROWS * 128), F32),),
        in_specs=[pl.BlockSpec(memory_space=pltpu.SMEM)] + [block] * 4,
        out_specs=(block,) * 5,
        compiler_params=pltpu.CompilerParams(vmem_limit_bytes=32 << 20),
        name="optimize",
    )(rates, grads, master, first, second)


def fast_body(
    frames,
    lengths,
    key_mask,
    cotangent,
    gain_one,
    shift_one,
    query_weight,
    query_bias,
    key_weight,
    value_weight,
    value_bias,
    out_weight,
    out_bias,
    gain_two,
    shift_two,
    up_weight,
    up_bias,
    down_weight,
    down_bias,
    master,
    moment_one,
    moment_two,
    adam_step,
    hyper_rates,
):
    group = lax.axis_index("dp")
    position = jnp.arange(1024, dtype=jnp.int32)
    keep_query = position[None, :] < lengths[:, None]
    keep_key = jnp.logical_and(keep_query, key_mask == 1)
    mask = jnp.where(keep_key, 0.0, MASK_VALUE)[:, :, None]
    live = keep_query.astype(F32)[:, None, :]
    gain_first = gain_one.astype(F32)
    shift_first = shift_one.astype(F32)
    gain_second = gain_two.astype(F32)
    shift_second = shift_two.astype(F32)
    inputs = frames.transpose(1, 0, 2).reshape(ROWS, 1280).astype(F32)
    upstream_low = cotangent.transpose(1, 0, 2).reshape(ROWS, 1280)
    upstream = upstream_low.astype(F32)
    def head_lanes(bias):
        lanes = bias.astype(F32).reshape(2, HD)
        return jnp.pad(lanes, ((0, 0), (0, 128 - HD))).reshape(256)

    joined_bias = jnp.concatenate(
        [head_lanes(query_bias), jnp.zeros((256,), F32), head_lanes(value_bias)]
    )[None]
    frame_rows = frames.transpose(1, 0, 2).reshape(ROWS, 1280)
    normed_full, qkv, upstream_full, joined_weight = project(
        frame_rows,
        gain_first[None],
        shift_first[None],
        upstream_low,
        query_weight.T,
        key_weight.T,
        value_weight.T,
        joined_bias,
    )
    qkv = qkv.reshape(8, 3, 128, 768)

    quarter = group * 160
    up_share = lax.dynamic_slice_in_dim(up_weight, quarter, 160, 1).T
    down_share = lax.dynamic_slice_in_dim(down_weight, quarter, 160, 0)
    bias_share = lax.dynamic_slice_in_dim(up_bias, quarter, 160, 0)
    bias_rows = jnp.pad(bias_share[None], ((0, 15), (0, 1280 - 160)))
    message = jnp.concatenate([up_share, bias_rows])
    outer = jnp.pad(lax.dynamic_slice_in_dim(out_weight, group * 40, 40, 0), ((0, 8), (0, 0)))
    attended, logs, peaks, gathered, outer_all = attend(qkv, mask, live, message, outer)
    up_lanes = gathered[:, 160, :160].reshape(1, 640).astype(F32)
    out_rows = outer_all.reshape(4, 2, 4, 48, 1280)[:, :, :, :40]
    out_rows = out_rows.transpose(2, 1, 0, 3, 4).reshape(8, 160, 1280)

    branch = jnp.einsum("schr,shd->crd", attended, out_rows, preferred_element_type=F32)
    middle = inputs + branch.reshape(ROWS, 1280) + out_bias.astype(F32)
    normed_two = layer_norm(middle, gain_second, shift_second).astype(BF)
    normed_two_grad, hidden, feed_grads, _, down_all = feed_forward(
        normed_two, upstream_full, gathered, down_share, up_lanes
    )

    _, norm_two_pull = jax.vjp(layer_norm, middle, gain_second, shift_second)
    middle_norm_grad, gain_two_grad, shift_two_grad = norm_two_pull(normed_two_grad)
    middle_grad = upstream + middle_norm_grad
    branch_grad = middle_grad.astype(BF)
    branch_clips = branch_grad.reshape(3, 128, 1280)
    out_grad = jnp.einsum("schr,crd->shd", attended, branch_clips, preferred_element_type=F32)
    attended_grad = jnp.einsum(
        "shd,crd->schr", out_rows, branch_clips, preferred_element_type=F32
    ).astype(BF)
    out_quarters = jnp.pad(
        out_grad.astype(BF).reshape(4, 2, 4, 40, 1280), ((0, 0),) * 3 + ((0, 8), (0, 0))
    )
    out_quarters = out_quarters.transpose(2, 1, 0, 3, 4).reshape(4, 2, 192, 1280)
    joined_grad, feed, feed_sum, out_sum = attend_back(
        qkv, mask, logs, attended_grad, hidden, down_all, feed_grads, out_quarters
    )
    layer_out = (middle + feed + down_bias.astype(F32)).astype(BF)
    joined_grad = joined_grad.reshape(8, ROWS, 768)
    joined_weight_grad = jnp.einsum(
        "prd,pre->de", normed_full, joined_grad, preferred_element_type=F32
    )
    joined_bias_grad = jnp.sum(joined_grad.astype(F32), axis=(0, 1))

    level = lax.axis_index("mp") // 2
    up_bias_share = lax.dynamic_slice_in_dim(feed_sum[320], level * 160, 160, 0)
    up_bias_rows = lax.dynamic_update_slice(
        jnp.zeros((640,), F32), up_bias_share, (quarter,)
    ).reshape(5, 128)
    small_rows = jnp.concatenate(
        [
            jnp.sum(branch_grad.astype(F32), axis=0),
            gain_two_grad,
            shift_two_grad,
            jnp.sum(upstream, axis=0),
            jnp.zeros((512,), F32),
        ]
    ).reshape(44, 128)
    first_grad, grad_rows, small_sum, peak_sum = finish(
        joined_grad,
        joined_weight,
        joined_weight_grad,
        joined_bias_grad,
        feed_sum,
        out_sum,
        up_bias_rows,
        small_rows,
        peaks,
        frame_rows,
        middle_grad,
        gain_first[None],
        shift_first[None],
    )
    small_total = small_sum.reshape(1024)[:960]
    head_peak = jnp.max(peak_sum, axis=(1, 2)) / math.sqrt(HD)
    learn_rate = hyper_rates[0]
    weight_decay = hyper_rates[1]
    logit_cap = hyper_rates[2]
    step_count = adam_step[0].astype(F32)
    root_factor = jnp.sqrt(logit_cap / jnp.maximum(head_peak, logit_cap))
    root_factor = jnp.where(group == 0, root_factor, 1.0)
    rates = jnp.stack(
        [
            learn_rate / (1.0 - jnp.power(BETA_FIRST, step_count)),
            1.0 / (1.0 - jnp.power(BETA_SECOND, step_count)),
            1.0 - learn_rate * weight_decay,
            root_factor[0],
            root_factor[1],
        ]
    )
    owned_grads, master_new, first_new, second_new, padded = optimize(
        rates, grad_rows.reshape(1, SHARE_ROWS * 128), master, moment_one, moment_two
    )
    whole, second_grad = share_master(
        padded.reshape(SHARE_ROWS, 128),
        joined_grad,
        joined_weight,
        frame_rows,
        middle_grad,
        gain_first[None],
    )
    input_grad = jnp.concatenate([first_grad, second_grad])
    whole = lax.optimization_barrier(whole.reshape(1, PACK_END * 128))
    weights_new = whole[:, : 4 * SHARE_ENTRIES].astype(BF)
    return (
        layer_out.reshape(3, 128, 1280).transpose(1, 0, 2),
        input_grad.reshape(3, 128, 1280).transpose(1, 0, 2),
        owned_grads,
        master_new,
        first_new,
        second_new,
        weights_new,
        small_total,
    )


def body(
    frames,
    lengths,
    key_mask,
    cotangent,
    gain_one,
    shift_one,
    query_weight,
    query_bias,
    key_weight,
    value_weight,
    value_bias,
    out_weight,
    out_bias,
    gain_two,
    shift_two,
    up_weight,
    up_bias,
    down_weight,
    down_bias,
    master,
    moment_one,
    moment_two,
    adam_step,
    hyper_rates,
):
    local_rows, clip_count, model_width = frames.shape
    total_rows = key_mask.shape[1]
    head_cols = query_weight.shape[1]
    heads_here = head_cols // HD
    block_rows = min(512, total_rows)
    blocks = total_rows // block_rows
    score_scale = 1.0 / math.sqrt(HD)
    position = jnp.arange(total_rows, dtype=jnp.int32)
    keep_query = position[None, :] < lengths[:, None]
    keep_key = jnp.logical_and(keep_query, key_mask == 1)
    gain_first = gain_one.astype(jnp.float32)
    shift_first = shift_one.astype(jnp.float32)
    gain_second = gain_two.astype(jnp.float32)
    shift_second = shift_two.astype(jnp.float32)
    inputs = frames.astype(jnp.float32)
    normed = layer_norm(inputs, gain_first, shift_first).astype(jnp.bfloat16)
    joined_weight = jnp.concatenate([query_weight, key_weight, value_weight], axis=1)
    joined_bias = jnp.concatenate(
        [
            query_bias.astype(jnp.float32),
            jnp.zeros((head_cols,), jnp.float32),
            value_bias.astype(jnp.float32),
        ]
    )
    normed_full = lax.all_gather(normed, "mp", axis=0, tiled=True)
    projected = (
        jnp.einsum("rcd,de->rce", normed_full, joined_weight, preferred_element_type=jnp.float32)
        + joined_bias
    ).astype(jnp.bfloat16)
    query = projected[:, :, :head_cols].reshape(total_rows, clip_count, heads_here, HD)
    keys = projected[:, :, head_cols : 2 * head_cols].reshape(
        total_rows, clip_count, heads_here, HD
    )
    values = projected[:, :, 2 * head_cols :].reshape(total_rows, clip_count, heads_here, HD)

    def scores_of(row_start):
        query_block = lax.dynamic_slice_in_dim(query, row_start, block_rows, 0)
        raw_scores = (
            jnp.einsum("qchd,kchd->chqk", query_block, keys, preferred_element_type=jnp.float32)
            * score_scale
        )
        return (query_block, jnp.where(keep_key[:, None, None, :], raw_scores, MASK_VALUE))

    def forward_block(block_index):
        row_start = block_index * block_rows
        _, masked = scores_of(row_start)
        row_peak = jnp.max(masked, axis=-1, keepdims=True)
        exp_scores = jnp.exp(masked - row_peak)
        row_total = jnp.sum(exp_scores, axis=-1, keepdims=True)
        probability = (exp_scores / row_total).astype(jnp.bfloat16)
        attended = jnp.einsum(
            "chqk,kchd->qchd", probability, values, preferred_element_type=jnp.float32
        ).astype(jnp.bfloat16)
        live_rows = lax.dynamic_slice_in_dim(keep_query, row_start, block_rows, 1)
        block_peak = jnp.max(
            jnp.where(live_rows[:, None, :], row_peak[..., 0], MASK_VALUE), axis=(0, 2)
        )
        return (attended, (row_peak + jnp.log(row_total))[..., 0], block_peak)

    attended_blocks, log_totals, block_peaks = lax.map(forward_block, jnp.arange(blocks))
    attended_full = attended_blocks.reshape(total_rows, clip_count, head_cols)
    head_peak = lax.pmax(jnp.max(block_peaks, axis=0), "dp")
    rows_here = attended_full
    attn_branch = lax.psum_scatter(
        jnp.einsum("rck,kd->rcd", rows_here, out_weight, preferred_element_type=jnp.float32),
        "mp",
        scatter_dimension=0,
        tiled=True,
    ) + out_bias.astype(jnp.float32)
    middle = inputs + attn_branch
    normed_two = layer_norm(middle, gain_second, shift_second).astype(jnp.bfloat16)
    upstream = cotangent.astype(jnp.float32)
    normed_two_full = lax.all_gather(normed_two, "mp", axis=0, tiled=True)
    before = jnp.einsum(
        "rcd,df->rcf", normed_two_full, up_weight, preferred_element_type=jnp.float32
    ) + up_bias.astype(jnp.float32)
    hidden = exact_gelu(before).astype(jnp.bfloat16)
    rows_here = hidden
    feed = lax.psum_scatter(
        jnp.einsum(
            "rcf,fd->rcd", rows_here, down_weight, preferred_element_type=jnp.float32
        ).astype(jnp.bfloat16),
        "mp",
        scatter_dimension=0,
        tiled=True,
    ).astype(jnp.float32) + down_bias.astype(jnp.float32)
    layer_out = (middle + feed).astype(jnp.bfloat16)
    feed_grad_full = lax.all_gather(cotangent, "mp", axis=0, tiled=True)
    down_grad = jnp.einsum(
        "rcf,rcd->fd", hidden, feed_grad_full, preferred_element_type=jnp.float32
    )
    hidden_grad = jnp.einsum(
        "rcd,fd->rcf", feed_grad_full, down_weight, preferred_element_type=jnp.float32
    )
    _, gelu_pull = jax.vjp(exact_gelu, before)
    before_grad = gelu_pull(hidden_grad)[0].astype(jnp.bfloat16)
    up_bias_grad = jnp.sum(before_grad.astype(jnp.float32), axis=(0, 1))
    up_grad = jnp.einsum(
        "rcd,rcf->df", normed_two_full, before_grad, preferred_element_type=jnp.float32
    )
    rows_here = before_grad
    normed_two_grad = lax.psum_scatter(
        jnp.einsum("rcf,df->rcd", rows_here, up_weight, preferred_element_type=jnp.float32),
        "mp",
        scatter_dimension=0,
        tiled=True,
    )
    _, norm_two_pull = jax.vjp(layer_norm, middle, gain_second, shift_second)
    middle_norm_grad, gain_two_grad, shift_two_grad = norm_two_pull(normed_two_grad)
    middle_grad = upstream + middle_norm_grad
    branch_grad = middle_grad.astype(jnp.bfloat16)
    branch_grad_full = lax.all_gather(branch_grad, "mp", axis=0, tiled=True)
    out_grad = jnp.einsum(
        "rck,rcd->kd", attended_full, branch_grad_full, preferred_element_type=jnp.float32
    )
    attended_grad = jnp.einsum(
        "rcd,kd->rck", branch_grad_full, out_weight, preferred_element_type=jnp.float32
    ).astype(jnp.bfloat16)
    attended_grad = attended_grad.reshape(total_rows, clip_count, heads_here, HD)

    def backward_block(carry, block_index):
        key_total, value_total = carry
        row_start = block_index * block_rows
        query_block, masked = scores_of(row_start)
        log_total = log_totals[block_index]
        probability = jnp.exp(masked - log_total[..., None])
        grad_block = lax.dynamic_slice_in_dim(attended_grad, row_start, block_rows, 0)
        value_total = value_total + jnp.einsum(
            "chqk,qchd->kchd",
            probability.astype(jnp.bfloat16),
            grad_block,
            preferred_element_type=jnp.float32,
        )
        prob_grad = jnp.einsum(
            "qchd,kchd->chqk", grad_block, values, preferred_element_type=jnp.float32
        )
        score_grad = (
            probability * (prob_grad - jnp.sum(probability * prob_grad, axis=-1, keepdims=True))
        ).astype(jnp.bfloat16)
        query_grad = (
            jnp.einsum("chqk,kchd->qchd", score_grad, keys, preferred_element_type=jnp.float32)
            * score_scale
        ).astype(jnp.bfloat16)
        key_total = (
            key_total
            + jnp.einsum(
                "chqk,qchd->kchd", score_grad, query_block, preferred_element_type=jnp.float32
            )
            * score_scale
        )
        return ((key_total, value_total), query_grad)

    empty_grad = jnp.zeros((total_rows, clip_count, heads_here, HD), jnp.float32)
    (key_total, value_total), query_blocks = lax.scan(
        backward_block, (empty_grad, empty_grad), jnp.arange(blocks)
    )
    joined_grad = jnp.concatenate(
        [
            query_blocks.reshape(total_rows, clip_count, head_cols),
            key_total.reshape(total_rows, clip_count, head_cols).astype(jnp.bfloat16),
            value_total.reshape(total_rows, clip_count, head_cols).astype(jnp.bfloat16),
        ],
        axis=-1,
    )
    joined_bias_grad = jnp.sum(joined_grad.astype(jnp.float32), axis=(0, 1))
    normed_back = lax.all_gather(normed, "mp", axis=0, tiled=True)
    joined_weight_grad = jnp.einsum(
        "rcd,rce->de", normed_back, joined_grad, preferred_element_type=jnp.float32
    )
    rows_here = joined_grad
    normed_grad = lax.psum_scatter(
        jnp.einsum(
            "rce,de->rcd", rows_here, joined_weight, preferred_element_type=jnp.float32
        ).astype(jnp.bfloat16),
        "mp",
        scatter_dimension=0,
        tiled=True,
    ).astype(jnp.float32)
    _, norm_one_pull = jax.vjp(layer_norm, inputs, gain_first, shift_first)
    input_norm_grad, gain_one_grad, shift_one_grad = norm_one_pull(normed_grad)
    input_grad = middle_grad + input_norm_grad
    out_bias_grad = jnp.sum(branch_grad.astype(jnp.float32), axis=(0, 1))
    down_bias_grad = jnp.sum(upstream, axis=(0, 1))
    small_terms = jnp.concatenate(
        [
            gain_one_grad,
            shift_one_grad,
            out_bias_grad,
            gain_two_grad,
            shift_two_grad,
            down_bias_grad,
        ]
    )
    small_share = lax.psum_scatter(small_terms, "mp", scatter_dimension=0, tiled=True)
    small_total = lax.psum(small_share, "dp")
    packed = jnp.concatenate(
        [
            joined_weight_grad[:, :head_cols].reshape(-1),
            joined_bias_grad[:head_cols],
            joined_weight_grad[:, head_cols : 2 * head_cols].reshape(-1),
            joined_weight_grad[:, 2 * head_cols :].reshape(-1),
            joined_bias_grad[2 * head_cols :],
            out_grad.reshape(-1),
            up_grad.reshape(-1),
            up_bias_grad,
            down_grad.reshape(-1),
            small_share,
        ]
    )
    owned_grads = lax.psum_scatter(
        packed.astype(jnp.bfloat16), "dp", scatter_dimension=0, tiled=True
    ).astype(jnp.float32)
    share_size = owned_grads.shape[0]
    learn_rate = hyper_rates[0]
    weight_decay = hyper_rates[1]
    logit_cap = hyper_rates[2]
    step_count = adam_step[0].astype(jnp.float32)
    first_new = BETA_FIRST * moment_one[0] + (1.0 - BETA_FIRST) * owned_grads
    second_new = BETA_SECOND * moment_two[0] + (1.0 - BETA_SECOND) * owned_grads * owned_grads
    first_hat = first_new / (1.0 - jnp.power(BETA_FIRST, step_count))
    second_hat = second_new / (1.0 - jnp.power(BETA_SECOND, step_count))
    entry_index = lax.axis_index("dp") * share_size + jnp.arange(share_size, dtype=jnp.int32)
    query_end = model_width * head_cols
    query_bias_end = query_end + head_cols
    key_end = query_bias_end + model_width * head_cols
    column = jnp.where(
        entry_index < query_end,
        entry_index % head_cols,
        jnp.where(
            entry_index < query_bias_end,
            entry_index - query_end,
            (entry_index - query_bias_end) % head_cols,
        ),
    )
    head_index = column // HD
    root_factor = jnp.sqrt(logit_cap / jnp.maximum(head_peak, logit_cap))
    head_factor = jnp.zeros((share_size,), jnp.float32)
    for head_number in range(heads_here):
        head_factor = head_factor + jnp.where(
            head_index == head_number, root_factor[head_number], 0.0
        )
    factor = jnp.where(entry_index < key_end, head_factor, 1.0)
    master_here = master[0]
    master_new = (
        master_here
        - learn_rate
        * (first_hat / (jnp.sqrt(second_hat) + ADAM_EPSILON) + weight_decay * master_here)
    ) * factor
    weights_full = lax.all_gather(master_new.astype(jnp.bfloat16), "dp", axis=0, tiled=True)
    return (
        layer_out,
        input_grad,
        owned_grads[None],
        master_new[None],
        first_new[None],
        second_new[None],
        weights_full[None],
        small_total,
    )


def solution(mesh):
    chosen = fast_body if dict(mesh.shape) == {"dp": 4, "mp": 8} else body
    placed = (
        P("mp", "dp", None),
        P("dp"),
        P("dp", None),
        P("mp", "dp", None),
        P(),
        P(),
        P(None, "mp"),
        P("mp"),
        P(None, "mp"),
        P(None, "mp"),
        P("mp"),
        P("mp", None),
        P(),
        P(),
        P(),
        P(None, "mp"),
        P("mp"),
        P("mp", None),
        P(),
        P("mp", "dp"),
        P("mp", "dp"),
        P("mp", "dp"),
        P(),
        P(),
    )
    return jax.shard_map(
        chosen,
        mesh=mesh,
        in_specs=placed,
        out_specs=(
            P("mp", "dp", None),
            P("mp", "dp", None),
            P("mp", "dp"),
            P("mp", "dp"),
            P("mp", "dp"),
            P("mp", "dp"),
            P("mp", None),
            P("mp"),
        ),
        check_vma=False,
    )
```

```python
import functools
import math

import jax
import jax.numpy as jnp
from jax import lax
from jax.experimental import pallas as pl
from jax.experimental.pallas import tpu as pltpu
from jax.sharding import PartitionSpec as P

HD = 80


NORM_EPSILON = 1e-05
ADAM_EPSILON = 1e-08
BETA_FIRST = 0.9
BETA_SECOND = 0.999
MASK_VALUE = -1e30


def layer_norm(value, gain, shift):
    center = value - jnp.mean(value, axis=-1, keepdims=True)
    spread = jnp.mean(center * center, axis=-1, keepdims=True)
    return center * lax.rsqrt(spread + NORM_EPSILON) * gain + shift


def exact_gelu(argument):
    return jax.nn.gelu(argument, approximate=False)


MESH = pl.DeviceIdType.MESH
ANY = pl.BlockSpec(memory_space=pl.ANY)
VMEM = pl.BlockSpec(memory_space=pltpu.VMEM)
LINE = 4
ROWS = 384
BF = jnp.bfloat16
F32 = jnp.float32


class Place:
    def __init__(self):
        self.dp = lax.axis_index("dp")
        self.mp = lax.axis_index("mp")
        self.z = self.mp // 2
        self.c = self.mp % 2
        self.pair = self.z * 2 + 1 - self.c
        self.dpx = self.dp + 1 - 2 * (self.dp % 2)
        self.dpy = (self.dp + 2) % 4
        self.dpd = 3 - self.dp

    def zorder(self, event):
        if event == 0:
            return self.z
        if event == 1:
            return self.z + 1 - 2 * (self.z % 2)
        if event == 2:
            return 2 - self.z // 2
        return 3 - 3 * (self.z // 2)


def greet(place, mp_all=False, line=False, plane=False, pair=True):
    barrier = pltpu.get_barrier_semaphore()
    count = 0

    def signal(dp, mp):
        pl.semaphore_signal(barrier, inc=1, device_id=(dp, mp), device_id_type=MESH)

    if mp_all:
        for hop in range(1, 8):
            signal(place.dp, (place.mp + hop) % 8)
        count += 7
    else:
        if pair:
            signal(place.dp, place.pair)
            count += 1
        if line:

            @pl.when(place.z > 0)
            def _():
                signal(place.dp, place.mp - 2)

            @pl.when(place.z < LINE - 1)
            def _():
                signal(place.dp, place.mp + 2)

    if plane:
        for other in (place.dpx, place.dpy, place.dpd):
            signal(other, place.mp)
        count += 3
    if line and not mp_all:
        pl.semaphore_wait(barrier, count + 1 + (place.z + 1) // 2 % 2)
    else:
        pl.semaphore_wait(barrier, count)


def remote(src, dst, send, recv, dp, mp):
    return pltpu.make_async_remote_copy(
        src_ref=src,
        dst_ref=dst,
        send_sem=send,
        recv_sem=recv,
        device_id=(dp, mp),
        device_id_type=MESH,
    )


def line_gather(place, src, out, local, send, recv, paired, ready=None, rows=None):
    dp, z, c, mp, pair = place.dp, place.z, place.c, place.mp, place.pair

    def at(slot):
        if rows is None:
            return out.at[slot]
        return out.at[pl.ds(pl.multiple_of(slot * rows, 16), rows)]

    def slot_of(level, core):
        return level * 2 + core if paired else level

    def hop(event, slot, source, direction, target):
        return remote(source, at(slot), send.at[event, direction], recv.at[slot], dp, target)

    own = slot_of(z, c)
    keep = pltpu.make_async_copy(src, at(own), local)
    keep.start()

    def ways(event, level, slot, source, act):
        up = z < LINE - 1
        down = z > 0
        if event > 0:
            up = jnp.logical_and(up, level < z)
            down = jnp.logical_and(down, level > z)

        @pl.when(up)
        def _():
            act(hop(event, slot, source, 1, mp + 2))

        @pl.when(down)
        def _():
            act(hop(event, slot, source, 2, mp - 2))

        if paired:
            act(hop(event, slot, source, 0, pair))

    ways(0, z, own, src, lambda copy: copy.start())
    yield
    if ready is not None:
        keep.wait()
        ready(own)
        if paired:
            other = slot_of(z, 1 - c)
            hop(0, other, at(other), 0, pair).wait_recv()
            ready(other)

    def settle(event):
        level = place.zorder(event)
        ready(slot_of(level, c))
        if paired:
            other = slot_of(level, 1 - c)
            hop(event, other, at(other), 0, pair).wait_recv()
            ready(other)

    for event in range(1, LINE):
        level = place.zorder(event)
        slot = slot_of(level, c)
        hop(event, slot, at(slot), 0, pair).wait_recv()
        ways(event, level, slot, at(slot), lambda copy: copy.start())
        if ready is not None and event > 1:
            if event == 2:
                settle(1)
            settle(event)
        yield
    if ready is None:
        if paired:
            for level in range(LINE):
                other = slot_of(level, 1 - c)
                hop(0, other, at(other), 0, pair).wait_recv()
        keep.wait()
    for event in range(LINE):
        level = place.zorder(event)
        slot = slot_of(level, c)
        ways(event, level, slot, at(slot), lambda copy: copy.wait_send())
    yield


def plane_gather(place, src, out, local, send, recv, ready=None, primed=False):
    dp, c, mp, pair = place.dp, place.c, place.mp, place.pair
    dpx, dpy, dpd = place.dpx, place.dpy, place.dpd
    half = src.shape[0] // 2
    part_a, part_b = pl.ds(0, half), pl.ds(half, half)

    def at(group, core):
        return out.at[group * 2 + core]

    def hop(index, block, group, target):
        return remote(block, block, send.at[index], recv.at[index], group, target)

    def done(group, core):
        if ready is not None:
            ready(group * 2 + core)

    keep = pltpu.make_async_copy(src, at(dp, c), local)
    here = at(dp, c)
    from_x, from_y, from_d = at(dpx, c), at(dpy, c), at(dpd, c)
    firsts = [
        remote(src, here, send.at[0], recv.at[0], dp, pair),
        remote(src, here, send.at[1], recv.at[1], dpx, mp),
        remote(src, here, send.at[2], recv.at[2], dpy, mp),
    ]
    seconds = [
        hop(3, from_x.at[part_a], dpy, mp),
        hop(4, from_y.at[part_b], dpx, mp),
        hop(5, from_x, dp, pair),
        hop(6, from_y, dp, pair),
        hop(7, from_d.at[part_a], dp, pair),
        hop(8, from_d.at[part_b], dp, pair),
    ]
    if primed:
        yield
    keep.start()
    for copy in firsts:
        copy.start()
    yield
    if ready is not None:
        keep.wait()
        done(dp, c)
        hop(0, at(dp, 1 - c), dp, pair).wait_recv()
        done(dp, 1 - c)
    hop(1, from_x, dpx, mp).wait_recv()
    seconds[0].start()
    hop(2, from_y, dpy, mp).wait_recv()
    seconds[1].start()
    seconds[2].start()
    seconds[3].start()
    yield
    done(dpx, c)
    hop(5, at(dpx, 1 - c), dp, pair).wait_recv()
    done(dpx, 1 - c)
    if ready is not None:
        yield
    done(dpy, c)
    hop(6, at(dpy, 1 - c), dp, pair).wait_recv()
    done(dpy, 1 - c)
    if ready is not None:
        yield
    hop(3, from_d.at[part_a], dpy, mp).wait_recv()
    seconds[4].start()
    hop(4, from_d.at[part_b], dpx, mp).wait_recv()
    seconds[5].start()
    done(dpd, c)
    other = at(dpd, 1 - c)
    hop(7, other.at[part_a], dp, pair).wait_recv()
    hop(8, other.at[part_b], dp, pair).wait_recv()
    done(dpd, 1 - c)
    yield
    if ready is None:
        hop(0, at(dp, 1 - c), dp, pair).wait_recv()
        keep.wait()
    for copy in firsts + seconds:
        copy.wait_send()
    yield


def drive(*programs):
    live = list(programs)
    while live:
        for program in list(live):
            try:
                next(program)
            except StopIteration:
                live.remove(program)


def dma(*shape):
    return pltpu.SemaphoreType.DMA(shape)


def params(cid, vmem=40):
    return pltpu.CompilerParams(
        collective_id=cid, has_side_effects=True, vmem_limit_bytes=vmem << 20
    )


def exchange(place, src, out, local, send, recv):
    dp, mp = place.dp, place.mp
    keep = pltpu.make_async_copy(src.at[mp], out.at[mp], local)
    keep.start()
    sends = []
    for hop in range(1, 8):
        target = (mp + hop) % 8
        sends.append(
            remote(src.at[target], out.at[mp], send.at[hop], recv.at[hop], dp, target)
        )
        sends[-1].start()
    yield
    keep.wait()
    for hop in range(1, 8):
        origin = (mp + 8 - hop) % 8
        remote(out.at[origin], out.at[origin], send.at[hop], recv.at[hop], dp, origin).wait_recv()
    for copy in sends:
        copy.wait_send()
    yield


def line_reduce(place, produce, tiles, result, bufs, sems, paired):
    dp, z, c, mp, pair = place.dp, place.z, place.c, place.mp, place.pair
    above_block, below_block, out_block = bufs["above"], bufs["below"], bufs["out"]
    order = [place.zorder(event) for event in (3, 2, 1, 0)]
    inner = jnp.logical_and(z > 0, z < LINE - 1)
    outer = jnp.logical_or(z == 0, z == LINE - 1)

    @pl.when(z == LINE - 1)
    def _():
        above_block[...] = jnp.zeros(above_block.shape, BF)

    @pl.when(z == 0)
    def _():
        below_block[...] = jnp.zeros(below_block.shape, BF)

    def from_above(level):
        return above_block.at[jnp.minimum(level, LINE - 2)]

    def from_below(level):
        return below_block.at[jnp.maximum(level - 1, 0)]

    def across(step, level):
        return remote(
            bufs["pair_out"].at[step % 2],
            bufs["pair_in"].at[level],
            sems["pair_send"].at[step % 2],
            sems["pair_recv"].at[level],
            dp,
            pair,
        )

    if paired:
        for step, level in enumerate(order):
            if step > 1:
                across(step - 2, order[step - 2]).wait_send()
            for rows in tiles:
                bufs["pair_out"][step % 2, rows] = produce(level, 1 - c, rows).astype(BF)
            across(step, level).start()
    yield

    def toward(step, level, act):
        @pl.when(level < z)
        def _():
            act(
                remote(
                    out_block.at[step],
                    from_above(level),
                    sems["line_send"].at[step],
                    sems["above"].at[level],
                    dp,
                    mp - 2,
                )
            )

        @pl.when(level > z)
        def _():
            act(
                remote(
                    out_block.at[step],
                    from_below(level),
                    sems["line_send"].at[step],
                    sems["below"].at[level],
                    dp,
                    mp + 2,
                )
            )

    def arrive(level, above):
        if above:
            remote(
                from_above(level),
                from_above(level),
                sems["line_send"].at[0],
                sems["above"].at[level],
                dp,
                mp,
            ).wait_recv()
        else:
            remote(
                from_below(level),
                from_below(level),
                sems["line_send"].at[0],
                sems["below"].at[level],
                dp,
                mp,
            ).wait_recv()

    def advance(step):
        level = order[step]
        if paired:
            across(step, level).wait_recv()

        @pl.when(jnp.logical_and(level < z, z < LINE - 1))
        def _():
            arrive(level, True)

        @pl.when(jnp.logical_and(level > z, z > 0))
        def _():
            arrive(level, False)

        for rows in tiles:
            total = produce(level, c, rows)
            if paired:
                total = total + bufs["pair_in"][level, rows].astype(F32)

            @pl.when(level < z)
            def _():
                out_block[step, rows] = (total + from_above(level)[rows].astype(F32)).astype(BF)

            @pl.when(level > z)
            def _():
                out_block[step, rows] = (total + from_below(level)[rows].astype(F32)).astype(BF)

        toward(step, level, lambda copy: copy.start())

    advance(0)
    for step in (1, 2):

        @pl.when(outer)
        def _():
            advance(step)

    yield
    for step in (1, 2):

        @pl.when(inner)
        def _():
            advance(step)

        yield

    if paired:
        across(3, z).wait_recv()

    @pl.when(z < LINE - 1)
    def _():
        arrive(z, True)

    @pl.when(z > 0)
    def _():
        arrive(z, False)

    for rows in tiles:
        total = produce(z, c, rows)
        if paired:
            total = total + bufs["pair_in"][z, rows].astype(F32)
        total = total + from_above(z)[rows].astype(F32) + from_below(z)[rows].astype(F32)
        result(rows, total)
    for step, level in enumerate(order):
        if paired and step > 1:
            across(step, level).wait_send()
        if step < 3:
            toward(step, level, lambda copy: copy.wait_send())
    yield


def line_reduce_scratch(rows, cols, paired):
    block = lambda n: pltpu.VMEM((n, rows, cols), BF)
    scratch = {"above": block(3), "below": block(3), "out": block(3)}
    sems = {"line_send": dma(3), "above": dma(4), "below": dma(4)}
    if paired:
        scratch.update({"pair_out": block(2), "pair_in": block(4)})
        sems.update({"pair_send": dma(2), "pair_recv": dma(4)})
    return scratch, sems


def plane_reduce(place, produce, tile, half, result, bufs, sems, paired=True, early=False):
    dp, c, mp, pair = place.dp, place.c, place.mp, place.pair
    dpx, dpy, dpd = place.dpx, place.dpy, place.dpd
    starts = range(0, half, tile)
    send, recv = sems["send"], sems["recv"]
    out_block, landed = bufs["out"], bufs["in"]
    groups = {"far": dpd, "x": dpx, "y": dpy, "own": dp}
    steps = ["x", "y", "far", "own"] if early else ["far", "x", "y", "own"]

    def across(name):
        step = steps.index(name)
        return remote(
            bufs["pair_out"].at[step % 2],
            bufs["pair_in"].at[step],
            sems["pair_send"].at[step % 2],
            sems["pair_recv"].at[step],
            dp,
            pair,
        )

    def cross(name):
        if not paired:
            return
        step = steps.index(name)
        if step > 1:
            across(steps[step - 2]).wait_send()
        bufs["pair_out"][step % 2] = produce(groups[name], 1 - c, 0, 2 * half).astype(BF)
        across(name).start()

    def crossed(name):
        if paired:
            across(name).wait_recv()

    def share(name, start):
        total = produce(groups[name], c, start, tile)
        if paired:
            total = total + bufs["pair_in"][steps.index(name), pl.ds(start, tile)].astype(F32)
        return total

    def hop(index):
        target = (dpx, dpy, dpx, dpx, dpy, dpy)[index]
        return remote(
            out_block.at[index], landed.at[index], send.at[index], recv.at[index], target, mp
        )

    def fill(index, name, base, extra=None):
        for start in starts:
            total = share(name, base + start)
            if extra is not None:
                total = total + landed[extra, pl.ds(start, tile)].astype(F32)
            out_block[index, pl.ds(start, tile)] = total.astype(BF)
        hop(index).start()

    def far():
        crossed("far")
        fill(0, "far", 0)
        fill(1, "far", half)

    def near():
        crossed("x")
        fill(2, "x", 0)
        crossed("y")
        fill(4, "y", half)

    if early:
        cross("x")
        yield
        cross("y")
        near()
        yield
        cross("far")
        far()
        yield
        cross("own")
    else:
        cross("far")
        cross("x")
        yield
        far()
        cross("y")
        near()
        cross("own")
    yield
    hop(1).wait_recv()
    fill(3, "x", half, extra=1)
    hop(0).wait_recv()
    fill(5, "y", 0, extra=0)
    yield
    crossed("own")
    for index in (2, 3, 4, 5):
        hop(index).wait_recv()
    for base, pieces in ((0, (2, 5)), (half, (3, 4))):
        for start in starts:
            total = share("own", base + start)
            for piece in pieces:
                total = total + landed[piece, pl.ds(start, tile)].astype(F32)
            result(pl.ds(base + start, tile), total)
    for index in range(6):
        hop(index).wait_send()
    if paired:
        for name in steps[2:]:
            across(name).wait_send()
    yield


def plane_reduce_scratch(half, cols, paired=True):
    block = lambda n, rows: pltpu.VMEM((n, rows, cols), BF)
    scratch = {"out": block(6, half), "in": block(6, half)}
    sems = {"send": dma(6), "recv": dma(6)}
    if paired:
        scratch.update({"pair_out": block(2, 2 * half), "pair_in": block(4, 2 * half)})
        sems.update({"pair_send": dma(2), "pair_recv": dma(4)})
    return scratch, sems


OUTER_STARTS = (0, 48, 96, 112)


def attention_kernel(
    frames_ref, gain_ref, shift_ref, cot_ref, query_ref, key_ref, value_ref, bias_ref,
    mask_ref, live_ref, weights_ref, outer_ref, out_bias_ref, gain_two_ref, shift_two_ref,
    nfull_ref, qkv_ref, cfull_ref, weight_ref, att_ref, logs_ref, peak_ref, wfull_ref,
    rows_ref, middle_ref, two_ref,
    normed_ref, out_ref, vt_ref, outer_all, outer_full,
    local, first_send, first_recv, cot_send, cot_recv, send, recv, line_send, line_recv,
    outer_send, outer_recv, plane_send, plane_recv,
):
    place = Place()
    weight_ref[...] = jnp.zeros(weight_ref.shape, BF)
    for index, ref in enumerate((query_ref, key_ref, value_ref)):
        for head in range(2):
            weight_ref[pl.ds(index * 256 + head * 128, HD)] = ref[pl.ds(head * HD, HD)]
    for start in range(0, ROWS, 128):
        rows = pl.ds(start, 128)
        normed_ref[rows] = layer_norm(
            frames_ref[rows].astype(F32), gain_ref[...], shift_ref[...]
        ).astype(BF)
    greet(place, mp_all=True, plane=True)

    def ready(slot):
        product = lax.dot_general(
            nfull_ref[slot],
            weight_ref[...],
            (((1,), (1,)), ((), ())),
            preferred_element_type=F32,
        )
        qkv_ref[slot] = (product + bias_ref[...]).astype(BF).reshape(3, 128, 768)

    drive(
        line_gather(
            place, normed_ref, nfull_ref, local.at[4], first_send, first_recv, True, ready
        ),
        plane_gather(place, cot_ref, cfull_ref, local.at[5], cot_send, cot_recv),
    )
    outer = line_gather(
        place, outer_ref, outer_all, local.at[2], outer_send, outer_recv, False, None, 48
    )
    next(outer)
    gather = line_gather(
        place, weights_ref, wfull_ref, local.at[1], line_send, line_recv, False
    )
    next(gather)
    factor = math.log2(math.e) / math.sqrt(HD)
    peak_ref[...] = jnp.full(peak_ref.shape, MASK_VALUE, F32)

    @pl.loop(0, 6)
    def _(turn):
        clip = turn // 2
        head = turn % 2
        lane = pl.multiple_of(head * 128, 128)
        row = pl.multiple_of(head * HD, 16)
        keys = qkv_ref[:, clip, :, pl.ds(256 + lane, 128)].reshape(1024, 128)
        vt_ref[...] = qkv_ref[:, clip, :, pl.ds(512 + lane, 128)].reshape(1024, 128).T

        @pl.loop(0, 4)
        def _(block):
            query = qkv_ref[pl.ds(block * 2, 2), clip, :, pl.ds(lane, 128)].reshape(256, 128)
            columns = pl.ds(pl.multiple_of(block * 256, 256), 256)
            scores = lax.dot_general(
                keys, query, (((1,), (1,)), ((), ())), preferred_element_type=F32
            )
            scores = scores + mask_ref[clip]
            peak = jnp.max(scores, axis=0, keepdims=True)
            powers = jnp.exp2((scores - peak) * factor)
            total = jnp.sum(powers, axis=0, keepdims=True)
            mixed = lax.dot_general(
                vt_ref[...],
                powers.astype(BF),
                (((1,), (0,)), ((), ())),
                preferred_element_type=F32,
            )
            mixed = (mixed / total).astype(BF)
            for part in range(2):
                out_ref[block * 2 + part, clip, pl.ds(row, HD)] = mixed[
                    :HD, part * 128 : part * 128 + 128
                ]
            logs_ref[turn, :, columns] = peak * factor + jnp.log2(total)
            peak_ref[head] = jnp.maximum(
                peak_ref[head], jnp.where(live_ref[clip, :, columns] > 0, peak, MASK_VALUE)
            )

        @pl.when(turn == 2)
        def _():
            next(outer)

        @pl.when(turn == 4)
        def _():
            next(outer)
            next(gather)

    mixing = exchange(place, out_ref, att_ref, local.at[0], send, recv)
    next(mixing)
    for _ in outer:
        pass
    spread = plane_gather(place, outer_all, outer_full, local.at[3], plane_send, plane_recv)
    drive(spread, mixing)
    for level in range(LINE):
        for core in range(2):
            for group, start in enumerate(OUTER_STARTS):
                rows_ref[pl.ds((level * 2 + core) * 160 + start, 48)] = outer_full[
                    group * 2 + core, pl.ds(level * 48, 48)
                ]
    for clip in range(3):
        rows = pl.ds(clip * 128, 128)
        branch = lax.dot_general(
            att_ref[:, clip].reshape(1280, 128),
            rows_ref[...],
            (((0,), (0,)), ((), ())),
            preferred_element_type=F32,
        )
        middle = frames_ref[rows].astype(F32) + (branch + out_bias_ref[...])
        middle_ref[rows] = middle
        two_ref[rows] = layer_norm(middle, gain_two_ref[...], shift_two_ref[...]).astype(BF)
    drive(gather)


def attention(
    frames, gain, shift, cotangent, query, key, value, bias, mask, live, weights, outer,
    out_bias, gain_two, shift_two,
):
    return pl.pallas_call(
        attention_kernel,
        out_shape=(
            jax.ShapeDtypeStruct((8,) + frames.shape, BF),
            jax.ShapeDtypeStruct((8, 3, 128, 768), BF),
            jax.ShapeDtypeStruct((8,) + cotangent.shape, BF),
            jax.ShapeDtypeStruct((768, 1280), BF),
            jax.ShapeDtypeStruct((8, 3, 160, 128), BF),
            jax.ShapeDtypeStruct((6, 1, 1024), F32),
            jax.ShapeDtypeStruct((2, 8, 256), F32),
            jax.ShapeDtypeStruct((4,) + weights.shape, BF),
            jax.ShapeDtypeStruct((1280, 1280), BF),
            jax.ShapeDtypeStruct((ROWS, 1280), F32),
            jax.ShapeDtypeStruct((ROWS, 1280), BF),
        ),
        in_specs=[VMEM] * 3 + [ANY] + [VMEM] * 6 + [ANY, ANY] + [VMEM] * 3,
        out_specs=(VMEM, VMEM, ANY, VMEM, VMEM, VMEM, VMEM, ANY, VMEM, VMEM, VMEM),
        scratch_shapes=[
            pltpu.VMEM((ROWS, 1280), BF),
            pltpu.VMEM((8, 3, 160, 128), BF),
            pltpu.VMEM((128, 1024), BF),
            pltpu.VMEM((192, 1280), BF),
            pltpu.VMEM((8, 192, 1280), BF),
            dma(6),
            dma(4, 3),
            dma(8),
            dma(9),
            dma(9),
            dma(8),
            dma(8),
            dma(4, 3),
            dma(4),
            dma(4, 3),
            dma(4),
            dma(9),
            dma(9),
        ],
        compiler_params=params(0, 56),
        name="attention",
    )(
        frames, gain, shift, cotangent, query, key, value, bias, mask, live, weights, outer,
        out_bias, gain_two, shift_two,
    )


def flatten(*pairs):
    names, shapes = [], []
    for number, group in enumerate(pairs):
        for name, shape in group.items():
            names.append((number, name))
            shapes.append(shape)

    def split(refs):
        groups = [{} for _ in pairs]
        for (number, name), ref in zip(names, refs):
            groups[number][name] = ref
        return groups

    return shapes, split


def feed_forward_kernel(
    split, normed_ref, upstream_ref, weights_ref, down_ref, bias_ref,
    total_ref, hidden_ref, grads_ref, bias_out, down_all,
    normed_all, upstream_all, slope_all, rate_ref, sum_ref,
    load, local, line_local, gather_send, gather_recv, line_send, line_recv, *scratch,
):
    place = Place()
    bufs, sems = split(scratch)
    loads = []
    for slot in range(8):
        loads.append(
            pltpu.make_async_copy(upstream_ref.at[slot], upstream_all.at[slot], load.at[slot])
        )
        loads[-1].start()
    greet(place, line=True, plane=True)
    bias_out[...] = jnp.zeros(bias_out.shape, F32)

    def up_rows():
        return weights_ref[:, pl.ds(0, 160)].reshape(640, 1280)

    def down_rows():
        return down_all[...].reshape(640, 1280)

    def activate(slot, rows):
        before = (
            lax.dot_general(
                normed_all[slot, rows],
                up_rows(),
                (((1,), (1,)), ((), ())),
                preferred_element_type=F32,
            )
            + bias_ref[...]
        )
        share = 0.5 + 0.5 * lax.erf(before * math.sqrt(0.5))
        hidden_ref[slot, rows] = (before * share).astype(BF)
        density = jnp.exp(before * before * -0.5) * (1.0 / math.sqrt(2.0 * math.pi))
        return share + before * density

    def pull_back(slot, rows, rate):
        pull = lax.dot_general(
            upstream_all[slot, rows],
            down_rows(),
            (((1,), (1,)), ((), ())),
            preferred_element_type=F32,
        )
        slope = (pull * rate).astype(BF)
        slope_all[slot, rows] = slope
        bias_out[...] += jnp.sum(slope.astype(F32), axis=0, keepdims=True)

    here = [place.dp * 2 + place.c, place.dp * 2 + 1 - place.c]
    seen = []

    def ready(slot):
        index = len(seen)
        seen.append(slot)

        rows = pl.ds(0, ROWS)
        rate = activate(slot, rows)
        if index < 2:
            rate_ref[index] = rate
        else:
            pull_back(slot, rows, rate)

        if index < 2:
            next(down)

    def finish_here():
        for index in range(2):
            pull_back(here[index], pl.ds(0, ROWS), rate_ref[index])

    down = line_gather(
        place, down_ref, down_all, line_local, line_send, line_recv, False
    )
    gather = plane_gather(
        place, normed_ref, normed_all, local, gather_send, gather_recv, ready
    )

    def produce(group, core, start, rows):
        return jnp.dot(
            slope_all[group * 2 + core, pl.ds(start, rows)],
            up_rows(),
            preferred_element_type=F32,
        )

    def result(rows, total):
        total_ref[rows] = total

    reduce = plane_reduce(place, produce, 192, 192, result, bufs, sems, True, True)
    next(down)
    next(gather)
    for copy in loads:
        copy.wait()
    next(gather)
    for _ in down:
        pass
    next(gather)
    next(reduce)
    next(gather)
    next(reduce)
    next(gather)
    next(reduce)
    finish_here()
    next(reduce)

    def weight_grads(left_all, right_all, base):
        @pl.loop(0, 8)
        def _(slot):
            product = lax.dot_general(
                left_all[slot],
                right_all[slot],
                (((0,), (0,)), ((), ())),
                preferred_element_type=F32,
            )
            sum_ref[...] = jnp.where(slot == 0, product, sum_ref[...] + product)

        for level in range(4):
            grads_ref[level, pl.ds(base, 160)] = sum_ref[pl.ds(level * 160, 160)].astype(BF)

    weight_grads(slope_all, normed_all, 0)
    next(reduce)
    weight_grads(hidden_ref, upstream_all, 160)
    for level in range(4):
        grads_ref[level, pl.ds(320, 16)] = jnp.zeros((16, 1280), BF)
        grads_ref[level, pl.ds(320, 16), pl.ds(0, 640)] = jnp.broadcast_to(
            bias_out[...], (16, 640)
        ).astype(BF)
    drive(reduce, gather)


def feed_forward(normed, upstream, weights, down, bias):
    shapes, split = flatten(*plane_reduce_scratch(192, 1280))
    return pl.pallas_call(
        functools.partial(feed_forward_kernel, split),
        out_shape=(
            jax.ShapeDtypeStruct((ROWS, 1280), F32),
            jax.ShapeDtypeStruct((8, ROWS, 640), BF),
            jax.ShapeDtypeStruct((4, 336, 1280), BF),
            jax.ShapeDtypeStruct((1, 640), F32),
            jax.ShapeDtypeStruct((4, 160, 1280), BF),
        ),
        in_specs=[ANY, ANY, VMEM, ANY, VMEM],
        out_specs=(VMEM,) * 5,
        scratch_shapes=[
            pltpu.VMEM((8, ROWS, 1280), BF),
            pltpu.VMEM((8, ROWS, 1280), BF),
            pltpu.VMEM((8, ROWS, 640), BF),
            pltpu.VMEM((2, ROWS, 640), F32),
            pltpu.VMEM((640, 1280), F32),
            dma(8),
            pltpu.SemaphoreType.DMA(()),
            pltpu.SemaphoreType.DMA(()),
            dma(9),
            dma(9),
            dma(4, 3),
            dma(4),
            *shapes,
        ],
        compiler_params=params(3, 60),
        name="feed_forward",
    )(normed, upstream, weights, down, bias)


def attend_back_kernel(
    split, qkv_in, mask_ref, logs_ref, pull_ref, hidden_in, weights_ref, feed_grads_in,
    out_grad_in, dqkv_ref, feed_ref, feed_sum_ref, out_sum_ref,
    qkv_ref, hidden_ref, feed_grads_ref, out_grad_ref, load,
    grad_ref, kt_ref, dk_ref, dv_ref, block_ref, middle_ref, local, send, recv, *scratch,
):
    place = Place()
    (
        line_bufs, line_sems, plane_bufs, plane_sems,
        out_plane_bufs, out_plane_sems, out_line_bufs, out_line_sems,
    ) = split(scratch)
    loads = [
        pltpu.make_async_copy(source, target, load.at[index])
        for index, (source, target) in enumerate(
            (
                (out_grad_in, out_grad_ref),
                (feed_grads_in, feed_grads_ref),
                (hidden_in, hidden_ref),
                (qkv_in, qkv_ref),
            )
        )
    ]
    for copy in loads:
        copy.start()
    greet(place, mp_all=True, plane=True)
    scale = 1.0 / math.sqrt(HD)
    factor = math.log2(math.e) * scale
    arriving = exchange(place, pull_ref, grad_ref, local, send, recv)
    next(arriving)

    def feed_block(group, core, start, rows):
        return jnp.dot(
            hidden_ref[group * 2 + core, pl.ds(start, rows)],
            weights_ref[...].reshape(640, 1280),
            preferred_element_type=F32,
        )

    def feed_result(rows, total):
        feed_ref[rows] = total

    def sum_result(rows, total):
        feed_sum_ref[rows] = total

    plane = plane_reduce(
        place, feed_block, 192, 192, feed_result, plane_bufs, plane_sems, True
    )
    line = line_reduce(
        place,
        lambda level, core, rows: feed_grads_ref[level, rows].astype(F32),
        [pl.ds(start, 112) for start in range(0, 336, 112)],
        sum_result,
        line_bufs,
        line_sems,
        False,
    )
    def middle(rows, total):
        middle_ref[rows] = total

    def out_result(rows, total):
        out_sum_ref[rows] = total

    out_plane = plane_reduce(
        place,
        lambda group, core, start, rows: out_grad_ref[group, core, pl.ds(start, rows)].astype(F32),
        96,
        96,
        middle,
        out_plane_bufs,
        out_plane_sems,
    )
    out_line = line_reduce(
        place,
        lambda level, core, rows: middle_ref[
            pl.ds(pl.multiple_of(level * 48 + rows.start, 16), rows.size)
        ],
        [pl.ds(0, 48)],
        out_result,
        out_line_bufs,
        out_line_sems,
        False,
    )
    loads[0].wait()
    next(out_plane)
    next(out_plane)
    loads[2].wait()
    next(plane)
    next(plane)
    loads[1].wait()
    next(line)
    next(line)
    next(out_line)
    loads[3].wait()
    for _ in arriving:
        pass
    block_ref[...] = jnp.zeros(block_ref.shape, BF)

    @pl.loop(0, 6)
    def _(turn):
        clip = turn // 2
        head = turn % 2
        lane = pl.multiple_of(head * 128, 128)
        row = pl.multiple_of(head * HD, 16)
        kt_ref[...] = qkv_ref[:, clip, :, pl.ds(256 + lane, 128)].reshape(1024, 128).T
        dk_ref[...] = jnp.zeros(dk_ref.shape, F32)
        dv_ref[...] = jnp.zeros(dv_ref.shape, F32)

        @pl.loop(0, 4)
        def _(block):
            query = qkv_ref[pl.ds(block * 2, 2), clip, :, pl.ds(lane, 128)].reshape(256, 128)
            values = qkv_ref[:, clip, :, pl.ds(512 + lane, 128)].reshape(1024, 128)
            keys = qkv_ref[:, clip, :, pl.ds(256 + lane, 128)].reshape(1024, 128)
            columns = pl.ds(pl.multiple_of(block * 256, 256), 256)
            for part in range(2):
                block_ref[:HD, part * 128 : part * 128 + 128] = grad_ref[
                    block * 2 + part, clip, pl.ds(row, HD)
                ]
            scores = lax.dot_general(
                keys, query, (((1,), (1,)), ((), ())), preferred_element_type=F32
            )
            chance = jnp.exp2((scores + mask_ref[clip]) * factor - logs_ref[turn, :, columns])
            dv_ref[...] += lax.dot_general(
                chance.astype(BF),
                block_ref[...],
                (((1,), (1,)), ((), ())),
                preferred_element_type=F32,
            )
            slope = lax.dot_general(
                values, block_ref[...], (((1,), (0,)), ((), ())), preferred_element_type=F32
            )
            center = jnp.sum(chance * slope, axis=0, keepdims=True)
            change = (chance * (slope - center)).astype(BF)
            dk_ref[...] += lax.dot_general(
                change, query, (((1,), (0,)), ((), ())), preferred_element_type=F32
            )
            dq = lax.dot_general(
                kt_ref[...], change, (((1,), (0,)), ((), ())), preferred_element_type=F32
            )
            dqkv_ref[pl.ds(block * 2, 2), clip, :, pl.ds(lane, 128)] = (
                (dq.T * scale).astype(BF).reshape(2, 128, 128)
            )

        dqkv_ref[:, clip, :, pl.ds(256 + lane, 128)] = (
            (dk_ref[...] * scale).astype(BF).reshape(8, 128, 128)
        )
        dqkv_ref[:, clip, :, pl.ds(512 + lane, 128)] = (
            dv_ref[...].astype(BF).reshape(8, 128, 128)
        )

        @pl.when(turn == 2)
        def _():
            next(out_plane)
            next(plane)

        @pl.when(turn == 5)
        def _():
            next(out_plane)

    drive(line, out_line, plane, out_plane)


def attend_back(qkv, mask, logs, pull, hidden, weights, feed_grads, out_grad):
    shapes, split = flatten(
        *line_reduce_scratch(336, 1280, False),
        *plane_reduce_scratch(192, 1280),
        *plane_reduce_scratch(96, 1280),
        *line_reduce_scratch(48, 1280, False),
    )
    return pl.pallas_call(
        functools.partial(attend_back_kernel, split),
        out_shape=(
            jax.ShapeDtypeStruct(qkv.shape, BF),
            jax.ShapeDtypeStruct((ROWS, 1280), F32),
            jax.ShapeDtypeStruct((336, 1280), F32),
            jax.ShapeDtypeStruct((48, 1280), F32),
        ),
        in_specs=[ANY, VMEM, VMEM, ANY, ANY, VMEM, ANY, ANY],
        out_specs=(VMEM,) * 4,
        scratch_shapes=[
            *(pltpu.VMEM(ref.shape, BF) for ref in (qkv, hidden, feed_grads, out_grad)),
            dma(4),
            pltpu.VMEM((8, 3, 160, 128), BF),
            pltpu.VMEM((128, 1024), BF),
            pltpu.VMEM((1024, 128), F32),
            pltpu.VMEM((1024, 128), F32),
            pltpu.VMEM((128, 256), BF),
            pltpu.VMEM((192, 1280), F32),
            pltpu.SemaphoreType.DMA(()),
            dma(8),
            dma(8),
            *shapes,
        ],
        compiler_params=params(2, 62),
        name="attend_back",
    )(qkv, mask, logs, pull, hidden, weights, feed_grads, out_grad)


GROUP_ROWS = 4832
GROUP_STEP = 4800
PACK_ROWS = GROUP_STEP * 3 + GROUP_ROWS
SEGMENTS = (
    ("query", 0, 1600),
    ("query_bias", 204800, 2),
    ("key", 204960, 1600),
    ("value", 409760, 1600),
    ("value_bias", 614560, 2),
    ("out", 614720, 1600),
    ("up", 819520, 6400),
    ("up_bias", 1638720, 5),
    ("down", 1639360, 6400),
)
PACK_END = 19216
SHARE_ROWS = 4808


def segment_table():
    table, cursor = {}, 0
    for name, start, rows in SEGMENTS:
        row = start // 128
        cursor += 32
        cursor += (row - cursor) % 8
        table[name] = (cursor, row, rows, start % 128)
        cursor += rows
    return table, (cursor + 32 + 7) // 8 * 8


TABLE, STAGE_ROWS = segment_table()


def lane_of(rows):
    return lax.broadcasted_iota(jnp.int32, (rows, 128), 1)


def pack_rows(stage, packed):
    def piece(name, first, rows):
        base, row, _, shift = TABLE[name]
        at = base - row + first
        here = stage[pl.ds(at, rows)]
        if shift == 0:
            return here
        above = stage[pl.ds(at - 1, rows)]
        return jnp.where(
            lane_of(rows) >= shift, pltpu.roll(here, shift, 1), pltpu.roll(above, shift, 1)
        )

    done = set()
    for name, _, _ in SEGMENTS:
        _, row, rows, shift = TABLE[name]
        low = -(-(row + (1 if shift else 0)) // 16) * 16
        high = (row + rows) // 16 * 16
        if high <= low:
            continue
        done.update(range(low, high, 16))
        turns = (high - low) // 128

        @pl.loop(0, turns)
        def _(turn):
            first = pl.multiple_of(low + turn * 128, 16)
            packed[pl.ds(first, 128)] = piece(name, first, 128).astype(BF)

        for first in range(low + turns * 128, high, 16):
            packed[pl.ds(first, 16)] = piece(name, first, 16).astype(BF)
    for first in range(0, PACK_ROWS, 16):
        if first in done:
            continue
        total = jnp.zeros((16, 128), F32)
        for name, _, _ in SEGMENTS:
            _, row, rows, shift = TABLE[name]
            if row < first + 16 and row + rows + (1 if shift else 0) > first:
                total = total + piece(name, first, 16)
        packed[pl.ds(first, 16)] = total.astype(BF)


def stage_wide(stage, name, ref, step):
    base = TABLE[name][0]
    rows, wide = ref.shape[0], ref.shape[1] // 128

    @pl.loop(0, rows // step)
    def _(turn):
        first = pl.multiple_of(turn * step, step)
        for block in range(wide):
            stage[pl.ds(base + first * wide + block, step, stride=wide), :] = ref[
                pl.ds(first, step), pl.ds(block * 128, 128)
            ].astype(F32)


def stage_heads(stage, name, ref, lanes, column):
    base = TABLE[name][0]
    for head in range(2):
        column[head] = ref[:, pl.ds(lanes + head * 128, 128)]

    @pl.loop(0, 5)
    def _(turn):
        lane = lane_of(64)
        rows = [jnp.zeros((64, 128), F32) for _ in range(5)]
        for block in range(8):
            item, head = block // 2, block % 2
            value = column[head, pl.ds(turn * 256 + item, 64, stride=4)]
            offset = block * HD
            first, shift = offset // 128, offset % 128
            if shift:
                value = pltpu.roll(value, shift, 1)
            if shift + HD > 128:
                rows[first] = rows[first] + jnp.where(lane >= shift, value, 0.0)
                rows[first + 1] = rows[first + 1] + jnp.where(
                    lane < shift + HD - 128, value, 0.0
                )
            else:
                rows[first] = rows[first] + value
        for index in range(5):
            stage[pl.ds(base + turn * 320 + index, 64, stride=5), :] = rows[index]


def stage_head_bias(stage, name, ref, lanes):
    base = TABLE[name][0]
    lane = lane_of(1)
    first = ref[0:1, pl.ds(lanes, 128)]
    second = pltpu.roll(ref[0:1, pl.ds(lanes + 128, 128)], HD, 1)
    stage[pl.ds(base, 1)] = first + jnp.where(lane >= HD, second, 0.0)
    stage[pl.ds(base + 1, 1)] = jnp.where(lane < 2 * HD - 128, second, 0.0)


def stage_share(stage, name, ref, first, count, place):
    base = TABLE[name][0] + place.dp * count * 10
    for block in range(10):
        stage[pl.ds(base + block, count, stride=10), :] = ref[
            pl.ds(first, count), pl.ds(block * 128, 128)
        ]


def stage_up(stage, ref, place):
    base = TABLE["up"][0]
    lane = lane_of(128)
    for quarter in range(4):

        @pl.when(place.dp == quarter)
        def _():
            for block in range(10):
                columns = pl.ds(block * 128, 128)
                first = ref[pl.ds(0, 128), columns].T
                second = jnp.where(lane < 32, ref[pl.ds(128, 128), columns].T, 0.0)
                shift = 32 * quarter
                if shift:
                    first = pltpu.roll(first, shift, 1)
                    second = pltpu.roll(second, shift, 1)
                    second = second + jnp.where(lane < shift, first, 0.0)
                    first = jnp.where(lane >= shift, first, 0.0)
                at = base + block * 640 + quarter
                stage[pl.ds(at, 128, stride=5), :] = first
                stage[pl.ds(at + 1, 128, stride=5), :] = second


def norm_back(frames_ref, middle_ref, gain_ref, grad_ref):
    def write(rows, total):
        value = frames_ref[rows].astype(F32)
        center = value - jnp.mean(value, axis=-1, keepdims=True)
        spread = jnp.mean(center * center, axis=-1, keepdims=True)
        root = lax.rsqrt(spread + NORM_EPSILON)
        scaled = center * root
        pull = total * gain_ref[...]
        along = jnp.mean(pull * scaled, axis=-1, keepdims=True)
        grad_ref[rows] = middle_ref[rows] + root * (
            pull - jnp.mean(pull, axis=-1, keepdims=True) - scaled * along
        )

    return write


def fetch(first, rows, sems, grad, weight, frames, middle):
    span = pl.ds(first, rows)
    pairs = (
        (grad[0].at[:, span], grad[1]),
        weight,
        (frames[0].at[span], frames[1]),
        (middle[0].at[span], middle[1]),
    )
    copies = [
        pltpu.make_async_copy(source, target, sems.at[index])
        for index, (source, target) in enumerate(pairs)
    ]
    for copy in copies:
        copy.start()
    return copies


def fetch_scratch(rows):
    return [
        pltpu.VMEM((8, rows, 768), BF),
        pltpu.VMEM((768, 1280), BF),
        pltpu.VMEM((rows, 1280), BF),
        pltpu.VMEM((rows, 1280), F32),
        dma(4),
    ]


def line_product(place, grad_ref, weight_ref, rows, result, bufs, sems):
    def produce(level, core, tile):
        return jnp.dot(
            grad_ref[level * 2 + core, tile],
            weight_ref[...],
            preferred_element_type=F32,
        )

    tiles = [pl.ds(0, rows)]
    return line_reduce(place, produce, tiles, result, bufs, sems, True)


FIRST_ROWS = 128


def finish_kernel(
    split, grad_in, weight_in, joined_ref, bias_ref, bias_column_ref, sum_ref, out_ref,
    up_bias_ref, small_ref, peak_ref, frames_in, middle_in, gain_ref, shift_ref, cap_ref,
    input_grad_ref, grads_ref, small_out, roots_out,
    grad_ref, weight_ref, frames_ref, middle_ref, load,
    stage, packed, sum_rows, column, tiles, small_in, small_all, peak_all, edge,
    local, small_send, small_recv, plane_send, plane_recv, *scratch,
):
    place = Place()
    line_bufs, line_sems, bufs, sems = split(scratch)
    loads = fetch(
        0,
        FIRST_ROWS,
        load,
        (grad_in, grad_ref),
        (weight_in, weight_ref),
        (frames_in, frames_ref),
        (middle_in, middle_ref),
    )
    greet(place, mp_all=True, plane=True)
    peers = (place.dpx, place.dpy, place.dpd)

    def tell(index, source, target, group, act):
        act(
            remote(
                source,
                target.at[place.dp],
                plane_send.at[index],
                plane_recv.at[index],
                group,
                place.mp,
            )
        )

    def heard(index, target, group):
        block = target.at[group]
        remote(
            block, block, plane_send.at[index], plane_recv.at[index], group, place.mp
        ).wait_recv()

    line = line_product(
        place,
        grad_ref,
        weight_ref,
        FIRST_ROWS,
        norm_back(frames_ref, middle_ref, gain_ref, input_grad_ref),
        line_bufs,
        line_sems,
    )
    for index, group in enumerate(peers):
        tell(index, peak_ref, peak_all, group, lambda copy: copy.start())
    for copy in loads:
        copy.wait()

    for block in range(10):
        lanes = pl.ds(block * 128, 128)
        weight = weight_ref[:, lanes].astype(F32)
        turned = joined_ref[lanes].T
        whole = jnp.sum(weight * bias_column_ref[...], axis=0, keepdims=True)
        along = jnp.sum(weight * turned, axis=0, keepdims=True)
        tiles[pl.ds(block, 1)] = (along - shift_ref[:, lanes] * whole) / gain_ref[:, lanes]
        tiles[pl.ds(10 + block, 1)] = whole
    tiles[pl.ds(20, 44)] = small_ref[...]
    for run in range(8):
        edge[run] = tiles[pl.ds(run * 15 // 2, 8)]
    mixing = exchange(place, edge, small_in, local, small_send, small_recv)
    next(mixing)

    stage[...] = jnp.zeros(stage.shape, F32)
    for name, lanes in (("query", 0), ("key", 256), ("value", 512)):
        stage_heads(stage, name, joined_ref, lanes, column)
    stage_head_bias(stage, "query_bias", bias_ref, 0)
    stage_head_bias(stage, "value_bias", bias_ref, 512)
    stage_share(stage, "out", out_ref, 0, 40, place)
    stage_share(stage, "down", sum_ref, 160, 160, place)
    stage_up(stage, sum_ref, place)
    stage[pl.ds(TABLE["up_bias"][0], 5)] = up_bias_ref[...]
    pack_rows(stage, packed)

    def produce(group, core, start, rows):
        first = pl.multiple_of(group * GROUP_STEP + start, 16)
        return packed[pl.ds(first, GROUP_ROWS // 2)].astype(F32)

    def result(rows, total):
        sum_rows[rows] = total

    half = GROUP_ROWS // 2
    plane = plane_reduce(place, produce, half, half, result, bufs, sems, False)
    next(plane)
    next(plane)
    next(line)
    next(line)
    for _ in mixing:
        pass
    small_all[place.dp] = jnp.sum(small_in[...], axis=0)
    for index, group in enumerate(peers):
        tell(3 + index, small_all.at[place.dp], small_all, group, lambda copy: copy.start())
    next(plane)
    next(line)
    next(line)
    drive(line, plane)
    for index, group in enumerate(peers):
        heard(index, peak_all, group)
        heard(3 + index, small_all, group)
    top = peak_ref[...]
    for group in peers:
        top = jnp.maximum(top, peak_all[group])
    for head in range(2):
        peak = jnp.max(jnp.max(top[head], axis=0, keepdims=True), axis=1, keepdims=True)
        root = jnp.sqrt(cap_ref[...] / jnp.maximum(peak * (1.0 / math.sqrt(HD)), cap_ref[...]))
        roots_out[head] = jnp.broadcast_to(jnp.where(place.dp == 0, root, 1.0), (8, 128))
    whole = jnp.sum(small_all[...], axis=0)
    lane = lane_of(8)
    row = lax.broadcasted_iota(jnp.int32, (8, 128), 0)
    tiles[...] = jnp.zeros((64, 128), F32)
    tiles[pl.ds(8, 8)] = whole
    ahead = pltpu.roll(tiles[pl.ds(9, 8)], 64, 1)
    here = pltpu.roll(whole, 64, 1)
    odd = jnp.where(lane < 64, here, ahead)
    run_of = jnp.where(place.c == 1, odd, whole)
    run_of = jnp.where(jnp.logical_and(row == 7, lane >= 64), 0.0, run_of)
    small_out[...] = run_of
    tiles[pl.ds(8, 8)] = run_of
    wide = lane_of(16)
    entry = jnp.where(
        wide >= 64, pltpu.roll(tiles[pl.ds(1, 16)], 64, 1), pltpu.roll(tiles[pl.ds(0, 16)], 64, 1)
    )

    @pl.when(place.dp == 3)
    def _():
        sum_rows[pl.ds(GROUP_STEP, 16)] += entry

    for group in range(4):

        @pl.when(place.dp == group)
        def _():
            down, shift = 480 * group // 128, 480 * group % 128
            if shift == 0:
                grads_ref[...] = sum_rows[pl.ds(0, SHARE_ROWS)]
            else:
                for first in range(0, SHARE_ROWS, 1208):
                    size = min(1208, SHARE_ROWS - first)
                    grads_ref[pl.ds(first, size)] = jnp.where(
                        lane_of(size) < 128 - shift,
                        pltpu.roll(sum_rows[pl.ds(first + down, size)], 128 - shift, 1),
                        pltpu.roll(sum_rows[pl.ds(first + down + 1, size)], 128 - shift, 1),
                    )

    for index, group in enumerate(peers):
        tell(index, peak_ref, peak_all, group, lambda copy: copy.wait_send())
        tell(3 + index, small_all.at[place.dp], small_all, group, lambda copy: copy.wait_send())


def finish(grads, weight, joined, bias, sums, out, up_bias, small, peaks, frames, middle, gain, shift, cap):
    shapes, split = flatten(
        *line_reduce_scratch(FIRST_ROWS, 1280, True),
        *plane_reduce_scratch(GROUP_ROWS // 2, 128, False),
    )
    return pl.pallas_call(
        functools.partial(finish_kernel, split),
        out_shape=(
            jax.ShapeDtypeStruct((FIRST_ROWS, 1280), F32),
            jax.ShapeDtypeStruct((SHARE_ROWS, 128), F32),
            jax.ShapeDtypeStruct((8, 128), F32),
            jax.ShapeDtypeStruct((2, 8, 128), F32),
        ),
        in_specs=[ANY, ANY] + [VMEM] * 8 + [ANY, ANY, VMEM, VMEM, VMEM],
        out_specs=(VMEM,) * 4,
        scratch_shapes=[
            *fetch_scratch(FIRST_ROWS),
            pltpu.VMEM((STAGE_ROWS, 128), F32),
            pltpu.VMEM((PACK_ROWS, 128), BF),
            pltpu.VMEM((GROUP_ROWS, 128), F32),
            pltpu.VMEM((2, 1280, 128), F32),
            pltpu.VMEM((64, 128), F32),
            pltpu.VMEM((8, 8, 128), F32),
            pltpu.VMEM((4, 8, 128), F32),
            pltpu.VMEM((4,) + peaks.shape, F32),
            pltpu.VMEM((8, 8, 128), F32),
            pltpu.SemaphoreType.DMA(()),
            dma(8),
            dma(8),
            dma(6),
            dma(6),
            *shapes,
        ],
        compiler_params=params(7, 62),
        name="finish",
    )(
        grads, weight, joined, bias[None], bias[:, None], sums, out, up_bias, small, peaks,
        frames, middle, gain, shift, cap,
    )


def share_master_kernel(
    split, rows_ref, grad_in, weight_in, frames_in, middle_in, gain_ref,
    whole_out, input_grad_ref,
    grad_ref, weight_ref, frames_ref, middle_ref, load,
    whole_ref, parts, turned, store, send, recv, *scratch,
):
    place = Place()
    line_bufs, line_sems = split(scratch)
    loads = fetch(
        FIRST_ROWS,
        ROWS - FIRST_ROWS,
        load,
        (grad_in, grad_ref),
        (weight_in, weight_ref),
        (frames_in, frames_ref),
        (middle_in, middle_ref),
    )
    greet(place, line=True, plane=True)
    line = line_product(
        place,
        grad_ref,
        weight_ref,
        ROWS - FIRST_ROWS,
        norm_back(frames_ref, middle_ref, gain_ref, input_grad_ref),
        line_bufs,
        line_sems,
    )
    dp, mp, dpx, dpy, dpd = place.dp, place.mp, place.dpx, place.dpy, place.dpd
    half = GROUP_ROWS // 2
    part_a, part_b = pl.ds(0, half), pl.ds(half, half)
    for group in range(4):

        @pl.when(dp == group)
        def _():
            down, shift = 480 * group // 128, 480 * group % 128
            turned[pl.ds(0, 16)] = jnp.zeros((16, 128), F32)
            turned[pl.ds(16, SHARE_ROWS)] = rows_ref[...]
            turned[pl.ds(16 + SHARE_ROWS, 24)] = jnp.zeros((24, 128), F32)
            for first in range(0, GROUP_ROWS, 1208):
                here = turned[pl.ds(16 + first - down, 1208)]
                if shift:
                    here = jnp.where(
                        lane_of(1208) >= shift,
                        pltpu.roll(here, shift, 1),
                        pltpu.roll(turned[pl.ds(15 + first - down, 1208)], shift, 1),
                    )
                parts[dp, pl.ds(first, 1208)] = here.astype(BF)


    def hop(index, block, target):
        return remote(block, block, send.at[index], recv.at[index], target, mp)

    own = parts.at[dp]
    sends = [hop(0, own, dpx), hop(1, own, dpy)]
    for copy in sends:
        copy.start()

    stores = []

    def keep(index, first, rows):
        span = pl.ds(pl.multiple_of(first, 16), rows)
        stores.append(
            pltpu.make_async_copy(whole_ref.at[span], whole_out.at[span], store.at[index])
        )
        stores[-1].start()

    def unpack(group):
        for start in range(32, GROUP_STEP, 2384):
            at = pl.multiple_of(group * GROUP_STEP + start, 16)
            whole_ref[pl.ds(at, 2384)] = parts[group, pl.ds(start, 2384)].astype(F32)
        keep(len(stores), group * GROUP_STEP + 32, GROUP_STEP - 32)

    for copy in loads:
        copy.wait()
    next(line)
    next(line)
    unpack(dp)
    hop(0, parts.at[dpx], dpx).wait_recv()
    sends.append(hop(2, parts.at[dpx, part_a], dpy))
    sends[-1].start()
    hop(1, parts.at[dpy], dpy).wait_recv()
    sends.append(hop(3, parts.at[dpy, part_b], dpx))
    sends[-1].start()
    unpack(dpx)
    unpack(dpy)
    next(line)
    next(line)
    hop(2, parts.at[dpd, part_a], dpy).wait_recv()
    hop(3, parts.at[dpd, part_b], dpx).wait_recv()
    unpack(dpd)
    for group in range(4):
        first = parts[group, pl.ds(0, 32)].astype(F32)
        if group > 0:
            first = first + parts[group - 1, pl.ds(GROUP_STEP, 32)].astype(F32)
        whole_ref[pl.ds(group * GROUP_STEP, 32)] = first
        keep(4 + group, group * GROUP_STEP, 32)
    whole_ref[pl.ds(4 * GROUP_STEP, 16)] = parts[3, pl.ds(GROUP_STEP, 16)].astype(F32)
    keep(8, 4 * GROUP_STEP, 16)
    for copy in sends:
        copy.wait_send()
    drive(line)
    for copy in stores:
        copy.wait()


def share_master(rows, grads, weight, frames, middle, gain):
    shapes, split = flatten(*line_reduce_scratch(ROWS - FIRST_ROWS, 1280, True))
    return pl.pallas_call(
        functools.partial(share_master_kernel, split),
        out_shape=(
            jax.ShapeDtypeStruct((PACK_END, 128), F32),
            jax.ShapeDtypeStruct((ROWS - FIRST_ROWS, 1280), F32),
        ),
        in_specs=[VMEM, ANY, ANY, ANY, ANY, VMEM],
        out_specs=(ANY, VMEM),
        scratch_shapes=[
            *fetch_scratch(ROWS - FIRST_ROWS),
            pltpu.VMEM((PACK_END, 128), F32),
            pltpu.VMEM((4, GROUP_ROWS, 128), BF),
            pltpu.VMEM((SHARE_ROWS + 40, 128), F32),
            dma(9),
            dma(4),
            dma(4),
            *shapes,
        ],
        compiler_params=params(8, 60),
        name="share_master",
    )(rows, grads, weight, frames, middle, gain)


STEP_ENTRIES = 1024 * 76


def optimize_kernel(
    rates_ref, roots_ref, grads_ref, master_ref, first_ref, second_ref,
    owned_out, master_out, first_out, second_out, padded_out,
):
    entry = lax.broadcasted_iota(jnp.int32, (1, STEP_ENTRIES), 1)
    entry = entry + pl.program_id(0) * STEP_ENTRIES
    grads = grads_ref[...]
    first = BETA_FIRST * first_ref[...] + (1.0 - BETA_FIRST) * grads
    second = BETA_SECOND * second_ref[...] + (1.0 - BETA_SECOND) * grads * grads
    change = first * rates_ref[0] / (jnp.sqrt(second * rates_ref[1]) + ADAM_EPSILON)
    block = jnp.floor((entry.astype(F32) + 0.5) * (1.0 / HD))
    odd = block - 2.0 * jnp.floor(block * 0.5) > 0.5
    factor = jnp.where(
        entry < KEY_END, jnp.where(odd, roots_ref[1, 0:1, 0:1], roots_ref[0, 0:1, 0:1]), 1.0
    )
    master = (master_ref[...] * rates_ref[2] - change) * factor
    owned_out[...] = grads
    master_out[...] = master
    first_out[...] = first
    second_out[...] = second
    padded_out[...] = jnp.where(entry < SHARE_ENTRIES, master, 0.0)


KEY_END = 409760
SHARE_ENTRIES = 614880


def optimize(rates, roots, grads, master, first, second):
    block = pl.BlockSpec((1, STEP_ENTRIES), lambda step: (0, step))
    share = jax.ShapeDtypeStruct((1, SHARE_ENTRIES), F32)
    return pl.pallas_call(
        optimize_kernel,
        grid=(pl.cdiv(SHARE_ENTRIES, STEP_ENTRIES),),
        out_shape=(share,) * 4 + (jax.ShapeDtypeStruct((1, SHARE_ROWS * 128), F32),),
        in_specs=[
            pl.BlockSpec(memory_space=pltpu.SMEM),
            pl.BlockSpec((2, 8, 128), lambda step: (0, 0, 0)),
        ]
        + [block] * 4,
        out_specs=(block,) * 5,
        compiler_params=pltpu.CompilerParams(vmem_limit_bytes=62 << 20),
        name="optimize",
    )(rates, roots, grads, master, first, second)


def fast_body(
    frames,
    lengths,
    key_mask,
    cotangent,
    gain_one,
    shift_one,
    query_weight,
    query_bias,
    key_weight,
    value_weight,
    value_bias,
    out_weight,
    out_bias,
    gain_two,
    shift_two,
    up_weight,
    up_bias,
    down_weight,
    down_bias,
    master,
    moment_one,
    moment_two,
    adam_step,
    hyper_rates,
):
    group = lax.axis_index("dp")
    position = jnp.arange(1024, dtype=jnp.int32)
    keep_query = position[None, :] < lengths[:, None]
    keep_key = jnp.logical_and(keep_query, key_mask == 1)
    mask = jnp.where(keep_key, 0.0, MASK_VALUE)[:, :, None]
    live = keep_query.astype(F32)[:, None, :]
    gain_first = gain_one.astype(F32)
    shift_first = shift_one.astype(F32)
    gain_second = gain_two.astype(F32)
    shift_second = shift_two.astype(F32)
    inputs = frames.transpose(1, 0, 2).reshape(ROWS, 1280).astype(F32)
    upstream_low = cotangent.transpose(1, 0, 2).reshape(ROWS, 1280)
    upstream = upstream_low.astype(F32)
    def head_lanes(bias):
        lanes = bias.astype(F32).reshape(2, HD)
        return jnp.pad(lanes, ((0, 0), (0, 128 - HD))).reshape(256)

    joined_bias = jnp.concatenate(
        [head_lanes(query_bias), jnp.zeros((256,), F32), head_lanes(value_bias)]
    )[None]
    frame_rows = frames.transpose(1, 0, 2).reshape(ROWS, 1280)
    quarter = group * 160
    up_share = lax.dynamic_slice_in_dim(up_weight, quarter, 160, 1).T
    down_share = lax.dynamic_slice_in_dim(down_weight, quarter, 160, 0)
    bias_share = lax.dynamic_slice_in_dim(up_bias, quarter, 160, 0)
    bias_rows = jnp.pad(bias_share[None], ((0, 15), (0, 1280 - 160)))
    message = jnp.concatenate([up_share, bias_rows])
    outer_start = jnp.minimum(group * 48, 112)
    outer = lax.dynamic_slice_in_dim(out_weight, outer_start, 48, 0)
    (
        normed_full, qkv, upstream_full, joined_weight, attended, logs, peaks, gathered,
        out_rows, middle, normed_two,
    ) = attention(
        frame_rows,
        gain_first[None],
        shift_first[None],
        upstream_low,
        query_weight.T,
        key_weight.T,
        value_weight.T,
        joined_bias,
        mask,
        live,
        message,
        outer,
        out_bias.astype(F32)[None],
        gain_second[None],
        shift_second[None],
    )
    up_lanes = gathered[:, 160, :160].reshape(1, 640).astype(F32)
    out_rows = out_rows.reshape(8, 160, 1280)

    normed_two_grad, hidden, feed_grads, _, down_all = feed_forward(
        normed_two, upstream_full, gathered, down_share, up_lanes
    )

    _, norm_two_pull = jax.vjp(layer_norm, middle, gain_second, shift_second)
    middle_norm_grad, gain_two_grad, shift_two_grad = norm_two_pull(normed_two_grad)
    middle_grad = upstream + middle_norm_grad
    branch_grad = middle_grad.astype(BF)
    branch_clips = branch_grad.reshape(3, 128, 1280)
    out_grad = jnp.einsum("schr,crd->shd", attended, branch_clips, preferred_element_type=F32)
    attended_grad = jnp.einsum(
        "shd,crd->schr", out_rows, branch_clips, preferred_element_type=F32
    ).astype(BF)
    out_quarters = jnp.pad(
        out_grad.astype(BF).reshape(4, 2, 4, 40, 1280), ((0, 0),) * 3 + ((0, 8), (0, 0))
    )
    out_quarters = out_quarters.transpose(2, 1, 0, 3, 4).reshape(4, 2, 192, 1280)
    joined_grad, feed, feed_sum, out_sum = attend_back(
        qkv, mask, logs, attended_grad, hidden, down_all, feed_grads, out_quarters
    )
    layer_out = (middle + feed + down_bias.astype(F32)).astype(BF)
    joined_grad = joined_grad.reshape(8, ROWS, 768)
    joined_weight_grad = jnp.einsum(
        "prd,pre->de", normed_full, joined_grad, preferred_element_type=F32
    )
    joined_bias_grad = jnp.sum(joined_grad.astype(F32), axis=(0, 1))

    level = lax.axis_index("mp") // 2
    up_bias_share = lax.dynamic_slice_in_dim(feed_sum[320], level * 160, 160, 0)
    up_bias_rows = lax.dynamic_update_slice(
        jnp.zeros((640,), F32), up_bias_share, (quarter,)
    ).reshape(5, 128)
    small_rows = jnp.concatenate(
        [
            jnp.sum(branch_grad.astype(F32), axis=0),
            gain_two_grad,
            shift_two_grad,
            jnp.sum(upstream, axis=0),
            jnp.zeros((512,), F32),
        ]
    ).reshape(44, 128)
    first_grad, grad_rows, small_sum, roots = finish(
        joined_grad,
        joined_weight,
        joined_weight_grad,
        joined_bias_grad,
        feed_sum,
        out_sum,
        up_bias_rows,
        small_rows,
        peaks,
        frame_rows,
        middle_grad,
        gain_first[None],
        shift_first[None],
        hyper_rates[2].reshape(1, 1),
    )
    small_total = small_sum.reshape(1024)[:960]
    learn_rate = hyper_rates[0]
    weight_decay = hyper_rates[1]
    step_count = adam_step[0].astype(F32)
    rates = jnp.stack(
        [
            learn_rate / (1.0 - jnp.power(BETA_FIRST, step_count)),
            1.0 / (1.0 - jnp.power(BETA_SECOND, step_count)),
            1.0 - learn_rate * weight_decay,
        ]
    )
    owned_grads, master_new, first_new, second_new, padded = optimize(
        rates, roots, grad_rows.reshape(1, SHARE_ROWS * 128), master, moment_one, moment_two
    )
    whole, second_grad = share_master(
        padded.reshape(SHARE_ROWS, 128),
        joined_grad,
        joined_weight,
        frame_rows,
        middle_grad,
        gain_first[None],
    )
    input_grad = jnp.concatenate([first_grad, second_grad])
    whole = lax.optimization_barrier(whole.reshape(1, PACK_END * 128))
    weights_new = whole[:, : 4 * SHARE_ENTRIES].astype(BF)
    return (
        layer_out.reshape(3, 128, 1280).transpose(1, 0, 2),
        input_grad.reshape(3, 128, 1280).transpose(1, 0, 2),
        owned_grads,
        master_new,
        first_new,
        second_new,
        weights_new,
        small_total,
    )


def body(
    frames,
    lengths,
    key_mask,
    cotangent,
    gain_one,
    shift_one,
    query_weight,
    query_bias,
    key_weight,
    value_weight,
    value_bias,
    out_weight,
    out_bias,
    gain_two,
    shift_two,
    up_weight,
    up_bias,
    down_weight,
    down_bias,
    master,
    moment_one,
    moment_two,
    adam_step,
    hyper_rates,
):
    local_rows, clip_count, model_width = frames.shape
    total_rows = key_mask.shape[1]
    head_cols = query_weight.shape[1]
    heads_here = head_cols // HD
    block_rows = min(512, total_rows)
    blocks = total_rows // block_rows
    score_scale = 1.0 / math.sqrt(HD)
    position = jnp.arange(total_rows, dtype=jnp.int32)
    keep_query = position[None, :] < lengths[:, None]
    keep_key = jnp.logical_and(keep_query, key_mask == 1)
    gain_first = gain_one.astype(jnp.float32)
    shift_first = shift_one.astype(jnp.float32)
    gain_second = gain_two.astype(jnp.float32)
    shift_second = shift_two.astype(jnp.float32)
    inputs = frames.astype(jnp.float32)
    normed = layer_norm(inputs, gain_first, shift_first).astype(jnp.bfloat16)
    joined_weight = jnp.concatenate([query_weight, key_weight, value_weight], axis=1)
    joined_bias = jnp.concatenate(
        [
            query_bias.astype(jnp.float32),
            jnp.zeros((head_cols,), jnp.float32),
            value_bias.astype(jnp.float32),
        ]
    )
    normed_full = lax.all_gather(normed, "mp", axis=0, tiled=True)
    projected = (
        jnp.einsum("rcd,de->rce", normed_full, joined_weight, preferred_element_type=jnp.float32)
        + joined_bias
    ).astype(jnp.bfloat16)
    query = projected[:, :, :head_cols].reshape(total_rows, clip_count, heads_here, HD)
    keys = projected[:, :, head_cols : 2 * head_cols].reshape(
        total_rows, clip_count, heads_here, HD
    )
    values = projected[:, :, 2 * head_cols :].reshape(total_rows, clip_count, heads_here, HD)

    def scores_of(row_start):
        query_block = lax.dynamic_slice_in_dim(query, row_start, block_rows, 0)
        raw_scores = (
            jnp.einsum("qchd,kchd->chqk", query_block, keys, preferred_element_type=jnp.float32)
            * score_scale
        )
        return (query_block, jnp.where(keep_key[:, None, None, :], raw_scores, MASK_VALUE))

    def forward_block(block_index):
        row_start = block_index * block_rows
        _, masked = scores_of(row_start)
        row_peak = jnp.max(masked, axis=-1, keepdims=True)
        exp_scores = jnp.exp(masked - row_peak)
        row_total = jnp.sum(exp_scores, axis=-1, keepdims=True)
        probability = (exp_scores / row_total).astype(jnp.bfloat16)
        attended = jnp.einsum(
            "chqk,kchd->qchd", probability, values, preferred_element_type=jnp.float32
        ).astype(jnp.bfloat16)
        live_rows = lax.dynamic_slice_in_dim(keep_query, row_start, block_rows, 1)
        block_peak = jnp.max(
            jnp.where(live_rows[:, None, :], row_peak[..., 0], MASK_VALUE), axis=(0, 2)
        )
        return (attended, (row_peak + jnp.log(row_total))[..., 0], block_peak)

    attended_blocks, log_totals, block_peaks = lax.map(forward_block, jnp.arange(blocks))
    attended_full = attended_blocks.reshape(total_rows, clip_count, head_cols)
    head_peak = lax.pmax(jnp.max(block_peaks, axis=0), "dp")
    rows_here = attended_full
    attn_branch = lax.psum_scatter(
        jnp.einsum("rck,kd->rcd", rows_here, out_weight, preferred_element_type=jnp.float32),
        "mp",
        scatter_dimension=0,
        tiled=True,
    ) + out_bias.astype(jnp.float32)
    middle = inputs + attn_branch
    normed_two = layer_norm(middle, gain_second, shift_second).astype(jnp.bfloat16)
    upstream = cotangent.astype(jnp.float32)
    normed_two_full = lax.all_gather(normed_two, "mp", axis=0, tiled=True)
    before = jnp.einsum(
        "rcd,df->rcf", normed_two_full, up_weight, preferred_element_type=jnp.float32
    ) + up_bias.astype(jnp.float32)
    hidden = exact_gelu(before).astype(jnp.bfloat16)
    rows_here = hidden
    feed = lax.psum_scatter(
        jnp.einsum(
            "rcf,fd->rcd", rows_here, down_weight, preferred_element_type=jnp.float32
        ).astype(jnp.bfloat16),
        "mp",
        scatter_dimension=0,
        tiled=True,
    ).astype(jnp.float32) + down_bias.astype(jnp.float32)
    layer_out = (middle + feed).astype(jnp.bfloat16)
    feed_grad_full = lax.all_gather(cotangent, "mp", axis=0, tiled=True)
    down_grad = jnp.einsum(
        "rcf,rcd->fd", hidden, feed_grad_full, preferred_element_type=jnp.float32
    )
    hidden_grad = jnp.einsum(
        "rcd,fd->rcf", feed_grad_full, down_weight, preferred_element_type=jnp.float32
    )
    _, gelu_pull = jax.vjp(exact_gelu, before)
    before_grad = gelu_pull(hidden_grad)[0].astype(jnp.bfloat16)
    up_bias_grad = jnp.sum(before_grad.astype(jnp.float32), axis=(0, 1))
    up_grad = jnp.einsum(
        "rcd,rcf->df", normed_two_full, before_grad, preferred_element_type=jnp.float32
    )
    rows_here = before_grad
    normed_two_grad = lax.psum_scatter(
        jnp.einsum("rcf,df->rcd", rows_here, up_weight, preferred_element_type=jnp.float32),
        "mp",
        scatter_dimension=0,
        tiled=True,
    )
    _, norm_two_pull = jax.vjp(layer_norm, middle, gain_second, shift_second)
    middle_norm_grad, gain_two_grad, shift_two_grad = norm_two_pull(normed_two_grad)
    middle_grad = upstream + middle_norm_grad
    branch_grad = middle_grad.astype(jnp.bfloat16)
    branch_grad_full = lax.all_gather(branch_grad, "mp", axis=0, tiled=True)
    out_grad = jnp.einsum(
        "rck,rcd->kd", attended_full, branch_grad_full, preferred_element_type=jnp.float32
    )
    attended_grad = jnp.einsum(
        "rcd,kd->rck", branch_grad_full, out_weight, preferred_element_type=jnp.float32
    ).astype(jnp.bfloat16)
    attended_grad = attended_grad.reshape(total_rows, clip_count, heads_here, HD)

    def backward_block(carry, block_index):
        key_total, value_total = carry
        row_start = block_index * block_rows
        query_block, masked = scores_of(row_start)
        log_total = log_totals[block_index]
        probability = jnp.exp(masked - log_total[..., None])
        grad_block = lax.dynamic_slice_in_dim(attended_grad, row_start, block_rows, 0)
        value_total = value_total + jnp.einsum(
            "chqk,qchd->kchd",
            probability.astype(jnp.bfloat16),
            grad_block,
            preferred_element_type=jnp.float32,
        )
        prob_grad = jnp.einsum(
            "qchd,kchd->chqk", grad_block, values, preferred_element_type=jnp.float32
        )
        score_grad = (
            probability * (prob_grad - jnp.sum(probability * prob_grad, axis=-1, keepdims=True))
        ).astype(jnp.bfloat16)
        query_grad = (
            jnp.einsum("chqk,kchd->qchd", score_grad, keys, preferred_element_type=jnp.float32)
            * score_scale
        ).astype(jnp.bfloat16)
        key_total = (
            key_total
            + jnp.einsum(
                "chqk,qchd->kchd", score_grad, query_block, preferred_element_type=jnp.float32
            )
            * score_scale
        )
        return ((key_total, value_total), query_grad)

    empty_grad = jnp.zeros((total_rows, clip_count, heads_here, HD), jnp.float32)
    (key_total, value_total), query_blocks = lax.scan(
        backward_block, (empty_grad, empty_grad), jnp.arange(blocks)
    )
    joined_grad = jnp.concatenate(
        [
            query_blocks.reshape(total_rows, clip_count, head_cols),
            key_total.reshape(total_rows, clip_count, head_cols).astype(jnp.bfloat16),
            value_total.reshape(total_rows, clip_count, head_cols).astype(jnp.bfloat16),
        ],
        axis=-1,
    )
    joined_bias_grad = jnp.sum(joined_grad.astype(jnp.float32), axis=(0, 1))
    normed_back = lax.all_gather(normed, "mp", axis=0, tiled=True)
    joined_weight_grad = jnp.einsum(
        "rcd,rce->de", normed_back, joined_grad, preferred_element_type=jnp.float32
    )
    rows_here = joined_grad
    normed_grad = lax.psum_scatter(
        jnp.einsum(
            "rce,de->rcd", rows_here, joined_weight, preferred_element_type=jnp.float32
        ).astype(jnp.bfloat16),
        "mp",
        scatter_dimension=0,
        tiled=True,
    ).astype(jnp.float32)
    _, norm_one_pull = jax.vjp(layer_norm, inputs, gain_first, shift_first)
    input_norm_grad, gain_one_grad, shift_one_grad = norm_one_pull(normed_grad)
    input_grad = middle_grad + input_norm_grad
    out_bias_grad = jnp.sum(branch_grad.astype(jnp.float32), axis=(0, 1))
    down_bias_grad = jnp.sum(upstream, axis=(0, 1))
    small_terms = jnp.concatenate(
        [
            gain_one_grad,
            shift_one_grad,
            out_bias_grad,
            gain_two_grad,
            shift_two_grad,
            down_bias_grad,
        ]
    )
    small_share = lax.psum_scatter(small_terms, "mp", scatter_dimension=0, tiled=True)
    small_total = lax.psum(small_share, "dp")
    packed = jnp.concatenate(
        [
            joined_weight_grad[:, :head_cols].reshape(-1),
            joined_bias_grad[:head_cols],
            joined_weight_grad[:, head_cols : 2 * head_cols].reshape(-1),
            joined_weight_grad[:, 2 * head_cols :].reshape(-1),
            joined_bias_grad[2 * head_cols :],
            out_grad.reshape(-1),
            up_grad.reshape(-1),
            up_bias_grad,
            down_grad.reshape(-1),
            small_share,
        ]
    )
    owned_grads = lax.psum_scatter(
        packed.astype(jnp.bfloat16), "dp", scatter_dimension=0, tiled=True
    ).astype(jnp.float32)
    share_size = owned_grads.shape[0]
    learn_rate = hyper_rates[0]
    weight_decay = hyper_rates[1]
    logit_cap = hyper_rates[2]
    step_count = adam_step[0].astype(jnp.float32)
    first_new = BETA_FIRST * moment_one[0] + (1.0 - BETA_FIRST) * owned_grads
    second_new = BETA_SECOND * moment_two[0] + (1.0 - BETA_SECOND) * owned_grads * owned_grads
    first_hat = first_new / (1.0 - jnp.power(BETA_FIRST, step_count))
    second_hat = second_new / (1.0 - jnp.power(BETA_SECOND, step_count))
    entry_index = lax.axis_index("dp") * share_size + jnp.arange(share_size, dtype=jnp.int32)
    query_end = model_width * head_cols
    query_bias_end = query_end + head_cols
    key_end = query_bias_end + model_width * head_cols
    column = jnp.where(
        entry_index < query_end,
        entry_index % head_cols,
        jnp.where(
            entry_index < query_bias_end,
            entry_index - query_end,
            (entry_index - query_bias_end) % head_cols,
        ),
    )
    head_index = column // HD
    root_factor = jnp.sqrt(logit_cap / jnp.maximum(head_peak, logit_cap))
    head_factor = jnp.zeros((share_size,), jnp.float32)
    for head_number in range(heads_here):
        head_factor = head_factor + jnp.where(
            head_index == head_number, root_factor[head_number], 0.0
        )
    factor = jnp.where(entry_index < key_end, head_factor, 1.0)
    master_here = master[0]
    master_new = (
        master_here
        - learn_rate
        * (first_hat / (jnp.sqrt(second_hat) + ADAM_EPSILON) + weight_decay * master_here)
    ) * factor
    weights_full = lax.all_gather(master_new.astype(jnp.bfloat16), "dp", axis=0, tiled=True)
    return (
        layer_out,
        input_grad,
        owned_grads[None],
        master_new[None],
        first_new[None],
        second_new[None],
        weights_full[None],
        small_total,
    )


def solution(mesh):
    chosen = fast_body if dict(mesh.shape) == {"dp": 4, "mp": 8} else body
    placed = (
        P("mp", "dp", None),
        P("dp"),
        P("dp", None),
        P("mp", "dp", None),
        P(),
        P(),
        P(None, "mp"),
        P("mp"),
        P(None, "mp"),
        P(None, "mp"),
        P("mp"),
        P("mp", None),
        P(),
        P(),
        P(),
        P(None, "mp"),
        P("mp"),
        P("mp", None),
        P(),
        P("mp", "dp"),
        P("mp", "dp"),
        P("mp", "dp"),
        P(),
        P(),
    )
    return jax.shard_map(
        chosen,
        mesh=mesh,
        in_specs=placed,
        out_specs=(
            P("mp", "dp", None),
            P("mp", "dp", None),
            P("mp", "dp"),
            P("mp", "dp"),
            P("mp", "dp"),
            P("mp", "dp"),
            P("mp", None),
            P("mp"),
        ),
        check_vma=False,
    )
```

```python
import functools
import math

import jax
import jax.numpy as jnp
from jax import lax
from jax.experimental import pallas as pl
from jax.experimental.pallas import tpu as pltpu
from jax.sharding import PartitionSpec as P

HD = 80


NORM_EPSILON = 1e-05
ADAM_EPSILON = 1e-08
BETA_FIRST = 0.9
BETA_SECOND = 0.999
MASK_VALUE = -1e30


def layer_norm(value, gain, shift):
    center = value - jnp.mean(value, axis=-1, keepdims=True)
    spread = jnp.mean(center * center, axis=-1, keepdims=True)
    return center * lax.rsqrt(spread + NORM_EPSILON) * gain + shift


def exact_gelu(argument):
    return jax.nn.gelu(argument, approximate=False)


MESH = pl.DeviceIdType.MESH
ANY = pl.BlockSpec(memory_space=pl.ANY)
VMEM = pl.BlockSpec(memory_space=pltpu.VMEM)
LINE = 4
ROWS = 384
BF = jnp.bfloat16
F32 = jnp.float32


class Place:
    def __init__(self):
        self.dp = lax.axis_index("dp")
        self.mp = lax.axis_index("mp")
        self.z = self.mp // 2
        self.c = self.mp % 2
        self.pair = self.z * 2 + 1 - self.c
        self.dpx = self.dp + 1 - 2 * (self.dp % 2)
        self.dpy = (self.dp + 2) % 4
        self.dpd = 3 - self.dp

    def zorder(self, event):
        if event == 0:
            return self.z
        if event == 1:
            return self.z + 1 - 2 * (self.z % 2)
        if event == 2:
            return 2 - self.z // 2
        return 3 - 3 * (self.z // 2)


def greet(place, mp_all=False, line=False, plane=False, pair=True):
    barrier = pltpu.get_barrier_semaphore()
    count = 0

    def signal(dp, mp):
        pl.semaphore_signal(barrier, inc=1, device_id=(dp, mp), device_id_type=MESH)

    if mp_all:
        for hop in range(1, 8):
            signal(place.dp, (place.mp + hop) % 8)
        count += 7
    else:
        if pair:
            signal(place.dp, place.pair)
            count += 1
        if line:

            @pl.when(place.z > 0)
            def _():
                signal(place.dp, place.mp - 2)

            @pl.when(place.z < LINE - 1)
            def _():
                signal(place.dp, place.mp + 2)

    if plane:
        for other in (place.dpx, place.dpy, place.dpd):
            signal(other, place.mp)
        count += 3
    if line and not mp_all:
        pl.semaphore_wait(barrier, count + 1 + (place.z + 1) // 2 % 2)
    else:
        pl.semaphore_wait(barrier, count)


def remote(src, dst, send, recv, dp, mp):
    return pltpu.make_async_remote_copy(
        src_ref=src,
        dst_ref=dst,
        send_sem=send,
        recv_sem=recv,
        device_id=(dp, mp),
        device_id_type=MESH,
    )


def line_gather(place, src, out, local, send, recv, paired, ready=None, rows=None):
    dp, z, c, mp, pair = place.dp, place.z, place.c, place.mp, place.pair

    def at(slot):
        if rows is None:
            return out.at[slot]
        return out.at[pl.ds(pl.multiple_of(slot * rows, 16), rows)]

    def slot_of(level, core):
        return level * 2 + core if paired else level

    def hop(event, slot, source, direction, target):
        return remote(source, at(slot), send.at[event, direction], recv.at[slot], dp, target)

    own = slot_of(z, c)
    keep = pltpu.make_async_copy(src, at(own), local)
    keep.start()

    def ways(event, level, slot, source, act):
        up = z < LINE - 1
        down = z > 0
        if event > 0:
            up = jnp.logical_and(up, level < z)
            down = jnp.logical_and(down, level > z)

        @pl.when(up)
        def _():
            act(hop(event, slot, source, 1, mp + 2))

        @pl.when(down)
        def _():
            act(hop(event, slot, source, 2, mp - 2))

        if paired:
            act(hop(event, slot, source, 0, pair))

    ways(0, z, own, src, lambda copy: copy.start())
    yield
    if ready is not None:
        keep.wait()
        ready(own)
        if paired:
            other = slot_of(z, 1 - c)
            hop(0, other, at(other), 0, pair).wait_recv()
            ready(other)

    def settle(event):
        level = place.zorder(event)
        ready(slot_of(level, c))
        if paired:
            other = slot_of(level, 1 - c)
            hop(event, other, at(other), 0, pair).wait_recv()
            ready(other)

    for event in range(1, LINE):
        level = place.zorder(event)
        slot = slot_of(level, c)
        hop(event, slot, at(slot), 0, pair).wait_recv()
        ways(event, level, slot, at(slot), lambda copy: copy.start())
        if ready is not None and event > 1:
            if event == 2:
                settle(1)
            settle(event)
        yield
    if ready is None:
        if paired:
            for level in range(LINE):
                other = slot_of(level, 1 - c)
                hop(0, other, at(other), 0, pair).wait_recv()
        keep.wait()
    for event in range(LINE):
        level = place.zorder(event)
        slot = slot_of(level, c)
        ways(event, level, slot, at(slot), lambda copy: copy.wait_send())
    yield


def plane_gather(place, src, out, local, send, recv, ready=None, primed=False):
    dp, c, mp, pair = place.dp, place.c, place.mp, place.pair
    dpx, dpy, dpd = place.dpx, place.dpy, place.dpd
    half = src.shape[0] // 2
    part_a, part_b = pl.ds(0, half), pl.ds(half, half)

    def at(group, core):
        return out.at[group * 2 + core]

    def hop(index, block, group, target):
        return remote(block, block, send.at[index], recv.at[index], group, target)

    def done(group, core):
        if ready is not None:
            ready(group * 2 + core)

    keep = pltpu.make_async_copy(src, at(dp, c), local)
    here = at(dp, c)
    from_x, from_y, from_d = at(dpx, c), at(dpy, c), at(dpd, c)
    firsts = [
        remote(src, here, send.at[0], recv.at[0], dp, pair),
        remote(src, here, send.at[1], recv.at[1], dpx, mp),
        remote(src, here, send.at[2], recv.at[2], dpy, mp),
    ]
    seconds = [
        hop(3, from_x.at[part_a], dpy, mp),
        hop(4, from_y.at[part_b], dpx, mp),
        hop(5, from_x, dp, pair),
        hop(6, from_y, dp, pair),
        hop(7, from_d.at[part_a], dp, pair),
        hop(8, from_d.at[part_b], dp, pair),
    ]
    if primed:
        yield
    keep.start()
    for copy in firsts:
        copy.start()
    yield
    if ready is not None:
        keep.wait()
        done(dp, c)
        hop(0, at(dp, 1 - c), dp, pair).wait_recv()
        done(dp, 1 - c)
    hop(1, from_x, dpx, mp).wait_recv()
    seconds[0].start()
    hop(2, from_y, dpy, mp).wait_recv()
    seconds[1].start()
    seconds[2].start()
    seconds[3].start()
    yield
    done(dpx, c)
    hop(5, at(dpx, 1 - c), dp, pair).wait_recv()
    done(dpx, 1 - c)
    if ready is not None:
        yield
    done(dpy, c)
    hop(6, at(dpy, 1 - c), dp, pair).wait_recv()
    done(dpy, 1 - c)
    if ready is not None:
        yield
    hop(3, from_d.at[part_a], dpy, mp).wait_recv()
    seconds[4].start()
    hop(4, from_d.at[part_b], dpx, mp).wait_recv()
    seconds[5].start()
    done(dpd, c)
    other = at(dpd, 1 - c)
    hop(7, other.at[part_a], dp, pair).wait_recv()
    hop(8, other.at[part_b], dp, pair).wait_recv()
    done(dpd, 1 - c)
    yield
    if ready is None:
        hop(0, at(dp, 1 - c), dp, pair).wait_recv()
        keep.wait()
    for copy in firsts + seconds:
        copy.wait_send()
    yield


def drive(*programs):
    live = list(programs)
    while live:
        for program in list(live):
            try:
                next(program)
            except StopIteration:
                live.remove(program)


def dma(*shape):
    return pltpu.SemaphoreType.DMA(shape)


def params(cid, vmem=40):
    return pltpu.CompilerParams(
        collective_id=cid, has_side_effects=True, vmem_limit_bytes=vmem << 20
    )


def exchange(place, src, out, local, send, recv):
    dp, mp = place.dp, place.mp
    keep = pltpu.make_async_copy(src.at[mp], out.at[mp], local)
    keep.start()
    sends = []
    for hop in range(1, 8):
        target = (mp + hop) % 8
        sends.append(
            remote(src.at[target], out.at[mp], send.at[hop], recv.at[hop], dp, target)
        )
        sends[-1].start()
    yield
    keep.wait()
    for hop in range(1, 8):
        origin = (mp + 8 - hop) % 8
        remote(out.at[origin], out.at[origin], send.at[hop], recv.at[hop], dp, origin).wait_recv()
    for copy in sends:
        copy.wait_send()
    yield


def line_reduce(place, produce, tiles, result, bufs, sems, paired):
    dp, z, c, mp, pair = place.dp, place.z, place.c, place.mp, place.pair
    above_block, below_block, out_block = bufs["above"], bufs["below"], bufs["out"]
    order = [place.zorder(event) for event in (3, 2, 1, 0)]
    inner = jnp.logical_and(z > 0, z < LINE - 1)
    outer = jnp.logical_or(z == 0, z == LINE - 1)

    @pl.when(z == LINE - 1)
    def _():
        above_block[...] = jnp.zeros(above_block.shape, BF)

    @pl.when(z == 0)
    def _():
        below_block[...] = jnp.zeros(below_block.shape, BF)

    def from_above(level):
        return above_block.at[jnp.minimum(level, LINE - 2)]

    def from_below(level):
        return below_block.at[jnp.maximum(level - 1, 0)]

    def across(step, level):
        return remote(
            bufs["pair_out"].at[step % 2],
            bufs["pair_in"].at[level],
            sems["pair_send"].at[step % 2],
            sems["pair_recv"].at[level],
            dp,
            pair,
        )

    if paired:
        for step, level in enumerate(order):
            if step > 1:
                across(step - 2, order[step - 2]).wait_send()
            for rows in tiles:
                bufs["pair_out"][step % 2, rows] = produce(level, 1 - c, rows).astype(BF)
            across(step, level).start()
    yield

    def toward(step, level, act):
        @pl.when(level < z)
        def _():
            act(
                remote(
                    out_block.at[step],
                    from_above(level),
                    sems["line_send"].at[step],
                    sems["above"].at[level],
                    dp,
                    mp - 2,
                )
            )

        @pl.when(level > z)
        def _():
            act(
                remote(
                    out_block.at[step],
                    from_below(level),
                    sems["line_send"].at[step],
                    sems["below"].at[level],
                    dp,
                    mp + 2,
                )
            )

    def arrive(level, above):
        if above:
            remote(
                from_above(level),
                from_above(level),
                sems["line_send"].at[0],
                sems["above"].at[level],
                dp,
                mp,
            ).wait_recv()
        else:
            remote(
                from_below(level),
                from_below(level),
                sems["line_send"].at[0],
                sems["below"].at[level],
                dp,
                mp,
            ).wait_recv()

    def advance(step):
        level = order[step]
        if paired:
            across(step, level).wait_recv()

        @pl.when(jnp.logical_and(level < z, z < LINE - 1))
        def _():
            arrive(level, True)

        @pl.when(jnp.logical_and(level > z, z > 0))
        def _():
            arrive(level, False)

        for rows in tiles:
            total = produce(level, c, rows)
            if paired:
                total = total + bufs["pair_in"][level, rows].astype(F32)

            @pl.when(level < z)
            def _():
                out_block[step, rows] = (total + from_above(level)[rows].astype(F32)).astype(BF)

            @pl.when(level > z)
            def _():
                out_block[step, rows] = (total + from_below(level)[rows].astype(F32)).astype(BF)

        toward(step, level, lambda copy: copy.start())

    advance(0)
    for step in (1, 2):

        @pl.when(outer)
        def _():
            advance(step)

    yield
    for step in (1, 2):

        @pl.when(inner)
        def _():
            advance(step)

        yield

    if paired:
        across(3, z).wait_recv()

    @pl.when(z < LINE - 1)
    def _():
        arrive(z, True)

    @pl.when(z > 0)
    def _():
        arrive(z, False)

    for rows in tiles:
        total = produce(z, c, rows)
        if paired:
            total = total + bufs["pair_in"][z, rows].astype(F32)
        total = total + from_above(z)[rows].astype(F32) + from_below(z)[rows].astype(F32)
        result(rows, total)
    for step, level in enumerate(order):
        if paired and step > 1:
            across(step, level).wait_send()
        if step < 3:
            toward(step, level, lambda copy: copy.wait_send())
    yield


def line_reduce_scratch(rows, cols, paired):
    block = lambda n: pltpu.VMEM((n, rows, cols), BF)
    scratch = {"above": block(3), "below": block(3), "out": block(3)}
    sems = {"line_send": dma(3), "above": dma(4), "below": dma(4)}
    if paired:
        scratch.update({"pair_out": block(2), "pair_in": block(4)})
        sems.update({"pair_send": dma(2), "pair_recv": dma(4)})
    return scratch, sems


def plane_reduce(place, produce, tile, half, result, bufs, sems, paired=True, early=False):
    dp, c, mp, pair = place.dp, place.c, place.mp, place.pair
    dpx, dpy, dpd = place.dpx, place.dpy, place.dpd
    starts = range(0, half, tile)
    send, recv = sems["send"], sems["recv"]
    out_block, landed = bufs["out"], bufs["in"]
    groups = {"far": dpd, "x": dpx, "y": dpy, "own": dp}
    steps = ["x", "y", "far", "own"] if early else ["far", "x", "y", "own"]

    def across(name):
        step = steps.index(name)
        return remote(
            bufs["pair_out"].at[step % 2],
            bufs["pair_in"].at[step],
            sems["pair_send"].at[step % 2],
            sems["pair_recv"].at[step],
            dp,
            pair,
        )

    def cross(name):
        if not paired:
            return
        step = steps.index(name)
        if step > 1:
            across(steps[step - 2]).wait_send()
        bufs["pair_out"][step % 2] = produce(groups[name], 1 - c, 0, 2 * half).astype(BF)
        across(name).start()

    def crossed(name):
        if paired:
            across(name).wait_recv()

    def share(name, start):
        total = produce(groups[name], c, start, tile)
        if paired:
            total = total + bufs["pair_in"][steps.index(name), pl.ds(start, tile)].astype(F32)
        return total

    def hop(index):
        target = (dpx, dpy, dpx, dpx, dpy, dpy)[index]
        return remote(
            out_block.at[index], landed.at[index], send.at[index], recv.at[index], target, mp
        )

    def fill(index, name, base, extra=None):
        for start in starts:
            total = share(name, base + start)
            if extra is not None:
                total = total + landed[extra, pl.ds(start, tile)].astype(F32)
            out_block[index, pl.ds(start, tile)] = total.astype(BF)
        hop(index).start()

    def far():
        crossed("far")
        fill(0, "far", 0)
        fill(1, "far", half)

    def near():
        crossed("x")
        fill(2, "x", 0)
        crossed("y")
        fill(4, "y", half)

    if early:
        cross("x")
        yield
        cross("y")
        near()
        yield
        cross("far")
        far()
        yield
        cross("own")
    else:
        cross("far")
        cross("x")
        yield
        far()
        cross("y")
        near()
        cross("own")
    yield
    hop(1).wait_recv()
    fill(3, "x", half, extra=1)
    hop(0).wait_recv()
    fill(5, "y", 0, extra=0)
    yield
    crossed("own")
    for index in (2, 3, 4, 5):
        hop(index).wait_recv()
    for base, pieces in ((0, (2, 5)), (half, (3, 4))):
        for start in starts:
            total = share("own", base + start)
            for piece in pieces:
                total = total + landed[piece, pl.ds(start, tile)].astype(F32)
            result(pl.ds(base + start, tile), total)
    for index in range(6):
        hop(index).wait_send()
    if paired:
        for name in steps[2:]:
            across(name).wait_send()
    yield


def plane_reduce_scratch(half, cols, paired=True):
    block = lambda n, rows: pltpu.VMEM((n, rows, cols), BF)
    scratch = {"out": block(6, half), "in": block(6, half)}
    sems = {"send": dma(6), "recv": dma(6)}
    if paired:
        scratch.update({"pair_out": block(2, 2 * half), "pair_in": block(4, 2 * half)})
        sems.update({"pair_send": dma(2), "pair_recv": dma(4)})
    return scratch, sems


def project_kernel(
    frames_ref, gain_ref, shift_ref, cot_ref, query_ref, key_ref, value_ref, bias_ref,
    nfull_ref, qkv_ref, cfull_ref, weight_ref,
    normed_ref, local, line_send, line_recv, plane_send, plane_recv,
):
    place = Place()
    weight_ref[...] = jnp.zeros(weight_ref.shape, BF)
    for index, ref in enumerate((query_ref, key_ref, value_ref)):
        for head in range(2):
            weight_ref[pl.ds(index * 256 + head * 128, HD)] = ref[pl.ds(head * HD, HD)]
    for start in range(0, ROWS, 128):
        rows = pl.ds(start, 128)
        normed_ref[rows] = layer_norm(
            frames_ref[rows].astype(F32), gain_ref[...], shift_ref[...]
        ).astype(BF)
    greet(place, line=True, plane=True)

    def ready(slot):
        product = lax.dot_general(
            nfull_ref[slot],
            weight_ref[...],
            (((1,), (1,)), ((), ())),
            preferred_element_type=F32,
        )
        qkv_ref[slot] = (product + bias_ref[...]).astype(BF)

    drive(
        line_gather(
            place, normed_ref, nfull_ref, local.at[0], line_send, line_recv, True, ready
        ),
        plane_gather(place, cot_ref, cfull_ref, local.at[1], plane_send, plane_recv),
    )


def project(frames, gain, shift, cotangent, query, key, value, bias):
    return pl.pallas_call(
        project_kernel,
        out_shape=(
            jax.ShapeDtypeStruct((8,) + frames.shape, BF),
            jax.ShapeDtypeStruct((8, ROWS, 768), BF),
            jax.ShapeDtypeStruct((8,) + cotangent.shape, BF),
            jax.ShapeDtypeStruct((768, 1280), BF),
        ),
        in_specs=[VMEM, VMEM, VMEM, ANY, VMEM, VMEM, VMEM, VMEM],
        out_specs=(VMEM, VMEM, ANY, VMEM),
        scratch_shapes=[pltpu.VMEM((ROWS, 1280), BF), dma(2), dma(4, 3), dma(8), dma(9), dma(9)],
        compiler_params=params(0),
        name="project",
    )(frames, gain, shift, cotangent, query, key, value, bias)


OUTER_STARTS = (0, 48, 96, 112)


def attend_kernel(
    qkv_ref, mask_ref, live_ref, weights_ref, outer_ref, frames_ref, out_bias_ref,
    gain_two_ref, shift_two_ref,
    att_ref, logs_ref, peak_ref, wfull_ref, rows_ref, middle_ref, two_ref,
    out_ref, vt_ref, outer_all, outer_full, local, send, recv, line_send, line_recv,
    outer_send, outer_recv, plane_send, plane_recv,
):
    place = Place()
    greet(place, mp_all=True, plane=True)
    outer = line_gather(
        place, outer_ref, outer_all, local.at[2], outer_send, outer_recv, False, None, 48
    )
    next(outer)
    gather = line_gather(
        place, weights_ref, wfull_ref, local.at[1], line_send, line_recv, False
    )
    next(gather)
    factor = math.log2(math.e) / math.sqrt(HD)
    peak_ref[...] = jnp.full(peak_ref.shape, MASK_VALUE, F32)

    @pl.loop(0, 6)
    def _(turn):
        clip = turn // 2
        head = turn % 2
        lane = pl.multiple_of(head * 128, 128)
        row = pl.multiple_of(head * HD, 16)
        keys = qkv_ref[:, clip, :, pl.ds(256 + lane, 128)].reshape(1024, 128)
        vt_ref[...] = qkv_ref[:, clip, :, pl.ds(512 + lane, 128)].reshape(1024, 128).T

        @pl.loop(0, 4)
        def _(block):
            query = qkv_ref[pl.ds(block * 2, 2), clip, :, pl.ds(lane, 128)].reshape(256, 128)
            columns = pl.ds(pl.multiple_of(block * 256, 256), 256)
            scores = lax.dot_general(
                keys, query, (((1,), (1,)), ((), ())), preferred_element_type=F32
            )
            scores = scores + mask_ref[clip]
            peak = jnp.max(scores, axis=0, keepdims=True)
            powers = jnp.exp2((scores - peak) * factor)
            total = jnp.sum(powers, axis=0, keepdims=True)
            mixed = lax.dot_general(
                vt_ref[...],
                powers.astype(BF),
                (((1,), (0,)), ((), ())),
                preferred_element_type=F32,
            )
            mixed = (mixed / total).astype(BF)
            for part in range(2):
                out_ref[block * 2 + part, clip, pl.ds(row, HD)] = mixed[
                    :HD, part * 128 : part * 128 + 128
                ]
            logs_ref[turn, :, columns] = peak * factor + jnp.log2(total)
            peak_ref[head] = jnp.maximum(
                peak_ref[head], jnp.where(live_ref[clip, :, columns] > 0, peak, MASK_VALUE)
            )

        @pl.when(turn == 2)
        def _():
            next(outer)

        @pl.when(turn == 4)
        def _():
            next(outer)
            next(gather)

    mixing = exchange(place, out_ref, att_ref, local.at[0], send, recv)
    next(mixing)
    for _ in outer:
        pass
    spread = plane_gather(place, outer_all, outer_full, local.at[3], plane_send, plane_recv)
    drive(spread, mixing)
    for level in range(LINE):
        for core in range(2):
            for group, start in enumerate(OUTER_STARTS):
                rows_ref[pl.ds((level * 2 + core) * 160 + start, 48)] = outer_full[
                    group * 2 + core, pl.ds(level * 48, 48)
                ]
    for clip in range(3):
        rows = pl.ds(clip * 128, 128)
        branch = lax.dot_general(
            att_ref[:, clip].reshape(1280, 128),
            rows_ref[...],
            (((0,), (0,)), ((), ())),
            preferred_element_type=F32,
        )
        middle = frames_ref[rows].astype(F32) + (branch + out_bias_ref[...])
        middle_ref[rows] = middle
        two_ref[rows] = layer_norm(middle, gain_two_ref[...], shift_two_ref[...]).astype(BF)
    drive(gather)


def attend(qkv, mask, live, weights, outer, frames, out_bias, gain_two, shift_two):
    return pl.pallas_call(
        attend_kernel,
        out_shape=(
            jax.ShapeDtypeStruct((8, 3, 160, 128), BF),
            jax.ShapeDtypeStruct((6, 1, 1024), F32),
            jax.ShapeDtypeStruct((2, 8, 256), F32),
            jax.ShapeDtypeStruct((4,) + weights.shape, BF),
            jax.ShapeDtypeStruct((1280, 1280), BF),
            jax.ShapeDtypeStruct((ROWS, 1280), F32),
            jax.ShapeDtypeStruct((ROWS, 1280), BF),
        ),
        in_specs=[VMEM, VMEM, VMEM, ANY, ANY, VMEM, VMEM, VMEM, VMEM],
        out_specs=(VMEM, VMEM, VMEM, ANY, VMEM, VMEM, VMEM),
        scratch_shapes=[
            pltpu.VMEM((8, 3, 160, 128), BF),
            pltpu.VMEM((128, 1024), BF),
            pltpu.VMEM((192, 1280), BF),
            pltpu.VMEM((8, 192, 1280), BF),
            dma(4),
            dma(8),
            dma(8),
            dma(4, 3),
            dma(4),
            dma(4, 3),
            dma(4),
            dma(9),
            dma(9),
        ],
        compiler_params=params(1),
        name="attend",
    )(qkv, mask, live, weights, outer, frames, out_bias, gain_two, shift_two)


def flatten(*pairs):
    names, shapes = [], []
    for number, group in enumerate(pairs):
        for name, shape in group.items():
            names.append((number, name))
            shapes.append(shape)

    def split(refs):
        groups = [{} for _ in pairs]
        for (number, name), ref in zip(names, refs):
            groups[number][name] = ref
        return groups

    return shapes, split


def feed_forward_kernel(
    split, normed_ref, upstream_ref, weights_ref, down_ref, bias_ref,
    total_ref, hidden_ref, grads_ref, bias_out, down_all,
    normed_all, upstream_all, slope_all, rate_ref, sum_ref,
    load, local, line_local, gather_send, gather_recv, line_send, line_recv, *scratch,
):
    place = Place()
    bufs, sems = split(scratch)
    loads = []
    for slot in range(8):
        loads.append(
            pltpu.make_async_copy(upstream_ref.at[slot], upstream_all.at[slot], load.at[slot])
        )
        loads[-1].start()
    greet(place, line=True, plane=True)
    bias_out[...] = jnp.zeros(bias_out.shape, F32)

    def up_rows():
        return weights_ref[:, pl.ds(0, 160)].reshape(640, 1280)

    def down_rows():
        return down_all[...].reshape(640, 1280)

    def activate(slot, rows):
        before = (
            lax.dot_general(
                normed_all[slot, rows],
                up_rows(),
                (((1,), (1,)), ((), ())),
                preferred_element_type=F32,
            )
            + bias_ref[...]
        )
        share = 0.5 + 0.5 * lax.erf(before * math.sqrt(0.5))
        hidden_ref[slot, rows] = (before * share).astype(BF)
        density = jnp.exp(before * before * -0.5) * (1.0 / math.sqrt(2.0 * math.pi))
        return share + before * density

    def pull_back(slot, rows, rate):
        pull = lax.dot_general(
            upstream_all[slot, rows],
            down_rows(),
            (((1,), (1,)), ((), ())),
            preferred_element_type=F32,
        )
        slope = (pull * rate).astype(BF)
        slope_all[slot, rows] = slope
        bias_out[...] += jnp.sum(slope.astype(F32), axis=0, keepdims=True)

    here = [place.dp * 2 + place.c, place.dp * 2 + 1 - place.c]
    seen = []

    def ready(slot):
        index = len(seen)
        seen.append(slot)

        rows = pl.ds(0, ROWS)
        rate = activate(slot, rows)
        if index < 2:
            rate_ref[index] = rate
        else:
            pull_back(slot, rows, rate)

        if index < 2:
            next(down)

    def finish_here():
        for index in range(2):
            pull_back(here[index], pl.ds(0, ROWS), rate_ref[index])

    down = line_gather(
        place, down_ref, down_all, line_local, line_send, line_recv, False
    )
    gather = plane_gather(
        place, normed_ref, normed_all, local, gather_send, gather_recv, ready
    )

    def produce(group, core, start, rows):
        return jnp.dot(
            slope_all[group * 2 + core, pl.ds(start, rows)],
            up_rows(),
            preferred_element_type=F32,
        )

    def result(rows, total):
        total_ref[rows] = total

    reduce = plane_reduce(place, produce, 192, 192, result, bufs, sems, True, True)
    next(down)
    next(gather)
    for copy in loads:
        copy.wait()
    next(gather)
    for _ in down:
        pass
    next(gather)
    next(reduce)
    next(gather)
    next(reduce)
    next(gather)
    next(reduce)
    finish_here()
    next(reduce)

    def weight_grads(left_all, right_all, base):
        @pl.loop(0, 8)
        def _(slot):
            product = lax.dot_general(
                left_all[slot],
                right_all[slot],
                (((0,), (0,)), ((), ())),
                preferred_element_type=F32,
            )
            sum_ref[...] = jnp.where(slot == 0, product, sum_ref[...] + product)

        for level in range(4):
            grads_ref[level, pl.ds(base, 160)] = sum_ref[pl.ds(level * 160, 160)].astype(BF)

    weight_grads(slope_all, normed_all, 0)
    next(reduce)
    weight_grads(hidden_ref, upstream_all, 160)
    for level in range(4):
        grads_ref[level, pl.ds(320, 16)] = jnp.zeros((16, 1280), BF)
        grads_ref[level, pl.ds(320, 16), pl.ds(0, 640)] = jnp.broadcast_to(
            bias_out[...], (16, 640)
        ).astype(BF)
    drive(reduce, gather)


def feed_forward(normed, upstream, weights, down, bias):
    shapes, split = flatten(*plane_reduce_scratch(192, 1280))
    return pl.pallas_call(
        functools.partial(feed_forward_kernel, split),
        out_shape=(
            jax.ShapeDtypeStruct((ROWS, 1280), F32),
            jax.ShapeDtypeStruct((8, ROWS, 640), BF),
            jax.ShapeDtypeStruct((4, 336, 1280), BF),
            jax.ShapeDtypeStruct((1, 640), F32),
            jax.ShapeDtypeStruct((4, 160, 1280), BF),
        ),
        in_specs=[ANY, ANY, VMEM, ANY, VMEM],
        out_specs=(VMEM,) * 5,
        scratch_shapes=[
            pltpu.VMEM((8, ROWS, 1280), BF),
            pltpu.VMEM((8, ROWS, 1280), BF),
            pltpu.VMEM((8, ROWS, 640), BF),
            pltpu.VMEM((2, ROWS, 640), F32),
            pltpu.VMEM((640, 1280), F32),
            dma(8),
            pltpu.SemaphoreType.DMA(()),
            pltpu.SemaphoreType.DMA(()),
            dma(9),
            dma(9),
            dma(4, 3),
            dma(4),
            *shapes,
        ],
        compiler_params=params(3, 60),
        name="feed_forward",
    )(normed, upstream, weights, down, bias)


def attend_back_kernel(
    split, qkv_in, mask_ref, logs_ref, pull_ref, hidden_in, weights_ref, feed_grads_in,
    out_grad_in, normed_in, dqkv_ref, feed_ref, feed_sum_ref, out_sum_ref, joined_ref, column_ref,
    hidden_ref, feed_grads_ref, out_grad_ref, normed_ref, load, normed_load,
    grad_ref, kt_ref, dk_ref, dv_ref, block_ref, middle_ref, local, send, recv, *scratch,
):
    place = Place()
    qkv_ref = dqkv_ref
    (
        line_bufs, line_sems, plane_bufs, plane_sems,
        out_plane_bufs, out_plane_sems, out_line_bufs, out_line_sems,
    ) = split(scratch)
    loads = [
        pltpu.make_async_copy(source, target, load.at[index])
        for index, (source, target) in enumerate(
            (
                (out_grad_in, out_grad_ref),
                (feed_grads_in, feed_grads_ref),
                (hidden_in, hidden_ref),
                (qkv_in, qkv_ref),
            )
        )
    ]
    for copy in loads:
        copy.start()
    greet(place, mp_all=True, plane=True)
    scale = 1.0 / math.sqrt(HD)
    factor = math.log2(math.e) * scale
    arriving = exchange(place, pull_ref, grad_ref, local, send, recv)
    next(arriving)

    def feed_block(group, core, start, rows):
        return jnp.dot(
            hidden_ref[group * 2 + core, pl.ds(start, rows)],
            weights_ref[...].reshape(640, 1280),
            preferred_element_type=F32,
        )

    def feed_result(rows, total):
        feed_ref[rows] = total

    def sum_result(rows, total):
        feed_sum_ref[rows] = total

    plane = plane_reduce(
        place, feed_block, 192, 192, feed_result, plane_bufs, plane_sems, True
    )
    line = line_reduce(
        place,
        lambda level, core, rows: feed_grads_ref[level, rows].astype(F32),
        [pl.ds(start, 112) for start in range(0, 336, 112)],
        sum_result,
        line_bufs,
        line_sems,
        False,
    )
    def middle(rows, total):
        middle_ref[rows] = total

    def out_result(rows, total):
        out_sum_ref[rows] = total

    out_plane = plane_reduce(
        place,
        lambda group, core, start, rows: out_grad_ref[group, core, pl.ds(start, rows)].astype(F32),
        96,
        96,
        middle,
        out_plane_bufs,
        out_plane_sems,
    )
    out_line = line_reduce(
        place,
        lambda level, core, rows: middle_ref[
            pl.ds(pl.multiple_of(level * 48 + rows.start, 16), rows.size)
        ],
        [pl.ds(0, 48)],
        out_result,
        out_line_bufs,
        out_line_sems,
        False,
    )
    loads[0].wait()
    next(out_plane)
    next(out_plane)
    loads[2].wait()
    next(plane)
    next(plane)
    loads[1].wait()
    next(line)
    next(line)
    next(out_line)
    loads[3].wait()
    for _ in arriving:
        pass
    block_ref[...] = jnp.zeros(block_ref.shape, BF)

    @pl.loop(0, 6)
    def _(turn):
        clip = turn // 2
        head = turn % 2
        lane = pl.multiple_of(head * 128, 128)
        row = pl.multiple_of(head * HD, 16)
        kt_ref[...] = qkv_ref[:, clip, :, pl.ds(256 + lane, 128)].reshape(1024, 128).T
        dk_ref[...] = jnp.zeros(dk_ref.shape, F32)
        dv_ref[...] = jnp.zeros(dv_ref.shape, F32)

        @pl.loop(0, 4)
        def _(block):
            query = qkv_ref[pl.ds(block * 2, 2), clip, :, pl.ds(lane, 128)].reshape(256, 128)
            values = qkv_ref[:, clip, :, pl.ds(512 + lane, 128)].reshape(1024, 128)
            keys = qkv_ref[:, clip, :, pl.ds(256 + lane, 128)].reshape(1024, 128)
            columns = pl.ds(pl.multiple_of(block * 256, 256), 256)
            for part in range(2):
                block_ref[:HD, part * 128 : part * 128 + 128] = grad_ref[
                    block * 2 + part, clip, pl.ds(row, HD)
                ]
            scores = lax.dot_general(
                keys, query, (((1,), (1,)), ((), ())), preferred_element_type=F32
            )
            chance = jnp.exp2((scores + mask_ref[clip]) * factor - logs_ref[turn, :, columns])
            dv_ref[...] += lax.dot_general(
                chance.astype(BF),
                block_ref[...],
                (((1,), (1,)), ((), ())),
                preferred_element_type=F32,
            )
            slope = lax.dot_general(
                values, block_ref[...], (((1,), (0,)), ((), ())), preferred_element_type=F32
            )
            center = jnp.sum(chance * slope, axis=0, keepdims=True)
            change = (chance * (slope - center)).astype(BF)
            dk_ref[...] += lax.dot_general(
                change, query, (((1,), (0,)), ((), ())), preferred_element_type=F32
            )
            dq = lax.dot_general(
                kt_ref[...], change, (((1,), (0,)), ((), ())), preferred_element_type=F32
            )
            dqkv_ref[pl.ds(block * 2, 2), clip, :, pl.ds(lane, 128)] = (
                (dq.T * scale).astype(BF).reshape(2, 128, 128)
            )

        dqkv_ref[:, clip, :, pl.ds(256 + lane, 128)] = (
            (dk_ref[...] * scale).astype(BF).reshape(8, 128, 128)
        )
        dqkv_ref[:, clip, :, pl.ds(512 + lane, 128)] = (
            dv_ref[...].astype(BF).reshape(8, 128, 128)
        )

        @pl.when(turn == 2)
        def _():
            next(out_plane)
            next(plane)

        @pl.when(turn == 5)
        def _():
            next(out_plane)

    def bring(slot):
        return pltpu.make_async_copy(
            normed_in.at[slot], normed_ref.at[slot % 2], normed_load.at[slot % 2]
        )

    def weight_grad(slot):
        bring(slot).wait()
        if slot < 7:
            bring(slot + 1).start()
        grads = dqkv_ref[slot].reshape(ROWS, 768)
        product = lax.dot_general(
            normed_ref[slot % 2],
            grads,
            (((0,), (0,)), ((), ())),
            preferred_element_type=F32,
        )
        column = jnp.sum(grads.astype(F32), axis=0, keepdims=True)
        if slot == 0:
            joined_ref[...] = product
            column_ref[...] = column
        else:
            joined_ref[...] += product
            column_ref[...] += column

    bring(0).start()
    next(line)
    next(out_line)
    for slot in range(4):
        weight_grad(slot)
    next(line)
    next(out_line)
    for slot in range(4, 8):
        weight_grad(slot)
    drive(line, out_line, plane, out_plane)


def attend_back(qkv, mask, logs, pull, hidden, weights, feed_grads, out_grad, normed):
    shapes, split = flatten(
        *line_reduce_scratch(336, 1280, False),
        *plane_reduce_scratch(192, 1280),
        *plane_reduce_scratch(96, 1280),
        *line_reduce_scratch(48, 1280, False),
    )
    return pl.pallas_call(
        functools.partial(attend_back_kernel, split),
        out_shape=(
            jax.ShapeDtypeStruct(qkv.shape, BF),
            jax.ShapeDtypeStruct((ROWS, 1280), F32),
            jax.ShapeDtypeStruct((336, 1280), F32),
            jax.ShapeDtypeStruct((48, 1280), F32),
            jax.ShapeDtypeStruct((1280, 768), F32),
            jax.ShapeDtypeStruct((1, 768), F32),
        ),
        in_specs=[ANY, VMEM, VMEM, ANY, ANY, VMEM, ANY, ANY, ANY],
        out_specs=(VMEM,) * 6,
        scratch_shapes=[
            *(pltpu.VMEM(ref.shape, BF) for ref in (hidden, feed_grads, out_grad)),
            pltpu.VMEM((2, ROWS, 1280), BF),
            dma(4),
            dma(2),
            pltpu.VMEM((8, 3, 160, 128), BF),
            pltpu.VMEM((128, 1024), BF),
            pltpu.VMEM((1024, 128), F32),
            pltpu.VMEM((1024, 128), F32),
            pltpu.VMEM((128, 256), BF),
            pltpu.VMEM((192, 1280), F32),
            pltpu.SemaphoreType.DMA(()),
            dma(8),
            dma(8),
            *shapes,
        ],
        compiler_params=params(2, 62),
        name="attend_back",
    )(qkv, mask, logs, pull, hidden, weights, feed_grads, out_grad, normed)


GROUP_ROWS = 4832
GROUP_STEP = 4800
PACK_ROWS = GROUP_STEP * 3 + GROUP_ROWS
SEGMENTS = (
    ("query", 0, 1600),
    ("query_bias", 204800, 2),
    ("key", 204960, 1600),
    ("value", 409760, 1600),
    ("value_bias", 614560, 2),
    ("out", 614720, 1600),
    ("up", 819520, 6400),
    ("up_bias", 1638720, 5),
    ("down", 1639360, 6400),
)
PACK_END = 19216
SHARE_ROWS = 4808


def segment_table():
    table, cursor = {}, 0
    for name, start, rows in SEGMENTS:
        row = start // 128
        cursor += 32
        cursor += (row - cursor) % 8
        table[name] = (cursor, row, rows, start % 128)
        cursor += rows
    return table, (cursor + 32 + 7) // 8 * 8


TABLE, STAGE_ROWS = segment_table()


def lane_of(rows):
    return lax.broadcasted_iota(jnp.int32, (rows, 128), 1)


def pack_rows(stage, packed):
    def piece(name, first, rows):
        base, row, _, shift = TABLE[name]
        at = base - row + first
        here = stage[pl.ds(at, rows)]
        if shift == 0:
            return here
        above = stage[pl.ds(at - 1, rows)]
        return jnp.where(
            lane_of(rows) >= shift, pltpu.roll(here, shift, 1), pltpu.roll(above, shift, 1)
        )

    done = set()
    for name, _, _ in SEGMENTS:
        _, row, rows, shift = TABLE[name]
        low = -(-(row + (1 if shift else 0)) // 16) * 16
        high = (row + rows) // 16 * 16
        if high <= low:
            continue
        done.update(range(low, high, 16))
        turns = (high - low) // 128

        @pl.loop(0, turns)
        def _(turn):
            first = pl.multiple_of(low + turn * 128, 16)
            packed[pl.ds(first, 128)] = piece(name, first, 128).astype(BF)

        for first in range(low + turns * 128, high, 16):
            packed[pl.ds(first, 16)] = piece(name, first, 16).astype(BF)
    for first in range(0, PACK_ROWS, 16):
        if first in done:
            continue
        total = jnp.zeros((16, 128), F32)
        for name, _, _ in SEGMENTS:
            _, row, rows, shift = TABLE[name]
            if row < first + 16 and row + rows + (1 if shift else 0) > first:
                total = total + piece(name, first, 16)
        packed[pl.ds(first, 16)] = total.astype(BF)


def stage_wide(stage, name, ref, step):
    base = TABLE[name][0]
    rows, wide = ref.shape[0], ref.shape[1] // 128

    @pl.loop(0, rows // step)
    def _(turn):
        first = pl.multiple_of(turn * step, step)
        for block in range(wide):
            stage[pl.ds(base + first * wide + block, step, stride=wide), :] = ref[
                pl.ds(first, step), pl.ds(block * 128, 128)
            ].astype(F32)


def stage_heads(stage, name, ref, lanes, column):
    base = TABLE[name][0]
    for head in range(2):
        column[head] = ref[:, pl.ds(lanes + head * 128, 128)]

    @pl.loop(0, 5)
    def _(turn):
        lane = lane_of(64)
        rows = [jnp.zeros((64, 128), F32) for _ in range(5)]
        for block in range(8):
            item, head = block // 2, block % 2
            value = column[head, pl.ds(turn * 256 + item, 64, stride=4)]
            offset = block * HD
            first, shift = offset // 128, offset % 128
            if shift:
                value = pltpu.roll(value, shift, 1)
            if shift + HD > 128:
                rows[first] = rows[first] + jnp.where(lane >= shift, value, 0.0)
                rows[first + 1] = rows[first + 1] + jnp.where(
                    lane < shift + HD - 128, value, 0.0
                )
            else:
                rows[first] = rows[first] + value
        for index in range(5):
            stage[pl.ds(base + turn * 320 + index, 64, stride=5), :] = rows[index]


def stage_head_bias(stage, name, ref, lanes):
    base = TABLE[name][0]
    lane = lane_of(1)
    first = ref[0:1, pl.ds(lanes, 128)]
    second = pltpu.roll(ref[0:1, pl.ds(lanes + 128, 128)], HD, 1)
    stage[pl.ds(base, 1)] = first + jnp.where(lane >= HD, second, 0.0)
    stage[pl.ds(base + 1, 1)] = jnp.where(lane < 2 * HD - 128, second, 0.0)


def stage_share(stage, name, ref, first, count, place):
    base = TABLE[name][0] + place.dp * count * 10
    for block in range(10):
        stage[pl.ds(base + block, count, stride=10), :] = ref[
            pl.ds(first, count), pl.ds(block * 128, 128)
        ]


def stage_up(stage, ref, place):
    base = TABLE["up"][0]
    lane = lane_of(128)
    for quarter in range(4):

        @pl.when(place.dp == quarter)
        def _():
            for block in range(10):
                columns = pl.ds(block * 128, 128)
                first = ref[pl.ds(0, 128), columns].T
                second = jnp.where(lane < 32, ref[pl.ds(128, 128), columns].T, 0.0)
                shift = 32 * quarter
                if shift:
                    first = pltpu.roll(first, shift, 1)
                    second = pltpu.roll(second, shift, 1)
                    second = second + jnp.where(lane < shift, first, 0.0)
                    first = jnp.where(lane >= shift, first, 0.0)
                at = base + block * 640 + quarter
                stage[pl.ds(at, 128, stride=5), :] = first
                stage[pl.ds(at + 1, 128, stride=5), :] = second


def norm_back(frames_ref, middle_ref, gain_ref, grad_ref):
    def write(rows, total):
        value = frames_ref[rows].astype(F32)
        center = value - jnp.mean(value, axis=-1, keepdims=True)
        spread = jnp.mean(center * center, axis=-1, keepdims=True)
        root = lax.rsqrt(spread + NORM_EPSILON)
        scaled = center * root
        pull = total * gain_ref[...]
        along = jnp.mean(pull * scaled, axis=-1, keepdims=True)
        grad_ref[rows] = middle_ref[rows] + root * (
            pull - jnp.mean(pull, axis=-1, keepdims=True) - scaled * along
        )

    return write


def fetch(first, rows, sems, grad, weight, frames, middle):
    span = pl.ds(first, rows)
    pairs = (
        (grad[0].at[:, span], grad[1]),
        weight,
        (frames[0].at[span], frames[1]),
        (middle[0].at[span], middle[1]),
    )
    copies = [
        pltpu.make_async_copy(source, target, sems.at[index])
        for index, (source, target) in enumerate(pairs)
    ]
    for copy in copies:
        copy.start()
    return copies


def fetch_scratch(rows):
    return [
        pltpu.VMEM((8, rows, 768), BF),
        pltpu.VMEM((768, 1280), BF),
        pltpu.VMEM((rows, 1280), BF),
        pltpu.VMEM((rows, 1280), F32),
        dma(4),
    ]


def line_product(place, grad_ref, weight_ref, rows, result, bufs, sems):
    def produce(level, core, tile):
        return jnp.dot(
            grad_ref[level * 2 + core, tile],
            weight_ref[...],
            preferred_element_type=F32,
        )

    tiles = [pl.ds(0, rows)]
    return line_reduce(place, produce, tiles, result, bufs, sems, True)


FIRST_ROWS = 128


def finish_kernel(
    split, grad_in, weight_in, joined_ref, bias_ref, bias_column_ref, sum_ref, out_ref,
    up_bias_ref, small_ref, peak_ref, frames_in, middle_in, gain_ref, shift_ref, cap_ref,
    input_grad_ref, grads_ref, small_out, roots_out,
    grad_ref, weight_ref, frames_ref, middle_ref, load,
    stage, packed, sum_rows, column, tiles, small_in, small_all, peak_all, edge,
    local, small_send, small_recv, plane_send, plane_recv, *scratch,
):
    place = Place()
    line_bufs, line_sems, bufs, sems = split(scratch)
    loads = fetch(
        0,
        FIRST_ROWS,
        load,
        (grad_in, grad_ref),
        (weight_in, weight_ref),
        (frames_in, frames_ref),
        (middle_in, middle_ref),
    )
    greet(place, mp_all=True, plane=True)
    peers = (place.dpx, place.dpy, place.dpd)

    def tell(index, source, target, group, act):
        act(
            remote(
                source,
                target.at[place.dp],
                plane_send.at[index],
                plane_recv.at[index],
                group,
                place.mp,
            )
        )

    def heard(index, target, group):
        block = target.at[group]
        remote(
            block, block, plane_send.at[index], plane_recv.at[index], group, place.mp
        ).wait_recv()

    line = line_product(
        place,
        grad_ref,
        weight_ref,
        FIRST_ROWS,
        norm_back(frames_ref, middle_ref, gain_ref, input_grad_ref),
        line_bufs,
        line_sems,
    )
    for index, group in enumerate(peers):
        tell(index, peak_ref, peak_all, group, lambda copy: copy.start())
    for copy in loads:
        copy.wait()

    for block in range(10):
        lanes = pl.ds(block * 128, 128)
        weight = weight_ref[:, lanes].astype(F32)
        turned = joined_ref[lanes].T
        whole = jnp.sum(weight * bias_column_ref[...], axis=0, keepdims=True)
        along = jnp.sum(weight * turned, axis=0, keepdims=True)
        tiles[pl.ds(block, 1)] = (along - shift_ref[:, lanes] * whole) / gain_ref[:, lanes]
        tiles[pl.ds(10 + block, 1)] = whole
    tiles[pl.ds(20, 44)] = small_ref[...]
    for run in range(8):
        edge[run] = tiles[pl.ds(run * 15 // 2, 8)]
    mixing = exchange(place, edge, small_in, local, small_send, small_recv)
    next(mixing)

    stage[...] = jnp.zeros(stage.shape, F32)
    for name, lanes in (("query", 0), ("key", 256), ("value", 512)):
        stage_heads(stage, name, joined_ref, lanes, column)
    stage_head_bias(stage, "query_bias", bias_ref, 0)
    stage_head_bias(stage, "value_bias", bias_ref, 512)
    stage_share(stage, "out", out_ref, 0, 40, place)
    stage_share(stage, "down", sum_ref, 160, 160, place)
    stage_up(stage, sum_ref, place)
    stage[pl.ds(TABLE["up_bias"][0], 5)] = up_bias_ref[...]
    pack_rows(stage, packed)

    def produce(group, core, start, rows):
        first = pl.multiple_of(group * GROUP_STEP + start, 16)
        return packed[pl.ds(first, GROUP_ROWS // 2)].astype(F32)

    def result(rows, total):
        sum_rows[rows] = total

    half = GROUP_ROWS // 2
    plane = plane_reduce(place, produce, half, half, result, bufs, sems, False)
    next(plane)
    next(plane)
    next(line)
    next(line)
    for _ in mixing:
        pass
    small_all[place.dp] = jnp.sum(small_in[...], axis=0)
    for index, group in enumerate(peers):
        tell(3 + index, small_all.at[place.dp], small_all, group, lambda copy: copy.start())
    next(plane)
    next(line)
    next(line)
    drive(line, plane)
    for index, group in enumerate(peers):
        heard(index, peak_all, group)
        heard(3 + index, small_all, group)
    top = peak_ref[...]
    for group in peers:
        top = jnp.maximum(top, peak_all[group])
    for head in range(2):
        peak = jnp.max(jnp.max(top[head], axis=0, keepdims=True), axis=1, keepdims=True)
        root = jnp.sqrt(cap_ref[...] / jnp.maximum(peak * (1.0 / math.sqrt(HD)), cap_ref[...]))
        roots_out[head] = jnp.broadcast_to(jnp.where(place.dp == 0, root, 1.0), (8, 128))
    whole = jnp.sum(small_all[...], axis=0)
    lane = lane_of(8)
    row = lax.broadcasted_iota(jnp.int32, (8, 128), 0)
    tiles[...] = jnp.zeros((64, 128), F32)
    tiles[pl.ds(8, 8)] = whole
    ahead = pltpu.roll(tiles[pl.ds(9, 8)], 64, 1)
    here = pltpu.roll(whole, 64, 1)
    odd = jnp.where(lane < 64, here, ahead)
    run_of = jnp.where(place.c == 1, odd, whole)
    run_of = jnp.where(jnp.logical_and(row == 7, lane >= 64), 0.0, run_of)
    small_out[...] = run_of
    tiles[pl.ds(8, 8)] = run_of
    wide = lane_of(16)
    entry = jnp.where(
        wide >= 64, pltpu.roll(tiles[pl.ds(1, 16)], 64, 1), pltpu.roll(tiles[pl.ds(0, 16)], 64, 1)
    )

    @pl.when(place.dp == 3)
    def _():
        sum_rows[pl.ds(GROUP_STEP, 16)] += entry

    for group in range(4):

        @pl.when(place.dp == group)
        def _():
            down, shift = 480 * group // 128, 480 * group % 128
            if shift == 0:
                grads_ref[...] = sum_rows[pl.ds(0, SHARE_ROWS)]
            else:
                for first in range(0, SHARE_ROWS, 1208):
                    size = min(1208, SHARE_ROWS - first)
                    grads_ref[pl.ds(first, size)] = jnp.where(
                        lane_of(size) < 128 - shift,
                        pltpu.roll(sum_rows[pl.ds(first + down, size)], 128 - shift, 1),
                        pltpu.roll(sum_rows[pl.ds(first + down + 1, size)], 128 - shift, 1),
                    )

    for index, group in enumerate(peers):
        tell(index, peak_ref, peak_all, group, lambda copy: copy.wait_send())
        tell(3 + index, small_all.at[place.dp], small_all, group, lambda copy: copy.wait_send())


def finish(grads, weight, joined, bias, sums, out, up_bias, small, peaks, frames, middle, gain, shift, cap):
    shapes, split = flatten(
        *line_reduce_scratch(FIRST_ROWS, 1280, True),
        *plane_reduce_scratch(GROUP_ROWS // 2, 128, False),
    )
    return pl.pallas_call(
        functools.partial(finish_kernel, split),
        out_shape=(
            jax.ShapeDtypeStruct((FIRST_ROWS, 1280), F32),
            jax.ShapeDtypeStruct((SHARE_ROWS, 128), F32),
            jax.ShapeDtypeStruct((8, 128), F32),
            jax.ShapeDtypeStruct((2, 8, 128), F32),
        ),
        in_specs=[ANY, ANY] + [VMEM] * 8 + [ANY, ANY, VMEM, VMEM, VMEM],
        out_specs=(VMEM,) * 4,
        scratch_shapes=[
            *fetch_scratch(FIRST_ROWS),
            pltpu.VMEM((STAGE_ROWS, 128), F32),
            pltpu.VMEM((PACK_ROWS, 128), BF),
            pltpu.VMEM((GROUP_ROWS, 128), F32),
            pltpu.VMEM((2, 1280, 128), F32),
            pltpu.VMEM((64, 128), F32),
            pltpu.VMEM((8, 8, 128), F32),
            pltpu.VMEM((4, 8, 128), F32),
            pltpu.VMEM((4,) + peaks.shape, F32),
            pltpu.VMEM((8, 8, 128), F32),
            pltpu.SemaphoreType.DMA(()),
            dma(8),
            dma(8),
            dma(6),
            dma(6),
            *shapes,
        ],
        compiler_params=params(7, 62),
        name="finish",
    )(
        grads, weight, joined, bias[None], bias[:, None], sums, out, up_bias, small, peaks,
        frames, middle, gain, shift, cap,
    )


def share_master_kernel(
    split, rows_ref, grad_in, weight_in, frames_in, middle_in, gain_ref,
    whole_out, input_grad_ref,
    grad_ref, weight_ref, frames_ref, middle_ref, load,
    whole_ref, parts, turned, store, send, recv, *scratch,
):
    place = Place()
    line_bufs, line_sems = split(scratch)
    loads = fetch(
        FIRST_ROWS,
        ROWS - FIRST_ROWS,
        load,
        (grad_in, grad_ref),
        (weight_in, weight_ref),
        (frames_in, frames_ref),
        (middle_in, middle_ref),
    )
    greet(place, line=True, plane=True)
    line = line_product(
        place,
        grad_ref,
        weight_ref,
        ROWS - FIRST_ROWS,
        norm_back(frames_ref, middle_ref, gain_ref, input_grad_ref),
        line_bufs,
        line_sems,
    )
    dp, mp, dpx, dpy, dpd = place.dp, place.mp, place.dpx, place.dpy, place.dpd
    half = GROUP_ROWS // 2
    part_a, part_b = pl.ds(0, half), pl.ds(half, half)
    for group in range(4):

        @pl.when(dp == group)
        def _():
            down, shift = 480 * group // 128, 480 * group % 128
            turned[pl.ds(0, 16)] = jnp.zeros((16, 128), F32)
            turned[pl.ds(16, SHARE_ROWS)] = rows_ref[...]
            turned[pl.ds(16 + SHARE_ROWS, 24)] = jnp.zeros((24, 128), F32)
            for first in range(0, GROUP_ROWS, 1208):
                here = turned[pl.ds(16 + first - down, 1208)]
                if shift:
                    here = jnp.where(
                        lane_of(1208) >= shift,
                        pltpu.roll(here, shift, 1),
                        pltpu.roll(turned[pl.ds(15 + first - down, 1208)], shift, 1),
                    )
                parts[dp, pl.ds(first, 1208)] = here.astype(BF)


    def hop(index, block, target):
        return remote(block, block, send.at[index], recv.at[index], target, mp)

    own = parts.at[dp]
    sends = [hop(0, own, dpx), hop(1, own, dpy)]
    for copy in sends:
        copy.start()

    stores = []

    def keep(index, first, rows):
        span = pl.ds(pl.multiple_of(first, 16), rows)
        stores.append(
            pltpu.make_async_copy(whole_ref.at[span], whole_out.at[span], store.at[index])
        )
        stores[-1].start()

    def unpack(group):
        for start in range(32, GROUP_STEP, 2384):
            at = pl.multiple_of(group * GROUP_STEP + start, 16)
            whole_ref[pl.ds(at, 2384)] = parts[group, pl.ds(start, 2384)].astype(F32)
        keep(len(stores), group * GROUP_STEP + 32, GROUP_STEP - 32)

    for copy in loads:
        copy.wait()
    next(line)
    next(line)
    unpack(dp)
    hop(0, parts.at[dpx], dpx).wait_recv()
    sends.append(hop(2, parts.at[dpx, part_a], dpy))
    sends[-1].start()
    hop(1, parts.at[dpy], dpy).wait_recv()
    sends.append(hop(3, parts.at[dpy, part_b], dpx))
    sends[-1].start()
    unpack(dpx)
    unpack(dpy)
    next(line)
    next(line)
    hop(2, parts.at[dpd, part_a], dpy).wait_recv()
    hop(3, parts.at[dpd, part_b], dpx).wait_recv()
    unpack(dpd)
    for group in range(4):
        first = parts[group, pl.ds(0, 32)].astype(F32)
        if group > 0:
            first = first + parts[group - 1, pl.ds(GROUP_STEP, 32)].astype(F32)
        whole_ref[pl.ds(group * GROUP_STEP, 32)] = first
        keep(4 + group, group * GROUP_STEP, 32)
    whole_ref[pl.ds(4 * GROUP_STEP, 16)] = parts[3, pl.ds(GROUP_STEP, 16)].astype(F32)
    keep(8, 4 * GROUP_STEP, 16)
    for copy in sends:
        copy.wait_send()
    drive(line)
    for copy in stores:
        copy.wait()


def share_master(rows, grads, weight, frames, middle, gain):
    shapes, split = flatten(*line_reduce_scratch(ROWS - FIRST_ROWS, 1280, True))
    return pl.pallas_call(
        functools.partial(share_master_kernel, split),
        out_shape=(
            jax.ShapeDtypeStruct((PACK_END, 128), F32),
            jax.ShapeDtypeStruct((ROWS - FIRST_ROWS, 1280), F32),
        ),
        in_specs=[VMEM, ANY, ANY, ANY, ANY, VMEM],
        out_specs=(ANY, VMEM),
        scratch_shapes=[
            *fetch_scratch(ROWS - FIRST_ROWS),
            pltpu.VMEM((PACK_END, 128), F32),
            pltpu.VMEM((4, GROUP_ROWS, 128), BF),
            pltpu.VMEM((SHARE_ROWS + 40, 128), F32),
            dma(9),
            dma(4),
            dma(4),
            *shapes,
        ],
        compiler_params=params(8, 60),
        name="share_master",
    )(rows, grads, weight, frames, middle, gain)


STEP_ENTRIES = 1024 * 76


def optimize_kernel(
    rates_ref, roots_ref, grads_ref, master_ref, first_ref, second_ref,
    owned_out, master_out, first_out, second_out, padded_out,
):
    entry = lax.broadcasted_iota(jnp.int32, (1, STEP_ENTRIES), 1)
    entry = entry + pl.program_id(0) * STEP_ENTRIES
    grads = grads_ref[...]
    first = BETA_FIRST * first_ref[...] + (1.0 - BETA_FIRST) * grads
    second = BETA_SECOND * second_ref[...] + (1.0 - BETA_SECOND) * grads * grads
    change = first * rates_ref[0] / (jnp.sqrt(second * rates_ref[1]) + ADAM_EPSILON)
    block = jnp.floor((entry.astype(F32) + 0.5) * (1.0 / HD))
    odd = block - 2.0 * jnp.floor(block * 0.5) > 0.5
    factor = jnp.where(
        entry < KEY_END, jnp.where(odd, roots_ref[1, 0:1, 0:1], roots_ref[0, 0:1, 0:1]), 1.0
    )
    master = (master_ref[...] * rates_ref[2] - change) * factor
    owned_out[...] = grads
    master_out[...] = master
    first_out[...] = first
    second_out[...] = second
    padded_out[...] = jnp.where(entry < SHARE_ENTRIES, master, 0.0)


KEY_END = 409760
SHARE_ENTRIES = 614880


def optimize(rates, roots, grads, master, first, second):
    block = pl.BlockSpec((1, STEP_ENTRIES), lambda step: (0, step))
    share = jax.ShapeDtypeStruct((1, SHARE_ENTRIES), F32)
    return pl.pallas_call(
        optimize_kernel,
        grid=(pl.cdiv(SHARE_ENTRIES, STEP_ENTRIES),),
        out_shape=(share,) * 4 + (jax.ShapeDtypeStruct((1, SHARE_ROWS * 128), F32),),
        in_specs=[
            pl.BlockSpec(memory_space=pltpu.SMEM),
            pl.BlockSpec((2, 8, 128), lambda step: (0, 0, 0)),
        ]
        + [block] * 4,
        out_specs=(block,) * 5,
        compiler_params=pltpu.CompilerParams(vmem_limit_bytes=62 << 20),
        name="optimize",
    )(rates, roots, grads, master, first, second)


def fast_body(
    frames,
    lengths,
    key_mask,
    cotangent,
    gain_one,
    shift_one,
    query_weight,
    query_bias,
    key_weight,
    value_weight,
    value_bias,
    out_weight,
    out_bias,
    gain_two,
    shift_two,
    up_weight,
    up_bias,
    down_weight,
    down_bias,
    master,
    moment_one,
    moment_two,
    adam_step,
    hyper_rates,
):
    group = lax.axis_index("dp")
    position = jnp.arange(1024, dtype=jnp.int32)
    keep_query = position[None, :] < lengths[:, None]
    keep_key = jnp.logical_and(keep_query, key_mask == 1)
    mask = jnp.where(keep_key, 0.0, MASK_VALUE)[:, :, None]
    live = keep_query.astype(F32)[:, None, :]
    gain_first = gain_one.astype(F32)
    shift_first = shift_one.astype(F32)
    gain_second = gain_two.astype(F32)
    shift_second = shift_two.astype(F32)
    inputs = frames.transpose(1, 0, 2).reshape(ROWS, 1280).astype(F32)
    upstream_low = cotangent.transpose(1, 0, 2).reshape(ROWS, 1280)
    upstream = upstream_low.astype(F32)
    def head_lanes(bias):
        lanes = bias.astype(F32).reshape(2, HD)
        return jnp.pad(lanes, ((0, 0), (0, 128 - HD))).reshape(256)

    joined_bias = jnp.concatenate(
        [head_lanes(query_bias), jnp.zeros((256,), F32), head_lanes(value_bias)]
    )[None]
    frame_rows = frames.transpose(1, 0, 2).reshape(ROWS, 1280)
    quarter = group * 160
    up_share = lax.dynamic_slice_in_dim(up_weight, quarter, 160, 1).T
    down_share = lax.dynamic_slice_in_dim(down_weight, quarter, 160, 0)
    bias_share = lax.dynamic_slice_in_dim(up_bias, quarter, 160, 0)
    bias_rows = jnp.pad(bias_share[None], ((0, 15), (0, 1280 - 160)))
    message = jnp.concatenate([up_share, bias_rows])
    outer_start = jnp.minimum(group * 48, 112)
    outer = lax.dynamic_slice_in_dim(out_weight, outer_start, 48, 0)
    normed_full, qkv, upstream_full, joined_weight = project(
        frame_rows,
        gain_first[None],
        shift_first[None],
        upstream_low,
        query_weight.T,
        key_weight.T,
        value_weight.T,
        joined_bias,
    )
    qkv = qkv.reshape(8, 3, 128, 768)
    attended, logs, peaks, gathered, out_rows, middle, normed_two = attend(
        qkv,
        mask,
        live,
        message,
        outer,
        frame_rows,
        out_bias.astype(F32)[None],
        gain_second[None],
        shift_second[None],
    )
    up_lanes = gathered[:, 160, :160].reshape(1, 640).astype(F32)
    out_rows = out_rows.reshape(8, 160, 1280)

    normed_two_grad, hidden, feed_grads, _, down_all = feed_forward(
        normed_two, upstream_full, gathered, down_share, up_lanes
    )

    _, norm_two_pull = jax.vjp(layer_norm, middle, gain_second, shift_second)
    middle_norm_grad, gain_two_grad, shift_two_grad = norm_two_pull(normed_two_grad)
    middle_grad = upstream + middle_norm_grad
    branch_grad = middle_grad.astype(BF)
    branch_clips = branch_grad.reshape(3, 128, 1280)
    out_grad = jnp.einsum("schr,crd->shd", attended, branch_clips, preferred_element_type=F32)
    attended_grad = jnp.einsum(
        "shd,crd->schr", out_rows, branch_clips, preferred_element_type=F32
    ).astype(BF)
    out_quarters = jnp.pad(
        out_grad.astype(BF).reshape(4, 2, 4, 40, 1280), ((0, 0),) * 3 + ((0, 8), (0, 0))
    )
    out_quarters = out_quarters.transpose(2, 1, 0, 3, 4).reshape(4, 2, 192, 1280)
    joined_grad, feed, feed_sum, out_sum, joined_weight_grad, joined_bias_grad = attend_back(
        qkv, mask, logs, attended_grad, hidden, down_all, feed_grads, out_quarters, normed_full
    )
    layer_out = (middle + feed + down_bias.astype(F32)).astype(BF)
    joined_grad = joined_grad.reshape(8, ROWS, 768)
    joined_bias_grad = joined_bias_grad[0]

    level = lax.axis_index("mp") // 2
    up_bias_share = lax.dynamic_slice_in_dim(feed_sum[320], level * 160, 160, 0)
    up_bias_rows = lax.dynamic_update_slice(
        jnp.zeros((640,), F32), up_bias_share, (quarter,)
    ).reshape(5, 128)
    small_rows = jnp.concatenate(
        [
            jnp.sum(branch_grad.astype(F32), axis=0),
            gain_two_grad,
            shift_two_grad,
            jnp.sum(upstream, axis=0),
            jnp.zeros((512,), F32),
        ]
    ).reshape(44, 128)
    first_grad, grad_rows, small_sum, roots = finish(
        joined_grad,
        joined_weight,
        joined_weight_grad,
        joined_bias_grad,
        feed_sum,
        out_sum,
        up_bias_rows,
        small_rows,
        peaks,
        frame_rows,
        middle_grad,
        gain_first[None],
        shift_first[None],
        hyper_rates[2].reshape(1, 1),
    )
    small_total = small_sum.reshape(1024)[:960]
    learn_rate = hyper_rates[0]
    weight_decay = hyper_rates[1]
    step_count = adam_step[0].astype(F32)
    rates = jnp.stack(
        [
            learn_rate / (1.0 - jnp.power(BETA_FIRST, step_count)),
            1.0 / (1.0 - jnp.power(BETA_SECOND, step_count)),
            1.0 - learn_rate * weight_decay,
        ]
    )
    owned_grads, master_new, first_new, second_new, padded = optimize(
        rates, roots, grad_rows.reshape(1, SHARE_ROWS * 128), master, moment_one, moment_two
    )
    whole, second_grad = share_master(
        padded.reshape(SHARE_ROWS, 128),
        joined_grad,
        joined_weight,
        frame_rows,
        middle_grad,
        gain_first[None],
    )
    input_grad = jnp.concatenate([first_grad, second_grad])
    whole = lax.optimization_barrier(whole.reshape(1, PACK_END * 128))
    weights_new = whole[:, : 4 * SHARE_ENTRIES].astype(BF)
    return (
        layer_out.reshape(3, 128, 1280).transpose(1, 0, 2),
        input_grad.reshape(3, 128, 1280).transpose(1, 0, 2),
        owned_grads,
        master_new,
        first_new,
        second_new,
        weights_new,
        small_total,
    )


def body(
    frames,
    lengths,
    key_mask,
    cotangent,
    gain_one,
    shift_one,
    query_weight,
    query_bias,
    key_weight,
    value_weight,
    value_bias,
    out_weight,
    out_bias,
    gain_two,
    shift_two,
    up_weight,
    up_bias,
    down_weight,
    down_bias,
    master,
    moment_one,
    moment_two,
    adam_step,
    hyper_rates,
):
    local_rows, clip_count, model_width = frames.shape
    total_rows = key_mask.shape[1]
    head_cols = query_weight.shape[1]
    heads_here = head_cols // HD
    block_rows = min(512, total_rows)
    blocks = total_rows // block_rows
    score_scale = 1.0 / math.sqrt(HD)
    position = jnp.arange(total_rows, dtype=jnp.int32)
    keep_query = position[None, :] < lengths[:, None]
    keep_key = jnp.logical_and(keep_query, key_mask == 1)
    gain_first = gain_one.astype(jnp.float32)
    shift_first = shift_one.astype(jnp.float32)
    gain_second = gain_two.astype(jnp.float32)
    shift_second = shift_two.astype(jnp.float32)
    inputs = frames.astype(jnp.float32)
    normed = layer_norm(inputs, gain_first, shift_first).astype(jnp.bfloat16)
    joined_weight = jnp.concatenate([query_weight, key_weight, value_weight], axis=1)
    joined_bias = jnp.concatenate(
        [
            query_bias.astype(jnp.float32),
            jnp.zeros((head_cols,), jnp.float32),
            value_bias.astype(jnp.float32),
        ]
    )
    normed_full = lax.all_gather(normed, "mp", axis=0, tiled=True)
    projected = (
        jnp.einsum("rcd,de->rce", normed_full, joined_weight, preferred_element_type=jnp.float32)
        + joined_bias
    ).astype(jnp.bfloat16)
    query = projected[:, :, :head_cols].reshape(total_rows, clip_count, heads_here, HD)
    keys = projected[:, :, head_cols : 2 * head_cols].reshape(
        total_rows, clip_count, heads_here, HD
    )
    values = projected[:, :, 2 * head_cols :].reshape(total_rows, clip_count, heads_here, HD)

    def scores_of(row_start):
        query_block = lax.dynamic_slice_in_dim(query, row_start, block_rows, 0)
        raw_scores = (
            jnp.einsum("qchd,kchd->chqk", query_block, keys, preferred_element_type=jnp.float32)
            * score_scale
        )
        return (query_block, jnp.where(keep_key[:, None, None, :], raw_scores, MASK_VALUE))

    def forward_block(block_index):
        row_start = block_index * block_rows
        _, masked = scores_of(row_start)
        row_peak = jnp.max(masked, axis=-1, keepdims=True)
        exp_scores = jnp.exp(masked - row_peak)
        row_total = jnp.sum(exp_scores, axis=-1, keepdims=True)
        probability = (exp_scores / row_total).astype(jnp.bfloat16)
        attended = jnp.einsum(
            "chqk,kchd->qchd", probability, values, preferred_element_type=jnp.float32
        ).astype(jnp.bfloat16)
        live_rows = lax.dynamic_slice_in_dim(keep_query, row_start, block_rows, 1)
        block_peak = jnp.max(
            jnp.where(live_rows[:, None, :], row_peak[..., 0], MASK_VALUE), axis=(0, 2)
        )
        return (attended, (row_peak + jnp.log(row_total))[..., 0], block_peak)

    attended_blocks, log_totals, block_peaks = lax.map(forward_block, jnp.arange(blocks))
    attended_full = attended_blocks.reshape(total_rows, clip_count, head_cols)
    head_peak = lax.pmax(jnp.max(block_peaks, axis=0), "dp")
    rows_here = attended_full
    attn_branch = lax.psum_scatter(
        jnp.einsum("rck,kd->rcd", rows_here, out_weight, preferred_element_type=jnp.float32),
        "mp",
        scatter_dimension=0,
        tiled=True,
    ) + out_bias.astype(jnp.float32)
    middle = inputs + attn_branch
    normed_two = layer_norm(middle, gain_second, shift_second).astype(jnp.bfloat16)
    upstream = cotangent.astype(jnp.float32)
    normed_two_full = lax.all_gather(normed_two, "mp", axis=0, tiled=True)
    before = jnp.einsum(
        "rcd,df->rcf", normed_two_full, up_weight, preferred_element_type=jnp.float32
    ) + up_bias.astype(jnp.float32)
    hidden = exact_gelu(before).astype(jnp.bfloat16)
    rows_here = hidden
    feed = lax.psum_scatter(
        jnp.einsum(
            "rcf,fd->rcd", rows_here, down_weight, preferred_element_type=jnp.float32
        ).astype(jnp.bfloat16),
        "mp",
        scatter_dimension=0,
        tiled=True,
    ).astype(jnp.float32) + down_bias.astype(jnp.float32)
    layer_out = (middle + feed).astype(jnp.bfloat16)
    feed_grad_full = lax.all_gather(cotangent, "mp", axis=0, tiled=True)
    down_grad = jnp.einsum(
        "rcf,rcd->fd", hidden, feed_grad_full, preferred_element_type=jnp.float32
    )
    hidden_grad = jnp.einsum(
        "rcd,fd->rcf", feed_grad_full, down_weight, preferred_element_type=jnp.float32
    )
    _, gelu_pull = jax.vjp(exact_gelu, before)
    before_grad = gelu_pull(hidden_grad)[0].astype(jnp.bfloat16)
    up_bias_grad = jnp.sum(before_grad.astype(jnp.float32), axis=(0, 1))
    up_grad = jnp.einsum(
        "rcd,rcf->df", normed_two_full, before_grad, preferred_element_type=jnp.float32
    )
    rows_here = before_grad
    normed_two_grad = lax.psum_scatter(
        jnp.einsum("rcf,df->rcd", rows_here, up_weight, preferred_element_type=jnp.float32),
        "mp",
        scatter_dimension=0,
        tiled=True,
    )
    _, norm_two_pull = jax.vjp(layer_norm, middle, gain_second, shift_second)
    middle_norm_grad, gain_two_grad, shift_two_grad = norm_two_pull(normed_two_grad)
    middle_grad = upstream + middle_norm_grad
    branch_grad = middle_grad.astype(jnp.bfloat16)
    branch_grad_full = lax.all_gather(branch_grad, "mp", axis=0, tiled=True)
    out_grad = jnp.einsum(
        "rck,rcd->kd", attended_full, branch_grad_full, preferred_element_type=jnp.float32
    )
    attended_grad = jnp.einsum(
        "rcd,kd->rck", branch_grad_full, out_weight, preferred_element_type=jnp.float32
    ).astype(jnp.bfloat16)
    attended_grad = attended_grad.reshape(total_rows, clip_count, heads_here, HD)

    def backward_block(carry, block_index):
        key_total, value_total = carry
        row_start = block_index * block_rows
        query_block, masked = scores_of(row_start)
        log_total = log_totals[block_index]
        probability = jnp.exp(masked - log_total[..., None])
        grad_block = lax.dynamic_slice_in_dim(attended_grad, row_start, block_rows, 0)
        value_total = value_total + jnp.einsum(
            "chqk,qchd->kchd",
            probability.astype(jnp.bfloat16),
            grad_block,
            preferred_element_type=jnp.float32,
        )
        prob_grad = jnp.einsum(
            "qchd,kchd->chqk", grad_block, values, preferred_element_type=jnp.float32
        )
        score_grad = (
            probability * (prob_grad - jnp.sum(probability * prob_grad, axis=-1, keepdims=True))
        ).astype(jnp.bfloat16)
        query_grad = (
            jnp.einsum("chqk,kchd->qchd", score_grad, keys, preferred_element_type=jnp.float32)
            * score_scale
        ).astype(jnp.bfloat16)
        key_total = (
            key_total
            + jnp.einsum(
                "chqk,qchd->kchd", score_grad, query_block, preferred_element_type=jnp.float32
            )
            * score_scale
        )
        return ((key_total, value_total), query_grad)

    empty_grad = jnp.zeros((total_rows, clip_count, heads_here, HD), jnp.float32)
    (key_total, value_total), query_blocks = lax.scan(
        backward_block, (empty_grad, empty_grad), jnp.arange(blocks)
    )
    joined_grad = jnp.concatenate(
        [
            query_blocks.reshape(total_rows, clip_count, head_cols),
            key_total.reshape(total_rows, clip_count, head_cols).astype(jnp.bfloat16),
            value_total.reshape(total_rows, clip_count, head_cols).astype(jnp.bfloat16),
        ],
        axis=-1,
    )
    joined_bias_grad = jnp.sum(joined_grad.astype(jnp.float32), axis=(0, 1))
    normed_back = lax.all_gather(normed, "mp", axis=0, tiled=True)
    joined_weight_grad = jnp.einsum(
        "rcd,rce->de", normed_back, joined_grad, preferred_element_type=jnp.float32
    )
    rows_here = joined_grad
    normed_grad = lax.psum_scatter(
        jnp.einsum(
            "rce,de->rcd", rows_here, joined_weight, preferred_element_type=jnp.float32
        ).astype(jnp.bfloat16),
        "mp",
        scatter_dimension=0,
        tiled=True,
    ).astype(jnp.float32)
    _, norm_one_pull = jax.vjp(layer_norm, inputs, gain_first, shift_first)
    input_norm_grad, gain_one_grad, shift_one_grad = norm_one_pull(normed_grad)
    input_grad = middle_grad + input_norm_grad
    out_bias_grad = jnp.sum(branch_grad.astype(jnp.float32), axis=(0, 1))
    down_bias_grad = jnp.sum(upstream, axis=(0, 1))
    small_terms = jnp.concatenate(
        [
            gain_one_grad,
            shift_one_grad,
            out_bias_grad,
            gain_two_grad,
            shift_two_grad,
            down_bias_grad,
        ]
    )
    small_share = lax.psum_scatter(small_terms, "mp", scatter_dimension=0, tiled=True)
    small_total = lax.psum(small_share, "dp")
    packed = jnp.concatenate(
        [
            joined_weight_grad[:, :head_cols].reshape(-1),
            joined_bias_grad[:head_cols],
            joined_weight_grad[:, head_cols : 2 * head_cols].reshape(-1),
            joined_weight_grad[:, 2 * head_cols :].reshape(-1),
            joined_bias_grad[2 * head_cols :],
            out_grad.reshape(-1),
            up_grad.reshape(-1),
            up_bias_grad,
            down_grad.reshape(-1),
            small_share,
        ]
    )
    owned_grads = lax.psum_scatter(
        packed.astype(jnp.bfloat16), "dp", scatter_dimension=0, tiled=True
    ).astype(jnp.float32)
    share_size = owned_grads.shape[0]
    learn_rate = hyper_rates[0]
    weight_decay = hyper_rates[1]
    logit_cap = hyper_rates[2]
    step_count = adam_step[0].astype(jnp.float32)
    first_new = BETA_FIRST * moment_one[0] + (1.0 - BETA_FIRST) * owned_grads
    second_new = BETA_SECOND * moment_two[0] + (1.0 - BETA_SECOND) * owned_grads * owned_grads
    first_hat = first_new / (1.0 - jnp.power(BETA_FIRST, step_count))
    second_hat = second_new / (1.0 - jnp.power(BETA_SECOND, step_count))
    entry_index = lax.axis_index("dp") * share_size + jnp.arange(share_size, dtype=jnp.int32)
    query_end = model_width * head_cols
    query_bias_end = query_end + head_cols
    key_end = query_bias_end + model_width * head_cols
    column = jnp.where(
        entry_index < query_end,
        entry_index % head_cols,
        jnp.where(
            entry_index < query_bias_end,
            entry_index - query_end,
            (entry_index - query_bias_end) % head_cols,
        ),
    )
    head_index = column // HD
    root_factor = jnp.sqrt(logit_cap / jnp.maximum(head_peak, logit_cap))
    head_factor = jnp.zeros((share_size,), jnp.float32)
    for head_number in range(heads_here):
        head_factor = head_factor + jnp.where(
            head_index == head_number, root_factor[head_number], 0.0
        )
    factor = jnp.where(entry_index < key_end, head_factor, 1.0)
    master_here = master[0]
    master_new = (
        master_here
        - learn_rate
        * (first_hat / (jnp.sqrt(second_hat) + ADAM_EPSILON) + weight_decay * master_here)
    ) * factor
    weights_full = lax.all_gather(master_new.astype(jnp.bfloat16), "dp", axis=0, tiled=True)
    return (
        layer_out,
        input_grad,
        owned_grads[None],
        master_new[None],
        first_new[None],
        second_new[None],
        weights_full[None],
        small_total,
    )


def solution(mesh):
    chosen = fast_body if dict(mesh.shape) == {"dp": 4, "mp": 8} else body
    placed = (
        P("mp", "dp", None),
        P("dp"),
        P("dp", None),
        P("mp", "dp", None),
        P(),
        P(),
        P(None, "mp"),
        P("mp"),
        P(None, "mp"),
        P(None, "mp"),
        P("mp"),
        P("mp", None),
        P(),
        P(),
        P(),
        P(None, "mp"),
        P("mp"),
        P("mp", None),
        P(),
        P("mp", "dp"),
        P("mp", "dp"),
        P("mp", "dp"),
        P(),
        P(),
    )
    return jax.shard_map(
        chosen,
        mesh=mesh,
        in_specs=placed,
        out_specs=(
            P("mp", "dp", None),
            P("mp", "dp", None),
            P("mp", "dp"),
            P("mp", "dp"),
            P("mp", "dp"),
            P("mp", "dp"),
            P("mp", None),
            P("mp"),
        ),
        check_vma=False,
    )
```

```python
import functools
import math

import jax
import jax.numpy as jnp
from jax import lax
from jax.experimental import pallas as pl
from jax.experimental.pallas import tpu as pltpu
from jax.sharding import PartitionSpec as P

HD = 80


NORM_EPSILON = 1e-05
ADAM_EPSILON = 1e-08
BETA_FIRST = 0.9
BETA_SECOND = 0.999
MASK_VALUE = -1e30


def layer_norm(value, gain, shift):
    center = value - jnp.mean(value, axis=-1, keepdims=True)
    spread = jnp.mean(center * center, axis=-1, keepdims=True)
    return center * lax.rsqrt(spread + NORM_EPSILON) * gain + shift


def exact_gelu(argument):
    return jax.nn.gelu(argument, approximate=False)


MESH = pl.DeviceIdType.MESH
ANY = pl.BlockSpec(memory_space=pl.ANY)
VMEM = pl.BlockSpec(memory_space=pltpu.VMEM)
LINE = 4
ROWS = 384
BF = jnp.bfloat16
F32 = jnp.float32


class Place:
    def __init__(self):
        self.dp = lax.axis_index("dp")
        self.mp = lax.axis_index("mp")
        self.z = self.mp // 2
        self.c = self.mp % 2
        self.pair = self.z * 2 + 1 - self.c
        self.dpx = self.dp + 1 - 2 * (self.dp % 2)
        self.dpy = (self.dp + 2) % 4
        self.dpd = 3 - self.dp

    def zorder(self, event):
        if event == 0:
            return self.z
        if event == 1:
            return self.z + 1 - 2 * (self.z % 2)
        if event == 2:
            return 2 - self.z // 2
        return 3 - 3 * (self.z // 2)


def greet(place, mp_all=False, line=False, plane=False, pair=True):
    barrier = pltpu.get_barrier_semaphore()
    count = 0

    def signal(dp, mp):
        pl.semaphore_signal(barrier, inc=1, device_id=(dp, mp), device_id_type=MESH)

    if mp_all:
        for hop in range(1, 8):
            signal(place.dp, (place.mp + hop) % 8)
        count += 7
    else:
        if pair:
            signal(place.dp, place.pair)
            count += 1
        if line:

            @pl.when(place.z > 0)
            def _():
                signal(place.dp, place.mp - 2)

            @pl.when(place.z < LINE - 1)
            def _():
                signal(place.dp, place.mp + 2)

    if plane:
        for other in (place.dpx, place.dpy, place.dpd):
            signal(other, place.mp)
        count += 3
    if line and not mp_all:
        pl.semaphore_wait(barrier, count + 1 + (place.z + 1) // 2 % 2)
    else:
        pl.semaphore_wait(barrier, count)


def remote(src, dst, send, recv, dp, mp):
    return pltpu.make_async_remote_copy(
        src_ref=src,
        dst_ref=dst,
        send_sem=send,
        recv_sem=recv,
        device_id=(dp, mp),
        device_id_type=MESH,
    )


def line_gather(place, src, out, local, send, recv, paired, ready=None, rows=None):
    dp, z, c, mp, pair = place.dp, place.z, place.c, place.mp, place.pair

    def at(slot):
        if rows is None:
            return out.at[slot]
        return out.at[pl.ds(pl.multiple_of(slot * rows, 16), rows)]

    def slot_of(level, core):
        return level * 2 + core if paired else level

    def hop(event, slot, source, direction, target):
        return remote(source, at(slot), send.at[event, direction], recv.at[slot], dp, target)

    own = slot_of(z, c)
    keep = pltpu.make_async_copy(src, at(own), local)
    keep.start()

    def ways(event, level, slot, source, act):
        up = z < LINE - 1
        down = z > 0
        if event > 0:
            up = jnp.logical_and(up, level < z)
            down = jnp.logical_and(down, level > z)

        @pl.when(up)
        def _():
            act(hop(event, slot, source, 1, mp + 2))

        @pl.when(down)
        def _():
            act(hop(event, slot, source, 2, mp - 2))

        if paired:
            act(hop(event, slot, source, 0, pair))

    ways(0, z, own, src, lambda copy: copy.start())
    yield
    if ready is not None:
        keep.wait()
        ready(own)
        if paired:
            other = slot_of(z, 1 - c)
            hop(0, other, at(other), 0, pair).wait_recv()
            ready(other)

    def settle(event):
        level = place.zorder(event)
        ready(slot_of(level, c))
        if paired:
            other = slot_of(level, 1 - c)
            hop(event, other, at(other), 0, pair).wait_recv()
            ready(other)

    for event in range(1, LINE):
        level = place.zorder(event)
        slot = slot_of(level, c)
        hop(event, slot, at(slot), 0, pair).wait_recv()
        ways(event, level, slot, at(slot), lambda copy: copy.start())
        if ready is not None and event > 1:
            if event == 2:
                settle(1)
            settle(event)
        yield
    if ready is None:
        if paired:
            for level in range(LINE):
                other = slot_of(level, 1 - c)
                hop(0, other, at(other), 0, pair).wait_recv()
        keep.wait()
    for event in range(LINE):
        level = place.zorder(event)
        slot = slot_of(level, c)
        ways(event, level, slot, at(slot), lambda copy: copy.wait_send())
    yield


def plane_gather(place, src, out, local, send, recv, ready=None, primed=False):
    dp, c, mp, pair = place.dp, place.c, place.mp, place.pair
    dpx, dpy, dpd = place.dpx, place.dpy, place.dpd
    half = src.shape[0] // 2
    part_a, part_b = pl.ds(0, half), pl.ds(half, half)

    def at(group, core):
        return out.at[group * 2 + core]

    def hop(index, block, group, target):
        return remote(block, block, send.at[index], recv.at[index], group, target)

    def done(group, core):
        if ready is not None:
            ready(group * 2 + core)

    keep = pltpu.make_async_copy(src, at(dp, c), local)
    here = at(dp, c)
    from_x, from_y, from_d = at(dpx, c), at(dpy, c), at(dpd, c)
    firsts = [
        remote(src, here, send.at[0], recv.at[0], dp, pair),
        remote(src, here, send.at[1], recv.at[1], dpx, mp),
        remote(src, here, send.at[2], recv.at[2], dpy, mp),
    ]
    seconds = [
        hop(3, from_x.at[part_a], dpy, mp),
        hop(4, from_y.at[part_b], dpx, mp),
        hop(5, from_x, dp, pair),
        hop(6, from_y, dp, pair),
        hop(7, from_d.at[part_a], dp, pair),
        hop(8, from_d.at[part_b], dp, pair),
    ]
    if primed:
        yield
    keep.start()
    for copy in firsts:
        copy.start()
    yield
    if ready is not None:
        keep.wait()
        done(dp, c)
        hop(0, at(dp, 1 - c), dp, pair).wait_recv()
        done(dp, 1 - c)
    hop(1, from_x, dpx, mp).wait_recv()
    seconds[0].start()
    hop(2, from_y, dpy, mp).wait_recv()
    seconds[1].start()
    seconds[2].start()
    seconds[3].start()
    yield
    done(dpx, c)
    hop(5, at(dpx, 1 - c), dp, pair).wait_recv()
    done(dpx, 1 - c)
    if ready is not None:
        yield
    done(dpy, c)
    hop(6, at(dpy, 1 - c), dp, pair).wait_recv()
    done(dpy, 1 - c)
    if ready is not None:
        yield
    hop(3, from_d.at[part_a], dpy, mp).wait_recv()
    seconds[4].start()
    hop(4, from_d.at[part_b], dpx, mp).wait_recv()
    seconds[5].start()
    done(dpd, c)
    other = at(dpd, 1 - c)
    hop(7, other.at[part_a], dp, pair).wait_recv()
    hop(8, other.at[part_b], dp, pair).wait_recv()
    done(dpd, 1 - c)
    yield
    if ready is None:
        hop(0, at(dp, 1 - c), dp, pair).wait_recv()
        keep.wait()
    for copy in firsts + seconds:
        copy.wait_send()
    yield


def drive(*programs):
    live = list(programs)
    while live:
        for program in list(live):
            try:
                next(program)
            except StopIteration:
                live.remove(program)


def dma(*shape):
    return pltpu.SemaphoreType.DMA(shape)


def params(cid, vmem=40):
    return pltpu.CompilerParams(
        collective_id=cid, has_side_effects=True, vmem_limit_bytes=vmem << 20
    )


def exchange(place, src, out, local, send, recv):
    dp, mp = place.dp, place.mp
    keep = pltpu.make_async_copy(src.at[mp], out.at[mp], local)
    keep.start()
    sends = []
    for hop in range(1, 8):
        target = (mp + hop) % 8
        sends.append(
            remote(src.at[target], out.at[mp], send.at[hop], recv.at[hop], dp, target)
        )
        sends[-1].start()
    yield
    keep.wait()
    for hop in range(1, 8):
        origin = (mp + 8 - hop) % 8
        remote(out.at[origin], out.at[origin], send.at[hop], recv.at[hop], dp, origin).wait_recv()
    for copy in sends:
        copy.wait_send()
    yield


def line_reduce(place, produce, tiles, result, bufs, sems, paired):
    dp, z, c, mp, pair = place.dp, place.z, place.c, place.mp, place.pair
    above_block, below_block, out_block = bufs["above"], bufs["below"], bufs["out"]
    order = [place.zorder(event) for event in (3, 2, 1, 0)]
    inner = jnp.logical_and(z > 0, z < LINE - 1)
    outer = jnp.logical_or(z == 0, z == LINE - 1)

    @pl.when(z == LINE - 1)
    def _():
        above_block[...] = jnp.zeros(above_block.shape, BF)

    @pl.when(z == 0)
    def _():
        below_block[...] = jnp.zeros(below_block.shape, BF)

    def from_above(level):
        return above_block.at[jnp.minimum(level, LINE - 2)]

    def from_below(level):
        return below_block.at[jnp.maximum(level - 1, 0)]

    def across(step, level):
        return remote(
            bufs["pair_out"].at[step % 2],
            bufs["pair_in"].at[level],
            sems["pair_send"].at[step % 2],
            sems["pair_recv"].at[level],
            dp,
            pair,
        )

    if paired:
        for step, level in enumerate(order):
            if step > 1:
                across(step - 2, order[step - 2]).wait_send()
            for rows in tiles:
                bufs["pair_out"][step % 2, rows] = produce(level, 1 - c, rows).astype(BF)
            across(step, level).start()
    yield

    def toward(step, level, act):
        @pl.when(level < z)
        def _():
            act(
                remote(
                    out_block.at[step],
                    from_above(level),
                    sems["line_send"].at[step],
                    sems["above"].at[level],
                    dp,
                    mp - 2,
                )
            )

        @pl.when(level > z)
        def _():
            act(
                remote(
                    out_block.at[step],
                    from_below(level),
                    sems["line_send"].at[step],
                    sems["below"].at[level],
                    dp,
                    mp + 2,
                )
            )

    def arrive(level, above):
        if above:
            remote(
                from_above(level),
                from_above(level),
                sems["line_send"].at[0],
                sems["above"].at[level],
                dp,
                mp,
            ).wait_recv()
        else:
            remote(
                from_below(level),
                from_below(level),
                sems["line_send"].at[0],
                sems["below"].at[level],
                dp,
                mp,
            ).wait_recv()

    def advance(step):
        level = order[step]
        if paired:
            across(step, level).wait_recv()

        @pl.when(jnp.logical_and(level < z, z < LINE - 1))
        def _():
            arrive(level, True)

        @pl.when(jnp.logical_and(level > z, z > 0))
        def _():
            arrive(level, False)

        for rows in tiles:
            total = produce(level, c, rows)
            if paired:
                total = total + bufs["pair_in"][level, rows].astype(F32)

            @pl.when(level < z)
            def _():
                out_block[step, rows] = (total + from_above(level)[rows].astype(F32)).astype(BF)

            @pl.when(level > z)
            def _():
                out_block[step, rows] = (total + from_below(level)[rows].astype(F32)).astype(BF)

        toward(step, level, lambda copy: copy.start())

    advance(0)
    for step in (1, 2):

        @pl.when(outer)
        def _():
            advance(step)

    yield
    for step in (1, 2):

        @pl.when(inner)
        def _():
            advance(step)

        yield

    if paired:
        across(3, z).wait_recv()

    @pl.when(z < LINE - 1)
    def _():
        arrive(z, True)

    @pl.when(z > 0)
    def _():
        arrive(z, False)

    for rows in tiles:
        total = produce(z, c, rows)
        if paired:
            total = total + bufs["pair_in"][z, rows].astype(F32)
        total = total + from_above(z)[rows].astype(F32) + from_below(z)[rows].astype(F32)
        result(rows, total)
    for step, level in enumerate(order):
        if paired and step > 1:
            across(step, level).wait_send()
        if step < 3:
            toward(step, level, lambda copy: copy.wait_send())
    yield


def line_reduce_scratch(rows, cols, paired):
    block = lambda n: pltpu.VMEM((n, rows, cols), BF)
    scratch = {"above": block(3), "below": block(3), "out": block(3)}
    sems = {"line_send": dma(3), "above": dma(4), "below": dma(4)}
    if paired:
        scratch.update({"pair_out": block(2), "pair_in": block(4)})
        sems.update({"pair_send": dma(2), "pair_recv": dma(4)})
    return scratch, sems


def plane_reduce(place, produce, tile, half, result, bufs, sems, paired=True, early=False):
    dp, c, mp, pair = place.dp, place.c, place.mp, place.pair
    dpx, dpy, dpd = place.dpx, place.dpy, place.dpd
    starts = range(0, half, tile)
    send, recv = sems["send"], sems["recv"]
    out_block, landed = bufs["out"], bufs["in"]
    groups = {"far": dpd, "x": dpx, "y": dpy, "own": dp}
    steps = ["x", "y", "far", "own"] if early else ["far", "x", "y", "own"]

    def across(name):
        step = steps.index(name)
        return remote(
            bufs["pair_out"].at[step % 2],
            bufs["pair_in"].at[step],
            sems["pair_send"].at[step % 2],
            sems["pair_recv"].at[step],
            dp,
            pair,
        )

    def cross(name):
        if not paired:
            return
        step = steps.index(name)
        if step > 1:
            across(steps[step - 2]).wait_send()
        bufs["pair_out"][step % 2] = produce(groups[name], 1 - c, 0, 2 * half).astype(BF)
        across(name).start()

    def crossed(name):
        if paired:
            across(name).wait_recv()

    def share(name, start):
        total = produce(groups[name], c, start, tile)
        if paired:
            total = total + bufs["pair_in"][steps.index(name), pl.ds(start, tile)].astype(F32)
        return total

    def hop(index):
        target = (dpx, dpy, dpx, dpx, dpy, dpy)[index]
        return remote(
            out_block.at[index], landed.at[index], send.at[index], recv.at[index], target, mp
        )

    def fill(index, name, base, extra=None):
        for start in starts:
            total = share(name, base + start)
            if extra is not None:
                total = total + landed[extra, pl.ds(start, tile)].astype(F32)
            out_block[index, pl.ds(start, tile)] = total.astype(BF)
        hop(index).start()

    def far():
        crossed("far")
        fill(0, "far", 0)
        fill(1, "far", half)

    def near():
        crossed("x")
        fill(2, "x", 0)
        crossed("y")
        fill(4, "y", half)

    if early:
        cross("x")
        yield
        cross("y")
        near()
        yield
        cross("far")
        far()
        yield
        cross("own")
    else:
        cross("far")
        cross("x")
        yield
        far()
        cross("y")
        near()
        cross("own")
    yield
    hop(1).wait_recv()
    fill(3, "x", half, extra=1)
    hop(0).wait_recv()
    fill(5, "y", 0, extra=0)
    yield
    crossed("own")
    for index in (2, 3, 4, 5):
        hop(index).wait_recv()
    for base, pieces in ((0, (2, 5)), (half, (3, 4))):
        for start in starts:
            total = share("own", base + start)
            for piece in pieces:
                total = total + landed[piece, pl.ds(start, tile)].astype(F32)
            result(pl.ds(base + start, tile), total)
    for index in range(6):
        hop(index).wait_send()
    if paired:
        for name in steps[2:]:
            across(name).wait_send()
    yield


def plane_reduce_scratch(half, cols, paired=True):
    block = lambda n, rows: pltpu.VMEM((n, rows, cols), BF)
    scratch = {"out": block(6, half), "in": block(6, half)}
    sems = {"send": dma(6), "recv": dma(6)}
    if paired:
        scratch.update({"pair_out": block(2, 2 * half), "pair_in": block(4, 2 * half)})
        sems.update({"pair_send": dma(2), "pair_recv": dma(4)})
    return scratch, sems


def project_kernel(
    frames_ref, gain_ref, shift_ref, cot_ref, query_ref, key_ref, value_ref, bias_ref,
    nfull_ref, qkv_ref, cfull_ref, weight_ref,
    normed_ref, local, line_send, line_recv, plane_send, plane_recv,
):
    place = Place()
    weight_ref[...] = jnp.zeros(weight_ref.shape, BF)
    for index, ref in enumerate((query_ref, key_ref, value_ref)):
        for head in range(2):
            weight_ref[pl.ds(index * 256 + head * 128, HD)] = ref[pl.ds(head * HD, HD)]
    for start in range(0, ROWS, 128):
        rows = pl.ds(start, 128)
        normed_ref[rows] = layer_norm(
            frames_ref[rows].astype(F32), gain_ref[...], shift_ref[...]
        ).astype(BF)
    greet(place, line=True, plane=True)

    def ready(slot):
        product = lax.dot_general(
            nfull_ref[slot],
            weight_ref[...],
            (((1,), (1,)), ((), ())),
            preferred_element_type=F32,
        )
        qkv_ref[slot] = (product + bias_ref[...]).astype(BF)

    drive(
        line_gather(
            place, normed_ref, nfull_ref, local.at[0], line_send, line_recv, True, ready
        ),
        plane_gather(place, cot_ref, cfull_ref, local.at[1], plane_send, plane_recv),
    )


def project(frames, gain, shift, cotangent, query, key, value, bias):
    return pl.pallas_call(
        project_kernel,
        out_shape=(
            jax.ShapeDtypeStruct((8,) + frames.shape, BF),
            jax.ShapeDtypeStruct((8, ROWS, 768), BF),
            jax.ShapeDtypeStruct((8,) + cotangent.shape, BF),
            jax.ShapeDtypeStruct((768, 1280), BF),
        ),
        in_specs=[VMEM, VMEM, VMEM, ANY, VMEM, VMEM, VMEM, VMEM],
        out_specs=(VMEM, VMEM, ANY, VMEM),
        scratch_shapes=[pltpu.VMEM((ROWS, 1280), BF), dma(2), dma(4, 3), dma(8), dma(9), dma(9)],
        compiler_params=params(0),
        name="project",
    )(frames, gain, shift, cotangent, query, key, value, bias)


OUTER_STARTS = (0, 48, 96, 112)


def attend_kernel(
    qkv_ref, mask_ref, live_ref, weights_ref, outer_ref, frames_ref, out_bias_ref,
    gain_two_ref, shift_two_ref,
    att_ref, logs_ref, peak_ref, wfull_ref, rows_ref, middle_ref, two_ref,
    out_ref, vt_ref, outer_all, outer_full, local, send, recv, line_send, line_recv,
    outer_send, outer_recv, plane_send, plane_recv,
):
    place = Place()
    greet(place, mp_all=True, plane=True)
    outer = line_gather(
        place, outer_ref, outer_all, local.at[2], outer_send, outer_recv, False, None, 48
    )
    next(outer)
    gather = line_gather(
        place, weights_ref, wfull_ref, local.at[1], line_send, line_recv, False
    )
    next(gather)
    factor = math.log2(math.e) / math.sqrt(HD)
    peak_ref[...] = jnp.full(peak_ref.shape, MASK_VALUE, F32)

    @pl.loop(0, 6)
    def _(turn):
        clip = turn // 2
        head = turn % 2
        lane = pl.multiple_of(head * 128, 128)
        row = pl.multiple_of(head * HD, 16)
        keys = qkv_ref[:, clip, :, pl.ds(256 + lane, 128)].reshape(1024, 128)
        vt_ref[...] = qkv_ref[:, clip, :, pl.ds(512 + lane, 128)].reshape(1024, 128).T

        @pl.loop(0, 4)
        def _(block):
            query = qkv_ref[pl.ds(block * 2, 2), clip, :, pl.ds(lane, 128)].reshape(256, 128)
            columns = pl.ds(pl.multiple_of(block * 256, 256), 256)
            scores = lax.dot_general(
                keys, query, (((1,), (1,)), ((), ())), preferred_element_type=F32
            )
            scores = scores + mask_ref[clip]
            peak = jnp.max(scores, axis=0, keepdims=True)
            powers = jnp.exp2((scores - peak) * factor)
            total = jnp.sum(powers, axis=0, keepdims=True)
            mixed = lax.dot_general(
                vt_ref[...],
                powers.astype(BF),
                (((1,), (0,)), ((), ())),
                preferred_element_type=F32,
            )
            mixed = (mixed / total).astype(BF)
            for part in range(2):
                out_ref[block * 2 + part, clip, pl.ds(row, HD)] = mixed[
                    :HD, part * 128 : part * 128 + 128
                ]
            logs_ref[turn, :, columns] = peak * factor + jnp.log2(total)
            peak_ref[head] = jnp.maximum(
                peak_ref[head], jnp.where(live_ref[clip, :, columns] > 0, peak, MASK_VALUE)
            )

        @pl.when(turn == 2)
        def _():
            next(outer)

        @pl.when(turn == 4)
        def _():
            next(outer)
            next(gather)

    mixing = exchange(place, out_ref, att_ref, local.at[0], send, recv)
    next(mixing)
    for _ in outer:
        pass
    spread = plane_gather(place, outer_all, outer_full, local.at[3], plane_send, plane_recv)
    drive(spread, mixing)
    for level in range(LINE):
        for core in range(2):
            for group, start in enumerate(OUTER_STARTS):
                rows_ref[pl.ds((level * 2 + core) * 160 + start, 48)] = outer_full[
                    group * 2 + core, pl.ds(level * 48, 48)
                ]
    mixed = jnp.concatenate([att_ref[:, clip].reshape(1280, 128) for clip in range(3)], axis=1)
    middle_ref[...] = lax.dot_general(
        mixed, rows_ref[...], (((0,), (0,)), ((), ())), preferred_element_type=F32
    )
    for start in range(0, ROWS, 128):
        rows = pl.ds(start, 128)
        middle = frames_ref[rows].astype(F32) + (middle_ref[rows] + out_bias_ref[...])
        middle_ref[rows] = middle
        two_ref[rows] = layer_norm(middle, gain_two_ref[...], shift_two_ref[...]).astype(BF)
    drive(gather)


def attend(qkv, mask, live, weights, outer, frames, out_bias, gain_two, shift_two):
    return pl.pallas_call(
        attend_kernel,
        out_shape=(
            jax.ShapeDtypeStruct((8, 3, 160, 128), BF),
            jax.ShapeDtypeStruct((6, 1, 1024), F32),
            jax.ShapeDtypeStruct((2, 8, 256), F32),
            jax.ShapeDtypeStruct((4,) + weights.shape, BF),
            jax.ShapeDtypeStruct((1280, 1280), BF),
            jax.ShapeDtypeStruct((ROWS, 1280), F32),
            jax.ShapeDtypeStruct((ROWS, 1280), BF),
        ),
        in_specs=[VMEM, VMEM, VMEM, ANY, ANY, VMEM, VMEM, VMEM, VMEM],
        out_specs=(VMEM, VMEM, VMEM, ANY, VMEM, VMEM, VMEM),
        scratch_shapes=[
            pltpu.VMEM((8, 3, 160, 128), BF),
            pltpu.VMEM((128, 1024), BF),
            pltpu.VMEM((192, 1280), BF),
            pltpu.VMEM((8, 192, 1280), BF),
            dma(4),
            dma(8),
            dma(8),
            dma(4, 3),
            dma(4),
            dma(4, 3),
            dma(4),
            dma(9),
            dma(9),
        ],
        compiler_params=params(1),
        name="attend",
    )(qkv, mask, live, weights, outer, frames, out_bias, gain_two, shift_two)


def flatten(*pairs):
    names, shapes = [], []
    for number, group in enumerate(pairs):
        for name, shape in group.items():
            names.append((number, name))
            shapes.append(shape)

    def split(refs):
        groups = [{} for _ in pairs]
        for (number, name), ref in zip(names, refs):
            groups[number][name] = ref
        return groups

    return shapes, split


def feed_forward_kernel(
    split, normed_ref, upstream_ref, weights_ref, down_ref, bias_ref,
    total_ref, hidden_ref, grads_ref, bias_out, down_all,
    normed_all, upstream_all, slope_all, rate_ref, sum_ref,
    load, local, line_local, gather_send, gather_recv, line_send, line_recv, *scratch,
):
    place = Place()
    bufs, sems = split(scratch)
    loads = []
    for slot in range(8):
        loads.append(
            pltpu.make_async_copy(upstream_ref.at[slot], upstream_all.at[slot], load.at[slot])
        )
        loads[-1].start()
    greet(place, line=True, plane=True)
    bias_out[...] = jnp.zeros(bias_out.shape, F32)

    def up_rows():
        return weights_ref[:, pl.ds(0, 160)].reshape(640, 1280)

    def down_rows():
        return down_all[...].reshape(640, 1280)

    def activate(slot, rows):
        before = (
            lax.dot_general(
                normed_all[slot, rows],
                up_rows(),
                (((1,), (1,)), ((), ())),
                preferred_element_type=F32,
            )
            + bias_ref[...]
        )
        share = 0.5 + 0.5 * lax.erf(before * math.sqrt(0.5))
        hidden_ref[slot, rows] = (before * share).astype(BF)
        density = jnp.exp(before * before * -0.5) * (1.0 / math.sqrt(2.0 * math.pi))
        return share + before * density

    def pull_back(slot, rows, rate):
        pull = lax.dot_general(
            upstream_all[slot, rows],
            down_rows(),
            (((1,), (1,)), ((), ())),
            preferred_element_type=F32,
        )
        slope = (pull * rate).astype(BF)
        slope_all[slot, rows] = slope
        bias_out[...] += jnp.sum(slope.astype(F32), axis=0, keepdims=True)

    here = [place.dp * 2 + place.c, place.dp * 2 + 1 - place.c]
    seen = []

    def ready(slot):
        index = len(seen)
        seen.append(slot)

        rows = pl.ds(0, ROWS)
        rate = activate(slot, rows)
        if index < 2:
            rate_ref[index] = rate
        else:
            pull_back(slot, rows, rate)

        if index < 2:
            next(down)

    def finish_here():
        for index in range(2):
            pull_back(here[index], pl.ds(0, ROWS), rate_ref[index])

    down = line_gather(
        place, down_ref, down_all, line_local, line_send, line_recv, False
    )
    gather = plane_gather(
        place, normed_ref, normed_all, local, gather_send, gather_recv, ready
    )

    def produce(group, core, start, rows):
        return jnp.dot(
            slope_all[group * 2 + core, pl.ds(start, rows)],
            up_rows(),
            preferred_element_type=F32,
        )

    def result(rows, total):
        total_ref[rows] = total

    reduce = plane_reduce(place, produce, 192, 192, result, bufs, sems, True, True)
    next(down)
    next(gather)
    for copy in loads:
        copy.wait()
    next(gather)
    for _ in down:
        pass
    next(gather)
    next(reduce)
    next(gather)
    next(reduce)
    next(gather)
    next(reduce)
    finish_here()
    next(reduce)

    def weight_grads(left_all, right_all, base):
        @pl.loop(0, 8)
        def _(slot):
            product = lax.dot_general(
                left_all[slot],
                right_all[slot],
                (((0,), (0,)), ((), ())),
                preferred_element_type=F32,
            )
            sum_ref[...] = jnp.where(slot == 0, product, sum_ref[...] + product)

        for level in range(4):
            grads_ref[level, pl.ds(base, 160)] = sum_ref[pl.ds(level * 160, 160)].astype(BF)

    weight_grads(slope_all, normed_all, 0)
    next(reduce)
    weight_grads(hidden_ref, upstream_all, 160)
    for level in range(4):
        grads_ref[level, pl.ds(320, 16)] = jnp.zeros((16, 1280), BF)
        grads_ref[level, pl.ds(320, 16), pl.ds(0, 640)] = jnp.broadcast_to(
            bias_out[...], (16, 640)
        ).astype(BF)
    drive(reduce, gather)


def feed_forward(normed, upstream, weights, down, bias):
    shapes, split = flatten(*plane_reduce_scratch(192, 1280))
    return pl.pallas_call(
        functools.partial(feed_forward_kernel, split),
        out_shape=(
            jax.ShapeDtypeStruct((ROWS, 1280), F32),
            jax.ShapeDtypeStruct((8, ROWS, 640), BF),
            jax.ShapeDtypeStruct((4, 336, 1280), BF),
            jax.ShapeDtypeStruct((1, 640), F32),
            jax.ShapeDtypeStruct((4, 160, 1280), BF),
        ),
        in_specs=[ANY, ANY, VMEM, ANY, VMEM],
        out_specs=(VMEM,) * 5,
        scratch_shapes=[
            pltpu.VMEM((8, ROWS, 1280), BF),
            pltpu.VMEM((8, ROWS, 1280), BF),
            pltpu.VMEM((8, ROWS, 640), BF),
            pltpu.VMEM((2, ROWS, 640), F32),
            pltpu.VMEM((640, 1280), F32),
            dma(8),
            pltpu.SemaphoreType.DMA(()),
            pltpu.SemaphoreType.DMA(()),
            dma(9),
            dma(9),
            dma(4, 3),
            dma(4),
            *shapes,
        ],
        compiler_params=params(3, 60),
        name="feed_forward",
    )(normed, upstream, weights, down, bias)


def attend_back_kernel(
    split, qkv_in, mask_ref, logs_ref, pull_ref, hidden_in, weights_ref, feed_grads_in,
    out_grad_in, normed_in, dqkv_ref, feed_ref, feed_sum_ref, out_sum_ref, joined_ref, column_ref,
    hidden_ref, feed_grads_ref, out_grad_ref, normed_ref, load, normed_load,
    grad_ref, kt_ref, dk_ref, dv_ref, block_ref, middle_ref, local, send, recv, *scratch,
):
    place = Place()
    qkv_ref = dqkv_ref
    (
        line_bufs, line_sems, plane_bufs, plane_sems,
        out_plane_bufs, out_plane_sems, out_line_bufs, out_line_sems,
    ) = split(scratch)
    loads = [
        pltpu.make_async_copy(source, target, load.at[index])
        for index, (source, target) in enumerate(
            (
                (out_grad_in, out_grad_ref),
                (feed_grads_in, feed_grads_ref),
                (hidden_in, hidden_ref),
                (qkv_in, qkv_ref),
            )
        )
    ]
    for copy in loads:
        copy.start()
    greet(place, mp_all=True, plane=True)
    scale = 1.0 / math.sqrt(HD)
    factor = math.log2(math.e) * scale
    arriving = exchange(place, pull_ref, grad_ref, local, send, recv)
    next(arriving)

    def feed_block(group, core, start, rows):
        return jnp.dot(
            hidden_ref[group * 2 + core, pl.ds(start, rows)],
            weights_ref[...].reshape(640, 1280),
            preferred_element_type=F32,
        )

    def feed_result(rows, total):
        feed_ref[rows] = total

    def sum_result(rows, total):
        feed_sum_ref[rows] = total

    plane = plane_reduce(
        place, feed_block, 192, 192, feed_result, plane_bufs, plane_sems, True
    )
    line = line_reduce(
        place,
        lambda level, core, rows: feed_grads_ref[level, rows].astype(F32),
        [pl.ds(start, 112) for start in range(0, 336, 112)],
        sum_result,
        line_bufs,
        line_sems,
        False,
    )
    def middle(rows, total):
        middle_ref[rows] = total

    def out_result(rows, total):
        out_sum_ref[rows] = total

    out_plane = plane_reduce(
        place,
        lambda group, core, start, rows: out_grad_ref[group, core, pl.ds(start, rows)].astype(F32),
        96,
        96,
        middle,
        out_plane_bufs,
        out_plane_sems,
    )
    out_line = line_reduce(
        place,
        lambda level, core, rows: middle_ref[
            pl.ds(pl.multiple_of(level * 48 + rows.start, 16), rows.size)
        ],
        [pl.ds(0, 48)],
        out_result,
        out_line_bufs,
        out_line_sems,
        False,
    )
    loads[0].wait()
    next(out_plane)
    next(out_plane)
    loads[2].wait()
    next(plane)
    next(plane)
    loads[1].wait()
    next(line)
    next(line)
    next(out_line)
    loads[3].wait()
    for _ in arriving:
        pass
    block_ref[...] = jnp.zeros(block_ref.shape, BF)

    @pl.loop(0, 6)
    def _(turn):
        clip = turn // 2
        head = turn % 2
        lane = pl.multiple_of(head * 128, 128)
        row = pl.multiple_of(head * HD, 16)
        kt_ref[...] = qkv_ref[:, clip, :, pl.ds(256 + lane, 128)].reshape(1024, 128).T
        dk_ref[...] = jnp.zeros(dk_ref.shape, F32)
        dv_ref[...] = jnp.zeros(dv_ref.shape, F32)

        @pl.loop(0, 4)
        def _(block):
            query = qkv_ref[pl.ds(block * 2, 2), clip, :, pl.ds(lane, 128)].reshape(256, 128)
            values = qkv_ref[:, clip, :, pl.ds(512 + lane, 128)].reshape(1024, 128)
            keys = qkv_ref[:, clip, :, pl.ds(256 + lane, 128)].reshape(1024, 128)
            columns = pl.ds(pl.multiple_of(block * 256, 256), 256)
            for part in range(2):
                block_ref[:HD, part * 128 : part * 128 + 128] = grad_ref[
                    block * 2 + part, clip, pl.ds(row, HD)
                ]
            scores = lax.dot_general(
                keys, query, (((1,), (1,)), ((), ())), preferred_element_type=F32
            )
            chance = jnp.exp2((scores + mask_ref[clip]) * factor - logs_ref[turn, :, columns])
            dv_ref[...] += lax.dot_general(
                chance.astype(BF),
                block_ref[...],
                (((1,), (1,)), ((), ())),
                preferred_element_type=F32,
            )
            slope = lax.dot_general(
                values, block_ref[...], (((1,), (0,)), ((), ())), preferred_element_type=F32
            )
            center = jnp.sum(chance * slope, axis=0, keepdims=True)
            change = (chance * (slope - center)).astype(BF)
            dk_ref[...] += lax.dot_general(
                change, query, (((1,), (0,)), ((), ())), preferred_element_type=F32
            )
            dq = lax.dot_general(
                kt_ref[...], change, (((1,), (0,)), ((), ())), preferred_element_type=F32
            )
            dqkv_ref[pl.ds(block * 2, 2), clip, :, pl.ds(lane, 128)] = (
                (dq.T * scale).astype(BF).reshape(2, 128, 128)
            )

        dqkv_ref[:, clip, :, pl.ds(256 + lane, 128)] = (
            (dk_ref[...] * scale).astype(BF).reshape(8, 128, 128)
        )
        dqkv_ref[:, clip, :, pl.ds(512 + lane, 128)] = (
            dv_ref[...].astype(BF).reshape(8, 128, 128)
        )

        @pl.when(turn == 2)
        def _():
            next(out_plane)
            next(plane)

        @pl.when(turn == 5)
        def _():
            next(out_plane)

    def bring(slot):
        return pltpu.make_async_copy(
            normed_in.at[slot], normed_ref.at[slot % 2], normed_load.at[slot % 2]
        )

    def weight_grad(slot):
        bring(slot).wait()
        if slot < 7:
            bring(slot + 1).start()
        grads = dqkv_ref[slot].reshape(ROWS, 768)
        product = lax.dot_general(
            normed_ref[slot % 2],
            grads,
            (((0,), (0,)), ((), ())),
            preferred_element_type=F32,
        )
        column = jnp.sum(grads.astype(F32), axis=0, keepdims=True)
        if slot == 0:
            joined_ref[...] = product
            column_ref[...] = column
        else:
            joined_ref[...] += product
            column_ref[...] += column

    bring(0).start()
    next(line)
    next(out_line)
    for slot in range(4):
        weight_grad(slot)
    next(line)
    next(out_line)
    for slot in range(4, 8):
        weight_grad(slot)
    drive(line, out_line, plane, out_plane)


def attend_back(qkv, mask, logs, pull, hidden, weights, feed_grads, out_grad, normed):
    shapes, split = flatten(
        *line_reduce_scratch(336, 1280, False),
        *plane_reduce_scratch(192, 1280),
        *plane_reduce_scratch(96, 1280),
        *line_reduce_scratch(48, 1280, False),
    )
    return pl.pallas_call(
        functools.partial(attend_back_kernel, split),
        out_shape=(
            jax.ShapeDtypeStruct(qkv.shape, BF),
            jax.ShapeDtypeStruct((ROWS, 1280), F32),
            jax.ShapeDtypeStruct((336, 1280), F32),
            jax.ShapeDtypeStruct((48, 1280), F32),
            jax.ShapeDtypeStruct((1280, 768), F32),
            jax.ShapeDtypeStruct((1, 768), F32),
        ),
        in_specs=[ANY, VMEM, VMEM, ANY, ANY, VMEM, ANY, ANY, ANY],
        out_specs=(VMEM,) * 6,
        scratch_shapes=[
            *(pltpu.VMEM(ref.shape, BF) for ref in (hidden, feed_grads, out_grad)),
            pltpu.VMEM((2, ROWS, 1280), BF),
            dma(4),
            dma(2),
            pltpu.VMEM((8, 3, 160, 128), BF),
            pltpu.VMEM((128, 1024), BF),
            pltpu.VMEM((1024, 128), F32),
            pltpu.VMEM((1024, 128), F32),
            pltpu.VMEM((128, 256), BF),
            pltpu.VMEM((192, 1280), F32),
            pltpu.SemaphoreType.DMA(()),
            dma(8),
            dma(8),
            *shapes,
        ],
        compiler_params=params(2, 62),
        name="attend_back",
    )(qkv, mask, logs, pull, hidden, weights, feed_grads, out_grad, normed)


GROUP_ROWS = 4832
GROUP_STEP = 4800
PACK_ROWS = GROUP_STEP * 3 + GROUP_ROWS
SEGMENTS = (
    ("query", 0, 1600),
    ("query_bias", 204800, 2),
    ("key", 204960, 1600),
    ("value", 409760, 1600),
    ("value_bias", 614560, 2),
    ("out", 614720, 1600),
    ("up", 819520, 6400),
    ("up_bias", 1638720, 5),
    ("down", 1639360, 6400),
)
PACK_END = 19216
SHARE_ROWS = 4808
KEY_END = 409760
SHARE_ENTRIES = 614880


def segment_table():
    table, cursor = {}, 0
    for name, start, rows in SEGMENTS:
        row = start // 128
        cursor += 32
        cursor += (row - cursor) % 8
        table[name] = (cursor, row, rows, start % 128)
        cursor += rows
    return table, (cursor + 32 + 7) // 8 * 8


TABLE, STAGE_ROWS = segment_table()


def lane_of(rows):
    return lax.broadcasted_iota(jnp.int32, (rows, 128), 1)


def pack_rows(stage, packed):
    def piece(name, first, rows):
        base, row, _, shift = TABLE[name]
        at = base - row + first
        here = stage[pl.ds(at, rows)]
        if shift == 0:
            return here
        above = stage[pl.ds(at - 1, rows)]
        return jnp.where(
            lane_of(rows) >= shift, pltpu.roll(here, shift, 1), pltpu.roll(above, shift, 1)
        )

    done = set()
    for name, _, _ in SEGMENTS:
        _, row, rows, shift = TABLE[name]
        low = -(-(row + (1 if shift else 0)) // 16) * 16
        high = (row + rows) // 16 * 16
        if high <= low:
            continue
        done.update(range(low, high, 16))
        turns = (high - low) // 128

        @pl.loop(0, turns)
        def _(turn):
            first = pl.multiple_of(low + turn * 128, 16)
            packed[pl.ds(first, 128)] = piece(name, first, 128).astype(BF)

        for first in range(low + turns * 128, high, 16):
            packed[pl.ds(first, 16)] = piece(name, first, 16).astype(BF)
    for first in range(0, PACK_ROWS, 16):
        if first in done:
            continue
        total = jnp.zeros((16, 128), F32)
        for name, _, _ in SEGMENTS:
            _, row, rows, shift = TABLE[name]
            if row < first + 16 and row + rows + (1 if shift else 0) > first:
                total = total + piece(name, first, 16)
        packed[pl.ds(first, 16)] = total.astype(BF)


def stage_wide(stage, name, ref, step):
    base = TABLE[name][0]
    rows, wide = ref.shape[0], ref.shape[1] // 128

    @pl.loop(0, rows // step)
    def _(turn):
        first = pl.multiple_of(turn * step, step)
        for block in range(wide):
            stage[pl.ds(base + first * wide + block, step, stride=wide), :] = ref[
                pl.ds(first, step), pl.ds(block * 128, 128)
            ].astype(F32)


def stage_heads(stage, name, ref, lanes, column):
    base = TABLE[name][0]
    for head in range(2):
        column[head] = ref[:, pl.ds(lanes + head * 128, 128)]

    @pl.loop(0, 5)
    def _(turn):
        lane = lane_of(64)
        rows = [jnp.zeros((64, 128), F32) for _ in range(5)]
        for block in range(8):
            item, head = block // 2, block % 2
            value = column[head, pl.ds(turn * 256 + item, 64, stride=4)]
            offset = block * HD
            first, shift = offset // 128, offset % 128
            if shift:
                value = pltpu.roll(value, shift, 1)
            if shift + HD > 128:
                rows[first] = rows[first] + jnp.where(lane >= shift, value, 0.0)
                rows[first + 1] = rows[first + 1] + jnp.where(
                    lane < shift + HD - 128, value, 0.0
                )
            else:
                rows[first] = rows[first] + value
        for index in range(5):
            stage[pl.ds(base + turn * 320 + index, 64, stride=5), :] = rows[index]


def stage_head_bias(stage, name, ref, lanes):
    base = TABLE[name][0]
    lane = lane_of(1)
    first = ref[0:1, pl.ds(lanes, 128)]
    second = pltpu.roll(ref[0:1, pl.ds(lanes + 128, 128)], HD, 1)
    stage[pl.ds(base, 1)] = first + jnp.where(lane >= HD, second, 0.0)
    stage[pl.ds(base + 1, 1)] = jnp.where(lane < 2 * HD - 128, second, 0.0)


def stage_share(stage, name, ref, first, count, place):
    base = TABLE[name][0] + place.dp * count * 10
    for block in range(10):
        stage[pl.ds(base + block, count, stride=10), :] = ref[
            pl.ds(first, count), pl.ds(block * 128, 128)
        ]


def stage_up(stage, ref, place):
    base = TABLE["up"][0]
    lane = lane_of(128)
    for quarter in range(4):

        @pl.when(place.dp == quarter)
        def _():
            for block in range(10):
                columns = pl.ds(block * 128, 128)
                first = ref[pl.ds(0, 128), columns].T
                second = jnp.where(lane < 32, ref[pl.ds(128, 128), columns].T, 0.0)
                shift = 32 * quarter
                if shift:
                    first = pltpu.roll(first, shift, 1)
                    second = pltpu.roll(second, shift, 1)
                    second = second + jnp.where(lane < shift, first, 0.0)
                    first = jnp.where(lane >= shift, first, 0.0)
                at = base + block * 640 + quarter
                stage[pl.ds(at, 128, stride=5), :] = first
                stage[pl.ds(at + 1, 128, stride=5), :] = second


def norm_back(frames_ref, middle_ref, gain_ref, grad_ref):
    def write(rows, total):
        value = frames_ref[rows].astype(F32)
        center = value - jnp.mean(value, axis=-1, keepdims=True)
        spread = jnp.mean(center * center, axis=-1, keepdims=True)
        root = lax.rsqrt(spread + NORM_EPSILON)
        scaled = center * root
        pull = total * gain_ref[...]
        along = jnp.mean(pull * scaled, axis=-1, keepdims=True)
        grad_ref[rows] = middle_ref[rows] + root * (
            pull - jnp.mean(pull, axis=-1, keepdims=True) - scaled * along
        )

    return write


def fetch(first, rows, sems, grad, weight, frames, middle):
    span = pl.ds(first, rows)
    pairs = (
        (grad[0].at[:, span], grad[1]),
        weight,
        (frames[0].at[span], frames[1]),
        (middle[0].at[span], middle[1]),
    )
    copies = [
        pltpu.make_async_copy(source, target, sems.at[index])
        for index, (source, target) in enumerate(pairs)
    ]
    for copy in copies:
        copy.start()
    return copies


def fetch_scratch(rows):
    return [
        pltpu.VMEM((8, rows, 768), BF),
        pltpu.VMEM((768, 1280), BF),
        pltpu.VMEM((rows, 1280), BF),
        pltpu.VMEM((rows, 1280), F32),
        dma(4),
    ]


def line_product(place, grad_ref, weight_ref, rows, result, bufs, sems):
    def produce(level, core, tile):
        return jnp.dot(
            grad_ref[level * 2 + core, tile],
            weight_ref[...],
            preferred_element_type=F32,
        )

    tiles = [pl.ds(0, rows)]
    return line_reduce(place, produce, tiles, result, bufs, sems, True)


FIRST_ROWS = 128


def finish_kernel(
    split, grad_in, weight_in, joined_ref, bias_ref, bias_column_ref, sum_ref, out_ref,
    up_bias_ref, small_ref, peak_ref, frames_in, middle_in, gain_ref, shift_ref, cap_ref,
    input_grad_ref, grads_ref, small_out, factor_ref,
    grad_ref, weight_ref, frames_ref, middle_ref, load,
    stage, packed, sum_rows, column, tiles, small_in, small_all, peak_all, edge,
    local, small_send, small_recv, plane_send, plane_recv, *scratch,
):
    place = Place()
    line_bufs, line_sems, bufs, sems = split(scratch)
    loads = fetch(
        0,
        FIRST_ROWS,
        load,
        (grad_in, grad_ref),
        (weight_in, weight_ref),
        (frames_in, frames_ref),
        (middle_in, middle_ref),
    )
    greet(place, mp_all=True, plane=True)
    peers = (place.dpx, place.dpy, place.dpd)

    def tell(index, source, target, group, act):
        act(
            remote(
                source,
                target.at[place.dp],
                plane_send.at[index],
                plane_recv.at[index],
                group,
                place.mp,
            )
        )

    def heard(index, target, group):
        block = target.at[group]
        remote(
            block, block, plane_send.at[index], plane_recv.at[index], group, place.mp
        ).wait_recv()

    line = line_product(
        place,
        grad_ref,
        weight_ref,
        FIRST_ROWS,
        norm_back(frames_ref, middle_ref, gain_ref, input_grad_ref),
        line_bufs,
        line_sems,
    )
    for index, group in enumerate(peers):
        tell(index, peak_ref, peak_all, group, lambda copy: copy.start())
    for copy in loads:
        copy.wait()

    for block in range(10):
        lanes = pl.ds(block * 128, 128)
        weight = weight_ref[:, lanes].astype(F32)
        turned = joined_ref[lanes].T
        whole = jnp.sum(weight * bias_column_ref[...], axis=0, keepdims=True)
        along = jnp.sum(weight * turned, axis=0, keepdims=True)
        tiles[pl.ds(block, 1)] = (along - shift_ref[:, lanes] * whole) / gain_ref[:, lanes]
        tiles[pl.ds(10 + block, 1)] = whole
    tiles[pl.ds(20, 44)] = small_ref[...]
    for run in range(8):
        edge[run] = tiles[pl.ds(run * 15 // 2, 8)]
    mixing = exchange(place, edge, small_in, local, small_send, small_recv)
    next(mixing)

    stage[...] = jnp.zeros(stage.shape, F32)
    for name, lanes in (("query", 0), ("key", 256), ("value", 512)):
        stage_heads(stage, name, joined_ref, lanes, column)
    stage_head_bias(stage, "query_bias", bias_ref, 0)
    stage_head_bias(stage, "value_bias", bias_ref, 512)
    stage_share(stage, "out", out_ref, 0, 40, place)
    stage_share(stage, "down", sum_ref, 160, 160, place)
    stage_up(stage, sum_ref, place)
    stage[pl.ds(TABLE["up_bias"][0], 5)] = up_bias_ref[...]
    pack_rows(stage, packed)

    def produce(group, core, start, rows):
        first = pl.multiple_of(group * GROUP_STEP + start, 16)
        return packed[pl.ds(first, GROUP_ROWS // 2)].astype(F32)

    def result(rows, total):
        sum_rows[rows] = total

    half = GROUP_ROWS // 2
    plane = plane_reduce(place, produce, half, half, result, bufs, sems, False)
    next(plane)
    next(plane)
    next(line)
    next(line)
    for _ in mixing:
        pass
    small_all[place.dp] = jnp.sum(small_in[...], axis=0)
    for index, group in enumerate(peers):
        tell(3 + index, small_all.at[place.dp], small_all, group, lambda copy: copy.start())
    next(plane)
    next(line)
    next(line)
    drive(line, plane)
    for index, group in enumerate(peers):
        heard(index, peak_all, group)
        heard(3 + index, small_all, group)
    top = peak_ref[...]
    for group in peers:
        top = jnp.maximum(top, peak_all[group])
    roots = []
    for head in range(2):
        peak = jnp.max(jnp.max(top[head], axis=0, keepdims=True), axis=1, keepdims=True)
        roots.append(
            jnp.sqrt(cap_ref[...] / jnp.maximum(peak * (1.0 / math.sqrt(HD)), cap_ref[...]))
        )
    factor_ref[...] = jnp.ones(factor_ref.shape, F32)

    @pl.when(place.dp == 0)
    def _():
        full = KEY_END // 128 // 5 * 5
        for index in range(5):
            entry = (lane_of(1) + 128 * index).astype(F32)
            block = jnp.floor((entry + 0.5) * (1.0 / HD))
            odd = block - 2.0 * jnp.floor(block * 0.5) > 0.5
            factor = jnp.where(odd, roots[1], roots[0])
            factor_ref[pl.ds(index, full // 5, stride=5), :] = jnp.broadcast_to(
                factor, (full // 5, 128)
            )
            left = KEY_END - (full + index) * 128
            if left > 0:
                factor_ref[pl.ds(full + index, 1)] = jnp.where(lane_of(1) < left, factor, 1.0)

    whole = jnp.sum(small_all[...], axis=0)
    lane = lane_of(8)
    row = lax.broadcasted_iota(jnp.int32, (8, 128), 0)
    tiles[...] = jnp.zeros((64, 128), F32)
    tiles[pl.ds(8, 8)] = whole
    ahead = pltpu.roll(tiles[pl.ds(9, 8)], 64, 1)
    here = pltpu.roll(whole, 64, 1)
    odd = jnp.where(lane < 64, here, ahead)
    run_of = jnp.where(place.c == 1, odd, whole)
    run_of = jnp.where(jnp.logical_and(row == 7, lane >= 64), 0.0, run_of)
    small_out[...] = run_of
    tiles[pl.ds(8, 8)] = run_of
    wide = lane_of(16)
    entry = jnp.where(
        wide >= 64, pltpu.roll(tiles[pl.ds(1, 16)], 64, 1), pltpu.roll(tiles[pl.ds(0, 16)], 64, 1)
    )

    @pl.when(place.dp == 3)
    def _():
        sum_rows[pl.ds(GROUP_STEP, 16)] += entry

    for group in range(4):

        @pl.when(place.dp == group)
        def _():
            down, shift = 480 * group // 128, 480 * group % 128
            if shift == 0:
                grads_ref[...] = sum_rows[pl.ds(0, SHARE_ROWS)]
            else:
                for first in range(0, SHARE_ROWS, 1208):
                    size = min(1208, SHARE_ROWS - first)
                    grads_ref[pl.ds(first, size)] = jnp.where(
                        lane_of(size) < 128 - shift,
                        pltpu.roll(sum_rows[pl.ds(first + down, size)], 128 - shift, 1),
                        pltpu.roll(sum_rows[pl.ds(first + down + 1, size)], 128 - shift, 1),
                    )

    for index, group in enumerate(peers):
        tell(index, peak_ref, peak_all, group, lambda copy: copy.wait_send())
        tell(3 + index, small_all.at[place.dp], small_all, group, lambda copy: copy.wait_send())


def finish(grads, weight, joined, bias, sums, out, up_bias, small, peaks, frames, middle, gain, shift, cap):
    shapes, split = flatten(
        *line_reduce_scratch(FIRST_ROWS, 1280, True),
        *plane_reduce_scratch(GROUP_ROWS // 2, 128, False),
    )
    return pl.pallas_call(
        functools.partial(finish_kernel, split),
        out_shape=(
            jax.ShapeDtypeStruct((FIRST_ROWS, 1280), F32),
            jax.ShapeDtypeStruct((SHARE_ROWS, 128), F32),
            jax.ShapeDtypeStruct((8, 128), F32),
            jax.ShapeDtypeStruct((SHARE_ROWS, 128), F32),
        ),
        in_specs=[ANY, ANY] + [VMEM] * 8 + [ANY, ANY, VMEM, VMEM, VMEM],
        out_specs=(VMEM,) * 4,
        scratch_shapes=[
            *fetch_scratch(FIRST_ROWS),
            pltpu.VMEM((STAGE_ROWS, 128), F32),
            pltpu.VMEM((PACK_ROWS, 128), BF),
            pltpu.VMEM((GROUP_ROWS, 128), F32),
            pltpu.VMEM((2, 1280, 128), F32),
            pltpu.VMEM((64, 128), F32),
            pltpu.VMEM((8, 8, 128), F32),
            pltpu.VMEM((4, 8, 128), F32),
            pltpu.VMEM((4,) + peaks.shape, F32),
            pltpu.VMEM((8, 8, 128), F32),
            pltpu.SemaphoreType.DMA(()),
            dma(8),
            dma(8),
            dma(6),
            dma(6),
            *shapes,
        ],
        compiler_params=params(7, 62),
        name="finish",
    )(
        grads, weight, joined, bias[None], bias[:, None], sums, out, up_bias, small, peaks,
        frames, middle, gain, shift, cap,
    )


def share_master_kernel(
    split, rows_ref, grad_in, weight_in, frames_in, middle_in, gain_ref,
    whole_out, input_grad_ref,
    grad_ref, weight_ref, frames_ref, middle_ref, load,
    whole_ref, parts, turned, store, send, recv, *scratch,
):
    place = Place()
    line_bufs, line_sems = split(scratch)
    loads = fetch(
        FIRST_ROWS,
        ROWS - FIRST_ROWS,
        load,
        (grad_in, grad_ref),
        (weight_in, weight_ref),
        (frames_in, frames_ref),
        (middle_in, middle_ref),
    )
    greet(place, line=True, plane=True)
    line = line_product(
        place,
        grad_ref,
        weight_ref,
        ROWS - FIRST_ROWS,
        norm_back(frames_ref, middle_ref, gain_ref, input_grad_ref),
        line_bufs,
        line_sems,
    )
    dp, mp, dpx, dpy, dpd = place.dp, place.mp, place.dpx, place.dpy, place.dpd
    half = GROUP_ROWS // 2
    part_a, part_b = pl.ds(0, half), pl.ds(half, half)
    for group in range(4):

        @pl.when(dp == group)
        def _():
            down, shift = 480 * group // 128, 480 * group % 128
            turned[pl.ds(0, 16)] = jnp.zeros((16, 128), F32)
            turned[pl.ds(16, SHARE_ROWS)] = rows_ref[...]
            turned[pl.ds(16 + SHARE_ROWS, 24)] = jnp.zeros((24, 128), F32)
            for first in range(0, GROUP_ROWS, 1208):
                here = turned[pl.ds(16 + first - down, 1208)]
                if shift:
                    here = jnp.where(
                        lane_of(1208) >= shift,
                        pltpu.roll(here, shift, 1),
                        pltpu.roll(turned[pl.ds(15 + first - down, 1208)], shift, 1),
                    )
                parts[dp, pl.ds(first, 1208)] = here.astype(BF)


    def hop(index, block, target):
        return remote(block, block, send.at[index], recv.at[index], target, mp)

    own = parts.at[dp]
    sends = [hop(0, own, dpx), hop(1, own, dpy)]
    for copy in sends:
        copy.start()

    stores = []

    def keep(index, first, rows):
        span = pl.ds(pl.multiple_of(first, 16), rows)
        stores.append(
            pltpu.make_async_copy(whole_ref.at[span], whole_out.at[span], store.at[index])
        )
        stores[-1].start()

    def unpack(group):
        for start in range(32, GROUP_STEP, 2384):
            at = pl.multiple_of(group * GROUP_STEP + start, 16)
            whole_ref[pl.ds(at, 2384)] = parts[group, pl.ds(start, 2384)].astype(F32)
        keep(len(stores), group * GROUP_STEP + 32, GROUP_STEP - 32)

    for copy in loads:
        copy.wait()
    next(line)
    next(line)
    unpack(dp)
    hop(0, parts.at[dpx], dpx).wait_recv()
    sends.append(hop(2, parts.at[dpx, part_a], dpy))
    sends[-1].start()
    hop(1, parts.at[dpy], dpy).wait_recv()
    sends.append(hop(3, parts.at[dpy, part_b], dpx))
    sends[-1].start()
    unpack(dpx)
    unpack(dpy)
    next(line)
    next(line)
    hop(2, parts.at[dpd, part_a], dpy).wait_recv()
    hop(3, parts.at[dpd, part_b], dpx).wait_recv()
    unpack(dpd)
    for group in range(4):
        first = parts[group, pl.ds(0, 32)].astype(F32)
        if group > 0:
            first = first + parts[group - 1, pl.ds(GROUP_STEP, 32)].astype(F32)
        whole_ref[pl.ds(group * GROUP_STEP, 32)] = first
        keep(4 + group, group * GROUP_STEP, 32)
    whole_ref[pl.ds(4 * GROUP_STEP, 16)] = parts[3, pl.ds(GROUP_STEP, 16)].astype(F32)
    keep(8, 4 * GROUP_STEP, 16)
    for copy in sends:
        copy.wait_send()
    drive(line)
    for copy in stores:
        copy.wait()


def share_master(rows, grads, weight, frames, middle, gain):
    shapes, split = flatten(*line_reduce_scratch(ROWS - FIRST_ROWS, 1280, True))
    return pl.pallas_call(
        functools.partial(share_master_kernel, split),
        out_shape=(
            jax.ShapeDtypeStruct((PACK_END, 128), F32),
            jax.ShapeDtypeStruct((ROWS - FIRST_ROWS, 1280), F32),
        ),
        in_specs=[VMEM, ANY, ANY, ANY, ANY, VMEM],
        out_specs=(ANY, VMEM),
        scratch_shapes=[
            *fetch_scratch(ROWS - FIRST_ROWS),
            pltpu.VMEM((PACK_END, 128), F32),
            pltpu.VMEM((4, GROUP_ROWS, 128), BF),
            pltpu.VMEM((SHARE_ROWS + 40, 128), F32),
            dma(9),
            dma(4),
            dma(4),
            *shapes,
        ],
        compiler_params=params(8, 60),
        name="share_master",
    )(rows, grads, weight, frames, middle, gain)


STEP_ENTRIES = 1024 * 76


def optimize_kernel(
    rates_ref, factor_ref, grads_ref, master_ref, first_ref, second_ref,
    owned_out, master_out, first_out, second_out, padded_out,
):
    entry = lax.broadcasted_iota(jnp.int32, (1, STEP_ENTRIES), 1)
    grads = grads_ref[...]
    first = BETA_FIRST * first_ref[...] + (1.0 - BETA_FIRST) * grads
    second = BETA_SECOND * second_ref[...] + (1.0 - BETA_SECOND) * grads * grads
    change = first * rates_ref[0] / (jnp.sqrt(second * rates_ref[1]) + ADAM_EPSILON)
    master = (master_ref[...] * rates_ref[2] - change) * factor_ref[...]
    owned_out[...] = grads
    master_out[...] = master
    first_out[...] = first
    second_out[...] = second
    left = SHARE_ENTRIES - pl.program_id(0) * STEP_ENTRIES
    padded_out[...] = jnp.where(entry < left, master, 0.0)


def optimize(rates, factor, grads, master, first, second):
    block = pl.BlockSpec((1, STEP_ENTRIES), lambda step: (0, step))
    share = jax.ShapeDtypeStruct((1, SHARE_ENTRIES), F32)
    return pl.pallas_call(
        optimize_kernel,
        grid=(pl.cdiv(SHARE_ENTRIES, STEP_ENTRIES),),
        out_shape=(share,) * 4 + (jax.ShapeDtypeStruct((1, SHARE_ROWS * 128), F32),),
        in_specs=[pl.BlockSpec(memory_space=pltpu.SMEM)] + [block] * 5,
        out_specs=(block,) * 5,
        compiler_params=pltpu.CompilerParams(vmem_limit_bytes=62 << 20),
        name="optimize",
    )(rates, factor, grads, master, first, second)


def fast_body(
    frames,
    lengths,
    key_mask,
    cotangent,
    gain_one,
    shift_one,
    query_weight,
    query_bias,
    key_weight,
    value_weight,
    value_bias,
    out_weight,
    out_bias,
    gain_two,
    shift_two,
    up_weight,
    up_bias,
    down_weight,
    down_bias,
    master,
    moment_one,
    moment_two,
    adam_step,
    hyper_rates,
):
    group = lax.axis_index("dp")
    position = jnp.arange(1024, dtype=jnp.int32)
    keep_query = position[None, :] < lengths[:, None]
    keep_key = jnp.logical_and(keep_query, key_mask == 1)
    mask = jnp.where(keep_key, 0.0, MASK_VALUE)[:, :, None]
    live = keep_query.astype(F32)[:, None, :]
    gain_first = gain_one.astype(F32)
    shift_first = shift_one.astype(F32)
    gain_second = gain_two.astype(F32)
    shift_second = shift_two.astype(F32)
    inputs = frames.transpose(1, 0, 2).reshape(ROWS, 1280).astype(F32)
    upstream_low = cotangent.transpose(1, 0, 2).reshape(ROWS, 1280)
    upstream = upstream_low.astype(F32)
    def head_lanes(bias):
        lanes = bias.astype(F32).reshape(2, HD)
        return jnp.pad(lanes, ((0, 0), (0, 128 - HD))).reshape(256)

    joined_bias = jnp.concatenate(
        [head_lanes(query_bias), jnp.zeros((256,), F32), head_lanes(value_bias)]
    )[None]
    frame_rows = frames.transpose(1, 0, 2).reshape(ROWS, 1280)
    quarter = group * 160
    up_share = lax.dynamic_slice_in_dim(up_weight, quarter, 160, 1).T
    down_share = lax.dynamic_slice_in_dim(down_weight, quarter, 160, 0)
    bias_share = lax.dynamic_slice_in_dim(up_bias, quarter, 160, 0)
    bias_rows = jnp.pad(bias_share[None], ((0, 15), (0, 1280 - 160)))
    message = jnp.concatenate([up_share, bias_rows])
    outer_start = jnp.minimum(group * 48, 112)
    outer = lax.dynamic_slice_in_dim(out_weight, outer_start, 48, 0)
    normed_full, qkv, upstream_full, joined_weight = project(
        frame_rows,
        gain_first[None],
        shift_first[None],
        upstream_low,
        query_weight.T,
        key_weight.T,
        value_weight.T,
        joined_bias,
    )
    qkv = qkv.reshape(8, 3, 128, 768)
    attended, logs, peaks, gathered, out_rows, middle, normed_two = attend(
        qkv,
        mask,
        live,
        message,
        outer,
        frame_rows,
        out_bias.astype(F32)[None],
        gain_second[None],
        shift_second[None],
    )
    up_lanes = gathered[:, 160, :160].reshape(1, 640).astype(F32)
    out_rows = out_rows.reshape(8, 160, 1280)

    normed_two_grad, hidden, feed_grads, _, down_all = feed_forward(
        normed_two, upstream_full, gathered, down_share, up_lanes
    )

    _, norm_two_pull = jax.vjp(layer_norm, middle, gain_second, shift_second)
    middle_norm_grad, gain_two_grad, shift_two_grad = norm_two_pull(normed_two_grad)
    middle_grad = upstream + middle_norm_grad
    branch_grad = middle_grad.astype(BF)
    branch_clips = branch_grad.reshape(3, 128, 1280)
    out_grad = jnp.einsum("schr,crd->shd", attended, branch_clips, preferred_element_type=F32)
    attended_grad = jnp.einsum(
        "shd,crd->schr", out_rows, branch_clips, preferred_element_type=F32
    ).astype(BF)
    out_quarters = jnp.pad(
        out_grad.astype(BF).reshape(4, 2, 4, 40, 1280), ((0, 0),) * 3 + ((0, 8), (0, 0))
    )
    out_quarters = out_quarters.transpose(2, 1, 0, 3, 4).reshape(4, 2, 192, 1280)
    joined_grad, feed, feed_sum, out_sum, joined_weight_grad, joined_bias_grad = attend_back(
        qkv, mask, logs, attended_grad, hidden, down_all, feed_grads, out_quarters, normed_full
    )
    layer_out = (middle + feed + down_bias.astype(F32)).astype(BF)
    joined_grad = joined_grad.reshape(8, ROWS, 768)
    joined_bias_grad = joined_bias_grad[0]

    level = lax.axis_index("mp") // 2
    up_bias_share = lax.dynamic_slice_in_dim(feed_sum[320], level * 160, 160, 0)
    up_bias_rows = lax.dynamic_update_slice(
        jnp.zeros((640,), F32), up_bias_share, (quarter,)
    ).reshape(5, 128)
    small_rows = jnp.concatenate(
        [
            jnp.sum(branch_grad.astype(F32), axis=0),
            gain_two_grad,
            shift_two_grad,
            jnp.sum(upstream, axis=0),
            jnp.zeros((512,), F32),
        ]
    ).reshape(44, 128)
    first_grad, grad_rows, small_sum, factor_rows = finish(
        joined_grad,
        joined_weight,
        joined_weight_grad,
        joined_bias_grad,
        feed_sum,
        out_sum,
        up_bias_rows,
        small_rows,
        peaks,
        frame_rows,
        middle_grad,
        gain_first[None],
        shift_first[None],
        hyper_rates[2].reshape(1, 1),
    )
    small_total = small_sum.reshape(1024)[:960]
    learn_rate = hyper_rates[0]
    weight_decay = hyper_rates[1]
    step_count = adam_step[0].astype(F32)
    rates = jnp.stack(
        [
            learn_rate / (1.0 - jnp.power(BETA_FIRST, step_count)),
            1.0 / (1.0 - jnp.power(BETA_SECOND, step_count)),
            1.0 - learn_rate * weight_decay,
        ]
    )
    owned_grads, master_new, first_new, second_new, padded = optimize(
        rates,
        factor_rows.reshape(1, SHARE_ROWS * 128),
        grad_rows.reshape(1, SHARE_ROWS * 128),
        master,
        moment_one,
        moment_two,
    )
    whole, second_grad = share_master(
        padded.reshape(SHARE_ROWS, 128),
        joined_grad,
        joined_weight,
        frame_rows,
        middle_grad,
        gain_first[None],
    )
    input_grad = jnp.concatenate([first_grad, second_grad])
    whole = lax.optimization_barrier(whole.reshape(1, PACK_END * 128))
    weights_new = whole[:, : 4 * SHARE_ENTRIES].astype(BF)
    return (
        layer_out.reshape(3, 128, 1280).transpose(1, 0, 2),
        input_grad.reshape(3, 128, 1280).transpose(1, 0, 2),
        owned_grads,
        master_new,
        first_new,
        second_new,
        weights_new,
        small_total,
    )


def body(
    frames,
    lengths,
    key_mask,
    cotangent,
    gain_one,
    shift_one,
    query_weight,
    query_bias,
    key_weight,
    value_weight,
    value_bias,
    out_weight,
    out_bias,
    gain_two,
    shift_two,
    up_weight,
    up_bias,
    down_weight,
    down_bias,
    master,
    moment_one,
    moment_two,
    adam_step,
    hyper_rates,
):
    local_rows, clip_count, model_width = frames.shape
    total_rows = key_mask.shape[1]
    head_cols = query_weight.shape[1]
    heads_here = head_cols // HD
    block_rows = min(512, total_rows)
    blocks = total_rows // block_rows
    score_scale = 1.0 / math.sqrt(HD)
    position = jnp.arange(total_rows, dtype=jnp.int32)
    keep_query = position[None, :] < lengths[:, None]
    keep_key = jnp.logical_and(keep_query, key_mask == 1)
    gain_first = gain_one.astype(jnp.float32)
    shift_first = shift_one.astype(jnp.float32)
    gain_second = gain_two.astype(jnp.float32)
    shift_second = shift_two.astype(jnp.float32)
    inputs = frames.astype(jnp.float32)
    normed = layer_norm(inputs, gain_first, shift_first).astype(jnp.bfloat16)
    joined_weight = jnp.concatenate([query_weight, key_weight, value_weight], axis=1)
    joined_bias = jnp.concatenate(
        [
            query_bias.astype(jnp.float32),
            jnp.zeros((head_cols,), jnp.float32),
            value_bias.astype(jnp.float32),
        ]
    )
    normed_full = lax.all_gather(normed, "mp", axis=0, tiled=True)
    projected = (
        jnp.einsum("rcd,de->rce", normed_full, joined_weight, preferred_element_type=jnp.float32)
        + joined_bias
    ).astype(jnp.bfloat16)
    query = projected[:, :, :head_cols].reshape(total_rows, clip_count, heads_here, HD)
    keys = projected[:, :, head_cols : 2 * head_cols].reshape(
        total_rows, clip_count, heads_here, HD
    )
    values = projected[:, :, 2 * head_cols :].reshape(total_rows, clip_count, heads_here, HD)

    def scores_of(row_start):
        query_block = lax.dynamic_slice_in_dim(query, row_start, block_rows, 0)
        raw_scores = (
            jnp.einsum("qchd,kchd->chqk", query_block, keys, preferred_element_type=jnp.float32)
            * score_scale
        )
        return (query_block, jnp.where(keep_key[:, None, None, :], raw_scores, MASK_VALUE))

    def forward_block(block_index):
        row_start = block_index * block_rows
        _, masked = scores_of(row_start)
        row_peak = jnp.max(masked, axis=-1, keepdims=True)
        exp_scores = jnp.exp(masked - row_peak)
        row_total = jnp.sum(exp_scores, axis=-1, keepdims=True)
        probability = (exp_scores / row_total).astype(jnp.bfloat16)
        attended = jnp.einsum(
            "chqk,kchd->qchd", probability, values, preferred_element_type=jnp.float32
        ).astype(jnp.bfloat16)
        live_rows = lax.dynamic_slice_in_dim(keep_query, row_start, block_rows, 1)
        block_peak = jnp.max(
            jnp.where(live_rows[:, None, :], row_peak[..., 0], MASK_VALUE), axis=(0, 2)
        )
        return (attended, (row_peak + jnp.log(row_total))[..., 0], block_peak)

    attended_blocks, log_totals, block_peaks = lax.map(forward_block, jnp.arange(blocks))
    attended_full = attended_blocks.reshape(total_rows, clip_count, head_cols)
    head_peak = lax.pmax(jnp.max(block_peaks, axis=0), "dp")
    rows_here = attended_full
    attn_branch = lax.psum_scatter(
        jnp.einsum("rck,kd->rcd", rows_here, out_weight, preferred_element_type=jnp.float32),
        "mp",
        scatter_dimension=0,
        tiled=True,
    ) + out_bias.astype(jnp.float32)
    middle = inputs + attn_branch
    normed_two = layer_norm(middle, gain_second, shift_second).astype(jnp.bfloat16)
    upstream = cotangent.astype(jnp.float32)
    normed_two_full = lax.all_gather(normed_two, "mp", axis=0, tiled=True)
    before = jnp.einsum(
        "rcd,df->rcf", normed_two_full, up_weight, preferred_element_type=jnp.float32
    ) + up_bias.astype(jnp.float32)
    hidden = exact_gelu(before).astype(jnp.bfloat16)
    rows_here = hidden
    feed = lax.psum_scatter(
        jnp.einsum(
            "rcf,fd->rcd", rows_here, down_weight, preferred_element_type=jnp.float32
        ).astype(jnp.bfloat16),
        "mp",
        scatter_dimension=0,
        tiled=True,
    ).astype(jnp.float32) + down_bias.astype(jnp.float32)
    layer_out = (middle + feed).astype(jnp.bfloat16)
    feed_grad_full = lax.all_gather(cotangent, "mp", axis=0, tiled=True)
    down_grad = jnp.einsum(
        "rcf,rcd->fd", hidden, feed_grad_full, preferred_element_type=jnp.float32
    )
    hidden_grad = jnp.einsum(
        "rcd,fd->rcf", feed_grad_full, down_weight, preferred_element_type=jnp.float32
    )
    _, gelu_pull = jax.vjp(exact_gelu, before)
    before_grad = gelu_pull(hidden_grad)[0].astype(jnp.bfloat16)
    up_bias_grad = jnp.sum(before_grad.astype(jnp.float32), axis=(0, 1))
    up_grad = jnp.einsum(
        "rcd,rcf->df", normed_two_full, before_grad, preferred_element_type=jnp.float32
    )
    rows_here = before_grad
    normed_two_grad = lax.psum_scatter(
        jnp.einsum("rcf,df->rcd", rows_here, up_weight, preferred_element_type=jnp.float32),
        "mp",
        scatter_dimension=0,
        tiled=True,
    )
    _, norm_two_pull = jax.vjp(layer_norm, middle, gain_second, shift_second)
    middle_norm_grad, gain_two_grad, shift_two_grad = norm_two_pull(normed_two_grad)
    middle_grad = upstream + middle_norm_grad
    branch_grad = middle_grad.astype(jnp.bfloat16)
    branch_grad_full = lax.all_gather(branch_grad, "mp", axis=0, tiled=True)
    out_grad = jnp.einsum(
        "rck,rcd->kd", attended_full, branch_grad_full, preferred_element_type=jnp.float32
    )
    attended_grad = jnp.einsum(
        "rcd,kd->rck", branch_grad_full, out_weight, preferred_element_type=jnp.float32
    ).astype(jnp.bfloat16)
    attended_grad = attended_grad.reshape(total_rows, clip_count, heads_here, HD)

    def backward_block(carry, block_index):
        key_total, value_total = carry
        row_start = block_index * block_rows
        query_block, masked = scores_of(row_start)
        log_total = log_totals[block_index]
        probability = jnp.exp(masked - log_total[..., None])
        grad_block = lax.dynamic_slice_in_dim(attended_grad, row_start, block_rows, 0)
        value_total = value_total + jnp.einsum(
            "chqk,qchd->kchd",
            probability.astype(jnp.bfloat16),
            grad_block,
            preferred_element_type=jnp.float32,
        )
        prob_grad = jnp.einsum(
            "qchd,kchd->chqk", grad_block, values, preferred_element_type=jnp.float32
        )
        score_grad = (
            probability * (prob_grad - jnp.sum(probability * prob_grad, axis=-1, keepdims=True))
        ).astype(jnp.bfloat16)
        query_grad = (
            jnp.einsum("chqk,kchd->qchd", score_grad, keys, preferred_element_type=jnp.float32)
            * score_scale
        ).astype(jnp.bfloat16)
        key_total = (
            key_total
            + jnp.einsum(
                "chqk,qchd->kchd", score_grad, query_block, preferred_element_type=jnp.float32
            )
            * score_scale
        )
        return ((key_total, value_total), query_grad)

    empty_grad = jnp.zeros((total_rows, clip_count, heads_here, HD), jnp.float32)
    (key_total, value_total), query_blocks = lax.scan(
        backward_block, (empty_grad, empty_grad), jnp.arange(blocks)
    )
    joined_grad = jnp.concatenate(
        [
            query_blocks.reshape(total_rows, clip_count, head_cols),
            key_total.reshape(total_rows, clip_count, head_cols).astype(jnp.bfloat16),
            value_total.reshape(total_rows, clip_count, head_cols).astype(jnp.bfloat16),
        ],
        axis=-1,
    )
    joined_bias_grad = jnp.sum(joined_grad.astype(jnp.float32), axis=(0, 1))
    normed_back = lax.all_gather(normed, "mp", axis=0, tiled=True)
    joined_weight_grad = jnp.einsum(
        "rcd,rce->de", normed_back, joined_grad, preferred_element_type=jnp.float32
    )
    rows_here = joined_grad
    normed_grad = lax.psum_scatter(
        jnp.einsum(
            "rce,de->rcd", rows_here, joined_weight, preferred_element_type=jnp.float32
        ).astype(jnp.bfloat16),
        "mp",
        scatter_dimension=0,
        tiled=True,
    ).astype(jnp.float32)
    _, norm_one_pull = jax.vjp(layer_norm, inputs, gain_first, shift_first)
    input_norm_grad, gain_one_grad, shift_one_grad = norm_one_pull(normed_grad)
    input_grad = middle_grad + input_norm_grad
    out_bias_grad = jnp.sum(branch_grad.astype(jnp.float32), axis=(0, 1))
    down_bias_grad = jnp.sum(upstream, axis=(0, 1))
    small_terms = jnp.concatenate(
        [
            gain_one_grad,
            shift_one_grad,
            out_bias_grad,
            gain_two_grad,
            shift_two_grad,
            down_bias_grad,
        ]
    )
    small_share = lax.psum_scatter(small_terms, "mp", scatter_dimension=0, tiled=True)
    small_total = lax.psum(small_share, "dp")
    packed = jnp.concatenate(
        [
            joined_weight_grad[:, :head_cols].reshape(-1),
            joined_bias_grad[:head_cols],
            joined_weight_grad[:, head_cols : 2 * head_cols].reshape(-1),
            joined_weight_grad[:, 2 * head_cols :].reshape(-1),
            joined_bias_grad[2 * head_cols :],
            out_grad.reshape(-1),
            up_grad.reshape(-1),
            up_bias_grad,
            down_grad.reshape(-1),
            small_share,
        ]
    )
    owned_grads = lax.psum_scatter(
        packed.astype(jnp.bfloat16), "dp", scatter_dimension=0, tiled=True
    ).astype(jnp.float32)
    share_size = owned_grads.shape[0]
    learn_rate = hyper_rates[0]
    weight_decay = hyper_rates[1]
    logit_cap = hyper_rates[2]
    step_count = adam_step[0].astype(jnp.float32)
    first_new = BETA_FIRST * moment_one[0] + (1.0 - BETA_FIRST) * owned_grads
    second_new = BETA_SECOND * moment_two[0] + (1.0 - BETA_SECOND) * owned_grads * owned_grads
    first_hat = first_new / (1.0 - jnp.power(BETA_FIRST, step_count))
    second_hat = second_new / (1.0 - jnp.power(BETA_SECOND, step_count))
    entry_index = lax.axis_index("dp") * share_size + jnp.arange(share_size, dtype=jnp.int32)
    query_end = model_width * head_cols
    query_bias_end = query_end + head_cols
    key_end = query_bias_end + model_width * head_cols
    column = jnp.where(
        entry_index < query_end,
        entry_index % head_cols,
        jnp.where(
            entry_index < query_bias_end,
            entry_index - query_end,
            (entry_index - query_bias_end) % head_cols,
        ),
    )
    head_index = column // HD
    root_factor = jnp.sqrt(logit_cap / jnp.maximum(head_peak, logit_cap))
    head_factor = jnp.zeros((share_size,), jnp.float32)
    for head_number in range(heads_here):
        head_factor = head_factor + jnp.where(
            head_index == head_number, root_factor[head_number], 0.0
        )
    factor = jnp.where(entry_index < key_end, head_factor, 1.0)
    master_here = master[0]
    master_new = (
        master_here
        - learn_rate
        * (first_hat / (jnp.sqrt(second_hat) + ADAM_EPSILON) + weight_decay * master_here)
    ) * factor
    weights_full = lax.all_gather(master_new.astype(jnp.bfloat16), "dp", axis=0, tiled=True)
    return (
        layer_out,
        input_grad,
        owned_grads[None],
        master_new[None],
        first_new[None],
        second_new[None],
        weights_full[None],
        small_total,
    )


def solution(mesh):
    chosen = fast_body if dict(mesh.shape) == {"dp": 4, "mp": 8} else body
    placed = (
        P("mp", "dp", None),
        P("dp"),
        P("dp", None),
        P("mp", "dp", None),
        P(),
        P(),
        P(None, "mp"),
        P("mp"),
        P(None, "mp"),
        P(None, "mp"),
        P("mp"),
        P("mp", None),
        P(),
        P(),
        P(),
        P(None, "mp"),
        P("mp"),
        P("mp", None),
        P(),
        P("mp", "dp"),
        P("mp", "dp"),
        P("mp", "dp"),
        P(),
        P(),
    )
    return jax.shard_map(
        chosen,
        mesh=mesh,
        in_specs=placed,
        out_specs=(
            P("mp", "dp", None),
            P("mp", "dp", None),
            P("mp", "dp"),
            P("mp", "dp"),
            P("mp", "dp"),
            P("mp", "dp"),
            P("mp", None),
            P("mp"),
        ),
        check_vma=False,
    )
```

```python
import functools
import math

import jax
import jax.numpy as jnp
from jax import lax
from jax.experimental import pallas as pl
from jax.experimental.pallas import tpu as pltpu
from jax.sharding import PartitionSpec as P

HD = 80


NORM_EPSILON = 1e-05
ADAM_EPSILON = 1e-08
BETA_FIRST = 0.9
BETA_SECOND = 0.999
MASK_VALUE = -1e30


def layer_norm(value, gain, shift):
    center = value - jnp.mean(value, axis=-1, keepdims=True)
    spread = jnp.mean(center * center, axis=-1, keepdims=True)
    return center * lax.rsqrt(spread + NORM_EPSILON) * gain + shift


def exact_gelu(argument):
    return jax.nn.gelu(argument, approximate=False)


MESH = pl.DeviceIdType.MESH
ANY = pl.BlockSpec(memory_space=pl.ANY)
VMEM = pl.BlockSpec(memory_space=pltpu.VMEM)
LINE = 4
ROWS = 384
BF = jnp.bfloat16
F32 = jnp.float32


class Place:
    def __init__(self):
        self.dp = lax.axis_index("dp")
        self.mp = lax.axis_index("mp")
        self.z = self.mp // 2
        self.c = self.mp % 2
        self.pair = self.z * 2 + 1 - self.c
        self.dpx = self.dp + 1 - 2 * (self.dp % 2)
        self.dpy = (self.dp + 2) % 4
        self.dpd = 3 - self.dp

    def zorder(self, event):
        if event == 0:
            return self.z
        if event == 1:
            return self.z + 1 - 2 * (self.z % 2)
        if event == 2:
            return 2 - self.z // 2
        return 3 - 3 * (self.z // 2)


def greet(place, mp_all=False, line=False, plane=False, pair=True):
    barrier = pltpu.get_barrier_semaphore()
    count = 0

    def signal(dp, mp):
        pl.semaphore_signal(barrier, inc=1, device_id=(dp, mp), device_id_type=MESH)

    if mp_all:
        for hop in range(1, 8):
            signal(place.dp, (place.mp + hop) % 8)
        count += 7
    else:
        if pair:
            signal(place.dp, place.pair)
            count += 1
        if line:

            @pl.when(place.z > 0)
            def _():
                signal(place.dp, place.mp - 2)

            @pl.when(place.z < LINE - 1)
            def _():
                signal(place.dp, place.mp + 2)

    if plane:
        for other in (place.dpx, place.dpy, place.dpd):
            signal(other, place.mp)
        count += 3
    if line and not mp_all:
        pl.semaphore_wait(barrier, count + 1 + (place.z + 1) // 2 % 2)
    else:
        pl.semaphore_wait(barrier, count)


def remote(src, dst, send, recv, dp, mp):
    return pltpu.make_async_remote_copy(
        src_ref=src,
        dst_ref=dst,
        send_sem=send,
        recv_sem=recv,
        device_id=(dp, mp),
        device_id_type=MESH,
    )


def line_gather(place, src, out, local, send, recv, paired, ready=None, rows=None):
    dp, z, c, mp, pair = place.dp, place.z, place.c, place.mp, place.pair

    def at(slot):
        if rows is None:
            return out.at[slot]
        return out.at[pl.ds(pl.multiple_of(slot * rows, 16), rows)]

    def slot_of(level, core):
        return level * 2 + core if paired else level

    def hop(event, slot, source, direction, target):
        return remote(source, at(slot), send.at[event, direction], recv.at[slot], dp, target)

    own = slot_of(z, c)
    keep = pltpu.make_async_copy(src, at(own), local)
    keep.start()

    def ways(event, level, slot, source, act):
        up = z < LINE - 1
        down = z > 0
        if event > 0:
            up = jnp.logical_and(up, level < z)
            down = jnp.logical_and(down, level > z)

        @pl.when(up)
        def _():
            act(hop(event, slot, source, 1, mp + 2))

        @pl.when(down)
        def _():
            act(hop(event, slot, source, 2, mp - 2))

        if paired:
            act(hop(event, slot, source, 0, pair))

    ways(0, z, own, src, lambda copy: copy.start())
    yield
    if ready is not None:
        keep.wait()
        ready(own)
        if paired:
            other = slot_of(z, 1 - c)
            hop(0, other, at(other), 0, pair).wait_recv()
            ready(other)

    def settle(event):
        level = place.zorder(event)
        ready(slot_of(level, c))
        if paired:
            other = slot_of(level, 1 - c)
            hop(event, other, at(other), 0, pair).wait_recv()
            ready(other)

    for event in range(1, LINE):
        level = place.zorder(event)
        slot = slot_of(level, c)
        hop(event, slot, at(slot), 0, pair).wait_recv()
        ways(event, level, slot, at(slot), lambda copy: copy.start())
        if ready is not None and event > 1:
            if event == 2:
                settle(1)
            settle(event)
        yield
    if ready is None:
        if paired:
            for level in range(LINE):
                other = slot_of(level, 1 - c)
                hop(0, other, at(other), 0, pair).wait_recv()
        keep.wait()
    for event in range(LINE):
        level = place.zorder(event)
        slot = slot_of(level, c)
        ways(event, level, slot, at(slot), lambda copy: copy.wait_send())
    yield


def plane_gather(place, src, out, local, send, recv, ready=None, primed=False):
    dp, c, mp, pair = place.dp, place.c, place.mp, place.pair
    dpx, dpy, dpd = place.dpx, place.dpy, place.dpd
    half = src.shape[0] // 2
    part_a, part_b = pl.ds(0, half), pl.ds(half, half)

    def at(group, core):
        return out.at[group * 2 + core]

    def hop(index, block, group, target):
        return remote(block, block, send.at[index], recv.at[index], group, target)

    def done(group, core):
        if ready is not None:
            ready(group * 2 + core)

    keep = pltpu.make_async_copy(src, at(dp, c), local)
    here = at(dp, c)
    from_x, from_y, from_d = at(dpx, c), at(dpy, c), at(dpd, c)
    firsts = [
        remote(src, here, send.at[0], recv.at[0], dp, pair),
        remote(src, here, send.at[1], recv.at[1], dpx, mp),
        remote(src, here, send.at[2], recv.at[2], dpy, mp),
    ]
    seconds = [
        hop(3, from_x.at[part_a], dpy, mp),
        hop(4, from_y.at[part_b], dpx, mp),
        hop(5, from_x, dp, pair),
        hop(6, from_y, dp, pair),
        hop(7, from_d.at[part_a], dp, pair),
        hop(8, from_d.at[part_b], dp, pair),
    ]
    if primed:
        yield
    keep.start()
    for copy in firsts:
        copy.start()
    yield
    if ready is not None:
        keep.wait()
        done(dp, c)
        hop(0, at(dp, 1 - c), dp, pair).wait_recv()
        done(dp, 1 - c)
    hop(1, from_x, dpx, mp).wait_recv()
    seconds[0].start()
    hop(2, from_y, dpy, mp).wait_recv()
    seconds[1].start()
    seconds[2].start()
    seconds[3].start()
    yield
    done(dpx, c)
    hop(5, at(dpx, 1 - c), dp, pair).wait_recv()
    done(dpx, 1 - c)
    if ready is not None:
        yield
    done(dpy, c)
    hop(6, at(dpy, 1 - c), dp, pair).wait_recv()
    done(dpy, 1 - c)
    if ready is not None:
        yield
    hop(3, from_d.at[part_a], dpy, mp).wait_recv()
    seconds[4].start()
    hop(4, from_d.at[part_b], dpx, mp).wait_recv()
    seconds[5].start()
    done(dpd, c)
    other = at(dpd, 1 - c)
    hop(7, other.at[part_a], dp, pair).wait_recv()
    hop(8, other.at[part_b], dp, pair).wait_recv()
    done(dpd, 1 - c)
    yield
    if ready is None:
        hop(0, at(dp, 1 - c), dp, pair).wait_recv()
        keep.wait()
    for copy in firsts + seconds:
        copy.wait_send()
    yield


def drive(*programs):
    live = list(programs)
    while live:
        for program in list(live):
            try:
                next(program)
            except StopIteration:
                live.remove(program)


def dma(*shape):
    return pltpu.SemaphoreType.DMA(shape)


def params(cid, vmem=40):
    return pltpu.CompilerParams(
        collective_id=cid, has_side_effects=True, vmem_limit_bytes=vmem << 20
    )


def exchange(place, src, out, local, send, recv):
    dp, mp = place.dp, place.mp
    keep = pltpu.make_async_copy(src.at[mp], out.at[mp], local)
    keep.start()
    sends = []
    for hop in range(1, 8):
        target = (mp + hop) % 8
        sends.append(
            remote(src.at[target], out.at[mp], send.at[hop], recv.at[hop], dp, target)
        )
        sends[-1].start()
    yield
    keep.wait()
    for hop in range(1, 8):
        origin = (mp + 8 - hop) % 8
        remote(out.at[origin], out.at[origin], send.at[hop], recv.at[hop], dp, origin).wait_recv()
    for copy in sends:
        copy.wait_send()
    yield


def line_reduce(place, produce, tiles, result, bufs, sems, paired):
    dp, z, c, mp, pair = place.dp, place.z, place.c, place.mp, place.pair
    above_block, below_block, out_block = bufs["above"], bufs["below"], bufs["out"]
    order = [place.zorder(event) for event in (3, 2, 1, 0)]
    inner = jnp.logical_and(z > 0, z < LINE - 1)
    outer = jnp.logical_or(z == 0, z == LINE - 1)

    @pl.when(z == LINE - 1)
    def _():
        above_block[...] = jnp.zeros(above_block.shape, BF)

    @pl.when(z == 0)
    def _():
        below_block[...] = jnp.zeros(below_block.shape, BF)

    def from_above(level):
        return above_block.at[jnp.minimum(level, LINE - 2)]

    def from_below(level):
        return below_block.at[jnp.maximum(level - 1, 0)]

    def across(step, level):
        return remote(
            bufs["pair_out"].at[step % 2],
            bufs["pair_in"].at[level],
            sems["pair_send"].at[step % 2],
            sems["pair_recv"].at[level],
            dp,
            pair,
        )

    if paired:
        for step, level in enumerate(order):
            if step > 1:
                across(step - 2, order[step - 2]).wait_send()
            for rows in tiles:
                bufs["pair_out"][step % 2, rows] = produce(level, 1 - c, rows).astype(BF)
            across(step, level).start()
    yield

    def toward(step, level, act):
        @pl.when(level < z)
        def _():
            act(
                remote(
                    out_block.at[step],
                    from_above(level),
                    sems["line_send"].at[step],
                    sems["above"].at[level],
                    dp,
                    mp - 2,
                )
            )

        @pl.when(level > z)
        def _():
            act(
                remote(
                    out_block.at[step],
                    from_below(level),
                    sems["line_send"].at[step],
                    sems["below"].at[level],
                    dp,
                    mp + 2,
                )
            )

    def arrive(level, above):
        if above:
            remote(
                from_above(level),
                from_above(level),
                sems["line_send"].at[0],
                sems["above"].at[level],
                dp,
                mp,
            ).wait_recv()
        else:
            remote(
                from_below(level),
                from_below(level),
                sems["line_send"].at[0],
                sems["below"].at[level],
                dp,
                mp,
            ).wait_recv()

    def advance(step):
        level = order[step]
        if paired:
            across(step, level).wait_recv()

        @pl.when(jnp.logical_and(level < z, z < LINE - 1))
        def _():
            arrive(level, True)

        @pl.when(jnp.logical_and(level > z, z > 0))
        def _():
            arrive(level, False)

        for rows in tiles:
            total = produce(level, c, rows)
            if paired:
                total = total + bufs["pair_in"][level, rows].astype(F32)

            @pl.when(level < z)
            def _():
                out_block[step, rows] = (total + from_above(level)[rows].astype(F32)).astype(BF)

            @pl.when(level > z)
            def _():
                out_block[step, rows] = (total + from_below(level)[rows].astype(F32)).astype(BF)

        toward(step, level, lambda copy: copy.start())

    advance(0)
    for step in (1, 2):

        @pl.when(outer)
        def _():
            advance(step)

    yield
    for step in (1, 2):

        @pl.when(inner)
        def _():
            advance(step)

        yield

    if paired:
        across(3, z).wait_recv()

    @pl.when(z < LINE - 1)
    def _():
        arrive(z, True)

    @pl.when(z > 0)
    def _():
        arrive(z, False)

    for rows in tiles:
        total = produce(z, c, rows)
        if paired:
            total = total + bufs["pair_in"][z, rows].astype(F32)
        total = total + from_above(z)[rows].astype(F32) + from_below(z)[rows].astype(F32)
        result(rows, total)
    for step, level in enumerate(order):
        if paired and step > 1:
            across(step, level).wait_send()
        if step < 3:
            toward(step, level, lambda copy: copy.wait_send())
    yield


def line_reduce_scratch(rows, cols, paired):
    block = lambda n: pltpu.VMEM((n, rows, cols), BF)
    scratch = {"above": block(3), "below": block(3), "out": block(3)}
    sems = {"line_send": dma(3), "above": dma(4), "below": dma(4)}
    if paired:
        scratch.update({"pair_out": block(2), "pair_in": block(4)})
        sems.update({"pair_send": dma(2), "pair_recv": dma(4)})
    return scratch, sems


def plane_reduce(place, produce, tile, half, result, bufs, sems, paired=True, early=False):
    dp, c, mp, pair = place.dp, place.c, place.mp, place.pair
    dpx, dpy, dpd = place.dpx, place.dpy, place.dpd
    starts = range(0, half, tile)
    send, recv = sems["send"], sems["recv"]
    out_block, landed = bufs["out"], bufs["in"]
    groups = {"far": dpd, "x": dpx, "y": dpy, "own": dp}
    steps = ["x", "y", "far", "own"] if early else ["far", "x", "y", "own"]

    def across(name):
        step = steps.index(name)
        return remote(
            bufs["pair_out"].at[step % 2],
            bufs["pair_in"].at[step],
            sems["pair_send"].at[step % 2],
            sems["pair_recv"].at[step],
            dp,
            pair,
        )

    def cross(name):
        if not paired:
            return
        step = steps.index(name)
        if step > 1:
            across(steps[step - 2]).wait_send()
        bufs["pair_out"][step % 2] = produce(groups[name], 1 - c, 0, 2 * half).astype(BF)
        across(name).start()

    def crossed(name):
        if paired:
            across(name).wait_recv()

    def share(name, start):
        total = produce(groups[name], c, start, tile)
        if paired:
            total = total + bufs["pair_in"][steps.index(name), pl.ds(start, tile)].astype(F32)
        return total

    def hop(index):
        target = (dpx, dpy, dpx, dpx, dpy, dpy)[index]
        return remote(
            out_block.at[index], landed.at[index], send.at[index], recv.at[index], target, mp
        )

    def fill(index, name, base, extra=None):
        for start in starts:
            total = share(name, base + start)
            if extra is not None:
                total = total + landed[extra, pl.ds(start, tile)].astype(F32)
            out_block[index, pl.ds(start, tile)] = total.astype(BF)
        hop(index).start()

    def far():
        crossed("far")
        fill(0, "far", 0)
        fill(1, "far", half)

    def near():
        crossed("x")
        fill(2, "x", 0)
        crossed("y")
        fill(4, "y", half)

    if early:
        cross("x")
        yield
        cross("y")
        near()
        yield
        cross("far")
        far()
        yield
        cross("own")
    else:
        cross("far")
        cross("x")
        yield
        far()
        cross("y")
        near()
        cross("own")
    yield
    hop(1).wait_recv()
    fill(3, "x", half, extra=1)
    hop(0).wait_recv()
    fill(5, "y", 0, extra=0)
    yield
    crossed("own")
    for index in (2, 3, 4, 5):
        hop(index).wait_recv()
    for base, pieces in ((0, (2, 5)), (half, (3, 4))):
        for start in starts:
            total = share("own", base + start)
            for piece in pieces:
                total = total + landed[piece, pl.ds(start, tile)].astype(F32)
            result(pl.ds(base + start, tile), total)
    for index in range(6):
        hop(index).wait_send()
    if paired:
        for name in steps[2:]:
            across(name).wait_send()
    yield


def plane_reduce_scratch(half, cols, paired=True):
    block = lambda n, rows: pltpu.VMEM((n, rows, cols), BF)
    scratch = {"out": block(6, half), "in": block(6, half)}
    sems = {"send": dma(6), "recv": dma(6)}
    if paired:
        scratch.update({"pair_out": block(2, 2 * half), "pair_in": block(4, 2 * half)})
        sems.update({"pair_send": dma(2), "pair_recv": dma(4)})
    return scratch, sems


def project_kernel(
    frames_ref, gain_ref, shift_ref, cot_ref, query_ref, key_ref, value_ref, bias_ref,
    nfull_ref, qkv_ref, cfull_ref, weight_ref,
    normed_ref, local, line_send, line_recv, plane_send, plane_recv,
):
    place = Place()
    weight_ref[...] = jnp.zeros(weight_ref.shape, BF)
    for index, ref in enumerate((query_ref, key_ref, value_ref)):
        for head in range(2):
            weight_ref[pl.ds(index * 256 + head * 128, HD)] = ref[pl.ds(head * HD, HD)]
    for start in range(0, ROWS, 128):
        rows = pl.ds(start, 128)
        normed_ref[rows] = layer_norm(
            frames_ref[rows].astype(F32), gain_ref[...], shift_ref[...]
        ).astype(BF)
    greet(place, line=True, plane=True)

    def ready(slot):
        product = lax.dot_general(
            nfull_ref[slot],
            weight_ref[...],
            (((1,), (1,)), ((), ())),
            preferred_element_type=F32,
        )
        qkv_ref[slot] = (product + bias_ref[...]).astype(BF)

    drive(
        line_gather(
            place, normed_ref, nfull_ref, local.at[0], line_send, line_recv, True, ready
        ),
        plane_gather(place, cot_ref, cfull_ref, local.at[1], plane_send, plane_recv),
    )


def project(frames, gain, shift, cotangent, query, key, value, bias):
    return pl.pallas_call(
        project_kernel,
        out_shape=(
            jax.ShapeDtypeStruct((8,) + frames.shape, BF),
            jax.ShapeDtypeStruct((8, ROWS, 768), BF),
            jax.ShapeDtypeStruct((8,) + cotangent.shape, BF),
            jax.ShapeDtypeStruct((768, 1280), BF),
        ),
        in_specs=[VMEM, VMEM, VMEM, ANY, VMEM, VMEM, VMEM, VMEM],
        out_specs=(VMEM, VMEM, ANY, VMEM),
        scratch_shapes=[pltpu.VMEM((ROWS, 1280), BF), dma(2), dma(4, 3), dma(8), dma(9), dma(9)],
        compiler_params=params(0),
        name="project",
    )(frames, gain, shift, cotangent, query, key, value, bias)


OUTER_STARTS = (0, 48, 96, 112)


def attend_kernel(
    qkv_ref, mask_ref, live_ref, weights_ref, outer_ref, frames_ref, out_bias_ref,
    gain_two_ref, shift_two_ref,
    att_ref, logs_ref, peak_ref, wfull_ref, rows_ref, middle_ref, two_ref,
    out_ref, vt_ref, outer_all, outer_full, local, send, recv, line_send, line_recv,
    outer_send, outer_recv, plane_send, plane_recv,
):
    place = Place()
    greet(place, mp_all=True, plane=True)
    outer = line_gather(
        place, outer_ref, outer_all, local.at[2], outer_send, outer_recv, False, None, 48
    )
    next(outer)
    gather = line_gather(
        place, weights_ref, wfull_ref, local.at[1], line_send, line_recv, False
    )
    next(gather)
    factor = math.log2(math.e) / math.sqrt(HD)
    peak_ref[...] = jnp.full(peak_ref.shape, MASK_VALUE, F32)

    @pl.loop(0, 6)
    def _(turn):
        clip = turn // 2
        head = turn % 2
        lane = pl.multiple_of(head * 128, 128)
        row = pl.multiple_of(head * HD, 16)
        keys = qkv_ref[:, clip, :, pl.ds(256 + lane, 128)].reshape(1024, 128)
        vt_ref[...] = qkv_ref[:, clip, :, pl.ds(512 + lane, 128)].reshape(1024, 128).T

        @pl.loop(0, 4)
        def _(block):
            query = qkv_ref[pl.ds(block * 2, 2), clip, :, pl.ds(lane, 128)].reshape(256, 128)
            columns = pl.ds(pl.multiple_of(block * 256, 256), 256)
            scores = lax.dot_general(
                keys, query, (((1,), (1,)), ((), ())), preferred_element_type=F32
            )
            scores = scores + mask_ref[clip]
            peak = jnp.max(scores, axis=0, keepdims=True)
            powers = jnp.exp2((scores - peak) * factor)
            total = jnp.sum(powers, axis=0, keepdims=True)
            mixed = lax.dot_general(
                vt_ref[...],
                powers.astype(BF),
                (((1,), (0,)), ((), ())),
                preferred_element_type=F32,
            )
            mixed = (mixed / total).astype(BF)
            for part in range(2):
                out_ref[block * 2 + part, clip, pl.ds(row, HD)] = mixed[
                    :HD, part * 128 : part * 128 + 128
                ]
            logs_ref[turn, :, columns] = peak * factor + jnp.log2(total)
            peak_ref[head] = jnp.maximum(
                peak_ref[head], jnp.where(live_ref[clip, :, columns] > 0, peak, MASK_VALUE)
            )

        @pl.when(turn == 2)
        def _():
            next(outer)

        @pl.when(turn == 4)
        def _():
            next(outer)
            next(gather)

    mixing = exchange(place, out_ref, att_ref, local.at[0], send, recv)
    next(mixing)
    for _ in outer:
        pass
    spread = plane_gather(place, outer_all, outer_full, local.at[3], plane_send, plane_recv)
    drive(spread, gather, mixing)
    for level in range(LINE):
        for core in range(2):
            for group, start in enumerate(OUTER_STARTS):
                rows_ref[pl.ds((level * 2 + core) * 160 + start, 48)] = outer_full[
                    group * 2 + core, pl.ds(level * 48, 48)
                ]
    mixed = jnp.concatenate([att_ref[:, clip].reshape(1280, 128) for clip in range(3)], axis=1)
    middle_ref[...] = lax.dot_general(
        mixed, rows_ref[...], (((0,), (0,)), ((), ())), preferred_element_type=F32
    )
    for start in range(0, ROWS, 128):
        rows = pl.ds(start, 128)
        middle = frames_ref[rows].astype(F32) + (middle_ref[rows] + out_bias_ref[...])
        middle_ref[rows] = middle
        two_ref[rows] = layer_norm(middle, gain_two_ref[...], shift_two_ref[...]).astype(BF)


def attend(qkv, mask, live, weights, outer, frames, out_bias, gain_two, shift_two):
    return pl.pallas_call(
        attend_kernel,
        out_shape=(
            jax.ShapeDtypeStruct((8, 3, 160, 128), BF),
            jax.ShapeDtypeStruct((6, 1, 1024), F32),
            jax.ShapeDtypeStruct((2, 8, 256), F32),
            jax.ShapeDtypeStruct((4,) + weights.shape, BF),
            jax.ShapeDtypeStruct((1280, 1280), BF),
            jax.ShapeDtypeStruct((ROWS, 1280), F32),
            jax.ShapeDtypeStruct((ROWS, 1280), BF),
        ),
        in_specs=[VMEM, VMEM, VMEM, ANY, ANY, VMEM, VMEM, VMEM, VMEM],
        out_specs=(VMEM, VMEM, VMEM, ANY, VMEM, VMEM, VMEM),
        scratch_shapes=[
            pltpu.VMEM((8, 3, 160, 128), BF),
            pltpu.VMEM((128, 1024), BF),
            pltpu.VMEM((192, 1280), BF),
            pltpu.VMEM((8, 192, 1280), BF),
            dma(4),
            dma(8),
            dma(8),
            dma(4, 3),
            dma(4),
            dma(4, 3),
            dma(4),
            dma(9),
            dma(9),
        ],
        compiler_params=params(1),
        name="attend",
    )(qkv, mask, live, weights, outer, frames, out_bias, gain_two, shift_two)


def flatten(*pairs):
    names, shapes = [], []
    for number, group in enumerate(pairs):
        for name, shape in group.items():
            names.append((number, name))
            shapes.append(shape)

    def split(refs):
        groups = [{} for _ in pairs]
        for (number, name), ref in zip(names, refs):
            groups[number][name] = ref
        return groups

    return shapes, split


def feed_forward_kernel(
    split, normed_ref, upstream_ref, weights_ref, down_ref, bias_ref,
    total_ref, hidden_ref, grads_ref, bias_out, down_all,
    normed_all, upstream_all, slope_all, rate_ref, sum_ref,
    load, local, line_local, gather_send, gather_recv, line_send, line_recv, *scratch,
):
    place = Place()
    bufs, sems = split(scratch)
    loads = []
    for slot in range(8):
        loads.append(
            pltpu.make_async_copy(upstream_ref.at[slot], upstream_all.at[slot], load.at[slot])
        )
        loads[-1].start()
    greet(place, line=True, plane=True)
    bias_out[...] = jnp.zeros(bias_out.shape, F32)

    def up_rows():
        return weights_ref[:, pl.ds(0, 160)].reshape(640, 1280)

    def down_rows():
        return down_all[...].reshape(640, 1280)

    def activate(slot, rows):
        before = (
            lax.dot_general(
                normed_all[slot, rows],
                up_rows(),
                (((1,), (1,)), ((), ())),
                preferred_element_type=F32,
            )
            + bias_ref[...]
        )
        share = 0.5 + 0.5 * lax.erf(before * math.sqrt(0.5))
        hidden_ref[slot, rows] = (before * share).astype(BF)
        density = jnp.exp(before * before * -0.5) * (1.0 / math.sqrt(2.0 * math.pi))
        return share + before * density

    def pull_back(slot, rows, rate):
        pull = lax.dot_general(
            upstream_all[slot, rows],
            down_rows(),
            (((1,), (1,)), ((), ())),
            preferred_element_type=F32,
        )
        slope = (pull * rate).astype(BF)
        slope_all[slot, rows] = slope
        bias_out[...] += jnp.sum(slope.astype(F32), axis=0, keepdims=True)

    here = [place.dp * 2 + place.c, place.dp * 2 + 1 - place.c]
    seen = []

    def ready(slot):
        index = len(seen)
        seen.append(slot)

        rows = pl.ds(0, ROWS)
        rate = activate(slot, rows)
        if index < 2:
            rate_ref[index] = rate
        else:
            pull_back(slot, rows, rate)

        if index < 2:
            next(down)

    def finish_here():
        for index in range(2):
            pull_back(here[index], pl.ds(0, ROWS), rate_ref[index])

    down = line_gather(
        place, down_ref, down_all, line_local, line_send, line_recv, False
    )
    gather = plane_gather(
        place, normed_ref, normed_all, local, gather_send, gather_recv, ready
    )

    def produce(group, core, start, rows):
        return jnp.dot(
            slope_all[group * 2 + core, pl.ds(start, rows)],
            up_rows(),
            preferred_element_type=F32,
        )

    def result(rows, total):
        total_ref[rows] = total

    reduce = plane_reduce(place, produce, 192, 192, result, bufs, sems, True, True)
    next(down)
    next(gather)
    for copy in loads:
        copy.wait()
    next(gather)
    for _ in down:
        pass
    next(gather)
    next(reduce)
    next(gather)
    next(reduce)
    next(gather)
    next(reduce)
    finish_here()
    next(reduce)

    def weight_grads(left_all, right_all, base):
        @pl.loop(0, 8)
        def _(slot):
            product = lax.dot_general(
                left_all[slot],
                right_all[slot],
                (((0,), (0,)), ((), ())),
                preferred_element_type=F32,
            )
            sum_ref[...] = jnp.where(slot == 0, product, sum_ref[...] + product)

        for level in range(4):
            grads_ref[level, pl.ds(base, 160)] = sum_ref[pl.ds(level * 160, 160)].astype(BF)

    weight_grads(slope_all, normed_all, 0)
    next(reduce)
    weight_grads(hidden_ref, upstream_all, 160)
    for level in range(4):
        grads_ref[level, pl.ds(320, 16)] = jnp.zeros((16, 1280), BF)
        grads_ref[level, pl.ds(320, 16), pl.ds(0, 640)] = jnp.broadcast_to(
            bias_out[...], (16, 640)
        ).astype(BF)
    drive(reduce, gather)


def feed_forward(normed, upstream, weights, down, bias):
    shapes, split = flatten(*plane_reduce_scratch(192, 1280))
    return pl.pallas_call(
        functools.partial(feed_forward_kernel, split),
        out_shape=(
            jax.ShapeDtypeStruct((ROWS, 1280), F32),
            jax.ShapeDtypeStruct((8, ROWS, 640), BF),
            jax.ShapeDtypeStruct((4, 336, 1280), BF),
            jax.ShapeDtypeStruct((1, 640), F32),
            jax.ShapeDtypeStruct((4, 160, 1280), BF),
        ),
        in_specs=[ANY, ANY, VMEM, ANY, VMEM],
        out_specs=(VMEM,) * 5,
        scratch_shapes=[
            pltpu.VMEM((8, ROWS, 1280), BF),
            pltpu.VMEM((8, ROWS, 1280), BF),
            pltpu.VMEM((8, ROWS, 640), BF),
            pltpu.VMEM((2, ROWS, 640), F32),
            pltpu.VMEM((640, 1280), F32),
            dma(8),
            pltpu.SemaphoreType.DMA(()),
            pltpu.SemaphoreType.DMA(()),
            dma(9),
            dma(9),
            dma(4, 3),
            dma(4),
            *shapes,
        ],
        compiler_params=params(3, 60),
        name="feed_forward",
    )(normed, upstream, weights, down, bias)


def attend_back_kernel(
    split, qkv_in, mask_ref, logs_ref, pull_ref, hidden_in, weights_ref, feed_grads_in,
    out_grad_in, normed_in, dqkv_ref, feed_ref, feed_sum_ref, out_sum_ref, joined_ref, column_ref,
    hidden_ref, feed_grads_ref, out_grad_ref, normed_ref, load, normed_load,
    grad_ref, kt_ref, dk_ref, dv_ref, block_ref, middle_ref, local, send, recv, *scratch,
):
    place = Place()
    qkv_ref = dqkv_ref
    (
        line_bufs, line_sems, plane_bufs, plane_sems,
        out_plane_bufs, out_plane_sems, out_line_bufs, out_line_sems,
    ) = split(scratch)
    loads = [
        pltpu.make_async_copy(source, target, load.at[index])
        for index, (source, target) in enumerate(
            (
                (out_grad_in, out_grad_ref),
                (feed_grads_in, feed_grads_ref),
                (hidden_in, hidden_ref),
                (qkv_in, qkv_ref),
            )
        )
    ]
    for copy in loads:
        copy.start()
    greet(place, mp_all=True, plane=True)
    scale = 1.0 / math.sqrt(HD)
    factor = math.log2(math.e) * scale
    arriving = exchange(place, pull_ref, grad_ref, local, send, recv)
    next(arriving)

    def feed_block(group, core, start, rows):
        return jnp.dot(
            hidden_ref[group * 2 + core, pl.ds(start, rows)],
            weights_ref[...].reshape(640, 1280),
            preferred_element_type=F32,
        )

    def feed_result(rows, total):
        feed_ref[rows] = total

    def sum_result(rows, total):
        feed_sum_ref[rows] = total

    plane = plane_reduce(
        place, feed_block, 192, 192, feed_result, plane_bufs, plane_sems, True
    )
    line = line_reduce(
        place,
        lambda level, core, rows: feed_grads_ref[level, rows].astype(F32),
        [pl.ds(start, 112) for start in range(0, 336, 112)],
        sum_result,
        line_bufs,
        line_sems,
        False,
    )
    def middle(rows, total):
        middle_ref[rows] = total

    def out_result(rows, total):
        out_sum_ref[rows] = total

    out_plane = plane_reduce(
        place,
        lambda group, core, start, rows: out_grad_ref[group, core, pl.ds(start, rows)].astype(F32),
        96,
        96,
        middle,
        out_plane_bufs,
        out_plane_sems,
    )
    out_line = line_reduce(
        place,
        lambda level, core, rows: middle_ref[
            pl.ds(pl.multiple_of(level * 48 + rows.start, 16), rows.size)
        ],
        [pl.ds(0, 48)],
        out_result,
        out_line_bufs,
        out_line_sems,
        False,
    )
    loads[0].wait()
    next(out_plane)
    next(out_plane)
    loads[2].wait()
    next(plane)
    next(plane)
    loads[1].wait()
    next(line)
    next(line)
    next(out_line)
    loads[3].wait()
    for _ in arriving:
        pass
    block_ref[...] = jnp.zeros(block_ref.shape, BF)

    @pl.loop(0, 6)
    def _(turn):
        clip = turn // 2
        head = turn % 2
        lane = pl.multiple_of(head * 128, 128)
        row = pl.multiple_of(head * HD, 16)
        kt_ref[...] = qkv_ref[:, clip, :, pl.ds(256 + lane, 128)].reshape(1024, 128).T
        dk_ref[...] = jnp.zeros(dk_ref.shape, F32)
        dv_ref[...] = jnp.zeros(dv_ref.shape, F32)

        @pl.loop(0, 4)
        def _(block):
            query = qkv_ref[pl.ds(block * 2, 2), clip, :, pl.ds(lane, 128)].reshape(256, 128)
            values = qkv_ref[:, clip, :, pl.ds(512 + lane, 128)].reshape(1024, 128)
            keys = qkv_ref[:, clip, :, pl.ds(256 + lane, 128)].reshape(1024, 128)
            columns = pl.ds(pl.multiple_of(block * 256, 256), 256)
            for part in range(2):
                block_ref[:HD, part * 128 : part * 128 + 128] = grad_ref[
                    block * 2 + part, clip, pl.ds(row, HD)
                ]
            scores = lax.dot_general(
                keys, query, (((1,), (1,)), ((), ())), preferred_element_type=F32
            )
            chance = jnp.exp2((scores + mask_ref[clip]) * factor - logs_ref[turn, :, columns])
            dv_ref[...] += lax.dot_general(
                chance.astype(BF),
                block_ref[...],
                (((1,), (1,)), ((), ())),
                preferred_element_type=F32,
            )
            slope = lax.dot_general(
                values, block_ref[...], (((1,), (0,)), ((), ())), preferred_element_type=F32
            )
            center = jnp.sum(chance * slope, axis=0, keepdims=True)
            change = (chance * (slope - center)).astype(BF)
            dk_ref[...] += lax.dot_general(
                change, query, (((1,), (0,)), ((), ())), preferred_element_type=F32
            )
            dq = lax.dot_general(
                kt_ref[...], change, (((1,), (0,)), ((), ())), preferred_element_type=F32
            )
            dqkv_ref[pl.ds(block * 2, 2), clip, :, pl.ds(lane, 128)] = (
                (dq.T * scale).astype(BF).reshape(2, 128, 128)
            )

        dqkv_ref[:, clip, :, pl.ds(256 + lane, 128)] = (
            (dk_ref[...] * scale).astype(BF).reshape(8, 128, 128)
        )
        dqkv_ref[:, clip, :, pl.ds(512 + lane, 128)] = (
            dv_ref[...].astype(BF).reshape(8, 128, 128)
        )

        @pl.when(turn == 2)
        def _():
            next(out_plane)
            next(plane)

        @pl.when(turn == 5)
        def _():
            next(out_plane)

    def bring(slot):
        return pltpu.make_async_copy(
            normed_in.at[slot], normed_ref.at[slot % 2], normed_load.at[slot % 2]
        )

    def weight_grad(slot):
        bring(slot).wait()
        if slot < 7:
            bring(slot + 1).start()
        grads = dqkv_ref[slot].reshape(ROWS, 768)
        product = lax.dot_general(
            normed_ref[slot % 2],
            grads,
            (((0,), (0,)), ((), ())),
            preferred_element_type=F32,
        )
        column = jnp.sum(grads.astype(F32), axis=0, keepdims=True)
        if slot == 0:
            joined_ref[...] = product
            column_ref[...] = column
        else:
            joined_ref[...] += product
            column_ref[...] += column

    bring(0).start()
    next(line)
    next(out_line)
    for slot in range(4):
        weight_grad(slot)
    next(line)
    next(out_line)
    for slot in range(4, 8):
        weight_grad(slot)
    drive(line, out_line, plane, out_plane)


def attend_back(qkv, mask, logs, pull, hidden, weights, feed_grads, out_grad, normed):
    shapes, split = flatten(
        *line_reduce_scratch(336, 1280, False),
        *plane_reduce_scratch(192, 1280),
        *plane_reduce_scratch(96, 1280),
        *line_reduce_scratch(48, 1280, False),
    )
    return pl.pallas_call(
        functools.partial(attend_back_kernel, split),
        out_shape=(
            jax.ShapeDtypeStruct(qkv.shape, BF),
            jax.ShapeDtypeStruct((ROWS, 1280), F32),
            jax.ShapeDtypeStruct((336, 1280), F32),
            jax.ShapeDtypeStruct((48, 1280), F32),
            jax.ShapeDtypeStruct((1280, 768), F32),
            jax.ShapeDtypeStruct((1, 768), F32),
        ),
        in_specs=[ANY, VMEM, VMEM, ANY, ANY, VMEM, ANY, ANY, ANY],
        out_specs=(VMEM,) * 6,
        scratch_shapes=[
            *(pltpu.VMEM(ref.shape, BF) for ref in (hidden, feed_grads, out_grad)),
            pltpu.VMEM((2, ROWS, 1280), BF),
            dma(4),
            dma(2),
            pltpu.VMEM((8, 3, 160, 128), BF),
            pltpu.VMEM((128, 1024), BF),
            pltpu.VMEM((1024, 128), F32),
            pltpu.VMEM((1024, 128), F32),
            pltpu.VMEM((128, 256), BF),
            pltpu.VMEM((192, 1280), F32),
            pltpu.SemaphoreType.DMA(()),
            dma(8),
            dma(8),
            *shapes,
        ],
        compiler_params=params(2, 62),
        name="attend_back",
    )(qkv, mask, logs, pull, hidden, weights, feed_grads, out_grad, normed)


GROUP_ROWS = 4832
GROUP_STEP = 4800
PACK_ROWS = GROUP_STEP * 3 + GROUP_ROWS
SEGMENTS = (
    ("query", 0, 1600),
    ("query_bias", 204800, 2),
    ("key", 204960, 1600),
    ("value", 409760, 1600),
    ("value_bias", 614560, 2),
    ("out", 614720, 1600),
    ("up", 819520, 6400),
    ("up_bias", 1638720, 5),
    ("down", 1639360, 6400),
)
PACK_END = 19216
SHARE_ROWS = 4808
KEY_END = 409760
SHARE_ENTRIES = 614880


def segment_table():
    table, cursor = {}, 0
    for name, start, rows in SEGMENTS:
        row = start // 128
        cursor += 32
        cursor += (row - cursor) % 8
        table[name] = (cursor, row, rows, start % 128)
        cursor += rows
    return table, (cursor + 32 + 7) // 8 * 8


TABLE, STAGE_ROWS = segment_table()


def lane_of(rows):
    return lax.broadcasted_iota(jnp.int32, (rows, 128), 1)


def pack_rows(stage, packed):
    def piece(name, first, rows):
        base, row, _, shift = TABLE[name]
        at = base - row + first
        here = stage[pl.ds(at, rows)]
        if shift == 0:
            return here
        above = stage[pl.ds(at - 1, rows)]
        return jnp.where(
            lane_of(rows) >= shift, pltpu.roll(here, shift, 1), pltpu.roll(above, shift, 1)
        )

    done = set()
    for name, _, _ in SEGMENTS:
        _, row, rows, shift = TABLE[name]
        low = -(-(row + (1 if shift else 0)) // 16) * 16
        high = (row + rows) // 16 * 16
        if high <= low:
            continue
        done.update(range(low, high, 16))
        turns = (high - low) // 128

        @pl.loop(0, turns)
        def _(turn):
            first = pl.multiple_of(low + turn * 128, 16)
            packed[pl.ds(first, 128)] = piece(name, first, 128).astype(BF)

        for first in range(low + turns * 128, high, 16):
            packed[pl.ds(first, 16)] = piece(name, first, 16).astype(BF)
    for first in range(0, PACK_ROWS, 16):
        if first in done:
            continue
        total = jnp.zeros((16, 128), F32)
        for name, _, _ in SEGMENTS:
            _, row, rows, shift = TABLE[name]
            if row < first + 16 and row + rows + (1 if shift else 0) > first:
                total = total + piece(name, first, 16)
        packed[pl.ds(first, 16)] = total.astype(BF)


def stage_wide(stage, name, ref, step):
    base = TABLE[name][0]
    rows, wide = ref.shape[0], ref.shape[1] // 128

    @pl.loop(0, rows // step)
    def _(turn):
        first = pl.multiple_of(turn * step, step)
        for block in range(wide):
            stage[pl.ds(base + first * wide + block, step, stride=wide), :] = ref[
                pl.ds(first, step), pl.ds(block * 128, 128)
            ].astype(F32)


def stage_heads(stage, name, ref, lanes, column):
    base = TABLE[name][0]
    for head in range(2):
        column[head] = ref[:, pl.ds(lanes + head * 128, 128)]

    @pl.loop(0, 5)
    def _(turn):
        lane = lane_of(64)
        rows = [jnp.zeros((64, 128), F32) for _ in range(5)]
        for block in range(8):
            item, head = block // 2, block % 2
            value = column[head, pl.ds(turn * 256 + item, 64, stride=4)]
            offset = block * HD
            first, shift = offset // 128, offset % 128
            if shift:
                value = pltpu.roll(value, shift, 1)
            if shift + HD > 128:
                rows[first] = rows[first] + jnp.where(lane >= shift, value, 0.0)
                rows[first + 1] = rows[first + 1] + jnp.where(
                    lane < shift + HD - 128, value, 0.0
                )
            else:
                rows[first] = rows[first] + value
        for index in range(5):
            stage[pl.ds(base + turn * 320 + index, 64, stride=5), :] = rows[index]


def stage_head_bias(stage, name, ref, lanes):
    base = TABLE[name][0]
    lane = lane_of(1)
    first = ref[0:1, pl.ds(lanes, 128)]
    second = pltpu.roll(ref[0:1, pl.ds(lanes + 128, 128)], HD, 1)
    stage[pl.ds(base, 1)] = first + jnp.where(lane >= HD, second, 0.0)
    stage[pl.ds(base + 1, 1)] = jnp.where(lane < 2 * HD - 128, second, 0.0)


def stage_share(stage, name, ref, first, count, place):
    base = TABLE[name][0] + place.dp * count * 10
    for block in range(10):
        stage[pl.ds(base + block, count, stride=10), :] = ref[
            pl.ds(first, count), pl.ds(block * 128, 128)
        ]


def stage_up(stage, ref, place):
    base = TABLE["up"][0]
    lane = lane_of(128)
    for quarter in range(4):

        @pl.when(place.dp == quarter)
        def _():
            for block in range(10):
                columns = pl.ds(block * 128, 128)
                first = ref[pl.ds(0, 128), columns].T
                second = jnp.where(lane < 32, ref[pl.ds(128, 128), columns].T, 0.0)
                shift = 32 * quarter
                if shift:
                    first = pltpu.roll(first, shift, 1)
                    second = pltpu.roll(second, shift, 1)
                    second = second + jnp.where(lane < shift, first, 0.0)
                    first = jnp.where(lane >= shift, first, 0.0)
                at = base + block * 640 + quarter
                stage[pl.ds(at, 128, stride=5), :] = first
                stage[pl.ds(at + 1, 128, stride=5), :] = second


def norm_back(frames_ref, middle_ref, gain_ref, grad_ref):
    def write(rows, total):
        value = frames_ref[rows].astype(F32)
        center = value - jnp.mean(value, axis=-1, keepdims=True)
        spread = jnp.mean(center * center, axis=-1, keepdims=True)
        root = lax.rsqrt(spread + NORM_EPSILON)
        scaled = center * root
        pull = total * gain_ref[...]
        along = jnp.mean(pull * scaled, axis=-1, keepdims=True)
        grad_ref[rows] = middle_ref[rows] + root * (
            pull - jnp.mean(pull, axis=-1, keepdims=True) - scaled * along
        )

    return write


def fetch(first, rows, sems, grad, weight, frames, middle):
    span = pl.ds(first, rows)
    pairs = (
        (grad[0].at[:, span], grad[1]),
        weight,
        (frames[0].at[span], frames[1]),
        (middle[0].at[span], middle[1]),
    )
    copies = [
        pltpu.make_async_copy(source, target, sems.at[index])
        for index, (source, target) in enumerate(pairs)
    ]
    for copy in copies:
        copy.start()
    return copies


def fetch_scratch(rows):
    return [
        pltpu.VMEM((8, rows, 768), BF),
        pltpu.VMEM((768, 1280), BF),
        pltpu.VMEM((rows, 1280), BF),
        pltpu.VMEM((rows, 1280), F32),
        dma(4),
    ]


def line_product(place, grad_ref, weight_ref, rows, result, bufs, sems):
    def produce(level, core, tile):
        return jnp.dot(
            grad_ref[level * 2 + core, tile],
            weight_ref[...],
            preferred_element_type=F32,
        )

    tiles = [pl.ds(0, rows)]
    return line_reduce(place, produce, tiles, result, bufs, sems, True)


FIRST_ROWS = 128


def finish_kernel(
    split, grad_in, weight_in, joined_ref, bias_ref, bias_column_ref, sum_ref, out_ref,
    up_bias_ref, small_ref, peak_ref, frames_in, middle_in, gain_ref, shift_ref, cap_ref,
    input_grad_ref, grads_ref, small_out, factor_ref,
    grad_ref, weight_ref, frames_ref, middle_ref, load,
    stage, packed, sum_rows, column, tiles, small_in, small_all, peak_all, edge,
    local, small_send, small_recv, plane_send, plane_recv, *scratch,
):
    place = Place()
    line_bufs, line_sems, bufs, sems = split(scratch)
    loads = fetch(
        0,
        FIRST_ROWS,
        load,
        (grad_in, grad_ref),
        (weight_in, weight_ref),
        (frames_in, frames_ref),
        (middle_in, middle_ref),
    )
    greet(place, mp_all=True, plane=True)
    peers = (place.dpx, place.dpy, place.dpd)

    def tell(index, source, target, group, act):
        act(
            remote(
                source,
                target.at[place.dp],
                plane_send.at[index],
                plane_recv.at[index],
                group,
                place.mp,
            )
        )

    def heard(index, target, group):
        block = target.at[group]
        remote(
            block, block, plane_send.at[index], plane_recv.at[index], group, place.mp
        ).wait_recv()

    line = line_product(
        place,
        grad_ref,
        weight_ref,
        FIRST_ROWS,
        norm_back(frames_ref, middle_ref, gain_ref, input_grad_ref),
        line_bufs,
        line_sems,
    )
    for index, group in enumerate(peers):
        tell(index, peak_ref, peak_all, group, lambda copy: copy.start())
    for copy in loads:
        copy.wait()

    for block in range(10):
        lanes = pl.ds(block * 128, 128)
        weight = weight_ref[:, lanes].astype(F32)
        turned = joined_ref[lanes].T
        whole = jnp.sum(weight * bias_column_ref[...], axis=0, keepdims=True)
        along = jnp.sum(weight * turned, axis=0, keepdims=True)
        tiles[pl.ds(block, 1)] = (along - shift_ref[:, lanes] * whole) / gain_ref[:, lanes]
        tiles[pl.ds(10 + block, 1)] = whole
    tiles[pl.ds(20, 44)] = small_ref[...]
    for run in range(8):
        edge[run] = tiles[pl.ds(run * 15 // 2, 8)]
    mixing = exchange(place, edge, small_in, local, small_send, small_recv)
    next(mixing)

    stage[...] = jnp.zeros(stage.shape, F32)
    for name, lanes in (("query", 0), ("key", 256), ("value", 512)):
        stage_heads(stage, name, joined_ref, lanes, column)
    stage_head_bias(stage, "query_bias", bias_ref, 0)
    stage_head_bias(stage, "value_bias", bias_ref, 512)
    stage_share(stage, "out", out_ref, 0, 40, place)
    stage_share(stage, "down", sum_ref, 160, 160, place)
    stage_up(stage, sum_ref, place)
    stage[pl.ds(TABLE["up_bias"][0], 5)] = up_bias_ref[...]
    pack_rows(stage, packed)

    def produce(group, core, start, rows):
        first = pl.multiple_of(group * GROUP_STEP + start, 16)
        return packed[pl.ds(first, GROUP_ROWS // 2)].astype(F32)

    def result(rows, total):
        sum_rows[rows] = total

    half = GROUP_ROWS // 2
    plane = plane_reduce(place, produce, half, half, result, bufs, sems, False)
    next(plane)
    next(plane)
    next(line)
    next(line)
    for _ in mixing:
        pass
    small_all[place.dp] = jnp.sum(small_in[...], axis=0)
    for index, group in enumerate(peers):
        tell(3 + index, small_all.at[place.dp], small_all, group, lambda copy: copy.start())
    next(plane)
    next(line)
    next(line)
    drive(line, plane)
    for index, group in enumerate(peers):
        heard(index, peak_all, group)
        heard(3 + index, small_all, group)
    top = peak_ref[...]
    for group in peers:
        top = jnp.maximum(top, peak_all[group])
    roots = []
    for head in range(2):
        peak = jnp.max(jnp.max(top[head], axis=0, keepdims=True), axis=1, keepdims=True)
        roots.append(
            jnp.sqrt(cap_ref[...] / jnp.maximum(peak * (1.0 / math.sqrt(HD)), cap_ref[...]))
        )
    factor_ref[...] = jnp.ones(factor_ref.shape, F32)

    @pl.when(place.dp == 0)
    def _():
        full = KEY_END // 128 // 5 * 5
        for index in range(5):
            entry = (lane_of(1) + 128 * index).astype(F32)
            block = jnp.floor((entry + 0.5) * (1.0 / HD))
            odd = block - 2.0 * jnp.floor(block * 0.5) > 0.5
            factor = jnp.where(odd, roots[1], roots[0])
            factor_ref[pl.ds(index, full // 5, stride=5), :] = jnp.broadcast_to(
                factor, (full // 5, 128)
            )
            left = KEY_END - (full + index) * 128
            if left > 0:
                factor_ref[pl.ds(full + index, 1)] = jnp.where(lane_of(1) < left, factor, 1.0)

    whole = jnp.sum(small_all[...], axis=0)
    lane = lane_of(8)
    row = lax.broadcasted_iota(jnp.int32, (8, 128), 0)
    tiles[...] = jnp.zeros((64, 128), F32)
    tiles[pl.ds(8, 8)] = whole
    ahead = pltpu.roll(tiles[pl.ds(9, 8)], 64, 1)
    here = pltpu.roll(whole, 64, 1)
    odd = jnp.where(lane < 64, here, ahead)
    run_of = jnp.where(place.c == 1, odd, whole)
    run_of = jnp.where(jnp.logical_and(row == 7, lane >= 64), 0.0, run_of)
    small_out[...] = run_of
    tiles[pl.ds(8, 8)] = run_of
    wide = lane_of(16)
    entry = jnp.where(
        wide >= 64, pltpu.roll(tiles[pl.ds(1, 16)], 64, 1), pltpu.roll(tiles[pl.ds(0, 16)], 64, 1)
    )

    @pl.when(place.dp == 3)
    def _():
        sum_rows[pl.ds(GROUP_STEP, 16)] += entry

    for group in range(4):

        @pl.when(place.dp == group)
        def _():
            down, shift = 480 * group // 128, 480 * group % 128
            if shift == 0:
                grads_ref[...] = sum_rows[pl.ds(0, SHARE_ROWS)]
            else:
                for first in range(0, SHARE_ROWS, 1208):
                    size = min(1208, SHARE_ROWS - first)
                    grads_ref[pl.ds(first, size)] = jnp.where(
                        lane_of(size) < 128 - shift,
                        pltpu.roll(sum_rows[pl.ds(first + down, size)], 128 - shift, 1),
                        pltpu.roll(sum_rows[pl.ds(first + down + 1, size)], 128 - shift, 1),
                    )

    for index, group in enumerate(peers):
        tell(index, peak_ref, peak_all, group, lambda copy: copy.wait_send())
        tell(3 + index, small_all.at[place.dp], small_all, group, lambda copy: copy.wait_send())


def finish(grads, weight, joined, bias, sums, out, up_bias, small, peaks, frames, middle, gain, shift, cap):
    shapes, split = flatten(
        *line_reduce_scratch(FIRST_ROWS, 1280, True),
        *plane_reduce_scratch(GROUP_ROWS // 2, 128, False),
    )
    return pl.pallas_call(
        functools.partial(finish_kernel, split),
        out_shape=(
            jax.ShapeDtypeStruct((FIRST_ROWS, 1280), F32),
            jax.ShapeDtypeStruct((SHARE_ROWS, 128), F32),
            jax.ShapeDtypeStruct((8, 128), F32),
            jax.ShapeDtypeStruct((SHARE_ROWS, 128), F32),
        ),
        in_specs=[ANY, ANY] + [VMEM] * 8 + [ANY, ANY, VMEM, VMEM, VMEM],
        out_specs=(VMEM,) * 4,
        scratch_shapes=[
            *fetch_scratch(FIRST_ROWS),
            pltpu.VMEM((STAGE_ROWS, 128), F32),
            pltpu.VMEM((PACK_ROWS, 128), BF),
            pltpu.VMEM((GROUP_ROWS, 128), F32),
            pltpu.VMEM((2, 1280, 128), F32),
            pltpu.VMEM((64, 128), F32),
            pltpu.VMEM((8, 8, 128), F32),
            pltpu.VMEM((4, 8, 128), F32),
            pltpu.VMEM((4,) + peaks.shape, F32),
            pltpu.VMEM((8, 8, 128), F32),
            pltpu.SemaphoreType.DMA(()),
            dma(8),
            dma(8),
            dma(6),
            dma(6),
            *shapes,
        ],
        compiler_params=params(7, 62),
        name="finish",
    )(
        grads, weight, joined, bias[None], bias[:, None], sums, out, up_bias, small, peaks,
        frames, middle, gain, shift, cap,
    )


def share_master_kernel(
    split, rows_ref, grad_in, weight_in, frames_in, middle_in, gain_ref,
    whole_out, input_grad_ref,
    grad_ref, weight_ref, frames_ref, middle_ref, load,
    whole_ref, parts, turned, store, send, recv, *scratch,
):
    place = Place()
    line_bufs, line_sems = split(scratch)
    loads = fetch(
        FIRST_ROWS,
        ROWS - FIRST_ROWS,
        load,
        (grad_in, grad_ref),
        (weight_in, weight_ref),
        (frames_in, frames_ref),
        (middle_in, middle_ref),
    )
    greet(place, line=True, plane=True)
    line = line_product(
        place,
        grad_ref,
        weight_ref,
        ROWS - FIRST_ROWS,
        norm_back(frames_ref, middle_ref, gain_ref, input_grad_ref),
        line_bufs,
        line_sems,
    )
    dp, mp, dpx, dpy, dpd = place.dp, place.mp, place.dpx, place.dpy, place.dpd
    half = GROUP_ROWS // 2
    part_a, part_b = pl.ds(0, half), pl.ds(half, half)
    for group in range(4):

        @pl.when(dp == group)
        def _():
            down, shift = 480 * group // 128, 480 * group % 128
            turned[pl.ds(0, 16)] = jnp.zeros((16, 128), F32)
            turned[pl.ds(16, SHARE_ROWS)] = rows_ref[...]
            turned[pl.ds(16 + SHARE_ROWS, 24)] = jnp.zeros((24, 128), F32)
            for first in range(0, GROUP_ROWS, 1208):
                here = turned[pl.ds(16 + first - down, 1208)]
                if shift:
                    here = jnp.where(
                        lane_of(1208) >= shift,
                        pltpu.roll(here, shift, 1),
                        pltpu.roll(turned[pl.ds(15 + first - down, 1208)], shift, 1),
                    )
                parts[dp, pl.ds(first, 1208)] = here.astype(BF)


    def hop(index, block, target):
        return remote(block, block, send.at[index], recv.at[index], target, mp)

    own = parts.at[dp]
    sends = [hop(0, own, dpx), hop(1, own, dpy)]
    for copy in sends:
        copy.start()

    stores = []

    def keep(index, first, rows):
        span = pl.ds(pl.multiple_of(first, 16), rows)
        stores.append(
            pltpu.make_async_copy(whole_ref.at[span], whole_out.at[span], store.at[index])
        )
        stores[-1].start()

    def unpack(group):
        for start in range(32, GROUP_STEP, 2384):
            at = pl.multiple_of(group * GROUP_STEP + start, 16)
            whole_ref[pl.ds(at, 2384)] = parts[group, pl.ds(start, 2384)].astype(F32)
        keep(len(stores), group * GROUP_STEP + 32, GROUP_STEP - 32)

    for copy in loads:
        copy.wait()
    next(line)
    next(line)
    unpack(dp)
    hop(0, parts.at[dpx], dpx).wait_recv()
    sends.append(hop(2, parts.at[dpx, part_a], dpy))
    sends[-1].start()
    hop(1, parts.at[dpy], dpy).wait_recv()
    sends.append(hop(3, parts.at[dpy, part_b], dpx))
    sends[-1].start()
    unpack(dpx)
    unpack(dpy)
    next(line)
    next(line)
    hop(2, parts.at[dpd, part_a], dpy).wait_recv()
    hop(3, parts.at[dpd, part_b], dpx).wait_recv()
    unpack(dpd)
    for group in range(4):
        first = parts[group, pl.ds(0, 32)].astype(F32)
        if group > 0:
            first = first + parts[group - 1, pl.ds(GROUP_STEP, 32)].astype(F32)
        whole_ref[pl.ds(group * GROUP_STEP, 32)] = first
        keep(4 + group, group * GROUP_STEP, 32)
    whole_ref[pl.ds(4 * GROUP_STEP, 16)] = parts[3, pl.ds(GROUP_STEP, 16)].astype(F32)
    keep(8, 4 * GROUP_STEP, 16)
    for copy in sends:
        copy.wait_send()
    drive(line)
    for copy in stores:
        copy.wait()


def share_master(rows, grads, weight, frames, middle, gain):
    shapes, split = flatten(*line_reduce_scratch(ROWS - FIRST_ROWS, 1280, True))
    return pl.pallas_call(
        functools.partial(share_master_kernel, split),
        out_shape=(
            jax.ShapeDtypeStruct((PACK_END, 128), F32),
            jax.ShapeDtypeStruct((ROWS - FIRST_ROWS, 1280), F32),
        ),
        in_specs=[VMEM, ANY, ANY, ANY, ANY, VMEM],
        out_specs=(ANY, VMEM),
        scratch_shapes=[
            *fetch_scratch(ROWS - FIRST_ROWS),
            pltpu.VMEM((PACK_END, 128), F32),
            pltpu.VMEM((4, GROUP_ROWS, 128), BF),
            pltpu.VMEM((SHARE_ROWS + 40, 128), F32),
            dma(9),
            dma(4),
            dma(4),
            *shapes,
        ],
        compiler_params=params(8, 60),
        name="share_master",
    )(rows, grads, weight, frames, middle, gain)


STEP_ENTRIES = 1024 * 76


def optimize_kernel(
    rates_ref, factor_ref, grads_ref, master_ref, first_ref, second_ref,
    owned_out, master_out, first_out, second_out, padded_out,
):
    entry = lax.broadcasted_iota(jnp.int32, (1, STEP_ENTRIES), 1)
    grads = grads_ref[...]
    first = BETA_FIRST * first_ref[...] + (1.0 - BETA_FIRST) * grads
    second = BETA_SECOND * second_ref[...] + (1.0 - BETA_SECOND) * grads * grads
    change = first * rates_ref[0] / (jnp.sqrt(second * rates_ref[1]) + ADAM_EPSILON)
    master = (master_ref[...] * rates_ref[2] - change) * factor_ref[...]
    owned_out[...] = grads
    master_out[...] = master
    first_out[...] = first
    second_out[...] = second
    left = SHARE_ENTRIES - pl.program_id(0) * STEP_ENTRIES
    padded_out[...] = jnp.where(entry < left, master, 0.0)


def optimize(rates, factor, grads, master, first, second):
    block = pl.BlockSpec((1, STEP_ENTRIES), lambda step: (0, step))
    share = jax.ShapeDtypeStruct((1, SHARE_ENTRIES), F32)
    return pl.pallas_call(
        optimize_kernel,
        grid=(pl.cdiv(SHARE_ENTRIES, STEP_ENTRIES),),
        out_shape=(share,) * 4 + (jax.ShapeDtypeStruct((1, SHARE_ROWS * 128), F32),),
        in_specs=[pl.BlockSpec(memory_space=pltpu.SMEM)] + [block] * 5,
        out_specs=(block,) * 5,
        compiler_params=pltpu.CompilerParams(vmem_limit_bytes=62 << 20),
        name="optimize",
    )(rates, factor, grads, master, first, second)


def fast_body(
    frames,
    lengths,
    key_mask,
    cotangent,
    gain_one,
    shift_one,
    query_weight,
    query_bias,
    key_weight,
    value_weight,
    value_bias,
    out_weight,
    out_bias,
    gain_two,
    shift_two,
    up_weight,
    up_bias,
    down_weight,
    down_bias,
    master,
    moment_one,
    moment_two,
    adam_step,
    hyper_rates,
):
    group = lax.axis_index("dp")
    position = jnp.arange(1024, dtype=jnp.int32)
    keep_query = position[None, :] < lengths[:, None]
    keep_key = jnp.logical_and(keep_query, key_mask == 1)
    mask = jnp.where(keep_key, 0.0, MASK_VALUE)[:, :, None]
    live = keep_query.astype(F32)[:, None, :]
    gain_first = gain_one.astype(F32)
    shift_first = shift_one.astype(F32)
    gain_second = gain_two.astype(F32)
    shift_second = shift_two.astype(F32)
    inputs = frames.transpose(1, 0, 2).reshape(ROWS, 1280).astype(F32)
    upstream_low = cotangent.transpose(1, 0, 2).reshape(ROWS, 1280)
    upstream = upstream_low.astype(F32)
    def head_lanes(bias):
        lanes = bias.astype(F32).reshape(2, HD)
        return jnp.pad(lanes, ((0, 0), (0, 128 - HD))).reshape(256)

    joined_bias = jnp.concatenate(
        [head_lanes(query_bias), jnp.zeros((256,), F32), head_lanes(value_bias)]
    )[None]
    frame_rows = frames.transpose(1, 0, 2).reshape(ROWS, 1280)
    quarter = group * 160
    up_share = lax.dynamic_slice_in_dim(up_weight, quarter, 160, 1).T
    down_share = lax.dynamic_slice_in_dim(down_weight, quarter, 160, 0)
    bias_share = lax.dynamic_slice_in_dim(up_bias, quarter, 160, 0)
    bias_rows = jnp.pad(bias_share[None], ((0, 15), (0, 1280 - 160)))
    message = jnp.concatenate([up_share, bias_rows])
    outer_start = jnp.minimum(group * 48, 112)
    outer = lax.dynamic_slice_in_dim(out_weight, outer_start, 48, 0)
    normed_full, qkv, upstream_full, joined_weight = project(
        frame_rows,
        gain_first[None],
        shift_first[None],
        upstream_low,
        query_weight.T,
        key_weight.T,
        value_weight.T,
        joined_bias,
    )
    qkv = qkv.reshape(8, 3, 128, 768)
    attended, logs, peaks, gathered, out_rows, middle, normed_two = attend(
        qkv,
        mask,
        live,
        message,
        outer,
        frame_rows,
        out_bias.astype(F32)[None],
        gain_second[None],
        shift_second[None],
    )
    up_lanes = gathered[:, 160, :160].reshape(1, 640).astype(F32)
    out_rows = out_rows.reshape(8, 160, 1280)

    normed_two_grad, hidden, feed_grads, _, down_all = feed_forward(
        normed_two, upstream_full, gathered, down_share, up_lanes
    )

    _, norm_two_pull = jax.vjp(layer_norm, middle, gain_second, shift_second)
    middle_norm_grad, gain_two_grad, shift_two_grad = norm_two_pull(normed_two_grad)
    middle_grad = upstream + middle_norm_grad
    branch_grad = middle_grad.astype(BF)
    branch_clips = branch_grad.reshape(3, 128, 1280)
    out_grad = jnp.einsum("schr,crd->shd", attended, branch_clips, preferred_element_type=F32)
    attended_grad = jnp.einsum(
        "shd,crd->schr", out_rows, branch_clips, preferred_element_type=F32
    ).astype(BF)
    out_quarters = jnp.pad(
        out_grad.astype(BF).reshape(4, 2, 4, 40, 1280), ((0, 0),) * 3 + ((0, 8), (0, 0))
    )
    out_quarters = out_quarters.transpose(2, 1, 0, 3, 4).reshape(4, 2, 192, 1280)
    joined_grad, feed, feed_sum, out_sum, joined_weight_grad, joined_bias_grad = attend_back(
        qkv, mask, logs, attended_grad, hidden, down_all, feed_grads, out_quarters, normed_full
    )
    layer_out = (middle + feed + down_bias.astype(F32)).astype(BF)
    joined_grad = joined_grad.reshape(8, ROWS, 768)
    joined_bias_grad = joined_bias_grad[0]

    level = lax.axis_index("mp") // 2
    up_bias_share = lax.dynamic_slice_in_dim(feed_sum[320], level * 160, 160, 0)
    up_bias_rows = lax.dynamic_update_slice(
        jnp.zeros((640,), F32), up_bias_share, (quarter,)
    ).reshape(5, 128)
    small_rows = jnp.concatenate(
        [
            jnp.sum(branch_grad.astype(F32), axis=0),
            gain_two_grad,
            shift_two_grad,
            jnp.sum(upstream, axis=0),
            jnp.zeros((512,), F32),
        ]
    ).reshape(44, 128)
    first_grad, grad_rows, small_sum, factor_rows = finish(
        joined_grad,
        joined_weight,
        joined_weight_grad,
        joined_bias_grad,
        feed_sum,
        out_sum,
        up_bias_rows,
        small_rows,
        peaks,
        frame_rows,
        middle_grad,
        gain_first[None],
        shift_first[None],
        hyper_rates[2].reshape(1, 1),
    )
    small_total = small_sum.reshape(1024)[:960]
    learn_rate = hyper_rates[0]
    weight_decay = hyper_rates[1]
    step_count = adam_step[0].astype(F32)
    rates = jnp.stack(
        [
            learn_rate / (1.0 - jnp.power(BETA_FIRST, step_count)),
            1.0 / (1.0 - jnp.power(BETA_SECOND, step_count)),
            1.0 - learn_rate * weight_decay,
        ]
    )
    owned_grads, master_new, first_new, second_new, padded = optimize(
        rates,
        factor_rows.reshape(1, SHARE_ROWS * 128),
        grad_rows.reshape(1, SHARE_ROWS * 128),
        master,
        moment_one,
        moment_two,
    )
    whole, second_grad = share_master(
        padded.reshape(SHARE_ROWS, 128),
        joined_grad,
        joined_weight,
        frame_rows,
        middle_grad,
        gain_first[None],
    )
    input_grad = jnp.concatenate([first_grad, second_grad])
    whole = lax.optimization_barrier(whole.reshape(1, PACK_END * 128))
    weights_new = whole[:, : 4 * SHARE_ENTRIES].astype(BF)
    return (
        layer_out.reshape(3, 128, 1280).transpose(1, 0, 2),
        input_grad.reshape(3, 128, 1280).transpose(1, 0, 2),
        owned_grads,
        master_new,
        first_new,
        second_new,
        weights_new,
        small_total,
    )


def body(
    frames,
    lengths,
    key_mask,
    cotangent,
    gain_one,
    shift_one,
    query_weight,
    query_bias,
    key_weight,
    value_weight,
    value_bias,
    out_weight,
    out_bias,
    gain_two,
    shift_two,
    up_weight,
    up_bias,
    down_weight,
    down_bias,
    master,
    moment_one,
    moment_two,
    adam_step,
    hyper_rates,
):
    local_rows, clip_count, model_width = frames.shape
    total_rows = key_mask.shape[1]
    head_cols = query_weight.shape[1]
    heads_here = head_cols // HD
    block_rows = min(512, total_rows)
    blocks = total_rows // block_rows
    score_scale = 1.0 / math.sqrt(HD)
    position = jnp.arange(total_rows, dtype=jnp.int32)
    keep_query = position[None, :] < lengths[:, None]
    keep_key = jnp.logical_and(keep_query, key_mask == 1)
    gain_first = gain_one.astype(jnp.float32)
    shift_first = shift_one.astype(jnp.float32)
    gain_second = gain_two.astype(jnp.float32)
    shift_second = shift_two.astype(jnp.float32)
    inputs = frames.astype(jnp.float32)
    normed = layer_norm(inputs, gain_first, shift_first).astype(jnp.bfloat16)
    joined_weight = jnp.concatenate([query_weight, key_weight, value_weight], axis=1)
    joined_bias = jnp.concatenate(
        [
            query_bias.astype(jnp.float32),
            jnp.zeros((head_cols,), jnp.float32),
            value_bias.astype(jnp.float32),
        ]
    )
    normed_full = lax.all_gather(normed, "mp", axis=0, tiled=True)
    projected = (
        jnp.einsum("rcd,de->rce", normed_full, joined_weight, preferred_element_type=jnp.float32)
        + joined_bias
    ).astype(jnp.bfloat16)
    query = projected[:, :, :head_cols].reshape(total_rows, clip_count, heads_here, HD)
    keys = projected[:, :, head_cols : 2 * head_cols].reshape(
        total_rows, clip_count, heads_here, HD
    )
    values = projected[:, :, 2 * head_cols :].reshape(total_rows, clip_count, heads_here, HD)

    def scores_of(row_start):
        query_block = lax.dynamic_slice_in_dim(query, row_start, block_rows, 0)
        raw_scores = (
            jnp.einsum("qchd,kchd->chqk", query_block, keys, preferred_element_type=jnp.float32)
            * score_scale
        )
        return (query_block, jnp.where(keep_key[:, None, None, :], raw_scores, MASK_VALUE))

    def forward_block(block_index):
        row_start = block_index * block_rows
        _, masked = scores_of(row_start)
        row_peak = jnp.max(masked, axis=-1, keepdims=True)
        exp_scores = jnp.exp(masked - row_peak)
        row_total = jnp.sum(exp_scores, axis=-1, keepdims=True)
        probability = (exp_scores / row_total).astype(jnp.bfloat16)
        attended = jnp.einsum(
            "chqk,kchd->qchd", probability, values, preferred_element_type=jnp.float32
        ).astype(jnp.bfloat16)
        live_rows = lax.dynamic_slice_in_dim(keep_query, row_start, block_rows, 1)
        block_peak = jnp.max(
            jnp.where(live_rows[:, None, :], row_peak[..., 0], MASK_VALUE), axis=(0, 2)
        )
        return (attended, (row_peak + jnp.log(row_total))[..., 0], block_peak)

    attended_blocks, log_totals, block_peaks = lax.map(forward_block, jnp.arange(blocks))
    attended_full = attended_blocks.reshape(total_rows, clip_count, head_cols)
    head_peak = lax.pmax(jnp.max(block_peaks, axis=0), "dp")
    rows_here = attended_full
    attn_branch = lax.psum_scatter(
        jnp.einsum("rck,kd->rcd", rows_here, out_weight, preferred_element_type=jnp.float32),
        "mp",
        scatter_dimension=0,
        tiled=True,
    ) + out_bias.astype(jnp.float32)
    middle = inputs + attn_branch
    normed_two = layer_norm(middle, gain_second, shift_second).astype(jnp.bfloat16)
    upstream = cotangent.astype(jnp.float32)
    normed_two_full = lax.all_gather(normed_two, "mp", axis=0, tiled=True)
    before = jnp.einsum(
        "rcd,df->rcf", normed_two_full, up_weight, preferred_element_type=jnp.float32
    ) + up_bias.astype(jnp.float32)
    hidden = exact_gelu(before).astype(jnp.bfloat16)
    rows_here = hidden
    feed = lax.psum_scatter(
        jnp.einsum(
            "rcf,fd->rcd", rows_here, down_weight, preferred_element_type=jnp.float32
        ).astype(jnp.bfloat16),
        "mp",
        scatter_dimension=0,
        tiled=True,
    ).astype(jnp.float32) + down_bias.astype(jnp.float32)
    layer_out = (middle + feed).astype(jnp.bfloat16)
    feed_grad_full = lax.all_gather(cotangent, "mp", axis=0, tiled=True)
    down_grad = jnp.einsum(
        "rcf,rcd->fd", hidden, feed_grad_full, preferred_element_type=jnp.float32
    )
    hidden_grad = jnp.einsum(
        "rcd,fd->rcf", feed_grad_full, down_weight, preferred_element_type=jnp.float32
    )
    _, gelu_pull = jax.vjp(exact_gelu, before)
    before_grad = gelu_pull(hidden_grad)[0].astype(jnp.bfloat16)
    up_bias_grad = jnp.sum(before_grad.astype(jnp.float32), axis=(0, 1))
    up_grad = jnp.einsum(
        "rcd,rcf->df", normed_two_full, before_grad, preferred_element_type=jnp.float32
    )
    rows_here = before_grad
    normed_two_grad = lax.psum_scatter(
        jnp.einsum("rcf,df->rcd", rows_here, up_weight, preferred_element_type=jnp.float32),
        "mp",
        scatter_dimension=0,
        tiled=True,
    )
    _, norm_two_pull = jax.vjp(layer_norm, middle, gain_second, shift_second)
    middle_norm_grad, gain_two_grad, shift_two_grad = norm_two_pull(normed_two_grad)
    middle_grad = upstream + middle_norm_grad
    branch_grad = middle_grad.astype(jnp.bfloat16)
    branch_grad_full = lax.all_gather(branch_grad, "mp", axis=0, tiled=True)
    out_grad = jnp.einsum(
        "rck,rcd->kd", attended_full, branch_grad_full, preferred_element_type=jnp.float32
    )
    attended_grad = jnp.einsum(
        "rcd,kd->rck", branch_grad_full, out_weight, preferred_element_type=jnp.float32
    ).astype(jnp.bfloat16)
    attended_grad = attended_grad.reshape(total_rows, clip_count, heads_here, HD)

    def backward_block(carry, block_index):
        key_total, value_total = carry
        row_start = block_index * block_rows
        query_block, masked = scores_of(row_start)
        log_total = log_totals[block_index]
        probability = jnp.exp(masked - log_total[..., None])
        grad_block = lax.dynamic_slice_in_dim(attended_grad, row_start, block_rows, 0)
        value_total = value_total + jnp.einsum(
            "chqk,qchd->kchd",
            probability.astype(jnp.bfloat16),
            grad_block,
            preferred_element_type=jnp.float32,
        )
        prob_grad = jnp.einsum(
            "qchd,kchd->chqk", grad_block, values, preferred_element_type=jnp.float32
        )
        score_grad = (
            probability * (prob_grad - jnp.sum(probability * prob_grad, axis=-1, keepdims=True))
        ).astype(jnp.bfloat16)
        query_grad = (
            jnp.einsum("chqk,kchd->qchd", score_grad, keys, preferred_element_type=jnp.float32)
            * score_scale
        ).astype(jnp.bfloat16)
        key_total = (
            key_total
            + jnp.einsum(
                "chqk,qchd->kchd", score_grad, query_block, preferred_element_type=jnp.float32
            )
            * score_scale
        )
        return ((key_total, value_total), query_grad)

    empty_grad = jnp.zeros((total_rows, clip_count, heads_here, HD), jnp.float32)
    (key_total, value_total), query_blocks = lax.scan(
        backward_block, (empty_grad, empty_grad), jnp.arange(blocks)
    )
    joined_grad = jnp.concatenate(
        [
            query_blocks.reshape(total_rows, clip_count, head_cols),
            key_total.reshape(total_rows, clip_count, head_cols).astype(jnp.bfloat16),
            value_total.reshape(total_rows, clip_count, head_cols).astype(jnp.bfloat16),
        ],
        axis=-1,
    )
    joined_bias_grad = jnp.sum(joined_grad.astype(jnp.float32), axis=(0, 1))
    normed_back = lax.all_gather(normed, "mp", axis=0, tiled=True)
    joined_weight_grad = jnp.einsum(
        "rcd,rce->de", normed_back, joined_grad, preferred_element_type=jnp.float32
    )
    rows_here = joined_grad
    normed_grad = lax.psum_scatter(
        jnp.einsum(
            "rce,de->rcd", rows_here, joined_weight, preferred_element_type=jnp.float32
        ).astype(jnp.bfloat16),
        "mp",
        scatter_dimension=0,
        tiled=True,
    ).astype(jnp.float32)
    _, norm_one_pull = jax.vjp(layer_norm, inputs, gain_first, shift_first)
    input_norm_grad, gain_one_grad, shift_one_grad = norm_one_pull(normed_grad)
    input_grad = middle_grad + input_norm_grad
    out_bias_grad = jnp.sum(branch_grad.astype(jnp.float32), axis=(0, 1))
    down_bias_grad = jnp.sum(upstream, axis=(0, 1))
    small_terms = jnp.concatenate(
        [
            gain_one_grad,
            shift_one_grad,
            out_bias_grad,
            gain_two_grad,
            shift_two_grad,
            down_bias_grad,
        ]
    )
    small_share = lax.psum_scatter(small_terms, "mp", scatter_dimension=0, tiled=True)
    small_total = lax.psum(small_share, "dp")
    packed = jnp.concatenate(
        [
            joined_weight_grad[:, :head_cols].reshape(-1),
            joined_bias_grad[:head_cols],
            joined_weight_grad[:, head_cols : 2 * head_cols].reshape(-1),
            joined_weight_grad[:, 2 * head_cols :].reshape(-1),
            joined_bias_grad[2 * head_cols :],
            out_grad.reshape(-1),
            up_grad.reshape(-1),
            up_bias_grad,
            down_grad.reshape(-1),
            small_share,
        ]
    )
    owned_grads = lax.psum_scatter(
        packed.astype(jnp.bfloat16), "dp", scatter_dimension=0, tiled=True
    ).astype(jnp.float32)
    share_size = owned_grads.shape[0]
    learn_rate = hyper_rates[0]
    weight_decay = hyper_rates[1]
    logit_cap = hyper_rates[2]
    step_count = adam_step[0].astype(jnp.float32)
    first_new = BETA_FIRST * moment_one[0] + (1.0 - BETA_FIRST) * owned_grads
    second_new = BETA_SECOND * moment_two[0] + (1.0 - BETA_SECOND) * owned_grads * owned_grads
    first_hat = first_new / (1.0 - jnp.power(BETA_FIRST, step_count))
    second_hat = second_new / (1.0 - jnp.power(BETA_SECOND, step_count))
    entry_index = lax.axis_index("dp") * share_size + jnp.arange(share_size, dtype=jnp.int32)
    query_end = model_width * head_cols
    query_bias_end = query_end + head_cols
    key_end = query_bias_end + model_width * head_cols
    column = jnp.where(
        entry_index < query_end,
        entry_index % head_cols,
        jnp.where(
            entry_index < query_bias_end,
            entry_index - query_end,
            (entry_index - query_bias_end) % head_cols,
        ),
    )
    head_index = column // HD
    root_factor = jnp.sqrt(logit_cap / jnp.maximum(head_peak, logit_cap))
    head_factor = jnp.zeros((share_size,), jnp.float32)
    for head_number in range(heads_here):
        head_factor = head_factor + jnp.where(
            head_index == head_number, root_factor[head_number], 0.0
        )
    factor = jnp.where(entry_index < key_end, head_factor, 1.0)
    master_here = master[0]
    master_new = (
        master_here
        - learn_rate
        * (first_hat / (jnp.sqrt(second_hat) + ADAM_EPSILON) + weight_decay * master_here)
    ) * factor
    weights_full = lax.all_gather(master_new.astype(jnp.bfloat16), "dp", axis=0, tiled=True)
    return (
        layer_out,
        input_grad,
        owned_grads[None],
        master_new[None],
        first_new[None],
        second_new[None],
        weights_full[None],
        small_total,
    )


def solution(mesh):
    chosen = fast_body if dict(mesh.shape) == {"dp": 4, "mp": 8} else body
    placed = (
        P("mp", "dp", None),
        P("dp"),
        P("dp", None),
        P("mp", "dp", None),
        P(),
        P(),
        P(None, "mp"),
        P("mp"),
        P(None, "mp"),
        P(None, "mp"),
        P("mp"),
        P("mp", None),
        P(),
        P(),
        P(),
        P(None, "mp"),
        P("mp"),
        P("mp", None),
        P(),
        P("mp", "dp"),
        P("mp", "dp"),
        P("mp", "dp"),
        P(),
        P(),
    )
    return jax.shard_map(
        chosen,
        mesh=mesh,
        in_specs=placed,
        out_specs=(
            P("mp", "dp", None),
            P("mp", "dp", None),
            P("mp", "dp"),
            P("mp", "dp"),
            P("mp", "dp"),
            P("mp", "dp"),
            P("mp", None),
            P("mp"),
        ),
        check_vma=False,
    )
```
